32 devices in a mesh: dp: 8 (over z, y), ctx: 4 (over x, core).
Axes of the slice: x: 2, y: 2, z: 4, core: 2. Of those that a mesh axis runs over, the one named last changes fastest.
Arguments:
- tokens: bfloat16 [32768, 768], P(('dp', 'ctx')), may hold values from -6 to 6
- out_grad: bfloat16 [32768, 768], P(('dp', 'ctx')), may hold values from -6 to 6
- positions: int32 [32768], P(('dp', 'ctx')), may hold values from -1 to 2047, as said below
- master: float32 [55392, 128], P(('dp', 'ctx'))
- first_moment: float32 [55392, 128], P(('dp', 'ctx'))
- second_moment: float32 [55392, 128], P(('dp', 'ctx'))
- step_count: int32 [1], replicated, may hold values from 2 to 20
Outputs:
- layer_out: bfloat16 [32768, 768], P(('dp', 'ctx'))
- input_grad: float32 [32768, 768], P(('dp', 'ctx'))
- new_master: float32 [55392, 128], P(('dp', 'ctx'))
- new_first: float32 [55392, 128], P(('dp', 'ctx'))
- new_second: float32 [55392, 128], P(('dp', 'ctx'))
- weight_copy: bfloat16 [55392, 128], P(('dp', 'ctx'))
The draws below stay inside these ranges and needn't reach their ends.
Inputs may be any that keep to these rules, and one draw needn't show every extreme that they name: `positions`: rows form blocks of 4096, one per index of dp. In a block, sequences of 1024 or 2048 rows start at multiples of 1024 from the block's start, each row holding its place in its sequence (0, 1, 2, ...); a block's first row holds 0, and the rows after its last sequence hold -1.
All inputs are finite; a program needn't handle non-finite values.
Results may differ from the reference program's by a relative error of at most 0.015.
The reference program's roundings to bfloat16 on the way count: a program that leaves them out, or rounds other values in their place, can miss the bound.
Values may be sent and summed in bfloat16 or wider, within the bound.
No kernel may reach another device: no remote copies, remote signals or barrier semaphores. Data moves between devices by JAX's collectives and lax.ppermute only.
A program may use at most 448 MiB of HBM per device.

```python
import math
import jax
import jax.numpy as jnp
from jax import lax

D = 768
HEADS = 12
HEAD_DIM = 64
FF = 3072
SEQ_MIN = 1024
GROUP_TOKENS = 4096
TOKENS = 32768
WROWS = 55392


def draw_positions(key, part):
    group_count = TOKENS // GROUP_TOKENS
    unit_count = GROUP_TOKENS // SEQ_MIN
    pair_count = unit_count // 2
    key_fill, key_join, key_lead = jax.random.split(key, 3)
    filled = jax.random.randint(key_fill, (group_count,), (pair_count + 1) // 2, pair_count + 2)
    filled = filled.at[0].set(pair_count).at[1].set(pair_count + 1)
    lead_single = jax.random.randint(key_lead, (group_count,), 0, 2)
    lead_single = lead_single.at[0].set(1).at[1].set(0)
    joined = jax.random.randint(key_join, (group_count, pair_count + 1), 0, 2)
    joined = joined.at[1, 0].set(1)
    row_place = jnp.arange(GROUP_TOKENS, dtype=jnp.int32)
    unit_of = row_place // SEQ_MIN
    offset_in = row_place % SEQ_MIN
    shifted = unit_of[None, :] + lead_single[:, None]
    pair_of = shifted // 2
    later = (shifted % 2 == 1) & (unit_of[None, :] >= 1)
    join_here = jnp.take_along_axis(joined, pair_of, axis=1)
    placed = jnp.where((join_here == 1) & later, offset_in[None, :] + SEQ_MIN, offset_in[None, :] + 0 * pair_of)
    placed = jnp.where(pair_of < filled[:, None], placed, -1)
    return placed.reshape(-1).astype(jnp.int32)


def draw_master(key, part):
    key_normal, key_even = jax.random.split(key)
    normal_part = jax.random.truncated_normal(key_normal, -4.0, 4.0, (WROWS, 128), jnp.float32)
    even_part = jax.random.uniform(key_even, (WROWS, 128), jnp.float32)
    row_index = jnp.arange(WROWS, dtype=jnp.int32)[:, None]
    column = jnp.arange(128, dtype=jnp.int32)[None, :]
    square_rows = D * D // 128
    wide_rows = D * FF // 128
    matrix_rows = 4 * square_rows + 2 * wide_rows
    base_scale = D ** (-0.5)
    out_scale = base_scale * max(1.0, math.sqrt(SEQ_MIN) / 4.0)
    row_scale = jnp.where(row_index < 3 * square_rows, base_scale, jnp.where(row_index < 4 * square_rows, out_scale, jnp.where(row_index < 4 * square_rows + wide_rows, base_scale, jnp.where(row_index < matrix_rows, FF ** (-0.5), 0.02))))
    entry_at = (row_index - matrix_rows) * 128 + column
    small_part = jnp.where(entry_at < 2 * D, 1.0 + 0.3 * (even_part - 0.5), jnp.where(entry_at < 5 * D, 0.5 + even_part, 1.2 * (even_part - 0.5)))
    inside = (row_index >= matrix_rows) & (entry_at < 11 * D)
    return jnp.where(inside, small_part, normal_part * row_scale).astype(jnp.float32)


def gradient_size():
    return 0.5 * math.sqrt(0.75 * TOKENS)


def draw_first_moment(key, part):
    key_sign, key_size = jax.random.split(key)
    signs = jax.random.randint(key_sign, (WROWS, 128), 0, 2) * 2 - 1
    magnitude = jax.random.uniform(key_size, (WROWS, 128), jnp.float32, 0.5, 1.5)
    return (signs.astype(jnp.float32) * magnitude * (gradient_size() / 9.0)).astype(jnp.float32)


def draw_second_moment(key, part):
    factor = jnp.exp(jax.random.uniform(key, (WROWS, 128), jnp.float32, 0.0, math.log(4.0)))
    return (factor * (gradient_size() ** 2 * 0.001 / 0.999)).astype(jnp.float32)


def block_levels(stream_key, extent, shards, smallest, high):
    factor_of = 1.0
    for dim, parts in shards:
        steps = jax.random.uniform(jax.random.fold_in(jax.random.fold_in(stream_key, 6), dim), (parts,), jnp.float32, smallest / len(shards), high / len(shards))
        factor_of = factor_of * jnp.repeat(jnp.exp(steps), extent[dim] // parts).reshape((-1,) + (1,) * (len(extent) - 1 - dim))
    return factor_of


def centred(own_key, shape, scale, bound, cuts=(), held_as=jnp.bfloat16):
    factor_of = block_levels(own_key, shape, cuts, -0.22, 0.18) if cuts else 1.0
    values = jax.random.normal(own_key, shape, jnp.float32) * scale * factor_of
    return jnp.minimum(jnp.maximum(values, -bound), bound).astype(held_as)


def setup_inputs(seed: int = 0) -> dict:
    key_of = jax.random.split(jax.random.key(seed), 8)
    tokens = centred(key_of[0], (TOKENS, D), 1.0, 6.0, ((0, 32),))
    out_grad = centred(key_of[1], (TOKENS, D), 1.0, 6.0, ((0, 32),))
    positions = draw_positions(jax.random.fold_in(key_of[7], 71), 0)
    master = draw_master(jax.random.fold_in(key_of[7], 71), 0)
    first_moment = draw_first_moment(jax.random.fold_in(key_of[7], 71), 0)
    second_moment = draw_second_moment(jax.random.fold_in(key_of[7], 71), 0)
    step_count = jax.random.randint(key_of[6], (1,), 2, 21).astype(jnp.int32)
    return dict(tokens=tokens, out_grad=out_grad, positions=positions, master=master, first_moment=first_moment, second_moment=second_moment, step_count=step_count)


@jax.custom_vjp
def low(v):
    return lax.optimization_barrier(v.astype(jnp.bfloat16)).astype(jnp.float32)

@jax.custom_vjp
def low_back(v):
    return v

def low_keep(v):
    return (low(v), None)

def low_pass(kept, grad):
    return (grad,)

def back_keep(v):
    return (v, None)

def back_low(kept, grad):
    return (low(grad),)
low.defvjp(low_keep, low_pass)
low_back.defvjp(back_keep, back_low)

def product(left, right):
    return jnp.dot(left, right, preferred_element_type=jnp.float32, precision=lax.Precision.HIGHEST)

def unpack(wflat):
    values = wflat.reshape(-1)
    square_size = D * D
    wide_size = D * FF
    in_weight = jnp.concatenate([values[0:square_size].reshape(D, D), values[square_size:2 * square_size].reshape(D, D), values[2 * square_size:3 * square_size].reshape(D, D)], 1)
    out_weight = values[3 * square_size:4 * square_size].reshape(D, D)
    up_weight = values[4 * square_size:4 * square_size + wide_size].reshape(D, FF)
    down_weight = values[4 * square_size + wide_size:4 * square_size + 2 * wide_size].reshape(FF, D)
    small_start = 4 * square_size + 2 * wide_size
    gain_first = values[small_start:small_start + D]
    gain_second = values[small_start + D:small_start + 2 * D]
    conv_taps = values[small_start + 2 * D:small_start + 11 * D].reshape(3, 3 * D)
    return (in_weight, out_weight, up_weight, down_weight, gain_first, gain_second, conv_taps)

def rms_norm(values, gain):
    return values * lax.rsqrt(lax.optimization_barrier(jnp.mean(values * values, axis=-1, keepdims=True)) + 1e-06) * gain

def attend(mixed_full, positions):
    row_total = mixed_full.shape[0]
    query_heads = mixed_full[:, :D].reshape(row_total, HEADS, HEAD_DIM)
    key_heads = mixed_full[:, D:2 * D].reshape(row_total, HEADS, HEAD_DIM)
    value_heads = mixed_full[:, 2 * D:].reshape(row_total, HEADS, HEAD_DIM)
    span_rows = min(512, row_total)
    row_index = jnp.arange(row_total, dtype=jnp.int32)
    lowest = row_index - jnp.maximum(positions, 0)

    def one_span(span_at):
        start_row = (span_at * span_rows).astype(jnp.int32)
        query_part = lax.dynamic_slice_in_dim(query_heads, start_row, span_rows, 0)
        query_rows = lax.dynamic_slice_in_dim(row_index, start_row, span_rows, 0)
        lowest_part = lax.dynamic_slice_in_dim(lowest, start_row, span_rows, 0)
        scores = jnp.einsum('qhd,khd->hqk', query_part, key_heads, precision=lax.Precision.HIGHEST) * 0.125
        allowed = (row_index[None, :] <= query_rows[:, None]) & (row_index[None, :] >= lowest_part[:, None])
        scores = low_back(jnp.where(allowed[None], scores, -1e+30))
        peak_score = lax.optimization_barrier(jnp.max(scores, axis=-1, keepdims=True))
        raised = jnp.exp(scores - peak_score)
        probs = raised / lax.optimization_barrier(jnp.sum(raised, axis=-1, keepdims=True))
        outputs = jnp.einsum('hqk,khd->qhd', low(probs), value_heads, precision=lax.Precision.HIGHEST)
        return outputs.reshape(span_rows, D)
    spans = lax.map(jax.checkpoint(one_span), jnp.arange(row_total // span_rows, dtype=jnp.int32))
    return spans.reshape(row_total, D)

def block_forward(inputs, wflat, positions):
    in_weight, out_weight, up_weight, down_weight, gain_first, gain_second, conv_taps = unpack(wflat)
    normed_one = low(rms_norm(inputs, gain_first))
    projected = low(low_back(product(normed_one, in_weight)))
    after_one = (positions >= 1).astype(jnp.float32)[:, None]
    after_two = (positions >= 2).astype(jnp.float32)[:, None]
    triple_width = 3 * D
    shift_one = jnp.concatenate([jnp.zeros((1, triple_width), jnp.float32), projected[:-1]], 0)
    shift_two = jnp.concatenate([jnp.zeros((2, triple_width), jnp.float32), projected[:-2]], 0)
    mixed_full = low(conv_taps[0] * projected + after_one * conv_taps[1] * shift_one + after_two * conv_taps[2] * shift_two)
    attended = low(low_back(attend(mixed_full, positions)))
    hidden = inputs + low_back(product(attended, out_weight))
    normed_two = low(rms_norm(hidden, gain_second))
    before = low_back(product(normed_two, up_weight))
    active = jnp.maximum(before, 0.0)
    squared = low(active * active)
    return hidden + product(squared, down_weight)

def adam_update(master, moment_one, moment_two, gradient, step_count, row_start):
    row_index = row_start + jnp.arange(master.shape[0], dtype=jnp.int32)
    matrix_rows = (4 * D * D + 2 * D * FF) // 128
    out_first = 3 * D * D // 128
    out_last = 4 * D * D // 128
    is_matrix = (row_index < matrix_rows)[:, None]
    is_out = ((row_index >= out_first) & (row_index < out_last))[:, None]
    step_rate = jnp.where(is_matrix, jnp.where(is_out, 0.5, 0.1), 1.0)
    decay_rate = jnp.where(is_matrix, 0.1, 0.0)
    step_value = step_count[0].astype(jnp.float32)
    new_one = 0.9 * moment_one + 0.1 * gradient
    new_two = 0.999 * moment_two + 0.001 * gradient * gradient
    corr_first = 1.0 - jnp.power(0.9, step_value)
    corr_second = 1.0 - jnp.power(0.999, step_value)
    new_weights = master - step_rate * (new_one / corr_first / (jnp.sqrt(new_two / corr_second) + 1e-08) + decay_rate * master)
    return (new_weights, new_one, new_two)

def reference(tokens, out_grad, positions, master, first_moment, second_moment, step_count):
    wflat = master.astype(jnp.bfloat16).astype(jnp.float32)
    group_count = TOKENS // GROUP_TOKENS
    inputs = tokens.astype(jnp.float32).reshape(group_count, GROUP_TOKENS, D)
    cotangent = out_grad.astype(jnp.float32).reshape(group_count, GROUP_TOKENS, D)
    places = positions.reshape(group_count, GROUP_TOKENS)

    def one_group(carry, item):
        group_in, group_cot, group_pos = item
        outputs, pullback = jax.vjp(lambda values_in, weights_in: block_forward(values_in, weights_in, group_pos), group_in, wflat)
        keep_rows = (group_pos >= 0).astype(jnp.float32)[:, None]
        grad_in, grad_weights = pullback(group_cot * keep_rows)
        return (carry + grad_weights, (outputs.astype(jnp.bfloat16), grad_in))
    total_grad, (layer_out, input_grad) = lax.scan(one_group, jnp.zeros_like(wflat), (inputs, cotangent, places))
    new_weights, new_one, new_two = adam_update(master, first_moment, second_moment, total_grad, step_count, 0)
    return (layer_out.reshape(TOKENS, D), input_grad.reshape(TOKENS, D), new_weights, new_one, new_two, new_weights.astype(jnp.bfloat16))
```

```python
import jax
import jax.numpy as jnp
from jax import lax
from jax.experimental import pallas as pl
from jax.experimental.pallas import tpu as pltpu
from jax.sharding import PartitionSpec as P

D = 768
HEADS = 12
HEAD_DIM = 64
FF = 3072
SEQ_MIN = 1024
AXES = ("dp", "ctx")
QB = 256
F32 = jnp.float32
BF = jnp.bfloat16
NT = (((1,), (1,)), ((), ()))
TN = (((0,), (0,)), ((), ()))
norm_eps = 1e-06
VMEM_LIMIT = 56 << 20


def dot(left, right):
    return jnp.dot(left, right, preferred_element_type=F32)


def dot_nt(left, right):
    return lax.dot_general(left, right, NT, preferred_element_type=F32)


def dot_tn(left, right):
    return lax.dot_general(left, right, TN, preferred_element_type=F32)


def cost(flops, nbytes, exps=0):
    return pl.CostEstimate(flops=int(flops), bytes_accessed=int(nbytes), transcendentals=int(exps))


def conv(x, taps, mask_one, mask_two):
    one = pltpu.roll(x, 1, 0) * mask_one
    two = pltpu.roll(x, 2, 0) * mask_two
    return (taps[0:1] * x + taps[1:2] * one + taps[2:3] * two).astype(BF)


def att_fwd_kernel(
    state_ref, tail_ref, q_ref, k_ref, v_ref, tq_ref, tk_ref, tv_ref, one_ref, two_ref,
    o_ref, l_ref, qm_ref, km_ref, vm_ref,
):
    rows = q_ref.shape[0]
    lane = lax.broadcasted_iota(jnp.int32, (1, 128), 1)
    state = state_ref[0]
    second = state == 2
    empty = state == 0
    one = one_ref[...]
    two = two_ref[...]
    x = jnp.concatenate([tail_ref[...].astype(F32), q_ref[...].astype(F32)], 0)
    qm_ref[...] = conv(x, tq_ref[...], one[rows - 8 :], two[rows - 8 :])[8:]
    km_ref[...] = conv(k_ref[...].astype(F32), tk_ref[...], one, two)
    vm_ref[...] = conv(v_ref[...].astype(F32), tv_ref[...], one, two)
    for i in range(rows // QB):
        rs = pl.ds(i * QB, QB)
        outs = []
        sums = []
        qf = qm_ref[rs, :].astype(F32) * 0.125
        for h in range(2):
            mine = (lane < 64) if h == 0 else (lane >= 64)
            qh = jnp.where(mine, qf, 0.0).astype(BF)
            nk = (i + 1) * QB
            vh = jnp.where(mine, vm_ref[rows : rows + nk, :], jnp.ones((), BF))
            s = dot_nt(qh, km_ref[rows : rows + nk, :])
            r = lax.broadcasted_iota(jnp.int32, (QB, QB), 0)
            c = lax.broadcasted_iota(jnp.int32, (QB, QB), 1)
            sd = jnp.where(c <= r, s[:, i * QB :], -1e30)
            m = jnp.max(sd, axis=1, keepdims=True)
            if i > 0:
                m = jnp.maximum(m, jnp.max(s[:, : i * QB], axis=1, keepdims=True))
            o = dot(jnp.exp(sd - m).astype(BF), vh[i * QB :])
            if i > 0:
                o = o + dot(jnp.exp(s[:, : i * QB] - m).astype(BF), vh[: i * QB])

            def prev(args):
                o1, m1 = args
                s2 = dot_nt(qh, km_ref[0:rows, :])
                m2 = jnp.maximum(m1, jnp.max(s2, axis=1, keepdims=True))
                p2 = jnp.exp(s2 - m2).astype(BF)
                vph = jnp.where(mine, vm_ref[0:rows, :], jnp.ones((), BF))
                return o1 * jnp.exp(m1 - m2) + dot(p2, vph), m2

            o, m = lax.cond(second, prev, lambda a: a, (o, m))
            outs.append(o / pltpu.roll(o, 64, 1))
            sums.append(m + jnp.log(o))
        res = jnp.where(lane < 64, outs[0], outs[1])
        res = jnp.where(empty, vm_ref[pl.ds(rows + i * QB, QB), :].astype(F32), res)
        o_ref[rs, :] = res.astype(BF)
        l_ref[rs, :] = jnp.where(lane < 64, sums[1], sums[0])


def att_fwd(state, projected, taps, one, two, rows):
    def cols(height, row, off):
        return pl.BlockSpec((height, 128), lambda p: (row, p + off))

    full = pl.BlockSpec((2 * rows, 128), lambda p: (0, 0))
    taps_at = [pl.BlockSpec((3, 128), lambda p, off=off: (0, p + off)) for off in (0, 6, 12)]
    return pl.pallas_call(
        att_fwd_kernel,
        grid=(6,),
        in_specs=[
            pl.BlockSpec(memory_space=pltpu.SMEM),
            cols(8, rows // 8 - 1, 0),
            cols(rows, 1, 0),
            cols(2 * rows, 0, 6),
            cols(2 * rows, 0, 12),
            *taps_at,
            full,
            full,
        ],
        out_specs=[cols(rows, 0, 0)] * 3 + [cols(2 * rows, 0, 0)] * 2,
        out_shape=[
            jax.ShapeDtypeStruct((rows, D), BF),
            jax.ShapeDtypeStruct((rows, D), F32),
            jax.ShapeDtypeStruct((rows, D), BF),
            jax.ShapeDtypeStruct((2 * rows, D), BF),
            jax.ShapeDtypeStruct((2 * rows, D), BF),
        ],
        compiler_params=pltpu.CompilerParams(vmem_limit_bytes=VMEM_LIMIT),
        cost_estimate=cost(2 * 2 * 12 * rows * rows * 1.5 * 256, rows * D * 30, 12 * rows * rows * 1.5),
        name="att_fwd",
    )(state, projected, projected, projected, projected, taps, taps, taps, one, two)


def three(x, lane, base):
    hi = x.astype(BF).astype(F32)
    r = x - hi
    mid = r.astype(BF).astype(F32)
    lo = r - mid
    return jnp.where(
        lane == base, hi, jnp.where(lane == base + 1, mid, jnp.where(lane == base + 2, lo, 0.0))
    )


def conv_back(grad, x, taps, mask_one, mask_two):
    height = grad.shape[0]
    one = pltpu.roll(grad, height - 1, 0) * mask_one
    two = pltpu.roll(grad, height - 2, 0) * mask_two
    back = (taps[0:1] * grad + taps[1:2] * one + taps[2:3] * two).astype(BF)
    sums = [jnp.sum(g * x, axis=0, keepdims=True) for g in (grad, one, two)]
    return back, sums


def att_bwd_kernel(
    state_ref, q_ref, k_ref, v_ref, o_ref, l_ref, do_ref, xt_ref, xq_ref, xk_ref, xv_ref,
    tq_ref, tk_ref, tv_ref, one_ref, two_ref,
    pq_ref, pt_ref, pk_ref, pv_ref, tg_ref, qa, da, dqs, dks, dvs,
):
    rows = q_ref.shape[0]
    lane = lax.broadcasted_iota(jnp.int32, (1, 128), 1)
    second = state_ref[0] == 2
    do = do_ref[...].astype(F32)
    od = do * o_ref[...].astype(F32)
    qf = q_ref[...].astype(F32) * 0.125
    lv = l_ref[...]
    zero = jnp.zeros((), BF)
    dks[...] = jnp.zeros(dks.shape, F32)
    dvs[...] = jnp.zeros(dvs.shape, F32)
    dqs[...] = jnp.zeros(dqs.shape, F32)
    for h in range(2):
        mine = (lane < 64) if h == 0 else (lane >= 64)
        base = 64 if h == 0 else 0
        ones3 = ((lane >= base) & (lane < base + 3)).astype(BF)
        delta = jnp.sum(jnp.where(mine, od, 0.0), axis=1, keepdims=True)
        qa[...] = jnp.where(mine, qf, three(-lv, lane, base)).astype(BF)
        da[...] = jnp.where(mine, do, three(-delta, lane, base)).astype(BF)

        def part(ks, qs, dos, mask):
            kk = k_ref[ks, :]
            st = dot_nt(jnp.where(mine, kk, ones3), qs)
            dp = dot_nt(jnp.where(mine, v_ref[ks, :], ones3), dos)
            p = jnp.exp(st)
            if mask is not None:
                p = jnp.where(mask, p, 0.0)
            ds = (p * dp).astype(BF)
            dvs[ks, :] += dot(p.astype(BF), jnp.where(mine, dos, zero))
            dks[ks, :] += dot(ds, jnp.where(mine, qs, zero))
            return dot_tn(ds, jnp.where(mine, kk, zero))

        for i in range(rows // QB):
            qs = qa[pl.ds(i * QB, QB), :]
            dos = da[pl.ds(i * QB, QB), :]
            kr = lax.broadcasted_iota(jnp.int32, (QB, QB), 0)
            qr = lax.broadcasted_iota(jnp.int32, (QB, QB), 1)
            dq = part(pl.ds(rows + i * QB, QB), qs, dos, kr <= qr)
            if i > 0:
                dq = dq + part(pl.ds(rows, i * QB), qs, dos, None)
            dqs[pl.ds(8 + i * QB, QB), :] += dq * 0.125

        @pl.when(second)
        def _():
            for i in range(rows // QB):
                rs = pl.ds(i * QB, QB)
                dq = part(pl.ds(0, rows), qa[rs, :], da[rs, :], None)
                dqs[pl.ds(8 + i * QB, QB), :] += dq * 0.125

    one = one_ref[...]
    two = two_ref[...]
    xq = jnp.concatenate([xt_ref[...].astype(F32), xq_ref[...].astype(F32)], 0)
    pq, sq = conv_back(dqs[...], xq, tq_ref[...], one[rows - 8 :], two[rows - 8 :])
    pt_ref[...] = pq[:8]
    pq_ref[...] = pq[8:]
    pk_ref[...], sk = conv_back(dks[...], xk_ref[...].astype(F32), tk_ref[...], one, two)
    pv_ref[...], sv = conv_back(dvs[...], xv_ref[...].astype(F32), tv_ref[...], one, two)
    tg_ref[...] = jnp.zeros(tg_ref.shape, F32)
    for j in range(3):
        for m, s in enumerate((sq, sk, sv)):
            tg_ref[3 * j + m : 3 * j + m + 1, :] = s[j]


def att_bwd(state, mixed, attended, logs, grad, projected, taps, one, two, rows):
    def cols(height, row, off):
        return pl.BlockSpec((height, 128), lambda p: (row, p + off))

    full = pl.BlockSpec((2 * rows, 128), lambda p: (0, 0))
    taps_at = [pl.BlockSpec((3, 128), lambda p, off=off: (0, p + off)) for off in (0, 6, 12)]
    own = cols(rows, 0, 0)
    both = cols(2 * rows, 0, 0)
    return pl.pallas_call(
        att_bwd_kernel,
        grid=(6,),
        in_specs=[
            pl.BlockSpec(memory_space=pltpu.SMEM),
            own, both, both, own, own, own,
            cols(8, rows // 8 - 1, 0),
            cols(rows, 1, 0),
            cols(2 * rows, 0, 6),
            cols(2 * rows, 0, 12),
            *taps_at,
            full,
            full,
        ],
        out_specs=[own, cols(8, 0, 0), both, both, cols(16, 0, 0)],
        out_shape=[
            jax.ShapeDtypeStruct((rows, D), BF),
            jax.ShapeDtypeStruct((8, D), BF),
            jax.ShapeDtypeStruct((2 * rows, D), BF),
            jax.ShapeDtypeStruct((2 * rows, D), BF),
            jax.ShapeDtypeStruct((16, D), F32),
        ],
        scratch_shapes=[
            pltpu.VMEM((rows, 128), BF),
            pltpu.VMEM((rows, 128), BF),
            pltpu.VMEM((rows + 8, 128), F32),
            pltpu.VMEM((2 * rows, 128), F32),
            pltpu.VMEM((2 * rows, 128), F32),
        ],
        compiler_params=pltpu.CompilerParams(vmem_limit_bytes=VMEM_LIMIT),
        cost_estimate=cost(5 * 2 * 12 * rows * rows * 1.5 * 256, rows * D * 40, 12 * rows * rows * 1.5),
        name="att_bwd",
    )(state, *mixed, attended, logs, grad, projected, projected, projected, projected,
      taps, taps, taps, one, two)


def qkv_bwd_kernel(
    core_ref, x_ref, dq_ref, dt_ref, dk_ref, dv_ref, w_ref, gain_ref, gain_two_ref, tg_ref,
    *refs, pieces, blocks,
):
    if pieces:
        send_ref, keep_ref, prev_ref, own_ref, acc, gacc = refs
    else:
        keep_ref, small_ref, prev_ref, own_ref, acc, gacc = refs
    i = pl.program_id(0)
    half = blocks // 2

    @pl.when(i == 0)
    def _():
        acc[...] = jnp.zeros(acc.shape, F32)
        gacc[...] = jnp.zeros(gacc.shape, F32)

    x = x_ref[...].astype(F32)
    hat = x * lax.rsqrt(jnp.mean(x * x, axis=-1, keepdims=True) + norm_eps)
    low = (hat * gain_ref[...]).astype(BF)
    dk = dk_ref[...]
    dv = dv_ref[...]
    gn = dot_nt(dk, w_ref[D : 2 * D, :]) + dot_nt(dv, w_ref[2 * D : 3 * D, :])
    acc[D : 2 * D, :] += dot_tn(low, dk)
    acc[2 * D : 3 * D, :] += dot_tn(low, dv)

    @pl.when(i < half - 1)
    def _():
        prev_ref[...] = gn.astype(BF)
        gacc[0:1, :] += jnp.sum(gn * hat, axis=0, keepdims=True)

    @pl.when(i == half - 1)
    def _():
        dt = dt_ref[...]
        last = gn.shape[0] - 8
        acc[0:D, :] += dot_tn(low[last:], dt)
        full = jnp.concatenate([gn[:last], gn[last:] + dot_nt(dt, w_ref[0:D, :])], 0)
        prev_ref[...] = full.astype(BF)
        gacc[0:1, :] += jnp.sum(full * hat, axis=0, keepdims=True)

    @pl.when(i >= half)
    def _():
        dq = dq_ref[...]
        acc[0:D, :] += dot_tn(low, dq)
        full = gn + dot_nt(dq, w_ref[0:D, :])
        own_ref[...] = full
        gacc[0:1, :] += jnp.sum(full * hat, axis=0, keepdims=True)

    @pl.when(i == blocks - 1)
    def _():
        small = jnp.concatenate(
            [gacc[0:1, :], gain_two_ref[...], tg_ref[0:9, :], jnp.zeros((5, D), F32)], 0
        )
        if pieces:
            core = core_ref[0]
            height = 3 * D // (2 * pieces)
            for j in range(pieces):
                to = pl.ds(j * height, height)
                away = pl.ds(pl.multiple_of((2 * j + 1 - core) * height, 16), height)
                here = pl.ds(pl.multiple_of((2 * j + core) * height, 16), height)
                send_ref[to, :] = acc[away, :].astype(BF)
                keep_ref[to, :] = acc[here, :]
            send_ref[pieces * height :, :] = small.astype(BF)
            keep_ref[pieces * height :, :] = small
        else:
            keep_ref[...] = acc[...].astype(BF)
            small_ref[...] = small


def qkv_bwd(core, x_both, back, wide, gain, gain_two_grad, tap_grads, rows, pieces):
    dq, dt, dk, dv = back
    blocks = 4
    half = blocks // 2
    height = 2 * rows // blocks
    step = pl.BlockSpec((height, D), lambda i: (i, 0))
    late = pl.BlockSpec((height, D), lambda i: (jnp.maximum(i - half, 0), 0))
    early = pl.BlockSpec((height, D), lambda i: (jnp.minimum(i, half - 1), 0))

    def whole(shape):
        return pl.BlockSpec(shape, lambda i: (0, 0))

    if pieces:
        packed = 3 * D // 2 + 16
        outs = [jax.ShapeDtypeStruct((packed, D), BF), jax.ShapeDtypeStruct((packed, D), F32)]
        out_at = [whole((packed, D))] * 2
    else:
        outs = [jax.ShapeDtypeStruct((3 * D, D), BF), jax.ShapeDtypeStruct((16, D), F32)]
        out_at = [whole((3 * D, D)), whole((16, D))]

    def body(*refs):
        qkv_bwd_kernel(*refs, pieces=pieces, blocks=blocks)

    return pl.pallas_call(
        body,
        grid=(blocks,),
        in_specs=[
            pl.BlockSpec(memory_space=pltpu.SMEM),
            step, late, whole((8, D)), step, step, whole((3 * D, D)),
            whole((1, D)), whole((1, D)), whole((16, D)),
        ],
        out_specs=out_at + [early, late],
        out_shape=outs
        + [jax.ShapeDtypeStruct((rows, D), BF), jax.ShapeDtypeStruct((rows, D), F32)],
        scratch_shapes=[pltpu.VMEM((3 * D, D), F32), pltpu.VMEM((8, D), F32)],
        compiler_params=pltpu.CompilerParams(vmem_limit_bytes=VMEM_LIMIT),
        cost_estimate=cost(2 * 2 * D * D * 5 * rows, rows * D * 30),
        name="qkv_bwd",
    )(core, x_both, dq, dt, dk, dv, wide, gain, gain_two_grad, tap_grads)


def merge(index, keep, got, height, taken):
    rows = keep.shape[0]
    out_rows = taken * height + 16 if taken else rows

    def body(index_ref, keep_ref, got_ref, send_ref, stay_ref):
        if not taken:
            total = keep_ref[...] + got_ref[...].astype(F32)
            send_ref[...] = total.astype(BF)
            stay_ref[...] = total
            return
        for j in range(taken):
            to = pl.ds(j * height, height)
            away = pl.ds(pl.multiple_of(index_ref[j] * height, 16), height)
            here = pl.ds(pl.multiple_of(index_ref[taken + j] * height, 16), height)
            send_ref[to, :] = (keep_ref[away, :] + got_ref[away, :].astype(F32)).astype(BF)
            stay_ref[to, :] = keep_ref[here, :] + got_ref[here, :].astype(F32)
        end = keep_ref[rows - 16 :, :] + got_ref[rows - 16 :, :].astype(F32)
        send_ref[taken * height :, :] = end.astype(BF)
        stay_ref[taken * height :, :] = end

    vmem = pl.BlockSpec(memory_space=pltpu.VMEM)
    return pl.pallas_call(
        body,
        in_specs=[pl.BlockSpec(memory_space=pltpu.SMEM), vmem, vmem],
        out_specs=[vmem, vmem],
        out_shape=[
            jax.ShapeDtypeStruct((out_rows, D), BF),
            jax.ShapeDtypeStruct((out_rows, D), F32),
        ],
        compiler_params=pltpu.CompilerParams(vmem_limit_bytes=32 << 20),
        cost_estimate=cost(rows * D, rows * D * 12),
        name="merge",
    )(index, keep, got)


def shift_flat(block, distance):
    count = lax.axis_size(AXES)
    route = [(i - distance, i) for i in range(count) if 0 <= i - distance < count]
    return lax.ppermute(block, AXES, route)


def shift_ctx(block, distance):
    count = lax.axis_size("ctx")
    route = [(i - distance, i) for i in range(count) if 0 <= i - distance < count]
    return lax.ppermute(block, "ctx", route)


def swap(block, even_bit, odd_bit):
    count = lax.axis_size(AXES)
    route = [(i, i ^ (odd_bit if i & 1 else even_bit)) for i in range(count)]
    return lax.ppermute(block, AXES, route)


def to_aligned(shard, place, count, delta):
    rows = shard.shape[0]
    lag = delta * (count - 1)
    back = -(-lag // rows)
    if back == 1:
        keep = -(-lag // 8) * 8
        parts = [shift_flat(shard[rows - keep :], 1), shard]
    else:
        keep = back * rows
        parts = [shift_flat(shard, s) for s in range(back, 0, -1)] + [shard]
    joined = jnp.concatenate(parts, 0)
    return lax.dynamic_slice_in_dim(joined, keep - delta * place, rows - delta, 0)


def small_part(shard, place, count, delta):
    rows = shard.shape[0]
    extra = count * delta
    zeros = jnp.zeros((extra, 128), shard.dtype)
    joined = jnp.concatenate([zeros, shard, zeros], 0)
    start = extra + count * (rows - delta) - place * rows
    return lax.dynamic_slice_in_dim(joined, jnp.minimum(start, rows + extra), extra, 0)


def from_aligned(chunk, small, place, count, delta, rows):
    aligned = rows - delta
    ahead = -(-(count * delta) // aligned)
    parts = [chunk]
    if ahead == 1:
        keep = small.shape[0]
        got = shift_flat(chunk[:keep], -1)
        parts.append(jnp.where(place == count - 1, small, got))
    else:
        pad = ahead * aligned - small.shape[0]
        tail = jnp.concatenate([small, jnp.zeros((pad, 128), small.dtype)], 0)
        for s in range(1, ahead + 1):
            got = shift_flat(chunk, -s)
            for e in range(s):
                piece = tail[e * aligned : (e + 1) * aligned]
                got = jnp.where(place == count - s + e, piece, got)
            parts.append(got)
    return lax.dynamic_slice_in_dim(jnp.concatenate(parts, 0), delta * place, rows, 0)


def normalize(values, gain):
    factor = lax.rsqrt(jnp.mean(values * values, axis=-1, keepdims=True) + norm_eps)
    scaled = values * factor
    return (scaled, factor, scaled * gain)


def norm_back(grad_in, scaled, factor, gain):
    weighted = grad_in * gain
    inner_mean = jnp.mean(weighted * scaled, axis=-1, keepdims=True)
    return factor * (weighted - scaled * inner_mean)


def adam_update(master, moment_one, moment_two, gradient, step_count, row_start):
    row_index = row_start + jnp.arange(master.shape[0], dtype=jnp.int32)
    matrix_rows = (4 * D * D + 2 * D * FF) // 128
    out_first = 3 * D * D // 128
    out_last = 4 * D * D // 128
    is_matrix = (row_index < matrix_rows)[:, None]
    is_out = ((row_index >= out_first) & (row_index < out_last))[:, None]
    step_rate = jnp.where(is_matrix, jnp.where(is_out, 0.5, 0.1), 1.0)
    decay_rate = jnp.where(is_matrix, 0.1, 0.0)
    step_value = step_count[0].astype(jnp.float32)
    new_one = 0.9 * moment_one + 0.1 * gradient
    new_two = 0.999 * moment_two + 0.001 * gradient * gradient
    corr_first = 1.0 - jnp.power(0.9, step_value)
    corr_second = 1.0 - jnp.power(0.999, step_value)
    new_weights = master - step_rate * (
        new_one / corr_first / (jnp.sqrt(new_two / corr_second) + 1e-08) + decay_rate * master
    )
    return (new_weights, new_one, new_two)


def shards(tokens, out_grad, positions, master, first_moment, second_moment, step_count):
    rows = tokens.shape[0]
    assert rows == SEQ_MIN
    count = lax.axis_size(AXES)
    place = lax.axis_index(AXES).astype(jnp.int32)
    owned = master.shape[0]
    aligned = (4 * D * D + 2 * D * FF) // 128 // count
    delta = owned - aligned
    height = aligned * 128 // D
    staged = count == 32
    first_place = positions[0]
    state = jnp.where(first_place < 0, 0, jnp.where(first_place >= SEQ_MIN, 2, 1)).astype(jnp.int32)
    state_vec = state[None]

    tokens_before = shift_ctx(tokens, 1)
    chunk = to_aligned(master, place, count, delta).reshape(-1, D).astype(BF)
    wide = lax.all_gather(chunk, AXES, axis=0, tiled=True)
    small = lax.psum(lax.reduce_precision(small_part(master, place, count, delta), 8, 7), AXES)
    small = small.reshape(-1)
    gain_first = small[:D]
    gain_second = small[D : 2 * D]
    taps = small[2 * D : 11 * D].reshape(3, 3 * D)
    in_weight = jnp.concatenate([wide[:D], wide[D : 2 * D], wide[2 * D : 3 * D]], 1)
    out_weight = wide[3 * D : 4 * D]
    up_weight = wide[4 * D : 8 * D].reshape(D, FF)
    down_weight = wide[8 * D : 12 * D]

    tokens_both = jnp.concatenate([tokens_before, tokens], 0)
    inputs_both = tokens_both.astype(F32)
    normed_low = normalize(inputs_both, gain_first)[2].astype(BF)
    projected = dot(normed_low, in_weight).astype(BF)

    def masks(row_id):
        own_one = (state == 2) | ((state == 1) & (row_id > rows))
        own_two = (state == 2) | ((state == 1) & (row_id > rows + 1))
        one = jnp.where(row_id < rows, row_id >= 1, own_one) & (row_id < 2 * rows)
        two = jnp.where(row_id < rows, row_id >= 2, own_two) & (row_id < 2 * rows)
        return one.astype(F32), two.astype(F32)

    row_id = lax.broadcasted_iota(jnp.int32, (2 * rows, 128), 0)
    after_one, after_two = masks(row_id)
    ahead_one = masks(row_id + 1)[0]
    ahead_two = masks(row_id + 2)[1]
    attn_low, logs, *mixed = att_fwd(state_vec, projected, taps, after_one, after_two, rows)

    inputs = tokens.astype(F32)
    hidden = inputs + dot(attn_low, out_weight)
    scaled_two, factor_two, normed_two = normalize(hidden, gain_second)
    second_low = normed_two.astype(BF)
    active = jnp.maximum(dot(second_low, up_weight), 0.0)
    squared_low = (active * active).astype(BF)
    layer_out = (hidden + dot(squared_low, down_weight)).astype(BF)

    grad_low = jnp.where(state > 0, out_grad, jnp.zeros((), BF))
    grad_out = grad_low.astype(F32)
    grad_down = dot_tn(squared_low, grad_low)
    grad_before = (dot_nt(grad_low, down_weight) * 2.0 * active).astype(BF)
    grad_up = dot_tn(second_low, grad_before)
    grad_normed_two = dot_nt(grad_before, up_weight)
    grad_gain_two = jnp.sum(grad_normed_two * scaled_two, axis=0)
    grad_hidden = grad_out + norm_back(grad_normed_two, scaled_two, factor_two, gain_second)
    hidden_low = grad_hidden.astype(BF)
    grad_outw = dot_tn(attn_low, hidden_low)
    grad_attended = dot_nt(hidden_low, out_weight).astype(BF)

    if staged:
        late_grad = jnp.concatenate(
            [
                jnp.zeros((3 * D, D), BF),
                grad_outw.astype(BF),
                grad_up.astype(BF).reshape(-1, D),
                grad_down.astype(BF),
            ],
            0,
        )
        late_chunk = lax.psum_scatter(late_grad, AXES, scatter_dimension=0, tiled=True)

    *back, tap_grads = att_bwd(
        state_vec, mixed, attn_low, logs, grad_attended, projected, taps, ahead_one, ahead_two, rows
    )
    core = (place & 1)[None]
    sums = qkv_bwd(
        core, tokens_both, back, wide, gain_first[None], grad_gain_two[None], tap_grads, rows,
        4 if staged else 0,
    )
    grads_before, grad_normed_one = sums[2:]
    from_next = shift_ctx(grads_before, -1)
    scaled_one, factor_one, _ = normalize(inputs, gain_first)
    input_grad = grad_hidden + norm_back(
        grad_normed_one + from_next.astype(F32), scaled_one, factor_one, gain_first
    )

    if staged:
        send, keep = sums[:2]
        x_bit = (place >> 1) & 1
        y_bit = (place >> 2) & 1
        got = swap(send, 1, 1)
        even = (place & 1) == 0
        stay = [jnp.where(even, 2 * j + x_bit, 2 * y_bit + j) for j in range(2)]
        away = [jnp.where(even, 2 * j + 1 - x_bit, 2 * (1 - y_bit) + j) for j in range(2)]
        send, keep = merge(jnp.stack(away + stay), keep, got, height, 2)
        got = swap(send, 2, 4)
        other = jnp.where(even, y_bit, x_bit)
        send, keep = merge(jnp.stack([1 - other, other]), keep, got, height, 1)
        got = swap(send, 4, 2)
        send, keep = merge(core, keep, got, height, 0)
        got = swap(send, 8, 8)
        send, keep = merge(core, keep, got, height, 0)
        got = swap(send, 16, 16)
        first = keep + got.astype(F32)
        small_grad = first[height:].reshape(-1, 128)
        chunk_grad = jnp.where(place < count // 4, first[:height], late_chunk.astype(F32))
    else:
        wide_grad = jnp.concatenate(
            [
                sums[0],
                grad_outw.astype(BF),
                grad_up.astype(BF).reshape(-1, D),
                grad_down.astype(BF),
            ],
            0,
        )
        chunk_grad = lax.psum_scatter(wide_grad, AXES, scatter_dimension=0, tiled=True).astype(F32)
        used = sums[1].reshape(-1, 128)
        extra = count * delta
        small_grad = jnp.concatenate([used, jnp.zeros((extra - used.shape[0], 128), F32)], 0)
        small_grad = lax.psum(small_grad, AXES)
    gradient = from_aligned(chunk_grad.reshape(-1, 128), small_grad, place, count, delta, owned)
    new_weights, new_one, new_two = adam_update(
        master, first_moment, second_moment, gradient, step_count, place * owned
    )
    return (layer_out, input_grad, new_weights, new_one, new_two, new_weights.astype(BF))


def solution(mesh):
    spread = P(AXES, None)
    return jax.shard_map(
        shards,
        mesh=mesh,
        in_specs=(spread, spread, P(AXES), spread, spread, spread, P()),
        out_specs=(spread,) * 6,
        check_vma=False,
    )
```

```python
import jax
import jax.numpy as jnp
from jax import lax
from jax.experimental import pallas as pl
from jax.experimental.pallas import tpu as pltpu
from jax.sharding import PartitionSpec as P

D = 768
HEADS = 12
HEAD_DIM = 64
FF = 3072
SEQ_MIN = 1024
AXES = ("dp", "ctx")
QB = 256
F32 = jnp.float32
BF = jnp.bfloat16
NT = (((1,), (1,)), ((), ()))
TN = (((0,), (0,)), ((), ()))
norm_eps = 1e-06
VMEM_LIMIT = 56 << 20


def dot(left, right):
    return jnp.dot(left, right, preferred_element_type=F32)


def dot_nt(left, right):
    return lax.dot_general(left, right, NT, preferred_element_type=F32)


def dot_tn(left, right):
    return lax.dot_general(left, right, TN, preferred_element_type=F32)


def cost(flops, nbytes, exps=0):
    return pl.CostEstimate(flops=int(flops), bytes_accessed=int(nbytes), transcendentals=int(exps))


def conv(x, taps, mask_one, mask_two):
    one = pltpu.roll(x, 1, 0) * mask_one
    two = pltpu.roll(x, 2, 0) * mask_two
    return (taps[0:1] * x + taps[1:2] * one + taps[2:3] * two).astype(BF)


def att_fwd_kernel(
    state_ref, tail_ref, q_ref, k_ref, v_ref, tq_ref, tk_ref, tv_ref, one_ref, two_ref,
    o_ref, l_ref, qm_ref, km_ref, vm_ref,
):
    rows = q_ref.shape[0]
    lane = lax.broadcasted_iota(jnp.int32, (1, 128), 1)
    state = state_ref[0]
    second = state == 2
    empty = state == 0
    one = one_ref[...]
    two = two_ref[...]
    x = jnp.concatenate([tail_ref[...].astype(F32), q_ref[...].astype(F32)], 0)
    qm_ref[...] = conv(x, tq_ref[...], one[rows - 8 :], two[rows - 8 :])[8:]
    km_ref[...] = conv(k_ref[...].astype(F32), tk_ref[...], one, two)
    vm_ref[...] = conv(v_ref[...].astype(F32), tv_ref[...], one, two)
    for i in range(rows // QB):
        rs = pl.ds(i * QB, QB)
        outs = []
        sums = []
        qf = qm_ref[rs, :].astype(F32) * 0.125
        for h in range(2):
            mine = (lane < 64) if h == 0 else (lane >= 64)
            qh = jnp.where(mine, qf, 0.0).astype(BF)
            nk = (i + 1) * QB
            vh = jnp.where(mine, vm_ref[rows : rows + nk, :], jnp.ones((), BF))
            s = dot_nt(qh, km_ref[rows : rows + nk, :])
            r = lax.broadcasted_iota(jnp.int32, (QB, QB), 0)
            c = lax.broadcasted_iota(jnp.int32, (QB, QB), 1)
            sd = jnp.where(c <= r, s[:, i * QB :], -1e30)
            m = jnp.max(sd, axis=1, keepdims=True)
            if i > 0:
                m = jnp.maximum(m, jnp.max(s[:, : i * QB], axis=1, keepdims=True))
            o = dot(jnp.exp(sd - m).astype(BF), vh[i * QB :])
            if i > 0:
                o = o + dot(jnp.exp(s[:, : i * QB] - m).astype(BF), vh[: i * QB])

            def prev(args):
                o1, m1 = args
                s2 = dot_nt(qh, km_ref[0:rows, :])
                m2 = jnp.maximum(m1, jnp.max(s2, axis=1, keepdims=True))
                p2 = jnp.exp(s2 - m2).astype(BF)
                vph = jnp.where(mine, vm_ref[0:rows, :], jnp.ones((), BF))
                return o1 * jnp.exp(m1 - m2) + dot(p2, vph), m2

            o, m = lax.cond(second, prev, lambda a: a, (o, m))
            outs.append(o / pltpu.roll(o, 64, 1))
            sums.append(m + jnp.log(o))
        res = jnp.where(lane < 64, outs[0], outs[1])
        res = jnp.where(empty, vm_ref[pl.ds(rows + i * QB, QB), :].astype(F32), res)
        o_ref[rs, :] = res.astype(BF)
        l_ref[rs, :] = jnp.where(lane < 64, sums[1], sums[0])


def att_fwd(state, projected, taps, one, two, rows):
    def cols(height, row, off):
        return pl.BlockSpec((height, 128), lambda p: (row, p + off))

    full = pl.BlockSpec((2 * rows, 128), lambda p: (0, 0))
    taps_at = [pl.BlockSpec((3, 128), lambda p, off=off: (0, p + off)) for off in (0, 6, 12)]
    return pl.pallas_call(
        att_fwd_kernel,
        grid=(6,),
        in_specs=[
            pl.BlockSpec(memory_space=pltpu.SMEM),
            cols(8, rows // 8 - 1, 0),
            cols(rows, 1, 0),
            cols(2 * rows, 0, 6),
            cols(2 * rows, 0, 12),
            *taps_at,
            full,
            full,
        ],
        out_specs=[cols(rows, 0, 0)] * 3 + [cols(2 * rows, 0, 0)] * 2,
        out_shape=[
            jax.ShapeDtypeStruct((rows, D), BF),
            jax.ShapeDtypeStruct((rows, D), F32),
            jax.ShapeDtypeStruct((rows, D), BF),
            jax.ShapeDtypeStruct((2 * rows, D), BF),
            jax.ShapeDtypeStruct((2 * rows, D), BF),
        ],
        compiler_params=pltpu.CompilerParams(vmem_limit_bytes=VMEM_LIMIT),
        cost_estimate=cost(2 * 2 * 12 * rows * rows * 1.5 * 256, rows * D * 30, 12 * rows * rows * 1.5),
        name="att_fwd",
    )(state, projected, projected, projected, projected, taps, taps, taps, one, two)


def three(x, lane, base):
    hi = x.astype(BF).astype(F32)
    r = x - hi
    mid = r.astype(BF).astype(F32)
    lo = r - mid
    return jnp.where(
        lane == base, hi, jnp.where(lane == base + 1, mid, jnp.where(lane == base + 2, lo, 0.0))
    )


def conv_back(grad, x, taps, mask_one, mask_two):
    height = grad.shape[0]
    one = pltpu.roll(grad, height - 1, 0) * mask_one
    two = pltpu.roll(grad, height - 2, 0) * mask_two
    back = (taps[0:1] * grad + taps[1:2] * one + taps[2:3] * two).astype(BF)
    sums = [jnp.sum(g * x, axis=0, keepdims=True) for g in (grad, one, two)]
    return back, sums


def att_bwd_kernel(
    state_ref, q_ref, k_ref, v_ref, o_ref, l_ref, do_ref, xt_ref, xq_ref, xk_ref, xv_ref,
    tq_ref, tk_ref, tv_ref, one_ref, two_ref,
    pq_ref, pt_ref, pk_ref, pv_ref, tg_ref, qa, da, dqs, dks, dvs,
):
    rows = q_ref.shape[0]
    lane = lax.broadcasted_iota(jnp.int32, (1, 128), 1)
    second = state_ref[0] == 2
    do = do_ref[...].astype(F32)
    od = do * o_ref[...].astype(F32)
    qf = q_ref[...].astype(F32) * 0.125
    lv = l_ref[...]
    zero = jnp.zeros((), BF)
    dks[...] = jnp.zeros(dks.shape, F32)
    dvs[...] = jnp.zeros(dvs.shape, F32)
    dqs[...] = jnp.zeros(dqs.shape, F32)
    for h in range(2):
        mine = (lane < 64) if h == 0 else (lane >= 64)
        base = 64 if h == 0 else 0
        ones3 = ((lane >= base) & (lane < base + 3)).astype(BF)
        delta = jnp.sum(jnp.where(mine, od, 0.0), axis=1, keepdims=True)
        qa[...] = jnp.where(mine, qf, three(-lv, lane, base)).astype(BF)
        da[...] = jnp.where(mine, do, three(-delta, lane, base)).astype(BF)

        def part(ks, qs, dos, mask):
            kk = k_ref[ks, :]
            st = dot_nt(jnp.where(mine, kk, ones3), qs)
            dp = dot_nt(jnp.where(mine, v_ref[ks, :], ones3), dos)
            p = jnp.exp(st)
            if mask is not None:
                p = jnp.where(mask, p, 0.0)
            ds = (p * dp).astype(BF)
            dvs[ks, :] += dot(p.astype(BF), jnp.where(mine, dos, zero))
            dks[ks, :] += dot(ds, jnp.where(mine, qs, zero))
            return dot_tn(ds, jnp.where(mine, kk, zero))

        for i in range(rows // QB):
            qs = qa[pl.ds(i * QB, QB), :]
            dos = da[pl.ds(i * QB, QB), :]
            kr = lax.broadcasted_iota(jnp.int32, (QB, QB), 0)
            qr = lax.broadcasted_iota(jnp.int32, (QB, QB), 1)
            dq = part(pl.ds(rows + i * QB, QB), qs, dos, kr <= qr)
            if i > 0:
                dq = dq + part(pl.ds(rows, i * QB), qs, dos, None)
            dqs[pl.ds(8 + i * QB, QB), :] += dq * 0.125

        @pl.when(second)
        def _():
            for i in range(rows // QB):
                rs = pl.ds(i * QB, QB)
                dq = part(pl.ds(0, rows), qa[rs, :], da[rs, :], None)
                dqs[pl.ds(8 + i * QB, QB), :] += dq * 0.125

    one = one_ref[...]
    two = two_ref[...]
    xq = jnp.concatenate([xt_ref[...].astype(F32), xq_ref[...].astype(F32)], 0)
    pq, sq = conv_back(dqs[...], xq, tq_ref[...], one[rows - 8 :], two[rows - 8 :])
    pt_ref[...] = pq[:8]
    pq_ref[...] = pq[8:]
    pk_ref[...], sk = conv_back(dks[...], xk_ref[...].astype(F32), tk_ref[...], one, two)
    pv_ref[...], sv = conv_back(dvs[...], xv_ref[...].astype(F32), tv_ref[...], one, two)
    tg_ref[...] = jnp.zeros(tg_ref.shape, F32)
    for j in range(3):
        for m, s in enumerate((sq, sk, sv)):
            tg_ref[3 * j + m : 3 * j + m + 1, :] = s[j]


def att_bwd(state, mixed, attended, logs, grad, projected, taps, one, two, rows):
    def cols(height, row, off):
        return pl.BlockSpec((height, 128), lambda p: (row, p + off))

    full = pl.BlockSpec((2 * rows, 128), lambda p: (0, 0))
    taps_at = [pl.BlockSpec((3, 128), lambda p, off=off: (0, p + off)) for off in (0, 6, 12)]
    own = cols(rows, 0, 0)
    both = cols(2 * rows, 0, 0)
    return pl.pallas_call(
        att_bwd_kernel,
        grid=(6,),
        in_specs=[
            pl.BlockSpec(memory_space=pltpu.SMEM),
            own, both, both, own, own, own,
            cols(8, rows // 8 - 1, 0),
            cols(rows, 1, 0),
            cols(2 * rows, 0, 6),
            cols(2 * rows, 0, 12),
            *taps_at,
            full,
            full,
        ],
        out_specs=[own, cols(8, 0, 0), both, both, cols(16, 0, 0)],
        out_shape=[
            jax.ShapeDtypeStruct((rows, D), BF),
            jax.ShapeDtypeStruct((8, D), BF),
            jax.ShapeDtypeStruct((2 * rows, D), BF),
            jax.ShapeDtypeStruct((2 * rows, D), BF),
            jax.ShapeDtypeStruct((16, D), F32),
        ],
        scratch_shapes=[
            pltpu.VMEM((rows, 128), BF),
            pltpu.VMEM((rows, 128), BF),
            pltpu.VMEM((rows + 8, 128), F32),
            pltpu.VMEM((2 * rows, 128), F32),
            pltpu.VMEM((2 * rows, 128), F32),
        ],
        compiler_params=pltpu.CompilerParams(vmem_limit_bytes=VMEM_LIMIT),
        cost_estimate=cost(5 * 2 * 12 * rows * rows * 1.5 * 256, rows * D * 40, 12 * rows * rows * 1.5),
        name="att_bwd",
    )(state, *mixed, attended, logs, grad, projected, projected, projected, projected,
      taps, taps, taps, one, two)


def qkv_bwd_kernel(
    core_ref, x_ref, dq_ref, dt_ref, dk_ref, dv_ref, w_ref, gain_ref, gain_two_ref, tg_ref,
    *refs, pieces, blocks,
):
    if pieces:
        send_ref, keep_ref, prev_ref, own_ref, acc, gacc = refs
    else:
        keep_ref, small_ref, prev_ref, own_ref, acc, gacc = refs
    i = pl.program_id(0)
    half = blocks // 2

    @pl.when(i == 0)
    def _():
        acc[...] = jnp.zeros(acc.shape, F32)
        gacc[...] = jnp.zeros(gacc.shape, F32)

    x = x_ref[...].astype(F32)
    hat = x * lax.rsqrt(jnp.mean(x * x, axis=-1, keepdims=True) + norm_eps)
    low = (hat * gain_ref[...]).astype(BF)
    dk = dk_ref[...]
    dv = dv_ref[...]
    gn = dot_nt(dk, w_ref[D : 2 * D, :]) + dot_nt(dv, w_ref[2 * D : 3 * D, :])
    acc[D : 2 * D, :] += dot_tn(low, dk)
    acc[2 * D : 3 * D, :] += dot_tn(low, dv)

    @pl.when(i < half - 1)
    def _():
        prev_ref[...] = gn.astype(BF)
        gacc[0:1, :] += jnp.sum(gn * hat, axis=0, keepdims=True)

    @pl.when(i == half - 1)
    def _():
        dt = dt_ref[...]
        last = gn.shape[0] - 8
        acc[0:D, :] += dot_tn(low[last:], dt)
        full = jnp.concatenate([gn[:last], gn[last:] + dot_nt(dt, w_ref[0:D, :])], 0)
        prev_ref[...] = full.astype(BF)
        gacc[0:1, :] += jnp.sum(full * hat, axis=0, keepdims=True)

    @pl.when(i >= half)
    def _():
        dq = dq_ref[...]
        acc[0:D, :] += dot_tn(low, dq)
        full = gn + dot_nt(dq, w_ref[0:D, :])
        own_ref[...] = full
        gacc[0:1, :] += jnp.sum(full * hat, axis=0, keepdims=True)

    @pl.when(i == blocks - 1)
    def _():
        small = jnp.concatenate(
            [gacc[0:1, :], gain_two_ref[...], tg_ref[0:9, :], jnp.zeros((5, D), F32)], 0
        )
        if pieces:
            core = core_ref[0]
            height = 3 * D // (2 * pieces)
            for j in range(pieces):
                to = pl.ds(j * height, height)
                away = pl.ds(pl.multiple_of((2 * j + 1 - core) * height, 16), height)
                here = pl.ds(pl.multiple_of((2 * j + core) * height, 16), height)
                send_ref[to, :] = acc[away, :].astype(BF)
                keep_ref[to, :] = acc[here, :]
            send_ref[pieces * height :, :] = small.astype(BF)
            keep_ref[pieces * height :, :] = small
        else:
            keep_ref[...] = acc[...].astype(BF)
            small_ref[...] = small


def qkv_bwd(core, x_both, back, wide, gain, gain_two_grad, tap_grads, rows, pieces):
    dq, dt, dk, dv = back
    blocks = 4
    half = blocks // 2
    height = 2 * rows // blocks
    step = pl.BlockSpec((height, D), lambda i: (i, 0))
    late = pl.BlockSpec((height, D), lambda i: (jnp.maximum(i - half, 0), 0))
    early = pl.BlockSpec((height, D), lambda i: (jnp.minimum(i, half - 1), 0))

    def whole(shape):
        return pl.BlockSpec(shape, lambda i: (0, 0))

    if pieces:
        packed = 3 * D // 2 + 16
        outs = [jax.ShapeDtypeStruct((packed, D), BF), jax.ShapeDtypeStruct((packed, D), F32)]
        out_at = [whole((packed, D))] * 2
    else:
        outs = [jax.ShapeDtypeStruct((3 * D, D), BF), jax.ShapeDtypeStruct((16, D), F32)]
        out_at = [whole((3 * D, D)), whole((16, D))]

    def body(*refs):
        qkv_bwd_kernel(*refs, pieces=pieces, blocks=blocks)

    return pl.pallas_call(
        body,
        grid=(blocks,),
        in_specs=[
            pl.BlockSpec(memory_space=pltpu.SMEM),
            step, late, whole((8, D)), step, step, whole((3 * D, D)),
            whole((1, D)), whole((1, D)), whole((16, D)),
        ],
        out_specs=out_at + [early, late],
        out_shape=outs
        + [jax.ShapeDtypeStruct((rows, D), BF), jax.ShapeDtypeStruct((rows, D), F32)],
        scratch_shapes=[pltpu.VMEM((3 * D, D), F32), pltpu.VMEM((8, D), F32)],
        compiler_params=pltpu.CompilerParams(vmem_limit_bytes=VMEM_LIMIT),
        cost_estimate=cost(2 * 2 * D * D * 5 * rows, rows * D * 30),
        name="qkv_bwd",
    )(core, x_both, dq, dt, dk, dv, wide, gain, gain_two_grad, tap_grads)


def merge(index, keep, got, height, taken):
    rows = keep.shape[0]
    out_rows = taken * height + 16 if taken else rows

    def body(index_ref, keep_ref, got_ref, send_ref, stay_ref):
        if not taken:
            total = keep_ref[...] + got_ref[...].astype(F32)
            send_ref[...] = total.astype(BF)
            stay_ref[...] = total
            return
        for j in range(taken):
            to = pl.ds(j * height, height)
            away = pl.ds(pl.multiple_of(index_ref[j] * height, 16), height)
            here = pl.ds(pl.multiple_of(index_ref[taken + j] * height, 16), height)
            send_ref[to, :] = (keep_ref[away, :] + got_ref[away, :].astype(F32)).astype(BF)
            stay_ref[to, :] = keep_ref[here, :] + got_ref[here, :].astype(F32)
        end = keep_ref[rows - 16 :, :] + got_ref[rows - 16 :, :].astype(F32)
        send_ref[taken * height :, :] = end.astype(BF)
        stay_ref[taken * height :, :] = end

    vmem = pl.BlockSpec(memory_space=pltpu.VMEM)
    return pl.pallas_call(
        body,
        in_specs=[pl.BlockSpec(memory_space=pltpu.SMEM), vmem, vmem],
        out_specs=[vmem, vmem],
        out_shape=[
            jax.ShapeDtypeStruct((out_rows, D), BF),
            jax.ShapeDtypeStruct((out_rows, D), F32),
        ],
        compiler_params=pltpu.CompilerParams(vmem_limit_bytes=32 << 20),
        cost_estimate=cost(rows * D, rows * D * 12),
        name="merge",
    )(index, keep, got)


def ffn_kernel(
    state_ref, x_ref, att_ref, cot_ref, gain_ref, wo_ref, up_ref, down_ref,
    out_ref, gh_ref, ga_ref, gain_grad_ref, flat_ref,
    hidden, low, total, back, cot, sq, gb, stage_up, stage_down, stage_out, sems,
):
    c = pl.program_id(0)
    rows = x_ref.shape[0]
    blocks = [pl.ds(i * QB, QB) for i in range(rows // QB)]
    last = c == pl.num_programs(0) - 1

    def put_zero(i):
        return pltpu.make_async_copy(stage_out, flat_ref.at[pl.ds(8 * i, 8)], sems.at[8 + i])

    def put_up(i):
        return pltpu.make_async_copy(stage_up.at[i], flat_ref.at[pl.ds(32, 32), i], sems.at[i])

    def put_down(i):
        return pltpu.make_async_copy(stage_down.at[i], flat_ref.at[pl.ds(64 + 8 * i, 8)], sems.at[4 + i])

    def put_out():
        return pltpu.make_async_copy(stage_out, flat_ref.at[pl.ds(24, 8)], sems.at[11])

    @pl.when(c == 0)
    def _():
        stage_out[...] = jnp.zeros(stage_out.shape, BF)
        for i in range(3):
            put_zero(i).start()
        cot[...] = jnp.where(state_ref[0] > 0, cot_ref[...], jnp.zeros((), BF))
        total[...] = jnp.zeros(total.shape, F32)
        back[...] = jnp.zeros(back.shape, F32)
        for b in blocks:
            h = x_ref[b, :].astype(F32) + dot(att_ref[b, :], wo_ref[...])
            hidden[b, :] = h
            hat = h * lax.rsqrt(jnp.mean(h * h, axis=-1, keepdims=True) + norm_eps)
            low[b, :] = (hat * gain_ref[...]).astype(BF)

    up = up_ref[...].reshape(D, D)
    for b in blocks:
        act = jnp.maximum(dot(low[b, :], up), 0.0)
        s = (act * act).astype(BF)
        sq[b, :] = s
        total[b, :] += dot(s, down_ref[...])
        g = (dot_nt(cot[b, :], down_ref[...]) * 2.0 * act).astype(BF)
        gb[b, :] = g
        back[b, :] += dot_nt(g, up)
    stage_down[c] = dot_tn(sq[...], cot[...]).reshape(8, 4, 24, D).astype(BF)
    stage_up[c] = dot_tn(low[...], gb[...]).reshape(32, 24, D).astype(BF)
    put_down(c).start()
    put_up(c).start()

    @pl.when(last)
    def _():
        for i in range(3):
            put_zero(i).wait()
        gain = gain_ref[...]
        sums = jnp.zeros((1, D), F32)
        for b in blocks:
            h = hidden[b, :]
            out_ref[b, :] = (h + total[b, :]).astype(BF)
            factor = lax.rsqrt(jnp.mean(h * h, axis=-1, keepdims=True) + norm_eps)
            hat = h * factor
            g = back[b, :]
            sums = sums + jnp.sum(g * hat, axis=0, keepdims=True)
            weighted = g * gain
            inner = jnp.mean(weighted * hat, axis=-1, keepdims=True)
            grad = cot[b, :].astype(F32) + factor * (weighted - hat * inner)
            gh_ref[b, :] = grad
            grad_low = grad.astype(BF)
            gb[b, :] = grad_low
            ga_ref[b, :] = dot_nt(grad_low, wo_ref[...]).astype(BF)
        gain_grad_ref[...] = sums
        stage_out[...] = dot_tn(att_ref[...], gb[...]).reshape(8, 4, 24, D).astype(BF)
        put_out().start()
        for i in range(pl.num_programs(0)):
            put_down(i).wait()
            put_up(i).wait()
        put_out().wait()


def ffn(state, tokens, attended, out_grad, gain, wide, rows):
    def whole(shape):
        return pl.BlockSpec(shape, lambda c: (0,) * len(shape))

    act = whole((rows, D))
    square = wide.reshape(12 * D, D)
    return pl.pallas_call(
        ffn_kernel,
        grid=(4,),
        in_specs=[
            pl.BlockSpec(memory_space=pltpu.SMEM),
            act, act, act, whole((1, D)),
            pl.BlockSpec((D, D), lambda c: (3, 0)),
            pl.BlockSpec((32, 1, 24, D), lambda c: (1, c, 0, 0)),
            pl.BlockSpec((D, D), lambda c: (8 + c, 0)),
        ],
        out_specs=[act, act, act, whole((1, D)), pl.BlockSpec(memory_space=pl.ANY)],
        out_shape=[
            jax.ShapeDtypeStruct((rows, D), BF),
            jax.ShapeDtypeStruct((rows, D), F32),
            jax.ShapeDtypeStruct((rows, D), BF),
            jax.ShapeDtypeStruct((1, D), F32),
            jax.ShapeDtypeStruct((96, 4, 24, D), BF),
        ],
        scratch_shapes=[
            pltpu.VMEM((rows, D), F32),
            pltpu.VMEM((rows, D), BF),
            pltpu.VMEM((rows, D), F32),
            pltpu.VMEM((rows, D), F32),
            pltpu.VMEM((rows, D), BF),
            pltpu.VMEM((rows, D), BF),
            pltpu.VMEM((rows, D), BF),
            pltpu.VMEM((4, 32, 24, D), BF),
            pltpu.VMEM((4, 8, 4, 24, D), BF),
            pltpu.VMEM((8, 4, 24, D), BF),
            pltpu.SemaphoreType.DMA((12,)),
        ],
        compiler_params=pltpu.CompilerParams(vmem_limit_bytes=60 << 20),
        cost_estimate=cost(2 * rows * D * D * (24 + 3), 2 * 12 * D * D * 2 + rows * D * 16),
        name="ffn",
    )(state, tokens, attended, out_grad, gain, square, wide, square)


def shift_flat(block, distance):
    count = lax.axis_size(AXES)
    route = [(i - distance, i) for i in range(count) if 0 <= i - distance < count]
    return lax.ppermute(block, AXES, route)


def shift_ctx(block, distance):
    count = lax.axis_size("ctx")
    route = [(i - distance, i) for i in range(count) if 0 <= i - distance < count]
    return lax.ppermute(block, "ctx", route)


def swap(block, even_bit, odd_bit):
    count = lax.axis_size(AXES)
    route = [(i, i ^ (odd_bit if i & 1 else even_bit)) for i in range(count)]
    return lax.ppermute(block, AXES, route)


def to_aligned(shard, place, count, delta):
    rows = shard.shape[0]
    lag = delta * (count - 1)
    back = -(-lag // rows)
    if back == 1:
        keep = -(-lag // 8) * 8
        parts = [shift_flat(shard[rows - keep :], 1), shard]
    else:
        keep = back * rows
        parts = [shift_flat(shard, s) for s in range(back, 0, -1)] + [shard]
    joined = jnp.concatenate(parts, 0)
    return lax.dynamic_slice_in_dim(joined, keep - delta * place, rows - delta, 0)


def small_part(shard, place, count, delta):
    rows = shard.shape[0]
    extra = count * delta
    zeros = jnp.zeros((extra, 128), shard.dtype)
    joined = jnp.concatenate([zeros, shard, zeros], 0)
    start = extra + count * (rows - delta) - place * rows
    return lax.dynamic_slice_in_dim(joined, jnp.minimum(start, rows + extra), extra, 0)


def from_aligned(chunk, small, place, count, delta, rows):
    aligned = rows - delta
    ahead = -(-(count * delta) // aligned)
    parts = [chunk]
    if ahead == 1:
        keep = small.shape[0]
        got = shift_flat(chunk[:keep], -1)
        parts.append(jnp.where(place == count - 1, small, got))
    else:
        pad = ahead * aligned - small.shape[0]
        tail = jnp.concatenate([small, jnp.zeros((pad, 128), small.dtype)], 0)
        for s in range(1, ahead + 1):
            got = shift_flat(chunk, -s)
            for e in range(s):
                piece = tail[e * aligned : (e + 1) * aligned]
                got = jnp.where(place == count - s + e, piece, got)
            parts.append(got)
    return lax.dynamic_slice_in_dim(jnp.concatenate(parts, 0), delta * place, rows, 0)


def regroup(block):
    return block.reshape(-1, 24, 4, D).transpose(0, 2, 1, 3)


def ungroup(block):
    return block.reshape(-1, 4, 24, D).transpose(0, 2, 1, 3)


def normalize(values, gain):
    factor = lax.rsqrt(jnp.mean(values * values, axis=-1, keepdims=True) + norm_eps)
    scaled = values * factor
    return (scaled, factor, scaled * gain)


def norm_back(grad_in, scaled, factor, gain):
    weighted = grad_in * gain
    inner_mean = jnp.mean(weighted * scaled, axis=-1, keepdims=True)
    return factor * (weighted - scaled * inner_mean)


def adam_update(master, moment_one, moment_two, gradient, step_count, row_start):
    row_index = row_start + jnp.arange(master.shape[0], dtype=jnp.int32)
    matrix_rows = (4 * D * D + 2 * D * FF) // 128
    out_first = 3 * D * D // 128
    out_last = 4 * D * D // 128
    is_matrix = (row_index < matrix_rows)[:, None]
    is_out = ((row_index >= out_first) & (row_index < out_last))[:, None]
    step_rate = jnp.where(is_matrix, jnp.where(is_out, 0.5, 0.1), 1.0)
    decay_rate = jnp.where(is_matrix, 0.1, 0.0)
    step_value = step_count[0].astype(jnp.float32)
    new_one = 0.9 * moment_one + 0.1 * gradient
    new_two = 0.999 * moment_two + 0.001 * gradient * gradient
    corr_first = 1.0 - jnp.power(0.9, step_value)
    corr_second = 1.0 - jnp.power(0.999, step_value)
    new_weights = master - step_rate * (
        new_one / corr_first / (jnp.sqrt(new_two / corr_second) + 1e-08) + decay_rate * master
    )
    return (new_weights, new_one, new_two)


def shards(tokens, out_grad, positions, master, first_moment, second_moment, step_count):
    rows = tokens.shape[0]
    assert rows == SEQ_MIN
    count = lax.axis_size(AXES)
    place = lax.axis_index(AXES).astype(jnp.int32)
    owned = master.shape[0]
    aligned = (4 * D * D + 2 * D * FF) // 128 // count
    delta = owned - aligned
    height = aligned * 128 // D
    staged = count == 32
    first_place = positions[0]
    state = jnp.where(first_place < 0, 0, jnp.where(first_place >= SEQ_MIN, 2, 1)).astype(jnp.int32)
    state_vec = state[None]

    tokens_before = shift_ctx(tokens, 1)
    chunk = to_aligned(master, place, count, delta).reshape(-1, D)
    if staged:
        group = 3 * place + jnp.arange(3, dtype=jnp.int32)
        in_up = ((group >= 32) & (group < 64))[:, None, None, None]
        chunk = jnp.where(in_up, regroup(chunk), chunk.reshape(3, 4, 24, D)).reshape(-1, D)
    wide = lax.all_gather(chunk.astype(BF), AXES, axis=0, tiled=True)
    small = lax.psum(lax.reduce_precision(small_part(master, place, count, delta), 8, 7), AXES)
    small = small.reshape(-1)
    gain_first = small[:D]
    gain_second = small[D : 2 * D]
    taps = small[2 * D : 11 * D].reshape(3, 3 * D)
    in_weight = jnp.concatenate([wide[:D], wide[D : 2 * D], wide[2 * D : 3 * D]], 1)
    if staged:
        grouped = wide.reshape(96, 4, 24, D)
    else:
        grouped = jnp.concatenate(
            [wide[: 4 * D].reshape(-1, 4, 24, D), regroup(wide[4 * D : 8 * D]), wide[8 * D :].reshape(-1, 4, 24, D)], 0
        )

    tokens_both = jnp.concatenate([tokens_before, tokens], 0)
    inputs_both = tokens_both.astype(F32)
    normed_low = normalize(inputs_both, gain_first)[2].astype(BF)
    projected = dot(normed_low, in_weight).astype(BF)

    def masks(row_id):
        own_one = (state == 2) | ((state == 1) & (row_id > rows))
        own_two = (state == 2) | ((state == 1) & (row_id > rows + 1))
        one = jnp.where(row_id < rows, row_id >= 1, own_one) & (row_id < 2 * rows)
        two = jnp.where(row_id < rows, row_id >= 2, own_two) & (row_id < 2 * rows)
        return one.astype(F32), two.astype(F32)

    row_id = lax.broadcasted_iota(jnp.int32, (2 * rows, 128), 0)
    after_one, after_two = masks(row_id)
    ahead_one = masks(row_id + 1)[0]
    ahead_two = masks(row_id + 2)[1]
    attn_low, logs, *mixed = att_fwd(state_vec, projected, taps, after_one, after_two, rows)

    layer_out, grad_hidden, grad_attended, grad_gain_two, flat_grad = ffn(
        state_vec, tokens, attn_low, out_grad, gain_second[None], grouped, rows
    )
    if staged:
        late_chunk = lax.psum_scatter(
            flat_grad.reshape(12 * D, D), AXES, scatter_dimension=0, tiled=True
        )

    *back, tap_grads = att_bwd(
        state_vec, mixed, attn_low, logs, grad_attended, projected, taps, ahead_one, ahead_two, rows
    )
    core = (place & 1)[None]
    sums = qkv_bwd(
        core, tokens_both, back, wide, gain_first[None], grad_gain_two, tap_grads, rows,
        4 if staged else 0,
    )
    grads_before, grad_normed_one = sums[2:]
    from_next = shift_ctx(grads_before, -1)
    scaled_one, factor_one, _ = normalize(tokens.astype(F32), gain_first)
    input_grad = grad_hidden + norm_back(
        grad_normed_one + from_next.astype(F32), scaled_one, factor_one, gain_first
    )

    if staged:
        send, keep = sums[:2]
        x_bit = (place >> 1) & 1
        y_bit = (place >> 2) & 1
        got = swap(send, 1, 1)
        even = (place & 1) == 0
        stay = [jnp.where(even, 2 * j + x_bit, 2 * y_bit + j) for j in range(2)]
        away = [jnp.where(even, 2 * j + 1 - x_bit, 2 * (1 - y_bit) + j) for j in range(2)]
        send, keep = merge(jnp.stack(away + stay), keep, got, height, 2)
        got = swap(send, 2, 4)
        other = jnp.where(even, y_bit, x_bit)
        send, keep = merge(jnp.stack([1 - other, other]), keep, got, height, 1)
        got = swap(send, 4, 2)
        send, keep = merge(core, keep, got, height, 0)
        got = swap(send, 8, 8)
        send, keep = merge(core, keep, got, height, 0)
        got = swap(send, 16, 16)
        first = keep + got.astype(F32)
        small_grad = first[height:].reshape(-1, 128)
        late_grad = late_chunk.astype(F32)
        late_grad = jnp.where(in_up, ungroup(late_grad).reshape(3, 4, 24, D), late_grad.reshape(3, 4, 24, D))
        chunk_grad = jnp.where(place < count // 4, first[:height], late_grad.reshape(-1, D))
    else:
        wide_grad = jnp.concatenate(
            [
                sums[0],
                flat_grad[24:32].reshape(-1, D),
                ungroup(flat_grad[32:64]).reshape(-1, D),
                flat_grad[64:].reshape(-1, D),
            ],
            0,
        )
        chunk_grad = lax.psum_scatter(wide_grad, AXES, scatter_dimension=0, tiled=True).astype(F32)
        used = sums[1].reshape(-1, 128)
        extra = count * delta
        small_grad = jnp.concatenate([used, jnp.zeros((extra - used.shape[0], 128), F32)], 0)
        small_grad = lax.psum(small_grad, AXES)
    gradient = from_aligned(chunk_grad.reshape(-1, 128), small_grad, place, count, delta, owned)
    new_weights, new_one, new_two = adam_update(
        master, first_moment, second_moment, gradient, step_count, place * owned
    )
    return (layer_out, input_grad, new_weights, new_one, new_two, new_weights.astype(BF))


def solution(mesh):
    spread = P(AXES, None)
    return jax.shard_map(
        shards,
        mesh=mesh,
        in_specs=(spread, spread, P(AXES), spread, spread, spread, P()),
        out_specs=(spread,) * 6,
        check_vma=False,
    )
```

```python
import jax
import jax.numpy as jnp
from jax import lax
from jax.experimental import pallas as pl
from jax.experimental.pallas import tpu as pltpu
from jax.sharding import PartitionSpec as P

D = 768
HEADS = 12
HEAD_DIM = 64
FF = 3072
SEQ_MIN = 1024
AXES = ("dp", "ctx")
QB = 256
F32 = jnp.float32
BF = jnp.bfloat16
NT = (((1,), (1,)), ((), ()))
TN = (((0,), (0,)), ((), ()))
norm_eps = 1e-06
VMEM_LIMIT = 56 << 20


def dot(left, right):
    return jnp.dot(left, right, preferred_element_type=F32)


def dot_nt(left, right):
    return lax.dot_general(left, right, NT, preferred_element_type=F32)


def dot_tn(left, right):
    return lax.dot_general(left, right, TN, preferred_element_type=F32)


def cost(flops, nbytes, exps=0):
    return pl.CostEstimate(flops=int(flops), bytes_accessed=int(nbytes), transcendentals=int(exps))


def taps_seen(height, start, rows, state, distance, ahead):
    row = lax.broadcasted_iota(jnp.int32, (height, 128), 0) + (start + ahead)
    own = row - rows
    inside = (own >= distance) | ((own < 0) & (row >= distance)) | ((own >= 0) & (state == 2))
    filled = ((own < 0) | (state > 0)) & (row < 2 * rows)
    return (inside & filled).astype(F32)


def conv(x, taps, mask_one, mask_two):
    one = pltpu.roll(x, 1, 0) * mask_one
    two = pltpu.roll(x, 2, 0) * mask_two
    return (taps[0:1] * x + taps[1:2] * one + taps[2:3] * two).astype(BF)


def att_fwd_kernel(
    state_ref, tail_ref, q_ref, k_ref, v_ref, tq_ref, tk_ref, tv_ref,
    o_ref, l_ref, qm_ref, km_ref, vm_ref,
):
    rows = q_ref.shape[0]
    lane = lax.broadcasted_iota(jnp.int32, (1, 128), 1)
    state = state_ref[0]
    second = state == 2
    empty = state == 0
    one = taps_seen(2 * rows, 0, rows, state, 1, 0)
    two = taps_seen(2 * rows, 0, rows, state, 2, 0)
    x = jnp.concatenate([tail_ref[...].astype(F32), q_ref[...].astype(F32)], 0)
    qm_ref[...] = conv(x, tq_ref[...], one[rows - 8 :], two[rows - 8 :])[8:]
    km_ref[...] = conv(k_ref[...].astype(F32), tk_ref[...], one, two)
    vm_ref[...] = conv(v_ref[...].astype(F32), tv_ref[...], one, two)
    for i in range(rows // QB):
        rs = pl.ds(i * QB, QB)
        outs = []
        sums = []
        qf = qm_ref[rs, :].astype(F32) * 0.125
        for h in range(2):
            mine = (lane < 64) if h == 0 else (lane >= 64)
            qh = jnp.where(mine, qf, 0.0).astype(BF)
            nk = (i + 1) * QB
            vh = jnp.where(mine, vm_ref[rows : rows + nk, :], jnp.ones((), BF))
            s = dot_nt(qh, km_ref[rows : rows + nk, :])
            r = lax.broadcasted_iota(jnp.int32, (QB, QB), 0)
            c = lax.broadcasted_iota(jnp.int32, (QB, QB), 1)
            sd = jnp.where(c <= r, s[:, i * QB :], -1e30)
            m = jnp.max(sd, axis=1, keepdims=True)
            if i > 0:
                m = jnp.maximum(m, jnp.max(s[:, : i * QB], axis=1, keepdims=True))
            o = dot(jnp.exp(sd - m).astype(BF), vh[i * QB :])
            if i > 0:
                o = o + dot(jnp.exp(s[:, : i * QB] - m).astype(BF), vh[: i * QB])

            def prev(args):
                o1, m1 = args
                s2 = dot_nt(qh, km_ref[0:rows, :])
                m2 = jnp.maximum(m1, jnp.max(s2, axis=1, keepdims=True))
                p2 = jnp.exp(s2 - m2).astype(BF)
                vph = jnp.where(mine, vm_ref[0:rows, :], jnp.ones((), BF))
                return o1 * jnp.exp(m1 - m2) + dot(p2, vph), m2

            o, m = lax.cond(second, prev, lambda a: a, (o, m))
            outs.append(o / pltpu.roll(o, 64, 1))
            sums.append(m + jnp.log(o))
        res = jnp.where(lane < 64, outs[0], outs[1])
        res = jnp.where(empty, vm_ref[pl.ds(rows + i * QB, QB), :].astype(F32), res)
        o_ref[rs, :] = res.astype(BF)
        l_ref[rs, :] = jnp.where(lane < 64, sums[1], sums[0])


def att_fwd(state, projected, taps, rows):
    def cols(height, row, off):
        return pl.BlockSpec((height, 128), lambda p: (row, p + off))

    taps_at = [pl.BlockSpec((3, 128), lambda p, off=off: (0, p + off)) for off in (0, 6, 12)]
    return pl.pallas_call(
        att_fwd_kernel,
        grid=(6,),
        in_specs=[
            pl.BlockSpec(memory_space=pltpu.SMEM),
            cols(8, rows // 8 - 1, 0),
            cols(rows, 1, 0),
            cols(2 * rows, 0, 6),
            cols(2 * rows, 0, 12),
            *taps_at,
        ],
        out_specs=[cols(rows, 0, 0)] * 3 + [cols(2 * rows, 0, 0)] * 2,
        out_shape=[
            jax.ShapeDtypeStruct((rows, D), BF),
            jax.ShapeDtypeStruct((rows, D), F32),
            jax.ShapeDtypeStruct((rows, D), BF),
            jax.ShapeDtypeStruct((2 * rows, D), BF),
            jax.ShapeDtypeStruct((2 * rows, D), BF),
        ],
        compiler_params=pltpu.CompilerParams(vmem_limit_bytes=VMEM_LIMIT),
        cost_estimate=cost(2 * 2 * 12 * rows * rows * 1.5 * 256, rows * D * 30, 12 * rows * rows * 1.5),
        name="att_fwd",
    )(state, projected, projected, projected, projected, taps, taps, taps)


def three(x, lane, base):
    hi = x.astype(BF).astype(F32)
    r = x - hi
    mid = r.astype(BF).astype(F32)
    lo = r - mid
    return jnp.where(
        lane == base, hi, jnp.where(lane == base + 1, mid, jnp.where(lane == base + 2, lo, 0.0))
    )


def conv_back(grad, x, taps, mask_one, mask_two):
    height = grad.shape[0]
    one = pltpu.roll(grad, height - 1, 0) * mask_one
    two = pltpu.roll(grad, height - 2, 0) * mask_two
    back = (taps[0:1] * grad + taps[1:2] * one + taps[2:3] * two).astype(BF)
    sums = [jnp.sum(g * x, axis=0, keepdims=True) for g in (grad, one, two)]
    return back, sums


def att_bwd_kernel(
    state_ref, q_ref, k_ref, v_ref, o_ref, l_ref, do_ref, xt_ref, xq_ref, xk_ref, xv_ref,
    tq_ref, tk_ref, tv_ref,
    pq_ref, pt_ref, pk_ref, pv_ref, tg_ref, qa, da, dqs, dks, dvs,
):
    rows = q_ref.shape[0]
    lane = lax.broadcasted_iota(jnp.int32, (1, 128), 1)
    second = state_ref[0] == 2
    do = do_ref[...].astype(F32)
    od = do * o_ref[...].astype(F32)
    qf = q_ref[...].astype(F32) * 0.125
    lv = l_ref[...]
    zero = jnp.zeros((), BF)
    dks[...] = jnp.zeros(dks.shape, F32)
    dvs[...] = jnp.zeros(dvs.shape, F32)
    dqs[...] = jnp.zeros(dqs.shape, F32)
    for h in range(2):
        mine = (lane < 64) if h == 0 else (lane >= 64)
        base = 64 if h == 0 else 0
        ones3 = ((lane >= base) & (lane < base + 3)).astype(BF)
        delta = jnp.sum(jnp.where(mine, od, 0.0), axis=1, keepdims=True)
        qa[...] = jnp.where(mine, qf, three(-lv, lane, base)).astype(BF)
        da[...] = jnp.where(mine, do, three(-delta, lane, base)).astype(BF)

        def part(ks, qs, dos, mask):
            kk = k_ref[ks, :]
            st = dot_nt(jnp.where(mine, kk, ones3), qs)
            dp = dot_nt(jnp.where(mine, v_ref[ks, :], ones3), dos)
            p = jnp.exp(st)
            if mask is not None:
                p = jnp.where(mask, p, 0.0)
            ds = (p * dp).astype(BF)
            dvs[ks, :] += dot(p.astype(BF), jnp.where(mine, dos, zero))
            dks[ks, :] += dot(ds, jnp.where(mine, qs, zero))
            return dot_tn(ds, jnp.where(mine, kk, zero))

        for i in range(rows // QB):
            qs = qa[pl.ds(i * QB, QB), :]
            dos = da[pl.ds(i * QB, QB), :]
            kr = lax.broadcasted_iota(jnp.int32, (QB, QB), 0)
            qr = lax.broadcasted_iota(jnp.int32, (QB, QB), 1)
            dq = part(pl.ds(rows + i * QB, QB), qs, dos, kr <= qr)
            if i > 0:
                dq = dq + part(pl.ds(rows, i * QB), qs, dos, None)
            dqs[pl.ds(8 + i * QB, QB), :] += dq * 0.125

        @pl.when(second)
        def _():
            for i in range(rows // QB):
                rs = pl.ds(i * QB, QB)
                dq = part(pl.ds(0, rows), qa[rs, :], da[rs, :], None)
                dqs[pl.ds(8 + i * QB, QB), :] += dq * 0.125

    one = taps_seen(2 * rows, 0, rows, state_ref[0], 1, 1)
    two = taps_seen(2 * rows, 0, rows, state_ref[0], 2, 2)
    xq = jnp.concatenate([xt_ref[...].astype(F32), xq_ref[...].astype(F32)], 0)
    pq, sq = conv_back(dqs[...], xq, tq_ref[...], one[rows - 8 :], two[rows - 8 :])
    pt_ref[...] = pq[:8]
    pq_ref[...] = pq[8:]
    pk_ref[...], sk = conv_back(dks[...], xk_ref[...].astype(F32), tk_ref[...], one, two)
    pv_ref[...], sv = conv_back(dvs[...], xv_ref[...].astype(F32), tv_ref[...], one, two)
    tg_ref[...] = jnp.zeros(tg_ref.shape, F32)
    for j in range(3):
        for m, s in enumerate((sq, sk, sv)):
            tg_ref[3 * j + m : 3 * j + m + 1, :] = s[j]


def att_bwd(state, mixed, attended, logs, grad, projected, taps, rows):
    def cols(height, row, off):
        return pl.BlockSpec((height, 128), lambda p: (row, p + off))

    taps_at = [pl.BlockSpec((3, 128), lambda p, off=off: (0, p + off)) for off in (0, 6, 12)]
    own = cols(rows, 0, 0)
    both = cols(2 * rows, 0, 0)
    return pl.pallas_call(
        att_bwd_kernel,
        grid=(6,),
        in_specs=[
            pl.BlockSpec(memory_space=pltpu.SMEM),
            own, both, both, own, own, own,
            cols(8, rows // 8 - 1, 0),
            cols(rows, 1, 0),
            cols(2 * rows, 0, 6),
            cols(2 * rows, 0, 12),
            *taps_at,
        ],
        out_specs=[own, cols(8, 0, 0), both, both, cols(16, 0, 0)],
        out_shape=[
            jax.ShapeDtypeStruct((rows, D), BF),
            jax.ShapeDtypeStruct((8, D), BF),
            jax.ShapeDtypeStruct((2 * rows, D), BF),
            jax.ShapeDtypeStruct((2 * rows, D), BF),
            jax.ShapeDtypeStruct((16, D), F32),
        ],
        scratch_shapes=[
            pltpu.VMEM((rows, 128), BF),
            pltpu.VMEM((rows, 128), BF),
            pltpu.VMEM((rows + 8, 128), F32),
            pltpu.VMEM((2 * rows, 128), F32),
            pltpu.VMEM((2 * rows, 128), F32),
        ],
        compiler_params=pltpu.CompilerParams(vmem_limit_bytes=VMEM_LIMIT),
        cost_estimate=cost(5 * 2 * 12 * rows * rows * 1.5 * 256, rows * D * 40, 12 * rows * rows * 1.5),
        name="att_bwd",
    )(state, *mixed, attended, logs, grad, projected, projected, projected, projected,
      taps, taps, taps)


def qkv_bwd_kernel(
    core_ref, x_ref, dq_ref, dt_ref, dk_ref, dv_ref, w_ref, gain_ref, gain_two_ref, tg_ref,
    *refs, pieces, blocks,
):
    if pieces:
        send_ref, keep_ref, prev_ref, own_ref, acc, gacc = refs
    else:
        keep_ref, small_ref, prev_ref, own_ref, acc, gacc = refs
    i = pl.program_id(0)
    half = blocks // 2

    @pl.when(i == 0)
    def _():
        acc[...] = jnp.zeros(acc.shape, F32)
        gacc[...] = jnp.zeros(gacc.shape, F32)

    x = x_ref[...].astype(F32)
    hat = x * lax.rsqrt(jnp.mean(x * x, axis=-1, keepdims=True) + norm_eps)
    low = (hat * gain_ref[...]).astype(BF)
    dk = dk_ref[...]
    dv = dv_ref[...]
    gn = dot_nt(dk, w_ref[D : 2 * D, :]) + dot_nt(dv, w_ref[2 * D : 3 * D, :])
    acc[D : 2 * D, :] += dot_tn(low, dk)
    acc[2 * D : 3 * D, :] += dot_tn(low, dv)

    @pl.when(i < half - 1)
    def _():
        prev_ref[...] = gn.astype(BF)
        gacc[0:1, :] += jnp.sum(gn * hat, axis=0, keepdims=True)

    @pl.when(i == half - 1)
    def _():
        dt = dt_ref[...]
        last = gn.shape[0] - 8
        acc[0:D, :] += dot_tn(low[last:], dt)
        full = jnp.concatenate([gn[:last], gn[last:] + dot_nt(dt, w_ref[0:D, :])], 0)
        prev_ref[...] = full.astype(BF)
        gacc[0:1, :] += jnp.sum(full * hat, axis=0, keepdims=True)

    @pl.when(i >= half)
    def _():
        dq = dq_ref[...]
        acc[0:D, :] += dot_tn(low, dq)
        full = gn + dot_nt(dq, w_ref[0:D, :])
        own_ref[...] = full
        gacc[0:1, :] += jnp.sum(full * hat, axis=0, keepdims=True)

    @pl.when(i == blocks - 1)
    def _():
        small = jnp.concatenate(
            [gacc[0:1, :], gain_two_ref[...], tg_ref[0:9, :], jnp.zeros((5, D), F32)], 0
        )
        if pieces:
            core = core_ref[0]
            height = 3 * D // (2 * pieces)
            for j in range(pieces):
                to = pl.ds(j * height, height)
                away = pl.ds(pl.multiple_of((2 * j + 1 - core) * height, 16), height)
                here = pl.ds(pl.multiple_of((2 * j + core) * height, 16), height)
                send_ref[to, :] = acc[away, :].astype(BF)
                keep_ref[to, :] = acc[here, :]
            send_ref[pieces * height :, :] = small.astype(BF)
            keep_ref[pieces * height :, :] = small
        else:
            keep_ref[...] = acc[...].astype(BF)
            small_ref[...] = small


def qkv_bwd(core, x_both, back, wide, gain, gain_two_grad, tap_grads, rows, pieces):
    dq, dt, dk, dv = back
    blocks = 4
    half = blocks // 2
    height = 2 * rows // blocks
    step = pl.BlockSpec((height, D), lambda i: (i, 0))
    late = pl.BlockSpec((height, D), lambda i: (jnp.maximum(i - half, 0), 0))
    early = pl.BlockSpec((height, D), lambda i: (jnp.minimum(i, half - 1), 0))

    def whole(shape):
        return pl.BlockSpec(shape, lambda i: (0, 0))

    if pieces:
        packed = 3 * D // 2 + 16
        outs = [jax.ShapeDtypeStruct((packed, D), BF), jax.ShapeDtypeStruct((packed, D), F32)]
        out_at = [whole((packed, D))] * 2
    else:
        outs = [jax.ShapeDtypeStruct((3 * D, D), BF), jax.ShapeDtypeStruct((16, D), F32)]
        out_at = [whole((3 * D, D)), whole((16, D))]

    def body(*refs):
        qkv_bwd_kernel(*refs, pieces=pieces, blocks=blocks)

    return pl.pallas_call(
        body,
        grid=(blocks,),
        in_specs=[
            pl.BlockSpec(memory_space=pltpu.SMEM),
            step, late, whole((8, D)), step, step, whole((3 * D, D)),
            whole((1, D)), whole((1, D)), whole((16, D)),
        ],
        out_specs=out_at + [early, late],
        out_shape=outs
        + [jax.ShapeDtypeStruct((rows, D), BF), jax.ShapeDtypeStruct((rows, D), F32)],
        scratch_shapes=[pltpu.VMEM((3 * D, D), F32), pltpu.VMEM((8, D), F32)],
        compiler_params=pltpu.CompilerParams(vmem_limit_bytes=VMEM_LIMIT),
        cost_estimate=cost(2 * 2 * D * D * 5 * rows, rows * D * 30),
        name="qkv_bwd",
    )(core, x_both, dq, dt, dk, dv, wide, gain, gain_two_grad, tap_grads)


def merge(index, keep, got, height, taken):
    rows = keep.shape[0]
    out_rows = taken * height + 16 if taken else rows

    def body(index_ref, keep_ref, got_ref, send_ref, stay_ref):
        if not taken:
            total = keep_ref[...] + got_ref[...].astype(F32)
            send_ref[...] = total.astype(BF)
            stay_ref[...] = total
            return
        for j in range(taken):
            to = pl.ds(j * height, height)
            away = pl.ds(pl.multiple_of(index_ref[j] * height, 16), height)
            here = pl.ds(pl.multiple_of(index_ref[taken + j] * height, 16), height)
            send_ref[to, :] = (keep_ref[away, :] + got_ref[away, :].astype(F32)).astype(BF)
            stay_ref[to, :] = keep_ref[here, :] + got_ref[here, :].astype(F32)
        end = keep_ref[rows - 16 :, :] + got_ref[rows - 16 :, :].astype(F32)
        send_ref[taken * height :, :] = end.astype(BF)
        stay_ref[taken * height :, :] = end

    vmem = pl.BlockSpec(memory_space=pltpu.VMEM)
    return pl.pallas_call(
        body,
        in_specs=[pl.BlockSpec(memory_space=pltpu.SMEM), vmem, vmem],
        out_specs=[vmem, vmem],
        out_shape=[
            jax.ShapeDtypeStruct((out_rows, D), BF),
            jax.ShapeDtypeStruct((out_rows, D), F32),
        ],
        compiler_params=pltpu.CompilerParams(vmem_limit_bytes=32 << 20),
        cost_estimate=cost(rows * D, rows * D * 12),
        name="merge",
    )(index, keep, got)


def join(own, got, height):
    rows = own.shape[0]
    body_rows = rows - 16

    def body(own_ref, got_ref, out_ref):
        out_ref[0:body_rows, :] = own_ref[0:body_rows, :]
        out_ref[body_rows : 2 * body_rows, :] = got_ref[0:body_rows, :]
        out_ref[2 * body_rows :, :] = own_ref[body_rows:, :] + got_ref[body_rows:, :]

    vmem = pl.BlockSpec(memory_space=pltpu.VMEM)
    return pl.pallas_call(
        body,
        in_specs=[vmem, vmem],
        out_specs=vmem,
        out_shape=jax.ShapeDtypeStruct((2 * body_rows + 16, D), BF),
        compiler_params=pltpu.CompilerParams(vmem_limit_bytes=32 << 20),
        cost_estimate=cost(rows * D, rows * D * 8),
        name="join",
    )(own, got)


def qkv_fwd_kernel(index_ref, x_ref, *refs, pieces, blocks):
    if pieces:
        own_ref, got_ref, out_ref, small_ref, weight = refs
    else:
        weight, given_ref, out_ref, small_ref = refs
    i = pl.program_id(0)

    @pl.when(i == 0)
    def _():
        if pieces:
            height = 3 * D // (2 * pieces)
            for j in range(pieces):
                at = pl.ds(j * height, height)
                for k, ref in enumerate((own_ref, got_ref)):
                    to = pl.multiple_of(index_ref[k * pieces + j] * height, 16)
                    weight[pl.ds(to, height), :] = ref[at, :]
            end = pl.ds(pieces * height, 16)
            small_ref[...] = own_ref[end, :].astype(F32) + got_ref[end, :].astype(F32)
        else:
            small_ref[...] = given_ref[...]

    x = x_ref[...].astype(F32)
    hat = x * lax.rsqrt(jnp.mean(x * x, axis=-1, keepdims=True) + norm_eps)
    low = (hat * small_ref[0:1, :]).astype(BF)

    @pl.when(i >= blocks // 2 - 1)
    def _():
        out_ref[:, 0:D] = dot(low, weight[0:D, :]).astype(BF)

    out_ref[:, D : 2 * D] = dot(low, weight[D : 2 * D, :]).astype(BF)
    out_ref[:, 2 * D : 3 * D] = dot(low, weight[2 * D : 3 * D, :]).astype(BF)


def qkv_fwd(index, x_both, weights, rows, pieces):
    blocks = 4
    height = 2 * rows // blocks

    def body(*refs):
        qkv_fwd_kernel(*refs, pieces=pieces, blocks=blocks)

    return pl.pallas_call(
        body,
        grid=(blocks,),
        in_specs=[
            pl.BlockSpec(memory_space=pltpu.SMEM),
            pl.BlockSpec((height, D), lambda i: (i, 0)),
            *[pl.BlockSpec(w.shape, lambda i: (0, 0)) for w in weights],
        ],
        out_specs=[
            pl.BlockSpec((height, 3 * D), lambda i: (i, 0)),
            pl.BlockSpec((16, D), lambda i: (0, 0)),
        ],
        out_shape=[
            jax.ShapeDtypeStruct((2 * rows, 3 * D), BF),
            jax.ShapeDtypeStruct((16, D), F32),
        ],
        scratch_shapes=[pltpu.VMEM((3 * D, D), BF)] if pieces else [],
        compiler_params=pltpu.CompilerParams(vmem_limit_bytes=VMEM_LIMIT),
        cost_estimate=cost(2 * 2 * rows * D * 3 * D, rows * D * 20),
        name="qkv_fwd",
    )(index, x_both, *weights)


def ffn_kernel(
    state_ref, x_ref, att_ref, cot_ref, gain_ref, wo_ref, up_ref, down_ref,
    out_ref, gh_ref, ga_ref, gain_grad_ref, flat_ref,
    hidden, low, total, back, cot, sq, gb, stage_up, stage_down, stage_out, sems,
):
    c = pl.program_id(0)
    rows = x_ref.shape[0]
    blocks = [pl.ds(i * QB, QB) for i in range(rows // QB)]
    last = c == pl.num_programs(0) - 1

    def put_zero(i):
        return pltpu.make_async_copy(stage_out, flat_ref.at[pl.ds(8 * i, 8)], sems.at[8 + i])

    def put_up(i):
        return pltpu.make_async_copy(stage_up.at[i], flat_ref.at[pl.ds(32, 32), i], sems.at[i])

    def put_down(i):
        return pltpu.make_async_copy(stage_down.at[i], flat_ref.at[pl.ds(64 + 8 * i, 8)], sems.at[4 + i])

    def put_out():
        return pltpu.make_async_copy(stage_out, flat_ref.at[pl.ds(24, 8)], sems.at[11])

    @pl.when(c == 0)
    def _():
        stage_out[...] = jnp.zeros(stage_out.shape, BF)
        for i in range(3):
            put_zero(i).start()
        cot[...] = jnp.where(state_ref[0] > 0, cot_ref[...], jnp.zeros((), BF))
        total[...] = jnp.zeros(total.shape, F32)
        back[...] = jnp.zeros(back.shape, F32)
        for b in blocks:
            h = x_ref[b, :].astype(F32) + dot(att_ref[b, :], wo_ref[...])
            hidden[b, :] = h
            hat = h * lax.rsqrt(jnp.mean(h * h, axis=-1, keepdims=True) + norm_eps)
            low[b, :] = (hat * gain_ref[...]).astype(BF)

    up = up_ref[...].reshape(D, D)
    for b in blocks:
        act = jnp.maximum(dot(low[b, :], up), 0.0)
        s = (act * act).astype(BF)
        sq[b, :] = s
        total[b, :] += dot(s, down_ref[...])
        g = (dot_nt(cot[b, :], down_ref[...]) * 2.0 * act).astype(BF)
        gb[b, :] = g
        back[b, :] += dot_nt(g, up)
    stage_down[c] = dot_tn(sq[...], cot[...]).reshape(8, 4, 24, D).astype(BF)
    stage_up[c] = dot_tn(low[...], gb[...]).reshape(32, 24, D).astype(BF)
    put_down(c).start()
    put_up(c).start()

    @pl.when(last)
    def _():
        for i in range(3):
            put_zero(i).wait()
        gain = gain_ref[...]
        sums = jnp.zeros((1, D), F32)
        for b in blocks:
            h = hidden[b, :]
            out_ref[b, :] = (h + total[b, :]).astype(BF)
            factor = lax.rsqrt(jnp.mean(h * h, axis=-1, keepdims=True) + norm_eps)
            hat = h * factor
            g = back[b, :]
            sums = sums + jnp.sum(g * hat, axis=0, keepdims=True)
            weighted = g * gain
            inner = jnp.mean(weighted * hat, axis=-1, keepdims=True)
            grad = cot[b, :].astype(F32) + factor * (weighted - hat * inner)
            gh_ref[b, :] = grad
            grad_low = grad.astype(BF)
            gb[b, :] = grad_low
            ga_ref[b, :] = dot_nt(grad_low, wo_ref[...]).astype(BF)
        gain_grad_ref[...] = sums
        stage_out[...] = dot_tn(att_ref[...], gb[...]).reshape(8, 4, 24, D).astype(BF)
        put_out().start()
        for i in range(pl.num_programs(0)):
            put_down(i).wait()
            put_up(i).wait()
        put_out().wait()


def ffn(state, tokens, attended, out_grad, gain, wide, rows):
    def whole(shape):
        return pl.BlockSpec(shape, lambda c: (0,) * len(shape))

    act = whole((rows, D))
    square = wide.reshape(12 * D, D)
    return pl.pallas_call(
        ffn_kernel,
        grid=(4,),
        in_specs=[
            pl.BlockSpec(memory_space=pltpu.SMEM),
            act, act, act, whole((1, D)),
            pl.BlockSpec((D, D), lambda c: (3, 0)),
            pl.BlockSpec((32, 1, 24, D), lambda c: (1, c, 0, 0)),
            pl.BlockSpec((D, D), lambda c: (8 + c, 0)),
        ],
        out_specs=[act, act, act, whole((1, D)), pl.BlockSpec(memory_space=pl.ANY)],
        out_shape=[
            jax.ShapeDtypeStruct((rows, D), BF),
            jax.ShapeDtypeStruct((rows, D), F32),
            jax.ShapeDtypeStruct((rows, D), BF),
            jax.ShapeDtypeStruct((1, D), F32),
            jax.ShapeDtypeStruct((96, 4, 24, D), BF),
        ],
        scratch_shapes=[
            pltpu.VMEM((rows, D), F32),
            pltpu.VMEM((rows, D), BF),
            pltpu.VMEM((rows, D), F32),
            pltpu.VMEM((rows, D), F32),
            pltpu.VMEM((rows, D), BF),
            pltpu.VMEM((rows, D), BF),
            pltpu.VMEM((rows, D), BF),
            pltpu.VMEM((4, 32, 24, D), BF),
            pltpu.VMEM((4, 8, 4, 24, D), BF),
            pltpu.VMEM((8, 4, 24, D), BF),
            pltpu.SemaphoreType.DMA((12,)),
        ],
        compiler_params=pltpu.CompilerParams(vmem_limit_bytes=60 << 20),
        cost_estimate=cost(2 * rows * D * D * (24 + 3), 2 * 12 * D * D * 2 + rows * D * 16),
        name="ffn",
    )(state, tokens, attended, out_grad, gain, square, wide, square)


def shift_flat(block, distance):
    count = lax.axis_size(AXES)
    route = [(i - distance, i) for i in range(count) if 0 <= i - distance < count]
    return lax.ppermute(block, AXES, route)


def shift_ctx(block, distance):
    count = lax.axis_size("ctx")
    route = [(i - distance, i) for i in range(count) if 0 <= i - distance < count]
    return lax.ppermute(block, "ctx", route)


def swap(block, even_bit, odd_bit):
    count = lax.axis_size(AXES)
    route = [(i, i ^ (odd_bit if i & 1 else even_bit)) for i in range(count)]
    return lax.ppermute(block, AXES, route)


def to_aligned(shard, place, count, delta):
    rows = shard.shape[0]
    lag = delta * (count - 1)
    back = -(-lag // rows)
    if back == 1:
        keep = -(-lag // 8) * 8
        parts = [shift_flat(shard[rows - keep :], 1), shard]
    else:
        keep = back * rows
        parts = [shift_flat(shard, s) for s in range(back, 0, -1)] + [shard]
    joined = jnp.concatenate(parts, 0)
    return lax.dynamic_slice_in_dim(joined, keep - delta * place, rows - delta, 0)


def small_part(shard, place, count, delta):
    rows = shard.shape[0]
    extra = count * delta
    zeros = jnp.zeros((extra, 128), shard.dtype)
    joined = jnp.concatenate([zeros, shard, zeros], 0)
    start = extra + count * (rows - delta) - place * rows
    return lax.dynamic_slice_in_dim(joined, jnp.minimum(start, rows + extra), extra, 0)


def from_aligned(chunk, small, place, count, delta, rows):
    aligned = rows - delta
    ahead = -(-(count * delta) // aligned)
    parts = [chunk]
    if ahead == 1:
        keep = small.shape[0]
        got = shift_flat(chunk[:keep], -1)
        parts.append(jnp.where(place == count - 1, small, got))
    else:
        pad = ahead * aligned - small.shape[0]
        tail = jnp.concatenate([small, jnp.zeros((pad, 128), small.dtype)], 0)
        for s in range(1, ahead + 1):
            got = shift_flat(chunk, -s)
            for e in range(s):
                piece = tail[e * aligned : (e + 1) * aligned]
                got = jnp.where(place == count - s + e, piece, got)
            parts.append(got)
    return lax.dynamic_slice_in_dim(jnp.concatenate(parts, 0), delta * place, rows, 0)


def regroup(block):
    return block.reshape(-1, 24, 4, D).transpose(0, 2, 1, 3)


def ungroup(block):
    return block.reshape(-1, 4, 24, D).transpose(0, 2, 1, 3)


def normalize(values, gain):
    factor = lax.rsqrt(jnp.mean(values * values, axis=-1, keepdims=True) + norm_eps)
    scaled = values * factor
    return (scaled, factor, scaled * gain)


def norm_back(grad_in, scaled, factor, gain):
    weighted = grad_in * gain
    inner_mean = jnp.mean(weighted * scaled, axis=-1, keepdims=True)
    return factor * (weighted - scaled * inner_mean)


def adam_update(master, moment_one, moment_two, gradient, step_count, row_start):
    row_index = row_start + jnp.arange(master.shape[0], dtype=jnp.int32)
    matrix_rows = (4 * D * D + 2 * D * FF) // 128
    out_first = 3 * D * D // 128
    out_last = 4 * D * D // 128
    is_matrix = (row_index < matrix_rows)[:, None]
    is_out = ((row_index >= out_first) & (row_index < out_last))[:, None]
    step_rate = jnp.where(is_matrix, jnp.where(is_out, 0.5, 0.1), 1.0)
    decay_rate = jnp.where(is_matrix, 0.1, 0.0)
    step_value = step_count[0].astype(jnp.float32)
    new_one = 0.9 * moment_one + 0.1 * gradient
    new_two = 0.999 * moment_two + 0.001 * gradient * gradient
    corr_first = 1.0 - jnp.power(0.9, step_value)
    corr_second = 1.0 - jnp.power(0.999, step_value)
    new_weights = master - step_rate * (
        new_one / corr_first / (jnp.sqrt(new_two / corr_second) + 1e-08) + decay_rate * master
    )
    return (new_weights, new_one, new_two)


def shards(tokens, out_grad, positions, master, first_moment, second_moment, step_count):
    rows = tokens.shape[0]
    assert rows == SEQ_MIN
    count = lax.axis_size(AXES)
    place = lax.axis_index(AXES).astype(jnp.int32)
    owned = master.shape[0]
    aligned = (4 * D * D + 2 * D * FF) // 128 // count
    delta = owned - aligned
    height = aligned * 128 // D
    staged = count == 32
    first_place = positions[0]
    state = jnp.where(first_place < 0, 0, jnp.where(first_place >= SEQ_MIN, 2, 1)).astype(jnp.int32)
    state_vec = state[None]

    tokens_before = shift_ctx(tokens, 1)
    chunk = to_aligned(master, place, count, delta).reshape(-1, D)
    if staged:
        group = 3 * place + jnp.arange(3, dtype=jnp.int32)
        in_up = ((group >= 32) & (group < 64))[:, None, None, None]
        chunk = jnp.where(in_up, regroup(chunk), chunk.reshape(3, 4, 24, D)).reshape(-1, D)
    chunk = chunk.astype(BF)
    small = lax.reduce_precision(small_part(master, place, count, delta), 8, 7)
    core = (place & 1)[None]
    x_bit = (place >> 1) & 1
    y_bit = (place >> 2) & 1
    even = (place & 1) == 0
    tokens_both = jnp.concatenate([tokens_before, tokens], 0)
    if staged:
        mine = jnp.concatenate(
            [jnp.where(place < count // 4, chunk, jnp.zeros((), BF)), small.astype(BF).reshape(-1, D)], 0
        )
        mine = mine + swap(mine, 16, 16)
        mine = mine + swap(mine, 8, 8)
        mine = join(mine, swap(mine, 2, 4), height)
        mine = join(mine, swap(mine, 4, 2), height)
        got = swap(mine, 1, 1)
        where_at = []
        for k in (0, 1):
            turn = even if k == 0 else jnp.logical_not(even)
            for j in range(4):
                near, far = j & 1, j >> 1
                x_of = x_bit ^ jnp.where(turn, near, far)
                y_of = y_bit ^ jnp.where(turn, far, near)
                where_at.append(4 * y_of + 2 * x_of + (core[0] ^ k))
        index = jnp.stack(where_at).astype(jnp.int32)
        projected, small = qkv_fwd(index, tokens_both, (mine, got), rows, 4)
        wide = lax.all_gather(chunk, AXES, axis=0, tiled=True)
    else:
        wide = lax.all_gather(chunk, AXES, axis=0, tiled=True)
        small = lax.psum(small, AXES)[:96].reshape(-1, D)
        projected, small = qkv_fwd(core, tokens_both, (wide[: 3 * D], small), rows, 0)
    gain_first = small[0]
    gain_second = small[1]
    taps = small[2:11].reshape(3, 3 * D)
    if staged:
        grouped = wide.reshape(96, 4, 24, D)
    else:
        grouped = jnp.concatenate(
            [wide[: 4 * D].reshape(-1, 4, 24, D), regroup(wide[4 * D : 8 * D]), wide[8 * D :].reshape(-1, 4, 24, D)], 0
        )

    attn_low, logs, *mixed = att_fwd(state_vec, projected, taps, rows)

    layer_out, grad_hidden, grad_attended, grad_gain_two, flat_grad = ffn(
        state_vec, tokens, attn_low, out_grad, gain_second[None], grouped, rows
    )
    if staged:
        late_chunk = lax.psum_scatter(
            flat_grad.reshape(12 * D, D), AXES, scatter_dimension=0, tiled=True
        )

    *back, tap_grads = att_bwd(
        state_vec, mixed, attn_low, logs, grad_attended, projected, taps, rows
    )
    sums = qkv_bwd(
        core, tokens_both, back, wide, gain_first[None], grad_gain_two, tap_grads, rows,
        4 if staged else 0,
    )
    grads_before, grad_normed_one = sums[2:]
    from_next = shift_ctx(grads_before, -1)
    scaled_one, factor_one, _ = normalize(tokens.astype(F32), gain_first)
    input_grad = grad_hidden + norm_back(
        grad_normed_one + from_next.astype(F32), scaled_one, factor_one, gain_first
    )

    if staged:
        send, keep = sums[:2]
        got = swap(send, 1, 1)
        stay = [jnp.where(even, 2 * j + x_bit, 2 * y_bit + j) for j in range(2)]
        away = [jnp.where(even, 2 * j + 1 - x_bit, 2 * (1 - y_bit) + j) for j in range(2)]
        send, keep = merge(jnp.stack(away + stay), keep, got, height, 2)
        got = swap(send, 2, 4)
        other = jnp.where(even, y_bit, x_bit)
        send, keep = merge(jnp.stack([1 - other, other]), keep, got, height, 1)
        got = swap(send, 4, 2)
        send, keep = merge(core, keep, got, height, 0)
        got = swap(send, 8, 8)
        send, keep = merge(core, keep, got, height, 0)
        got = swap(send, 16, 16)
        first = keep + got.astype(F32)
        small_grad = first[height:].reshape(-1, 128)
        late_grad = late_chunk.astype(F32)
        late_grad = jnp.where(in_up, ungroup(late_grad).reshape(3, 4, 24, D), late_grad.reshape(3, 4, 24, D))
        chunk_grad = jnp.where(place < count // 4, first[:height], late_grad.reshape(-1, D))
    else:
        wide_grad = jnp.concatenate(
            [
                sums[0],
                flat_grad[24:32].reshape(-1, D),
                ungroup(flat_grad[32:64]).reshape(-1, D),
                flat_grad[64:].reshape(-1, D),
            ],
            0,
        )
        chunk_grad = lax.psum_scatter(wide_grad, AXES, scatter_dimension=0, tiled=True).astype(F32)
        used = sums[1].reshape(-1, 128)
        extra = count * delta
        small_grad = jnp.concatenate([used, jnp.zeros((extra - used.shape[0], 128), F32)], 0)
        small_grad = lax.psum(small_grad, AXES)
    gradient = from_aligned(chunk_grad.reshape(-1, 128), small_grad, place, count, delta, owned)
    new_weights, new_one, new_two = adam_update(
        master, first_moment, second_moment, gradient, step_count, place * owned
    )
    return (layer_out, input_grad, new_weights, new_one, new_two, new_weights.astype(BF))


def solution(mesh):
    spread = P(AXES, None)
    return jax.shard_map(
        shards,
        mesh=mesh,
        in_specs=(spread, spread, P(AXES), spread, spread, spread, P()),
        out_specs=(spread,) * 6,
        check_vma=False,
    )
```

```python
import jax
import jax.numpy as jnp
from jax import lax
from jax.experimental import pallas as pl
from jax.experimental.pallas import tpu as pltpu
from jax.sharding import PartitionSpec as P

D = 768
HEADS = 12
HEAD_DIM = 64
FF = 3072
SEQ_MIN = 1024
AXES = ("dp", "ctx")
QB = 256
PARTS = 3
F32 = jnp.float32
BF = jnp.bfloat16
NT = (((1,), (1,)), ((), ()))
TN = (((0,), (0,)), ((), ()))
norm_eps = 1e-06
VMEM_LIMIT = 56 << 20


def dot(left, right):
    return jnp.dot(left, right, preferred_element_type=F32)


def dot_nt(left, right):
    return lax.dot_general(left, right, NT, preferred_element_type=F32)


def dot_tn(left, right):
    return lax.dot_general(left, right, TN, preferred_element_type=F32)


def cost(flops, nbytes, exps=0):
    return pl.CostEstimate(flops=int(flops), bytes_accessed=int(nbytes), transcendentals=int(exps))


def taps_seen(height, start, rows, state, distance, ahead):
    row = lax.broadcasted_iota(jnp.int32, (height, 128), 0) + (start + ahead)
    own = row - rows
    inside = (own >= distance) | ((own < 0) & (row >= distance)) | ((own >= 0) & (state == 2))
    filled = ((own < 0) | (state > 0)) & (row < 2 * rows)
    return (inside & filled).astype(F32)


def conv(x, taps, mask_one, mask_two):
    one = pltpu.roll(x, 1, 0) * mask_one
    two = pltpu.roll(x, 2, 0) * mask_two
    return (taps[0:1] * x + taps[1:2] * one + taps[2:3] * two).astype(BF)


def att_fwd_kernel(
    state_ref, tail_ref, q_ref, k_ref, v_ref, tq_ref, tk_ref, tv_ref,
    o_ref, l_ref, qm_ref, km_ref, vm_ref,
):
    rows = q_ref.shape[0]
    lane = lax.broadcasted_iota(jnp.int32, (1, 128), 1)
    state = state_ref[0]
    second = state == 2
    empty = state == 0
    one = taps_seen(2 * rows, 0, rows, state, 1, 0)
    two = taps_seen(2 * rows, 0, rows, state, 2, 0)
    x = jnp.concatenate([tail_ref[...].astype(F32), q_ref[...].astype(F32)], 0)
    qm_ref[...] = conv(x, tq_ref[...], one[rows - 8 :], two[rows - 8 :])[8:]
    km_ref[...] = conv(k_ref[...].astype(F32), tk_ref[...], one, two)
    vm_ref[...] = conv(v_ref[...].astype(F32), tv_ref[...], one, two)
    for i in range(rows // QB):
        rs = pl.ds(i * QB, QB)
        outs = []
        sums = []
        qf = qm_ref[rs, :].astype(F32) * 0.125
        for h in range(2):
            mine = (lane < 64) if h == 0 else (lane >= 64)
            qh = jnp.where(mine, qf, 0.0).astype(BF)
            nk = (i + 1) * QB
            vh = jnp.where(mine, vm_ref[rows : rows + nk, :], jnp.ones((), BF))
            s = dot_nt(qh, km_ref[rows : rows + nk, :])
            r = lax.broadcasted_iota(jnp.int32, (QB, QB), 0)
            c = lax.broadcasted_iota(jnp.int32, (QB, QB), 1)
            sd = jnp.where(c <= r, s[:, i * QB :], -1e30)
            m = jnp.max(sd, axis=1, keepdims=True)
            if i > 0:
                m = jnp.maximum(m, jnp.max(s[:, : i * QB], axis=1, keepdims=True))
            o = dot(jnp.exp(sd - m).astype(BF), vh[i * QB :])
            if i > 0:
                o = o + dot(jnp.exp(s[:, : i * QB] - m).astype(BF), vh[: i * QB])

            def prev(args):
                o1, m1 = args
                s2 = dot_nt(qh, km_ref[0:rows, :])
                m2 = jnp.maximum(m1, jnp.max(s2, axis=1, keepdims=True))
                p2 = jnp.exp(s2 - m2).astype(BF)
                vph = jnp.where(mine, vm_ref[0:rows, :], jnp.ones((), BF))
                return o1 * jnp.exp(m1 - m2) + dot(p2, vph), m2

            o, m = lax.cond(second, prev, lambda a: a, (o, m))
            outs.append(o / pltpu.roll(o, 64, 1))
            sums.append(m + jnp.log(o))
        res = jnp.where(lane < 64, outs[0], outs[1])
        res = jnp.where(empty, vm_ref[pl.ds(rows + i * QB, QB), :].astype(F32), res)
        o_ref[rs, :] = res.astype(BF)
        l_ref[rs, :] = jnp.where(lane < 64, sums[1], sums[0])


def call_in_parts(body, in_specs, out_specs, out_shape, earlier, part, **options):
    used = len(in_specs)

    def kernel(*refs):
        body(*refs[:used], *refs[used + len(earlier) :])

    return pl.pallas_call(
        kernel,
        grid=(6 // PARTS,),
        in_specs=in_specs + [pl.BlockSpec(memory_space=pl.ANY)] * len(earlier),
        out_specs=out_specs,
        out_shape=out_shape,
        input_output_aliases={used + i: i for i in range(len(earlier))},
        compiler_params=pltpu.CompilerParams(vmem_limit_bytes=VMEM_LIMIT),
        **options,
    )


def columns(part):
    first = part * (6 // PARTS)

    def cols(height, row, off):
        return pl.BlockSpec((height, 128), lambda p: (row, p + first + off))

    taps_at = [
        pl.BlockSpec((3, 128), lambda p, off=off: (0, p + first + off)) for off in (0, 6, 12)
    ]
    return cols, taps_at


def att_fwd(state, projected, taps, earlier, part, rows):
    cols, taps_at = columns(part)
    return call_in_parts(
        att_fwd_kernel,
        [
            pl.BlockSpec(memory_space=pltpu.SMEM),
            cols(8, rows // 8 - 1, 0),
            cols(rows, 1, 0),
            cols(2 * rows, 0, 6),
            cols(2 * rows, 0, 12),
            *taps_at,
        ],
        [cols(rows, 0, 0)] * 3 + [cols(2 * rows, 0, 0)] * 2,
        [
            jax.ShapeDtypeStruct((rows, D), BF),
            jax.ShapeDtypeStruct((rows, D), F32),
            jax.ShapeDtypeStruct((rows, D), BF),
            jax.ShapeDtypeStruct((2 * rows, D), BF),
            jax.ShapeDtypeStruct((2 * rows, D), BF),
        ],
        earlier,
        part,
        cost_estimate=cost(
            2 * 2 * 12 * rows * rows * 1.5 * 256 / PARTS,
            rows * D * 30 / PARTS,
            12 * rows * rows * 1.5 / PARTS,
        ),
        name="att_fwd",
    )(state, projected, projected, projected, projected, taps, taps, taps, *earlier)


def three(x, lane, base):
    hi = x.astype(BF).astype(F32)
    r = x - hi
    mid = r.astype(BF).astype(F32)
    lo = r - mid
    return jnp.where(
        lane == base, hi, jnp.where(lane == base + 1, mid, jnp.where(lane == base + 2, lo, 0.0))
    )


def conv_back(grad, x, taps, mask_one, mask_two):
    height = grad.shape[0]
    one = pltpu.roll(grad, height - 1, 0) * mask_one
    two = pltpu.roll(grad, height - 2, 0) * mask_two
    back = (taps[0:1] * grad + taps[1:2] * one + taps[2:3] * two).astype(BF)
    sums = [jnp.sum(g * x, axis=0, keepdims=True) for g in (grad, one, two)]
    return back, sums


def att_bwd_kernel(
    state_ref, q_ref, k_ref, v_ref, o_ref, l_ref, do_ref, xt_ref, xq_ref, xk_ref, xv_ref,
    tq_ref, tk_ref, tv_ref,
    pq_ref, pt_ref, pk_ref, pv_ref, tg_ref, qa, da, dqs, dks, dvs,
):
    rows = q_ref.shape[0]
    lane = lax.broadcasted_iota(jnp.int32, (1, 128), 1)
    second = state_ref[0] == 2
    do = do_ref[...].astype(F32)
    od = do * o_ref[...].astype(F32)
    qf = q_ref[...].astype(F32) * 0.125
    lv = l_ref[...]
    zero = jnp.zeros((), BF)
    dks[...] = jnp.zeros(dks.shape, F32)
    dvs[...] = jnp.zeros(dvs.shape, F32)
    dqs[...] = jnp.zeros(dqs.shape, F32)
    for h in range(2):
        mine = (lane < 64) if h == 0 else (lane >= 64)
        base = 64 if h == 0 else 0
        ones3 = ((lane >= base) & (lane < base + 3)).astype(BF)
        delta = jnp.sum(jnp.where(mine, od, 0.0), axis=1, keepdims=True)
        qa[...] = jnp.where(mine, qf, three(-lv, lane, base)).astype(BF)
        da[...] = jnp.where(mine, do, three(-delta, lane, base)).astype(BF)

        def part(ks, qs, dos, mask):
            kk = k_ref[ks, :]
            st = dot_nt(jnp.where(mine, kk, ones3), qs)
            dp = dot_nt(jnp.where(mine, v_ref[ks, :], ones3), dos)
            p = jnp.exp(st)
            if mask is not None:
                p = jnp.where(mask, p, 0.0)
            ds = (p * dp).astype(BF)
            dvs[ks, :] += dot(p.astype(BF), jnp.where(mine, dos, zero))
            dks[ks, :] += dot(ds, jnp.where(mine, qs, zero))
            return dot_tn(ds, jnp.where(mine, kk, zero))

        for i in range(rows // QB):
            qs = qa[pl.ds(i * QB, QB), :]
            dos = da[pl.ds(i * QB, QB), :]
            kr = lax.broadcasted_iota(jnp.int32, (QB, QB), 0)
            qr = lax.broadcasted_iota(jnp.int32, (QB, QB), 1)
            dq = part(pl.ds(rows + i * QB, QB), qs, dos, kr <= qr)
            if i > 0:
                dq = dq + part(pl.ds(rows, i * QB), qs, dos, None)
            dqs[pl.ds(8 + i * QB, QB), :] += dq * 0.125

        @pl.when(second)
        def _():
            for i in range(rows // QB):
                rs = pl.ds(i * QB, QB)
                dq = part(pl.ds(0, rows), qa[rs, :], da[rs, :], None)
                dqs[pl.ds(8 + i * QB, QB), :] += dq * 0.125

    one = taps_seen(2 * rows, 0, rows, state_ref[0], 1, 1)
    two = taps_seen(2 * rows, 0, rows, state_ref[0], 2, 2)
    xq = jnp.concatenate([xt_ref[...].astype(F32), xq_ref[...].astype(F32)], 0)
    pq, sq = conv_back(dqs[...], xq, tq_ref[...], one[rows - 8 :], two[rows - 8 :])
    pt_ref[...] = pq[:8]
    pq_ref[...] = pq[8:]
    pk_ref[...], sk = conv_back(dks[...], xk_ref[...].astype(F32), tk_ref[...], one, two)
    pv_ref[...], sv = conv_back(dvs[...], xv_ref[...].astype(F32), tv_ref[...], one, two)
    tg_ref[...] = jnp.zeros(tg_ref.shape, F32)
    for j in range(3):
        for m, s in enumerate((sq, sk, sv)):
            tg_ref[3 * j + m : 3 * j + m + 1, :] = s[j]


def att_bwd(state, mixed, attended, logs, grad, projected, taps, earlier, part, rows):
    cols, taps_at = columns(part)
    own = cols(rows, 0, 0)
    both = cols(2 * rows, 0, 0)
    return call_in_parts(
        att_bwd_kernel,
        [
            pl.BlockSpec(memory_space=pltpu.SMEM),
            own, both, both, own, own, own,
            cols(8, rows // 8 - 1, 0),
            cols(rows, 1, 0),
            cols(2 * rows, 0, 6),
            cols(2 * rows, 0, 12),
            *taps_at,
        ],
        [own, cols(8, 0, 0), both, both, cols(16, 0, 0)],
        [
            jax.ShapeDtypeStruct((rows, D), BF),
            jax.ShapeDtypeStruct((8, D), BF),
            jax.ShapeDtypeStruct((2 * rows, D), BF),
            jax.ShapeDtypeStruct((2 * rows, D), BF),
            jax.ShapeDtypeStruct((16, D), F32),
        ],
        earlier,
        part,
        scratch_shapes=[
            pltpu.VMEM((rows, 128), BF),
            pltpu.VMEM((rows, 128), BF),
            pltpu.VMEM((rows + 8, 128), F32),
            pltpu.VMEM((2 * rows, 128), F32),
            pltpu.VMEM((2 * rows, 128), F32),
        ],
        cost_estimate=cost(
            5 * 2 * 12 * rows * rows * 1.5 * 256 / PARTS,
            rows * D * 40 / PARTS,
            12 * rows * rows * 1.5 / PARTS,
        ),
        name="att_bwd",
    )(state, *mixed, attended, logs, grad, projected, projected, projected, projected,
      taps, taps, taps, *earlier)


def qkv_bwd_kernel(
    core_ref, x_ref, dq_ref, dt_ref, dk_ref, dv_ref, w_ref, gain_ref, gain_two_ref, tg_ref,
    *refs, pieces, blocks,
):
    if pieces:
        send_ref, keep_ref, prev_ref, own_ref, acc, gacc = refs
    else:
        keep_ref, small_ref, prev_ref, own_ref, acc, gacc = refs
    i = pl.program_id(0)
    half = blocks // 2

    @pl.when(i == 0)
    def _():
        acc[...] = jnp.zeros(acc.shape, F32)
        gacc[...] = jnp.zeros(gacc.shape, F32)

    x = x_ref[...].astype(F32)
    hat = x * lax.rsqrt(jnp.mean(x * x, axis=-1, keepdims=True) + norm_eps)
    low = (hat * gain_ref[...]).astype(BF)
    dk = dk_ref[...]
    dv = dv_ref[...]
    gn = dot_nt(dk, w_ref[D : 2 * D, :]) + dot_nt(dv, w_ref[2 * D : 3 * D, :])
    acc[D : 2 * D, :] += dot_tn(low, dk)
    acc[2 * D : 3 * D, :] += dot_tn(low, dv)

    @pl.when(i < half - 1)
    def _():
        prev_ref[...] = gn.astype(BF)
        gacc[0:1, :] += jnp.sum(gn * hat, axis=0, keepdims=True)

    @pl.when(i == half - 1)
    def _():
        dt = dt_ref[...]
        last = gn.shape[0] - 8
        acc[0:D, :] += dot_tn(low[last:], dt)
        full = jnp.concatenate([gn[:last], gn[last:] + dot_nt(dt, w_ref[0:D, :])], 0)
        prev_ref[...] = full.astype(BF)
        gacc[0:1, :] += jnp.sum(full * hat, axis=0, keepdims=True)

    @pl.when(i >= half)
    def _():
        dq = dq_ref[...]
        acc[0:D, :] += dot_tn(low, dq)
        full = gn + dot_nt(dq, w_ref[0:D, :])
        own_ref[...] = full
        gacc[0:1, :] += jnp.sum(full * hat, axis=0, keepdims=True)

    @pl.when(i == blocks - 1)
    def _():
        small = jnp.concatenate(
            [gacc[0:1, :], gain_two_ref[...], tg_ref[0:9, :], jnp.zeros((5, D), F32)], 0
        )
        if pieces:
            core = core_ref[0]
            height = 3 * D // (2 * pieces)
            for j in range(pieces):
                to = pl.ds(j * height, height)
                away = pl.ds(pl.multiple_of((2 * j + 1 - core) * height, 16), height)
                here = pl.ds(pl.multiple_of((2 * j + core) * height, 16), height)
                send_ref[to, :] = acc[away, :].astype(BF)
                keep_ref[to, :] = acc[here, :]
            send_ref[pieces * height :, :] = small.astype(BF)
            keep_ref[pieces * height :, :] = small
        else:
            keep_ref[...] = acc[...].astype(BF)
            small_ref[...] = small


def qkv_bwd(core, x_both, back, wide, gain, gain_two_grad, tap_grads, rows, pieces):
    dq, dt, dk, dv = back
    blocks = 4
    half = blocks // 2
    height = 2 * rows // blocks
    step = pl.BlockSpec((height, D), lambda i: (i, 0))
    late = pl.BlockSpec((height, D), lambda i: (jnp.maximum(i - half, 0), 0))
    early = pl.BlockSpec((height, D), lambda i: (jnp.minimum(i, half - 1), 0))

    def whole(shape):
        return pl.BlockSpec(shape, lambda i: (0, 0))

    if pieces:
        packed = 3 * D // 2 + 16
        outs = [jax.ShapeDtypeStruct((packed, D), BF), jax.ShapeDtypeStruct((packed, D), F32)]
        out_at = [whole((packed, D))] * 2
    else:
        outs = [jax.ShapeDtypeStruct((3 * D, D), BF), jax.ShapeDtypeStruct((16, D), F32)]
        out_at = [whole((3 * D, D)), whole((16, D))]

    def body(*refs):
        qkv_bwd_kernel(*refs, pieces=pieces, blocks=blocks)

    return pl.pallas_call(
        body,
        grid=(blocks,),
        in_specs=[
            pl.BlockSpec(memory_space=pltpu.SMEM),
            step, late, whole((8, D)), step, step, whole((3 * D, D)),
            whole((1, D)), whole((1, D)), whole((16, D)),
        ],
        out_specs=out_at + [early, late],
        out_shape=outs
        + [jax.ShapeDtypeStruct((rows, D), BF), jax.ShapeDtypeStruct((rows, D), F32)],
        scratch_shapes=[pltpu.VMEM((3 * D, D), F32), pltpu.VMEM((8, D), F32)],
        compiler_params=pltpu.CompilerParams(vmem_limit_bytes=VMEM_LIMIT),
        cost_estimate=cost(2 * 2 * D * D * 5 * rows, rows * D * 30),
        name="qkv_bwd",
    )(core, x_both, dq, dt, dk, dv, wide, gain, gain_two_grad, tap_grads)


def merge(index, keep, got, height, taken):
    rows = keep.shape[0]
    out_rows = taken * height + 16 if taken else rows

    def body(index_ref, keep_ref, got_ref, send_ref, stay_ref):
        if not taken:
            total = keep_ref[...] + got_ref[...].astype(F32)
            send_ref[...] = total.astype(BF)
            stay_ref[...] = total
            return
        for j in range(taken):
            to = pl.ds(j * height, height)
            away = pl.ds(pl.multiple_of(index_ref[j] * height, 16), height)
            here = pl.ds(pl.multiple_of(index_ref[taken + j] * height, 16), height)
            send_ref[to, :] = (keep_ref[away, :] + got_ref[away, :].astype(F32)).astype(BF)
            stay_ref[to, :] = keep_ref[here, :] + got_ref[here, :].astype(F32)
        end = keep_ref[rows - 16 :, :] + got_ref[rows - 16 :, :].astype(F32)
        send_ref[taken * height :, :] = end.astype(BF)
        stay_ref[taken * height :, :] = end

    vmem = pl.BlockSpec(memory_space=pltpu.VMEM)
    return pl.pallas_call(
        body,
        in_specs=[pl.BlockSpec(memory_space=pltpu.SMEM), vmem, vmem],
        out_specs=[vmem, vmem],
        out_shape=[
            jax.ShapeDtypeStruct((out_rows, D), BF),
            jax.ShapeDtypeStruct((out_rows, D), F32),
        ],
        compiler_params=pltpu.CompilerParams(vmem_limit_bytes=32 << 20),
        cost_estimate=cost(rows * D, rows * D * 12),
        name="merge",
    )(index, keep, got)


def merge_grid(index, keep, got, taken):
    height = keep.shape[1]

    def body(index_ref, ka_ref, ga_ref, kb_ref, gb_ref, send_ref, stay_ref):
        send_ref[...] = (ka_ref[...].astype(F32) + ga_ref[...].astype(F32)).astype(BF)
        stay_ref[...] = kb_ref[...].astype(F32) + gb_ref[...].astype(F32)

    away = pl.BlockSpec((1, height, D), lambda i, index: (index[i], 0, 0))
    here = pl.BlockSpec((1, height, D), lambda i, index: (index[taken + i], 0, 0))
    step = pl.BlockSpec((1, height, D), lambda i, index: (i, 0, 0))
    return pl.pallas_call(
        body,
        grid_spec=pltpu.PrefetchScalarGridSpec(
            num_scalar_prefetch=1,
            grid=(taken,),
            in_specs=[away, away, here, here],
            out_specs=[step, step],
        ),
        out_shape=[
            jax.ShapeDtypeStruct((taken, height, D), BF),
            jax.ShapeDtypeStruct((taken, height, D), F32),
        ],
        compiler_params=pltpu.CompilerParams(vmem_limit_bytes=32 << 20),
        cost_estimate=cost(taken * height * D * 2, taken * height * D * 16),
        name="merge_grid",
    )(index, keep, got, keep, got)


def arrange(index, one, two, taken):
    half = one.shape[0]
    height = one.shape[1]

    def body(index_ref, one_ref, two_ref, out_ref):
        for i in range(taken):
            at = index_ref[i]

            @pl.when(at < half)
            def _():
                out_ref[i] = one_ref[jnp.minimum(at, half - 1)]

            @pl.when(at >= half)
            def _():
                out_ref[i] = two_ref[jnp.maximum(at - half, 0)]

    vmem = pl.BlockSpec(memory_space=pltpu.VMEM)
    return pl.pallas_call(
        body,
        in_specs=[pl.BlockSpec(memory_space=pltpu.SMEM), vmem, vmem],
        out_specs=vmem,
        out_shape=jax.ShapeDtypeStruct((taken, height, D), BF),
        compiler_params=pltpu.CompilerParams(vmem_limit_bytes=32 << 20),
        cost_estimate=cost(taken * height * D, taken * height * D * 8),
        name="arrange",
    )(index, one, two)


def join(own, got, shared=16):
    rows = own.shape[0]
    body_rows = rows - shared

    def body(own_ref, got_ref, out_ref):
        out_ref[0:body_rows, :] = own_ref[0:body_rows, :]
        out_ref[body_rows : 2 * body_rows, :] = got_ref[0:body_rows, :]
        if shared:
            out_ref[2 * body_rows :, :] = own_ref[body_rows:, :] + got_ref[body_rows:, :]

    vmem = pl.BlockSpec(memory_space=pltpu.VMEM)
    return pl.pallas_call(
        body,
        in_specs=[vmem, vmem],
        out_specs=vmem,
        out_shape=jax.ShapeDtypeStruct((2 * body_rows + shared, D), BF),
        compiler_params=pltpu.CompilerParams(vmem_limit_bytes=32 << 20),
        cost_estimate=cost(rows * D, rows * D * 8),
        name="join",
    )(own, got)


def qkv_fwd_kernel(index_ref, x_ref, *refs, pieces, blocks):
    if pieces:
        own_ref, got_ref, out_ref, small_ref, weight = refs
    else:
        weight, given_ref, out_ref, small_ref = refs
    i = pl.program_id(0)

    @pl.when(i == 0)
    def _():
        if pieces:
            height = 3 * D // (2 * pieces)
            for j in range(pieces):
                at = pl.ds(j * height, height)
                for k, ref in enumerate((own_ref, got_ref)):
                    to = pl.multiple_of(index_ref[k * pieces + j] * height, 16)
                    weight[pl.ds(to, height), :] = ref[at, :]
            end = pl.ds(pieces * height, 16)
            small_ref[...] = own_ref[end, :].astype(F32) + got_ref[end, :].astype(F32)
        else:
            small_ref[...] = given_ref[...]

    x = x_ref[...].astype(F32)
    hat = x * lax.rsqrt(jnp.mean(x * x, axis=-1, keepdims=True) + norm_eps)
    low = (hat * small_ref[0:1, :]).astype(BF)

    @pl.when(i >= blocks // 2 - 1)
    def _():
        out_ref[:, 0:D] = dot(low, weight[0:D, :]).astype(BF)

    out_ref[:, D : 2 * D] = dot(low, weight[D : 2 * D, :]).astype(BF)
    out_ref[:, 2 * D : 3 * D] = dot(low, weight[2 * D : 3 * D, :]).astype(BF)


def qkv_fwd(index, x_both, weights, rows, pieces):
    blocks = 4
    height = 2 * rows // blocks

    def body(*refs):
        qkv_fwd_kernel(*refs, pieces=pieces, blocks=blocks)

    return pl.pallas_call(
        body,
        grid=(blocks,),
        in_specs=[
            pl.BlockSpec(memory_space=pltpu.SMEM),
            pl.BlockSpec((height, D), lambda i: (i, 0)),
            *[pl.BlockSpec(w.shape, lambda i: (0, 0)) for w in weights],
        ],
        out_specs=[
            pl.BlockSpec((height, 3 * D), lambda i: (i, 0)),
            pl.BlockSpec((16, D), lambda i: (0, 0)),
        ]
        + ([pl.BlockSpec((3 * D, D), lambda i: (0, 0))] if pieces else []),
        out_shape=[
            jax.ShapeDtypeStruct((2 * rows, 3 * D), BF),
            jax.ShapeDtypeStruct((16, D), F32),
        ]
        + ([jax.ShapeDtypeStruct((3 * D, D), BF)] if pieces else []),
        compiler_params=pltpu.CompilerParams(vmem_limit_bytes=VMEM_LIMIT),
        cost_estimate=cost(2 * 2 * rows * D * 3 * D, rows * D * 20),
        name="qkv_fwd",
    )(index, x_both, *weights)


def ffn_kernel(
    state_ref, index_ref, x_ref, att_ref, cot_ref, gain_ref, own_ref, got_ref,
    out_ref, gh_ref, ga_ref, gain_grad_ref, away_ref, here_ref,
    hidden, low, total, back, cot, sq, gb, weights, stage_up, stage_down, stage_out, in_sems, sems,
):
    c = pl.program_id(0)
    rows = x_ref.shape[0]
    blocks = [pl.ds(i * QB, QB) for i in range(rows // QB)]
    last = c == pl.num_programs(0) - 1
    core = index_ref[24]

    def fetch(k, j):
        ref = own_ref if k == 0 else got_ref
        to = weights.at[pl.ds(3 * index_ref[12 * k + j], 3)]
        return pltpu.make_async_copy(ref.at[pl.ds(3 * j, 3)], to, in_sems.at[12 * k + j])

    def put(source, group, count, column, sem, wait=False):
        piece = group // 3
        at = (piece // 2) * 3 + group % 3

        def copy(ref):
            to = ref.at[pl.ds(at, count)] if column is None else ref.at[pl.ds(at, count), column]
            return pltpu.make_async_copy(source, to, sems.at[sem])

        if wait:
            copy(here_ref).wait()
            return
        mine = piece % 2 == core

        @pl.when(mine)
        def _():
            copy(here_ref).start()

        @pl.when(jnp.logical_not(mine))
        def _():
            copy(away_ref).start()

    def put_up(i, wait=False):
        start = 0
        k = 0
        while start < 32:
            count = min(3 - (8 + start) % 3, 32 - start)
            put(stage_up.at[i, pl.ds(start, count)], 8 + start, count, i, 20 * i + k, wait)
            start += count
            k += 1

    def put_down(i, wait=False):
        for k in range(8):
            put(stage_down.at[i, pl.ds(k, 1)], 40 + 8 * i + k, 1, None, 20 * i + 12 + k, wait)

    def put_out(wait=False):
        for k in range(8):
            put(stage_out.at[pl.ds(k, 1)], k, 1, None, 80 + k, wait)

    def square(first):
        return weights[first : first + 8].reshape(D, D)

    @pl.when(c == 0)
    def _():
        for k in range(2):
            for j in range(12):
                fetch(k, j).start()
        cot[...] = jnp.where(state_ref[0] > 0, cot_ref[...], jnp.zeros((), BF))
        total[...] = jnp.zeros(total.shape, F32)
        back[...] = jnp.zeros(back.shape, F32)
        for k in range(2):
            for j in range(12):
                fetch(k, j).wait()
        wo = square(0)
        for b in blocks:
            h = x_ref[b, :].astype(F32) + dot(att_ref[b, :], wo)
            hidden[b, :] = h
            hat = h * lax.rsqrt(jnp.mean(h * h, axis=-1, keepdims=True) + norm_eps)
            low[b, :] = (hat * gain_ref[...]).astype(BF)

    up = weights[8:40, c].reshape(D, D)
    down = weights[pl.ds(40 + 8 * c, 8)].reshape(D, D)
    for b in blocks:
        act = jnp.maximum(dot(low[b, :], up), 0.0)
        s = (act * act).astype(BF)
        sq[b, :] = s
        total[b, :] += dot(s, down)
        g = (dot_nt(cot[b, :], down) * 2.0 * act).astype(BF)
        gb[b, :] = g
        back[b, :] += dot_nt(g, up)
    stage_down[c] = dot_tn(sq[...], cot[...]).reshape(8, 4, 24, D).astype(BF)
    stage_up[c] = dot_tn(low[...], gb[...]).reshape(32, 24, D).astype(BF)
    put_down(c)
    put_up(c)

    @pl.when(last)
    def _():
        gain = gain_ref[...]
        wo = square(0)
        sums = jnp.zeros((1, D), F32)
        for b in blocks:
            h = hidden[b, :]
            out_ref[b, :] = (h + total[b, :]).astype(BF)
            factor = lax.rsqrt(jnp.mean(h * h, axis=-1, keepdims=True) + norm_eps)
            hat = h * factor
            g = back[b, :]
            sums = sums + jnp.sum(g * hat, axis=0, keepdims=True)
            weighted = g * gain
            inner = jnp.mean(weighted * hat, axis=-1, keepdims=True)
            grad = cot[b, :].astype(F32) + factor * (weighted - hat * inner)
            gh_ref[b, :] = grad
            grad_low = grad.astype(BF)
            gb[b, :] = grad_low
            ga_ref[b, :] = dot_nt(grad_low, wo).astype(BF)
        gain_grad_ref[...] = sums
        stage_out[...] = dot_tn(att_ref[...], gb[...]).reshape(8, 4, 24, D).astype(BF)
        put_out()
        for i in range(4):
            put_down(i, True)
            put_up(i, True)
        put_out(True)


def ffn(state, index, tokens, attended, out_grad, gain, own, got, rows):
    def whole(shape):
        return pl.BlockSpec(shape, lambda c: (0,) * len(shape), pipeline_mode=pl.Buffered(1))

    act = whole((rows, D))
    held = pl.BlockSpec(memory_space=pl.ANY)
    scalars = pl.BlockSpec(memory_space=pltpu.SMEM)
    half = (36, 4, 24, D)
    return pl.pallas_call(
        ffn_kernel,
        grid=(4,),
        in_specs=[scalars, scalars, act, act, act, whole((1, D)), held, held],
        out_specs=[act, act, act, whole((1, D)), held, held],
        out_shape=[
            jax.ShapeDtypeStruct((rows, D), BF),
            jax.ShapeDtypeStruct((rows, D), F32),
            jax.ShapeDtypeStruct((rows, D), BF),
            jax.ShapeDtypeStruct((1, D), F32),
            jax.ShapeDtypeStruct(half, BF),
            jax.ShapeDtypeStruct(half, BF),
        ],
        scratch_shapes=[
            pltpu.VMEM((rows, D), F32),
            pltpu.VMEM((rows, D), BF),
            pltpu.VMEM((rows, D), F32),
            pltpu.VMEM((rows, D), F32),
            pltpu.VMEM((rows, D), BF),
            pltpu.VMEM((rows, D), BF),
            pltpu.VMEM((rows, D), BF),
            pltpu.VMEM((72, 4, 24, D), BF),
            pltpu.VMEM((4, 32, 24, D), BF),
            pltpu.VMEM((4, 8, 4, 24, D), BF),
            pltpu.VMEM((8, 4, 24, D), BF),
            pltpu.SemaphoreType.DMA((24,)),
            pltpu.SemaphoreType.DMA((88,)),
        ],
        compiler_params=pltpu.CompilerParams(vmem_limit_bytes=60 << 20),
        cost_estimate=cost(2 * rows * D * D * (24 + 3), 2 * 12 * D * D * 2 + rows * D * 16),
        name="ffn",
    )(state, index, tokens, attended, out_grad, gain, own, got)


def shift_flat(block, distance):
    count = lax.axis_size(AXES)
    route = [(i - distance, i) for i in range(count) if 0 <= i - distance < count]
    return lax.ppermute(block, AXES, route)


def shift_ctx(block, distance):
    count = lax.axis_size("ctx")
    route = [(i - distance, i) for i in range(count) if 0 <= i - distance < count]
    return lax.ppermute(block, "ctx", route)


def after(value, *others):
    return lax.optimization_barrier((value, *others))[0]


def swap(block, even_bit, odd_bit):
    count = lax.axis_size(AXES)
    route = [(i, i ^ (odd_bit if i & 1 else even_bit)) for i in range(count)]
    return lax.ppermute(block, AXES, route)


def to_aligned(shard, place, count, delta):
    rows = shard.shape[0]
    lag = delta * (count - 1)
    back = -(-lag // rows)
    if back == 1:
        keep = -(-lag // 8) * 8
        parts = [shift_flat(shard[rows - keep :], 1), shard]
    else:
        keep = back * rows
        parts = [shift_flat(shard, s) for s in range(back, 0, -1)] + [shard]
    joined = jnp.concatenate(parts, 0)
    return lax.dynamic_slice_in_dim(joined, keep - delta * place, rows - delta, 0)


def small_part(shard, place, count, delta):
    rows = shard.shape[0]
    extra = count * delta
    zeros = jnp.zeros((extra, 128), shard.dtype)
    joined = jnp.concatenate([zeros, shard, zeros], 0)
    start = extra + count * (rows - delta) - place * rows
    return lax.dynamic_slice_in_dim(joined, jnp.minimum(start, rows + extra), extra, 0)


def from_aligned(chunk, small, place, count, delta, rows):
    aligned = rows - delta
    ahead = -(-(count * delta) // aligned)
    parts = [chunk]
    if ahead == 1:
        keep = small.shape[0]
        got = shift_flat(chunk[:keep], -1)
        parts.append(jnp.where(place == count - 1, small, got))
    else:
        pad = ahead * aligned - small.shape[0]
        tail = jnp.concatenate([small, jnp.zeros((pad, 128), small.dtype)], 0)
        for s in range(1, ahead + 1):
            got = shift_flat(chunk, -s)
            for e in range(s):
                piece = tail[e * aligned : (e + 1) * aligned]
                got = jnp.where(place == count - s + e, piece, got)
            parts.append(got)
    return lax.dynamic_slice_in_dim(jnp.concatenate(parts, 0), delta * place, rows, 0)


def regroup(block):
    return block.reshape(-1, 24, 4, D).transpose(0, 2, 1, 3)


def ungroup(block):
    return block.reshape(-1, 4, 24, D).transpose(0, 2, 1, 3)


def normalize(values, gain):
    factor = lax.rsqrt(jnp.mean(values * values, axis=-1, keepdims=True) + norm_eps)
    scaled = values * factor
    return (scaled, factor, scaled * gain)


def norm_back(grad_in, scaled, factor, gain):
    weighted = grad_in * gain
    inner_mean = jnp.mean(weighted * scaled, axis=-1, keepdims=True)
    return factor * (weighted - scaled * inner_mean)


def adam_update(master, moment_one, moment_two, gradient, step_count, row_start):
    row_index = row_start + jnp.arange(master.shape[0], dtype=jnp.int32)
    matrix_rows = (4 * D * D + 2 * D * FF) // 128
    out_first = 3 * D * D // 128
    out_last = 4 * D * D // 128
    is_matrix = (row_index < matrix_rows)[:, None]
    is_out = ((row_index >= out_first) & (row_index < out_last))[:, None]
    step_rate = jnp.where(is_matrix, jnp.where(is_out, 0.5, 0.1), 1.0)
    decay_rate = jnp.where(is_matrix, 0.1, 0.0)
    step_value = step_count[0].astype(jnp.float32)
    new_one = 0.9 * moment_one + 0.1 * gradient
    new_two = 0.999 * moment_two + 0.001 * gradient * gradient
    corr_first = 1.0 - jnp.power(0.9, step_value)
    corr_second = 1.0 - jnp.power(0.999, step_value)
    new_weights = master - step_rate * (
        new_one / corr_first / (jnp.sqrt(new_two / corr_second) + 1e-08) + decay_rate * master
    )
    return (new_weights, new_one, new_two)


def shards(tokens, out_grad, positions, master, first_moment, second_moment, step_count):
    rows = tokens.shape[0]
    assert rows == SEQ_MIN
    count = lax.axis_size(AXES)
    place = lax.axis_index(AXES).astype(jnp.int32)
    owned = master.shape[0]
    aligned = (4 * D * D + 2 * D * FF) // 128 // count
    delta = owned - aligned
    height = aligned * 128 // D
    staged = count == 32
    first_place = positions[0]
    state = jnp.where(first_place < 0, 0, jnp.where(first_place >= SEQ_MIN, 2, 1)).astype(jnp.int32)
    state_vec = state[None]

    tokens_before = shift_ctx(tokens, 1)
    chunk = to_aligned(master, place, count, delta).reshape(-1, D)
    if staged:
        group = 3 * place + jnp.arange(3, dtype=jnp.int32)
        in_up = ((group >= 32) & (group < 64))[:, None, None, None]
        chunk = jnp.where(in_up, regroup(chunk), chunk.reshape(3, 4, 24, D)).reshape(-1, D)
    chunk = chunk.astype(BF)
    small = lax.reduce_precision(small_part(master, place, count, delta), 8, 7)
    core = (place & 1)[None]
    x_bit = (place >> 1) & 1
    y_bit = (place >> 2) & 1
    even = (place & 1) == 0
    tokens_both = jnp.concatenate([tokens_before, tokens], 0)
    if staged:
        mine = jnp.concatenate(
            [jnp.where(place < count // 4, chunk, jnp.zeros((), BF)), small.astype(BF).reshape(-1, D)], 0
        )
        mine = mine + swap(mine, 16, 16)
        mine = mine + swap(mine, 8, 8)
        rest = after(chunk, mine)
        mine = join(mine, swap(mine, 2, 4))
        mine = join(mine, swap(mine, 4, 2))
        got = swap(mine, 1, 1)
        z = place >> 3
        rest = join(rest, swap(rest, 16, 16), 0)
        across = swap(rest, 8, 8)
        codes = [z ^ k for k in (1, 2, 3)]
        order = [jnp.where(j == 1, 2, jnp.where(j == 2, 1, j)) for j in codes]
        rest = arrange(
            jnp.stack(order).astype(jnp.int32), rest.reshape(2, height, D), across.reshape(2, height, D), 3
        ).reshape(-1, D)
        across = swap(rest, 2, 4)
        index = []
        late_index = []
        for k in (0, 1):
            turn = even if k == 0 else jnp.logical_not(even)
            for j in range(4):
                near, far = j & 1, j >> 1
                x_of = x_bit ^ jnp.where(turn, near, far)
                y_of = y_bit ^ jnp.where(turn, far, near)
                piece = 4 * y_of + 2 * x_of + (core[0] ^ k)
                index.append(piece)
                late_index += [piece, piece + 8, piece + 16]
        index = jnp.stack(index).astype(jnp.int32)
        late_index = jnp.stack(late_index + [core[0]]).astype(jnp.int32)
        projected, small, in_weight = qkv_fwd(index, tokens_both, (mine, got), rows, 4)
    else:
        wide = lax.all_gather(chunk, AXES, axis=0, tiled=True)
        small = lax.psum(small, AXES)[:96].reshape(-1, D)
        in_weight = wide[: 3 * D]
        projected, small = qkv_fwd(core, tokens_both, (in_weight, small), rows, 0)
        late_index = jnp.arange(25, dtype=jnp.int32) % 24
    gain_first = small[0]
    gain_second = small[1]
    taps = small[2:11].reshape(3, 3 * D)

    forward = []
    if staged:
        rest = join(after(rest, projected), across, 0)
        across = swap(rest, 4, 2)
        forward = att_fwd(after(state_vec, rest), projected, taps, forward, 0, rows)
        forward = att_fwd(state_vec, projected, taps, forward, 1, rows)
        rest = join(after(rest, forward[0]), across, 0)
        across = swap(rest, 1, 1)
        forward = att_fwd(after(state_vec, rest), projected, taps, forward, 2, rows)
        own_weights, got_weights = rest.reshape(36, 4, 24, D), across.reshape(36, 4, 24, D)
    else:
        for part in range(PARTS):
            forward = att_fwd(state_vec, projected, taps, forward, part, rows)
        grouped = jnp.concatenate(
            [
                wide[3 * D : 4 * D].reshape(-1, 4, 24, D),
                regroup(wide[4 * D : 8 * D]),
                wide[8 * D :].reshape(-1, 4, 24, D),
            ],
            0,
        )
        own_weights, got_weights = grouped[:36], grouped[36:]
    attn_low, logs, *mixed = forward

    layer_out, grad_hidden, grad_attended, grad_gain_two, away_grad, here_grad = ffn(
        state_vec, late_index, tokens, attn_low, out_grad, gain_second[None], own_weights, got_weights, rows
    )

    def backward(start, done, part):
        return att_bwd(
            start, mixed, attn_low, logs, grad_attended, projected, taps, done, part, rows
        )

    if staged:
        stay = [jnp.where(even, 2 * j + x_bit, 2 * y_bit + j) for j in range(2)]
        away = [jnp.where(even, 2 * j + 1 - x_bit, 2 * (1 - y_bit) + j) for j in range(2)]
        pick_plane = jnp.stack(away + stay).astype(jnp.int32)
        other = jnp.where(even, y_bit, x_bit)
        pick_line = jnp.stack([1 - other, other]).astype(jnp.int32)

        def of_quarters(pick, held):
            half = pick.shape[0] // 2
            steps = [pick[s * half + j] + held * t for s in range(2) for t in range(3) for j in range(half)]
            return jnp.stack(steps)

        late_keep = here_grad.reshape(12, height, D)
        late_got = swap(away_grad.reshape(12, height, D), 1, 1)
        done = backward(state_vec, [], 0)
        late_send, late_keep = merge_grid(
            after(of_quarters(pick_plane, 4), done[4]), late_keep, late_got, 6
        )
        late_got = swap(late_send, 2, 4)
        done = backward(after(state_vec, late_send), done, 1)
        late_send, late_keep = merge_grid(
            after(of_quarters(pick_line, 2), done[4]), late_keep, late_got, 3
        )
        late_got = swap(late_send, 4, 2)
        done = backward(after(state_vec, late_send), done, 2)
        z_even = (z & 1) == 0
        low_pair = [jnp.where(z_even, 0, 0), jnp.where(z_even, 2, 1)]
        high_pair = [jnp.where(z_even, 0, 0), jnp.where(z_even, 1, 2)]
        pick_z = jnp.stack(low_pair + high_pair).astype(jnp.int32)
        late_send, late_keep = merge_grid(after(pick_z, done[4]), late_keep, late_got, 2)
        late_got = swap(late_send, 8, 8)
        sums_state = after(core, late_send)
    else:
        done = []
        for part in range(PARTS):
            done = backward(state_vec, done, part)
        sums_state = core
    *back, tap_grads = done
    sums = qkv_bwd(
        sums_state, tokens_both, back, in_weight, gain_first[None], grad_gain_two, tap_grads, rows,
        4 if staged else 0,
    )
    grads_before, grad_normed_one = sums[2:]
    from_next = shift_ctx(grads_before, -1)
    scaled_one, factor_one, _ = normalize(tokens.astype(F32), gain_first)
    input_grad = grad_hidden + norm_back(
        grad_normed_one + from_next.astype(F32), scaled_one, factor_one, gain_first
    )

    if staged:
        send, keep = sums[:2]
        got = swap(send, 1, 1)
        high = z >> 1
        pick_last = jnp.stack([1 - high, high]).astype(jnp.int32)
        late_send, late_keep = merge_grid(after(pick_last, send), late_keep, late_got, 1)
        late_got = swap(late_send, 16, 16)
        send, keep = merge(pick_plane, keep, got, height, 2)
        got = swap(send, 2, 4)
        send, keep = merge(pick_line, keep, got, height, 1)
        got = swap(send, 4, 2)
        send, keep = merge(core, keep, got, height, 0)
        got = swap(send, 8, 8)
        send, keep = merge(core, keep, got, height, 0)
        got = swap(send, 16, 16)
        first = keep + got.astype(F32)
        late_chunk = late_keep[0] + late_got[0].astype(F32)
        small_grad = first[height:].reshape(-1, 128)
        late_grad = jnp.where(in_up, ungroup(late_chunk).reshape(3, 4, 24, D), late_chunk.reshape(3, 4, 24, D))
        chunk_grad = jnp.where(place < count // 4, first[:height], late_grad.reshape(-1, D))
    else:
        flat_grad = jnp.stack([here_grad.reshape(12, 3, 4, 24, D), away_grad.reshape(12, 3, 4, 24, D)], 1)
        flat_grad = flat_grad.reshape(72, 4, 24, D)
        wide_grad = jnp.concatenate(
            [
                sums[0],
                flat_grad[:8].reshape(-1, D),
                ungroup(flat_grad[8:40]).reshape(-1, D),
                flat_grad[40:].reshape(-1, D),
            ],
            0,
        )
        chunk_grad = lax.psum_scatter(wide_grad, AXES, scatter_dimension=0, tiled=True).astype(F32)
        used = sums[1].reshape(-1, 128)
        extra = count * delta
        small_grad = jnp.concatenate([used, jnp.zeros((extra - used.shape[0], 128), F32)], 0)
        small_grad = lax.psum(small_grad, AXES)
    gradient = from_aligned(chunk_grad.reshape(-1, 128), small_grad, place, count, delta, owned)
    new_weights, new_one, new_two = adam_update(
        master, first_moment, second_moment, gradient, step_count, place * owned
    )
    return (layer_out, input_grad, new_weights, new_one, new_two, new_weights.astype(BF))


def solution(mesh):
    spread = P(AXES, None)
    return jax.shard_map(
        shards,
        mesh=mesh,
        in_specs=(spread, spread, P(AXES), spread, spread, spread, P()),
        out_specs=(spread,) * 6,
        check_vma=False,
    )
```

```python
import jax
import jax.numpy as jnp
from jax import lax
from jax.experimental import pallas as pl
from jax.experimental.pallas import tpu as pltpu
from jax.sharding import PartitionSpec as P

D = 768
HEADS = 12
HEAD_DIM = 64
FF = 3072
SEQ_MIN = 1024
AXES = ("dp", "ctx")
QB = 256
PARTS = 3
F32 = jnp.float32
BF = jnp.bfloat16
NT = (((1,), (1,)), ((), ()))
TN = (((0,), (0,)), ((), ()))
norm_eps = 1e-06
VMEM_LIMIT = 56 << 20


def dot(left, right):
    return jnp.dot(left, right, preferred_element_type=F32)


def dot_nt(left, right):
    return lax.dot_general(left, right, NT, preferred_element_type=F32)


def dot_tn(left, right):
    return lax.dot_general(left, right, TN, preferred_element_type=F32)


def cost(flops, nbytes, exps=0):
    return pl.CostEstimate(flops=int(flops), bytes_accessed=int(nbytes), transcendentals=int(exps))


def taps_seen(height, start, rows, state, distance, ahead):
    row = lax.broadcasted_iota(jnp.int32, (height, 128), 0) + (start + ahead)
    own = row - rows
    inside = (own >= distance) | ((own < 0) & (row >= distance)) | ((own >= 0) & (state == 2))
    filled = ((own < 0) | (state > 0)) & (row < 2 * rows)
    return (inside & filled).astype(F32)


def conv(x, taps, mask_one, mask_two):
    one = pltpu.roll(x, 1, 0) * mask_one
    two = pltpu.roll(x, 2, 0) * mask_two
    return (taps[0:1] * x + taps[1:2] * one + taps[2:3] * two).astype(BF)


def att_fwd_kernel(
    state_ref, tail_ref, q_ref, k_ref, v_ref, tq_ref, tk_ref, tv_ref,
    o_ref, l_ref, qm_ref, km_ref, vm_ref,
):
    rows = q_ref.shape[0]
    lane = lax.broadcasted_iota(jnp.int32, (1, 128), 1)
    state = state_ref[0]
    second = state == 2
    empty = state == 0
    one = taps_seen(2 * rows, 0, rows, state, 1, 0)
    two = taps_seen(2 * rows, 0, rows, state, 2, 0)
    x = jnp.concatenate([tail_ref[...].astype(F32), q_ref[...].astype(F32)], 0)
    qm_ref[...] = conv(x, tq_ref[...], one[rows - 8 :], two[rows - 8 :])[8:]
    km_ref[...] = conv(k_ref[...].astype(F32), tk_ref[...], one, two)
    vm_ref[...] = conv(v_ref[...].astype(F32), tv_ref[...], one, two)
    for i in range(rows // QB):
        rs = pl.ds(i * QB, QB)
        outs = []
        sums = []
        qf = qm_ref[rs, :].astype(F32) * 0.125
        for h in range(2):
            mine = (lane < 64) if h == 0 else (lane >= 64)
            qh = jnp.where(mine, qf, 0.0).astype(BF)
            nk = (i + 1) * QB
            vh = jnp.where(mine, vm_ref[rows : rows + nk, :], jnp.ones((), BF))
            s = dot_nt(qh, km_ref[rows : rows + nk, :])
            r = lax.broadcasted_iota(jnp.int32, (QB, QB), 0)
            c = lax.broadcasted_iota(jnp.int32, (QB, QB), 1)
            sd = jnp.where(c <= r, s[:, i * QB :], -1e30)
            m = jnp.max(sd, axis=1, keepdims=True)
            if i > 0:
                m = jnp.maximum(m, jnp.max(s[:, : i * QB], axis=1, keepdims=True))
            o = dot(jnp.exp(sd - m).astype(BF), vh[i * QB :])
            if i > 0:
                o = o + dot(jnp.exp(s[:, : i * QB] - m).astype(BF), vh[: i * QB])

            def prev(args):
                o1, m1 = args
                s2 = dot_nt(qh, km_ref[0:rows, :])
                m2 = jnp.maximum(m1, jnp.max(s2, axis=1, keepdims=True))
                p2 = jnp.exp(s2 - m2).astype(BF)
                vph = jnp.where(mine, vm_ref[0:rows, :], jnp.ones((), BF))
                return o1 * jnp.exp(m1 - m2) + dot(p2, vph), m2

            o, m = lax.cond(second, prev, lambda a: a, (o, m))
            outs.append(o / pltpu.roll(o, 64, 1))
            sums.append(m + jnp.log(o))
        res = jnp.where(lane < 64, outs[0], outs[1])
        res = jnp.where(empty, vm_ref[pl.ds(rows + i * QB, QB), :].astype(F32), res)
        o_ref[rs, :] = res.astype(BF)
        l_ref[rs, :] = jnp.where(lane < 64, sums[1], sums[0])


def call_in_parts(body, in_specs, out_specs, out_shape, earlier, part, **options):
    used = len(in_specs)

    def kernel(*refs):
        body(*refs[:used], *refs[used + len(earlier) :])

    return pl.pallas_call(
        kernel,
        grid=(6 // PARTS,),
        in_specs=in_specs + [pl.BlockSpec(memory_space=pl.ANY)] * len(earlier),
        out_specs=out_specs,
        out_shape=out_shape,
        input_output_aliases={used + i: i for i in range(len(earlier))},
        compiler_params=pltpu.CompilerParams(vmem_limit_bytes=VMEM_LIMIT),
        **options,
    )


def columns(part):
    first = part * (6 // PARTS)

    def cols(height, row, off):
        return pl.BlockSpec((height, 128), lambda p: (row, p + first + off))

    taps_at = [
        pl.BlockSpec((3, 128), lambda p, off=off: (0, p + first + off)) for off in (0, 6, 12)
    ]
    return cols, taps_at


def att_fwd(state, projected, taps, earlier, part, rows):
    cols, taps_at = columns(part)
    return call_in_parts(
        att_fwd_kernel,
        [
            pl.BlockSpec(memory_space=pltpu.SMEM),
            cols(8, rows // 8 - 1, 0),
            cols(rows, 1, 0),
            cols(2 * rows, 0, 6),
            cols(2 * rows, 0, 12),
            *taps_at,
        ],
        [cols(rows, 0, 0)] * 3 + [cols(2 * rows, 0, 0)] * 2,
        [
            jax.ShapeDtypeStruct((rows, D), BF),
            jax.ShapeDtypeStruct((rows, D), F32),
            jax.ShapeDtypeStruct((rows, D), BF),
            jax.ShapeDtypeStruct((2 * rows, D), BF),
            jax.ShapeDtypeStruct((2 * rows, D), BF),
        ],
        earlier,
        part,
        cost_estimate=cost(
            2 * 2 * 12 * rows * rows * 1.5 * 256 / PARTS,
            rows * D * 30 / PARTS,
            12 * rows * rows * 1.5 / PARTS,
        ),
        name="att_fwd",
    )(state, projected, projected, projected, projected, taps, taps, taps, *earlier)


def three(x, lane, base):
    hi = x.astype(BF).astype(F32)
    r = x - hi
    mid = r.astype(BF).astype(F32)
    lo = r - mid
    return jnp.where(
        lane == base, hi, jnp.where(lane == base + 1, mid, jnp.where(lane == base + 2, lo, 0.0))
    )


def conv_back(grad, x, taps, mask_one, mask_two):
    height = grad.shape[0]
    one = pltpu.roll(grad, height - 1, 0) * mask_one
    two = pltpu.roll(grad, height - 2, 0) * mask_two
    back = (taps[0:1] * grad + taps[1:2] * one + taps[2:3] * two).astype(BF)
    sums = [jnp.sum(g * x, axis=0, keepdims=True) for g in (grad, one, two)]
    return back, sums


def att_bwd_kernel(
    state_ref, q_ref, k_ref, v_ref, o_ref, l_ref, do_ref, xt_ref, xq_ref, xk_ref, xv_ref,
    tq_ref, tk_ref, tv_ref,
    pq_ref, pt_ref, pk_ref, pv_ref, tg_ref, qa, da, dqs, dks, dvs,
):
    rows = q_ref.shape[0]
    lane = lax.broadcasted_iota(jnp.int32, (1, 128), 1)
    second = state_ref[0] == 2
    do = do_ref[...].astype(F32)
    od = do * o_ref[...].astype(F32)
    qf = q_ref[...].astype(F32) * 0.125
    lv = l_ref[...]
    zero = jnp.zeros((), BF)
    dks[...] = jnp.zeros(dks.shape, F32)
    dvs[...] = jnp.zeros(dvs.shape, F32)
    dqs[...] = jnp.zeros(dqs.shape, F32)
    for h in range(2):
        mine = (lane < 64) if h == 0 else (lane >= 64)
        base = 64 if h == 0 else 0
        ones3 = ((lane >= base) & (lane < base + 3)).astype(BF)
        delta = jnp.sum(jnp.where(mine, od, 0.0), axis=1, keepdims=True)
        qa[...] = jnp.where(mine, qf, three(-lv, lane, base)).astype(BF)
        da[...] = jnp.where(mine, do, three(-delta, lane, base)).astype(BF)

        def part(ks, qs, dos, mask):
            kk = k_ref[ks, :]
            st = dot_nt(jnp.where(mine, kk, ones3), qs)
            dp = dot_nt(jnp.where(mine, v_ref[ks, :], ones3), dos)
            p = jnp.exp(st)
            if mask is not None:
                p = jnp.where(mask, p, 0.0)
            ds = (p * dp).astype(BF)
            dvs[ks, :] += dot(p.astype(BF), jnp.where(mine, dos, zero))
            dks[ks, :] += dot(ds, jnp.where(mine, qs, zero))
            return dot_tn(ds, jnp.where(mine, kk, zero))

        for i in range(rows // QB):
            qs = qa[pl.ds(i * QB, QB), :]
            dos = da[pl.ds(i * QB, QB), :]
            kr = lax.broadcasted_iota(jnp.int32, (QB, QB), 0)
            qr = lax.broadcasted_iota(jnp.int32, (QB, QB), 1)
            dq = part(pl.ds(rows + i * QB, QB), qs, dos, kr <= qr)
            if i > 0:
                dq = dq + part(pl.ds(rows, i * QB), qs, dos, None)
            dqs[pl.ds(8 + i * QB, QB), :] += dq * 0.125

        @pl.when(second)
        def _():
            for i in range(rows // QB):
                rs = pl.ds(i * QB, QB)
                dq = part(pl.ds(0, rows), qa[rs, :], da[rs, :], None)
                dqs[pl.ds(8 + i * QB, QB), :] += dq * 0.125

    one = taps_seen(2 * rows, 0, rows, state_ref[0], 1, 1)
    two = taps_seen(2 * rows, 0, rows, state_ref[0], 2, 2)
    xq = jnp.concatenate([xt_ref[...].astype(F32), xq_ref[...].astype(F32)], 0)
    pq, sq = conv_back(dqs[...], xq, tq_ref[...], one[rows - 8 :], two[rows - 8 :])
    pt_ref[...] = pq[:8]
    pq_ref[...] = pq[8:]
    pk_ref[...], sk = conv_back(dks[...], xk_ref[...].astype(F32), tk_ref[...], one, two)
    pv_ref[...], sv = conv_back(dvs[...], xv_ref[...].astype(F32), tv_ref[...], one, two)
    tg_ref[...] = jnp.zeros(tg_ref.shape, F32)
    for j in range(3):
        for m, s in enumerate((sq, sk, sv)):
            tg_ref[3 * j + m : 3 * j + m + 1, :] = s[j]


def att_bwd(state, mixed, attended, logs, grad, projected, taps, earlier, part, rows):
    cols, taps_at = columns(part)
    own = cols(rows, 0, 0)
    both = cols(2 * rows, 0, 0)
    return call_in_parts(
        att_bwd_kernel,
        [
            pl.BlockSpec(memory_space=pltpu.SMEM),
            own, both, both, own, own, own,
            cols(8, rows // 8 - 1, 0),
            cols(rows, 1, 0),
            cols(2 * rows, 0, 6),
            cols(2 * rows, 0, 12),
            *taps_at,
        ],
        [own, cols(8, 0, 0), both, both, cols(16, 0, 0)],
        [
            jax.ShapeDtypeStruct((rows, D), BF),
            jax.ShapeDtypeStruct((8, D), BF),
            jax.ShapeDtypeStruct((2 * rows, D), BF),
            jax.ShapeDtypeStruct((2 * rows, D), BF),
            jax.ShapeDtypeStruct((16, D), F32),
        ],
        earlier,
        part,
        scratch_shapes=[
            pltpu.VMEM((rows, 128), BF),
            pltpu.VMEM((rows, 128), BF),
            pltpu.VMEM((rows + 8, 128), F32),
            pltpu.VMEM((2 * rows, 128), F32),
            pltpu.VMEM((2 * rows, 128), F32),
        ],
        cost_estimate=cost(
            5 * 2 * 12 * rows * rows * 1.5 * 256 / PARTS,
            rows * D * 40 / PARTS,
            12 * rows * rows * 1.5 / PARTS,
        ),
        name="att_bwd",
    )(state, *mixed, attended, logs, grad, projected, projected, projected, projected,
      taps, taps, taps, *earlier)


def qkv_bwd_kernel(
    core_ref, x_ref, dq_ref, dt_ref, dk_ref, dv_ref, w_ref, gain_ref, gain_two_ref, tg_ref,
    *refs, pieces, blocks,
):
    if pieces:
        send_ref, keep_ref, prev_ref, own_ref, acc, gacc = refs
    else:
        keep_ref, small_ref, prev_ref, own_ref, acc, gacc = refs
    i = pl.program_id(0)
    half = blocks // 2

    @pl.when(i == 0)
    def _():
        acc[...] = jnp.zeros(acc.shape, F32)
        gacc[...] = jnp.zeros(gacc.shape, F32)

    x = x_ref[...].astype(F32)
    hat = x * lax.rsqrt(jnp.mean(x * x, axis=-1, keepdims=True) + norm_eps)
    low = (hat * gain_ref[...]).astype(BF)
    dk = dk_ref[...]
    dv = dv_ref[...]
    gn = dot_nt(dk, w_ref[D : 2 * D, :]) + dot_nt(dv, w_ref[2 * D : 3 * D, :])
    acc[D : 2 * D, :] += dot_tn(low, dk)
    acc[2 * D : 3 * D, :] += dot_tn(low, dv)

    @pl.when(i < half - 1)
    def _():
        prev_ref[...] = gn.astype(BF)
        gacc[0:1, :] += jnp.sum(gn * hat, axis=0, keepdims=True)

    @pl.when(i == half - 1)
    def _():
        dt = dt_ref[...]
        last = gn.shape[0] - 8
        acc[0:D, :] += dot_tn(low[last:], dt)
        full = jnp.concatenate([gn[:last], gn[last:] + dot_nt(dt, w_ref[0:D, :])], 0)
        prev_ref[...] = full.astype(BF)
        gacc[0:1, :] += jnp.sum(full * hat, axis=0, keepdims=True)

    @pl.when(i >= half)
    def _():
        dq = dq_ref[...]
        acc[0:D, :] += dot_tn(low, dq)
        full = gn + dot_nt(dq, w_ref[0:D, :])
        own_ref[...] = full
        gacc[0:1, :] += jnp.sum(full * hat, axis=0, keepdims=True)

    @pl.when(i == blocks - 1)
    def _():
        small = jnp.concatenate(
            [gacc[0:1, :], gain_two_ref[...], tg_ref[0:9, :], jnp.zeros((5, D), F32)], 0
        )
        if pieces:
            core = core_ref[0]
            height = 3 * D // (2 * pieces)
            for j in range(pieces):
                to = pl.ds(j * height, height)
                away = pl.ds(pl.multiple_of((2 * j + 1 - core) * height, 16), height)
                here = pl.ds(pl.multiple_of((2 * j + core) * height, 16), height)
                send_ref[to, :] = acc[away, :].astype(BF)
                keep_ref[to, :] = acc[here, :]
            send_ref[pieces * height :, :] = small.astype(BF)
            keep_ref[pieces * height :, :] = small
        else:
            keep_ref[...] = acc[...].astype(BF)
            small_ref[...] = small


def qkv_bwd(core, x_both, back, wide, gain, gain_two_grad, tap_grads, rows, pieces):
    dq, dt, dk, dv = back
    blocks = 4
    half = blocks // 2
    height = 2 * rows // blocks
    step = pl.BlockSpec((height, D), lambda i: (i, 0))
    late = pl.BlockSpec((height, D), lambda i: (jnp.maximum(i - half, 0), 0))
    early = pl.BlockSpec((height, D), lambda i: (jnp.minimum(i, half - 1), 0))

    def whole(shape):
        return pl.BlockSpec(shape, lambda i: (0, 0))

    if pieces:
        packed = 3 * D // 2 + 16
        outs = [jax.ShapeDtypeStruct((packed, D), BF), jax.ShapeDtypeStruct((packed, D), F32)]
        out_at = [whole((packed, D))] * 2
    else:
        outs = [jax.ShapeDtypeStruct((3 * D, D), BF), jax.ShapeDtypeStruct((16, D), F32)]
        out_at = [whole((3 * D, D)), whole((16, D))]

    def body(*refs):
        qkv_bwd_kernel(*refs, pieces=pieces, blocks=blocks)

    return pl.pallas_call(
        body,
        grid=(blocks,),
        in_specs=[
            pl.BlockSpec(memory_space=pltpu.SMEM),
            step, late, whole((8, D)), step, step, whole((3 * D, D)),
            whole((1, D)), whole((1, D)), whole((16, D)),
        ],
        out_specs=out_at + [early, late],
        out_shape=outs
        + [jax.ShapeDtypeStruct((rows, D), BF), jax.ShapeDtypeStruct((rows, D), F32)],
        scratch_shapes=[pltpu.VMEM((3 * D, D), F32), pltpu.VMEM((8, D), F32)],
        compiler_params=pltpu.CompilerParams(vmem_limit_bytes=VMEM_LIMIT),
        cost_estimate=cost(2 * 2 * D * D * 5 * rows, rows * D * 30),
        name="qkv_bwd",
    )(core, x_both, dq, dt, dk, dv, wide, gain, gain_two_grad, tap_grads)


def merge(index, keep, got, height, taken):
    rows = keep.shape[0]
    out_rows = taken * height + 16 if taken else rows

    def body(index_ref, keep_ref, got_ref, send_ref, stay_ref):
        if not taken:
            total = keep_ref[...] + got_ref[...].astype(F32)
            send_ref[...] = total.astype(BF)
            stay_ref[...] = total
            return
        for j in range(taken):
            to = pl.ds(j * height, height)
            away = pl.ds(pl.multiple_of(index_ref[j] * height, 16), height)
            here = pl.ds(pl.multiple_of(index_ref[taken + j] * height, 16), height)
            send_ref[to, :] = (keep_ref[away, :] + got_ref[away, :].astype(F32)).astype(BF)
            stay_ref[to, :] = keep_ref[here, :] + got_ref[here, :].astype(F32)
        end = keep_ref[rows - 16 :, :] + got_ref[rows - 16 :, :].astype(F32)
        send_ref[taken * height :, :] = end.astype(BF)
        stay_ref[taken * height :, :] = end

    vmem = pl.BlockSpec(memory_space=pltpu.VMEM)
    return pl.pallas_call(
        body,
        in_specs=[pl.BlockSpec(memory_space=pltpu.SMEM), vmem, vmem],
        out_specs=[vmem, vmem],
        out_shape=[
            jax.ShapeDtypeStruct((out_rows, D), BF),
            jax.ShapeDtypeStruct((out_rows, D), F32),
        ],
        compiler_params=pltpu.CompilerParams(vmem_limit_bytes=32 << 20),
        cost_estimate=cost(rows * D, rows * D * 12),
        name="merge",
    )(index, keep, got)


def merge_grid(index, keep, got, taken):
    height = keep.shape[1]

    def body(index_ref, ka_ref, ga_ref, kb_ref, gb_ref, send_ref, stay_ref):
        send_ref[...] = (ka_ref[...].astype(F32) + ga_ref[...].astype(F32)).astype(BF)
        stay_ref[...] = kb_ref[...].astype(F32) + gb_ref[...].astype(F32)

    away = pl.BlockSpec((1, height, D), lambda i, index: (index[i], 0, 0))
    here = pl.BlockSpec((1, height, D), lambda i, index: (index[taken + i], 0, 0))
    step = pl.BlockSpec((1, height, D), lambda i, index: (i, 0, 0))
    return pl.pallas_call(
        body,
        grid_spec=pltpu.PrefetchScalarGridSpec(
            num_scalar_prefetch=1,
            grid=(taken,),
            in_specs=[away, away, here, here],
            out_specs=[step, step],
        ),
        out_shape=[
            jax.ShapeDtypeStruct((taken, height, D), BF),
            jax.ShapeDtypeStruct((taken, height, D), F32),
        ],
        compiler_params=pltpu.CompilerParams(vmem_limit_bytes=32 << 20),
        cost_estimate=cost(taken * height * D * 2, taken * height * D * 16),
        name="merge_grid",
    )(index, keep, got, keep, got)


def arrange(index, one, two, taken):
    half = one.shape[0]
    height = one.shape[1]

    def body(index_ref, one_ref, two_ref, out_ref):
        for i in range(taken):
            at = index_ref[i]

            @pl.when(at < half)
            def _():
                out_ref[i] = one_ref[jnp.minimum(at, half - 1)]

            @pl.when(at >= half)
            def _():
                out_ref[i] = two_ref[jnp.maximum(at - half, 0)]

    vmem = pl.BlockSpec(memory_space=pltpu.VMEM)
    return pl.pallas_call(
        body,
        in_specs=[pl.BlockSpec(memory_space=pltpu.SMEM), vmem, vmem],
        out_specs=vmem,
        out_shape=jax.ShapeDtypeStruct((taken, height, D), BF),
        compiler_params=pltpu.CompilerParams(vmem_limit_bytes=32 << 20),
        cost_estimate=cost(taken * height * D, taken * height * D * 8),
        name="arrange",
    )(index, one, two)


def join(own, got, shared=16):
    rows = own.shape[0]
    body_rows = rows - shared

    def body(own_ref, got_ref, out_ref):
        out_ref[0:body_rows, :] = own_ref[0:body_rows, :]
        out_ref[body_rows : 2 * body_rows, :] = got_ref[0:body_rows, :]
        if shared:
            out_ref[2 * body_rows :, :] = own_ref[body_rows:, :] + got_ref[body_rows:, :]

    vmem = pl.BlockSpec(memory_space=pltpu.VMEM)
    return pl.pallas_call(
        body,
        in_specs=[vmem, vmem],
        out_specs=vmem,
        out_shape=jax.ShapeDtypeStruct((2 * body_rows + shared, D), BF),
        compiler_params=pltpu.CompilerParams(vmem_limit_bytes=32 << 20),
        cost_estimate=cost(rows * D, rows * D * 8),
        name="join",
    )(own, got)


def qkv_fwd_kernel(index_ref, x_ref, *refs, pieces, blocks):
    if pieces:
        own_ref, got_ref, out_ref, small_ref, weight = refs
    else:
        weight, given_ref, out_ref, small_ref = refs
    i = pl.program_id(0)

    @pl.when(i == 0)
    def _():
        if pieces:
            height = 3 * D // (2 * pieces)
            for j in range(pieces):
                at = pl.ds(j * height, height)
                for k, ref in enumerate((own_ref, got_ref)):
                    to = pl.multiple_of(index_ref[k * pieces + j] * height, 16)
                    weight[pl.ds(to, height), :] = ref[at, :]
            end = pl.ds(pieces * height, 16)
            small_ref[...] = own_ref[end, :].astype(F32) + got_ref[end, :].astype(F32)
        else:
            small_ref[...] = given_ref[...]

    x = x_ref[...].astype(F32)
    hat = x * lax.rsqrt(jnp.mean(x * x, axis=-1, keepdims=True) + norm_eps)
    low = (hat * small_ref[0:1, :]).astype(BF)

    @pl.when(i >= blocks // 2 - 1)
    def _():
        out_ref[:, 0:D] = dot(low, weight[0:D, :]).astype(BF)

    out_ref[:, D : 2 * D] = dot(low, weight[D : 2 * D, :]).astype(BF)
    out_ref[:, 2 * D : 3 * D] = dot(low, weight[2 * D : 3 * D, :]).astype(BF)


def qkv_fwd(index, x_both, weights, rows, pieces):
    blocks = 4
    height = 2 * rows // blocks

    def body(*refs):
        qkv_fwd_kernel(*refs, pieces=pieces, blocks=blocks)

    return pl.pallas_call(
        body,
        grid=(blocks,),
        in_specs=[
            pl.BlockSpec(memory_space=pltpu.SMEM),
            pl.BlockSpec((height, D), lambda i: (i, 0)),
            *[pl.BlockSpec(w.shape, lambda i: (0, 0)) for w in weights],
        ],
        out_specs=[
            pl.BlockSpec((height, 3 * D), lambda i: (i, 0)),
            pl.BlockSpec((16, D), lambda i: (0, 0)),
        ]
        + ([pl.BlockSpec((3 * D, D), lambda i: (0, 0))] if pieces else []),
        out_shape=[
            jax.ShapeDtypeStruct((2 * rows, 3 * D), BF),
            jax.ShapeDtypeStruct((16, D), F32),
        ]
        + ([jax.ShapeDtypeStruct((3 * D, D), BF)] if pieces else []),
        compiler_params=pltpu.CompilerParams(vmem_limit_bytes=VMEM_LIMIT),
        cost_estimate=cost(2 * 2 * rows * D * 3 * D, rows * D * 20),
        name="qkv_fwd",
    )(index, x_both, *weights)


def ffn_kernel(
    state_ref, index_ref, x_ref, att_ref, cot_ref, gain_ref, own_ref, got_ref,
    out_ref, gh_ref, ga_ref, gain_grad_ref, away_ref, here_ref,
    hidden, low, total, back, cot, sq, gb, weights, stage_up, stage_down, stage_out, in_sems, sems,
):
    c = pl.program_id(0)
    rows = x_ref.shape[0]
    blocks = [pl.ds(i * QB, QB) for i in range(rows // QB)]
    last = c == pl.num_programs(0) - 1
    core = index_ref[24]

    def fetch(k, j):
        ref = own_ref if k == 0 else got_ref
        to = weights.at[pl.ds(3 * index_ref[12 * k + j], 3)]
        return pltpu.make_async_copy(ref.at[pl.ds(3 * j, 3)], to, in_sems.at[12 * k + j])

    def put(source, group, count, column, sem, wait=False):
        piece = group // 3
        at = (piece // 2) * 3 + group % 3

        def copy(ref):
            to = ref.at[pl.ds(at, count)] if column is None else ref.at[pl.ds(at, count), column]
            return pltpu.make_async_copy(source, to, sems.at[sem])

        if wait:
            copy(here_ref).wait()
            return
        mine = piece % 2 == core

        @pl.when(mine)
        def _():
            copy(here_ref).start()

        @pl.when(jnp.logical_not(mine))
        def _():
            copy(away_ref).start()

    def put_up(i, wait=False):
        start = 0
        k = 0
        while start < 32:
            count = min(3 - (8 + start) % 3, 32 - start)
            put(stage_up.at[i, pl.ds(start, count)], 8 + start, count, i, 20 * i + k, wait)
            start += count
            k += 1

    def put_down(i, wait=False):
        for k in range(8):
            put(stage_down.at[i, pl.ds(k, 1)], 40 + 8 * i + k, 1, None, 20 * i + 12 + k, wait)

    def put_out(wait=False):
        for k in range(8):
            put(stage_out.at[pl.ds(k, 1)], k, 1, None, 80 + k, wait)

    def square(first):
        return weights[first : first + 8].reshape(D, D)

    @pl.when(c == 0)
    def _():
        for k in range(2):
            for j in range(12):
                fetch(k, j).start()
        cot[...] = jnp.where(state_ref[0] > 0, cot_ref[...], jnp.zeros((), BF))
        total[...] = jnp.zeros(total.shape, F32)
        back[...] = jnp.zeros(back.shape, F32)
        for k in range(2):
            for j in range(12):
                fetch(k, j).wait()
        wo = square(0)
        for b in blocks:
            h = x_ref[b, :].astype(F32) + dot(att_ref[b, :], wo)
            hidden[b, :] = h
            hat = h * lax.rsqrt(jnp.mean(h * h, axis=-1, keepdims=True) + norm_eps)
            low[b, :] = (hat * gain_ref[...]).astype(BF)

    up = weights[8:40, c].reshape(D, D)
    down = weights[pl.ds(40 + 8 * c, 8)].reshape(D, D)
    for b in blocks:
        act = jnp.maximum(dot(low[b, :], up), 0.0)
        s = (act * act).astype(BF)
        sq[b, :] = s
        total[b, :] += dot(s, down)
        g = (dot_nt(cot[b, :], down) * 2.0 * act).astype(BF)
        gb[b, :] = g
        back[b, :] += dot_nt(g, up)
    stage_down[c] = dot_tn(sq[...], cot[...]).reshape(8, 4, 24, D).astype(BF)
    stage_up[c] = dot_tn(low[...], gb[...]).reshape(32, 24, D).astype(BF)
    put_down(c)
    put_up(c)

    @pl.when(last)
    def _():
        gain = gain_ref[...]
        wo = square(0)
        sums = jnp.zeros((1, D), F32)
        for b in blocks:
            h = hidden[b, :]
            out_ref[b, :] = (h + total[b, :]).astype(BF)
            factor = lax.rsqrt(jnp.mean(h * h, axis=-1, keepdims=True) + norm_eps)
            hat = h * factor
            g = back[b, :]
            sums = sums + jnp.sum(g * hat, axis=0, keepdims=True)
            weighted = g * gain
            inner = jnp.mean(weighted * hat, axis=-1, keepdims=True)
            grad = cot[b, :].astype(F32) + factor * (weighted - hat * inner)
            gh_ref[b, :] = grad
            grad_low = grad.astype(BF)
            gb[b, :] = grad_low
            ga_ref[b, :] = dot_nt(grad_low, wo).astype(BF)
        gain_grad_ref[...] = sums
        stage_out[...] = dot_tn(att_ref[...], gb[...]).reshape(8, 4, 24, D).astype(BF)
        put_out()
        for i in range(4):
            put_down(i, True)
            put_up(i, True)
        put_out(True)


def ffn(state, index, tokens, attended, out_grad, gain, own, got, rows):
    def whole(shape):
        return pl.BlockSpec(shape, lambda c: (0,) * len(shape), pipeline_mode=pl.Buffered(1))

    act = whole((rows, D))
    held = pl.BlockSpec(memory_space=pl.ANY)
    scalars = pl.BlockSpec(memory_space=pltpu.SMEM)
    half = (36, 4, 24, D)
    return pl.pallas_call(
        ffn_kernel,
        grid=(4,),
        in_specs=[scalars, scalars, act, act, act, whole((1, D)), held, held],
        out_specs=[act, act, act, whole((1, D)), held, held],
        out_shape=[
            jax.ShapeDtypeStruct((rows, D), BF),
            jax.ShapeDtypeStruct((rows, D), F32),
            jax.ShapeDtypeStruct((rows, D), BF),
            jax.ShapeDtypeStruct((1, D), F32),
            jax.ShapeDtypeStruct(half, BF),
            jax.ShapeDtypeStruct(half, BF),
        ],
        scratch_shapes=[
            pltpu.VMEM((rows, D), F32),
            pltpu.VMEM((rows, D), BF),
            pltpu.VMEM((rows, D), F32),
            pltpu.VMEM((rows, D), F32),
            pltpu.VMEM((rows, D), BF),
            pltpu.VMEM((rows, D), BF),
            pltpu.VMEM((rows, D), BF),
            pltpu.VMEM((72, 4, 24, D), BF),
            pltpu.VMEM((4, 32, 24, D), BF),
            pltpu.VMEM((4, 8, 4, 24, D), BF),
            pltpu.VMEM((8, 4, 24, D), BF),
            pltpu.SemaphoreType.DMA((24,)),
            pltpu.SemaphoreType.DMA((88,)),
        ],
        compiler_params=pltpu.CompilerParams(vmem_limit_bytes=60 << 20),
        cost_estimate=cost(2 * rows * D * D * (24 + 3), 2 * 12 * D * D * 2 + rows * D * 16),
        name="ffn",
    )(state, index, tokens, attended, out_grad, gain, own, got)


def shift_flat(block, distance):
    count = lax.axis_size(AXES)
    route = [(i - distance, i) for i in range(count) if 0 <= i - distance < count]
    return lax.ppermute(block, AXES, route)


def shift_ctx(block, distance):
    count = lax.axis_size("ctx")
    route = [(i - distance, i) for i in range(count) if 0 <= i - distance < count]
    return lax.ppermute(block, "ctx", route)


def after(value, *others):
    return lax.optimization_barrier((value, *others))[0]


def swap(block, even_bit, odd_bit, planes=None):
    count = lax.axis_size(AXES)
    route = [
        (i, i ^ (odd_bit if i & 1 else even_bit))
        for i in range(count)
        if planes is None or i >> 3 in planes
    ]
    return lax.ppermute(block, AXES, route)


def to_aligned(shard, place, count, delta):
    rows = shard.shape[0]
    lag = delta * (count - 1)
    back = -(-lag // rows)
    if back == 1:
        keep = -(-lag // 8) * 8
        parts = [shift_flat(shard[rows - keep :], 1), shard]
    else:
        keep = back * rows
        parts = [shift_flat(shard, s) for s in range(back, 0, -1)] + [shard]
    joined = jnp.concatenate(parts, 0)
    return lax.dynamic_slice_in_dim(joined, keep - delta * place, rows - delta, 0)


def small_part(shard, place, count, delta):
    rows = shard.shape[0]
    extra = count * delta
    zeros = jnp.zeros((extra, 128), shard.dtype)
    joined = jnp.concatenate([zeros, shard, zeros], 0)
    start = extra + count * (rows - delta) - place * rows
    return lax.dynamic_slice_in_dim(joined, jnp.minimum(start, rows + extra), extra, 0)


def from_aligned(chunk, small, place, count, delta, rows):
    aligned = rows - delta
    ahead = -(-(count * delta) // aligned)
    parts = [chunk]
    if ahead == 1:
        keep = small.shape[0]
        got = shift_flat(chunk[:keep], -1)
        parts.append(jnp.where(place == count - 1, small, got))
    else:
        pad = ahead * aligned - small.shape[0]
        tail = jnp.concatenate([small, jnp.zeros((pad, 128), small.dtype)], 0)
        for s in range(1, ahead + 1):
            got = shift_flat(chunk, -s)
            for e in range(s):
                piece = tail[e * aligned : (e + 1) * aligned]
                got = jnp.where(place == count - s + e, piece, got)
            parts.append(got)
    return lax.dynamic_slice_in_dim(jnp.concatenate(parts, 0), delta * place, rows, 0)


def regroup(block):
    return block.reshape(-1, 24, 4, D).transpose(0, 2, 1, 3)


def ungroup(block):
    return block.reshape(-1, 4, 24, D).transpose(0, 2, 1, 3)


def normalize(values, gain):
    factor = lax.rsqrt(jnp.mean(values * values, axis=-1, keepdims=True) + norm_eps)
    scaled = values * factor
    return (scaled, factor, scaled * gain)


def norm_back(grad_in, scaled, factor, gain):
    weighted = grad_in * gain
    inner_mean = jnp.mean(weighted * scaled, axis=-1, keepdims=True)
    return factor * (weighted - scaled * inner_mean)


def adam_update(master, moment_one, moment_two, gradient, step_count, row_start):
    row_index = row_start + jnp.arange(master.shape[0], dtype=jnp.int32)
    matrix_rows = (4 * D * D + 2 * D * FF) // 128
    out_first = 3 * D * D // 128
    out_last = 4 * D * D // 128
    is_matrix = (row_index < matrix_rows)[:, None]
    is_out = ((row_index >= out_first) & (row_index < out_last))[:, None]
    step_rate = jnp.where(is_matrix, jnp.where(is_out, 0.5, 0.1), 1.0)
    decay_rate = jnp.where(is_matrix, 0.1, 0.0)
    step_value = step_count[0].astype(jnp.float32)
    new_one = 0.9 * moment_one + 0.1 * gradient
    new_two = 0.999 * moment_two + 0.001 * gradient * gradient
    corr_first = 1.0 - jnp.power(0.9, step_value)
    corr_second = 1.0 - jnp.power(0.999, step_value)
    new_weights = master - step_rate * (
        new_one / corr_first / (jnp.sqrt(new_two / corr_second) + 1e-08) + decay_rate * master
    )
    return (new_weights, new_one, new_two)


def shards(tokens, out_grad, positions, master, first_moment, second_moment, step_count):
    rows = tokens.shape[0]
    assert rows == SEQ_MIN
    count = lax.axis_size(AXES)
    place = lax.axis_index(AXES).astype(jnp.int32)
    owned = master.shape[0]
    aligned = (4 * D * D + 2 * D * FF) // 128 // count
    delta = owned - aligned
    height = aligned * 128 // D
    staged = count == 32
    first_place = positions[0]
    state = jnp.where(first_place < 0, 0, jnp.where(first_place >= SEQ_MIN, 2, 1)).astype(jnp.int32)
    state_vec = state[None]

    tokens_before = shift_ctx(tokens, 1)
    chunk = to_aligned(master, place, count, delta).reshape(-1, D)
    if staged:
        group = 3 * place + jnp.arange(3, dtype=jnp.int32)
        in_up = ((group >= 32) & (group < 64))[:, None, None, None]
        chunk = jnp.where(in_up, regroup(chunk), chunk.reshape(3, 4, 24, D)).reshape(-1, D)
    chunk = chunk.astype(BF)
    small = lax.reduce_precision(small_part(master, place, count, delta), 8, 7)
    core = (place & 1)[None]
    x_bit = (place >> 1) & 1
    y_bit = (place >> 2) & 1
    even = (place & 1) == 0
    tokens_both = jnp.concatenate([tokens_before, tokens], 0)
    if staged:
        mine = jnp.concatenate(
            [jnp.where(place < count // 4, chunk, jnp.zeros((), BF)), small.astype(BF).reshape(-1, D)], 0
        )
        mine = mine + swap(mine, 16, 16, (0, 3))
        mine = mine + swap(mine, 8, 8)
        rest = after(chunk, mine)
        mine = join(mine, swap(mine, 2, 4))
        mine = join(mine, swap(mine, 4, 2))
        got = swap(mine, 1, 1)
        z = place >> 3
        rest = join(rest, swap(rest, 16, 16, (1, 2, 3)), 0)
        across = swap(rest, 8, 8)
        index = []
        late_index = []
        for k in (0, 1):
            turn = even if k == 0 else jnp.logical_not(even)
            for j in range(4):
                near, far = j & 1, j >> 1
                x_of = x_bit ^ jnp.where(turn, near, far)
                y_of = y_bit ^ jnp.where(turn, far, near)
                piece = 4 * y_of + 2 * x_of + (core[0] ^ k)
                index.append(piece)
                late_index += [piece, piece + 8, piece + 16]
        index = jnp.stack(index).astype(jnp.int32)
        late_index = jnp.stack(late_index + [core[0]]).astype(jnp.int32)
        projected, small, in_weight = qkv_fwd(index, tokens_both, (mine, got), rows, 4)
        codes = [z ^ k for k in (1, 2, 3)]
        order = [jnp.where(j == 1, 2, jnp.where(j == 2, 1, j)) for j in codes]
        rest = arrange(
            after(jnp.stack(order).astype(jnp.int32), projected), rest.reshape(2, height, D), across.reshape(2, height, D), 3
        ).reshape(-1, D)
        across = swap(rest, 2, 4)
    else:
        wide = lax.all_gather(chunk, AXES, axis=0, tiled=True)
        small = lax.psum(small, AXES)[:96].reshape(-1, D)
        in_weight = wide[: 3 * D]
        projected, small = qkv_fwd(core, tokens_both, (in_weight, small), rows, 0)
        late_index = jnp.arange(25, dtype=jnp.int32) % 24
    gain_first = small[0]
    gain_second = small[1]
    taps = small[2:11].reshape(3, 3 * D)

    forward = []
    if staged:
        forward = att_fwd(after(state_vec, rest), projected, taps, forward, 0, rows)
        rest = join(after(rest, forward[0]), across, 0)
        across = swap(rest, 4, 2)
        forward = att_fwd(after(state_vec, rest), projected, taps, forward, 1, rows)
        rest = join(after(rest, forward[0]), across, 0)
        across = swap(rest, 1, 1)
        forward = att_fwd(after(state_vec, rest), projected, taps, forward, 2, rows)
        own_weights, got_weights = rest.reshape(36, 4, 24, D), across.reshape(36, 4, 24, D)
    else:
        for part in range(PARTS):
            forward = att_fwd(state_vec, projected, taps, forward, part, rows)
        grouped = jnp.concatenate(
            [
                wide[3 * D : 4 * D].reshape(-1, 4, 24, D),
                regroup(wide[4 * D : 8 * D]),
                wide[8 * D :].reshape(-1, 4, 24, D),
            ],
            0,
        )
        own_weights, got_weights = grouped[:36], grouped[36:]
    attn_low, logs, *mixed = forward

    layer_out, grad_hidden, grad_attended, grad_gain_two, away_grad, here_grad = ffn(
        state_vec, late_index, tokens, attn_low, out_grad, gain_second[None], own_weights, got_weights, rows
    )

    def backward(start, done, part):
        return att_bwd(
            start, mixed, attn_low, logs, grad_attended, projected, taps, done, part, rows
        )

    if staged:
        stay = [jnp.where(even, 2 * j + x_bit, 2 * y_bit + j) for j in range(2)]
        away = [jnp.where(even, 2 * j + 1 - x_bit, 2 * (1 - y_bit) + j) for j in range(2)]
        pick_plane = jnp.stack(away + stay).astype(jnp.int32)
        other = jnp.where(even, y_bit, x_bit)
        pick_line = jnp.stack([1 - other, other]).astype(jnp.int32)

        def of_quarters(pick, held):
            half = pick.shape[0] // 2
            steps = [pick[s * half + j] + held * t for s in range(2) for t in range(3) for j in range(half)]
            return jnp.stack(steps)

        late_keep = here_grad.reshape(12, height, D)
        late_got = swap(away_grad.reshape(12, height, D), 1, 1)
        done = backward(state_vec, [], 0)
        late_send, late_keep = merge_grid(
            after(of_quarters(pick_plane, 4), done[4]), late_keep, late_got, 6
        )
        late_got = swap(late_send, 2, 4)
        done = backward(after(state_vec, late_send), done, 1)
        late_send, late_keep = merge_grid(
            after(of_quarters(pick_line, 2), done[4]), late_keep, late_got, 3
        )
        late_got = swap(late_send, 4, 2)
        done = backward(after(state_vec, late_send), done, 2)
        z_even = (z & 1) == 0
        low_pair = [jnp.where(z_even, 0, 0), jnp.where(z_even, 2, 1)]
        high_pair = [jnp.where(z_even, 0, 0), jnp.where(z_even, 1, 2)]
        pick_z = jnp.stack(low_pair + high_pair).astype(jnp.int32)
        late_send, late_keep = merge_grid(after(pick_z, done[4]), late_keep, late_got, 2)
        late_got = swap(late_send, 8, 8)
        sums_state = after(core, late_send)
    else:
        done = []
        for part in range(PARTS):
            done = backward(state_vec, done, part)
        sums_state = core
    *back, tap_grads = done
    sums = qkv_bwd(
        sums_state, tokens_both, back, in_weight, gain_first[None], grad_gain_two, tap_grads, rows,
        4 if staged else 0,
    )
    grads_before, grad_normed_one = sums[2:]
    from_next = shift_ctx(grads_before, -1)
    scaled_one, factor_one, _ = normalize(tokens.astype(F32), gain_first)
    input_grad = grad_hidden + norm_back(
        grad_normed_one + from_next.astype(F32), scaled_one, factor_one, gain_first
    )

    if staged:
        send, keep = sums[:2]
        high = z >> 1
        pick_last = jnp.stack([1 - high, high]).astype(jnp.int32)
        late_send, late_keep = merge_grid(after(pick_last, send), late_keep, late_got, 1)
        late_got = swap(late_send, 16, 16, (0, 1, 3))
        got = swap(after(send, late_send), 1, 1)
        send, keep = merge(pick_plane, keep, got, height, 2)
        got = swap(send, 2, 4)
        send, keep = merge(pick_line, keep, got, height, 1)
        got = swap(send, 4, 2)
        send, keep = merge(core, keep, got, height, 0)
        got = swap(send, 8, 8)
        late_chunk = late_keep[0] + late_got[0].astype(F32)
        send, keep = merge(after(core, input_grad, late_chunk), keep, got, height, 0)
        got = swap(send, 16, 16, (1, 2))
        first = keep + got.astype(F32)
        small_grad = first[height:].reshape(-1, 128)
        late_grad = jnp.where(in_up, ungroup(late_chunk).reshape(3, 4, 24, D), late_chunk.reshape(3, 4, 24, D))
        chunk_grad = jnp.where(place < count // 4, first[:height], late_grad.reshape(-1, D))
    else:
        flat_grad = jnp.stack([here_grad.reshape(12, 3, 4, 24, D), away_grad.reshape(12, 3, 4, 24, D)], 1)
        flat_grad = flat_grad.reshape(72, 4, 24, D)
        wide_grad = jnp.concatenate(
            [
                sums[0],
                flat_grad[:8].reshape(-1, D),
                ungroup(flat_grad[8:40]).reshape(-1, D),
                flat_grad[40:].reshape(-1, D),
            ],
            0,
        )
        chunk_grad = lax.psum_scatter(wide_grad, AXES, scatter_dimension=0, tiled=True).astype(F32)
        used = sums[1].reshape(-1, 128)
        extra = count * delta
        small_grad = jnp.concatenate([used, jnp.zeros((extra - used.shape[0], 128), F32)], 0)
        small_grad = lax.psum(small_grad, AXES)
    gradient = from_aligned(chunk_grad.reshape(-1, 128), small_grad, place, count, delta, owned)
    new_weights, new_one, new_two = adam_update(
        master, first_moment, second_moment, gradient, step_count, place * owned
    )
    return (layer_out, input_grad, new_weights, new_one, new_two, new_weights.astype(BF))


def solution(mesh):
    spread = P(AXES, None)
    return jax.shard_map(
        shards,
        mesh=mesh,
        in_specs=(spread, spread, P(AXES), spread, spread, spread, P()),
        out_specs=(spread,) * 6,
        check_vma=False,
    )
```

```python
import jax
import jax.numpy as jnp
from jax import lax
from jax.experimental import pallas as pl
from jax.experimental.pallas import tpu as pltpu
from jax.sharding import PartitionSpec as P

D = 768
HEADS = 12
HEAD_DIM = 64
FF = 3072
SEQ_MIN = 1024
AXES = ("dp", "ctx")
QB = 256
PARTS = 3
F32 = jnp.float32
BF = jnp.bfloat16
NT = (((1,), (1,)), ((), ()))
TN = (((0,), (0,)), ((), ()))
norm_eps = 1e-06
VMEM_LIMIT = 56 << 20


def dot(left, right):
    return jnp.dot(left, right, preferred_element_type=F32)


def dot_nt(left, right):
    return lax.dot_general(left, right, NT, preferred_element_type=F32)


def dot_tn(left, right):
    return lax.dot_general(left, right, TN, preferred_element_type=F32)


def cost(flops, nbytes, exps=0):
    return pl.CostEstimate(flops=int(flops), bytes_accessed=int(nbytes), transcendentals=int(exps))


def taps_seen(height, start, rows, state, distance, ahead):
    row = lax.broadcasted_iota(jnp.int32, (height, 128), 0) + (start + ahead)
    own = row - rows
    inside = (own >= distance) | ((own < 0) & (row >= distance)) | ((own >= 0) & (state == 2))
    filled = ((own < 0) | (state > 0)) & (row < 2 * rows)
    return (inside & filled).astype(F32)


def conv(x, taps, mask_one, mask_two):
    one = pltpu.roll(x, 1, 0) * mask_one
    two = pltpu.roll(x, 2, 0) * mask_two
    return (taps[0:1] * x + taps[1:2] * one + taps[2:3] * two).astype(BF)


def att_fwd_kernel(
    state_ref, tail_ref, q_ref, k_ref, v_ref, tq_ref, tk_ref, tv_ref,
    o_ref, l_ref, qm_ref, km_ref, vm_ref, ka, va,
):
    rows = q_ref.shape[0]
    lane = lax.broadcasted_iota(jnp.int32, (1, 128), 1)
    state = state_ref[0]
    one = taps_seen(2 * rows, 0, rows, state, 1, 0)
    two = taps_seen(2 * rows, 0, rows, state, 2, 0)
    x = jnp.concatenate([tail_ref[...].astype(F32), q_ref[...].astype(F32)], 0)
    qm_ref[...] = conv(x, tq_ref[...], one[rows - 8 :], two[rows - 8 :])[8:]
    k = conv(k_ref[...].astype(F32), tk_ref[...], one, two)
    v = conv(v_ref[...].astype(F32), tv_ref[...], one, two)
    km_ref[...] = k
    vm_ref[...] = v
    bias = jnp.where(state == 2, 0.0, -1e30)
    for h in range(2):
        mine = (lane < 64) if h == 0 else (lane >= 64)
        base = 64 if h == 0 else 0
        first = jnp.where(lane == base, bias, 0.0).astype(BF)
        ka[h, 0:rows, :] = jnp.where(mine, k[:rows], first)
        ka[h, rows:, :] = jnp.where(mine, k[rows:], jnp.zeros((), BF))
        va[h] = jnp.where(mine, v, jnp.ones((), BF))
    for i in range(rows // QB):
        rs = pl.ds(i * QB, QB)
        outs = []
        sums = []
        qf = qm_ref[rs, :].astype(F32) * 0.125
        for h in range(2):
            mine = (lane < 64) if h == 0 else (lane >= 64)
            base = 64 if h == 0 else 0
            qh = jnp.where(mine, qf, jnp.where(lane == base, 1.0, 0.0)).astype(BF)
            nk = rows + (i + 1) * QB
            s = dot_nt(qh, ka[h, 0:nk, :])
            r = lax.broadcasted_iota(jnp.int32, (QB, QB), 0)
            c = lax.broadcasted_iota(jnp.int32, (QB, QB), 1)
            sd = jnp.where(c <= r, s[:, nk - QB :], -1e30)
            se = s[:, : nk - QB]
            m = jnp.maximum(
                jnp.max(sd, axis=1, keepdims=True), jnp.max(se, axis=1, keepdims=True)
            )
            p = jnp.concatenate([jnp.exp(se - m).astype(BF), jnp.exp(sd - m).astype(BF)], 1)
            o = dot(p, va[h, 0:nk, :])
            outs.append(o / pltpu.roll(o, 64, 1))
            sums.append(m + jnp.log(o))
        res = jnp.where(lane < 64, outs[0], outs[1])
        res = jnp.where(state == 0, vm_ref[pl.ds(rows + i * QB, QB), :].astype(F32), res)
        o_ref[rs, :] = res.astype(BF)
        l_ref[rs, :] = jnp.where(lane < 64, sums[1], sums[0])


def call_in_parts(body, in_specs, out_specs, out_shape, earlier, part, **options):
    used = len(in_specs)

    def kernel(*refs):
        body(*refs[:used], *refs[used + len(earlier) :])

    return pl.pallas_call(
        kernel,
        grid=(6 // PARTS,),
        in_specs=in_specs + [pl.BlockSpec(memory_space=pl.ANY)] * len(earlier),
        out_specs=out_specs,
        out_shape=out_shape,
        input_output_aliases={used + i: i for i in range(len(earlier))},
        compiler_params=pltpu.CompilerParams(vmem_limit_bytes=VMEM_LIMIT),
        **options,
    )


def columns(part):
    first = part * (6 // PARTS)

    def cols(height, row, off):
        return pl.BlockSpec((height, 128), lambda p: (row, p + first + off))

    taps_at = [
        pl.BlockSpec((3, 128), lambda p, off=off: (0, p + first + off)) for off in (0, 6, 12)
    ]
    return cols, taps_at


def att_fwd(state, projected, taps, earlier, part, rows):
    cols, taps_at = columns(part)
    return call_in_parts(
        att_fwd_kernel,
        [
            pl.BlockSpec(memory_space=pltpu.SMEM),
            cols(8, rows // 8 - 1, 0),
            cols(rows, 1, 0),
            cols(2 * rows, 0, 6),
            cols(2 * rows, 0, 12),
            *taps_at,
        ],
        [cols(rows, 0, 0)] * 3 + [cols(2 * rows, 0, 0)] * 2,
        [
            jax.ShapeDtypeStruct((rows, D), BF),
            jax.ShapeDtypeStruct((rows, D), F32),
            jax.ShapeDtypeStruct((rows, D), BF),
            jax.ShapeDtypeStruct((2 * rows, D), BF),
            jax.ShapeDtypeStruct((2 * rows, D), BF),
        ],
        earlier,
        part,
        scratch_shapes=[pltpu.VMEM((2, 2 * rows, 128), BF)] * 2,
        cost_estimate=cost(
            2 * 2 * 12 * rows * rows * 1.5 * 256 / PARTS,
            rows * D * 30 / PARTS,
            12 * rows * rows * 1.5 / PARTS,
        ),
        name="att_fwd",
    )(state, projected, projected, projected, projected, taps, taps, taps, *earlier)


def three(x, lane, base):
    hi = x.astype(BF).astype(F32)
    r = x - hi
    mid = r.astype(BF).astype(F32)
    lo = r - mid
    return jnp.where(
        lane == base, hi, jnp.where(lane == base + 1, mid, jnp.where(lane == base + 2, lo, 0.0))
    )


def conv_back(grad, x, taps, mask_one, mask_two):
    height = grad.shape[0]
    one = pltpu.roll(grad, height - 1, 0) * mask_one
    two = pltpu.roll(grad, height - 2, 0) * mask_two
    back = (taps[0:1] * grad + taps[1:2] * one + taps[2:3] * two).astype(BF)
    sums = [jnp.sum(g * x, axis=0, keepdims=True) for g in (grad, one, two)]
    return back, sums


def att_bwd_kernel(
    state_ref, q_ref, k_ref, v_ref, o_ref, l_ref, do_ref, xt_ref, xq_ref, xk_ref, xv_ref,
    tq_ref, tk_ref, tv_ref,
    pq_ref, pt_ref, pk_ref, pv_ref, tg_ref, qa, da, qt, dt, kt, dqt, dqs, dks, dvs,
):
    rows = q_ref.shape[0]
    lane = lax.broadcasted_iota(jnp.int32, (1, 128), 1)
    second = state_ref[0] == 2
    do = do_ref[...].astype(F32)
    od = do * o_ref[...].astype(F32)
    qf = q_ref[...].astype(F32) * 0.125
    lv = l_ref[...]
    for h in range(2):
        mine = (lane < 64) if h == 0 else (lane >= 64)
        base = 64 if h == 0 else 0
        delta = jnp.sum(jnp.where(mine, od, 0.0), axis=1, keepdims=True)
        qa[h] = jnp.where(mine, qf, three(-lv, lane, base)).astype(BF)
        da[h] = jnp.where(mine, do, three(-delta, lane, base)).astype(BF)
    qt[...] = jnp.transpose(qf).astype(BF)
    dt[...] = jnp.transpose(do).astype(BF)
    kt[...] = jnp.transpose(k_ref[...].astype(F32)).astype(BF)
    dqt[...] = jnp.zeros(dqt.shape, F32)

    def keys(ks, first, diagonal):
        kk = k_ref[ks, :]
        vv = v_ref[ks, :]
        dv = []
        dk = []
        for h in range(2):
            mine = (lane < 64) if h == 0 else (lane >= 64)
            base = 64 if h == 0 else 0
            ones3 = ((lane >= base) & (lane < base + 3)).astype(BF)
            hs = slice(64 * h, 64 * h + 64)
            st = dot_nt(jnp.where(mine, kk, ones3), qa[h, first:rows, :])
            dp = dot_nt(jnp.where(mine, vv, ones3), da[h, first:rows, :])
            p = jnp.exp(st)
            if diagonal:
                r = lax.broadcasted_iota(jnp.int32, (QB, QB), 0)
                c = lax.broadcasted_iota(jnp.int32, (QB, QB), 1)
                seen = jnp.where(r <= c, p[:, :QB], 0.0)
                p = jnp.concatenate([seen, p[:, QB:]], 1) if first + QB < rows else seen
            ds = (p * dp).astype(BF)
            dv.append(dot_nt(dt[hs, first:rows], p.astype(BF)))
            dk.append(dot_nt(qt[hs, first:rows], ds))
            dqt[hs, first:rows] += dot(kt[hs, ks], ds)
        dvs[ks, :] = jnp.transpose(jnp.concatenate(dv, 0))
        dks[ks, :] = jnp.transpose(jnp.concatenate(dk, 0))

    for j in range(rows // QB):
        keys(pl.ds(rows + j * QB, QB), j * QB, True)

    @pl.when(second)
    def _():
        def step(j, carry):
            keys(pl.ds(pl.multiple_of(j * QB, QB), QB), 0, False)
            return carry

        lax.fori_loop(0, rows // QB, step, 0)

    @pl.when(jnp.logical_not(second))
    def _():
        dks[0:rows, :] = jnp.zeros((rows, 128), F32)
        dvs[0:rows, :] = jnp.zeros((rows, 128), F32)

    dqs[0:8, :] = jnp.zeros((8, 128), F32)
    dqs[8:, :] = jnp.transpose(dqt[...]) * 0.125
    one = taps_seen(2 * rows, 0, rows, state_ref[0], 1, 1)
    two = taps_seen(2 * rows, 0, rows, state_ref[0], 2, 2)
    xq = jnp.concatenate([xt_ref[...].astype(F32), xq_ref[...].astype(F32)], 0)
    pq, sq = conv_back(dqs[...], xq, tq_ref[...], one[rows - 8 :], two[rows - 8 :])
    pt_ref[...] = pq[:8]
    pq_ref[...] = pq[8:]
    pk_ref[...], sk = conv_back(dks[...], xk_ref[...].astype(F32), tk_ref[...], one, two)
    pv_ref[...], sv = conv_back(dvs[...], xv_ref[...].astype(F32), tv_ref[...], one, two)
    tg_ref[...] = jnp.zeros(tg_ref.shape, F32)
    for j in range(3):
        for m, s in enumerate((sq, sk, sv)):
            tg_ref[3 * j + m : 3 * j + m + 1, :] = s[j]


def att_bwd(state, mixed, attended, logs, grad, projected, taps, earlier, part, rows):
    cols, taps_at = columns(part)
    own = cols(rows, 0, 0)
    both = cols(2 * rows, 0, 0)
    return call_in_parts(
        att_bwd_kernel,
        [
            pl.BlockSpec(memory_space=pltpu.SMEM),
            own, both, both, own, own, own,
            cols(8, rows // 8 - 1, 0),
            cols(rows, 1, 0),
            cols(2 * rows, 0, 6),
            cols(2 * rows, 0, 12),
            *taps_at,
        ],
        [own, cols(8, 0, 0), both, both, cols(16, 0, 0)],
        [
            jax.ShapeDtypeStruct((rows, D), BF),
            jax.ShapeDtypeStruct((8, D), BF),
            jax.ShapeDtypeStruct((2 * rows, D), BF),
            jax.ShapeDtypeStruct((2 * rows, D), BF),
            jax.ShapeDtypeStruct((16, D), F32),
        ],
        earlier,
        part,
        scratch_shapes=[
            pltpu.VMEM((2, rows, 128), BF),
            pltpu.VMEM((2, rows, 128), BF),
            pltpu.VMEM((128, rows), BF),
            pltpu.VMEM((128, rows), BF),
            pltpu.VMEM((128, 2 * rows), BF),
            pltpu.VMEM((128, rows), F32),
            pltpu.VMEM((rows + 8, 128), F32),
            pltpu.VMEM((2 * rows, 128), F32),
            pltpu.VMEM((2 * rows, 128), F32),
        ],
        cost_estimate=cost(
            5 * 2 * 12 * rows * rows * 1.5 * 256 / PARTS,
            rows * D * 40 / PARTS,
            12 * rows * rows * 1.5 / PARTS,
        ),
        name="att_bwd",
    )(state, *mixed, attended, logs, grad, projected, projected, projected, projected,
      taps, taps, taps, *earlier)


def qkv_bwd_kernel(
    core_ref, x_ref, dq_ref, dt_ref, dk_ref, dv_ref, w_ref, gain_ref, gain_two_ref, tg_ref,
    *refs, pieces, blocks,
):
    if pieces:
        send_ref, keep_ref, prev_ref, own_ref, acc, gacc = refs
    else:
        keep_ref, small_ref, prev_ref, own_ref, acc, gacc = refs
    i = pl.program_id(0)
    half = blocks // 2

    @pl.when(i == 0)
    def _():
        acc[...] = jnp.zeros(acc.shape, F32)
        gacc[...] = jnp.zeros(gacc.shape, F32)

    x = x_ref[...].astype(F32)
    hat = x * lax.rsqrt(jnp.mean(x * x, axis=-1, keepdims=True) + norm_eps)
    low = (hat * gain_ref[...]).astype(BF)
    dk = dk_ref[...]
    dv = dv_ref[...]
    gn = dot_nt(dk, w_ref[D : 2 * D, :]) + dot_nt(dv, w_ref[2 * D : 3 * D, :])
    acc[D : 2 * D, :] += dot_tn(low, dk)
    acc[2 * D : 3 * D, :] += dot_tn(low, dv)

    @pl.when(i < half - 1)
    def _():
        prev_ref[...] = gn.astype(BF)
        gacc[0:1, :] += jnp.sum(gn * hat, axis=0, keepdims=True)

    @pl.when(i == half - 1)
    def _():
        dt = dt_ref[...]
        last = gn.shape[0] - 8
        acc[0:D, :] += dot_tn(low[last:], dt)
        full = jnp.concatenate([gn[:last], gn[last:] + dot_nt(dt, w_ref[0:D, :])], 0)
        prev_ref[...] = full.astype(BF)
        gacc[0:1, :] += jnp.sum(full * hat, axis=0, keepdims=True)

    @pl.when(i >= half)
    def _():
        dq = dq_ref[...]
        acc[0:D, :] += dot_tn(low, dq)
        full = gn + dot_nt(dq, w_ref[0:D, :])
        own_ref[...] = full
        gacc[0:1, :] += jnp.sum(full * hat, axis=0, keepdims=True)

    @pl.when(i == blocks - 1)
    def _():
        small = jnp.concatenate(
            [gacc[0:1, :], gain_two_ref[...], tg_ref[0:9, :], jnp.zeros((5, D), F32)], 0
        )
        if pieces:
            core = core_ref[0]
            height = 3 * D // (2 * pieces)
            for j in range(pieces):
                to = pl.ds(j * height, height)
                away = pl.ds(pl.multiple_of((2 * j + 1 - core) * height, 16), height)
                here = pl.ds(pl.multiple_of((2 * j + core) * height, 16), height)
                send_ref[to, :] = acc[away, :].astype(BF)
                keep_ref[to, :] = acc[here, :]
            send_ref[pieces * height :, :] = small.astype(BF)
            keep_ref[pieces * height :, :] = small
        else:
            keep_ref[...] = acc[...].astype(BF)
            small_ref[...] = small


def qkv_bwd(core, x_both, back, wide, gain, gain_two_grad, tap_grads, rows, pieces):
    dq, dt, dk, dv = back
    blocks = 4
    half = blocks // 2
    height = 2 * rows // blocks
    step = pl.BlockSpec((height, D), lambda i: (i, 0))
    late = pl.BlockSpec((height, D), lambda i: (jnp.maximum(i - half, 0), 0))
    early = pl.BlockSpec((height, D), lambda i: (jnp.minimum(i, half - 1), 0))

    def whole(shape):
        return pl.BlockSpec(shape, lambda i: (0, 0))

    if pieces:
        packed = 3 * D // 2 + 16
        outs = [jax.ShapeDtypeStruct((packed, D), BF), jax.ShapeDtypeStruct((packed, D), F32)]
        out_at = [whole((packed, D))] * 2
    else:
        outs = [jax.ShapeDtypeStruct((3 * D, D), BF), jax.ShapeDtypeStruct((16, D), F32)]
        out_at = [whole((3 * D, D)), whole((16, D))]

    def body(*refs):
        qkv_bwd_kernel(*refs, pieces=pieces, blocks=blocks)

    return pl.pallas_call(
        body,
        grid=(blocks,),
        in_specs=[
            pl.BlockSpec(memory_space=pltpu.SMEM),
            step, late, whole((8, D)), step, step, whole((3 * D, D)),
            whole((1, D)), whole((1, D)), whole((16, D)),
        ],
        out_specs=out_at + [early, late],
        out_shape=outs
        + [jax.ShapeDtypeStruct((rows, D), BF), jax.ShapeDtypeStruct((rows, D), F32)],
        scratch_shapes=[pltpu.VMEM((3 * D, D), F32), pltpu.VMEM((8, D), F32)],
        compiler_params=pltpu.CompilerParams(vmem_limit_bytes=VMEM_LIMIT),
        cost_estimate=cost(2 * 2 * D * D * 5 * rows, rows * D * 30),
        name="qkv_bwd",
    )(core, x_both, dq, dt, dk, dv, wide, gain, gain_two_grad, tap_grads)


def merge(index, keep, got, height, taken):
    rows = keep.shape[0]
    out_rows = taken * height + 16 if taken else rows

    def body(index_ref, keep_ref, got_ref, send_ref, stay_ref):
        if not taken:
            total = keep_ref[...] + got_ref[...].astype(F32)
            send_ref[...] = total.astype(BF)
            stay_ref[...] = total
            return
        for j in range(taken):
            to = pl.ds(j * height, height)
            away = pl.ds(pl.multiple_of(index_ref[j] * height, 16), height)
            here = pl.ds(pl.multiple_of(index_ref[taken + j] * height, 16), height)
            send_ref[to, :] = (keep_ref[away, :] + got_ref[away, :].astype(F32)).astype(BF)
            stay_ref[to, :] = keep_ref[here, :] + got_ref[here, :].astype(F32)
        end = keep_ref[rows - 16 :, :] + got_ref[rows - 16 :, :].astype(F32)
        send_ref[taken * height :, :] = end.astype(BF)
        stay_ref[taken * height :, :] = end

    vmem = pl.BlockSpec(memory_space=pltpu.VMEM)
    return pl.pallas_call(
        body,
        in_specs=[pl.BlockSpec(memory_space=pltpu.SMEM), vmem, vmem],
        out_specs=[vmem, vmem],
        out_shape=[
            jax.ShapeDtypeStruct((out_rows, D), BF),
            jax.ShapeDtypeStruct((out_rows, D), F32),
        ],
        compiler_params=pltpu.CompilerParams(vmem_limit_bytes=32 << 20),
        cost_estimate=cost(rows * D, rows * D * 12),
        name="merge",
    )(index, keep, got)


def merge_grid(index, keep, got, taken):
    height = keep.shape[1]

    def body(index_ref, ka_ref, ga_ref, kb_ref, gb_ref, send_ref, stay_ref):
        send_ref[...] = (ka_ref[...].astype(F32) + ga_ref[...].astype(F32)).astype(BF)
        stay_ref[...] = kb_ref[...].astype(F32) + gb_ref[...].astype(F32)

    away = pl.BlockSpec((1, height, D), lambda i, index: (index[i], 0, 0))
    here = pl.BlockSpec((1, height, D), lambda i, index: (index[taken + i], 0, 0))
    step = pl.BlockSpec((1, height, D), lambda i, index: (i, 0, 0))
    return pl.pallas_call(
        body,
        grid_spec=pltpu.PrefetchScalarGridSpec(
            num_scalar_prefetch=1,
            grid=(taken,),
            in_specs=[away, away, here, here],
            out_specs=[step, step],
        ),
        out_shape=[
            jax.ShapeDtypeStruct((taken, height, D), BF),
            jax.ShapeDtypeStruct((taken, height, D), F32),
        ],
        compiler_params=pltpu.CompilerParams(vmem_limit_bytes=32 << 20),
        cost_estimate=cost(taken * height * D * 2, taken * height * D * 16),
        name="merge_grid",
    )(index, keep, got, keep, got)


def arrange(index, one, two, taken):
    half = one.shape[0]
    height = one.shape[1]

    def body(index_ref, one_ref, two_ref, out_ref):
        for i in range(taken):
            at = index_ref[i]

            @pl.when(at < half)
            def _():
                out_ref[i] = one_ref[jnp.minimum(at, half - 1)]

            @pl.when(at >= half)
            def _():
                out_ref[i] = two_ref[jnp.maximum(at - half, 0)]

    vmem = pl.BlockSpec(memory_space=pltpu.VMEM)
    return pl.pallas_call(
        body,
        in_specs=[pl.BlockSpec(memory_space=pltpu.SMEM), vmem, vmem],
        out_specs=vmem,
        out_shape=jax.ShapeDtypeStruct((taken, height, D), BF),
        compiler_params=pltpu.CompilerParams(vmem_limit_bytes=32 << 20),
        cost_estimate=cost(taken * height * D, taken * height * D * 8),
        name="arrange",
    )(index, one, two)


def join(own, got, shared=16):
    rows = own.shape[0]
    body_rows = rows - shared

    def body(own_ref, got_ref, out_ref):
        out_ref[0:body_rows, :] = own_ref[0:body_rows, :]
        out_ref[body_rows : 2 * body_rows, :] = got_ref[0:body_rows, :]
        if shared:
            out_ref[2 * body_rows :, :] = own_ref[body_rows:, :] + got_ref[body_rows:, :]

    vmem = pl.BlockSpec(memory_space=pltpu.VMEM)
    return pl.pallas_call(
        body,
        in_specs=[vmem, vmem],
        out_specs=vmem,
        out_shape=jax.ShapeDtypeStruct((2 * body_rows + shared, D), BF),
        compiler_params=pltpu.CompilerParams(vmem_limit_bytes=32 << 20),
        cost_estimate=cost(rows * D, rows * D * 8),
        name="join",
    )(own, got)


def qkv_fwd_kernel(index_ref, x_ref, *refs, pieces, blocks):
    if pieces:
        own_ref, got_ref, out_ref, small_ref, weight = refs
    else:
        weight, given_ref, out_ref, small_ref = refs
    i = pl.program_id(0)

    @pl.when(i == 0)
    def _():
        if pieces:
            height = 3 * D // (2 * pieces)
            for j in range(pieces):
                at = pl.ds(j * height, height)
                for k, ref in enumerate((own_ref, got_ref)):
                    to = pl.multiple_of(index_ref[k * pieces + j] * height, 16)
                    weight[pl.ds(to, height), :] = ref[at, :]
            end = pl.ds(pieces * height, 16)
            small_ref[...] = own_ref[end, :].astype(F32) + got_ref[end, :].astype(F32)
        else:
            small_ref[...] = given_ref[...]

    x = x_ref[...].astype(F32)
    hat = x * lax.rsqrt(jnp.mean(x * x, axis=-1, keepdims=True) + norm_eps)
    low = (hat * small_ref[0:1, :]).astype(BF)

    @pl.when(i >= blocks // 2 - 1)
    def _():
        out_ref[:, 0:D] = dot(low, weight[0:D, :]).astype(BF)

    out_ref[:, D : 2 * D] = dot(low, weight[D : 2 * D, :]).astype(BF)
    out_ref[:, 2 * D : 3 * D] = dot(low, weight[2 * D : 3 * D, :]).astype(BF)


def qkv_fwd(index, x_both, weights, rows, pieces):
    blocks = 4
    height = 2 * rows // blocks

    def body(*refs):
        qkv_fwd_kernel(*refs, pieces=pieces, blocks=blocks)

    return pl.pallas_call(
        body,
        grid=(blocks,),
        in_specs=[
            pl.BlockSpec(memory_space=pltpu.SMEM),
            pl.BlockSpec((height, D), lambda i: (i, 0)),
            *[pl.BlockSpec(w.shape, lambda i: (0, 0)) for w in weights],
        ],
        out_specs=[
            pl.BlockSpec((height, 3 * D), lambda i: (i, 0)),
            pl.BlockSpec((16, D), lambda i: (0, 0)),
        ]
        + ([pl.BlockSpec((3 * D, D), lambda i: (0, 0))] if pieces else []),
        out_shape=[
            jax.ShapeDtypeStruct((2 * rows, 3 * D), BF),
            jax.ShapeDtypeStruct((16, D), F32),
        ]
        + ([jax.ShapeDtypeStruct((3 * D, D), BF)] if pieces else []),
        compiler_params=pltpu.CompilerParams(vmem_limit_bytes=VMEM_LIMIT),
        cost_estimate=cost(2 * 2 * rows * D * 3 * D, rows * D * 20),
        name="qkv_fwd",
    )(index, x_both, *weights)


def ffn_kernel(
    state_ref, index_ref, x_ref, att_ref, cot_ref, gain_ref, own_ref, got_ref,
    out_ref, gh_ref, ga_ref, gain_grad_ref, away_ref, here_ref,
    hidden, low, total, back, cot, sq, gb, weights, stage_up, stage_down, stage_out, in_sems, sems,
):
    c = pl.program_id(0)
    rows = x_ref.shape[0]
    blocks = [pl.ds(i * QB, QB) for i in range(rows // QB)]
    last = c == pl.num_programs(0) - 1
    core = index_ref[24]

    def fetch(k, j):
        ref = own_ref if k == 0 else got_ref
        to = weights.at[pl.ds(3 * index_ref[12 * k + j], 3)]
        return pltpu.make_async_copy(ref.at[pl.ds(3 * j, 3)], to, in_sems.at[12 * k + j])

    def put(source, group, count, column, sem, wait=False):
        piece = group // 3
        at = (piece // 2) * 3 + group % 3

        def copy(ref):
            to = ref.at[pl.ds(at, count)] if column is None else ref.at[pl.ds(at, count), column]
            return pltpu.make_async_copy(source, to, sems.at[sem])

        if wait:
            copy(here_ref).wait()
            return
        mine = piece % 2 == core

        @pl.when(mine)
        def _():
            copy(here_ref).start()

        @pl.when(jnp.logical_not(mine))
        def _():
            copy(away_ref).start()

    def put_up(i, wait=False):
        start = 0
        k = 0
        while start < 32:
            count = min(3 - (8 + start) % 3, 32 - start)
            put(stage_up.at[i, pl.ds(start, count)], 8 + start, count, i, 20 * i + k, wait)
            start += count
            k += 1

    def put_down(i, wait=False):
        for k in range(8):
            put(stage_down.at[i, pl.ds(k, 1)], 40 + 8 * i + k, 1, None, 20 * i + 12 + k, wait)

    def put_out(wait=False):
        for k in range(8):
            put(stage_out.at[pl.ds(k, 1)], k, 1, None, 80 + k, wait)

    def square(first):
        return weights[first : first + 8].reshape(D, D)

    @pl.when(c == 0)
    def _():
        for k in range(2):
            for j in range(12):
                fetch(k, j).start()
        cot[...] = jnp.where(state_ref[0] > 0, cot_ref[...], jnp.zeros((), BF))
        total[...] = jnp.zeros(total.shape, F32)
        back[...] = jnp.zeros(back.shape, F32)
        for k in range(2):
            for j in range(12):
                fetch(k, j).wait()
        wo = square(0)
        for b in blocks:
            h = x_ref[b, :].astype(F32) + dot(att_ref[b, :], wo)
            hidden[b, :] = h
            hat = h * lax.rsqrt(jnp.mean(h * h, axis=-1, keepdims=True) + norm_eps)
            low[b, :] = (hat * gain_ref[...]).astype(BF)

    up = weights[8:40, c].reshape(D, D)
    down = weights[pl.ds(40 + 8 * c, 8)].reshape(D, D)
    for b in blocks:
        act = jnp.maximum(dot(low[b, :], up), 0.0)
        s = (act * act).astype(BF)
        sq[b, :] = s
        total[b, :] += dot(s, down)
        g = (dot_nt(cot[b, :], down) * 2.0 * act).astype(BF)
        gb[b, :] = g
        back[b, :] += dot_nt(g, up)
    stage_down[c] = dot_tn(sq[...], cot[...]).reshape(8, 4, 24, D).astype(BF)
    stage_up[c] = dot_tn(low[...], gb[...]).reshape(32, 24, D).astype(BF)
    put_down(c)
    put_up(c)

    @pl.when(last)
    def _():
        gain = gain_ref[...]
        wo = square(0)
        sums = jnp.zeros((1, D), F32)
        for b in blocks:
            h = hidden[b, :]
            out_ref[b, :] = (h + total[b, :]).astype(BF)
            factor = lax.rsqrt(jnp.mean(h * h, axis=-1, keepdims=True) + norm_eps)
            hat = h * factor
            g = back[b, :]
            sums = sums + jnp.sum(g * hat, axis=0, keepdims=True)
            weighted = g * gain
            inner = jnp.mean(weighted * hat, axis=-1, keepdims=True)
            grad = cot[b, :].astype(F32) + factor * (weighted - hat * inner)
            gh_ref[b, :] = grad
            grad_low = grad.astype(BF)
            gb[b, :] = grad_low
            ga_ref[b, :] = dot_nt(grad_low, wo).astype(BF)
        gain_grad_ref[...] = sums
        stage_out[...] = dot_tn(att_ref[...], gb[...]).reshape(8, 4, 24, D).astype(BF)
        put_out()
        for i in range(4):
            put_down(i, True)
            put_up(i, True)
        put_out(True)


def ffn(state, index, tokens, attended, out_grad, gain, own, got, rows):
    def whole(shape):
        return pl.BlockSpec(shape, lambda c: (0,) * len(shape), pipeline_mode=pl.Buffered(1))

    act = whole((rows, D))
    held = pl.BlockSpec(memory_space=pl.ANY)
    scalars = pl.BlockSpec(memory_space=pltpu.SMEM)
    half = (36, 4, 24, D)
    return pl.pallas_call(
        ffn_kernel,
        grid=(4,),
        in_specs=[scalars, scalars, act, act, act, whole((1, D)), held, held],
        out_specs=[act, act, act, whole((1, D)), held, held],
        out_shape=[
            jax.ShapeDtypeStruct((rows, D), BF),
            jax.ShapeDtypeStruct((rows, D), F32),
            jax.ShapeDtypeStruct((rows, D), BF),
            jax.ShapeDtypeStruct((1, D), F32),
            jax.ShapeDtypeStruct(half, BF),
            jax.ShapeDtypeStruct(half, BF),
        ],
        scratch_shapes=[
            pltpu.VMEM((rows, D), F32),
            pltpu.VMEM((rows, D), BF),
            pltpu.VMEM((rows, D), F32),
            pltpu.VMEM((rows, D), F32),
            pltpu.VMEM((rows, D), BF),
            pltpu.VMEM((rows, D), BF),
            pltpu.VMEM((rows, D), BF),
            pltpu.VMEM((72, 4, 24, D), BF),
            pltpu.VMEM((4, 32, 24, D), BF),
            pltpu.VMEM((4, 8, 4, 24, D), BF),
            pltpu.VMEM((8, 4, 24, D), BF),
            pltpu.SemaphoreType.DMA((24,)),
            pltpu.SemaphoreType.DMA((88,)),
        ],
        compiler_params=pltpu.CompilerParams(vmem_limit_bytes=60 << 20),
        cost_estimate=cost(2 * rows * D * D * (24 + 3), 2 * 12 * D * D * 2 + rows * D * 16),
        name="ffn",
    )(state, index, tokens, attended, out_grad, gain, own, got)


def shift_flat(block, distance):
    count = lax.axis_size(AXES)
    route = [(i - distance, i) for i in range(count) if 0 <= i - distance < count]
    return lax.ppermute(block, AXES, route)


def shift_ctx(block, distance):
    count = lax.axis_size("ctx")
    route = [(i - distance, i) for i in range(count) if 0 <= i - distance < count]
    return lax.ppermute(block, "ctx", route)


def after(value, *others):
    return lax.optimization_barrier((value, *others))[0]


def swap(block, even_bit, odd_bit, planes=None):
    count = lax.axis_size(AXES)
    route = [
        (i, i ^ (odd_bit if i & 1 else even_bit))
        for i in range(count)
        if planes is None or i >> 3 in planes
    ]
    return lax.ppermute(block, AXES, route)


def to_aligned(shard, place, count, delta):
    rows = shard.shape[0]
    lag = delta * (count - 1)
    back = -(-lag // rows)
    if back == 1:
        keep = -(-lag // 8) * 8
        parts = [shift_flat(shard[rows - keep :], 1), shard]
    else:
        keep = back * rows
        parts = [shift_flat(shard, s) for s in range(back, 0, -1)] + [shard]
    joined = jnp.concatenate(parts, 0)
    return lax.dynamic_slice_in_dim(joined, keep - delta * place, rows - delta, 0)


def small_part(shard, place, count, delta):
    rows = shard.shape[0]
    extra = count * delta
    zeros = jnp.zeros((extra, 128), shard.dtype)
    joined = jnp.concatenate([zeros, shard, zeros], 0)
    start = extra + count * (rows - delta) - place * rows
    return lax.dynamic_slice_in_dim(joined, jnp.minimum(start, rows + extra), extra, 0)


def from_aligned(chunk, small, place, count, delta, rows):
    aligned = rows - delta
    ahead = -(-(count * delta) // aligned)
    parts = [chunk]
    if ahead == 1:
        keep = small.shape[0]
        got = shift_flat(chunk[:keep], -1)
        parts.append(jnp.where(place == count - 1, small, got))
    else:
        pad = ahead * aligned - small.shape[0]
        tail = jnp.concatenate([small, jnp.zeros((pad, 128), small.dtype)], 0)
        for s in range(1, ahead + 1):
            got = shift_flat(chunk, -s)
            for e in range(s):
                piece = tail[e * aligned : (e + 1) * aligned]
                got = jnp.where(place == count - s + e, piece, got)
            parts.append(got)
    return lax.dynamic_slice_in_dim(jnp.concatenate(parts, 0), delta * place, rows, 0)


def regroup(block):
    return block.reshape(-1, 24, 4, D).transpose(0, 2, 1, 3)


def ungroup(block):
    return block.reshape(-1, 4, 24, D).transpose(0, 2, 1, 3)


def normalize(values, gain):
    factor = lax.rsqrt(jnp.mean(values * values, axis=-1, keepdims=True) + norm_eps)
    scaled = values * factor
    return (scaled, factor, scaled * gain)


def norm_back(grad_in, scaled, factor, gain):
    weighted = grad_in * gain
    inner_mean = jnp.mean(weighted * scaled, axis=-1, keepdims=True)
    return factor * (weighted - scaled * inner_mean)


def adam_update(master, moment_one, moment_two, gradient, step_count, row_start):
    row_index = row_start + jnp.arange(master.shape[0], dtype=jnp.int32)
    matrix_rows = (4 * D * D + 2 * D * FF) // 128
    out_first = 3 * D * D // 128
    out_last = 4 * D * D // 128
    is_matrix = (row_index < matrix_rows)[:, None]
    is_out = ((row_index >= out_first) & (row_index < out_last))[:, None]
    step_rate = jnp.where(is_matrix, jnp.where(is_out, 0.5, 0.1), 1.0)
    decay_rate = jnp.where(is_matrix, 0.1, 0.0)
    step_value = step_count[0].astype(jnp.float32)
    new_one = 0.9 * moment_one + 0.1 * gradient
    new_two = 0.999 * moment_two + 0.001 * gradient * gradient
    corr_first = 1.0 - jnp.power(0.9, step_value)
    corr_second = 1.0 - jnp.power(0.999, step_value)
    new_weights = master - step_rate * (
        new_one / corr_first / (jnp.sqrt(new_two / corr_second) + 1e-08) + decay_rate * master
    )
    return (new_weights, new_one, new_two)


def shards(tokens, out_grad, positions, master, first_moment, second_moment, step_count):
    rows = tokens.shape[0]
    assert rows == SEQ_MIN
    count = lax.axis_size(AXES)
    place = lax.axis_index(AXES).astype(jnp.int32)
    owned = master.shape[0]
    aligned = (4 * D * D + 2 * D * FF) // 128 // count
    delta = owned - aligned
    height = aligned * 128 // D
    staged = count == 32
    first_place = positions[0]
    state = jnp.where(first_place < 0, 0, jnp.where(first_place >= SEQ_MIN, 2, 1)).astype(jnp.int32)
    state_vec = state[None]

    tokens_before = shift_ctx(tokens, 1)
    chunk = to_aligned(master, place, count, delta).reshape(-1, D)
    if staged:
        group = 3 * place + jnp.arange(3, dtype=jnp.int32)
        in_up = ((group >= 32) & (group < 64))[:, None, None, None]
        chunk = jnp.where(in_up, regroup(chunk), chunk.reshape(3, 4, 24, D)).reshape(-1, D)
    chunk = chunk.astype(BF)
    small = lax.reduce_precision(small_part(master, place, count, delta), 8, 7)
    core = (place & 1)[None]
    x_bit = (place >> 1) & 1
    y_bit = (place >> 2) & 1
    even = (place & 1) == 0
    tokens_both = jnp.concatenate([tokens_before, tokens], 0)
    if staged:
        z = place >> 3
        mine = jnp.concatenate([chunk, small.astype(BF).reshape(-1, D)], 0)
        got = swap(mine, 16, 16)
        rest = jnp.concatenate([chunk, got[:height]], 0)
        none = jnp.zeros((), BF)
        first = jnp.where(z == 0, chunk, jnp.where(z == 2, got[:height], none))
        mine = jnp.concatenate([first, mine[height:] + got[height:]], 0)
        mine = mine + swap(mine, 8, 8)
        across = swap(after(rest, mine), 8, 8)
        mine = join(mine, swap(mine, 2, 4))
        mine = join(mine, swap(mine, 4, 2))
        got = swap(mine, 1, 1)
        index = []
        late_index = []
        for k in (0, 1):
            turn = even if k == 0 else jnp.logical_not(even)
            for j in range(4):
                near, far = j & 1, j >> 1
                x_of = x_bit ^ jnp.where(turn, near, far)
                y_of = y_bit ^ jnp.where(turn, far, near)
                piece = 4 * y_of + 2 * x_of + (core[0] ^ k)
                index.append(piece)
                late_index += [piece, piece + 8, piece + 16]
        index = jnp.stack(index).astype(jnp.int32)
        late_index = jnp.stack(late_index + [core[0]]).astype(jnp.int32)
        projected, small, in_weight = qkv_fwd(index, tokens_both, (mine, got), rows, 4)
        codes = [z ^ k for k in (1, 2, 3)]
        order = [jnp.where(j == 1, 2, jnp.where(j == 2, 1, j)) for j in codes]
        rest = arrange(
            after(jnp.stack(order).astype(jnp.int32), projected), rest.reshape(2, height, D), across.reshape(2, height, D), 3
        ).reshape(-1, D)
        across = swap(rest, 2, 4)
    else:
        wide = lax.all_gather(chunk, AXES, axis=0, tiled=True)
        small = lax.psum(small, AXES)[:96].reshape(-1, D)
        in_weight = wide[: 3 * D]
        projected, small = qkv_fwd(core, tokens_both, (in_weight, small), rows, 0)
        late_index = jnp.arange(25, dtype=jnp.int32) % 24
    gain_first = small[0]
    gain_second = small[1]
    taps = small[2:11].reshape(3, 3 * D)

    forward = []
    if staged:
        forward = att_fwd(after(state_vec, rest), projected, taps, forward, 0, rows)
        rest = join(after(rest, forward[0]), across, 0)
        across = swap(rest, 4, 2)
        forward = att_fwd(after(state_vec, rest), projected, taps, forward, 1, rows)
        rest = join(after(rest, forward[0]), across, 0)
        across = swap(rest, 1, 1)
        forward = att_fwd(after(state_vec, rest), projected, taps, forward, 2, rows)
        own_weights, got_weights = rest.reshape(36, 4, 24, D), across.reshape(36, 4, 24, D)
    else:
        for part in range(PARTS):
            forward = att_fwd(state_vec, projected, taps, forward, part, rows)
        grouped = jnp.concatenate(
            [
                wide[3 * D : 4 * D].reshape(-1, 4, 24, D),
                regroup(wide[4 * D : 8 * D]),
                wide[8 * D :].reshape(-1, 4, 24, D),
            ],
            0,
        )
        own_weights, got_weights = grouped[:36], grouped[36:]
    attn_low, logs, *mixed = forward

    layer_out, grad_hidden, grad_attended, grad_gain_two, away_grad, here_grad = ffn(
        state_vec, late_index, tokens, attn_low, out_grad, gain_second[None], own_weights, got_weights, rows
    )

    def backward(start, done, part):
        return att_bwd(
            start, mixed, attn_low, logs, grad_attended, projected, taps, done, part, rows
        )

    if staged:
        stay = [jnp.where(even, 2 * j + x_bit, 2 * y_bit + j) for j in range(2)]
        away = [jnp.where(even, 2 * j + 1 - x_bit, 2 * (1 - y_bit) + j) for j in range(2)]
        pick_plane = jnp.stack(away + stay).astype(jnp.int32)
        other = jnp.where(even, y_bit, x_bit)
        pick_line = jnp.stack([1 - other, other]).astype(jnp.int32)

        def of_quarters(pick, held):
            half = pick.shape[0] // 2
            steps = [pick[s * half + j] + held * t for s in range(2) for t in range(3) for j in range(half)]
            return jnp.stack(steps)

        late_keep = here_grad.reshape(12, height, D)
        late_got = swap(away_grad.reshape(12, height, D), 1, 1)
        done = backward(state_vec, [], 0)
        late_send, late_keep = merge_grid(
            after(of_quarters(pick_plane, 4), done[4]), late_keep, late_got, 6
        )
        late_got = swap(late_send, 2, 4)
        done = backward(after(state_vec, late_send), done, 1)
        late_send, late_keep = merge_grid(
            after(of_quarters(pick_line, 2), done[4]), late_keep, late_got, 3
        )
        late_got = swap(late_send, 4, 2)
        done = backward(after(state_vec, late_send), done, 2)
        z_even = (z & 1) == 0
        low_pair = [jnp.where(z_even, 0, 0), jnp.where(z_even, 2, 1)]
        high_pair = [jnp.where(z_even, 0, 0), jnp.where(z_even, 1, 2)]
        pick_z = jnp.stack(low_pair + high_pair).astype(jnp.int32)
        late_send, late_keep = merge_grid(after(pick_z, done[4]), late_keep, late_got, 2)
        late_got = swap(late_send, 8, 8)
        sums_state = after(core, late_send)
    else:
        done = []
        for part in range(PARTS):
            done = backward(state_vec, done, part)
        sums_state = core
    *back, tap_grads = done
    sums = qkv_bwd(
        sums_state, tokens_both, back, in_weight, gain_first[None], grad_gain_two, tap_grads, rows,
        4 if staged else 0,
    )
    grads_before, grad_normed_one = sums[2:]
    if staged:
        send, keep = sums[:2]
        high = z >> 1
        pick_last = jnp.stack([1 - high, high]).astype(jnp.int32)
        late_send, late_keep = merge_grid(after(pick_last, send), late_keep, late_got, 1)
        late_got = swap(late_send, 16, 16, (0, 1, 3))
        got = swap(after(send, late_send), 1, 1)
        send, keep = merge(pick_plane, keep, got, height, 2)
        got = swap(send, 2, 4)
        send, keep = merge(pick_line, keep, got, height, 1)
        got = swap(send, 4, 2)
        send, keep = merge(core, keep, got, height, 0)
        got = swap(send, 8, 8)
        from_next = shift_ctx(after(grads_before, send), -1)
        late_chunk = late_keep[0] + late_got[0].astype(F32)
        send, keep = merge(after(core, late_chunk), keep, got, height, 0)
        got = swap(send, 16, 16, (1, 2))
        first = keep + got.astype(F32)
        small_grad = first[height:].reshape(-1, 128)
        late_grad = jnp.where(in_up, ungroup(late_chunk).reshape(3, 4, 24, D), late_chunk.reshape(3, 4, 24, D))
        chunk_grad = jnp.where(place < count // 4, first[:height], late_grad.reshape(-1, D))
    else:
        from_next = shift_ctx(grads_before, -1)
        flat_grad = jnp.stack([here_grad.reshape(12, 3, 4, 24, D), away_grad.reshape(12, 3, 4, 24, D)], 1)
        flat_grad = flat_grad.reshape(72, 4, 24, D)
        wide_grad = jnp.concatenate(
            [
                sums[0],
                flat_grad[:8].reshape(-1, D),
                ungroup(flat_grad[8:40]).reshape(-1, D),
                flat_grad[40:].reshape(-1, D),
            ],
            0,
        )
        chunk_grad = lax.psum_scatter(wide_grad, AXES, scatter_dimension=0, tiled=True).astype(F32)
        used = sums[1].reshape(-1, 128)
        extra = count * delta
        small_grad = jnp.concatenate([used, jnp.zeros((extra - used.shape[0], 128), F32)], 0)
        small_grad = lax.psum(small_grad, AXES)
    scaled_one, factor_one, _ = normalize(tokens.astype(F32), gain_first)
    input_grad = grad_hidden + norm_back(
        grad_normed_one + from_next.astype(F32), scaled_one, factor_one, gain_first
    )

    gradient = from_aligned(chunk_grad.reshape(-1, 128), small_grad, place, count, delta, owned)
    new_weights, new_one, new_two = adam_update(
        master, first_moment, second_moment, gradient, step_count, place * owned
    )
    return (layer_out, input_grad, new_weights, new_one, new_two, new_weights.astype(BF))


def solution(mesh):
    spread = P(AXES, None)
    return jax.shard_map(
        shards,
        mesh=mesh,
        in_specs=(spread, spread, P(AXES), spread, spread, spread, P()),
        out_specs=(spread,) * 6,
        check_vma=False,
    )
```

```python
import jax
import jax.numpy as jnp
from jax import lax
from jax.experimental import pallas as pl
from jax.experimental.pallas import tpu as pltpu
from jax.sharding import PartitionSpec as P

D = 768
HEADS = 12
HEAD_DIM = 64
FF = 3072
SEQ_MIN = 1024
AXES = ("dp", "ctx")
QB = 256
PARTS = 3
F32 = jnp.float32
BF = jnp.bfloat16
NT = (((1,), (1,)), ((), ()))
TN = (((0,), (0,)), ((), ()))
norm_eps = 1e-06
VMEM_LIMIT = 56 << 20


def dot(left, right):
    return jnp.dot(left, right, preferred_element_type=F32)


def dot_nt(left, right):
    return lax.dot_general(left, right, NT, preferred_element_type=F32)


def dot_tn(left, right):
    return lax.dot_general(left, right, TN, preferred_element_type=F32)


def cost(flops, nbytes, exps=0):
    return pl.CostEstimate(flops=int(flops), bytes_accessed=int(nbytes), transcendentals=int(exps))


def row_ids(height):
    return lax.broadcasted_iota(jnp.int32, (height, 128), 0)


def conv(out_ref, x_ref, start, tail_ref, taps, rows, state):
    height = x_ref.shape[0]
    for r in range(0, height, QB):
        at = start + r
        if r:
            x = x_ref[r - 16 : r + QB, :].astype(F32)
        else:
            before = jnp.zeros((16, 128), F32)
            if tail_ref is not None:
                before = jnp.concatenate([before[8:], tail_ref[...].astype(F32)], 0)
            x = jnp.concatenate([before, x_ref[0:QB, :].astype(F32)], 0)
        one = pltpu.roll(x, 1, 0)[16:]
        two = pltpu.roll(x, 2, 0)[16:]
        x = x[16:]
        scale = 1.0
        if at >= rows:
            scale = jnp.where(state > 0, 1.0, 0.0)
        if at == 0 or at == rows:
            seen = jnp.where(state == 2, 1.0, 0.0) if at else 0.0
            row = row_ids(QB)
            one = jnp.where(row < 1, one * seen, one)
            two = jnp.where(row < 2, two * seen, two)
        c_one = taps[1:2] * scale
        c_two = taps[2:3] * scale
        out_ref[r : r + QB, :] = (taps[0:1] * x + c_one * one + c_two * two).astype(BF)


def att_fwd_kernel(
    state_ref, tail_ref, q_ref, k_ref, v_ref, tq_ref, tk_ref, tv_ref,
    o_ref, l_ref, qm_ref, km_ref, vm_ref, ka, va,
):
    rows = q_ref.shape[0]
    lane = lax.broadcasted_iota(jnp.int32, (1, 128), 1)
    state = state_ref[0]
    conv(qm_ref, q_ref, rows, tail_ref, tq_ref[...], rows, state)
    conv(km_ref, k_ref, 0, None, tk_ref[...], rows, state)
    conv(vm_ref, v_ref, 0, None, tv_ref[...], rows, state)
    bias = jnp.where(state == 2, 0.0, -1e30)
    for h in range(2):
        mine = (lane < 64) if h == 0 else (lane >= 64)
        base = 64 if h == 0 else 0
        first = jnp.where(lane == base, bias, 0.0).astype(BF)
        for r in range(0, 2 * rows, QB):
            at = pl.ds(r, QB)
            ka[h, at, :] = jnp.where(mine, km_ref[at, :], first if r < rows else jnp.zeros((), BF))
            va[h, at, :] = jnp.where(mine, vm_ref[at, :], jnp.ones((), BF))
    for i in range(rows // QB):
        rs = pl.ds(i * QB, QB)
        outs = []
        sums = []
        qf = qm_ref[rs, :].astype(F32) * 0.125
        for h in range(2):
            mine = (lane < 64) if h == 0 else (lane >= 64)
            base = 64 if h == 0 else 0
            qh = jnp.where(mine, qf, jnp.where(lane == base, 1.0, 0.0)).astype(BF)
            nk = rows + (i + 1) * QB
            s = dot_nt(qh, ka[h, 0:nk, :])
            r = lax.broadcasted_iota(jnp.int32, (QB, QB), 0)
            c = lax.broadcasted_iota(jnp.int32, (QB, QB), 1)
            sd = jnp.where(c <= r, s[:, nk - QB :], -1e30)
            se = s[:, : nk - QB]
            m = jnp.maximum(
                jnp.max(sd, axis=1, keepdims=True), jnp.max(se, axis=1, keepdims=True)
            )
            p = jnp.concatenate([jnp.exp(se - m).astype(BF), jnp.exp(sd - m).astype(BF)], 1)
            o = dot(p, va[h, 0:nk, :])
            outs.append(o / pltpu.roll(o, 64, 1))
            sums.append(m + jnp.log(o))
        res = jnp.where(lane < 64, outs[0], outs[1])
        res = jnp.where(state == 0, vm_ref[pl.ds(rows + i * QB, QB), :].astype(F32), res)
        o_ref[rs, :] = res.astype(BF)
        l_ref[rs, :] = jnp.where(lane < 64, sums[1], sums[0])


def call_in_parts(body, in_specs, out_specs, out_shape, earlier, part, **options):
    used = len(in_specs)

    def kernel(*refs):
        body(*refs[:used], *refs[used + len(earlier) :])

    return pl.pallas_call(
        kernel,
        grid=(6 // PARTS,),
        in_specs=in_specs + [pl.BlockSpec(memory_space=pl.ANY)] * len(earlier),
        out_specs=out_specs,
        out_shape=out_shape,
        input_output_aliases={used + i: i for i in range(len(earlier))},
        compiler_params=pltpu.CompilerParams(vmem_limit_bytes=VMEM_LIMIT),
        **options,
    )


def columns(part):
    first = part * (6 // PARTS)

    def cols(height, row, off):
        return pl.BlockSpec((height, 128), lambda p: (row, p + first + off))

    taps_at = [
        pl.BlockSpec((3, 128), lambda p, off=off: (0, p + first + off)) for off in (0, 6, 12)
    ]
    return cols, taps_at


def att_fwd(state, projected, taps, earlier, part, rows):
    cols, taps_at = columns(part)
    return call_in_parts(
        att_fwd_kernel,
        [
            pl.BlockSpec(memory_space=pltpu.SMEM),
            cols(8, rows // 8 - 1, 0),
            cols(rows, 1, 0),
            cols(2 * rows, 0, 6),
            cols(2 * rows, 0, 12),
            *taps_at,
        ],
        [cols(rows, 0, 0)] * 3 + [cols(2 * rows, 0, 0)] * 2,
        [
            jax.ShapeDtypeStruct((rows, D), BF),
            jax.ShapeDtypeStruct((rows, D), F32),
            jax.ShapeDtypeStruct((rows, D), BF),
            jax.ShapeDtypeStruct((2 * rows, D), BF),
            jax.ShapeDtypeStruct((2 * rows, D), BF),
        ],
        earlier,
        part,
        scratch_shapes=[pltpu.VMEM((2, 2 * rows, 128), BF)] * 2,
        cost_estimate=cost(
            2 * 2 * 12 * rows * rows * 1.5 * 256 / PARTS,
            rows * D * 30 / PARTS,
            12 * rows * rows * 1.5 / PARTS,
        ),
        name="att_fwd",
    )(state, projected, projected, projected, projected, taps, taps, taps, *earlier)


def three(x, lane, base):
    hi = x.astype(BF).astype(F32)
    r = x - hi
    mid = r.astype(BF).astype(F32)
    lo = r - mid
    return jnp.where(
        lane == base, hi, jnp.where(lane == base + 1, mid, jnp.where(lane == base + 2, lo, 0.0))
    )


def conv_back(out_ref, grad_ref, x_ref, start, tail, taps, rows, state):
    height = grad_ref.shape[0]
    joint = jnp.where(state == 2, 1.0, 0.0)
    sums = [jnp.zeros((1, 128), F32)] * 3

    def add(parts, x):
        return [s + jnp.sum(g * x, axis=0, keepdims=True) for s, g in zip(sums, parts)]

    for r in range(0, height, QB):
        ends = r + QB == height
        meets = start + r + QB == rows
        if ends:
            grad = jnp.concatenate([grad_ref[r : r + QB, :], jnp.zeros((8, 128), F32)], 0)
        else:
            grad = grad_ref[r : r + QB + 8, :]
        one = pltpu.roll(grad, QB + 7, 0)[:QB]
        two = pltpu.roll(grad, QB + 6, 0)[:QB]
        grad = grad[:QB]
        if meets and not ends:
            row = row_ids(QB)
            one = jnp.where(row >= QB - 1, one * joint, one)
            two = jnp.where(row >= QB - 2, two * joint, two)
        out_ref[r : r + QB, :] = (taps[0:1] * grad + taps[1:2] * one + taps[2:3] * two).astype(BF)
        sums = add((grad, one, two), x_ref[r : r + QB, :].astype(F32))
    if tail is not None:
        grad = jnp.concatenate([jnp.zeros((8, 128), F32), grad_ref[0:8, :]], 0)
        one = pltpu.roll(grad, 15, 0)[:8] * joint
        two = pltpu.roll(grad, 14, 0)[:8] * joint
        tail[0][...] = (taps[1:2] * one + taps[2:3] * two).astype(BF)
        sums = add((grad[:8], one, two), tail[1][...].astype(F32))
    return sums


def att_bwd_kernel(
    state_ref, q_ref, k_ref, v_ref, o_ref, l_ref, do_ref, xt_ref, xq_ref, xk_ref, xv_ref,
    tq_ref, tk_ref, tv_ref,
    pq_ref, pt_ref, pk_ref, pv_ref, tg_ref, qa, da, qt, dt, kt, dqt, dqs, dks, dvs,
):
    rows = q_ref.shape[0]
    lane = lax.broadcasted_iota(jnp.int32, (1, 128), 1)
    second = state_ref[0] == 2
    for r in range(0, rows, QB):
        at = pl.ds(r, QB)
        do = do_ref[at, :].astype(F32)
        od = do * o_ref[at, :].astype(F32)
        qf = q_ref[at, :].astype(F32) * 0.125
        lv = l_ref[at, :]
        for h in range(2):
            mine = (lane < 64) if h == 0 else (lane >= 64)
            base = 64 if h == 0 else 0
            delta = jnp.sum(jnp.where(mine, od, 0.0), axis=1, keepdims=True)
            qa[h, at, :] = jnp.where(mine, qf, three(-lv, lane, base)).astype(BF)
            da[h, at, :] = jnp.where(mine, do, three(-delta, lane, base)).astype(BF)
        qt[:, at] = jnp.transpose(qf).astype(BF)
        dt[:, at] = jnp.transpose(do).astype(BF)
    for r in range(0, 2 * rows, QB):
        at = pl.ds(r, QB)
        kt[:, at] = jnp.transpose(k_ref[at, :].astype(F32)).astype(BF)
    dqt[...] = jnp.zeros(dqt.shape, F32)

    def keys(ks, first, diagonal):
        kk = k_ref[ks, :]
        vv = v_ref[ks, :]
        dv = []
        dk = []
        for h in range(2):
            mine = (lane < 64) if h == 0 else (lane >= 64)
            base = 64 if h == 0 else 0
            ones3 = ((lane >= base) & (lane < base + 3)).astype(BF)
            hs = slice(64 * h, 64 * h + 64)
            st = dot_nt(jnp.where(mine, kk, ones3), qa[h, first:rows, :])
            dp = dot_nt(jnp.where(mine, vv, ones3), da[h, first:rows, :])
            p = jnp.exp(st)
            if diagonal:
                r = lax.broadcasted_iota(jnp.int32, (QB, QB), 0)
                c = lax.broadcasted_iota(jnp.int32, (QB, QB), 1)
                seen = jnp.where(r <= c, p[:, :QB], 0.0)
                p = jnp.concatenate([seen, p[:, QB:]], 1) if first + QB < rows else seen
            ds = (p * dp).astype(BF)
            dv.append(dot_nt(dt[hs, first:rows], p.astype(BF)))
            dk.append(dot_nt(qt[hs, first:rows], ds))
            dqt[hs, first:rows] += dot(kt[hs, ks], ds)
        dvs[ks, :] = jnp.transpose(jnp.concatenate(dv, 0))
        dks[ks, :] = jnp.transpose(jnp.concatenate(dk, 0))

    for j in range(rows // QB):
        keys(pl.ds(rows + j * QB, QB), j * QB, True)

    @pl.when(second)
    def _():
        def step(j, carry):
            keys(pl.ds(pl.multiple_of(j * QB, QB), QB), 0, False)
            return carry

        lax.fori_loop(0, rows // QB, step, 0)

    @pl.when(jnp.logical_not(second))
    def _():
        dks[0:rows, :] = jnp.zeros((rows, 128), F32)
        dvs[0:rows, :] = jnp.zeros((rows, 128), F32)

    for r in range(0, rows, QB):
        dqs[r : r + QB, :] = jnp.transpose(dqt[:, r : r + QB]) * 0.125
    state = state_ref[0]
    sq = conv_back(pq_ref, dqs, xq_ref, rows, (pt_ref, xt_ref), tq_ref[...], rows, state)
    sk = conv_back(pk_ref, dks, xk_ref, 0, None, tk_ref[...], rows, state)
    sv = conv_back(pv_ref, dvs, xv_ref, 0, None, tv_ref[...], rows, state)
    tg_ref[...] = jnp.zeros(tg_ref.shape, F32)
    for j in range(3):
        for m, s in enumerate((sq, sk, sv)):
            tg_ref[3 * j + m : 3 * j + m + 1, :] = s[j]


def att_bwd(state, mixed, attended, logs, grad, projected, taps, earlier, part, rows):
    cols, taps_at = columns(part)
    own = cols(rows, 0, 0)
    both = cols(2 * rows, 0, 0)
    return call_in_parts(
        att_bwd_kernel,
        [
            pl.BlockSpec(memory_space=pltpu.SMEM),
            own, both, both, own, own, own,
            cols(8, rows // 8 - 1, 0),
            cols(rows, 1, 0),
            cols(2 * rows, 0, 6),
            cols(2 * rows, 0, 12),
            *taps_at,
        ],
        [own, cols(8, 0, 0), both, both, cols(16, 0, 0)],
        [
            jax.ShapeDtypeStruct((rows, D), BF),
            jax.ShapeDtypeStruct((8, D), BF),
            jax.ShapeDtypeStruct((2 * rows, D), BF),
            jax.ShapeDtypeStruct((2 * rows, D), BF),
            jax.ShapeDtypeStruct((16, D), F32),
        ],
        earlier,
        part,
        scratch_shapes=[
            pltpu.VMEM((2, rows, 128), BF),
            pltpu.VMEM((2, rows, 128), BF),
            pltpu.VMEM((128, rows), BF),
            pltpu.VMEM((128, rows), BF),
            pltpu.VMEM((128, 2 * rows), BF),
            pltpu.VMEM((128, rows), F32),
            pltpu.VMEM((rows, 128), F32),
            pltpu.VMEM((2 * rows, 128), F32),
            pltpu.VMEM((2 * rows, 128), F32),
        ],
        cost_estimate=cost(
            5 * 2 * 12 * rows * rows * 1.5 * 256 / PARTS,
            rows * D * 40 / PARTS,
            12 * rows * rows * 1.5 / PARTS,
        ),
        name="att_bwd",
    )(state, *mixed, attended, logs, grad, projected, projected, projected, projected,
      taps, taps, taps, *earlier)


def unit_rows(x):
    return x * lax.rsqrt(jnp.mean(x * x, axis=-1, keepdims=True) + norm_eps)


def before_bwd_kernel(x_ref, dt_ref, dk_ref, dv_ref, w_ref, out_ref, gain_ref):
    i = pl.program_id(0)
    hat = unit_rows(x_ref[...].astype(F32))
    gn = dot_nt(dk_ref[...], w_ref[D : 2 * D, :]) + dot_nt(dv_ref[...], w_ref[2 * D : 3 * D, :])

    @pl.when(i == 0)
    def _():
        out_ref[...] = gn.astype(BF)
        gain_ref[...] = jnp.sum(gn * hat, axis=0, keepdims=True)

    @pl.when(i > 0)
    def _():
        last = gn.shape[0] - 8
        full = jnp.concatenate([gn[:last], gn[last:] + dot_nt(dt_ref[...], w_ref[0:D, :])], 0)
        out_ref[...] = full.astype(BF)
        gain_ref[...] += jnp.sum(full * hat, axis=0, keepdims=True)


def before_bwd(x_both, back, weight, rows):
    dt, dk, dv = back[1:]
    height = rows // 2
    step = pl.BlockSpec((height, D), lambda i: (i, 0))

    def whole(shape):
        return pl.BlockSpec(shape, lambda i: (0, 0))

    return pl.pallas_call(
        before_bwd_kernel,
        grid=(2,),
        in_specs=[step, whole((8, D)), step, step, whole((3 * D, D))],
        out_specs=[step, whole((1, D))],
        out_shape=[jax.ShapeDtypeStruct((rows, D), BF), jax.ShapeDtypeStruct((1, D), F32)],
        compiler_params=pltpu.CompilerParams(vmem_limit_bytes=VMEM_LIMIT),
        cost_estimate=cost(2 * rows * D * D * 2, rows * D * 12),
        name="before_bwd",
    )(x_both, dt, dk, dv, weight)


def qkv_bwd_kernel(
    core_ref, x_ref, dq_ref, dt_ref, dk_ref, dv_ref, w_ref, gain_ref, gain_one_ref, gain_two_ref, tg_ref,
    *refs, pieces, blocks,
):
    if pieces:
        send_ref, keep_ref, own_ref, acc, gacc = refs
    else:
        keep_ref, small_ref, own_ref, acc, gacc = refs
    i = pl.program_id(0)
    half = blocks // 2

    @pl.when(i == 0)
    def _():
        acc[...] = jnp.zeros(acc.shape, F32)
        gacc[0:1, :] = gain_one_ref[...]

    hat = unit_rows(x_ref[...].astype(F32))
    low = (hat * gain_ref[...]).astype(BF)
    dk = dk_ref[...]
    dv = dv_ref[...]
    acc[D : 2 * D, :] += dot_tn(low, dk)
    acc[2 * D : 3 * D, :] += dot_tn(low, dv)

    @pl.when(i == half - 1)
    def _():
        acc[0:D, :] += dot_tn(low[low.shape[0] - 8 :], dt_ref[...])

    @pl.when(i >= half)
    def _():
        dq = dq_ref[...]
        acc[0:D, :] += dot_tn(low, dq)
        full = (
            dot_nt(dk, w_ref[D : 2 * D, :])
            + dot_nt(dv, w_ref[2 * D : 3 * D, :])
            + dot_nt(dq, w_ref[0:D, :])
        )
        own_ref[...] = full
        gacc[0:1, :] += jnp.sum(full * hat, axis=0, keepdims=True)

    @pl.when(i == blocks - 1)
    def _():
        small = jnp.concatenate(
            [gacc[0:1, :], gain_two_ref[...], tg_ref[0:9, :], jnp.zeros((5, D), F32)], 0
        )
        if pieces:
            core = core_ref[0]
            height = 3 * D // (2 * pieces)
            wide = height + 16
            for j in range(pieces):
                to = pl.ds(j * wide, wide)
                away = pl.ds(pl.multiple_of((2 * j + 1 - core) * height, 16), wide)
                here = pl.ds(pl.multiple_of((2 * j + core) * height, 16), wide)
                send_ref[to, :] = acc[away, :].astype(BF)
                keep_ref[to, :] = acc[here, :]
            send_ref[pieces * wide :, :] = small.astype(BF)
            keep_ref[pieces * wide :, :] = small
        else:
            keep_ref[...] = acc[0 : 3 * D, :].astype(BF)
            small_ref[...] = small


def qkv_bwd(core, x_both, back, weight, gain, gain_one_grad, gain_two_grad, tap_grads, rows, pieces):
    dq, dt, dk, dv = back
    blocks = 4
    half = blocks // 2
    height = 2 * rows // blocks
    step = pl.BlockSpec((height, D), lambda i: (i, 0))
    late = pl.BlockSpec((height, D), lambda i: (jnp.maximum(i - half, 0), 0))

    def whole(shape):
        return pl.BlockSpec(shape, lambda i: (0, 0))

    if pieces:
        packed = 3 * D // 2 + 16 * pieces + 16
        outs = [jax.ShapeDtypeStruct((packed, D), BF), jax.ShapeDtypeStruct((packed, D), F32)]
        out_at = [whole((packed, D))] * 2
    else:
        outs = [jax.ShapeDtypeStruct((3 * D, D), BF), jax.ShapeDtypeStruct((16, D), F32)]
        out_at = [whole((3 * D, D)), whole((16, D))]

    def body(*refs):
        qkv_bwd_kernel(*refs, pieces=pieces, blocks=blocks)

    return pl.pallas_call(
        body,
        grid=(blocks,),
        in_specs=[
            pl.BlockSpec(memory_space=pltpu.SMEM),
            step, late, whole((8, D)), step, step, whole((3 * D, D)),
            whole((1, D)), whole((1, D)), whole((1, D)), whole((16, D)),
        ],
        out_specs=out_at + [late],
        out_shape=outs + [jax.ShapeDtypeStruct((rows, D), F32)],
        scratch_shapes=[pltpu.VMEM((3 * D + 16, D), F32), pltpu.VMEM((8, D), F32)],
        compiler_params=pltpu.CompilerParams(vmem_limit_bytes=VMEM_LIMIT),
        cost_estimate=cost(2 * 2 * D * D * 4 * rows, rows * D * 30),
        name="qkv_bwd",
    )(core, x_both, dq, dt, dk, dv, weight, gain, gain_one_grad, gain_two_grad, tap_grads)


def merge(index, keep, got, height, taken):
    rows = keep.shape[0]
    out_rows = taken * height + 16 if taken else rows

    def body(index_ref, keep_ref, got_ref, send_ref, stay_ref):
        if not taken:
            total = keep_ref[...] + got_ref[...].astype(F32)
            send_ref[...] = total.astype(BF)
            stay_ref[...] = total
            return
        for j in range(taken):
            to = pl.ds(j * height, height)
            away = pl.ds(pl.multiple_of(index_ref[j] * height, 16), height)
            here = pl.ds(pl.multiple_of(index_ref[taken + j] * height, 16), height)
            send_ref[to, :] = (keep_ref[away, :] + got_ref[away, :].astype(F32)).astype(BF)
            stay_ref[to, :] = keep_ref[here, :] + got_ref[here, :].astype(F32)
        end = keep_ref[rows - 16 :, :] + got_ref[rows - 16 :, :].astype(F32)
        send_ref[taken * height :, :] = end.astype(BF)
        stay_ref[taken * height :, :] = end

    vmem = pl.BlockSpec(memory_space=pltpu.VMEM)
    return pl.pallas_call(
        body,
        in_specs=[pl.BlockSpec(memory_space=pltpu.SMEM), vmem, vmem],
        out_specs=[vmem, vmem],
        out_shape=[
            jax.ShapeDtypeStruct((out_rows, D), BF),
            jax.ShapeDtypeStruct((out_rows, D), F32),
        ],
        compiler_params=pltpu.CompilerParams(vmem_limit_bytes=32 << 20),
        cost_estimate=cost(rows * D, rows * D * 12),
        name="merge",
    )(index, keep, got)


def merge_grid(index, keep, got, taken):
    height = keep.shape[1]

    def body(index_ref, ka_ref, ga_ref, kb_ref, gb_ref, send_ref, stay_ref):
        send_ref[...] = (ka_ref[...].astype(F32) + ga_ref[...].astype(F32)).astype(BF)
        stay_ref[...] = kb_ref[...].astype(F32) + gb_ref[...].astype(F32)

    away = pl.BlockSpec((1, height, D), lambda i, index: (index[i], 0, 0))
    here = pl.BlockSpec((1, height, D), lambda i, index: (index[taken + i], 0, 0))
    step = pl.BlockSpec((1, height, D), lambda i, index: (i, 0, 0))
    return pl.pallas_call(
        body,
        grid_spec=pltpu.PrefetchScalarGridSpec(
            num_scalar_prefetch=1,
            grid=(taken,),
            in_specs=[away, away, here, here],
            out_specs=[step, step],
        ),
        out_shape=[
            jax.ShapeDtypeStruct((taken, height, D), BF),
            jax.ShapeDtypeStruct((taken, height, D), F32),
        ],
        compiler_params=pltpu.CompilerParams(vmem_limit_bytes=32 << 20),
        cost_estimate=cost(taken * height * D * 2, taken * height * D * 16),
        name="merge_grid",
    )(index, keep, got, keep, got)


def arrange(index, one, two, taken):
    half = one.shape[0]
    height = one.shape[1]

    def body(index_ref, one_ref, two_ref, out_ref):
        for i in range(taken):
            at = index_ref[i]

            @pl.when(at < half)
            def _():
                out_ref[i] = one_ref[jnp.minimum(at, half - 1)]

            @pl.when(at >= half)
            def _():
                out_ref[i] = two_ref[jnp.maximum(at - half, 0)]

    vmem = pl.BlockSpec(memory_space=pltpu.VMEM)
    return pl.pallas_call(
        body,
        in_specs=[pl.BlockSpec(memory_space=pltpu.SMEM), vmem, vmem],
        out_specs=vmem,
        out_shape=jax.ShapeDtypeStruct((taken, height, D), BF),
        compiler_params=pltpu.CompilerParams(vmem_limit_bytes=32 << 20),
        cost_estimate=cost(taken * height * D, taken * height * D * 8),
        name="arrange",
    )(index, one, two)


def join(own, got, shared=16):
    rows = own.shape[0]
    body_rows = rows - shared

    def body(own_ref, got_ref, out_ref):
        out_ref[0:body_rows, :] = own_ref[0:body_rows, :]
        out_ref[body_rows : 2 * body_rows, :] = got_ref[0:body_rows, :]
        if shared:
            out_ref[2 * body_rows :, :] = own_ref[body_rows:, :] + got_ref[body_rows:, :]

    vmem = pl.BlockSpec(memory_space=pltpu.VMEM)
    return pl.pallas_call(
        body,
        in_specs=[vmem, vmem],
        out_specs=vmem,
        out_shape=jax.ShapeDtypeStruct((2 * body_rows + shared, D), BF),
        compiler_params=pltpu.CompilerParams(vmem_limit_bytes=32 << 20),
        cost_estimate=cost(rows * D, rows * D * 8),
        name="join",
    )(own, got)


def qkv_fwd_kernel(index_ref, x_ref, *refs, pieces, blocks):
    if pieces:
        own_ref, got_ref, out_ref, small_ref, weight = refs
    else:
        weight, given_ref, out_ref, small_ref = refs
    i = pl.program_id(0)

    @pl.when(i == 0)
    def _():
        if pieces:
            height = 3 * D // (2 * pieces)
            for j in range(pieces):
                at = pl.ds(j * height, height)
                for k, ref in enumerate((own_ref, got_ref)):
                    to = pl.multiple_of(index_ref[k * pieces + j] * height, 16)
                    weight[pl.ds(to, height), :] = ref[at, :]
            end = pl.ds(pieces * height, 16)
            small_ref[...] = own_ref[end, :].astype(F32) + got_ref[end, :].astype(F32)
        else:
            small_ref[...] = given_ref[...]

    x = x_ref[...].astype(F32)
    hat = x * lax.rsqrt(jnp.mean(x * x, axis=-1, keepdims=True) + norm_eps)
    low = (hat * small_ref[0:1, :]).astype(BF)

    @pl.when(i >= blocks // 2 - 1)
    def _():
        out_ref[:, 0:D] = dot(low, weight[0:D, :]).astype(BF)

    out_ref[:, D : 2 * D] = dot(low, weight[D : 2 * D, :]).astype(BF)
    out_ref[:, 2 * D : 3 * D] = dot(low, weight[2 * D : 3 * D, :]).astype(BF)


def qkv_fwd(index, x_both, weights, rows, pieces):
    blocks = 4
    height = 2 * rows // blocks

    def body(*refs):
        qkv_fwd_kernel(*refs, pieces=pieces, blocks=blocks)

    return pl.pallas_call(
        body,
        grid=(blocks,),
        in_specs=[
            pl.BlockSpec(memory_space=pltpu.SMEM),
            pl.BlockSpec((height, D), lambda i: (i, 0)),
            *[pl.BlockSpec(w.shape, lambda i: (0, 0)) for w in weights],
        ],
        out_specs=[
            pl.BlockSpec((height, 3 * D), lambda i: (i, 0)),
            pl.BlockSpec((16, D), lambda i: (0, 0)),
        ]
        + ([pl.BlockSpec((3 * D, D), lambda i: (0, 0))] if pieces else []),
        out_shape=[
            jax.ShapeDtypeStruct((2 * rows, 3 * D), BF),
            jax.ShapeDtypeStruct((16, D), F32),
        ]
        + ([jax.ShapeDtypeStruct((3 * D, D), BF)] if pieces else []),
        compiler_params=pltpu.CompilerParams(vmem_limit_bytes=VMEM_LIMIT),
        cost_estimate=cost(2 * 2 * rows * D * 3 * D, rows * D * 20),
        name="qkv_fwd",
    )(index, x_both, *weights)


def ffn_kernel(
    state_ref, index_ref, x_ref, att_ref, cot_ref, gain_ref, own_ref, got_ref,
    out_ref, gh_ref, ga_ref, gain_grad_ref, away_ref, here_ref,
    hidden, low, total, back, cot, sq, gb, weights, stage_up, stage_down, stage_out, in_sems, sems,
):
    c = pl.program_id(0)
    rows = x_ref.shape[0]
    blocks = [pl.ds(i * QB, QB) for i in range(rows // QB)]
    last = c == pl.num_programs(0) - 1
    core = index_ref[24]

    def fetch(k, j):
        ref = own_ref if k == 0 else got_ref
        to = weights.at[pl.ds(3 * index_ref[12 * k + j], 3)]
        return pltpu.make_async_copy(ref.at[pl.ds(3 * j, 3)], to, in_sems.at[12 * k + j])

    def put(source, group, count, column, sem, wait=False):
        piece = group // 3
        at = (piece // 2) * 3 + group % 3

        def copy(ref):
            to = ref.at[pl.ds(at, count)] if column is None else ref.at[pl.ds(at, count), column]
            return pltpu.make_async_copy(source, to, sems.at[sem])

        if wait:
            copy(here_ref).wait()
            return
        mine = piece % 2 == core

        @pl.when(mine)
        def _():
            copy(here_ref).start()

        @pl.when(jnp.logical_not(mine))
        def _():
            copy(away_ref).start()

    def put_up(i, wait=False):
        start = 0
        k = 0
        while start < 32:
            count = min(3 - (8 + start) % 3, 32 - start)
            put(stage_up.at[i, pl.ds(start, count)], 8 + start, count, i, 20 * i + k, wait)
            start += count
            k += 1

    def put_down(i, wait=False):
        for k in range(8):
            put(stage_down.at[i, pl.ds(k, 1)], 40 + 8 * i + k, 1, None, 20 * i + 12 + k, wait)

    def put_out(wait=False):
        for k in range(8):
            put(stage_out.at[pl.ds(k, 1)], k, 1, None, 80 + k, wait)

    def square(first):
        return weights[first : first + 8].reshape(D, D)

    @pl.when(c == 0)
    def _():
        for k in range(2):
            for j in range(12):
                fetch(k, j).start()
        cot[...] = jnp.where(state_ref[0] > 0, cot_ref[...], jnp.zeros((), BF))
        total[...] = jnp.zeros(total.shape, F32)
        back[...] = jnp.zeros(back.shape, F32)
        for k in range(2):
            for j in range(12):
                fetch(k, j).wait()
        wo = square(0)
        for b in blocks:
            h = x_ref[b, :].astype(F32) + dot(att_ref[b, :], wo)
            hidden[b, :] = h
            hat = h * lax.rsqrt(jnp.mean(h * h, axis=-1, keepdims=True) + norm_eps)
            low[b, :] = (hat * gain_ref[...]).astype(BF)

    up = weights[8:40, c].reshape(D, D)
    down = weights[pl.ds(40 + 8 * c, 8)].reshape(D, D)
    for b in blocks:
        act = jnp.maximum(dot(low[b, :], up), 0.0)
        s = (act * act).astype(BF)
        sq[b, :] = s
        total[b, :] += dot(s, down)
        g = (dot_nt(cot[b, :], down) * 2.0 * act).astype(BF)
        gb[b, :] = g
        back[b, :] += dot_nt(g, up)
    stage_down[c] = dot_tn(sq[...], cot[...]).reshape(8, 4, 24, D).astype(BF)
    stage_up[c] = dot_tn(low[...], gb[...]).reshape(32, 24, D).astype(BF)
    put_down(c)
    put_up(c)

    @pl.when(last)
    def _():
        gain = gain_ref[...]
        wo = square(0)
        sums = jnp.zeros((1, D), F32)
        for b in blocks:
            h = hidden[b, :]
            out_ref[b, :] = (h + total[b, :]).astype(BF)
            factor = lax.rsqrt(jnp.mean(h * h, axis=-1, keepdims=True) + norm_eps)
            hat = h * factor
            g = back[b, :]
            sums = sums + jnp.sum(g * hat, axis=0, keepdims=True)
            weighted = g * gain
            inner = jnp.mean(weighted * hat, axis=-1, keepdims=True)
            grad = cot[b, :].astype(F32) + factor * (weighted - hat * inner)
            gh_ref[b, :] = grad
            grad_low = grad.astype(BF)
            gb[b, :] = grad_low
            ga_ref[b, :] = dot_nt(grad_low, wo).astype(BF)
        gain_grad_ref[...] = sums
        stage_out[...] = dot_tn(att_ref[...], gb[...]).reshape(8, 4, 24, D).astype(BF)
        put_out()
        for i in range(4):
            put_down(i, True)
            put_up(i, True)
        put_out(True)


def ffn(state, index, tokens, attended, out_grad, gain, own, got, rows):
    def whole(shape):
        return pl.BlockSpec(shape, lambda c: (0,) * len(shape), pipeline_mode=pl.Buffered(1))

    act = whole((rows, D))
    held = pl.BlockSpec(memory_space=pl.ANY)
    scalars = pl.BlockSpec(memory_space=pltpu.SMEM)
    half = (36, 4, 24, D)
    return pl.pallas_call(
        ffn_kernel,
        grid=(4,),
        in_specs=[scalars, scalars, act, act, act, whole((1, D)), held, held],
        out_specs=[act, act, act, whole((1, D)), held, held],
        out_shape=[
            jax.ShapeDtypeStruct((rows, D), BF),
            jax.ShapeDtypeStruct((rows, D), F32),
            jax.ShapeDtypeStruct((rows, D), BF),
            jax.ShapeDtypeStruct((1, D), F32),
            jax.ShapeDtypeStruct(half, BF),
            jax.ShapeDtypeStruct(half, BF),
        ],
        scratch_shapes=[
            pltpu.VMEM((rows, D), F32),
            pltpu.VMEM((rows, D), BF),
            pltpu.VMEM((rows, D), F32),
            pltpu.VMEM((rows, D), F32),
            pltpu.VMEM((rows, D), BF),
            pltpu.VMEM((rows, D), BF),
            pltpu.VMEM((rows, D), BF),
            pltpu.VMEM((72, 4, 24, D), BF),
            pltpu.VMEM((4, 32, 24, D), BF),
            pltpu.VMEM((4, 8, 4, 24, D), BF),
            pltpu.VMEM((8, 4, 24, D), BF),
            pltpu.SemaphoreType.DMA((24,)),
            pltpu.SemaphoreType.DMA((88,)),
        ],
        compiler_params=pltpu.CompilerParams(vmem_limit_bytes=60 << 20),
        cost_estimate=cost(2 * rows * D * D * (24 + 3), 2 * 12 * D * D * 2 + rows * D * 16),
        name="ffn",
    )(state, index, tokens, attended, out_grad, gain, own, got)


def shift_flat(block, distance):
    count = lax.axis_size(AXES)
    route = [(i - distance, i) for i in range(count) if 0 <= i - distance < count]
    return lax.ppermute(block, AXES, route)


def shift_ctx(block, distance):
    count = lax.axis_size("ctx")
    route = [(i - distance, i) for i in range(count) if 0 <= i - distance < count]
    return lax.ppermute(block, "ctx", route)


def after(value, *others):
    return lax.optimization_barrier((value, *others))[0]


def swap(block, even_bit, odd_bit, planes=None):
    count = lax.axis_size(AXES)
    route = [
        (i, i ^ (odd_bit if i & 1 else even_bit))
        for i in range(count)
        if planes is None or i >> 3 in planes
    ]
    return lax.ppermute(block, AXES, route)


def to_aligned(shard, place, count, delta):
    rows = shard.shape[0]
    lag = delta * (count - 1)
    back = -(-lag // rows)
    if back == 1:
        keep = -(-lag // 8) * 8
        parts = [shift_flat(shard[rows - keep :], 1), shard]
    else:
        keep = back * rows
        parts = [shift_flat(shard, s) for s in range(back, 0, -1)] + [shard]
    joined = jnp.concatenate(parts, 0)
    return lax.dynamic_slice_in_dim(joined, keep - delta * place, rows - delta, 0)


def small_part(shard, place, count, delta):
    rows = shard.shape[0]
    extra = count * delta
    zeros = jnp.zeros((extra, 128), shard.dtype)
    joined = jnp.concatenate([zeros, shard, zeros], 0)
    start = extra + count * (rows - delta) - place * rows
    return lax.dynamic_slice_in_dim(joined, jnp.minimum(start, rows + extra), extra, 0)


def from_aligned(chunk, small, place, count, delta, rows):
    aligned = rows - delta
    ahead = -(-(count * delta) // aligned)
    parts = [chunk]
    if ahead == 1:
        keep = small.shape[0]
        got = shift_flat(chunk[:keep], -1)
        parts.append(jnp.where(place == count - 1, small, got))
    else:
        pad = ahead * aligned - small.shape[0]
        tail = jnp.concatenate([small, jnp.zeros((pad, 128), small.dtype)], 0)
        for s in range(1, ahead + 1):
            got = shift_flat(chunk, -s)
            for e in range(s):
                piece = tail[e * aligned : (e + 1) * aligned]
                got = jnp.where(place == count - s + e, piece, got)
            parts.append(got)
    return lax.dynamic_slice_in_dim(jnp.concatenate(parts, 0), delta * place, rows, 0)


def regroup(block):
    return block.reshape(-1, 24, 4, D).transpose(0, 2, 1, 3)


def ungroup(block):
    return block.reshape(-1, 4, 24, D).transpose(0, 2, 1, 3)


def normalize(values, gain):
    factor = lax.rsqrt(jnp.mean(values * values, axis=-1, keepdims=True) + norm_eps)
    scaled = values * factor
    return (scaled, factor, scaled * gain)


def norm_back(grad_in, scaled, factor, gain):
    weighted = grad_in * gain
    inner_mean = jnp.mean(weighted * scaled, axis=-1, keepdims=True)
    return factor * (weighted - scaled * inner_mean)


def adam_update(master, moment_one, moment_two, gradient, step_count, row_start):
    row_index = row_start + jnp.arange(master.shape[0], dtype=jnp.int32)
    matrix_rows = (4 * D * D + 2 * D * FF) // 128
    out_first = 3 * D * D // 128
    out_last = 4 * D * D // 128
    is_matrix = (row_index < matrix_rows)[:, None]
    is_out = ((row_index >= out_first) & (row_index < out_last))[:, None]
    step_rate = jnp.where(is_matrix, jnp.where(is_out, 0.5, 0.1), 1.0)
    decay_rate = jnp.where(is_matrix, 0.1, 0.0)
    step_value = step_count[0].astype(jnp.float32)
    new_one = 0.9 * moment_one + 0.1 * gradient
    new_two = 0.999 * moment_two + 0.001 * gradient * gradient
    corr_first = 1.0 - jnp.power(0.9, step_value)
    corr_second = 1.0 - jnp.power(0.999, step_value)
    new_weights = master - step_rate * (
        new_one / corr_first / (jnp.sqrt(new_two / corr_second) + 1e-08) + decay_rate * master
    )
    return (new_weights, new_one, new_two)


def shards(tokens, out_grad, positions, master, first_moment, second_moment, step_count):
    rows = tokens.shape[0]
    assert rows == SEQ_MIN
    count = lax.axis_size(AXES)
    place = lax.axis_index(AXES).astype(jnp.int32)
    owned = master.shape[0]
    aligned = (4 * D * D + 2 * D * FF) // 128 // count
    delta = owned - aligned
    height = aligned * 128 // D
    staged = count == 32
    first_place = positions[0]
    state = jnp.where(first_place < 0, 0, jnp.where(first_place >= SEQ_MIN, 2, 1)).astype(jnp.int32)
    state_vec = state[None]

    tokens_before = shift_ctx(tokens, 1)
    chunk = to_aligned(master, place, count, delta).reshape(-1, D)
    if staged:
        group = 3 * place + jnp.arange(3, dtype=jnp.int32)
        in_up = ((group >= 32) & (group < 64))[:, None, None, None]
        chunk = jnp.where(in_up, regroup(chunk), chunk.reshape(3, 4, 24, D)).reshape(-1, D)
    chunk = chunk.astype(BF)
    small = lax.reduce_precision(small_part(master, place, count, delta), 8, 7)
    core = (place & 1)[None]
    x_bit = (place >> 1) & 1
    y_bit = (place >> 2) & 1
    even = (place & 1) == 0
    tokens_both = jnp.concatenate([tokens_before, tokens], 0)
    if staged:
        z = place >> 3
        mine = jnp.concatenate([chunk, small.astype(BF).reshape(-1, D)], 0)
        got = swap(mine, 16, 16)
        got = after(got, tokens_both)
        rest = jnp.concatenate([chunk, got[:height]], 0)
        none = jnp.zeros((), BF)
        first = jnp.where(z == 0, chunk, jnp.where(z == 2, got[:height], none))
        mine = jnp.concatenate([first, mine[height:] + got[height:]], 0)
        mine = mine + swap(mine, 8, 8)
        across = swap(after(rest, mine), 8, 8)
        mine = join(mine, swap(mine, 2, 4))
        mine = join(mine, swap(mine, 4, 2))
        codes = [z ^ k for k in (1, 2, 3)]
        order = [jnp.where(j == 1, 2, jnp.where(j == 2, 1, j)) for j in codes]
        rest = arrange(
            jnp.stack(order).astype(jnp.int32), rest.reshape(2, height, D), across.reshape(2, height, D), 3
        ).reshape(-1, D)
        across = swap(rest, 2, 4)
        got = swap(after(mine, rest), 1, 1)
        index = []
        late_index = []
        for k in (0, 1):
            turn = even if k == 0 else jnp.logical_not(even)
            for j in range(4):
                near, far = j & 1, j >> 1
                x_of = x_bit ^ jnp.where(turn, near, far)
                y_of = y_bit ^ jnp.where(turn, far, near)
                piece = 4 * y_of + 2 * x_of + (core[0] ^ k)
                index.append(piece)
                late_index += [piece, piece + 8, piece + 16]
        index = jnp.stack(index).astype(jnp.int32)
        late_index = jnp.stack(late_index + [core[0]]).astype(jnp.int32)
        projected, small, in_weight = qkv_fwd(index, tokens_both, (mine, got), rows, 4)
    else:
        wide = lax.all_gather(chunk, AXES, axis=0, tiled=True)
        small = lax.psum(small, AXES)[:96].reshape(-1, D)
        in_weight = wide[: 3 * D]
        projected, small = qkv_fwd(core, tokens_both, (in_weight, small), rows, 0)
        late_index = jnp.arange(25, dtype=jnp.int32) % 24
    gain_first = small[0]
    gain_second = small[1]
    taps = small[2:11].reshape(3, 3 * D)

    forward = []
    if staged:
        rest = join(after(rest, projected), across, 0)
        across = swap(rest, 4, 2)
        forward = att_fwd(after(state_vec, rest), projected, taps, forward, 0, rows)
        forward = att_fwd(state_vec, projected, taps, forward, 1, rows)
        rest = join(after(rest, forward[0]), across, 0)
        across = swap(rest, 1, 1)
        forward = att_fwd(after(state_vec, rest), projected, taps, forward, 2, rows)
        own_weights, got_weights = rest.reshape(36, 4, 24, D), across.reshape(36, 4, 24, D)
    else:
        for part in range(PARTS):
            forward = att_fwd(state_vec, projected, taps, forward, part, rows)
        grouped = jnp.concatenate(
            [
                wide[3 * D : 4 * D].reshape(-1, 4, 24, D),
                regroup(wide[4 * D : 8 * D]),
                wide[8 * D :].reshape(-1, 4, 24, D),
            ],
            0,
        )
        own_weights, got_weights = grouped[:36], grouped[36:]
    attn_low, logs, *mixed = forward

    layer_out, grad_hidden, grad_attended, grad_gain_two, away_grad, here_grad = ffn(
        state_vec, late_index, tokens, attn_low, out_grad, gain_second[None], own_weights, got_weights, rows
    )

    def backward(start, done, part):
        return att_bwd(
            start, mixed, attn_low, logs, grad_attended, projected, taps, done, part, rows
        )

    if staged:
        stay = [jnp.where(even, 2 * j + x_bit, 2 * y_bit + j) for j in range(2)]
        away = [jnp.where(even, 2 * j + 1 - x_bit, 2 * (1 - y_bit) + j) for j in range(2)]
        pick_plane = jnp.stack(away + stay).astype(jnp.int32)
        other = jnp.where(even, y_bit, x_bit)
        pick_line = jnp.stack([1 - other, other]).astype(jnp.int32)

        def of_quarters(pick, held):
            half = pick.shape[0] // 2
            steps = [pick[s * half + j] + held * t for s in range(2) for t in range(3) for j in range(half)]
            return jnp.stack(steps)

        late_keep = here_grad.reshape(12, height, D)
        late_got = swap(away_grad.reshape(12, height, D), 1, 1)
        done = backward(state_vec, [], 0)
        late_send, late_keep = merge_grid(
            after(of_quarters(pick_plane, 4), done[4]), late_keep, late_got, 6
        )
        late_got = swap(late_send, 2, 4)
        done = backward(after(state_vec, late_send), done, 1)
        late_send, late_keep = merge_grid(
            after(of_quarters(pick_line, 2), done[4]), late_keep, late_got, 3
        )
        late_got = swap(late_send, 4, 2)
        done = backward(after(state_vec, late_send), done, 2)
        z_even = (z & 1) == 0
        low_pair = [jnp.where(z_even, 0, 0), jnp.where(z_even, 2, 1)]
        high_pair = [jnp.where(z_even, 0, 0), jnp.where(z_even, 1, 2)]
        pick_z = jnp.stack(low_pair + high_pair).astype(jnp.int32)
        late_send, late_keep = merge_grid(after(pick_z, done[4]), late_keep, late_got, 2)
        late_got = swap(late_send, 8, 8)
        sums_state = after(core, late_send)
    else:
        done = []
        for part in range(PARTS):
            done = backward(state_vec, done, part)
        sums_state = core
    *back, tap_grads = done
    grads_before, gain_one_grad = before_bwd(tokens_both, back, in_weight, rows)
    from_next = shift_ctx(grads_before, -1)
    sums = qkv_bwd(
        after(sums_state, grads_before), tokens_both, back, in_weight, gain_first[None], gain_one_grad, grad_gain_two, tap_grads, rows,
        4 if staged else 0,
    )
    grad_normed_one = sums[2]
    scaled_one, factor_one, _ = normalize(tokens.astype(F32), gain_first)
    input_grad = grad_hidden + norm_back(
        grad_normed_one + from_next.astype(F32), scaled_one, factor_one, gain_first
    )

    if staged:
        send, keep = sums[:2]
        high = z >> 1
        pick_last = jnp.stack([1 - high, high]).astype(jnp.int32)
        late_send, late_keep = merge_grid(after(pick_last, send), late_keep, late_got, 1)
        late_got = swap(late_send, 16, 16, (0, 1, 3))
        got = swap(after(send, late_send, from_next), 1, 1)
        send, keep = merge(pick_plane, keep, got, height + 16, 2)
        got = swap(send, 2, 4)
        send, keep = merge(pick_line, keep, got, height + 16, 1)
        got = swap(send, 4, 2)
        send, keep = merge(core, keep, got, height + 16, 0)
        got = swap(send, 8, 8)
        late_chunk = late_keep[0] + late_got[0].astype(F32)
        late_chunk = jnp.where(in_up, ungroup(late_chunk).reshape(3, 4, 24, D), late_chunk.reshape(3, 4, 24, D))
        late_chunk = late_chunk.reshape(-1, D)
        late_next = shift_flat(late_chunk[:16], -1)
        send, keep = merge(after(core, late_next, input_grad), keep, got, height + 16, 0)
        got = swap(send, 16, 16, (1, 2))
        first = keep + got.astype(F32)
        quarter = count // 4
        follow = jnp.where(place < quarter - 1, first[height : height + 16], late_next)
        follow = jnp.where(place == count - 1, first[height + 16 :], follow)
        chunk_grad = jnp.where(place < quarter, first[:height], late_chunk)
        chunk_grad = jnp.concatenate([chunk_grad, follow], 0).reshape(-1, 128)
        gradient = lax.dynamic_slice_in_dim(chunk_grad, delta * place, owned, 0)
    else:
        flat_grad = jnp.stack([here_grad.reshape(12, 3, 4, 24, D), away_grad.reshape(12, 3, 4, 24, D)], 1)
        flat_grad = flat_grad.reshape(72, 4, 24, D)
        wide_grad = jnp.concatenate(
            [
                sums[0],
                flat_grad[:8].reshape(-1, D),
                ungroup(flat_grad[8:40]).reshape(-1, D),
                flat_grad[40:].reshape(-1, D),
            ],
            0,
        )
        chunk_grad = lax.psum_scatter(wide_grad, AXES, scatter_dimension=0, tiled=True).astype(F32)
        used = sums[1].reshape(-1, 128)
        extra = count * delta
        small_grad = jnp.concatenate([used, jnp.zeros((extra - used.shape[0], 128), F32)], 0)
        small_grad = lax.psum(small_grad, AXES)
        gradient = from_aligned(chunk_grad.reshape(-1, 128), small_grad, place, count, delta, owned)
    new_weights, new_one, new_two = adam_update(
        master, first_moment, second_moment, gradient, step_count, place * owned
    )
    return (layer_out, input_grad, new_weights, new_one, new_two, new_weights.astype(BF))


def solution(mesh):
    spread = P(AXES, None)
    return jax.shard_map(
        shards,
        mesh=mesh,
        in_specs=(spread, spread, P(AXES), spread, spread, spread, P()),
        out_specs=(spread,) * 6,
        check_vma=False,
    )
```

```python
import jax
import jax.numpy as jnp
from jax import lax
from jax.experimental import pallas as pl
from jax.experimental.pallas import tpu as pltpu
from jax.sharding import PartitionSpec as P

D = 768
HEADS = 12
HEAD_DIM = 64
FF = 3072
SEQ_MIN = 1024
AXES = ("dp", "ctx")
QB = 256
PARTS = 3
F32 = jnp.float32
BF = jnp.bfloat16
NT = (((1,), (1,)), ((), ()))
TN = (((0,), (0,)), ((), ()))
norm_eps = 1e-06
VMEM_LIMIT = 56 << 20


def dot(left, right):
    return jnp.dot(left, right, preferred_element_type=F32)


def dot_nt(left, right):
    return lax.dot_general(left, right, NT, preferred_element_type=F32)


def dot_tn(left, right):
    return lax.dot_general(left, right, TN, preferred_element_type=F32)


def cost(flops, nbytes, exps=0):
    return pl.CostEstimate(flops=int(flops), bytes_accessed=int(nbytes), transcendentals=int(exps))


def row_ids(height):
    return lax.broadcasted_iota(jnp.int32, (height, 128), 0)


def conv(out_ref, x_ref, start, tail_ref, taps, rows, state):
    height = x_ref.shape[0]
    for r in range(0, height, QB):
        at = start + r
        if r:
            x = x_ref[r - 16 : r + QB, :].astype(F32)
        else:
            before = jnp.zeros((16, 128), F32)
            if tail_ref is not None:
                before = jnp.concatenate([before[8:], tail_ref[...].astype(F32)], 0)
            x = jnp.concatenate([before, x_ref[0:QB, :].astype(F32)], 0)
        one = pltpu.roll(x, 1, 0)[16:]
        two = pltpu.roll(x, 2, 0)[16:]
        x = x[16:]
        scale = 1.0
        if at >= rows:
            scale = jnp.where(state > 0, 1.0, 0.0)
        if at == 0 or at == rows:
            seen = jnp.where(state == 2, 1.0, 0.0) if at else 0.0
            row = row_ids(QB)
            one = jnp.where(row < 1, one * seen, one)
            two = jnp.where(row < 2, two * seen, two)
        c_one = taps[1:2] * scale
        c_two = taps[2:3] * scale
        out_ref[r : r + QB, :] = (taps[0:1] * x + c_one * one + c_two * two).astype(BF)


def att_fwd_kernel(
    state_ref, tail_ref, q_ref, k_ref, v_ref, tq_ref, tk_ref, tv_ref,
    o_ref, l_ref, qm_ref, km_ref, vm_ref, ka, va,
):
    rows = q_ref.shape[0]
    lane = lax.broadcasted_iota(jnp.int32, (1, 128), 1)
    state = state_ref[0]
    conv(qm_ref, q_ref, rows, tail_ref, tq_ref[...], rows, state)
    conv(km_ref, k_ref, 0, None, tk_ref[...], rows, state)
    conv(vm_ref, v_ref, 0, None, tv_ref[...], rows, state)
    bias = jnp.where(state == 2, 0.0, -1e30)
    for h in range(2):
        mine = (lane < 64) if h == 0 else (lane >= 64)
        base = 64 if h == 0 else 0
        first = jnp.where(lane == base, bias, 0.0).astype(BF)
        for r in range(0, 2 * rows, QB):
            at = pl.ds(r, QB)
            ka[h, at, :] = jnp.where(mine, km_ref[at, :], first if r < rows else jnp.zeros((), BF))
            va[h, at, :] = jnp.where(mine, vm_ref[at, :], jnp.ones((), BF))
    for i in range(rows // QB):
        rs = pl.ds(i * QB, QB)
        outs = []
        sums = []
        qf = qm_ref[rs, :].astype(F32) * 0.125
        for h in range(2):
            mine = (lane < 64) if h == 0 else (lane >= 64)
            base = 64 if h == 0 else 0
            qh = jnp.where(mine, qf, jnp.where(lane == base, 1.0, 0.0)).astype(BF)
            nk = rows + (i + 1) * QB
            s = dot_nt(qh, ka[h, 0:nk, :])
            r = lax.broadcasted_iota(jnp.int32, (QB, QB), 0)
            c = lax.broadcasted_iota(jnp.int32, (QB, QB), 1)
            sd = jnp.where(c <= r, s[:, nk - QB :], -1e30)
            se = s[:, : nk - QB]
            m = jnp.maximum(
                jnp.max(sd, axis=1, keepdims=True), jnp.max(se, axis=1, keepdims=True)
            )
            p = jnp.concatenate([jnp.exp(se - m).astype(BF), jnp.exp(sd - m).astype(BF)], 1)
            o = dot(p, va[h, 0:nk, :])
            outs.append(o / pltpu.roll(o, 64, 1))
            sums.append(m + jnp.log(o))
        res = jnp.where(lane < 64, outs[0], outs[1])
        res = jnp.where(state == 0, vm_ref[pl.ds(rows + i * QB, QB), :].astype(F32), res)
        o_ref[rs, :] = res.astype(BF)
        l_ref[rs, :] = jnp.where(lane < 64, sums[1], sums[0])


def call_in_parts(body, in_specs, out_specs, out_shape, earlier, part, **options):
    used = len(in_specs)

    def kernel(*refs):
        body(*refs[:used], *refs[used + len(earlier) :])

    return pl.pallas_call(
        kernel,
        grid=(6 // PARTS,),
        in_specs=in_specs + [pl.BlockSpec(memory_space=pl.ANY)] * len(earlier),
        out_specs=out_specs,
        out_shape=out_shape,
        input_output_aliases={used + i: i for i in range(len(earlier))},
        compiler_params=pltpu.CompilerParams(vmem_limit_bytes=VMEM_LIMIT),
        **options,
    )


def columns(part):
    first = part * (6 // PARTS)

    def cols(height, row, off):
        return pl.BlockSpec((height, 128), lambda p: (row, p + first + off))

    taps_at = [
        pl.BlockSpec((3, 128), lambda p, off=off: (0, p + first + off)) for off in (0, 6, 12)
    ]
    return cols, taps_at


def att_fwd(state, projected, taps, earlier, part, rows):
    cols, taps_at = columns(part)
    return call_in_parts(
        att_fwd_kernel,
        [
            pl.BlockSpec(memory_space=pltpu.SMEM),
            cols(8, rows // 8 - 1, 0),
            cols(rows, 1, 0),
            cols(2 * rows, 0, 6),
            cols(2 * rows, 0, 12),
            *taps_at,
        ],
        [cols(rows, 0, 0)] * 3 + [cols(2 * rows, 0, 0)] * 2,
        [
            jax.ShapeDtypeStruct((rows, D), BF),
            jax.ShapeDtypeStruct((rows, D), F32),
            jax.ShapeDtypeStruct((rows, D), BF),
            jax.ShapeDtypeStruct((2 * rows, D), BF),
            jax.ShapeDtypeStruct((2 * rows, D), BF),
        ],
        earlier,
        part,
        scratch_shapes=[pltpu.VMEM((2, 2 * rows, 128), BF)] * 2,
        cost_estimate=cost(
            2 * 2 * 12 * rows * rows * 1.5 * 256 / PARTS,
            rows * D * 30 / PARTS,
            12 * rows * rows * 1.5 / PARTS,
        ),
        name="att_fwd",
    )(state, projected, projected, projected, projected, taps, taps, taps, *earlier)


def three(x, lane, base):
    hi = x.astype(BF).astype(F32)
    r = x - hi
    mid = r.astype(BF).astype(F32)
    lo = r - mid
    return jnp.where(
        lane == base, hi, jnp.where(lane == base + 1, mid, jnp.where(lane == base + 2, lo, 0.0))
    )


def conv_back(out_ref, grad_ref, x_ref, start, tail, taps, rows, state):
    height = grad_ref.shape[0]
    joint = jnp.where(state == 2, 1.0, 0.0)
    sums = [jnp.zeros((1, 128), F32)] * 3

    def add(parts, x):
        return [s + jnp.sum(g * x, axis=0, keepdims=True) for s, g in zip(sums, parts)]

    for r in range(0, height, QB):
        ends = r + QB == height
        meets = start + r + QB == rows
        if ends:
            grad = jnp.concatenate([grad_ref[r : r + QB, :], jnp.zeros((8, 128), F32)], 0)
        else:
            grad = grad_ref[r : r + QB + 8, :]
        one = pltpu.roll(grad, QB + 7, 0)[:QB]
        two = pltpu.roll(grad, QB + 6, 0)[:QB]
        grad = grad[:QB]
        if meets and not ends:
            row = row_ids(QB)
            one = jnp.where(row >= QB - 1, one * joint, one)
            two = jnp.where(row >= QB - 2, two * joint, two)
        out_ref[r : r + QB, :] = (taps[0:1] * grad + taps[1:2] * one + taps[2:3] * two).astype(BF)
        sums = add((grad, one, two), x_ref[r : r + QB, :].astype(F32))
    if tail is not None:
        grad = jnp.concatenate([jnp.zeros((8, 128), F32), grad_ref[0:8, :]], 0)
        one = pltpu.roll(grad, 15, 0)[:8] * joint
        two = pltpu.roll(grad, 14, 0)[:8] * joint
        tail[0][...] = (taps[1:2] * one + taps[2:3] * two).astype(BF)
        sums = add((grad[:8], one, two), tail[1][...].astype(F32))
    return sums


def att_bwd_kernel(
    state_ref, q_ref, k_ref, v_ref, o_ref, l_ref, do_ref, xt_ref, xq_ref, xk_ref, xv_ref,
    tq_ref, tk_ref, tv_ref,
    pq_ref, pt_ref, pk_ref, pv_ref, tg_ref, qa, da, qt, dt, kt, dqt, dqs, dks, dvs,
):
    rows = q_ref.shape[0]
    lane = lax.broadcasted_iota(jnp.int32, (1, 128), 1)
    second = state_ref[0] == 2
    for r in range(0, rows, QB):
        at = pl.ds(r, QB)
        do = do_ref[at, :].astype(F32)
        od = do * o_ref[at, :].astype(F32)
        qf = q_ref[at, :].astype(F32) * 0.125
        lv = l_ref[at, :]
        for h in range(2):
            mine = (lane < 64) if h == 0 else (lane >= 64)
            base = 64 if h == 0 else 0
            delta = jnp.sum(jnp.where(mine, od, 0.0), axis=1, keepdims=True)
            qa[h, at, :] = jnp.where(mine, qf, three(-lv, lane, base)).astype(BF)
            da[h, at, :] = jnp.where(mine, do, three(-delta, lane, base)).astype(BF)
        qt[:, at] = jnp.transpose(qf).astype(BF)
        dt[:, at] = jnp.transpose(do).astype(BF)
    for r in range(0, 2 * rows, QB):
        at = pl.ds(r, QB)
        kt[:, at] = jnp.transpose(k_ref[at, :].astype(F32)).astype(BF)
    dqt[...] = jnp.zeros(dqt.shape, F32)

    def keys(ks, first, diagonal):
        kk = k_ref[ks, :]
        vv = v_ref[ks, :]
        dv = []
        dk = []
        for h in range(2):
            mine = (lane < 64) if h == 0 else (lane >= 64)
            base = 64 if h == 0 else 0
            ones3 = ((lane >= base) & (lane < base + 3)).astype(BF)
            hs = slice(64 * h, 64 * h + 64)
            st = dot_nt(jnp.where(mine, kk, ones3), qa[h, first:rows, :])
            dp = dot_nt(jnp.where(mine, vv, ones3), da[h, first:rows, :])
            p = jnp.exp(st)
            if diagonal:
                r = lax.broadcasted_iota(jnp.int32, (QB, QB), 0)
                c = lax.broadcasted_iota(jnp.int32, (QB, QB), 1)
                seen = jnp.where(r <= c, p[:, :QB], 0.0)
                p = jnp.concatenate([seen, p[:, QB:]], 1) if first + QB < rows else seen
            ds = (p * dp).astype(BF)
            dv.append(dot_nt(dt[hs, first:rows], p.astype(BF)))
            dk.append(dot_nt(qt[hs, first:rows], ds))
            dqt[hs, first:rows] += dot(kt[hs, ks], ds)
        dvs[ks, :] = jnp.transpose(jnp.concatenate(dv, 0))
        dks[ks, :] = jnp.transpose(jnp.concatenate(dk, 0))

    for j in range(rows // QB):
        keys(pl.ds(rows + j * QB, QB), j * QB, True)

    @pl.when(second)
    def _():
        def step(j, carry):
            keys(pl.ds(pl.multiple_of(j * QB, QB), QB), 0, False)
            return carry

        lax.fori_loop(0, rows // QB, step, 0)

    @pl.when(jnp.logical_not(second))
    def _():
        dks[0:rows, :] = jnp.zeros((rows, 128), F32)
        dvs[0:rows, :] = jnp.zeros((rows, 128), F32)

    for r in range(0, rows, QB):
        dqs[r : r + QB, :] = jnp.transpose(dqt[:, r : r + QB]) * 0.125
    state = state_ref[0]
    sq = conv_back(pq_ref, dqs, xq_ref, rows, (pt_ref, xt_ref), tq_ref[...], rows, state)
    sk = conv_back(pk_ref, dks, xk_ref, 0, None, tk_ref[...], rows, state)
    sv = conv_back(pv_ref, dvs, xv_ref, 0, None, tv_ref[...], rows, state)
    tg_ref[...] = jnp.zeros(tg_ref.shape, F32)
    for j in range(3):
        for m, s in enumerate((sq, sk, sv)):
            tg_ref[3 * j + m : 3 * j + m + 1, :] = s[j]


def att_bwd(state, mixed, attended, logs, grad, projected, taps, earlier, part, rows):
    cols, taps_at = columns(part)
    own = cols(rows, 0, 0)
    both = cols(2 * rows, 0, 0)
    return call_in_parts(
        att_bwd_kernel,
        [
            pl.BlockSpec(memory_space=pltpu.SMEM),
            own, both, both, own, own, own,
            cols(8, rows // 8 - 1, 0),
            cols(rows, 1, 0),
            cols(2 * rows, 0, 6),
            cols(2 * rows, 0, 12),
            *taps_at,
        ],
        [own, cols(8, 0, 0), both, both, cols(16, 0, 0)],
        [
            jax.ShapeDtypeStruct((rows, D), BF),
            jax.ShapeDtypeStruct((8, D), BF),
            jax.ShapeDtypeStruct((2 * rows, D), BF),
            jax.ShapeDtypeStruct((2 * rows, D), BF),
            jax.ShapeDtypeStruct((16, D), F32),
        ],
        earlier,
        part,
        scratch_shapes=[
            pltpu.VMEM((2, rows, 128), BF),
            pltpu.VMEM((2, rows, 128), BF),
            pltpu.VMEM((128, rows), BF),
            pltpu.VMEM((128, rows), BF),
            pltpu.VMEM((128, 2 * rows), BF),
            pltpu.VMEM((128, rows), F32),
            pltpu.VMEM((rows, 128), F32),
            pltpu.VMEM((2 * rows, 128), F32),
            pltpu.VMEM((2 * rows, 128), F32),
        ],
        cost_estimate=cost(
            5 * 2 * 12 * rows * rows * 1.5 * 256 / PARTS,
            rows * D * 40 / PARTS,
            12 * rows * rows * 1.5 / PARTS,
        ),
        name="att_bwd",
    )(state, *mixed, attended, logs, grad, projected, projected, projected, projected,
      taps, taps, taps, *earlier)


def unit_rows(x):
    return x * lax.rsqrt(jnp.mean(x * x, axis=-1, keepdims=True) + norm_eps)


def before_bwd_kernel(x_ref, dt_ref, dk_ref, dv_ref, w_ref, out_ref, gain_ref):
    i = pl.program_id(0)
    hat = unit_rows(x_ref[...].astype(F32))
    gn = dot_nt(dk_ref[...], w_ref[D : 2 * D, :]) + dot_nt(dv_ref[...], w_ref[2 * D : 3 * D, :])

    @pl.when(i == 0)
    def _():
        out_ref[...] = gn.astype(BF)
        gain_ref[...] = jnp.sum(gn * hat, axis=0, keepdims=True)

    @pl.when(i > 0)
    def _():
        last = gn.shape[0] - 8
        full = jnp.concatenate([gn[:last], gn[last:] + dot_nt(dt_ref[...], w_ref[0:D, :])], 0)
        out_ref[...] = full.astype(BF)
        gain_ref[...] += jnp.sum(full * hat, axis=0, keepdims=True)


def before_bwd(x_both, back, weight, rows):
    dt, dk, dv = back[1:]
    height = rows // 2
    step = pl.BlockSpec((height, D), lambda i: (i, 0))

    def whole(shape):
        return pl.BlockSpec(shape, lambda i: (0, 0))

    return pl.pallas_call(
        before_bwd_kernel,
        grid=(2,),
        in_specs=[step, whole((8, D)), step, step, whole((3 * D, D))],
        out_specs=[step, whole((1, D))],
        out_shape=[jax.ShapeDtypeStruct((rows, D), BF), jax.ShapeDtypeStruct((1, D), F32)],
        compiler_params=pltpu.CompilerParams(vmem_limit_bytes=VMEM_LIMIT),
        cost_estimate=cost(2 * rows * D * D * 2, rows * D * 12),
        name="before_bwd",
    )(x_both, dt, dk, dv, weight)


def qkv_bwd_kernel(
    core_ref, x_ref, dq_ref, dt_ref, dk_ref, dv_ref, w_ref, gain_ref, gain_one_ref, gain_two_ref, tg_ref,
    *refs, pieces, blocks,
):
    if pieces:
        send_ref, keep_ref, own_ref, acc, gacc = refs
    else:
        keep_ref, small_ref, own_ref, acc, gacc = refs
    i = pl.program_id(0)
    half = blocks // 2

    @pl.when(i == 0)
    def _():
        acc[...] = jnp.zeros(acc.shape, F32)
        gacc[0:1, :] = gain_one_ref[...]

    hat = unit_rows(x_ref[...].astype(F32))
    low = (hat * gain_ref[...]).astype(BF)
    dk = dk_ref[...]
    dv = dv_ref[...]
    acc[D : 2 * D, :] += dot_tn(low, dk)
    acc[2 * D : 3 * D, :] += dot_tn(low, dv)

    @pl.when(i == half - 1)
    def _():
        acc[0:D, :] += dot_tn(low[low.shape[0] - 8 :], dt_ref[...])

    @pl.when(i >= half)
    def _():
        dq = dq_ref[...]
        acc[0:D, :] += dot_tn(low, dq)
        full = (
            dot_nt(dk, w_ref[D : 2 * D, :])
            + dot_nt(dv, w_ref[2 * D : 3 * D, :])
            + dot_nt(dq, w_ref[0:D, :])
        )
        own_ref[...] = full
        gacc[0:1, :] += jnp.sum(full * hat, axis=0, keepdims=True)

    @pl.when(i == blocks - 1)
    def _():
        small = jnp.concatenate(
            [gacc[0:1, :], gain_two_ref[...], tg_ref[0:9, :], jnp.zeros((5, D), F32)], 0
        )
        if pieces:
            core = core_ref[0]
            height = 3 * D // (2 * pieces)
            wide = height + 16
            for j in range(pieces):
                to = pl.ds(j * wide, wide)
                away = pl.ds(pl.multiple_of((2 * j + 1 - core) * height, 16), wide)
                here = pl.ds(pl.multiple_of((2 * j + core) * height, 16), wide)
                send_ref[to, :] = acc[away, :].astype(BF)
                keep_ref[to, :] = acc[here, :]
            send_ref[pieces * wide :, :] = small.astype(BF)
            keep_ref[pieces * wide :, :] = small
        else:
            keep_ref[...] = acc[0 : 3 * D, :].astype(BF)
            small_ref[...] = small


def qkv_bwd(core, x_both, back, weight, gain, gain_one_grad, gain_two_grad, tap_grads, rows, pieces):
    dq, dt, dk, dv = back
    blocks = 4
    half = blocks // 2
    height = 2 * rows // blocks
    step = pl.BlockSpec((height, D), lambda i: (i, 0))
    late = pl.BlockSpec((height, D), lambda i: (jnp.maximum(i - half, 0), 0))

    def whole(shape):
        return pl.BlockSpec(shape, lambda i: (0, 0))

    if pieces:
        packed = 3 * D // 2 + 16 * pieces + 16
        outs = [jax.ShapeDtypeStruct((packed, D), BF), jax.ShapeDtypeStruct((packed, D), F32)]
        out_at = [whole((packed, D))] * 2
    else:
        outs = [jax.ShapeDtypeStruct((3 * D, D), BF), jax.ShapeDtypeStruct((16, D), F32)]
        out_at = [whole((3 * D, D)), whole((16, D))]

    def body(*refs):
        qkv_bwd_kernel(*refs, pieces=pieces, blocks=blocks)

    return pl.pallas_call(
        body,
        grid=(blocks,),
        in_specs=[
            pl.BlockSpec(memory_space=pltpu.SMEM),
            step, late, whole((8, D)), step, step, whole((3 * D, D)),
            whole((1, D)), whole((1, D)), whole((1, D)), whole((16, D)),
        ],
        out_specs=out_at + [late],
        out_shape=outs + [jax.ShapeDtypeStruct((rows, D), F32)],
        scratch_shapes=[pltpu.VMEM((3 * D + 16, D), F32), pltpu.VMEM((8, D), F32)],
        compiler_params=pltpu.CompilerParams(vmem_limit_bytes=VMEM_LIMIT),
        cost_estimate=cost(2 * 2 * D * D * 4 * rows, rows * D * 30),
        name="qkv_bwd",
    )(core, x_both, dq, dt, dk, dv, weight, gain, gain_one_grad, gain_two_grad, tap_grads)


def merge(index, keep, got, height, taken):
    rows = keep.shape[0]
    out_rows = taken * height + 16 if taken else rows

    def body(index_ref, keep_ref, got_ref, send_ref, stay_ref):
        if not taken:
            total = keep_ref[...] + got_ref[...].astype(F32)
            send_ref[...] = total.astype(BF)
            stay_ref[...] = total
            return
        for j in range(taken):
            to = pl.ds(j * height, height)
            away = pl.ds(pl.multiple_of(index_ref[j] * height, 16), height)
            here = pl.ds(pl.multiple_of(index_ref[taken + j] * height, 16), height)
            send_ref[to, :] = (keep_ref[away, :] + got_ref[away, :].astype(F32)).astype(BF)
            stay_ref[to, :] = keep_ref[here, :] + got_ref[here, :].astype(F32)
        end = keep_ref[rows - 16 :, :] + got_ref[rows - 16 :, :].astype(F32)
        send_ref[taken * height :, :] = end.astype(BF)
        stay_ref[taken * height :, :] = end

    vmem = pl.BlockSpec(memory_space=pltpu.VMEM)
    return pl.pallas_call(
        body,
        in_specs=[pl.BlockSpec(memory_space=pltpu.SMEM), vmem, vmem],
        out_specs=[vmem, vmem],
        out_shape=[
            jax.ShapeDtypeStruct((out_rows, D), BF),
            jax.ShapeDtypeStruct((out_rows, D), F32),
        ],
        compiler_params=pltpu.CompilerParams(vmem_limit_bytes=32 << 20),
        cost_estimate=cost(rows * D, rows * D * 12),
        name="merge",
    )(index, keep, got)


def merge_grid(index, keep, got, taken):
    height = keep.shape[1]

    def body(index_ref, ka_ref, ga_ref, kb_ref, gb_ref, send_ref, stay_ref):
        send_ref[...] = (ka_ref[...].astype(F32) + ga_ref[...].astype(F32)).astype(BF)
        stay_ref[...] = kb_ref[...].astype(F32) + gb_ref[...].astype(F32)

    away = pl.BlockSpec((1, height, D), lambda i, index: (index[i], 0, 0))
    here = pl.BlockSpec((1, height, D), lambda i, index: (index[taken + i], 0, 0))
    step = pl.BlockSpec((1, height, D), lambda i, index: (i, 0, 0))
    return pl.pallas_call(
        body,
        grid_spec=pltpu.PrefetchScalarGridSpec(
            num_scalar_prefetch=1,
            grid=(taken,),
            in_specs=[away, away, here, here],
            out_specs=[step, step],
        ),
        out_shape=[
            pltpu.HBM((taken, height, D), BF),
            pltpu.HBM((taken, height, D), F32),
        ],
        compiler_params=pltpu.CompilerParams(vmem_limit_bytes=32 << 20),
        cost_estimate=cost(taken * height * D * 2, taken * height * D * 16),
        name="merge_grid",
    )(index, keep, got, keep, got)


def arrange(index, one, two, taken):
    half = one.shape[0]
    height = one.shape[1]

    def body(index_ref, one_ref, two_ref, out_ref):
        for i in range(taken):
            at = index_ref[i]

            @pl.when(at < half)
            def _():
                out_ref[i] = one_ref[jnp.minimum(at, half - 1)]

            @pl.when(at >= half)
            def _():
                out_ref[i] = two_ref[jnp.maximum(at - half, 0)]

    vmem = pl.BlockSpec(memory_space=pltpu.VMEM)
    return pl.pallas_call(
        body,
        in_specs=[pl.BlockSpec(memory_space=pltpu.SMEM), vmem, vmem],
        out_specs=vmem,
        out_shape=jax.ShapeDtypeStruct((taken, height, D), BF),
        compiler_params=pltpu.CompilerParams(vmem_limit_bytes=32 << 20),
        cost_estimate=cost(taken * height * D, taken * height * D * 8),
        name="arrange",
    )(index, one, two)


def join(own, got, shared=16):
    rows = own.shape[0]
    body_rows = rows - shared

    def body(own_ref, got_ref, out_ref):
        out_ref[0:body_rows, :] = own_ref[0:body_rows, :]
        out_ref[body_rows : 2 * body_rows, :] = got_ref[0:body_rows, :]
        if shared:
            out_ref[2 * body_rows :, :] = own_ref[body_rows:, :] + got_ref[body_rows:, :]

    vmem = pl.BlockSpec(memory_space=pltpu.VMEM)
    return pl.pallas_call(
        body,
        in_specs=[vmem, vmem],
        out_specs=vmem,
        out_shape=jax.ShapeDtypeStruct((2 * body_rows + shared, D), BF),
        compiler_params=pltpu.CompilerParams(vmem_limit_bytes=32 << 20),
        cost_estimate=cost(rows * D, rows * D * 8),
        name="join",
    )(own, got)


def join_held(own, got):
    rows = own.shape[0]
    cuts = 4
    size = rows // cuts

    def body(own_ref, got_ref, out_ref, sems):
        copies = []
        for k, ref in enumerate((own_ref, got_ref)):
            for j in range(cuts):
                source = ref.at[pl.ds(j * size, size)]
                to = out_ref.at[pl.ds(k * rows + j * size, size)]
                copies.append(pltpu.make_async_copy(source, to, sems.at[k * cuts + j]))
        for copy in copies:
            copy.start()
        for copy in copies:
            copy.wait()

    held = pl.BlockSpec(memory_space=pltpu.HBM)
    return pl.pallas_call(
        body,
        in_specs=[held, held],
        out_specs=held,
        out_shape=jax.ShapeDtypeStruct((2 * rows, D), BF),
        scratch_shapes=[pltpu.SemaphoreType.DMA((2 * cuts,))],
        compiler_params=pltpu.CompilerParams(vmem_limit_bytes=16 << 20),
        cost_estimate=cost(0, rows * D * 8),
        name="join_held",
    )(own, got)


def qkv_fwd_kernel(index_ref, x_ref, *refs, pieces, blocks):
    if pieces:
        own_ref, got_ref, out_ref, small_ref, weight = refs
    else:
        weight, given_ref, out_ref, small_ref = refs
    i = pl.program_id(0)

    @pl.when(i == 0)
    def _():
        if pieces:
            height = 3 * D // (2 * pieces)
            for j in range(pieces):
                at = pl.ds(j * height, height)
                for k, ref in enumerate((own_ref, got_ref)):
                    to = pl.multiple_of(index_ref[k * pieces + j] * height, 16)
                    weight[pl.ds(to, height), :] = ref[at, :]
            end = pl.ds(pieces * height, 16)
            small_ref[...] = own_ref[end, :].astype(F32) + got_ref[end, :].astype(F32)
        else:
            small_ref[...] = given_ref[...]

    x = x_ref[...].astype(F32)
    hat = x * lax.rsqrt(jnp.mean(x * x, axis=-1, keepdims=True) + norm_eps)
    low = (hat * small_ref[0:1, :]).astype(BF)

    @pl.when(i >= blocks // 2 - 1)
    def _():
        out_ref[:, 0:D] = dot(low, weight[0:D, :]).astype(BF)

    out_ref[:, D : 2 * D] = dot(low, weight[D : 2 * D, :]).astype(BF)
    out_ref[:, 2 * D : 3 * D] = dot(low, weight[2 * D : 3 * D, :]).astype(BF)


def qkv_fwd(index, x_both, weights, rows, pieces):
    blocks = 4
    height = 2 * rows // blocks

    def body(*refs):
        qkv_fwd_kernel(*refs, pieces=pieces, blocks=blocks)

    return pl.pallas_call(
        body,
        grid=(blocks,),
        in_specs=[
            pl.BlockSpec(memory_space=pltpu.SMEM),
            pl.BlockSpec((height, D), lambda i: (i, 0)),
            *[pl.BlockSpec(w.shape, lambda i: (0, 0)) for w in weights],
        ],
        out_specs=[
            pl.BlockSpec((height, 3 * D), lambda i: (i, 0)),
            pl.BlockSpec((16, D), lambda i: (0, 0)),
        ]
        + ([pl.BlockSpec((3 * D, D), lambda i: (0, 0))] if pieces else []),
        out_shape=[
            jax.ShapeDtypeStruct((2 * rows, 3 * D), BF),
            jax.ShapeDtypeStruct((16, D), F32),
        ]
        + ([jax.ShapeDtypeStruct((3 * D, D), BF)] if pieces else []),
        compiler_params=pltpu.CompilerParams(vmem_limit_bytes=VMEM_LIMIT),
        cost_estimate=cost(2 * 2 * rows * D * 3 * D, rows * D * 20),
        name="qkv_fwd",
    )(index, x_both, *weights)


def ffn_kernel(
    state_ref, index_ref, x_ref, att_ref, cot_ref, gain_ref, own_ref, got_ref,
    out_ref, gh_ref, ga_ref, gain_grad_ref, away_ref, here_ref,
    hidden, low, total, back, cot, sq, gb, weights, stage_up, stage_down, stage_out, in_sems, sems,
):
    c = pl.program_id(0)
    rows = x_ref.shape[0]
    blocks = [pl.ds(i * QB, QB) for i in range(rows // QB)]
    last = c == pl.num_programs(0) - 1
    core = index_ref[24]

    def fetch(k, j):
        ref = own_ref if k == 0 else got_ref
        to = weights.at[pl.ds(3 * index_ref[12 * k + j], 3)]
        return pltpu.make_async_copy(ref.at[pl.ds(3 * j, 3)], to, in_sems.at[12 * k + j])

    def put(source, group, count, column, sem, wait=False):
        piece = group // 3
        at = (piece // 2) * 3 + group % 3

        def copy(ref):
            to = ref.at[pl.ds(at, count)] if column is None else ref.at[pl.ds(at, count), column]
            return pltpu.make_async_copy(source, to, sems.at[sem])

        if wait:
            copy(here_ref).wait()
            return
        mine = piece % 2 == core

        @pl.when(mine)
        def _():
            copy(here_ref).start()

        @pl.when(jnp.logical_not(mine))
        def _():
            copy(away_ref).start()

    def put_up(i, wait=False):
        start = 0
        k = 0
        while start < 32:
            count = min(3 - (8 + start) % 3, 32 - start)
            put(stage_up.at[i, pl.ds(start, count)], 8 + start, count, i, 20 * i + k, wait)
            start += count
            k += 1

    def put_down(i, wait=False):
        for k in range(8):
            put(stage_down.at[i, pl.ds(k, 1)], 40 + 8 * i + k, 1, None, 20 * i + 12 + k, wait)

    def put_out(wait=False):
        for k in range(8):
            put(stage_out.at[pl.ds(k, 1)], k, 1, None, 80 + k, wait)

    def square(first):
        return weights[first : first + 8].reshape(D, D)

    @pl.when(c == 0)
    def _():
        for k in range(2):
            for j in range(12):
                fetch(k, j).start()
        cot[...] = jnp.where(state_ref[0] > 0, cot_ref[...], jnp.zeros((), BF))
        total[...] = jnp.zeros(total.shape, F32)
        back[...] = jnp.zeros(back.shape, F32)
        for k in range(2):
            for j in range(12):
                fetch(k, j).wait()
        wo = square(0)
        for b in blocks:
            h = x_ref[b, :].astype(F32) + dot(att_ref[b, :], wo)
            hidden[b, :] = h
            hat = h * lax.rsqrt(jnp.mean(h * h, axis=-1, keepdims=True) + norm_eps)
            low[b, :] = (hat * gain_ref[...]).astype(BF)

    up = weights[8:40, c].reshape(D, D)
    down = weights[pl.ds(40 + 8 * c, 8)].reshape(D, D)
    for b in blocks:
        act = jnp.maximum(dot(low[b, :], up), 0.0)
        s = (act * act).astype(BF)
        sq[b, :] = s
        total[b, :] += dot(s, down)
        g = (dot_nt(cot[b, :], down) * 2.0 * act).astype(BF)
        gb[b, :] = g
        back[b, :] += dot_nt(g, up)
    stage_down[c] = dot_tn(sq[...], cot[...]).reshape(8, 4, 24, D).astype(BF)
    stage_up[c] = dot_tn(low[...], gb[...]).reshape(32, 24, D).astype(BF)
    put_down(c)
    put_up(c)

    @pl.when(last)
    def _():
        gain = gain_ref[...]
        wo = square(0)
        sums = jnp.zeros((1, D), F32)
        for b in blocks:
            h = hidden[b, :]
            out_ref[b, :] = (h + total[b, :]).astype(BF)
            factor = lax.rsqrt(jnp.mean(h * h, axis=-1, keepdims=True) + norm_eps)
            hat = h * factor
            g = back[b, :]
            sums = sums + jnp.sum(g * hat, axis=0, keepdims=True)
            weighted = g * gain
            inner = jnp.mean(weighted * hat, axis=-1, keepdims=True)
            grad = cot[b, :].astype(F32) + factor * (weighted - hat * inner)
            gh_ref[b, :] = grad
            grad_low = grad.astype(BF)
            gb[b, :] = grad_low
            ga_ref[b, :] = dot_nt(grad_low, wo).astype(BF)
        gain_grad_ref[...] = sums
        stage_out[...] = dot_tn(att_ref[...], gb[...]).reshape(8, 4, 24, D).astype(BF)
        put_out()
        for i in range(4):
            put_down(i, True)
            put_up(i, True)
        put_out(True)


def ffn(state, index, tokens, attended, out_grad, gain, own, got, rows):
    def whole(shape):
        return pl.BlockSpec(shape, lambda c: (0,) * len(shape), pipeline_mode=pl.Buffered(1))

    act = whole((rows, D))
    held = pl.BlockSpec(memory_space=pl.ANY)
    scalars = pl.BlockSpec(memory_space=pltpu.SMEM)
    half = (36, 4, 24, D)
    return pl.pallas_call(
        ffn_kernel,
        grid=(4,),
        in_specs=[scalars, scalars, act, act, act, whole((1, D)), held, held],
        out_specs=[act, act, act, whole((1, D)), held, held],
        out_shape=[
            jax.ShapeDtypeStruct((rows, D), BF),
            jax.ShapeDtypeStruct((rows, D), F32),
            jax.ShapeDtypeStruct((rows, D), BF),
            jax.ShapeDtypeStruct((1, D), F32),
            jax.ShapeDtypeStruct(half, BF),
            jax.ShapeDtypeStruct(half, BF),
        ],
        scratch_shapes=[
            pltpu.VMEM((rows, D), F32),
            pltpu.VMEM((rows, D), BF),
            pltpu.VMEM((rows, D), F32),
            pltpu.VMEM((rows, D), F32),
            pltpu.VMEM((rows, D), BF),
            pltpu.VMEM((rows, D), BF),
            pltpu.VMEM((rows, D), BF),
            pltpu.VMEM((72, 4, 24, D), BF),
            pltpu.VMEM((4, 32, 24, D), BF),
            pltpu.VMEM((4, 8, 4, 24, D), BF),
            pltpu.VMEM((8, 4, 24, D), BF),
            pltpu.SemaphoreType.DMA((24,)),
            pltpu.SemaphoreType.DMA((88,)),
        ],
        compiler_params=pltpu.CompilerParams(vmem_limit_bytes=60 << 20),
        cost_estimate=cost(2 * rows * D * D * (24 + 3), 2 * 12 * D * D * 2 + rows * D * 16),
        name="ffn",
    )(state, index, tokens, attended, out_grad, gain, own, got)


def shift_flat(block, distance):
    count = lax.axis_size(AXES)
    route = [(i - distance, i) for i in range(count) if 0 <= i - distance < count]
    return lax.ppermute(block, AXES, route)


def shift_ctx(block, distance):
    count = lax.axis_size("ctx")
    route = [(i - distance, i) for i in range(count) if 0 <= i - distance < count]
    return lax.ppermute(block, "ctx", route)


def after(value, *others):
    return lax.optimization_barrier((value, *others))[0]


def swap(block, even_bit, odd_bit, planes=None):
    count = lax.axis_size(AXES)
    route = [
        (i, i ^ (odd_bit if i & 1 else even_bit))
        for i in range(count)
        if planes is None or i >> 3 in planes
    ]
    return lax.ppermute(block, AXES, route)


def to_aligned(shard, place, count, delta):
    rows = shard.shape[0]
    lag = delta * (count - 1)
    back = -(-lag // rows)
    if back == 1:
        keep = -(-lag // 8) * 8
        parts = [shift_flat(shard[rows - keep :], 1), shard]
    else:
        keep = back * rows
        parts = [shift_flat(shard, s) for s in range(back, 0, -1)] + [shard]
    joined = jnp.concatenate(parts, 0)
    return lax.dynamic_slice_in_dim(joined, keep - delta * place, rows - delta, 0)


def small_part(shard, place, count, delta):
    rows = shard.shape[0]
    extra = count * delta
    zeros = jnp.zeros((extra, 128), shard.dtype)
    joined = jnp.concatenate([zeros, shard, zeros], 0)
    start = extra + count * (rows - delta) - place * rows
    return lax.dynamic_slice_in_dim(joined, jnp.minimum(start, rows + extra), extra, 0)


def from_aligned(chunk, small, place, count, delta, rows):
    aligned = rows - delta
    ahead = -(-(count * delta) // aligned)
    parts = [chunk]
    if ahead == 1:
        keep = small.shape[0]
        got = shift_flat(chunk[:keep], -1)
        parts.append(jnp.where(place == count - 1, small, got))
    else:
        pad = ahead * aligned - small.shape[0]
        tail = jnp.concatenate([small, jnp.zeros((pad, 128), small.dtype)], 0)
        for s in range(1, ahead + 1):
            got = shift_flat(chunk, -s)
            for e in range(s):
                piece = tail[e * aligned : (e + 1) * aligned]
                got = jnp.where(place == count - s + e, piece, got)
            parts.append(got)
    return lax.dynamic_slice_in_dim(jnp.concatenate(parts, 0), delta * place, rows, 0)


def regroup(block):
    return block.reshape(-1, 24, 4, D).transpose(0, 2, 1, 3)


def ungroup(block):
    return block.reshape(-1, 4, 24, D).transpose(0, 2, 1, 3)


def normalize(values, gain):
    factor = lax.rsqrt(jnp.mean(values * values, axis=-1, keepdims=True) + norm_eps)
    scaled = values * factor
    return (scaled, factor, scaled * gain)


def norm_back(grad_in, scaled, factor, gain):
    weighted = grad_in * gain
    inner_mean = jnp.mean(weighted * scaled, axis=-1, keepdims=True)
    return factor * (weighted - scaled * inner_mean)


def adam_update(master, moment_one, moment_two, gradient, step_count, row_start):
    row_index = row_start + jnp.arange(master.shape[0], dtype=jnp.int32)
    matrix_rows = (4 * D * D + 2 * D * FF) // 128
    out_first = 3 * D * D // 128
    out_last = 4 * D * D // 128
    is_matrix = (row_index < matrix_rows)[:, None]
    is_out = ((row_index >= out_first) & (row_index < out_last))[:, None]
    step_rate = jnp.where(is_matrix, jnp.where(is_out, 0.5, 0.1), 1.0)
    decay_rate = jnp.where(is_matrix, 0.1, 0.0)
    step_value = step_count[0].astype(jnp.float32)
    new_one = 0.9 * moment_one + 0.1 * gradient
    new_two = 0.999 * moment_two + 0.001 * gradient * gradient
    corr_first = 1.0 - jnp.power(0.9, step_value)
    corr_second = 1.0 - jnp.power(0.999, step_value)
    new_weights = master - step_rate * (
        new_one / corr_first / (jnp.sqrt(new_two / corr_second) + 1e-08) + decay_rate * master
    )
    return (new_weights, new_one, new_two)


def shards(tokens, out_grad, positions, master, first_moment, second_moment, step_count):
    rows = tokens.shape[0]
    assert rows == SEQ_MIN
    count = lax.axis_size(AXES)
    place = lax.axis_index(AXES).astype(jnp.int32)
    owned = master.shape[0]
    aligned = (4 * D * D + 2 * D * FF) // 128 // count
    delta = owned - aligned
    height = aligned * 128 // D
    staged = count == 32
    first_place = positions[0]
    state = jnp.where(first_place < 0, 0, jnp.where(first_place >= SEQ_MIN, 2, 1)).astype(jnp.int32)
    state_vec = state[None]

    chunk = to_aligned(master, place, count, delta).reshape(-1, D)
    if staged:
        group = 3 * place + jnp.arange(3, dtype=jnp.int32)
        in_up = ((group >= 32) & (group < 64))[:, None, None, None]
        chunk = jnp.where(in_up, regroup(chunk), chunk.reshape(3, 4, 24, D)).reshape(-1, D)
    chunk = chunk.astype(BF)
    small = lax.reduce_precision(small_part(master, place, count, delta), 8, 7)
    core = (place & 1)[None]
    x_bit = (place >> 1) & 1
    y_bit = (place >> 2) & 1
    even = (place & 1) == 0
    if staged:
        z = place >> 3
        mine = jnp.concatenate([chunk, small.astype(BF).reshape(-1, D)], 0)
        tokens_before = shift_ctx(after(tokens, mine), 1)
        got = swap(mine, 16, 16)
        tokens_both = jnp.concatenate([tokens_before, tokens], 0)
        got = after(got, tokens_both)
        rest = jnp.concatenate([chunk, got[:height]], 0)
        none = jnp.zeros((), BF)
        first = jnp.where(z == 0, chunk, jnp.where(z == 2, got[:height], none))
        mine = jnp.concatenate([first, mine[height:] + got[height:]], 0)
        mine = mine + swap(mine, 8, 8)
        across = swap(after(rest, mine), 8, 8)
        mine = join(mine, swap(mine, 2, 4))
        mine = join(mine, swap(mine, 4, 2))
        got = swap(mine, 1, 1)
        index = []
        late_index = []
        for k in (0, 1):
            turn = even if k == 0 else jnp.logical_not(even)
            for j in range(4):
                near, far = j & 1, j >> 1
                x_of = x_bit ^ jnp.where(turn, near, far)
                y_of = y_bit ^ jnp.where(turn, far, near)
                piece = 4 * y_of + 2 * x_of + (core[0] ^ k)
                index.append(piece)
                late_index += [piece, piece + 8, piece + 16]
        index = jnp.stack(index).astype(jnp.int32)
        late_index = jnp.stack(late_index + [core[0]]).astype(jnp.int32)
        projected, small, in_weight = qkv_fwd(index, tokens_both, (mine, got), rows, 4)
        codes = [z ^ k for k in (1, 2, 3)]
        order = [jnp.where(j == 1, 2, jnp.where(j == 2, 1, j)) for j in codes]
        rest = arrange(
            after(jnp.stack(order).astype(jnp.int32), projected), rest.reshape(2, height, D), across.reshape(2, height, D), 3
        ).reshape(-1, D)
        across = swap(rest, 2, 4)
    else:
        tokens_both = jnp.concatenate([shift_ctx(tokens, 1), tokens], 0)
        wide = lax.all_gather(chunk, AXES, axis=0, tiled=True)
        small = lax.psum(small, AXES)[:96].reshape(-1, D)
        in_weight = wide[: 3 * D]
        projected, small = qkv_fwd(core, tokens_both, (in_weight, small), rows, 0)
        late_index = jnp.arange(25, dtype=jnp.int32) % 24
    gain_first = small[0]
    gain_second = small[1]
    taps = small[2:11].reshape(3, 3 * D)

    forward = []
    if staged:
        forward = att_fwd(after(state_vec, rest), projected, taps, forward, 0, rows)
        rest = join_held(after(rest, forward[0]), across)
        across = swap(rest, 4, 2)
        forward = att_fwd(after(state_vec, rest), projected, taps, forward, 1, rows)
        forward = att_fwd(state_vec, projected, taps, forward, 2, rows)
        rest = join_held(after(rest, forward[0]), across)
        across = swap(rest, 1, 1)
        own_weights, got_weights = rest.reshape(36, 4, 24, D), across.reshape(36, 4, 24, D)
    else:
        for part in range(PARTS):
            forward = att_fwd(state_vec, projected, taps, forward, part, rows)
        grouped = jnp.concatenate(
            [
                wide[3 * D : 4 * D].reshape(-1, 4, 24, D),
                regroup(wide[4 * D : 8 * D]),
                wide[8 * D :].reshape(-1, 4, 24, D),
            ],
            0,
        )
        own_weights, got_weights = grouped[:36], grouped[36:]
    attn_low, logs, *mixed = forward

    layer_out, grad_hidden, grad_attended, grad_gain_two, away_grad, here_grad = ffn(
        state_vec, late_index, tokens, attn_low, out_grad, gain_second[None], own_weights, got_weights, rows
    )

    def backward(start, done, part):
        return att_bwd(
            start, mixed, attn_low, logs, grad_attended, projected, taps, done, part, rows
        )

    if staged:
        stay = [jnp.where(even, 2 * j + x_bit, 2 * y_bit + j) for j in range(2)]
        away = [jnp.where(even, 2 * j + 1 - x_bit, 2 * (1 - y_bit) + j) for j in range(2)]
        pick_plane = jnp.stack(away + stay).astype(jnp.int32)
        other = jnp.where(even, y_bit, x_bit)
        pick_line = jnp.stack([1 - other, other]).astype(jnp.int32)

        def of_quarters(pick, held):
            half = pick.shape[0] // 2
            steps = [pick[s * half + j] + held * t for s in range(2) for t in range(3) for j in range(half)]
            return jnp.stack(steps)

        late_keep = here_grad.reshape(12, height, D)
        late_got = swap(away_grad.reshape(12, height, D), 1, 1)
        done = backward(state_vec, [], 0)
        late_send, late_keep = merge_grid(
            after(of_quarters(pick_plane, 4), done[4]), late_keep, late_got, 6
        )
        late_got = swap(late_send, 2, 4)
        done = backward(after(state_vec, late_send), done, 1)
        late_send, late_keep = merge_grid(
            after(of_quarters(pick_line, 2), done[4]), late_keep, late_got, 3
        )
        late_got = swap(late_send, 4, 2)
        done = backward(after(state_vec, late_send), done, 2)
        z_even = (z & 1) == 0
        low_pair = [jnp.where(z_even, 0, 0), jnp.where(z_even, 2, 1)]
        high_pair = [jnp.where(z_even, 0, 0), jnp.where(z_even, 1, 2)]
        pick_z = jnp.stack(low_pair + high_pair).astype(jnp.int32)
        late_send, late_keep = merge_grid(after(pick_z, done[4]), late_keep, late_got, 2)
        late_got = swap(late_send, 8, 8)
        sums_state = after(core, late_send)
    else:
        done = []
        for part in range(PARTS):
            done = backward(state_vec, done, part)
        sums_state = core
    *back, tap_grads = done
    grads_before, gain_one_grad = before_bwd(tokens_both, back, in_weight, rows)
    from_next = shift_ctx(grads_before, -1)
    sums = qkv_bwd(
        after(sums_state, grads_before), tokens_both, back, in_weight, gain_first[None], gain_one_grad, grad_gain_two, tap_grads, rows,
        4 if staged else 0,
    )
    grad_normed_one = sums[2]
    scaled_one, factor_one, _ = normalize(tokens.astype(F32), gain_first)
    input_grad = grad_hidden + norm_back(
        grad_normed_one + from_next.astype(F32), scaled_one, factor_one, gain_first
    )

    if staged:
        send, keep = sums[:2]
        high = z >> 1
        pick_last = jnp.stack([1 - high, high]).astype(jnp.int32)
        late_send, late_keep = merge_grid(after(pick_last, send), late_keep, late_got, 1)
        late_got = swap(late_send, 16, 16, (0, 1, 3))
        got = swap(after(send, late_send, from_next), 1, 1)
        send, keep = merge(pick_plane, keep, got, height + 16, 2)
        got = swap(send, 2, 4)
        send, keep = merge(pick_line, keep, got, height + 16, 1)
        got = swap(send, 4, 2)
        send, keep = merge(core, keep, got, height + 16, 0)
        got = swap(send, 8, 8)
        late_chunk = late_keep[0] + late_got[0].astype(F32)
        late_chunk = jnp.where(in_up, ungroup(late_chunk).reshape(3, 4, 24, D), late_chunk.reshape(3, 4, 24, D))
        late_chunk = late_chunk.reshape(-1, D)
        late_next = shift_flat(late_chunk[:16], -1)
        send, keep = merge(after(core, late_next, input_grad), keep, got, height + 16, 0)
        got = swap(send, 16, 16, (1, 2))
        first = keep + got.astype(F32)
        quarter = count // 4
        follow = jnp.where(place < quarter - 1, first[height : height + 16], late_next)
        follow = jnp.where(place == count - 1, first[height + 16 :], follow)
        chunk_grad = jnp.where(place < quarter, first[:height], late_chunk)
        chunk_grad = jnp.concatenate([chunk_grad, follow], 0).reshape(-1, 128)
        gradient = lax.dynamic_slice_in_dim(chunk_grad, delta * place, owned, 0)
    else:
        flat_grad = jnp.stack([here_grad.reshape(12, 3, 4, 24, D), away_grad.reshape(12, 3, 4, 24, D)], 1)
        flat_grad = flat_grad.reshape(72, 4, 24, D)
        wide_grad = jnp.concatenate(
            [
                sums[0],
                flat_grad[:8].reshape(-1, D),
                ungroup(flat_grad[8:40]).reshape(-1, D),
                flat_grad[40:].reshape(-1, D),
            ],
            0,
        )
        chunk_grad = lax.psum_scatter(wide_grad, AXES, scatter_dimension=0, tiled=True).astype(F32)
        used = sums[1].reshape(-1, 128)
        extra = count * delta
        small_grad = jnp.concatenate([used, jnp.zeros((extra - used.shape[0], 128), F32)], 0)
        small_grad = lax.psum(small_grad, AXES)
        gradient = from_aligned(chunk_grad.reshape(-1, 128), small_grad, place, count, delta, owned)
    new_weights, new_one, new_two = adam_update(
        master, first_moment, second_moment, gradient, step_count, place * owned
    )
    return (layer_out, input_grad, new_weights, new_one, new_two, new_weights.astype(BF))


def solution(mesh):
    spread = P(AXES, None)
    return jax.shard_map(
        shards,
        mesh=mesh,
        in_specs=(spread, spread, P(AXES), spread, spread, spread, P()),
        out_specs=(spread,) * 6,
        check_vma=False,
    )
```

```python
import jax
import jax.numpy as jnp
from jax import lax
from jax.experimental import pallas as pl
from jax.experimental.pallas import tpu as pltpu
from jax.sharding import PartitionSpec as P

D = 768
HEADS = 12
HEAD_DIM = 64
FF = 3072
SEQ_MIN = 1024
AXES = ("dp", "ctx")
QB = 256
PARTS = 3
F32 = jnp.float32
BF = jnp.bfloat16
NT = (((1,), (1,)), ((), ()))
TN = (((0,), (0,)), ((), ()))
norm_eps = 1e-06
VMEM_LIMIT = 56 << 20


def dot(left, right):
    return jnp.dot(left, right, preferred_element_type=F32)


def dot_nt(left, right):
    return lax.dot_general(left, right, NT, preferred_element_type=F32)


def dot_tn(left, right):
    return lax.dot_general(left, right, TN, preferred_element_type=F32)


def cost(flops, nbytes, exps=0):
    return pl.CostEstimate(flops=int(flops), bytes_accessed=int(nbytes), transcendentals=int(exps))


def row_ids(height):
    return lax.broadcasted_iota(jnp.int32, (height, 128), 0)


def conv(out_ref, x_ref, start, tail_ref, taps, rows, state):
    height = x_ref.shape[0]
    for r in range(0, height, QB):
        at = start + r
        if r:
            x = x_ref[r - 16 : r + QB, :].astype(F32)
        else:
            before = jnp.zeros((16, 128), F32)
            if tail_ref is not None:
                before = jnp.concatenate([before[8:], tail_ref[...].astype(F32)], 0)
            x = jnp.concatenate([before, x_ref[0:QB, :].astype(F32)], 0)
        one = pltpu.roll(x, 1, 0)[16:]
        two = pltpu.roll(x, 2, 0)[16:]
        x = x[16:]
        scale = 1.0
        if at >= rows:
            scale = jnp.where(state > 0, 1.0, 0.0)
        if at == 0 or at == rows:
            seen = jnp.where(state == 2, 1.0, 0.0) if at else 0.0
            row = row_ids(QB)
            one = jnp.where(row < 1, one * seen, one)
            two = jnp.where(row < 2, two * seen, two)
        c_one = taps[1:2] * scale
        c_two = taps[2:3] * scale
        out_ref[r : r + QB, :] = (taps[0:1] * x + c_one * one + c_two * two).astype(BF)


def att_fwd_kernel(
    state_ref, tail_ref, q_ref, k_ref, v_ref, tq_ref, tk_ref, tv_ref,
    o_ref, l_ref, qm_ref, km_ref, vm_ref, ka, va,
):
    rows = q_ref.shape[0]
    lane = lax.broadcasted_iota(jnp.int32, (1, 128), 1)
    state = state_ref[0]
    conv(qm_ref, q_ref, rows, tail_ref, tq_ref[...], rows, state)
    conv(km_ref, k_ref, 0, None, tk_ref[...], rows, state)
    conv(vm_ref, v_ref, 0, None, tv_ref[...], rows, state)
    bias = jnp.where(state == 2, 0.0, -1e30)
    for h in range(2):
        mine = (lane < 64) if h == 0 else (lane >= 64)
        base = 64 if h == 0 else 0
        first = jnp.where(lane == base, bias, 0.0).astype(BF)
        for r in range(0, 2 * rows, QB):
            at = pl.ds(r, QB)
            ka[h, at, :] = jnp.where(mine, km_ref[at, :], first if r < rows else jnp.zeros((), BF))
            va[h, at, :] = jnp.where(mine, vm_ref[at, :], jnp.ones((), BF))
    for i in range(rows // QB):
        rs = pl.ds(i * QB, QB)
        outs = []
        sums = []
        qf = qm_ref[rs, :].astype(F32) * 0.125
        for h in range(2):
            mine = (lane < 64) if h == 0 else (lane >= 64)
            base = 64 if h == 0 else 0
            qh = jnp.where(mine, qf, jnp.where(lane == base, 1.0, 0.0)).astype(BF)
            nk = rows + (i + 1) * QB
            s = dot_nt(qh, ka[h, 0:nk, :])
            r = lax.broadcasted_iota(jnp.int32, (QB, QB), 0)
            c = lax.broadcasted_iota(jnp.int32, (QB, QB), 1)
            sd = jnp.where(c <= r, s[:, nk - QB :], -1e30)
            se = s[:, : nk - QB]
            m = jnp.maximum(
                jnp.max(sd, axis=1, keepdims=True), jnp.max(se, axis=1, keepdims=True)
            )
            p = jnp.concatenate([jnp.exp(se - m).astype(BF), jnp.exp(sd - m).astype(BF)], 1)
            o = dot(p, va[h, 0:nk, :])
            outs.append(o / pltpu.roll(o, 64, 1))
            sums.append(m + jnp.log(o))
        res = jnp.where(lane < 64, outs[0], outs[1])
        res = jnp.where(state == 0, vm_ref[pl.ds(rows + i * QB, QB), :].astype(F32), res)
        o_ref[rs, :] = res.astype(BF)
        l_ref[rs, :] = jnp.where(lane < 64, sums[1], sums[0])


def call_in_parts(body, in_specs, out_specs, out_shape, earlier, part, **options):
    used = len(in_specs)

    def kernel(*refs):
        body(*refs[:used], *refs[used + len(earlier) :])

    return pl.pallas_call(
        kernel,
        grid=(6 // PARTS,),
        in_specs=in_specs + [pl.BlockSpec(memory_space=pl.ANY)] * len(earlier),
        out_specs=out_specs,
        out_shape=out_shape,
        input_output_aliases={used + i: i for i in range(len(earlier))},
        compiler_params=pltpu.CompilerParams(vmem_limit_bytes=VMEM_LIMIT),
        **options,
    )


def columns(part):
    first = part * (6 // PARTS)

    def cols(height, row, off):
        return pl.BlockSpec((height, 128), lambda p: (row, p + first + off))

    taps_at = [
        pl.BlockSpec((3, 128), lambda p, off=off: (0, p + first + off)) for off in (0, 6, 12)
    ]
    return cols, taps_at


def att_fwd(state, projected, taps, earlier, part, rows):
    cols, taps_at = columns(part)
    return call_in_parts(
        att_fwd_kernel,
        [
            pl.BlockSpec(memory_space=pltpu.SMEM),
            cols(8, rows // 8 - 1, 0),
            cols(rows, 1, 0),
            cols(2 * rows, 0, 6),
            cols(2 * rows, 0, 12),
            *taps_at,
        ],
        [cols(rows, 0, 0)] * 3 + [cols(2 * rows, 0, 0)] * 2,
        [
            jax.ShapeDtypeStruct((rows, D), BF),
            jax.ShapeDtypeStruct((rows, D), F32),
            jax.ShapeDtypeStruct((rows, D), BF),
            jax.ShapeDtypeStruct((2 * rows, D), BF),
            jax.ShapeDtypeStruct((2 * rows, D), BF),
        ],
        earlier,
        part,
        scratch_shapes=[pltpu.VMEM((2, 2 * rows, 128), BF)] * 2,
        cost_estimate=cost(
            2 * 2 * 12 * rows * rows * 1.5 * 256 / PARTS,
            rows * D * 30 / PARTS,
            12 * rows * rows * 1.5 / PARTS,
        ),
        name="att_fwd",
    )(state, projected, projected, projected, projected, taps, taps, taps, *earlier)


def three(x, lane, base):
    hi = x.astype(BF).astype(F32)
    r = x - hi
    mid = r.astype(BF).astype(F32)
    lo = r - mid
    return jnp.where(
        lane == base, hi, jnp.where(lane == base + 1, mid, jnp.where(lane == base + 2, lo, 0.0))
    )


def conv_back(out_ref, grad_ref, x_ref, start, tail, taps, rows, state):
    height = grad_ref.shape[0]
    joint = jnp.where(state == 2, 1.0, 0.0)
    sums = [jnp.zeros((1, 128), F32)] * 3

    def add(parts, x):
        return [s + jnp.sum(g * x, axis=0, keepdims=True) for s, g in zip(sums, parts)]

    for r in range(0, height, QB):
        ends = r + QB == height
        meets = start + r + QB == rows
        if ends:
            grad = jnp.concatenate([grad_ref[r : r + QB, :], jnp.zeros((8, 128), F32)], 0)
        else:
            grad = grad_ref[r : r + QB + 8, :]
        one = pltpu.roll(grad, QB + 7, 0)[:QB]
        two = pltpu.roll(grad, QB + 6, 0)[:QB]
        grad = grad[:QB]
        if meets and not ends:
            row = row_ids(QB)
            one = jnp.where(row >= QB - 1, one * joint, one)
            two = jnp.where(row >= QB - 2, two * joint, two)
        out_ref[r : r + QB, :] = (taps[0:1] * grad + taps[1:2] * one + taps[2:3] * two).astype(BF)
        sums = add((grad, one, two), x_ref[r : r + QB, :].astype(F32))
    if tail is not None:
        grad = jnp.concatenate([jnp.zeros((8, 128), F32), grad_ref[0:8, :]], 0)
        one = pltpu.roll(grad, 15, 0)[:8] * joint
        two = pltpu.roll(grad, 14, 0)[:8] * joint
        tail[0][...] = (taps[1:2] * one + taps[2:3] * two).astype(BF)
        sums = add((grad[:8], one, two), tail[1][...].astype(F32))
    return sums


def att_bwd_kernel(
    state_ref, q_ref, k_ref, v_ref, o_ref, l_ref, do_ref, xt_ref, xq_ref, xk_ref, xv_ref,
    tq_ref, tk_ref, tv_ref,
    pq_ref, pt_ref, pk_ref, pv_ref, tg_ref, qa, da, qt, dt, kt, dqt, dqs, dks, dvs,
):
    rows = q_ref.shape[0]
    lane = lax.broadcasted_iota(jnp.int32, (1, 128), 1)
    second = state_ref[0] == 2
    for r in range(0, rows, QB):
        at = pl.ds(r, QB)
        do = do_ref[at, :].astype(F32)
        od = do * o_ref[at, :].astype(F32)
        qf = q_ref[at, :].astype(F32) * 0.125
        lv = l_ref[at, :]
        for h in range(2):
            mine = (lane < 64) if h == 0 else (lane >= 64)
            base = 64 if h == 0 else 0
            delta = jnp.sum(jnp.where(mine, od, 0.0), axis=1, keepdims=True)
            qa[h, at, :] = jnp.where(mine, qf, three(-lv, lane, base)).astype(BF)
            da[h, at, :] = jnp.where(mine, do, three(-delta, lane, base)).astype(BF)
        qt[:, at] = jnp.transpose(qf).astype(BF)
        dt[:, at] = jnp.transpose(do).astype(BF)
    for r in range(0, 2 * rows, QB):
        at = pl.ds(r, QB)
        kt[:, at] = jnp.transpose(k_ref[at, :].astype(F32)).astype(BF)
    dqt[...] = jnp.zeros(dqt.shape, F32)

    def keys(ks, first, diagonal):
        kk = k_ref[ks, :]
        vv = v_ref[ks, :]
        dv = []
        dk = []
        for h in range(2):
            mine = (lane < 64) if h == 0 else (lane >= 64)
            base = 64 if h == 0 else 0
            ones3 = ((lane >= base) & (lane < base + 3)).astype(BF)
            hs = slice(64 * h, 64 * h + 64)
            st = dot_nt(jnp.where(mine, kk, ones3), qa[h, first:rows, :])
            dp = dot_nt(jnp.where(mine, vv, ones3), da[h, first:rows, :])
            p = jnp.exp(st)
            if diagonal:
                r = lax.broadcasted_iota(jnp.int32, (QB, QB), 0)
                c = lax.broadcasted_iota(jnp.int32, (QB, QB), 1)
                seen = jnp.where(r <= c, p[:, :QB], 0.0)
                p = jnp.concatenate([seen, p[:, QB:]], 1) if first + QB < rows else seen
            ds = (p * dp).astype(BF)
            dv.append(dot_nt(dt[hs, first:rows], p.astype(BF)))
            dk.append(dot_nt(qt[hs, first:rows], ds))
            dqt[hs, first:rows] += dot(kt[hs, ks], ds)
        dvs[ks, :] = jnp.transpose(jnp.concatenate(dv, 0))
        dks[ks, :] = jnp.transpose(jnp.concatenate(dk, 0))

    for j in range(rows // QB):
        keys(pl.ds(rows + j * QB, QB), j * QB, True)

    @pl.when(second)
    def _():
        def step(j, carry):
            keys(pl.ds(pl.multiple_of(j * QB, QB), QB), 0, False)
            return carry

        lax.fori_loop(0, rows // QB, step, 0)

    @pl.when(jnp.logical_not(second))
    def _():
        dks[0:rows, :] = jnp.zeros((rows, 128), F32)
        dvs[0:rows, :] = jnp.zeros((rows, 128), F32)

    for r in range(0, rows, QB):
        dqs[r : r + QB, :] = jnp.transpose(dqt[:, r : r + QB]) * 0.125
    state = state_ref[0]
    sq = conv_back(pq_ref, dqs, xq_ref, rows, (pt_ref, xt_ref), tq_ref[...], rows, state)
    sk = conv_back(pk_ref, dks, xk_ref, 0, None, tk_ref[...], rows, state)
    sv = conv_back(pv_ref, dvs, xv_ref, 0, None, tv_ref[...], rows, state)
    tg_ref[...] = jnp.zeros(tg_ref.shape, F32)
    for j in range(3):
        for m, s in enumerate((sq, sk, sv)):
            tg_ref[3 * j + m : 3 * j + m + 1, :] = s[j]


def att_bwd(state, mixed, attended, logs, grad, projected, taps, earlier, part, rows):
    cols, taps_at = columns(part)
    own = cols(rows, 0, 0)
    both = cols(2 * rows, 0, 0)
    return call_in_parts(
        att_bwd_kernel,
        [
            pl.BlockSpec(memory_space=pltpu.SMEM),
            own, both, both, own, own, own,
            cols(8, rows // 8 - 1, 0),
            cols(rows, 1, 0),
            cols(2 * rows, 0, 6),
            cols(2 * rows, 0, 12),
            *taps_at,
        ],
        [own, cols(8, 0, 0), both, both, cols(16, 0, 0)],
        [
            jax.ShapeDtypeStruct((rows, D), BF),
            jax.ShapeDtypeStruct((8, D), BF),
            jax.ShapeDtypeStruct((2 * rows, D), BF),
            jax.ShapeDtypeStruct((2 * rows, D), BF),
            jax.ShapeDtypeStruct((16, D), F32),
        ],
        earlier,
        part,
        scratch_shapes=[
            pltpu.VMEM((2, rows, 128), BF),
            pltpu.VMEM((2, rows, 128), BF),
            pltpu.VMEM((128, rows), BF),
            pltpu.VMEM((128, rows), BF),
            pltpu.VMEM((128, 2 * rows), BF),
            pltpu.VMEM((128, rows), F32),
            pltpu.VMEM((rows, 128), F32),
            pltpu.VMEM((2 * rows, 128), F32),
            pltpu.VMEM((2 * rows, 128), F32),
        ],
        cost_estimate=cost(
            5 * 2 * 12 * rows * rows * 1.5 * 256 / PARTS,
            rows * D * 40 / PARTS,
            12 * rows * rows * 1.5 / PARTS,
        ),
        name="att_bwd",
    )(state, *mixed, attended, logs, grad, projected, projected, projected, projected,
      taps, taps, taps, *earlier)


def unit_rows(x):
    return x * lax.rsqrt(jnp.mean(x * x, axis=-1, keepdims=True) + norm_eps)


def before_bwd_kernel(x_ref, dt_ref, dk_ref, dv_ref, w_ref, out_ref, gain_ref):
    i = pl.program_id(0)
    hat = unit_rows(x_ref[...].astype(F32))
    gn = dot_nt(dk_ref[...], w_ref[D : 2 * D, :]) + dot_nt(dv_ref[...], w_ref[2 * D : 3 * D, :])

    last_step = pl.num_programs(0) - 1

    @pl.when(i == 0)
    def _():
        gain_ref[...] = jnp.zeros(gain_ref.shape, F32)

    @pl.when(i < last_step)
    def _():
        out_ref[...] = gn.astype(BF)
        gain_ref[...] += jnp.sum(gn * hat, axis=0, keepdims=True)

    @pl.when(i == last_step)
    def _():
        last = gn.shape[0] - 8
        full = jnp.concatenate([gn[:last], gn[last:] + dot_nt(dt_ref[...], w_ref[0:D, :])], 0)
        out_ref[...] = full.astype(BF)
        gain_ref[...] += jnp.sum(full * hat, axis=0, keepdims=True)


def before_bwd(x_both, back, weight, rows):
    dt, dk, dv = back[1:]
    blocks = 4
    height = rows // blocks
    step = pl.BlockSpec((height, D), lambda i: (i, 0))

    def whole(shape):
        return pl.BlockSpec(shape, lambda i: (0, 0))

    return pl.pallas_call(
        before_bwd_kernel,
        grid=(blocks,),
        in_specs=[step, whole((8, D)), step, step, whole((3 * D, D))],
        out_specs=[step, whole((1, D))],
        out_shape=[jax.ShapeDtypeStruct((rows, D), BF), jax.ShapeDtypeStruct((1, D), F32)],
        compiler_params=pltpu.CompilerParams(vmem_limit_bytes=VMEM_LIMIT),
        cost_estimate=cost(2 * rows * D * D * 2, rows * D * 12),
        name="before_bwd",
    )(x_both, dt, dk, dv, weight)


def qkv_bwd_kernel(
    core_ref, x_ref, dq_ref, dt_ref, dk_ref, dv_ref, w_ref, gain_ref, gain_one_ref, gain_two_ref, tg_ref,
    *refs, pieces, blocks,
):
    if pieces:
        send_ref, keep_ref, own_ref, acc, gacc = refs
    else:
        keep_ref, small_ref, own_ref, acc, gacc = refs
    i = pl.program_id(0)
    half = blocks // 2

    @pl.when(i == 0)
    def _():
        acc[...] = jnp.zeros(acc.shape, F32)
        gacc[0:1, :] = gain_one_ref[...]

    hat = unit_rows(x_ref[...].astype(F32))
    low = (hat * gain_ref[...]).astype(BF)
    dk = dk_ref[...]
    dv = dv_ref[...]
    acc[D : 2 * D, :] += dot_tn(low, dk)
    acc[2 * D : 3 * D, :] += dot_tn(low, dv)

    @pl.when(i == half - 1)
    def _():
        acc[0:D, :] += dot_tn(low[low.shape[0] - 8 :], dt_ref[...])

    @pl.when(i >= half)
    def _():
        dq = dq_ref[...]
        acc[0:D, :] += dot_tn(low, dq)
        full = (
            dot_nt(dk, w_ref[D : 2 * D, :])
            + dot_nt(dv, w_ref[2 * D : 3 * D, :])
            + dot_nt(dq, w_ref[0:D, :])
        )
        own_ref[...] = full
        gacc[0:1, :] += jnp.sum(full * hat, axis=0, keepdims=True)

    @pl.when(i == blocks - 1)
    def _():
        small = jnp.concatenate(
            [gacc[0:1, :], gain_two_ref[...], tg_ref[0:9, :], jnp.zeros((5, D), F32)], 0
        )
        if pieces:
            core = core_ref[0]
            height = 3 * D // (2 * pieces)
            wide = height + 16
            for j in range(pieces):
                to = pl.ds(j * wide, wide)
                away = pl.ds(pl.multiple_of((2 * j + 1 - core) * height, 16), wide)
                here = pl.ds(pl.multiple_of((2 * j + core) * height, 16), wide)
                send_ref[to, :] = acc[away, :].astype(BF)
                keep_ref[to, :] = acc[here, :]
            send_ref[pieces * wide :, :] = small.astype(BF)
            keep_ref[pieces * wide :, :] = small
        else:
            keep_ref[...] = acc[0 : 3 * D, :].astype(BF)
            small_ref[...] = small


def qkv_bwd(core, x_both, back, weight, gain, gain_one_grad, gain_two_grad, tap_grads, rows, pieces):
    dq, dt, dk, dv = back
    blocks = 4
    half = blocks // 2
    height = 2 * rows // blocks
    step = pl.BlockSpec((height, D), lambda i: (i, 0))
    late = pl.BlockSpec((height, D), lambda i: (jnp.maximum(i - half, 0), 0))

    def whole(shape):
        return pl.BlockSpec(shape, lambda i: (0, 0))

    if pieces:
        packed = 3 * D // 2 + 16 * pieces + 16
        outs = [jax.ShapeDtypeStruct((packed, D), BF), jax.ShapeDtypeStruct((packed, D), F32)]
        out_at = [whole((packed, D))] * 2
    else:
        outs = [jax.ShapeDtypeStruct((3 * D, D), BF), jax.ShapeDtypeStruct((16, D), F32)]
        out_at = [whole((3 * D, D)), whole((16, D))]

    def body(*refs):
        qkv_bwd_kernel(*refs, pieces=pieces, blocks=blocks)

    return pl.pallas_call(
        body,
        grid=(blocks,),
        in_specs=[
            pl.BlockSpec(memory_space=pltpu.SMEM),
            step, late, whole((8, D)), step, step, whole((3 * D, D)),
            whole((1, D)), whole((1, D)), whole((1, D)), whole((16, D)),
        ],
        out_specs=out_at + [late],
        out_shape=outs + [jax.ShapeDtypeStruct((rows, D), F32)],
        scratch_shapes=[pltpu.VMEM((3 * D + 16, D), F32), pltpu.VMEM((8, D), F32)],
        compiler_params=pltpu.CompilerParams(vmem_limit_bytes=VMEM_LIMIT),
        cost_estimate=cost(2 * 2 * D * D * 4 * rows, rows * D * 30),
        name="qkv_bwd",
    )(core, x_both, dq, dt, dk, dv, weight, gain, gain_one_grad, gain_two_grad, tap_grads)


def merge(index, keep, got, height, taken):
    rows = keep.shape[0]
    out_rows = taken * height + 16 if taken else rows

    def body(index_ref, keep_ref, got_ref, send_ref, stay_ref):
        if not taken:
            total = keep_ref[...] + got_ref[...].astype(F32)
            send_ref[...] = total.astype(BF)
            stay_ref[...] = total
            return
        for j in range(taken):
            to = pl.ds(j * height, height)
            away = pl.ds(pl.multiple_of(index_ref[j] * height, 16), height)
            here = pl.ds(pl.multiple_of(index_ref[taken + j] * height, 16), height)
            send_ref[to, :] = (keep_ref[away, :] + got_ref[away, :].astype(F32)).astype(BF)
            stay_ref[to, :] = keep_ref[here, :] + got_ref[here, :].astype(F32)
        end = keep_ref[rows - 16 :, :] + got_ref[rows - 16 :, :].astype(F32)
        send_ref[taken * height :, :] = end.astype(BF)
        stay_ref[taken * height :, :] = end

    vmem = pl.BlockSpec(memory_space=pltpu.VMEM)
    return pl.pallas_call(
        body,
        in_specs=[pl.BlockSpec(memory_space=pltpu.SMEM), vmem, vmem],
        out_specs=[vmem, vmem],
        out_shape=[
            jax.ShapeDtypeStruct((out_rows, D), BF),
            jax.ShapeDtypeStruct((out_rows, D), F32),
        ],
        compiler_params=pltpu.CompilerParams(vmem_limit_bytes=32 << 20),
        cost_estimate=cost(rows * D, rows * D * 12),
        name="merge",
    )(index, keep, got)


def merge_grid(index, keep, got, taken):
    height = keep.shape[1]

    def body(index_ref, ka_ref, ga_ref, kb_ref, gb_ref, send_ref, stay_ref):
        send_ref[...] = (ka_ref[...].astype(F32) + ga_ref[...].astype(F32)).astype(BF)
        stay_ref[...] = kb_ref[...].astype(F32) + gb_ref[...].astype(F32)

    away = pl.BlockSpec((1, height, D), lambda i, index: (index[i], 0, 0))
    here = pl.BlockSpec((1, height, D), lambda i, index: (index[taken + i], 0, 0))
    step = pl.BlockSpec((1, height, D), lambda i, index: (i, 0, 0))
    return pl.pallas_call(
        body,
        grid_spec=pltpu.PrefetchScalarGridSpec(
            num_scalar_prefetch=1,
            grid=(taken,),
            in_specs=[away, away, here, here],
            out_specs=[step, step],
        ),
        out_shape=[
            pltpu.HBM((taken, height, D), BF),
            pltpu.HBM((taken, height, D), F32),
        ],
        compiler_params=pltpu.CompilerParams(vmem_limit_bytes=32 << 20),
        cost_estimate=cost(taken * height * D * 2, taken * height * D * 16),
        name="merge_grid",
    )(index, keep, got, keep, got)


def arrange(index, one, two, taken):
    half = one.shape[0]
    height = one.shape[1]

    def body(index_ref, one_ref, two_ref, out_ref):
        for i in range(taken):
            at = index_ref[i]

            @pl.when(at < half)
            def _():
                out_ref[i] = one_ref[jnp.minimum(at, half - 1)]

            @pl.when(at >= half)
            def _():
                out_ref[i] = two_ref[jnp.maximum(at - half, 0)]

    vmem = pl.BlockSpec(memory_space=pltpu.VMEM)
    return pl.pallas_call(
        body,
        in_specs=[pl.BlockSpec(memory_space=pltpu.SMEM), vmem, vmem],
        out_specs=vmem,
        out_shape=jax.ShapeDtypeStruct((taken, height, D), BF),
        compiler_params=pltpu.CompilerParams(vmem_limit_bytes=32 << 20),
        cost_estimate=cost(taken * height * D, taken * height * D * 8),
        name="arrange",
    )(index, one, two)


def join(own, got, shared=16):
    rows = own.shape[0]
    body_rows = rows - shared

    def body(own_ref, got_ref, out_ref):
        out_ref[0:body_rows, :] = own_ref[0:body_rows, :]
        out_ref[body_rows : 2 * body_rows, :] = got_ref[0:body_rows, :]
        if shared:
            out_ref[2 * body_rows :, :] = own_ref[body_rows:, :] + got_ref[body_rows:, :]

    vmem = pl.BlockSpec(memory_space=pltpu.VMEM)
    return pl.pallas_call(
        body,
        in_specs=[vmem, vmem],
        out_specs=vmem,
        out_shape=jax.ShapeDtypeStruct((2 * body_rows + shared, D), BF),
        compiler_params=pltpu.CompilerParams(vmem_limit_bytes=32 << 20),
        cost_estimate=cost(rows * D, rows * D * 8),
        name="join",
    )(own, got)


def join_held(own, got):
    rows = own.shape[0]
    cuts = 4
    size = rows // cuts

    def body(own_ref, got_ref, out_ref, sems):
        copies = []
        for k, ref in enumerate((own_ref, got_ref)):
            for j in range(cuts):
                source = ref.at[pl.ds(j * size, size)]
                to = out_ref.at[pl.ds(k * rows + j * size, size)]
                copies.append(pltpu.make_async_copy(source, to, sems.at[k * cuts + j]))
        for copy in copies:
            copy.start()
        for copy in copies:
            copy.wait()

    held = pl.BlockSpec(memory_space=pltpu.HBM)
    return pl.pallas_call(
        body,
        in_specs=[held, held],
        out_specs=held,
        out_shape=jax.ShapeDtypeStruct((2 * rows, D), BF),
        scratch_shapes=[pltpu.SemaphoreType.DMA((2 * cuts,))],
        compiler_params=pltpu.CompilerParams(vmem_limit_bytes=16 << 20),
        cost_estimate=cost(0, rows * D * 8),
        name="join_held",
    )(own, got)


def hold(block, other):
    held = pl.BlockSpec(memory_space=pl.ANY)
    return pl.pallas_call(
        lambda block_ref, other_ref, out_ref: None,
        in_specs=[held, held],
        out_specs=held,
        out_shape=jax.ShapeDtypeStruct(block.shape, block.dtype),
        input_output_aliases={0: 0},
        name="hold",
    )(block, other)


def qkv_fwd_kernel(index_ref, x_ref, *refs, pieces, blocks):
    if pieces:
        own_ref, got_ref, out_ref, small_ref, weight = refs
    else:
        weight, given_ref, out_ref, small_ref = refs
    i = pl.program_id(0)

    @pl.when(i == 0)
    def _():
        if pieces:
            height = 3 * D // (2 * pieces)
            for j in range(pieces):
                at = pl.ds(j * height, height)
                for k, ref in enumerate((own_ref, got_ref)):
                    to = pl.multiple_of(index_ref[k * pieces + j] * height, 16)
                    weight[pl.ds(to, height), :] = ref[at, :]
            end = pl.ds(pieces * height, 16)
            small_ref[...] = own_ref[end, :].astype(F32) + got_ref[end, :].astype(F32)
        else:
            small_ref[...] = given_ref[...]

    x = x_ref[...].astype(F32)
    hat = x * lax.rsqrt(jnp.mean(x * x, axis=-1, keepdims=True) + norm_eps)
    low = (hat * small_ref[0:1, :]).astype(BF)

    @pl.when(i >= blocks // 2 - 1)
    def _():
        out_ref[:, 0:D] = dot(low, weight[0:D, :]).astype(BF)

    out_ref[:, D : 2 * D] = dot(low, weight[D : 2 * D, :]).astype(BF)
    out_ref[:, 2 * D : 3 * D] = dot(low, weight[2 * D : 3 * D, :]).astype(BF)


def qkv_fwd(index, x_both, weights, rows, pieces):
    blocks = 4
    height = 2 * rows // blocks

    def body(*refs):
        qkv_fwd_kernel(*refs, pieces=pieces, blocks=blocks)

    return pl.pallas_call(
        body,
        grid=(blocks,),
        in_specs=[
            pl.BlockSpec(memory_space=pltpu.SMEM),
            pl.BlockSpec((height, D), lambda i: (i, 0)),
            *[pl.BlockSpec(w.shape, lambda i: (0, 0)) for w in weights],
        ],
        out_specs=[
            pl.BlockSpec((height, 3 * D), lambda i: (i, 0)),
            pl.BlockSpec((16, D), lambda i: (0, 0)),
        ]
        + ([pl.BlockSpec((3 * D, D), lambda i: (0, 0))] if pieces else []),
        out_shape=[
            jax.ShapeDtypeStruct((2 * rows, 3 * D), BF),
            jax.ShapeDtypeStruct((16, D), F32),
        ]
        + ([jax.ShapeDtypeStruct((3 * D, D), BF)] if pieces else []),
        compiler_params=pltpu.CompilerParams(vmem_limit_bytes=VMEM_LIMIT),
        cost_estimate=cost(2 * 2 * rows * D * 3 * D, rows * D * 20),
        name="qkv_fwd",
    )(index, x_both, *weights)


def ffn_kernel(
    state_ref, index_ref, x_ref, att_ref, cot_ref, gain_ref, own_ref, own_two_ref, got_ref, got_two_ref,
    out_ref, gh_ref, ga_ref, gain_grad_ref, away_ref, here_ref,
    hidden, low, total, back, cot, sq, gb, weights, stage_up, stage_down, stage_out, in_sems, sems,
):
    c = pl.program_id(0)
    rows = x_ref.shape[0]
    blocks = [pl.ds(i * QB, QB) for i in range(rows // QB)]
    last = c == pl.num_programs(0) - 1
    core = index_ref[24]

    def fetch(k, j):
        ref = ((own_ref, own_two_ref), (got_ref, got_two_ref))[k][j // 6]
        piece = index_ref[12 * k + j]
        to = weights.at[pl.ds(3 * piece, 3)]
        return pltpu.make_async_copy(ref.at[pl.ds(3 * (j % 6), 3)], to, in_sems.at[piece])

    def fetched(pieces):
        for piece in pieces:
            at = weights.at[pl.ds(3 * piece, 3)]
            pltpu.make_async_copy(own_ref.at[pl.ds(0, 3)], at, in_sems.at[piece]).wait()

    def put(source, group, count, column, sem, wait=False):
        piece = group // 3
        at = (piece // 2) * 3 + group % 3

        def copy(ref):
            to = ref.at[pl.ds(at, count)] if column is None else ref.at[pl.ds(at, count), column]
            return pltpu.make_async_copy(source, to, sems.at[sem])

        if wait:
            copy(here_ref).wait()
            return
        mine = piece % 2 == core

        @pl.when(mine)
        def _():
            copy(here_ref).start()

        @pl.when(jnp.logical_not(mine))
        def _():
            copy(away_ref).start()

    def put_up(i, wait=False):
        start = 0
        k = 0
        while start < 32:
            count = min(3 - (8 + start) % 3, 32 - start)
            put(stage_up.at[i, pl.ds(start, count)], 8 + start, count, i, 20 * i + k, wait)
            start += count
            k += 1

    def put_down(i, wait=False):
        for k in range(8):
            put(stage_down.at[i, pl.ds(k, 1)], 40 + 8 * i + k, 1, None, 20 * i + 12 + k, wait)

    def put_out(wait=False):
        for k in range(8):
            put(stage_out.at[pl.ds(k, 1)], k, 1, None, 80 + k, wait)

    def square(first):
        return weights[first : first + 8].reshape(D, D)

    @pl.when(c == 0)
    def _():
        for k in range(2):
            for j in range(12):
                fetch(k, j).start()
        cot[...] = jnp.where(state_ref[0] > 0, cot_ref[...], jnp.zeros((), BF))
        total[...] = jnp.zeros(total.shape, F32)
        back[...] = jnp.zeros(back.shape, F32)
        fetched(range(3))
        wo = square(0)
        for b in blocks:
            h = x_ref[b, :].astype(F32) + dot(att_ref[b, :], wo)
            hidden[b, :] = h
            hat = h * lax.rsqrt(jnp.mean(h * h, axis=-1, keepdims=True) + norm_eps)
            low[b, :] = (hat * gain_ref[...]).astype(BF)

    for i, pieces in enumerate((range(3, 16), range(16, 19), range(19, 22), range(22, 24))):

        @pl.when(c == i)
        def _():
            fetched(pieces)

    up = weights[8:40, c].reshape(D, D)
    down = weights[pl.ds(40 + 8 * c, 8)].reshape(D, D)
    for b in blocks:
        act = jnp.maximum(dot(low[b, :], up), 0.0)
        s = (act * act).astype(BF)
        sq[b, :] = s
        total[b, :] += dot(s, down)
        g = (dot_nt(cot[b, :], down) * 2.0 * act).astype(BF)
        gb[b, :] = g
        back[b, :] += dot_nt(g, up)
    stage_down[c] = dot_tn(sq[...], cot[...]).reshape(8, 4, 24, D).astype(BF)
    stage_up[c] = dot_tn(low[...], gb[...]).reshape(32, 24, D).astype(BF)
    put_down(c)
    put_up(c)

    @pl.when(last)
    def _():
        gain = gain_ref[...]
        wo = square(0)
        sums = jnp.zeros((1, D), F32)
        for b in blocks:
            h = hidden[b, :]
            out_ref[b, :] = (h + total[b, :]).astype(BF)
            factor = lax.rsqrt(jnp.mean(h * h, axis=-1, keepdims=True) + norm_eps)
            hat = h * factor
            g = back[b, :]
            sums = sums + jnp.sum(g * hat, axis=0, keepdims=True)
            weighted = g * gain
            inner = jnp.mean(weighted * hat, axis=-1, keepdims=True)
            grad = cot[b, :].astype(F32) + factor * (weighted - hat * inner)
            gh_ref[b, :] = grad
            grad_low = grad.astype(BF)
            gb[b, :] = grad_low
            ga_ref[b, :] = dot_nt(grad_low, wo).astype(BF)
        gain_grad_ref[...] = sums
        stage_out[...] = dot_tn(att_ref[...], gb[...]).reshape(8, 4, 24, D).astype(BF)
        put_out()
        for i in range(4):
            put_down(i, True)
            put_up(i, True)
        put_out(True)


def ffn(state, index, tokens, attended, out_grad, gain, weights, rows):
    def whole(shape):
        return pl.BlockSpec(shape, lambda c: (0,) * len(shape), pipeline_mode=pl.Buffered(1))

    act = whole((rows, D))
    held = pl.BlockSpec(memory_space=pl.ANY)
    scalars = pl.BlockSpec(memory_space=pltpu.SMEM)
    half = (36, 4, 24, D)
    return pl.pallas_call(
        ffn_kernel,
        grid=(4,),
        in_specs=[scalars, scalars, act, act, act, whole((1, D)), held, held, held, held],
        out_specs=[act, act, act, whole((1, D)), held, held],
        out_shape=[
            jax.ShapeDtypeStruct((rows, D), BF),
            jax.ShapeDtypeStruct((rows, D), F32),
            jax.ShapeDtypeStruct((rows, D), BF),
            jax.ShapeDtypeStruct((1, D), F32),
            jax.ShapeDtypeStruct(half, BF),
            jax.ShapeDtypeStruct(half, BF),
        ],
        scratch_shapes=[
            pltpu.VMEM((rows, D), F32),
            pltpu.VMEM((rows, D), BF),
            pltpu.VMEM((rows, D), F32),
            pltpu.VMEM((rows, D), F32),
            pltpu.VMEM((rows, D), BF),
            pltpu.VMEM((rows, D), BF),
            pltpu.VMEM((rows, D), BF),
            pltpu.VMEM((72, 4, 24, D), BF),
            pltpu.VMEM((4, 32, 24, D), BF),
            pltpu.VMEM((4, 8, 4, 24, D), BF),
            pltpu.VMEM((8, 4, 24, D), BF),
            pltpu.SemaphoreType.DMA((24,)),
            pltpu.SemaphoreType.DMA((88,)),
        ],
        compiler_params=pltpu.CompilerParams(vmem_limit_bytes=60 << 20),
        cost_estimate=cost(2 * rows * D * D * (24 + 3), 2 * 12 * D * D * 2 + rows * D * 16),
        name="ffn",
    )(state, index, tokens, attended, out_grad, gain, *weights)


def shift_flat(block, distance):
    count = lax.axis_size(AXES)
    route = [(i - distance, i) for i in range(count) if 0 <= i - distance < count]
    return lax.ppermute(block, AXES, route)


def shift_ctx(block, distance):
    count = lax.axis_size("ctx")
    route = [(i - distance, i) for i in range(count) if 0 <= i - distance < count]
    return lax.ppermute(block, "ctx", route)


def after(value, *others):
    return lax.optimization_barrier((value, *others))[0]


def swap(block, even_bit, odd_bit, planes=None):
    count = lax.axis_size(AXES)
    route = [
        (i, i ^ (odd_bit if i & 1 else even_bit))
        for i in range(count)
        if planes is None or i >> 3 in planes
    ]
    return lax.ppermute(block, AXES, route)


def to_aligned(shard, place, count, delta):
    rows = shard.shape[0]
    lag = delta * (count - 1)
    back = -(-lag // rows)
    if back == 1:
        keep = -(-lag // 8) * 8
        parts = [shift_flat(shard[rows - keep :], 1), shard]
    else:
        keep = back * rows
        parts = [shift_flat(shard, s) for s in range(back, 0, -1)] + [shard]
    joined = jnp.concatenate(parts, 0)
    return lax.dynamic_slice_in_dim(joined, keep - delta * place, rows - delta, 0)


def small_part(shard, place, count, delta):
    rows = shard.shape[0]
    extra = count * delta
    zeros = jnp.zeros((extra, 128), shard.dtype)
    joined = jnp.concatenate([zeros, shard, zeros], 0)
    start = extra + count * (rows - delta) - place * rows
    return lax.dynamic_slice_in_dim(joined, jnp.minimum(start, rows + extra), extra, 0)


def from_aligned(chunk, small, place, count, delta, rows):
    aligned = rows - delta
    ahead = -(-(count * delta) // aligned)
    parts = [chunk]
    if ahead == 1:
        keep = small.shape[0]
        got = shift_flat(chunk[:keep], -1)
        parts.append(jnp.where(place == count - 1, small, got))
    else:
        pad = ahead * aligned - small.shape[0]
        tail = jnp.concatenate([small, jnp.zeros((pad, 128), small.dtype)], 0)
        for s in range(1, ahead + 1):
            got = shift_flat(chunk, -s)
            for e in range(s):
                piece = tail[e * aligned : (e + 1) * aligned]
                got = jnp.where(place == count - s + e, piece, got)
            parts.append(got)
    return lax.dynamic_slice_in_dim(jnp.concatenate(parts, 0), delta * place, rows, 0)


def regroup(block):
    return block.reshape(-1, 24, 4, D).transpose(0, 2, 1, 3)


def ungroup(block):
    return block.reshape(-1, 4, 24, D).transpose(0, 2, 1, 3)


def normalize(values, gain):
    factor = lax.rsqrt(jnp.mean(values * values, axis=-1, keepdims=True) + norm_eps)
    scaled = values * factor
    return (scaled, factor, scaled * gain)


def norm_back(grad_in, scaled, factor, gain):
    weighted = grad_in * gain
    inner_mean = jnp.mean(weighted * scaled, axis=-1, keepdims=True)
    return factor * (weighted - scaled * inner_mean)


def adam_update(master, moment_one, moment_two, gradient, step_count, row_start):
    row_index = row_start + jnp.arange(master.shape[0], dtype=jnp.int32)
    matrix_rows = (4 * D * D + 2 * D * FF) // 128
    out_first = 3 * D * D // 128
    out_last = 4 * D * D // 128
    is_matrix = (row_index < matrix_rows)[:, None]
    is_out = ((row_index >= out_first) & (row_index < out_last))[:, None]
    step_rate = jnp.where(is_matrix, jnp.where(is_out, 0.5, 0.1), 1.0)
    decay_rate = jnp.where(is_matrix, 0.1, 0.0)
    step_value = step_count[0].astype(jnp.float32)
    new_one = 0.9 * moment_one + 0.1 * gradient
    new_two = 0.999 * moment_two + 0.001 * gradient * gradient
    corr_first = 1.0 - jnp.power(0.9, step_value)
    corr_second = 1.0 - jnp.power(0.999, step_value)
    new_weights = master - step_rate * (
        new_one / corr_first / (jnp.sqrt(new_two / corr_second) + 1e-08) + decay_rate * master
    )
    return (new_weights, new_one, new_two)


def shards(tokens, out_grad, positions, master, first_moment, second_moment, step_count):
    rows = tokens.shape[0]
    assert rows == SEQ_MIN
    count = lax.axis_size(AXES)
    place = lax.axis_index(AXES).astype(jnp.int32)
    owned = master.shape[0]
    aligned = (4 * D * D + 2 * D * FF) // 128 // count
    delta = owned - aligned
    height = aligned * 128 // D
    staged = count == 32
    first_place = positions[0]
    state = jnp.where(first_place < 0, 0, jnp.where(first_place >= SEQ_MIN, 2, 1)).astype(jnp.int32)
    state_vec = state[None]

    chunk = to_aligned(master, place, count, delta).reshape(-1, D)
    if staged:
        group = 3 * place + jnp.arange(3, dtype=jnp.int32)
        in_up = ((group >= 32) & (group < 64))[:, None, None, None]
        chunk = jnp.where(in_up, regroup(chunk), chunk.reshape(3, 4, 24, D)).reshape(-1, D)
    chunk = chunk.astype(BF)
    small = lax.reduce_precision(small_part(master, place, count, delta), 8, 7)
    core = (place & 1)[None]
    x_bit = (place >> 1) & 1
    y_bit = (place >> 2) & 1
    even = (place & 1) == 0
    if staged:
        z = place >> 3
        mine = jnp.concatenate([chunk, small.astype(BF).reshape(-1, D)], 0)
        tokens_before = shift_ctx(after(tokens, mine), 1)
        got = swap(mine, 16, 16)
        tokens_both = jnp.concatenate([tokens_before, tokens], 0)
        got = after(got, tokens_both)
        rest = jnp.concatenate([chunk, got[:height]], 0)
        none = jnp.zeros((), BF)
        first = jnp.where(z == 0, chunk, jnp.where(z == 2, got[:height], none))
        mine = jnp.concatenate([first, mine[height:] + got[height:]], 0)
        mine = mine + swap(mine, 8, 8)
        across = swap(after(rest, mine), 8, 8)
        mine = join(mine, swap(mine, 2, 4))
        mine = join(mine, swap(mine, 4, 2))
        got = swap(mine, 1, 1)
        index = []
        late_index = []
        for k in (0, 1):
            turn = even if k == 0 else jnp.logical_not(even)
            for j in range(4):
                near, far = j & 1, j >> 1
                x_of = x_bit ^ jnp.where(turn, near, far)
                y_of = y_bit ^ jnp.where(turn, far, near)
                piece = 4 * y_of + 2 * x_of + (core[0] ^ k)
                index.append(piece)
                late_index += [piece, piece + 8, piece + 16]
        index = jnp.stack(index).astype(jnp.int32)
        late_index = jnp.stack(late_index + [core[0]]).astype(jnp.int32)
        projected, small, in_weight = qkv_fwd(index, tokens_both, (mine, got), rows, 4)
        codes = [z ^ k for k in (1, 2, 3)]
        order = [jnp.where(j == 1, 2, jnp.where(j == 2, 1, j)) for j in codes]
        rest = arrange(
            after(jnp.stack(order).astype(jnp.int32), projected), rest.reshape(2, height, D), across.reshape(2, height, D), 3
        ).reshape(-1, D)
        across = swap(rest, 2, 4)
    else:
        tokens_both = jnp.concatenate([shift_ctx(tokens, 1), tokens], 0)
        wide = lax.all_gather(chunk, AXES, axis=0, tiled=True)
        small = lax.psum(small, AXES)[:96].reshape(-1, D)
        in_weight = wide[: 3 * D]
        projected, small = qkv_fwd(core, tokens_both, (in_weight, small), rows, 0)
        late_index = jnp.arange(25, dtype=jnp.int32) % 24
    gain_first = small[0]
    gain_second = small[1]
    taps = small[2:11].reshape(3, 3 * D)

    forward = []
    if staged:
        forward = att_fwd(after(state_vec, rest), projected, taps, forward, 0, rows)
        rest = join_held(after(rest, forward[0]), across)
        line = swap(rest, 4, 2)
        core_rest = swap(rest, 1, 1)
        forward = att_fwd(after(state_vec, rest), projected, taps, forward, 1, rows)
        forward = att_fwd(after(state_vec, core_rest), projected, taps, forward, 2, rows)
        line = hold(line, forward[0])
        core_line = swap(line, 1, 1)
        late_weights = [w.reshape(18, 4, 24, D) for w in (rest, line, core_rest, core_line)]
    else:
        for part in range(PARTS):
            forward = att_fwd(state_vec, projected, taps, forward, part, rows)
        grouped = jnp.concatenate(
            [
                wide[3 * D : 4 * D].reshape(-1, 4, 24, D),
                regroup(wide[4 * D : 8 * D]),
                wide[8 * D :].reshape(-1, 4, 24, D),
            ],
            0,
        )
        late_weights = [grouped[18 * k : 18 * k + 18] for k in range(4)]
    attn_low, logs, *mixed = forward

    layer_out, grad_hidden, grad_attended, grad_gain_two, away_grad, here_grad = ffn(
        state_vec, late_index, tokens, attn_low, out_grad, gain_second[None], late_weights, rows
    )

    def backward(start, done, part):
        return att_bwd(
            start, mixed, attn_low, logs, grad_attended, projected, taps, done, part, rows
        )

    if staged:
        stay = [jnp.where(even, 2 * j + x_bit, 2 * y_bit + j) for j in range(2)]
        away = [jnp.where(even, 2 * j + 1 - x_bit, 2 * (1 - y_bit) + j) for j in range(2)]
        pick_plane = jnp.stack(away + stay).astype(jnp.int32)
        other = jnp.where(even, y_bit, x_bit)
        pick_line = jnp.stack([1 - other, other]).astype(jnp.int32)

        def of_quarters(pick, held):
            half = pick.shape[0] // 2
            steps = [pick[s * half + j] + held * t for s in range(2) for t in range(3) for j in range(half)]
            return jnp.stack(steps)

        late_keep = here_grad.reshape(12, height, D)
        late_got = swap(away_grad.reshape(12, height, D), 1, 1)
        done = backward(state_vec, [], 0)
        late_send, late_keep = merge_grid(
            after(of_quarters(pick_plane, 4), done[4]), late_keep, late_got, 6
        )
        late_got = swap(late_send, 2, 4)
        done = backward(after(state_vec, late_send), done, 1)
        late_send, late_keep = merge_grid(
            after(of_quarters(pick_line, 2), done[4]), late_keep, late_got, 3
        )
        late_got = swap(late_send, 4, 2)
        done = backward(after(state_vec, late_send), done, 2)
        z_even = (z & 1) == 0
        low_pair = [jnp.where(z_even, 0, 0), jnp.where(z_even, 2, 1)]
        high_pair = [jnp.where(z_even, 0, 0), jnp.where(z_even, 1, 2)]
        pick_z = jnp.stack(low_pair + high_pair).astype(jnp.int32)
        late_send, late_keep = merge_grid(after(pick_z, done[4]), late_keep, late_got, 2)
        late_got = swap(late_send, 8, 8)
        sums_state = after(core, late_send)
    else:
        done = []
        for part in range(PARTS):
            done = backward(state_vec, done, part)
        sums_state = core
    *back, tap_grads = done
    grads_before, gain_one_grad = before_bwd(tokens_both, back, in_weight, rows)
    from_next = shift_ctx(grads_before, -1)
    sums = qkv_bwd(
        after(sums_state, grads_before), tokens_both, back, in_weight, gain_first[None], gain_one_grad, grad_gain_two, tap_grads, rows,
        4 if staged else 0,
    )
    grad_normed_one = sums[2]
    scaled_one, factor_one, _ = normalize(tokens.astype(F32), gain_first)
    input_grad = grad_hidden + norm_back(
        grad_normed_one + from_next.astype(F32), scaled_one, factor_one, gain_first
    )

    if staged:
        send, keep = sums[:2]
        high = z >> 1
        pick_last = jnp.stack([1 - high, high]).astype(jnp.int32)
        late_send, late_keep = merge_grid(after(pick_last, send), late_keep, late_got, 1)
        late_got = swap(late_send, 16, 16, (0, 1, 3))
        got = swap(after(send, late_send, from_next), 1, 1)
        send, keep = merge(pick_plane, keep, got, height + 16, 2)
        got = swap(send, 2, 4)
        send, keep = merge(pick_line, keep, got, height + 16, 1)
        got = swap(send, 4, 2)
        send, keep = merge(core, keep, got, height + 16, 0)
        got = swap(send, 8, 8)
        late_got = after(late_got, got)
        send, keep = merge(core, keep, got, height + 16, 0)
        late_chunk = late_keep[0] + late_got[0].astype(F32)
        late_chunk = jnp.where(in_up, ungroup(late_chunk).reshape(3, 4, 24, D), late_chunk.reshape(3, 4, 24, D))
        late_chunk = late_chunk.reshape(-1, D)
        late_next = shift_flat(late_chunk[:16], -1)
        got = swap(send, 16, 16, (1, 2))
        first = keep + got.astype(F32)
        quarter = count // 4
        follow = jnp.where(place < quarter - 1, first[height : height + 16], late_next)
        follow = jnp.where(place == count - 1, first[height + 16 :], follow)
        chunk_grad = jnp.where(place < quarter, first[:height], late_chunk)
        chunk_grad = jnp.concatenate([chunk_grad, follow], 0).reshape(-1, 128)
        gradient = lax.dynamic_slice_in_dim(chunk_grad, delta * place, owned, 0)
    else:
        flat_grad = jnp.stack([here_grad.reshape(12, 3, 4, 24, D), away_grad.reshape(12, 3, 4, 24, D)], 1)
        flat_grad = flat_grad.reshape(72, 4, 24, D)
        wide_grad = jnp.concatenate(
            [
                sums[0],
                flat_grad[:8].reshape(-1, D),
                ungroup(flat_grad[8:40]).reshape(-1, D),
                flat_grad[40:].reshape(-1, D),
            ],
            0,
        )
        chunk_grad = lax.psum_scatter(wide_grad, AXES, scatter_dimension=0, tiled=True).astype(F32)
        used = sums[1].reshape(-1, 128)
        extra = count * delta
        small_grad = jnp.concatenate([used, jnp.zeros((extra - used.shape[0], 128), F32)], 0)
        small_grad = lax.psum(small_grad, AXES)
        gradient = from_aligned(chunk_grad.reshape(-1, 128), small_grad, place, count, delta, owned)
    new_weights, new_one, new_two = adam_update(
        master, first_moment, second_moment, gradient, step_count, place * owned
    )
    return (layer_out, input_grad, new_weights, new_one, new_two, new_weights.astype(BF))


def solution(mesh):
    spread = P(AXES, None)
    return jax.shard_map(
        shards,
        mesh=mesh,
        in_specs=(spread, spread, P(AXES), spread, spread, spread, P()),
        out_specs=(spread,) * 6,
        check_vma=False,
    )
```

```python
import jax
import jax.numpy as jnp
from jax import lax
from jax.experimental import pallas as pl
from jax.experimental.pallas import tpu as pltpu
from jax.sharding import PartitionSpec as P

D = 768
HEADS = 12
HEAD_DIM = 64
FF = 3072
SEQ_MIN = 1024
AXES = ("dp", "ctx")
QB = 256
FORWARD_PARTS = ((0, 2), (2, 2), (4, 2))
BACKWARD_PARTS = ((0, 1), (1, 2), (3, 1), (4, 2))
F32 = jnp.float32
BF = jnp.bfloat16
NT = (((1,), (1,)), ((), ()))
TN = (((0,), (0,)), ((), ()))
norm_eps = 1e-06
VMEM_LIMIT = 56 << 20


def dot(left, right):
    return jnp.dot(left, right, preferred_element_type=F32)


def dot_nt(left, right):
    return lax.dot_general(left, right, NT, preferred_element_type=F32)


def dot_tn(left, right):
    return lax.dot_general(left, right, TN, preferred_element_type=F32)


def cost(flops, nbytes, exps=0):
    return pl.CostEstimate(flops=int(flops), bytes_accessed=int(nbytes), transcendentals=int(exps))


def row_ids(height):
    return lax.broadcasted_iota(jnp.int32, (height, 128), 0)


def conv(out_ref, x_ref, start, tail_ref, taps, rows, state):
    height = x_ref.shape[0]
    for r in range(0, height, QB):
        at = start + r
        if r:
            x = x_ref[r - 16 : r + QB, :].astype(F32)
        else:
            before = jnp.zeros((16, 128), F32)
            if tail_ref is not None:
                before = jnp.concatenate([before[8:], tail_ref[...].astype(F32)], 0)
            x = jnp.concatenate([before, x_ref[0:QB, :].astype(F32)], 0)
        one = pltpu.roll(x, 1, 0)[16:]
        two = pltpu.roll(x, 2, 0)[16:]
        x = x[16:]
        scale = 1.0
        if at >= rows:
            scale = jnp.where(state > 0, 1.0, 0.0)
        if at == 0 or at == rows:
            seen = jnp.where(state == 2, 1.0, 0.0) if at else 0.0
            row = row_ids(QB)
            one = jnp.where(row < 1, one * seen, one)
            two = jnp.where(row < 2, two * seen, two)
        c_one = taps[1:2] * scale
        c_two = taps[2:3] * scale
        out_ref[r : r + QB, :] = (taps[0:1] * x + c_one * one + c_two * two).astype(BF)


def att_fwd_kernel(
    state_ref, tail_ref, q_ref, k_ref, v_ref, tq_ref, tk_ref, tv_ref,
    o_ref, l_ref, qm_ref, km_ref, vm_ref, ka, va,
):
    rows = q_ref.shape[0]
    lane = lax.broadcasted_iota(jnp.int32, (1, 128), 1)
    state = state_ref[0]
    conv(qm_ref, q_ref, rows, tail_ref, tq_ref[...], rows, state)
    conv(km_ref, k_ref, 0, None, tk_ref[...], rows, state)
    conv(vm_ref, v_ref, 0, None, tv_ref[...], rows, state)
    bias = jnp.where(state == 2, 0.0, -1e30)
    for h in range(2):
        mine = (lane < 64) if h == 0 else (lane >= 64)
        base = 64 if h == 0 else 0
        first = jnp.where(lane == base, bias, 0.0).astype(BF)
        for r in range(0, 2 * rows, QB):
            at = pl.ds(r, QB)
            ka[h, at, :] = jnp.where(mine, km_ref[at, :], first if r < rows else jnp.zeros((), BF))
            va[h, at, :] = jnp.where(mine, vm_ref[at, :], jnp.ones((), BF))
    for i in range(rows // QB):
        rs = pl.ds(i * QB, QB)
        outs = []
        sums = []
        qf = qm_ref[rs, :].astype(F32) * 0.125
        for h in range(2):
            mine = (lane < 64) if h == 0 else (lane >= 64)
            base = 64 if h == 0 else 0
            qh = jnp.where(mine, qf, jnp.where(lane == base, 1.0, 0.0)).astype(BF)
            nk = rows + (i + 1) * QB
            s = dot_nt(qh, ka[h, 0:nk, :])
            r = lax.broadcasted_iota(jnp.int32, (QB, QB), 0)
            c = lax.broadcasted_iota(jnp.int32, (QB, QB), 1)
            sd = jnp.where(c <= r, s[:, nk - QB :], -1e30)
            se = s[:, : nk - QB]
            m = jnp.maximum(
                jnp.max(sd, axis=1, keepdims=True), jnp.max(se, axis=1, keepdims=True)
            )
            p = jnp.concatenate([jnp.exp(se - m).astype(BF), jnp.exp(sd - m).astype(BF)], 1)
            o = dot(p, va[h, 0:nk, :])
            outs.append(o / pltpu.roll(o, 64, 1))
            sums.append(m + jnp.log(o))
        res = jnp.where(lane < 64, outs[0], outs[1])
        res = jnp.where(state == 0, vm_ref[pl.ds(rows + i * QB, QB), :].astype(F32), res)
        o_ref[rs, :] = res.astype(BF)
        l_ref[rs, :] = jnp.where(lane < 64, sums[1], sums[0])


def call_in_parts(body, in_specs, out_specs, out_shape, earlier, part, **options):
    used = len(in_specs)

    def kernel(*refs):
        body(*refs[:used], *refs[used + len(earlier) :])

    return pl.pallas_call(
        kernel,
        grid=(part[1],),
        in_specs=in_specs + [pl.BlockSpec(memory_space=pl.ANY)] * len(earlier),
        out_specs=out_specs,
        out_shape=out_shape,
        input_output_aliases={used + i: i for i in range(len(earlier))},
        compiler_params=pltpu.CompilerParams(vmem_limit_bytes=VMEM_LIMIT),
        **options,
    )


def columns(part):
    first = part[0]

    def cols(height, row, off):
        return pl.BlockSpec((height, 128), lambda p: (row, p + first + off))

    taps_at = [
        pl.BlockSpec((3, 128), lambda p, off=off: (0, p + first + off)) for off in (0, 6, 12)
    ]
    return cols, taps_at


def att_fwd(state, projected, taps, earlier, part, rows):
    cols, taps_at = columns(part)
    return call_in_parts(
        att_fwd_kernel,
        [
            pl.BlockSpec(memory_space=pltpu.SMEM),
            cols(8, rows // 8 - 1, 0),
            cols(rows, 1, 0),
            cols(2 * rows, 0, 6),
            cols(2 * rows, 0, 12),
            *taps_at,
        ],
        [cols(rows, 0, 0)] * 3 + [cols(2 * rows, 0, 0)] * 2,
        [
            jax.ShapeDtypeStruct((rows, D), BF),
            jax.ShapeDtypeStruct((rows, D), F32),
            jax.ShapeDtypeStruct((rows, D), BF),
            jax.ShapeDtypeStruct((2 * rows, D), BF),
            jax.ShapeDtypeStruct((2 * rows, D), BF),
        ],
        earlier,
        part,
        scratch_shapes=[pltpu.VMEM((2, 2 * rows, 128), BF)] * 2,
        cost_estimate=cost(
            2 * 2 * 2 * rows * rows * 1.5 * 256 * part[1],
            rows * D * 5 * part[1],
            2 * rows * rows * 1.5 * part[1],
        ),
        name="att_fwd",
    )(state, projected, projected, projected, projected, taps, taps, taps, *earlier)


def three(x, lane, base):
    hi = x.astype(BF).astype(F32)
    r = x - hi
    mid = r.astype(BF).astype(F32)
    lo = r - mid
    return jnp.where(
        lane == base, hi, jnp.where(lane == base + 1, mid, jnp.where(lane == base + 2, lo, 0.0))
    )


def conv_back(out_ref, grad_ref, x_ref, start, tail, taps, rows, state):
    height = grad_ref.shape[0]
    joint = jnp.where(state == 2, 1.0, 0.0)
    sums = [jnp.zeros((1, 128), F32)] * 3

    def add(parts, x):
        return [s + jnp.sum(g * x, axis=0, keepdims=True) for s, g in zip(sums, parts)]

    for r in range(0, height, QB):
        ends = r + QB == height
        meets = start + r + QB == rows
        if ends:
            grad = jnp.concatenate([grad_ref[r : r + QB, :], jnp.zeros((8, 128), F32)], 0)
        else:
            grad = grad_ref[r : r + QB + 8, :]
        one = pltpu.roll(grad, QB + 7, 0)[:QB]
        two = pltpu.roll(grad, QB + 6, 0)[:QB]
        grad = grad[:QB]
        if meets and not ends:
            row = row_ids(QB)
            one = jnp.where(row >= QB - 1, one * joint, one)
            two = jnp.where(row >= QB - 2, two * joint, two)
        out_ref[r : r + QB, :] = (taps[0:1] * grad + taps[1:2] * one + taps[2:3] * two).astype(BF)
        sums = add((grad, one, two), x_ref[r : r + QB, :].astype(F32))
    if tail is not None:
        grad = jnp.concatenate([jnp.zeros((8, 128), F32), grad_ref[0:8, :]], 0)
        one = pltpu.roll(grad, 15, 0)[:8] * joint
        two = pltpu.roll(grad, 14, 0)[:8] * joint
        tail[0][...] = (taps[1:2] * one + taps[2:3] * two).astype(BF)
        sums = add((grad[:8], one, two), tail[1][...].astype(F32))
    return sums


def att_bwd_kernel(
    state_ref, q_ref, k_ref, v_ref, o_ref, l_ref, do_ref, xt_ref, xq_ref, xk_ref, xv_ref,
    tq_ref, tk_ref, tv_ref,
    pq_ref, pt_ref, pk_ref, pv_ref, tg_ref, qa, da, qt, dt, kt, dqt, dqs, dks, dvs,
):
    rows = q_ref.shape[0]
    lane = lax.broadcasted_iota(jnp.int32, (1, 128), 1)
    second = state_ref[0] == 2
    for r in range(0, rows, QB):
        at = pl.ds(r, QB)
        do = do_ref[at, :].astype(F32)
        od = do * o_ref[at, :].astype(F32)
        qf = q_ref[at, :].astype(F32) * 0.125
        lv = l_ref[at, :]
        for h in range(2):
            mine = (lane < 64) if h == 0 else (lane >= 64)
            base = 64 if h == 0 else 0
            delta = jnp.sum(jnp.where(mine, od, 0.0), axis=1, keepdims=True)
            qa[h, at, :] = jnp.where(mine, qf, three(-lv, lane, base)).astype(BF)
            da[h, at, :] = jnp.where(mine, do, three(-delta, lane, base)).astype(BF)
        qt[:, at] = jnp.transpose(qf).astype(BF)
        dt[:, at] = jnp.transpose(do).astype(BF)
    for r in range(0, 2 * rows, QB):
        at = pl.ds(r, QB)
        kt[:, at] = jnp.transpose(k_ref[at, :].astype(F32)).astype(BF)
    dqt[...] = jnp.zeros(dqt.shape, F32)

    def keys(ks, first, diagonal):
        kk = k_ref[ks, :]
        vv = v_ref[ks, :]
        dv = []
        dk = []
        for h in range(2):
            mine = (lane < 64) if h == 0 else (lane >= 64)
            base = 64 if h == 0 else 0
            ones3 = ((lane >= base) & (lane < base + 3)).astype(BF)
            hs = slice(64 * h, 64 * h + 64)
            st = dot_nt(jnp.where(mine, kk, ones3), qa[h, first:rows, :])
            dp = dot_nt(jnp.where(mine, vv, ones3), da[h, first:rows, :])
            p = jnp.exp(st)
            if diagonal:
                r = lax.broadcasted_iota(jnp.int32, (QB, QB), 0)
                c = lax.broadcasted_iota(jnp.int32, (QB, QB), 1)
                seen = jnp.where(r <= c, p[:, :QB], 0.0)
                p = jnp.concatenate([seen, p[:, QB:]], 1) if first + QB < rows else seen
            ds = (p * dp).astype(BF)
            dv.append(dot_nt(dt[hs, first:rows], p.astype(BF)))
            dk.append(dot_nt(qt[hs, first:rows], ds))
            dqt[hs, first:rows] += dot(kt[hs, ks], ds)
        dvs[ks, :] = jnp.transpose(jnp.concatenate(dv, 0))
        dks[ks, :] = jnp.transpose(jnp.concatenate(dk, 0))

    for j in range(rows // QB):
        keys(pl.ds(rows + j * QB, QB), j * QB, True)

    @pl.when(second)
    def _():
        def step(j, carry):
            keys(pl.ds(pl.multiple_of(j * QB, QB), QB), 0, False)
            return carry

        lax.fori_loop(0, rows // QB, step, 0)

    @pl.when(jnp.logical_not(second))
    def _():
        dks[0:rows, :] = jnp.zeros((rows, 128), F32)
        dvs[0:rows, :] = jnp.zeros((rows, 128), F32)

    for r in range(0, rows, QB):
        dqs[r : r + QB, :] = jnp.transpose(dqt[:, r : r + QB]) * 0.125
    state = state_ref[0]
    sq = conv_back(pq_ref, dqs, xq_ref, rows, (pt_ref, xt_ref), tq_ref[...], rows, state)
    sk = conv_back(pk_ref, dks, xk_ref, 0, None, tk_ref[...], rows, state)
    sv = conv_back(pv_ref, dvs, xv_ref, 0, None, tv_ref[...], rows, state)
    tg_ref[...] = jnp.zeros(tg_ref.shape, F32)
    for j in range(3):
        for m, s in enumerate((sq, sk, sv)):
            tg_ref[3 * j + m : 3 * j + m + 1, :] = s[j]


def att_bwd(state, mixed, attended, logs, grad, projected, taps, earlier, part, rows):
    cols, taps_at = columns(part)
    own = cols(rows, 0, 0)
    both = cols(2 * rows, 0, 0)
    return call_in_parts(
        att_bwd_kernel,
        [
            pl.BlockSpec(memory_space=pltpu.SMEM),
            own, both, both, own, own, own,
            cols(8, rows // 8 - 1, 0),
            cols(rows, 1, 0),
            cols(2 * rows, 0, 6),
            cols(2 * rows, 0, 12),
            *taps_at,
        ],
        [own, cols(8, 0, 0), both, both, cols(16, 0, 0)],
        [
            jax.ShapeDtypeStruct((rows, D), BF),
            jax.ShapeDtypeStruct((8, D), BF),
            jax.ShapeDtypeStruct((2 * rows, D), BF),
            jax.ShapeDtypeStruct((2 * rows, D), BF),
            jax.ShapeDtypeStruct((16, D), F32),
        ],
        earlier,
        part,
        scratch_shapes=[
            pltpu.VMEM((2, rows, 128), BF),
            pltpu.VMEM((2, rows, 128), BF),
            pltpu.VMEM((128, rows), BF),
            pltpu.VMEM((128, rows), BF),
            pltpu.VMEM((128, 2 * rows), BF),
            pltpu.VMEM((128, rows), F32),
            pltpu.VMEM((rows, 128), F32),
            pltpu.VMEM((2 * rows, 128), F32),
            pltpu.VMEM((2 * rows, 128), F32),
        ],
        cost_estimate=cost(
            5 * 2 * 2 * rows * rows * 1.5 * 256 * part[1],
            rows * D * 7 * part[1],
            2 * rows * rows * 1.5 * part[1],
        ),
        name="att_bwd",
    )(state, *mixed, attended, logs, grad, projected, projected, projected, projected,
      taps, taps, taps, *earlier)


def unit_rows(x):
    return x * lax.rsqrt(jnp.mean(x * x, axis=-1, keepdims=True) + norm_eps)


def before_bwd_kernel(x_ref, dt_ref, dk_ref, dv_ref, w_ref, out_ref, gain_ref):
    i = pl.program_id(0)
    hat = unit_rows(x_ref[...].astype(F32))
    gn = dot_nt(dk_ref[...], w_ref[D : 2 * D, :]) + dot_nt(dv_ref[...], w_ref[2 * D : 3 * D, :])

    last_step = pl.num_programs(0) - 1

    @pl.when(i == 0)
    def _():
        gain_ref[...] = jnp.zeros(gain_ref.shape, F32)

    @pl.when(i < last_step)
    def _():
        out_ref[...] = gn.astype(BF)
        gain_ref[...] += jnp.sum(gn * hat, axis=0, keepdims=True)

    @pl.when(i == last_step)
    def _():
        last = gn.shape[0] - 8
        full = jnp.concatenate([gn[:last], gn[last:] + dot_nt(dt_ref[...], w_ref[0:D, :])], 0)
        out_ref[...] = full.astype(BF)
        gain_ref[...] += jnp.sum(full * hat, axis=0, keepdims=True)


def before_bwd(x_both, back, weight, rows):
    dt, dk, dv = back[1:]
    blocks = 4
    height = rows // blocks
    step = pl.BlockSpec((height, D), lambda i: (i, 0))

    def whole(shape):
        return pl.BlockSpec(shape, lambda i: (0, 0))

    return pl.pallas_call(
        before_bwd_kernel,
        grid=(blocks,),
        in_specs=[step, whole((8, D)), step, step, whole((3 * D, D))],
        out_specs=[step, whole((1, D))],
        out_shape=[jax.ShapeDtypeStruct((rows, D), BF), jax.ShapeDtypeStruct((1, D), F32)],
        compiler_params=pltpu.CompilerParams(vmem_limit_bytes=VMEM_LIMIT),
        cost_estimate=cost(2 * rows * D * D * 2, rows * D * 12),
        name="before_bwd",
    )(x_both, dt, dk, dv, weight)


def qkv_bwd_kernel(
    core_ref, x_ref, dq_ref, dt_ref, dk_ref, dv_ref, w_ref, gain_ref, gain_one_ref, gain_two_ref, tg_ref,
    *refs, pieces, blocks,
):
    if pieces:
        send_ref, keep_ref, own_ref, acc, gacc = refs
    else:
        keep_ref, small_ref, own_ref, acc, gacc = refs
    i = pl.program_id(0)
    half = blocks // 2

    @pl.when(i == 0)
    def _():
        acc[...] = jnp.zeros(acc.shape, F32)
        gacc[0:1, :] = gain_one_ref[...]

    hat = unit_rows(x_ref[...].astype(F32))
    low = (hat * gain_ref[...]).astype(BF)
    dk = dk_ref[...]
    dv = dv_ref[...]
    acc[D : 2 * D, :] += dot_tn(low, dk)
    acc[2 * D : 3 * D, :] += dot_tn(low, dv)

    @pl.when(i == half - 1)
    def _():
        acc[0:D, :] += dot_tn(low[low.shape[0] - 8 :], dt_ref[...])

    @pl.when(i >= half)
    def _():
        dq = dq_ref[...]
        acc[0:D, :] += dot_tn(low, dq)
        full = (
            dot_nt(dk, w_ref[D : 2 * D, :])
            + dot_nt(dv, w_ref[2 * D : 3 * D, :])
            + dot_nt(dq, w_ref[0:D, :])
        )
        own_ref[...] = full
        gacc[0:1, :] += jnp.sum(full * hat, axis=0, keepdims=True)

    @pl.when(i == blocks - 1)
    def _():
        small = jnp.concatenate(
            [gacc[0:1, :], gain_two_ref[...], tg_ref[0:9, :], jnp.zeros((5, D), F32)], 0
        )
        if pieces:
            core = core_ref[0]
            height = 3 * D // (2 * pieces)
            wide = height + 16
            for j in range(pieces):
                to = pl.ds(j * wide, wide)
                away = pl.ds(pl.multiple_of((2 * j + 1 - core) * height, 16), wide)
                here = pl.ds(pl.multiple_of((2 * j + core) * height, 16), wide)
                send_ref[to, :] = acc[away, :].astype(BF)
                keep_ref[to, :] = acc[here, :]
            send_ref[pieces * wide :, :] = small.astype(BF)
            keep_ref[pieces * wide :, :] = small
        else:
            keep_ref[...] = acc[0 : 3 * D, :].astype(BF)
            small_ref[...] = small


def qkv_bwd(core, x_both, back, weight, gain, gain_one_grad, gain_two_grad, tap_grads, rows, pieces):
    dq, dt, dk, dv = back
    blocks = 4
    half = blocks // 2
    height = 2 * rows // blocks
    step = pl.BlockSpec((height, D), lambda i: (i, 0))
    late = pl.BlockSpec((height, D), lambda i: (jnp.maximum(i - half, 0), 0))

    def whole(shape):
        return pl.BlockSpec(shape, lambda i: (0, 0))

    if pieces:
        packed = 3 * D // 2 + 16 * pieces + 16
        outs = [jax.ShapeDtypeStruct((packed, D), BF), jax.ShapeDtypeStruct((packed, D), F32)]
        out_at = [whole((packed, D))] * 2
    else:
        outs = [jax.ShapeDtypeStruct((3 * D, D), BF), jax.ShapeDtypeStruct((16, D), F32)]
        out_at = [whole((3 * D, D)), whole((16, D))]

    def body(*refs):
        qkv_bwd_kernel(*refs, pieces=pieces, blocks=blocks)

    return pl.pallas_call(
        body,
        grid=(blocks,),
        in_specs=[
            pl.BlockSpec(memory_space=pltpu.SMEM),
            step, late, whole((8, D)), step, step, whole((3 * D, D)),
            whole((1, D)), whole((1, D)), whole((1, D)), whole((16, D)),
        ],
        out_specs=out_at + [late],
        out_shape=outs + [jax.ShapeDtypeStruct((rows, D), F32)],
        scratch_shapes=[pltpu.VMEM((3 * D + 16, D), F32), pltpu.VMEM((8, D), F32)],
        compiler_params=pltpu.CompilerParams(vmem_limit_bytes=VMEM_LIMIT),
        cost_estimate=cost(2 * 2 * D * D * 4 * rows, rows * D * 30),
        name="qkv_bwd",
    )(core, x_both, dq, dt, dk, dv, weight, gain, gain_one_grad, gain_two_grad, tap_grads)


def merge(index, keep, got, height, taken):
    rows = keep.shape[0]
    out_rows = taken * height + 16 if taken else rows

    def body(index_ref, keep_ref, got_ref, send_ref, stay_ref):
        if not taken:
            total = keep_ref[...] + got_ref[...].astype(F32)
            send_ref[...] = total.astype(BF)
            stay_ref[...] = total
            return
        for j in range(taken):
            to = pl.ds(j * height, height)
            away = pl.ds(pl.multiple_of(index_ref[j] * height, 16), height)
            here = pl.ds(pl.multiple_of(index_ref[taken + j] * height, 16), height)
            send_ref[to, :] = (keep_ref[away, :] + got_ref[away, :].astype(F32)).astype(BF)
            stay_ref[to, :] = keep_ref[here, :] + got_ref[here, :].astype(F32)
        end = keep_ref[rows - 16 :, :] + got_ref[rows - 16 :, :].astype(F32)
        send_ref[taken * height :, :] = end.astype(BF)
        stay_ref[taken * height :, :] = end

    vmem = pl.BlockSpec(memory_space=pltpu.VMEM)
    return pl.pallas_call(
        body,
        in_specs=[pl.BlockSpec(memory_space=pltpu.SMEM), vmem, vmem],
        out_specs=[vmem, vmem],
        out_shape=[
            jax.ShapeDtypeStruct((out_rows, D), BF),
            jax.ShapeDtypeStruct((out_rows, D), F32),
        ],
        compiler_params=pltpu.CompilerParams(vmem_limit_bytes=32 << 20),
        cost_estimate=cost(rows * D, rows * D * 12),
        name="merge",
    )(index, keep, got)


def merge_grid(index, keep, got, taken):
    height = keep.shape[1]

    def body(index_ref, ka_ref, ga_ref, kb_ref, gb_ref, send_ref, stay_ref):
        send_ref[...] = (ka_ref[...].astype(F32) + ga_ref[...].astype(F32)).astype(BF)
        stay_ref[...] = kb_ref[...].astype(F32) + gb_ref[...].astype(F32)

    away = pl.BlockSpec((1, height, D), lambda i, index: (index[i], 0, 0))
    here = pl.BlockSpec((1, height, D), lambda i, index: (index[taken + i], 0, 0))
    step = pl.BlockSpec((1, height, D), lambda i, index: (i, 0, 0))
    return pl.pallas_call(
        body,
        grid_spec=pltpu.PrefetchScalarGridSpec(
            num_scalar_prefetch=1,
            grid=(taken,),
            in_specs=[away, away, here, here],
            out_specs=[step, step],
        ),
        out_shape=[
            pltpu.HBM((taken, height, D), BF),
            pltpu.HBM((taken, height, D), F32),
        ],
        compiler_params=pltpu.CompilerParams(vmem_limit_bytes=32 << 20),
        cost_estimate=cost(taken * height * D * 2, taken * height * D * 16),
        name="merge_grid",
    )(index, keep, got, keep, got)


def arrange(index, one, two, taken):
    half = one.shape[0]
    height = one.shape[1]

    def body(index_ref, one_ref, two_ref, out_ref):
        for i in range(taken):
            at = index_ref[i]

            @pl.when(at < half)
            def _():
                out_ref[i] = one_ref[jnp.minimum(at, half - 1)]

            @pl.when(at >= half)
            def _():
                out_ref[i] = two_ref[jnp.maximum(at - half, 0)]

    vmem = pl.BlockSpec(memory_space=pltpu.VMEM)
    return pl.pallas_call(
        body,
        in_specs=[pl.BlockSpec(memory_space=pltpu.SMEM), vmem, vmem],
        out_specs=vmem,
        out_shape=jax.ShapeDtypeStruct((taken, height, D), BF),
        compiler_params=pltpu.CompilerParams(vmem_limit_bytes=32 << 20),
        cost_estimate=cost(taken * height * D, taken * height * D * 8),
        name="arrange",
    )(index, one, two)


def join(own, got, shared=16):
    rows = own.shape[0]
    body_rows = rows - shared

    def body(own_ref, got_ref, out_ref):
        out_ref[0:body_rows, :] = own_ref[0:body_rows, :]
        out_ref[body_rows : 2 * body_rows, :] = got_ref[0:body_rows, :]
        if shared:
            out_ref[2 * body_rows :, :] = own_ref[body_rows:, :] + got_ref[body_rows:, :]

    vmem = pl.BlockSpec(memory_space=pltpu.VMEM)
    return pl.pallas_call(
        body,
        in_specs=[vmem, vmem],
        out_specs=vmem,
        out_shape=jax.ShapeDtypeStruct((2 * body_rows + shared, D), BF),
        compiler_params=pltpu.CompilerParams(vmem_limit_bytes=32 << 20),
        cost_estimate=cost(rows * D, rows * D * 8),
        name="join",
    )(own, got)


def join_held(own, got):
    rows = own.shape[0]
    cuts = 4
    size = rows // cuts

    def body(own_ref, got_ref, out_ref, sems):
        copies = []
        for k, ref in enumerate((own_ref, got_ref)):
            for j in range(cuts):
                source = ref.at[pl.ds(j * size, size)]
                to = out_ref.at[pl.ds(k * rows + j * size, size)]
                copies.append(pltpu.make_async_copy(source, to, sems.at[k * cuts + j]))
        for copy in copies:
            copy.start()
        for copy in copies:
            copy.wait()

    held = pl.BlockSpec(memory_space=pltpu.HBM)
    return pl.pallas_call(
        body,
        in_specs=[held, held],
        out_specs=held,
        out_shape=jax.ShapeDtypeStruct((2 * rows, D), BF),
        scratch_shapes=[pltpu.SemaphoreType.DMA((2 * cuts,))],
        compiler_params=pltpu.CompilerParams(vmem_limit_bytes=16 << 20),
        cost_estimate=cost(0, rows * D * 8),
        name="join_held",
    )(own, got)


def hold(block, other):
    held = pl.BlockSpec(memory_space=pl.ANY)
    return pl.pallas_call(
        lambda block_ref, other_ref, out_ref: None,
        in_specs=[held, held],
        out_specs=held,
        out_shape=jax.ShapeDtypeStruct(block.shape, block.dtype),
        input_output_aliases={0: 0},
        name="hold",
    )(block, other)


def qkv_fwd_kernel(index_ref, x_ref, *refs, pieces, blocks):
    if pieces:
        own_ref, got_ref, out_ref, small_ref, weight = refs
    else:
        weight, given_ref, out_ref, small_ref = refs
    i = pl.program_id(0)

    @pl.when(i == 0)
    def _():
        if pieces:
            height = 3 * D // (2 * pieces)
            for j in range(pieces):
                at = pl.ds(j * height, height)
                for k, ref in enumerate((own_ref, got_ref)):
                    to = pl.multiple_of(index_ref[k * pieces + j] * height, 16)
                    weight[pl.ds(to, height), :] = ref[at, :]
            end = pl.ds(pieces * height, 16)
            small_ref[...] = own_ref[end, :].astype(F32) + got_ref[end, :].astype(F32)
        else:
            small_ref[...] = given_ref[...]

    x = x_ref[...].astype(F32)
    hat = x * lax.rsqrt(jnp.mean(x * x, axis=-1, keepdims=True) + norm_eps)
    low = (hat * small_ref[0:1, :]).astype(BF)

    @pl.when(i >= blocks // 2 - 1)
    def _():
        out_ref[:, 0:D] = dot(low, weight[0:D, :]).astype(BF)

    out_ref[:, D : 2 * D] = dot(low, weight[D : 2 * D, :]).astype(BF)
    out_ref[:, 2 * D : 3 * D] = dot(low, weight[2 * D : 3 * D, :]).astype(BF)


def qkv_fwd(index, x_both, weights, rows, pieces):
    blocks = 4
    height = 2 * rows // blocks

    def body(*refs):
        qkv_fwd_kernel(*refs, pieces=pieces, blocks=blocks)

    return pl.pallas_call(
        body,
        grid=(blocks,),
        in_specs=[
            pl.BlockSpec(memory_space=pltpu.SMEM),
            pl.BlockSpec((height, D), lambda i: (i, 0)),
            *[pl.BlockSpec(w.shape, lambda i: (0, 0)) for w in weights],
        ],
        out_specs=[
            pl.BlockSpec((height, 3 * D), lambda i: (i, 0)),
            pl.BlockSpec((16, D), lambda i: (0, 0)),
        ]
        + ([pl.BlockSpec((3 * D, D), lambda i: (0, 0))] if pieces else []),
        out_shape=[
            jax.ShapeDtypeStruct((2 * rows, 3 * D), BF),
            jax.ShapeDtypeStruct((16, D), F32),
        ]
        + ([jax.ShapeDtypeStruct((3 * D, D), BF)] if pieces else []),
        compiler_params=pltpu.CompilerParams(vmem_limit_bytes=VMEM_LIMIT),
        cost_estimate=cost(2 * 2 * rows * D * 3 * D, rows * D * 20),
        name="qkv_fwd",
    )(index, x_both, *weights)


def ffn_kernel(
    state_ref, index_ref, x_ref, att_ref, cot_ref, gain_ref, own_ref, own_two_ref, got_ref, got_two_ref,
    out_ref, gh_ref, ga_ref, gain_grad_ref, away_ref, here_ref,
    hidden, low, total, back, cot, sq, gb, weights, stage_up, stage_down, stage_out, in_sems, sems,
):
    c = pl.program_id(0)
    rows = x_ref.shape[0]
    blocks = [pl.ds(i * QB, QB) for i in range(rows // QB)]
    last = c == pl.num_programs(0) - 1
    core = index_ref[24]

    def fetch(k, j):
        ref = ((own_ref, own_two_ref), (got_ref, got_two_ref))[k][j // 6]
        piece = index_ref[12 * k + j]
        to = weights.at[pl.ds(3 * piece, 3)]
        return pltpu.make_async_copy(ref.at[pl.ds(3 * (j % 6), 3)], to, in_sems.at[piece])

    def fetched(pieces):
        for piece in pieces:
            at = weights.at[pl.ds(3 * piece, 3)]
            pltpu.make_async_copy(own_ref.at[pl.ds(0, 3)], at, in_sems.at[piece]).wait()

    def put(source, group, count, column, sem, wait=False):
        piece = group // 3
        at = (piece // 2) * 3 + group % 3

        def copy(ref):
            to = ref.at[pl.ds(at, count)] if column is None else ref.at[pl.ds(at, count), column]
            return pltpu.make_async_copy(source, to, sems.at[sem])

        if wait:
            copy(here_ref).wait()
            return
        mine = piece % 2 == core

        @pl.when(mine)
        def _():
            copy(here_ref).start()

        @pl.when(jnp.logical_not(mine))
        def _():
            copy(away_ref).start()

    def put_up(i, wait=False):
        start = 0
        k = 0
        while start < 32:
            count = min(3 - (8 + start) % 3, 32 - start)
            put(stage_up.at[i, pl.ds(start, count)], 8 + start, count, i, 20 * i + k, wait)
            start += count
            k += 1

    def put_down(i, wait=False):
        for k in range(8):
            put(stage_down.at[i, pl.ds(k, 1)], 40 + 8 * i + k, 1, None, 20 * i + 12 + k, wait)

    def put_out(wait=False):
        for k in range(8):
            put(stage_out.at[pl.ds(k, 1)], k, 1, None, 80 + k, wait)

    def square(first):
        return weights[first : first + 8].reshape(D, D)

    @pl.when(c == 0)
    def _():
        for k in range(2):
            for j in range(12):
                fetch(k, j).start()
        cot[...] = jnp.where(state_ref[0] > 0, cot_ref[...], jnp.zeros((), BF))
        total[...] = jnp.zeros(total.shape, F32)
        back[...] = jnp.zeros(back.shape, F32)
        fetched(range(3))
        wo = square(0)
        for b in blocks:
            h = x_ref[b, :].astype(F32) + dot(att_ref[b, :], wo)
            hidden[b, :] = h
            hat = h * lax.rsqrt(jnp.mean(h * h, axis=-1, keepdims=True) + norm_eps)
            low[b, :] = (hat * gain_ref[...]).astype(BF)

    for i, pieces in enumerate((range(3, 16), range(16, 19), range(19, 22), range(22, 24))):

        @pl.when(c == i)
        def _():
            fetched(pieces)

    up = weights[8:40, c].reshape(D, D)
    down = weights[pl.ds(40 + 8 * c, 8)].reshape(D, D)
    for b in blocks:
        act = jnp.maximum(dot(low[b, :], up), 0.0)
        s = (act * act).astype(BF)
        sq[b, :] = s
        total[b, :] += dot(s, down)
        g = (dot_nt(cot[b, :], down) * 2.0 * act).astype(BF)
        gb[b, :] = g
        back[b, :] += dot_nt(g, up)
    stage_down[c] = dot_tn(sq[...], cot[...]).reshape(8, 4, 24, D).astype(BF)
    stage_up[c] = dot_tn(low[...], gb[...]).reshape(32, 24, D).astype(BF)
    put_down(c)
    put_up(c)

    @pl.when(last)
    def _():
        gain = gain_ref[...]
        wo = square(0)
        sums = jnp.zeros((1, D), F32)
        for b in blocks:
            h = hidden[b, :]
            out_ref[b, :] = (h + total[b, :]).astype(BF)
            factor = lax.rsqrt(jnp.mean(h * h, axis=-1, keepdims=True) + norm_eps)
            hat = h * factor
            g = back[b, :]
            sums = sums + jnp.sum(g * hat, axis=0, keepdims=True)
            weighted = g * gain
            inner = jnp.mean(weighted * hat, axis=-1, keepdims=True)
            grad = cot[b, :].astype(F32) + factor * (weighted - hat * inner)
            gh_ref[b, :] = grad
            grad_low = grad.astype(BF)
            gb[b, :] = grad_low
            ga_ref[b, :] = dot_nt(grad_low, wo).astype(BF)
        gain_grad_ref[...] = sums
        stage_out[...] = dot_tn(att_ref[...], gb[...]).reshape(8, 4, 24, D).astype(BF)
        put_out()
        for i in range(4):
            put_down(i, True)
            put_up(i, True)
        put_out(True)


def ffn(state, index, tokens, attended, out_grad, gain, weights, rows):
    def whole(shape):
        return pl.BlockSpec(shape, lambda c: (0,) * len(shape), pipeline_mode=pl.Buffered(1))

    act = whole((rows, D))
    held = pl.BlockSpec(memory_space=pl.ANY)
    scalars = pl.BlockSpec(memory_space=pltpu.SMEM)
    half = (36, 4, 24, D)
    return pl.pallas_call(
        ffn_kernel,
        grid=(4,),
        in_specs=[scalars, scalars, act, act, act, whole((1, D)), held, held, held, held],
        out_specs=[act, act, act, whole((1, D)), held, held],
        out_shape=[
            jax.ShapeDtypeStruct((rows, D), BF),
            jax.ShapeDtypeStruct((rows, D), F32),
            jax.ShapeDtypeStruct((rows, D), BF),
            jax.ShapeDtypeStruct((1, D), F32),
            jax.ShapeDtypeStruct(half, BF),
            jax.ShapeDtypeStruct(half, BF),
        ],
        scratch_shapes=[
            pltpu.VMEM((rows, D), F32),
            pltpu.VMEM((rows, D), BF),
            pltpu.VMEM((rows, D), F32),
            pltpu.VMEM((rows, D), F32),
            pltpu.VMEM((rows, D), BF),
            pltpu.VMEM((rows, D), BF),
            pltpu.VMEM((rows, D), BF),
            pltpu.VMEM((72, 4, 24, D), BF),
            pltpu.VMEM((4, 32, 24, D), BF),
            pltpu.VMEM((4, 8, 4, 24, D), BF),
            pltpu.VMEM((8, 4, 24, D), BF),
            pltpu.SemaphoreType.DMA((24,)),
            pltpu.SemaphoreType.DMA((88,)),
        ],
        compiler_params=pltpu.CompilerParams(vmem_limit_bytes=60 << 20),
        cost_estimate=cost(2 * rows * D * D * (24 + 3), 2 * 12 * D * D * 2 + rows * D * 16),
        name="ffn",
    )(state, index, tokens, attended, out_grad, gain, *weights)


def shift_flat(block, distance):
    count = lax.axis_size(AXES)
    route = [(i - distance, i) for i in range(count) if 0 <= i - distance < count]
    return lax.ppermute(block, AXES, route)


def shift_ctx(block, distance):
    count = lax.axis_size("ctx")
    route = [(i - distance, i) for i in range(count) if 0 <= i - distance < count]
    return lax.ppermute(block, "ctx", route)


def after(value, *others):
    return lax.optimization_barrier((value, *others))[0]


def swap(block, even_bit, odd_bit, planes=None):
    count = lax.axis_size(AXES)
    route = [
        (i, i ^ (odd_bit if i & 1 else even_bit))
        for i in range(count)
        if planes is None or i >> 3 in planes
    ]
    return lax.ppermute(block, AXES, route)


def to_aligned(shard, place, count, delta):
    rows = shard.shape[0]
    lag = delta * (count - 1)
    back = -(-lag // rows)
    if back == 1:
        keep = -(-lag // 8) * 8
        parts = [shift_flat(shard[rows - keep :], 1), shard]
    else:
        keep = back * rows
        parts = [shift_flat(shard, s) for s in range(back, 0, -1)] + [shard]
    joined = jnp.concatenate(parts, 0)
    return lax.dynamic_slice_in_dim(joined, keep - delta * place, rows - delta, 0)


def small_part(shard, place, count, delta):
    rows = shard.shape[0]
    extra = count * delta
    zeros = jnp.zeros((extra, 128), shard.dtype)
    joined = jnp.concatenate([zeros, shard, zeros], 0)
    start = extra + count * (rows - delta) - place * rows
    return lax.dynamic_slice_in_dim(joined, jnp.minimum(start, rows + extra), extra, 0)


def from_aligned(chunk, small, place, count, delta, rows):
    aligned = rows - delta
    ahead = -(-(count * delta) // aligned)
    parts = [chunk]
    if ahead == 1:
        keep = small.shape[0]
        got = shift_flat(chunk[:keep], -1)
        parts.append(jnp.where(place == count - 1, small, got))
    else:
        pad = ahead * aligned - small.shape[0]
        tail = jnp.concatenate([small, jnp.zeros((pad, 128), small.dtype)], 0)
        for s in range(1, ahead + 1):
            got = shift_flat(chunk, -s)
            for e in range(s):
                piece = tail[e * aligned : (e + 1) * aligned]
                got = jnp.where(place == count - s + e, piece, got)
            parts.append(got)
    return lax.dynamic_slice_in_dim(jnp.concatenate(parts, 0), delta * place, rows, 0)


def regroup(block):
    return block.reshape(-1, 24, 4, D).transpose(0, 2, 1, 3)


def ungroup(block):
    return block.reshape(-1, 4, 24, D).transpose(0, 2, 1, 3)


def normalize(values, gain):
    factor = lax.rsqrt(jnp.mean(values * values, axis=-1, keepdims=True) + norm_eps)
    scaled = values * factor
    return (scaled, factor, scaled * gain)


def norm_back(grad_in, scaled, factor, gain):
    weighted = grad_in * gain
    inner_mean = jnp.mean(weighted * scaled, axis=-1, keepdims=True)
    return factor * (weighted - scaled * inner_mean)


def adam_update(master, moment_one, moment_two, gradient, step_count, row_start):
    row_index = row_start + jnp.arange(master.shape[0], dtype=jnp.int32)
    matrix_rows = (4 * D * D + 2 * D * FF) // 128
    out_first = 3 * D * D // 128
    out_last = 4 * D * D // 128
    is_matrix = (row_index < matrix_rows)[:, None]
    is_out = ((row_index >= out_first) & (row_index < out_last))[:, None]
    step_rate = jnp.where(is_matrix, jnp.where(is_out, 0.5, 0.1), 1.0)
    decay_rate = jnp.where(is_matrix, 0.1, 0.0)
    step_value = step_count[0].astype(jnp.float32)
    new_one = 0.9 * moment_one + 0.1 * gradient
    new_two = 0.999 * moment_two + 0.001 * gradient * gradient
    corr_first = 1.0 - jnp.power(0.9, step_value)
    corr_second = 1.0 - jnp.power(0.999, step_value)
    new_weights = master - step_rate * (
        new_one / corr_first / (jnp.sqrt(new_two / corr_second) + 1e-08) + decay_rate * master
    )
    return (new_weights, new_one, new_two)


def shards(tokens, out_grad, positions, master, first_moment, second_moment, step_count):
    rows = tokens.shape[0]
    assert rows == SEQ_MIN
    count = lax.axis_size(AXES)
    place = lax.axis_index(AXES).astype(jnp.int32)
    owned = master.shape[0]
    aligned = (4 * D * D + 2 * D * FF) // 128 // count
    delta = owned - aligned
    height = aligned * 128 // D
    staged = count == 32
    first_place = positions[0]
    state = jnp.where(first_place < 0, 0, jnp.where(first_place >= SEQ_MIN, 2, 1)).astype(jnp.int32)
    state_vec = state[None]

    chunk = to_aligned(master, place, count, delta).reshape(-1, D)
    if staged:
        group = 3 * place + jnp.arange(3, dtype=jnp.int32)
        in_up = ((group >= 32) & (group < 64))[:, None, None, None]
        chunk = jnp.where(in_up, regroup(chunk), chunk.reshape(3, 4, 24, D)).reshape(-1, D)
    chunk = chunk.astype(BF)
    small = lax.reduce_precision(small_part(master, place, count, delta), 8, 7)
    core = (place & 1)[None]
    x_bit = (place >> 1) & 1
    y_bit = (place >> 2) & 1
    even = (place & 1) == 0
    if staged:
        z = place >> 3
        mine = jnp.concatenate([chunk, small.astype(BF).reshape(-1, D)], 0)
        tokens_before = shift_ctx(after(tokens, mine), 1)
        got = swap(mine, 16, 16)
        tokens_both = jnp.concatenate([tokens_before, tokens], 0)
        got = after(got, tokens_both)
        rest = jnp.concatenate([chunk, got[:height]], 0)
        none = jnp.zeros((), BF)
        first = jnp.where(z == 0, chunk, jnp.where(z == 2, got[:height], none))
        mine = jnp.concatenate([first, mine[height:] + got[height:]], 0)
        mine = mine + swap(mine, 8, 8)
        across = swap(after(rest, mine), 8, 8)
        mine = join(mine, swap(mine, 2, 4))
        mine = join(mine, swap(mine, 4, 2))
        got = swap(mine, 1, 1)
        index = []
        late_index = []
        for k in (0, 1):
            turn = even if k == 0 else jnp.logical_not(even)
            for j in range(4):
                near, far = j & 1, j >> 1
                x_of = x_bit ^ jnp.where(turn, near, far)
                y_of = y_bit ^ jnp.where(turn, far, near)
                piece = 4 * y_of + 2 * x_of + (core[0] ^ k)
                index.append(piece)
                late_index += [piece, piece + 8, piece + 16]
        index = jnp.stack(index).astype(jnp.int32)
        late_index = jnp.stack(late_index + [core[0]]).astype(jnp.int32)
        projected, small, in_weight = qkv_fwd(index, tokens_both, (mine, got), rows, 4)
        codes = [z ^ k for k in (1, 2, 3)]
        order = [jnp.where(j == 1, 2, jnp.where(j == 2, 1, j)) for j in codes]
        rest = arrange(
            after(jnp.stack(order).astype(jnp.int32), projected), rest.reshape(2, height, D), across.reshape(2, height, D), 3
        ).reshape(-1, D)
        across = swap(rest, 2, 4)
    else:
        tokens_both = jnp.concatenate([shift_ctx(tokens, 1), tokens], 0)
        wide = lax.all_gather(chunk, AXES, axis=0, tiled=True)
        small = lax.psum(small, AXES)[:96].reshape(-1, D)
        in_weight = wide[: 3 * D]
        projected, small = qkv_fwd(core, tokens_both, (in_weight, small), rows, 0)
        late_index = jnp.arange(25, dtype=jnp.int32) % 24
    gain_first = small[0]
    gain_second = small[1]
    taps = small[2:11].reshape(3, 3 * D)

    forward = []
    if staged:
        forward = att_fwd(after(state_vec, rest), projected, taps, forward, FORWARD_PARTS[0], rows)
        rest = join_held(after(rest, forward[0]), across)
        line = swap(rest, 4, 2)
        core_rest = swap(rest, 1, 1)
        forward = att_fwd(after(state_vec, rest), projected, taps, forward, FORWARD_PARTS[1], rows)
        forward = att_fwd(after(state_vec, core_rest), projected, taps, forward, FORWARD_PARTS[2], rows)
        line = hold(line, forward[0])
        core_line = swap(line, 1, 1)
        late_weights = [w.reshape(18, 4, 24, D) for w in (rest, line, core_rest, core_line)]
    else:
        for part in FORWARD_PARTS:
            forward = att_fwd(state_vec, projected, taps, forward, part, rows)
        grouped = jnp.concatenate(
            [
                wide[3 * D : 4 * D].reshape(-1, 4, 24, D),
                regroup(wide[4 * D : 8 * D]),
                wide[8 * D :].reshape(-1, 4, 24, D),
            ],
            0,
        )
        late_weights = [grouped[18 * k : 18 * k + 18] for k in range(4)]
    attn_low, logs, *mixed = forward

    layer_out, grad_hidden, grad_attended, grad_gain_two, away_grad, here_grad = ffn(
        state_vec, late_index, tokens, attn_low, out_grad, gain_second[None], late_weights, rows
    )

    def backward(start, done, part):
        return att_bwd(
            start, mixed, attn_low, logs, grad_attended, projected, taps, done, BACKWARD_PARTS[part], rows
        )

    if staged:
        stay = [jnp.where(even, 2 * j + x_bit, 2 * y_bit + j) for j in range(2)]
        away = [jnp.where(even, 2 * j + 1 - x_bit, 2 * (1 - y_bit) + j) for j in range(2)]
        pick_plane = jnp.stack(away + stay).astype(jnp.int32)
        other = jnp.where(even, y_bit, x_bit)
        pick_line = jnp.stack([1 - other, other]).astype(jnp.int32)

        def of_quarters(pick, held):
            half = pick.shape[0] // 2
            steps = [pick[s * half + j] + held * t for s in range(2) for t in range(3) for j in range(half)]
            return jnp.stack(steps)

        late_keep = here_grad.reshape(12, height, D)
        late_got = swap(away_grad.reshape(12, height, D), 1, 1)
        done = backward(state_vec, [], 0)
        late_send, late_keep = merge_grid(
            after(of_quarters(pick_plane, 4), done[4]), late_keep, late_got, 6
        )
        late_got = swap(late_send, 2, 4)
        done = backward(after(state_vec, late_send), done, 1)
        late_send, late_keep = merge_grid(
            after(of_quarters(pick_line, 2), done[4]), late_keep, late_got, 3
        )
        late_got = swap(late_send, 4, 2)
        done = backward(after(state_vec, late_send), done, 2)
        z_even = (z & 1) == 0
        low_pair = [jnp.where(z_even, 0, 0), jnp.where(z_even, 2, 1)]
        high_pair = [jnp.where(z_even, 0, 0), jnp.where(z_even, 1, 2)]
        pick_z = jnp.stack(low_pair + high_pair).astype(jnp.int32)
        late_send, late_keep = merge_grid(after(pick_z, done[4]), late_keep, late_got, 2)
        late_got = swap(late_send, 8, 8)
        done = backward(after(state_vec, late_send), done, 3)
        high = z >> 1
        pick_last = jnp.stack([1 - high, high]).astype(jnp.int32)
        late_send, late_keep = merge_grid(after(pick_last, done[4]), late_keep, late_got, 1)
        late_got = swap(late_send, 16, 16, (0, 1, 3))
        sums_state = after(core, late_send)
    else:
        done = []
        for part in range(4):
            done = backward(state_vec, done, part)
        sums_state = core
    *back, tap_grads = done
    grads_before, gain_one_grad = before_bwd(tokens_both, back, in_weight, rows)
    from_next = shift_ctx(grads_before, -1)
    sums = qkv_bwd(
        after(sums_state, grads_before), tokens_both, back, in_weight, gain_first[None], gain_one_grad, grad_gain_two, tap_grads, rows,
        4 if staged else 0,
    )
    grad_normed_one = sums[2]
    scaled_one, factor_one, _ = normalize(tokens.astype(F32), gain_first)
    input_grad = grad_hidden + norm_back(
        grad_normed_one + from_next.astype(F32), scaled_one, factor_one, gain_first
    )

    if staged:
        send, keep = sums[:2]
        got = swap(after(send, late_got, from_next), 1, 1)
        send, keep = merge(pick_plane, keep, got, height + 16, 2)
        got = swap(send, 2, 4)
        late_chunk = late_keep[0] + late_got[0].astype(F32)
        late_chunk = jnp.where(in_up, ungroup(late_chunk).reshape(3, 4, 24, D), late_chunk.reshape(3, 4, 24, D))
        late_chunk = late_chunk.reshape(-1, D)
        late_next = shift_flat(late_chunk[:16], -1)
        send, keep = merge(after(pick_line, late_next), keep, got, height + 16, 1)
        got = swap(send, 4, 2)
        send, keep = merge(after(core, input_grad), keep, got, height + 16, 0)
        got = swap(send, 8, 8)
        send, keep = merge(core, keep, got, height + 16, 0)
        got = swap(send, 16, 16, (1, 2))
        first = keep + got.astype(F32)
        quarter = count // 4
        follow = jnp.where(place < quarter - 1, first[height : height + 16], late_next)
        follow = jnp.where(place == count - 1, first[height + 16 :], follow)
        chunk_grad = jnp.where(place < quarter, first[:height], late_chunk)
        chunk_grad = jnp.concatenate([chunk_grad, follow], 0).reshape(-1, 128)
        gradient = lax.dynamic_slice_in_dim(chunk_grad, delta * place, owned, 0)
    else:
        flat_grad = jnp.stack([here_grad.reshape(12, 3, 4, 24, D), away_grad.reshape(12, 3, 4, 24, D)], 1)
        flat_grad = flat_grad.reshape(72, 4, 24, D)
        wide_grad = jnp.concatenate(
            [
                sums[0],
                flat_grad[:8].reshape(-1, D),
                ungroup(flat_grad[8:40]).reshape(-1, D),
                flat_grad[40:].reshape(-1, D),
            ],
            0,
        )
        chunk_grad = lax.psum_scatter(wide_grad, AXES, scatter_dimension=0, tiled=True).astype(F32)
        used = sums[1].reshape(-1, 128)
        extra = count * delta
        small_grad = jnp.concatenate([used, jnp.zeros((extra - used.shape[0], 128), F32)], 0)
        small_grad = lax.psum(small_grad, AXES)
        gradient = from_aligned(chunk_grad.reshape(-1, 128), small_grad, place, count, delta, owned)
    new_weights, new_one, new_two = adam_update(
        master, first_moment, second_moment, gradient, step_count, place * owned
    )
    return (layer_out, input_grad, new_weights, new_one, new_two, new_weights.astype(BF))


def solution(mesh):
    spread = P(AXES, None)
    return jax.shard_map(
        shards,
        mesh=mesh,
        in_specs=(spread, spread, P(AXES), spread, spread, spread, P()),
        out_specs=(spread,) * 6,
        check_vma=False,
    )
```

```python
import jax
import jax.numpy as jnp
from jax import lax
from jax.experimental import pallas as pl
from jax.experimental.pallas import tpu as pltpu
from jax.sharding import PartitionSpec as P

D = 768
HEADS = 12
HEAD_DIM = 64
FF = 3072
SEQ_MIN = 1024
AXES = ("dp", "ctx")
QB = 256
FORWARD_PARTS = ((0, 2), (2, 2), (4, 2))
BACKWARD_PARTS = ((0, 1), (1, 2), (3, 1), (4, 2))
F32 = jnp.float32
BF = jnp.bfloat16
NT = (((1,), (1,)), ((), ()))
TN = (((0,), (0,)), ((), ()))
norm_eps = 1e-06
VMEM_LIMIT = 56 << 20


def dot(left, right):
    return jnp.dot(left, right, preferred_element_type=F32)


def dot_nt(left, right):
    return lax.dot_general(left, right, NT, preferred_element_type=F32)


def dot_tn(left, right):
    return lax.dot_general(left, right, TN, preferred_element_type=F32)


def cost(flops, nbytes, exps=0):
    return pl.CostEstimate(flops=int(flops), bytes_accessed=int(nbytes), transcendentals=int(exps))


def taps_of(small, matrix):
    return [small[2 + 3 * j + matrix : 3 + 3 * j + matrix, :] for j in range(3)]


def row_ids(height):
    return lax.broadcasted_iota(jnp.int32, (height, 128), 0)


def conv(out_ref, x_ref, start, tail_ref, taps, rows, state):
    height = x_ref.shape[0]
    for r in range(0, height, QB):
        at = start + r
        if r:
            x = x_ref[r - 16 : r + QB, :].astype(F32)
        else:
            before = jnp.zeros((16, 128), F32)
            if tail_ref is not None:
                before = jnp.concatenate([before[8:], tail_ref[...].astype(F32)], 0)
            x = jnp.concatenate([before, x_ref[0:QB, :].astype(F32)], 0)
        one = pltpu.roll(x, 1, 0)[16:]
        two = pltpu.roll(x, 2, 0)[16:]
        x = x[16:]
        scale = 1.0
        if at >= rows:
            scale = jnp.where(state > 0, 1.0, 0.0)
        if at == 0 or at == rows:
            seen = jnp.where(state == 2, 1.0, 0.0) if at else 0.0
            row = row_ids(QB)
            one = jnp.where(row < 1, one * seen, one)
            two = jnp.where(row < 2, two * seen, two)
        c_one = taps[1] * scale
        c_two = taps[2] * scale
        out_ref[r : r + QB, :] = (taps[0] * x + c_one * one + c_two * two).astype(BF)


def att_fwd_kernel(
    state_ref, tail_ref, q_ref, k_ref, v_ref, small_ref,
    o_ref, l_ref, qm_ref, km_ref, vm_ref, ka, va,
):
    rows = q_ref.shape[0]
    lane = lax.broadcasted_iota(jnp.int32, (1, 128), 1)
    state = state_ref[0]
    conv(qm_ref, q_ref, rows, tail_ref, taps_of(small_ref[...], 0), rows, state)
    conv(km_ref, k_ref, 0, None, taps_of(small_ref[...], 1), rows, state)
    conv(vm_ref, v_ref, 0, None, taps_of(small_ref[...], 2), rows, state)
    bias = jnp.where(state == 2, 0.0, -1e30)
    for h in range(2):
        mine = (lane < 64) if h == 0 else (lane >= 64)
        base = 64 if h == 0 else 0
        first = jnp.where(lane == base, bias, 0.0).astype(BF)
        for r in range(0, 2 * rows, QB):
            at = pl.ds(r, QB)
            ka[h, at, :] = jnp.where(mine, km_ref[at, :], first if r < rows else jnp.zeros((), BF))
            va[h, at, :] = jnp.where(mine, vm_ref[at, :], jnp.ones((), BF))
    for i in range(rows // QB):
        rs = pl.ds(i * QB, QB)
        outs = []
        sums = []
        qf = qm_ref[rs, :].astype(F32) * 0.125
        for h in range(2):
            mine = (lane < 64) if h == 0 else (lane >= 64)
            base = 64 if h == 0 else 0
            qh = jnp.where(mine, qf, jnp.where(lane == base, 1.0, 0.0)).astype(BF)
            nk = rows + (i + 1) * QB
            s = dot_nt(qh, ka[h, 0:nk, :])
            r = lax.broadcasted_iota(jnp.int32, (QB, QB), 0)
            c = lax.broadcasted_iota(jnp.int32, (QB, QB), 1)
            sd = jnp.where(c <= r, s[:, nk - QB :], -1e30)
            se = s[:, : nk - QB]
            m = jnp.maximum(
                jnp.max(sd, axis=1, keepdims=True), jnp.max(se, axis=1, keepdims=True)
            )
            p = jnp.concatenate([jnp.exp(se - m).astype(BF), jnp.exp(sd - m).astype(BF)], 1)
            o = dot(p, va[h, 0:nk, :])
            outs.append(o / pltpu.roll(o, 64, 1))
            sums.append(m + jnp.log(o))
        res = jnp.where(lane < 64, outs[0], outs[1])
        res = jnp.where(state == 0, vm_ref[pl.ds(rows + i * QB, QB), :].astype(F32), res)
        o_ref[rs, :] = res.astype(BF)
        l_ref[rs, :] = jnp.where(lane < 64, sums[1], sums[0])


def call_in_parts(body, in_specs, out_specs, out_shape, earlier, part, **options):
    used = len(in_specs)

    def kernel(*refs):
        body(*refs[:used], *refs[used + len(earlier) :])

    return pl.pallas_call(
        kernel,
        grid=(part[1],),
        in_specs=in_specs + [pl.BlockSpec(memory_space=pl.ANY)] * len(earlier),
        out_specs=out_specs,
        out_shape=out_shape,
        input_output_aliases={used + i: i for i in range(len(earlier))},
        compiler_params=pltpu.CompilerParams(vmem_limit_bytes=VMEM_LIMIT),
        **options,
    )


def columns(part):
    first = part[0]

    def cols(height, row, off):
        return pl.BlockSpec((height, 128), lambda p: (row, p + first + off))

    return cols


def att_fwd(state, projected, small, earlier, part, rows):
    cols = columns(part)
    return call_in_parts(
        att_fwd_kernel,
        [
            pl.BlockSpec(memory_space=pltpu.SMEM),
            cols(8, rows // 8 - 1, 0),
            cols(rows, 1, 0),
            cols(2 * rows, 0, 6),
            cols(2 * rows, 0, 12),
            cols(16, 0, 0),
        ],
        [cols(rows, 0, 0)] * 3 + [cols(2 * rows, 0, 0)] * 2,
        [
            jax.ShapeDtypeStruct((rows, D), BF),
            jax.ShapeDtypeStruct((rows, D), F32),
            jax.ShapeDtypeStruct((rows, D), BF),
            jax.ShapeDtypeStruct((2 * rows, D), BF),
            jax.ShapeDtypeStruct((2 * rows, D), BF),
        ],
        earlier,
        part,
        scratch_shapes=[pltpu.VMEM((2, 2 * rows, 128), BF)] * 2,
        cost_estimate=cost(
            2 * 2 * 2 * rows * rows * 1.5 * 256 * part[1],
            rows * D * 5 * part[1],
            2 * rows * rows * 1.5 * part[1],
        ),
        name="att_fwd",
    )(state, projected, projected, projected, projected, small, *earlier)


def three(x, lane, base):
    hi = x.astype(BF).astype(F32)
    r = x - hi
    mid = r.astype(BF).astype(F32)
    lo = r - mid
    return jnp.where(
        lane == base, hi, jnp.where(lane == base + 1, mid, jnp.where(lane == base + 2, lo, 0.0))
    )


def conv_back(out_ref, grad_ref, x_ref, start, tail, taps, rows, state):
    height = grad_ref.shape[0]
    joint = jnp.where(state == 2, 1.0, 0.0)
    sums = [jnp.zeros((1, 128), F32)] * 3

    def add(parts, x):
        return [s + jnp.sum(g * x, axis=0, keepdims=True) for s, g in zip(sums, parts)]

    for r in range(0, height, QB):
        ends = r + QB == height
        meets = start + r + QB == rows
        if ends:
            grad = jnp.concatenate([grad_ref[r : r + QB, :], jnp.zeros((8, 128), F32)], 0)
        else:
            grad = grad_ref[r : r + QB + 8, :]
        one = pltpu.roll(grad, QB + 7, 0)[:QB]
        two = pltpu.roll(grad, QB + 6, 0)[:QB]
        grad = grad[:QB]
        if meets and not ends:
            row = row_ids(QB)
            one = jnp.where(row >= QB - 1, one * joint, one)
            two = jnp.where(row >= QB - 2, two * joint, two)
        out_ref[r : r + QB, :] = (taps[0] * grad + taps[1] * one + taps[2] * two).astype(BF)
        sums = add((grad, one, two), x_ref[r : r + QB, :].astype(F32))
    if tail is not None:
        grad = jnp.concatenate([jnp.zeros((8, 128), F32), grad_ref[0:8, :]], 0)
        one = pltpu.roll(grad, 15, 0)[:8] * joint
        two = pltpu.roll(grad, 14, 0)[:8] * joint
        tail[0][...] = (taps[1] * one + taps[2] * two).astype(BF)
        sums = add((grad[:8], one, two), tail[1][...].astype(F32))
    return sums


def att_bwd_kernel(
    state_ref, q_ref, k_ref, v_ref, o_ref, l_ref, do_ref, xt_ref, xq_ref, xk_ref, xv_ref,
    small_ref,
    pq_ref, pt_ref, pk_ref, pv_ref, tg_ref, qa, da, qt, dt, kt, dqt, dqs, dks, dvs,
):
    rows = q_ref.shape[0]
    lane = lax.broadcasted_iota(jnp.int32, (1, 128), 1)
    second = state_ref[0] == 2
    for r in range(0, rows, QB):
        at = pl.ds(r, QB)
        do = do_ref[at, :].astype(F32)
        od = do * o_ref[at, :].astype(F32)
        qf = q_ref[at, :].astype(F32) * 0.125
        lv = l_ref[at, :]
        for h in range(2):
            mine = (lane < 64) if h == 0 else (lane >= 64)
            base = 64 if h == 0 else 0
            delta = jnp.sum(jnp.where(mine, od, 0.0), axis=1, keepdims=True)
            qa[h, at, :] = jnp.where(mine, qf, three(-lv, lane, base)).astype(BF)
            da[h, at, :] = jnp.where(mine, do, three(-delta, lane, base)).astype(BF)
        qt[:, at] = jnp.transpose(qf).astype(BF)
        dt[:, at] = jnp.transpose(do).astype(BF)
    for r in range(0, 2 * rows, QB):
        at = pl.ds(r, QB)
        kt[:, at] = jnp.transpose(k_ref[at, :].astype(F32)).astype(BF)
    dqt[...] = jnp.zeros(dqt.shape, F32)

    def keys(ks, first, diagonal):
        kk = k_ref[ks, :]
        vv = v_ref[ks, :]
        dv = []
        dk = []
        for h in range(2):
            mine = (lane < 64) if h == 0 else (lane >= 64)
            base = 64 if h == 0 else 0
            ones3 = ((lane >= base) & (lane < base + 3)).astype(BF)
            hs = slice(64 * h, 64 * h + 64)
            st = dot_nt(jnp.where(mine, kk, ones3), qa[h, first:rows, :])
            dp = dot_nt(jnp.where(mine, vv, ones3), da[h, first:rows, :])
            p = jnp.exp(st)
            if diagonal:
                r = lax.broadcasted_iota(jnp.int32, (QB, QB), 0)
                c = lax.broadcasted_iota(jnp.int32, (QB, QB), 1)
                seen = jnp.where(r <= c, p[:, :QB], 0.0)
                p = jnp.concatenate([seen, p[:, QB:]], 1) if first + QB < rows else seen
            ds = (p * dp).astype(BF)
            dv.append(dot_nt(dt[hs, first:rows], p.astype(BF)))
            dk.append(dot_nt(qt[hs, first:rows], ds))
            dqt[hs, first:rows] += dot(kt[hs, ks], ds)
        dvs[ks, :] = jnp.transpose(jnp.concatenate(dv, 0))
        dks[ks, :] = jnp.transpose(jnp.concatenate(dk, 0))

    for j in range(rows // QB):
        keys(pl.ds(rows + j * QB, QB), j * QB, True)

    @pl.when(second)
    def _():
        def step(j, carry):
            keys(pl.ds(pl.multiple_of(j * QB, QB), QB), 0, False)
            return carry

        lax.fori_loop(0, rows // QB, step, 0)

    @pl.when(jnp.logical_not(second))
    def _():
        dks[0:rows, :] = jnp.zeros((rows, 128), F32)
        dvs[0:rows, :] = jnp.zeros((rows, 128), F32)

    for r in range(0, rows, QB):
        dqs[r : r + QB, :] = jnp.transpose(dqt[:, r : r + QB]) * 0.125
    state = state_ref[0]
    sq = conv_back(pq_ref, dqs, xq_ref, rows, (pt_ref, xt_ref), taps_of(small_ref[...], 0), rows, state)
    sk = conv_back(pk_ref, dks, xk_ref, 0, None, taps_of(small_ref[...], 1), rows, state)
    sv = conv_back(pv_ref, dvs, xv_ref, 0, None, taps_of(small_ref[...], 2), rows, state)
    tg_ref[...] = jnp.zeros(tg_ref.shape, F32)
    for j in range(3):
        for m, s in enumerate((sq, sk, sv)):
            tg_ref[3 * j + m : 3 * j + m + 1, :] = s[j]


def att_bwd(state, mixed, attended, logs, grad, projected, small, earlier, part, rows):
    cols = columns(part)
    own = cols(rows, 0, 0)
    both = cols(2 * rows, 0, 0)
    return call_in_parts(
        att_bwd_kernel,
        [
            pl.BlockSpec(memory_space=pltpu.SMEM),
            own, both, both, own, own, own,
            cols(8, rows // 8 - 1, 0),
            cols(rows, 1, 0),
            cols(2 * rows, 0, 6),
            cols(2 * rows, 0, 12),
            cols(16, 0, 0),
        ],
        [own, cols(8, 0, 0), both, both, cols(16, 0, 0)],
        [
            jax.ShapeDtypeStruct((rows, D), BF),
            jax.ShapeDtypeStruct((8, D), BF),
            jax.ShapeDtypeStruct((2 * rows, D), BF),
            jax.ShapeDtypeStruct((2 * rows, D), BF),
            jax.ShapeDtypeStruct((16, D), F32),
        ],
        earlier,
        part,
        scratch_shapes=[
            pltpu.VMEM((2, rows, 128), BF),
            pltpu.VMEM((2, rows, 128), BF),
            pltpu.VMEM((128, rows), BF),
            pltpu.VMEM((128, rows), BF),
            pltpu.VMEM((128, 2 * rows), BF),
            pltpu.VMEM((128, rows), F32),
            pltpu.VMEM((rows, 128), F32),
            pltpu.VMEM((2 * rows, 128), F32),
            pltpu.VMEM((2 * rows, 128), F32),
        ],
        cost_estimate=cost(
            5 * 2 * 2 * rows * rows * 1.5 * 256 * part[1],
            rows * D * 7 * part[1],
            2 * rows * rows * 1.5 * part[1],
        ),
        name="att_bwd",
    )(state, *mixed, attended, logs, grad, projected, projected, projected, projected,
      small, *earlier)


def unit_rows(x):
    return x * lax.rsqrt(jnp.mean(x * x, axis=-1, keepdims=True) + norm_eps)


def before_bwd_kernel(x_ref, dt_ref, dk_ref, dv_ref, w_ref, out_ref, gain_ref):
    i = pl.program_id(0)
    hat = unit_rows(x_ref[...].astype(F32))
    gn = dot_nt(dk_ref[...], w_ref[D : 2 * D, :]) + dot_nt(dv_ref[...], w_ref[2 * D : 3 * D, :])

    last_step = pl.num_programs(0) - 1

    @pl.when(i == 0)
    def _():
        gain_ref[...] = jnp.zeros(gain_ref.shape, F32)

    @pl.when(i < last_step)
    def _():
        out_ref[...] = gn.astype(BF)
        gain_ref[...] += jnp.sum(gn * hat, axis=0, keepdims=True)

    @pl.when(i == last_step)
    def _():
        last = gn.shape[0] - 8
        full = jnp.concatenate([gn[:last], gn[last:] + dot_nt(dt_ref[...], w_ref[0:D, :])], 0)
        out_ref[...] = full.astype(BF)
        gain_ref[...] += jnp.sum(full * hat, axis=0, keepdims=True)


def before_bwd(x_both, back, weight, rows):
    dt, dk, dv = back[1:]
    blocks = 4
    height = rows // blocks
    step = pl.BlockSpec((height, D), lambda i: (i, 0))

    def whole(shape):
        return pl.BlockSpec(shape, lambda i: (0, 0))

    return pl.pallas_call(
        before_bwd_kernel,
        grid=(blocks,),
        in_specs=[step, whole((8, D)), step, step, whole((3 * D, D))],
        out_specs=[step, whole((1, D))],
        out_shape=[jax.ShapeDtypeStruct((rows, D), BF), jax.ShapeDtypeStruct((1, D), F32)],
        compiler_params=pltpu.CompilerParams(vmem_limit_bytes=VMEM_LIMIT),
        cost_estimate=cost(2 * rows * D * D * 2, rows * D * 12),
        name="before_bwd",
    )(x_both, dt, dk, dv, weight)


def qkv_bwd_kernel(
    core_ref, x_ref, dq_ref, dt_ref, dk_ref, dv_ref, w_ref, gain_ref, gain_one_ref, gain_two_ref, tg_ref,
    *refs, pieces, blocks,
):
    if pieces:
        send_ref, keep_ref, own_ref, acc, gacc = refs
    else:
        keep_ref, small_ref, own_ref, acc, gacc = refs
    i = pl.program_id(0)
    half = blocks // 2

    @pl.when(i == 0)
    def _():
        acc[...] = jnp.zeros(acc.shape, F32)
        gacc[0:1, :] = gain_one_ref[...]

    hat = unit_rows(x_ref[...].astype(F32))
    low = (hat * gain_ref[...]).astype(BF)
    dk = dk_ref[...]
    dv = dv_ref[...]
    acc[D : 2 * D, :] += dot_tn(low, dk)
    acc[2 * D : 3 * D, :] += dot_tn(low, dv)

    @pl.when(i == half - 1)
    def _():
        acc[0:D, :] += dot_tn(low[low.shape[0] - 8 :], dt_ref[...])

    @pl.when(i >= half)
    def _():
        dq = dq_ref[...]
        acc[0:D, :] += dot_tn(low, dq)
        full = (
            dot_nt(dk, w_ref[D : 2 * D, :])
            + dot_nt(dv, w_ref[2 * D : 3 * D, :])
            + dot_nt(dq, w_ref[0:D, :])
        )
        own_ref[...] = full
        gacc[0:1, :] += jnp.sum(full * hat, axis=0, keepdims=True)

    @pl.when(i == blocks - 1)
    def _():
        small = jnp.concatenate(
            [gacc[0:1, :], gain_two_ref[...], tg_ref[0:9, :], jnp.zeros((5, D), F32)], 0
        )
        if pieces:
            core = core_ref[0]
            height = 3 * D // (2 * pieces)
            wide = height + 16
            for j in range(pieces):
                to = pl.ds(j * wide, wide)
                away = pl.ds(pl.multiple_of((2 * j + 1 - core) * height, 16), wide)
                here = pl.ds(pl.multiple_of((2 * j + core) * height, 16), wide)
                send_ref[to, :] = acc[away, :].astype(BF)
                keep_ref[to, :] = acc[here, :]
            send_ref[pieces * wide :, :] = small.astype(BF)
            keep_ref[pieces * wide :, :] = small
        else:
            keep_ref[...] = acc[0 : 3 * D, :].astype(BF)
            small_ref[...] = small


def qkv_bwd(core, x_both, back, weight, gain, gain_one_grad, gain_two_grad, tap_grads, rows, pieces):
    dq, dt, dk, dv = back
    blocks = 4
    half = blocks // 2
    height = 2 * rows // blocks
    step = pl.BlockSpec((height, D), lambda i: (i, 0))
    late = pl.BlockSpec((height, D), lambda i: (jnp.maximum(i - half, 0), 0))

    def whole(shape):
        return pl.BlockSpec(shape, lambda i: (0, 0))

    if pieces:
        packed = 3 * D // 2 + 16 * pieces + 16
        outs = [jax.ShapeDtypeStruct((packed, D), BF), jax.ShapeDtypeStruct((packed, D), F32)]
        out_at = [whole((packed, D))] * 2
    else:
        outs = [jax.ShapeDtypeStruct((3 * D, D), BF), jax.ShapeDtypeStruct((16, D), F32)]
        out_at = [whole((3 * D, D)), whole((16, D))]

    def body(*refs):
        qkv_bwd_kernel(*refs, pieces=pieces, blocks=blocks)

    return pl.pallas_call(
        body,
        grid=(blocks,),
        in_specs=[
            pl.BlockSpec(memory_space=pltpu.SMEM),
            step, late, whole((8, D)), step, step, whole((3 * D, D)),
            whole((1, D)), whole((1, D)), whole((1, D)), whole((16, D)),
        ],
        out_specs=out_at + [late],
        out_shape=outs + [jax.ShapeDtypeStruct((rows, D), F32)],
        scratch_shapes=[pltpu.VMEM((3 * D + 16, D), F32), pltpu.VMEM((8, D), F32)],
        compiler_params=pltpu.CompilerParams(vmem_limit_bytes=VMEM_LIMIT),
        cost_estimate=cost(2 * 2 * D * D * 4 * rows, rows * D * 30),
        name="qkv_bwd",
    )(core, x_both, dq, dt, dk, dv, weight, gain, gain_one_grad, gain_two_grad, tap_grads)


def merge(index, keep, got, height, taken):
    rows = keep.shape[0]
    out_rows = taken * height + 16 if taken else rows

    def body(index_ref, keep_ref, got_ref, send_ref, stay_ref):
        if not taken:
            total = keep_ref[...] + got_ref[...].astype(F32)
            send_ref[...] = total.astype(BF)
            stay_ref[...] = total
            return
        for j in range(taken):
            to = pl.ds(j * height, height)
            away = pl.ds(pl.multiple_of(index_ref[j] * height, 16), height)
            here = pl.ds(pl.multiple_of(index_ref[taken + j] * height, 16), height)
            send_ref[to, :] = (keep_ref[away, :] + got_ref[away, :].astype(F32)).astype(BF)
            stay_ref[to, :] = keep_ref[here, :] + got_ref[here, :].astype(F32)
        end = keep_ref[rows - 16 :, :] + got_ref[rows - 16 :, :].astype(F32)
        send_ref[taken * height :, :] = end.astype(BF)
        stay_ref[taken * height :, :] = end

    vmem = pl.BlockSpec(memory_space=pltpu.VMEM)
    return pl.pallas_call(
        body,
        in_specs=[pl.BlockSpec(memory_space=pltpu.SMEM), vmem, vmem],
        out_specs=[vmem, vmem],
        out_shape=[
            jax.ShapeDtypeStruct((out_rows, D), BF),
            jax.ShapeDtypeStruct((out_rows, D), F32),
        ],
        compiler_params=pltpu.CompilerParams(vmem_limit_bytes=32 << 20),
        cost_estimate=cost(rows * D, rows * D * 12),
        name="merge",
    )(index, keep, got)


def merge_grid(index, keep, got, taken, kept=F32):
    height = keep.shape[1]

    def body(index_ref, ka_ref, ga_ref, kb_ref, gb_ref, send_ref, stay_ref):
        send_ref[...] = (ka_ref[...].astype(F32) + ga_ref[...].astype(F32)).astype(BF)
        stay_ref[...] = (kb_ref[...].astype(F32) + gb_ref[...].astype(F32)).astype(kept)

    away = pl.BlockSpec((1, height, D), lambda i, index: (index[i], 0, 0))
    here = pl.BlockSpec((1, height, D), lambda i, index: (index[taken + i], 0, 0))
    step = pl.BlockSpec((1, height, D), lambda i, index: (i, 0, 0))
    return pl.pallas_call(
        body,
        grid_spec=pltpu.PrefetchScalarGridSpec(
            num_scalar_prefetch=1,
            grid=(taken,),
            in_specs=[away, away, here, here],
            out_specs=[step, step],
        ),
        out_shape=[
            pltpu.HBM((taken, height, D), BF),
            pltpu.HBM((taken, height, D), kept),
        ],
        compiler_params=pltpu.CompilerParams(vmem_limit_bytes=32 << 20),
        cost_estimate=cost(taken * height * D * 2, taken * height * D * 16),
        name="merge_grid",
    )(index, keep, got, keep, got)


def arrange(index, one, two, taken):
    half = one.shape[0]
    height = one.shape[1]

    def body(index_ref, one_ref, two_ref, out_ref):
        for i in range(taken):
            at = index_ref[i]

            @pl.when(at < half)
            def _():
                out_ref[i] = one_ref[jnp.minimum(at, half - 1)]

            @pl.when(at >= half)
            def _():
                out_ref[i] = two_ref[jnp.maximum(at - half, 0)]

    vmem = pl.BlockSpec(memory_space=pltpu.VMEM)
    return pl.pallas_call(
        body,
        in_specs=[pl.BlockSpec(memory_space=pltpu.SMEM), vmem, vmem],
        out_specs=vmem,
        out_shape=jax.ShapeDtypeStruct((taken, height, D), BF),
        compiler_params=pltpu.CompilerParams(vmem_limit_bytes=32 << 20),
        cost_estimate=cost(taken * height * D, taken * height * D * 8),
        name="arrange",
    )(index, one, two)


def join(own, got, shared=16):
    rows = own.shape[0]
    body_rows = rows - shared

    def body(own_ref, got_ref, out_ref):
        out_ref[0:body_rows, :] = own_ref[0:body_rows, :]
        out_ref[body_rows : 2 * body_rows, :] = got_ref[0:body_rows, :]
        if shared:
            out_ref[2 * body_rows :, :] = own_ref[body_rows:, :] + got_ref[body_rows:, :]

    vmem = pl.BlockSpec(memory_space=pltpu.VMEM)
    return pl.pallas_call(
        body,
        in_specs=[vmem, vmem],
        out_specs=vmem,
        out_shape=jax.ShapeDtypeStruct((2 * body_rows + shared, D), BF),
        compiler_params=pltpu.CompilerParams(vmem_limit_bytes=32 << 20),
        cost_estimate=cost(rows * D, rows * D * 8),
        name="join",
    )(own, got)


def join_held(own, got):
    rows = own.shape[0]
    cuts = 4
    size = rows // cuts

    def body(own_ref, got_ref, out_ref, sems):
        copies = []
        for k, ref in enumerate((own_ref, got_ref)):
            for j in range(cuts):
                source = ref.at[pl.ds(j * size, size)]
                to = out_ref.at[pl.ds(k * rows + j * size, size)]
                copies.append(pltpu.make_async_copy(source, to, sems.at[k * cuts + j]))
        for copy in copies:
            copy.start()
        for copy in copies:
            copy.wait()

    held = pl.BlockSpec(memory_space=pltpu.HBM)
    return pl.pallas_call(
        body,
        in_specs=[held, held],
        out_specs=held,
        out_shape=jax.ShapeDtypeStruct((2 * rows, D), BF),
        scratch_shapes=[pltpu.SemaphoreType.DMA((2 * cuts,))],
        compiler_params=pltpu.CompilerParams(vmem_limit_bytes=16 << 20),
        cost_estimate=cost(0, rows * D * 8),
        name="join_held",
    )(own, got)


def hold(block, other):
    held = pl.BlockSpec(memory_space=pl.ANY)
    return pl.pallas_call(
        lambda block_ref, other_ref, out_ref: None,
        in_specs=[held, held],
        out_specs=held,
        out_shape=jax.ShapeDtypeStruct(block.shape, block.dtype),
        input_output_aliases={0: 0},
        name="hold",
    )(block, other)


def qkv_fwd_kernel(index_ref, x_ref, *refs, pieces, blocks):
    if pieces:
        own_ref, got_ref, out_ref, small_ref, weight = refs
    else:
        weight, given_ref, out_ref, small_ref = refs
    i = pl.program_id(0)

    @pl.when(i == 0)
    def _():
        if pieces:
            height = 3 * D // (2 * pieces)
            for j in range(pieces):
                at = pl.ds(j * height, height)
                for k, ref in enumerate((own_ref, got_ref)):
                    to = pl.multiple_of(index_ref[k * pieces + j] * height, 16)
                    weight[pl.ds(to, height), :] = ref[at, :]
            end = pl.ds(pieces * height, 16)
            small_ref[...] = own_ref[end, :].astype(F32) + got_ref[end, :].astype(F32)
        else:
            small_ref[...] = given_ref[...]

    x = x_ref[...].astype(F32)
    hat = x * lax.rsqrt(jnp.mean(x * x, axis=-1, keepdims=True) + norm_eps)
    low = (hat * small_ref[0:1, :]).astype(BF)

    @pl.when(i >= blocks // 2 - 1)
    def _():
        out_ref[:, 0:D] = dot(low, weight[0:D, :]).astype(BF)

    out_ref[:, D : 2 * D] = dot(low, weight[D : 2 * D, :]).astype(BF)
    out_ref[:, 2 * D : 3 * D] = dot(low, weight[2 * D : 3 * D, :]).astype(BF)


def qkv_fwd(index, x_both, weights, rows, pieces):
    blocks = 4
    height = 2 * rows // blocks

    def body(*refs):
        qkv_fwd_kernel(*refs, pieces=pieces, blocks=blocks)

    return pl.pallas_call(
        body,
        grid=(blocks,),
        in_specs=[
            pl.BlockSpec(memory_space=pltpu.SMEM),
            pl.BlockSpec((height, D), lambda i: (i, 0)),
            *[pl.BlockSpec(w.shape, lambda i: (0, 0)) for w in weights],
        ],
        out_specs=[
            pl.BlockSpec((height, 3 * D), lambda i: (i, 0)),
            pl.BlockSpec((16, D), lambda i: (0, 0)),
        ]
        + ([pl.BlockSpec((3 * D, D), lambda i: (0, 0))] if pieces else []),
        out_shape=[
            jax.ShapeDtypeStruct((2 * rows, 3 * D), BF),
            jax.ShapeDtypeStruct((16, D), F32),
        ]
        + ([jax.ShapeDtypeStruct((3 * D, D), BF)] if pieces else []),
        compiler_params=pltpu.CompilerParams(vmem_limit_bytes=VMEM_LIMIT),
        cost_estimate=cost(2 * 2 * rows * D * 3 * D, rows * D * 20),
        name="qkv_fwd",
    )(index, x_both, *weights)


def ffn_kernel(
    state_ref, index_ref, x_ref, att_ref, cot_ref, gain_ref, own_ref, own_two_ref, got_ref, got_two_ref,
    out_ref, gh_ref, ga_ref, gain_grad_ref, away_ref, here_ref,
    hidden, low, total, back, cot, sq, gb, weights, stage_up, stage_down, stage_out, in_sems, sems,
):
    c = pl.program_id(0)
    rows = x_ref.shape[0]
    blocks = [pl.ds(i * QB, QB) for i in range(rows // QB)]
    last = c == pl.num_programs(0) - 1
    core = index_ref[24]

    def fetch(k, j):
        ref = ((own_ref, own_two_ref), (got_ref, got_two_ref))[k][j // 6]
        piece = index_ref[12 * k + j]
        to = weights.at[pl.ds(3 * piece, 3)]
        return pltpu.make_async_copy(ref.at[pl.ds(3 * (j % 6), 3)], to, in_sems.at[piece])

    def fetched(pieces):
        for piece in pieces:
            at = weights.at[pl.ds(3 * piece, 3)]
            pltpu.make_async_copy(own_ref.at[pl.ds(0, 3)], at, in_sems.at[piece]).wait()

    def put(source, group, count, column, sem, wait=False):
        piece = group // 3
        at = (piece // 2) * 3 + group % 3

        def copy(ref):
            to = ref.at[pl.ds(at, count)] if column is None else ref.at[pl.ds(at, count), column]
            return pltpu.make_async_copy(source, to, sems.at[sem])

        if wait:
            copy(here_ref).wait()
            return
        mine = piece % 2 == core

        @pl.when(mine)
        def _():
            copy(here_ref).start()

        @pl.when(jnp.logical_not(mine))
        def _():
            copy(away_ref).start()

    def put_up(i, wait=False):
        start = 0
        k = 0
        while start < 32:
            count = min(3 - (8 + start) % 3, 32 - start)
            put(stage_up.at[i, pl.ds(start, count)], 8 + start, count, i, 20 * i + k, wait)
            start += count
            k += 1

    def put_down(i, wait=False):
        for k in range(8):
            put(stage_down.at[i, pl.ds(k, 1)], 40 + 8 * i + k, 1, None, 20 * i + 12 + k, wait)

    def put_out(wait=False):
        for k in range(8):
            put(stage_out.at[pl.ds(k, 1)], k, 1, None, 80 + k, wait)

    def square(first):
        return weights[first : first + 8].reshape(D, D)

    @pl.when(c == 0)
    def _():
        for early in (True, False):
            for k in range(2):
                for j in range(12):

                    @pl.when((index_ref[12 * k + j] < 3) == early)
                    def _():
                        fetch(k, j).start()

        cot[...] = jnp.where(state_ref[0] > 0, cot_ref[...], jnp.zeros((), BF))
        total[...] = jnp.zeros(total.shape, F32)
        back[...] = jnp.zeros(back.shape, F32)
        fetched(range(3))
        wo = square(0)
        for b in blocks:
            h = x_ref[b, :].astype(F32) + dot(att_ref[b, :], wo)
            hidden[b, :] = h
            hat = h * lax.rsqrt(jnp.mean(h * h, axis=-1, keepdims=True) + norm_eps)
            low[b, :] = (hat * gain_ref[...]).astype(BF)

    for i, pieces in enumerate((range(3, 16), range(16, 19), range(19, 22), range(22, 24))):

        @pl.when(c == i)
        def _():
            fetched(pieces)

    up = weights[8:40, c].reshape(D, D)
    down = weights[pl.ds(40 + 8 * c, 8)].reshape(D, D)
    for b in blocks:
        act = jnp.maximum(dot(low[b, :], up), 0.0)
        s = (act * act).astype(BF)
        sq[b, :] = s
        total[b, :] += dot(s, down)
        g = (dot_nt(cot[b, :], down) * 2.0 * act).astype(BF)
        gb[b, :] = g
        back[b, :] += dot_nt(g, up)
    stage_down[c] = dot_tn(sq[...], cot[...]).reshape(8, 4, 24, D).astype(BF)
    stage_up[c] = dot_tn(low[...], gb[...]).reshape(32, 24, D).astype(BF)
    put_down(c)
    put_up(c)

    @pl.when(last)
    def _():
        gain = gain_ref[...]
        wo = square(0)
        sums = jnp.zeros((1, D), F32)
        for b in blocks:
            h = hidden[b, :]
            out_ref[b, :] = (h + total[b, :]).astype(BF)
            factor = lax.rsqrt(jnp.mean(h * h, axis=-1, keepdims=True) + norm_eps)
            hat = h * factor
            g = back[b, :]
            sums = sums + jnp.sum(g * hat, axis=0, keepdims=True)
            weighted = g * gain
            inner = jnp.mean(weighted * hat, axis=-1, keepdims=True)
            grad = cot[b, :].astype(F32) + factor * (weighted - hat * inner)
            gh_ref[b, :] = grad
            grad_low = grad.astype(BF)
            gb[b, :] = grad_low
            ga_ref[b, :] = dot_nt(grad_low, wo).astype(BF)
        gain_grad_ref[...] = sums
        stage_out[...] = dot_tn(att_ref[...], gb[...]).reshape(8, 4, 24, D).astype(BF)
        put_out()
        for i in range(4):
            put_down(i, True)
            put_up(i, True)
        put_out(True)


def ffn(state, index, tokens, attended, out_grad, gain, weights, rows):
    def whole(shape):
        return pl.BlockSpec(shape, lambda c: (0,) * len(shape), pipeline_mode=pl.Buffered(1))

    act = whole((rows, D))
    held = pl.BlockSpec(memory_space=pl.ANY)
    scalars = pl.BlockSpec(memory_space=pltpu.SMEM)
    half = (36, 4, 24, D)
    return pl.pallas_call(
        ffn_kernel,
        grid=(4,),
        in_specs=[scalars, scalars, act, act, act, whole((1, D)), held, held, held, held],
        out_specs=[act, act, act, whole((1, D)), held, held],
        out_shape=[
            jax.ShapeDtypeStruct((rows, D), BF),
            jax.ShapeDtypeStruct((rows, D), F32),
            jax.ShapeDtypeStruct((rows, D), BF),
            jax.ShapeDtypeStruct((1, D), F32),
            jax.ShapeDtypeStruct(half, BF),
            jax.ShapeDtypeStruct(half, BF),
        ],
        scratch_shapes=[
            pltpu.VMEM((rows, D), F32),
            pltpu.VMEM((rows, D), BF),
            pltpu.VMEM((rows, D), F32),
            pltpu.VMEM((rows, D), F32),
            pltpu.VMEM((rows, D), BF),
            pltpu.VMEM((rows, D), BF),
            pltpu.VMEM((rows, D), BF),
            pltpu.VMEM((72, 4, 24, D), BF),
            pltpu.VMEM((4, 32, 24, D), BF),
            pltpu.VMEM((4, 8, 4, 24, D), BF),
            pltpu.VMEM((8, 4, 24, D), BF),
            pltpu.SemaphoreType.DMA((24,)),
            pltpu.SemaphoreType.DMA((88,)),
        ],
        compiler_params=pltpu.CompilerParams(vmem_limit_bytes=60 << 20),
        cost_estimate=cost(2 * rows * D * D * (24 + 3), 2 * 12 * D * D * 2 + rows * D * 16),
        name="ffn",
    )(state, index, tokens, attended, out_grad, gain, *weights)


def shift_flat(block, distance):
    count = lax.axis_size(AXES)
    route = [(i - distance, i) for i in range(count) if 0 <= i - distance < count]
    return lax.ppermute(block, AXES, route)


def shift_ctx(block, distance):
    count = lax.axis_size("ctx")
    route = [(i - distance, i) for i in range(count) if 0 <= i - distance < count]
    return lax.ppermute(block, "ctx", route)


def after(value, *others):
    return lax.optimization_barrier((value, *others))[0]


def swap(block, even_bit, odd_bit, planes=None):
    count = lax.axis_size(AXES)
    route = [
        (i, i ^ (odd_bit if i & 1 else even_bit))
        for i in range(count)
        if planes is None or i >> 3 in planes
    ]
    return lax.ppermute(block, AXES, route)


def to_aligned(shard, place, count, delta):
    rows = shard.shape[0]
    lag = delta * (count - 1)
    back = -(-lag // rows)
    if back == 1:
        keep = -(-lag // 8) * 8
        parts = [shift_flat(shard[rows - keep :], 1), shard]
    else:
        keep = back * rows
        parts = [shift_flat(shard, s) for s in range(back, 0, -1)] + [shard]
    joined = jnp.concatenate(parts, 0)
    return lax.dynamic_slice_in_dim(joined, keep - delta * place, rows - delta, 0)


def small_part(shard, place, count, delta):
    rows = shard.shape[0]
    extra = count * delta
    zeros = jnp.zeros((extra, 128), shard.dtype)
    joined = jnp.concatenate([zeros, shard, zeros], 0)
    start = extra + count * (rows - delta) - place * rows
    return lax.dynamic_slice_in_dim(joined, jnp.minimum(start, rows + extra), extra, 0)


def from_aligned(chunk, small, place, count, delta, rows):
    aligned = rows - delta
    ahead = -(-(count * delta) // aligned)
    parts = [chunk]
    if ahead == 1:
        keep = small.shape[0]
        got = shift_flat(chunk[:keep], -1)
        parts.append(jnp.where(place == count - 1, small, got))
    else:
        pad = ahead * aligned - small.shape[0]
        tail = jnp.concatenate([small, jnp.zeros((pad, 128), small.dtype)], 0)
        for s in range(1, ahead + 1):
            got = shift_flat(chunk, -s)
            for e in range(s):
                piece = tail[e * aligned : (e + 1) * aligned]
                got = jnp.where(place == count - s + e, piece, got)
            parts.append(got)
    return lax.dynamic_slice_in_dim(jnp.concatenate(parts, 0), delta * place, rows, 0)


def regroup(block):
    return block.reshape(-1, 24, 4, D).transpose(0, 2, 1, 3)


def ungroup(block):
    return block.reshape(-1, 4, 24, D).transpose(0, 2, 1, 3)


def normalize(values, gain):
    factor = lax.rsqrt(jnp.mean(values * values, axis=-1, keepdims=True) + norm_eps)
    scaled = values * factor
    return (scaled, factor, scaled * gain)


def norm_back(grad_in, scaled, factor, gain):
    weighted = grad_in * gain
    inner_mean = jnp.mean(weighted * scaled, axis=-1, keepdims=True)
    return factor * (weighted - scaled * inner_mean)


def adam_update(master, moment_one, moment_two, gradient, step_count, row_start):
    row_index = row_start + jnp.arange(master.shape[0], dtype=jnp.int32)
    matrix_rows = (4 * D * D + 2 * D * FF) // 128
    out_first = 3 * D * D // 128
    out_last = 4 * D * D // 128
    is_matrix = (row_index < matrix_rows)[:, None]
    is_out = ((row_index >= out_first) & (row_index < out_last))[:, None]
    step_rate = jnp.where(is_matrix, jnp.where(is_out, 0.5, 0.1), 1.0)
    decay_rate = jnp.where(is_matrix, 0.1, 0.0)
    step_value = step_count[0].astype(jnp.float32)
    new_one = 0.9 * moment_one + 0.1 * gradient
    new_two = 0.999 * moment_two + 0.001 * gradient * gradient
    corr_first = 1.0 - jnp.power(0.9, step_value)
    corr_second = 1.0 - jnp.power(0.999, step_value)
    new_weights = master - step_rate * (
        new_one / corr_first / (jnp.sqrt(new_two / corr_second) + 1e-08) + decay_rate * master
    )
    return (new_weights, new_one, new_two)


def shards(tokens, out_grad, positions, master, first_moment, second_moment, step_count):
    rows = tokens.shape[0]
    assert rows == SEQ_MIN
    count = lax.axis_size(AXES)
    place = lax.axis_index(AXES).astype(jnp.int32)
    owned = master.shape[0]
    aligned = (4 * D * D + 2 * D * FF) // 128 // count
    delta = owned - aligned
    height = aligned * 128 // D
    staged = count == 32
    first_place = positions[0]
    state = jnp.where(first_place < 0, 0, jnp.where(first_place >= SEQ_MIN, 2, 1)).astype(jnp.int32)
    state_vec = state[None]

    chunk = to_aligned(master, place, count, delta).reshape(-1, D)
    if staged:
        group = 3 * place + jnp.arange(3, dtype=jnp.int32)
        in_up = ((group >= 32) & (group < 64))[:, None, None, None]
        chunk = jnp.where(in_up, regroup(chunk), chunk.reshape(3, 4, 24, D)).reshape(-1, D)
    chunk = chunk.astype(BF)
    small = lax.reduce_precision(small_part(master, place, count, delta), 8, 7)
    core = (place & 1)[None]
    x_bit = (place >> 1) & 1
    y_bit = (place >> 2) & 1
    even = (place & 1) == 0
    if staged:
        z = place >> 3
        mine = jnp.concatenate([chunk, small.astype(BF).reshape(-1, D)], 0)
        tokens_before = shift_ctx(after(tokens, mine), 1)
        got = swap(mine, 16, 16)
        tokens_both = jnp.concatenate([tokens_before, tokens], 0)
        got = after(got, tokens_both)
        rest = jnp.concatenate([chunk, got[:height]], 0)
        none = jnp.zeros((), BF)
        first = jnp.where(z == 0, chunk, jnp.where(z == 2, got[:height], none))
        mine = jnp.concatenate([first, mine[height:] + got[height:]], 0)
        mine = mine + swap(mine, 8, 8)
        across = swap(after(rest, mine), 8, 8)
        mine = join(mine, swap(mine, 2, 4))
        mine = join(mine, swap(mine, 4, 2))
        codes = [z ^ k for k in (1, 2, 3)]
        order = [jnp.where(j == 1, 2, jnp.where(j == 2, 1, j)) for j in codes]
        rest = arrange(
            jnp.stack(order).astype(jnp.int32), rest.reshape(2, height, D), across.reshape(2, height, D), 3
        ).reshape(-1, D)
        across = swap(rest, 2, 4)
        got = swap(mine, 1, 1)
        index = []
        late_index = []
        for k in (0, 1):
            turn = even if k == 0 else jnp.logical_not(even)
            for j in range(4):
                near, far = j & 1, j >> 1
                x_of = x_bit ^ jnp.where(turn, near, far)
                y_of = y_bit ^ jnp.where(turn, far, near)
                piece = 4 * y_of + 2 * x_of + (core[0] ^ k)
                index.append(piece)
                late_index += [piece, piece + 8, piece + 16]
        index = jnp.stack(index).astype(jnp.int32)
        late_index = jnp.stack(late_index + [core[0]]).astype(jnp.int32)
        projected, small, in_weight = qkv_fwd(after(index, rest), tokens_both, (mine, got), rows, 4)
    else:
        tokens_both = jnp.concatenate([shift_ctx(tokens, 1), tokens], 0)
        wide = lax.all_gather(chunk, AXES, axis=0, tiled=True)
        small = lax.psum(small, AXES)[:96].reshape(-1, D)
        in_weight = wide[: 3 * D]
        projected, small = qkv_fwd(core, tokens_both, (in_weight, small), rows, 0)
        late_index = jnp.arange(25, dtype=jnp.int32) % 24
    gain_first = small[0]
    gain_second = small[1]

    forward = []
    if staged:
        rest = join_held(after(rest, projected), across)
        line = swap(rest, 4, 2)
        core_rest = swap(rest, 1, 1)
        forward = att_fwd(after(state_vec, rest), projected, small, forward, FORWARD_PARTS[0], rows)
        forward = att_fwd(after(state_vec, core_rest), projected, small, forward, FORWARD_PARTS[1], rows)
        line = hold(line, forward[0])
        core_line = swap(line, 1, 1)
        forward = att_fwd(after(state_vec, line), projected, small, forward, FORWARD_PARTS[2], rows)
        late_weights = [w.reshape(18, 4, 24, D) for w in (rest, line, core_rest, core_line)]
    else:
        for part in FORWARD_PARTS:
            forward = att_fwd(state_vec, projected, small, forward, part, rows)
        grouped = jnp.concatenate(
            [
                wide[3 * D : 4 * D].reshape(-1, 4, 24, D),
                regroup(wide[4 * D : 8 * D]),
                wide[8 * D :].reshape(-1, 4, 24, D),
            ],
            0,
        )
        late_weights = [grouped[18 * k : 18 * k + 18] for k in range(4)]
    attn_low, logs, *mixed = forward

    layer_out, grad_hidden, grad_attended, grad_gain_two, away_grad, here_grad = ffn(
        state_vec, late_index, tokens, attn_low, out_grad, gain_second[None], late_weights, rows
    )

    def backward(start, done, part):
        return att_bwd(
            start, mixed, attn_low, logs, grad_attended, projected, small, done, BACKWARD_PARTS[part], rows
        )

    if staged:
        stay = [jnp.where(even, 2 * j + x_bit, 2 * y_bit + j) for j in range(2)]
        away = [jnp.where(even, 2 * j + 1 - x_bit, 2 * (1 - y_bit) + j) for j in range(2)]
        pick_plane = jnp.stack(away + stay).astype(jnp.int32)
        other = jnp.where(even, y_bit, x_bit)
        pick_line = jnp.stack([1 - other, other]).astype(jnp.int32)

        def of_quarters(pick, held):
            half = pick.shape[0] // 2
            steps = [pick[s * half + j] + held * t for s in range(2) for t in range(3) for j in range(half)]
            return jnp.stack(steps)

        late_keep = here_grad.reshape(12, height, D)
        late_got = swap(away_grad.reshape(12, height, D), 1, 1)
        done = backward(state_vec, [], 0)
        late_send, late_keep = merge_grid(
            after(of_quarters(pick_plane, 4), done[4]), late_keep, late_got, 6, BF
        )
        late_got = swap(late_send, 2, 4)
        done = backward(after(state_vec, late_send), done, 1)
        late_send, late_keep = merge_grid(
            after(of_quarters(pick_line, 2), done[4]), late_keep, late_got, 3
        )
        late_got = swap(late_send, 4, 2)
        done = backward(after(state_vec, late_send), done, 2)
        z_even = (z & 1) == 0
        low_pair = [jnp.where(z_even, 0, 0), jnp.where(z_even, 2, 1)]
        high_pair = [jnp.where(z_even, 0, 0), jnp.where(z_even, 1, 2)]
        pick_z = jnp.stack(low_pair + high_pair).astype(jnp.int32)
        late_send, late_keep = merge_grid(after(pick_z, done[4]), late_keep, late_got, 2)
        late_got = swap(late_send, 8, 8)
        done = backward(after(state_vec, late_send), done, 3)
        high = z >> 1
        pick_last = jnp.stack([1 - high, high]).astype(jnp.int32)
        late_send, late_keep = merge_grid(after(pick_last, done[4]), late_keep, late_got, 1)
        late_got = swap(late_send, 16, 16, (0, 1, 3))
        sums_state = after(core, late_send)
    else:
        done = []
        for part in range(4):
            done = backward(state_vec, done, part)
        sums_state = core
    *back, tap_grads = done
    grads_before, gain_one_grad = before_bwd(tokens_both, back, in_weight, rows)
    from_next = shift_ctx(grads_before, -1)
    sums = qkv_bwd(
        after(sums_state, grads_before), tokens_both, back, in_weight, gain_first[None], gain_one_grad, grad_gain_two, tap_grads, rows,
        4 if staged else 0,
    )
    grad_normed_one = sums[2]
    scaled_one, factor_one, _ = normalize(tokens.astype(F32), gain_first)
    input_grad = grad_hidden + norm_back(
        grad_normed_one + from_next.astype(F32), scaled_one, factor_one, gain_first
    )

    if staged:
        send, keep = sums[:2]
        got = swap(after(send, late_got, from_next), 1, 1)
        send, keep = merge(pick_plane, keep, got, height + 16, 2)
        got = swap(send, 2, 4)
        late_got = after(late_got, send)
        late_chunk = late_keep[0] + late_got[0].astype(F32)
        late_chunk = jnp.where(in_up, ungroup(late_chunk).reshape(3, 4, 24, D), late_chunk.reshape(3, 4, 24, D))
        late_chunk = late_chunk.reshape(-1, D)
        late_next = shift_flat(late_chunk[:16], -1)
        send, keep = merge(pick_line, keep, got, height + 16, 1)
        got = swap(send, 4, 2)
        send, keep = merge(after(core, late_next), keep, got, height + 16, 0)
        got = swap(send, 8, 8)
        send, keep = merge(after(core, input_grad), keep, got, height + 16, 0)
        got = swap(send, 16, 16, (1, 2))
        first = keep + got.astype(F32)
        quarter = count // 4
        follow = jnp.where(place < quarter - 1, first[height : height + 16], late_next)
        follow = jnp.where(place == count - 1, first[height + 16 :], follow)
        chunk_grad = jnp.where(place < quarter, first[:height], late_chunk)
        chunk_grad = jnp.concatenate([chunk_grad, follow], 0).reshape(-1, 128)
        gradient = lax.dynamic_slice_in_dim(chunk_grad, delta * place, owned, 0)
    else:
        flat_grad = jnp.stack([here_grad.reshape(12, 3, 4, 24, D), away_grad.reshape(12, 3, 4, 24, D)], 1)
        flat_grad = flat_grad.reshape(72, 4, 24, D)
        wide_grad = jnp.concatenate(
            [
                sums[0],
                flat_grad[:8].reshape(-1, D),
                ungroup(flat_grad[8:40]).reshape(-1, D),
                flat_grad[40:].reshape(-1, D),
            ],
            0,
        )
        chunk_grad = lax.psum_scatter(wide_grad, AXES, scatter_dimension=0, tiled=True).astype(F32)
        used = sums[1].reshape(-1, 128)
        extra = count * delta
        small_grad = jnp.concatenate([used, jnp.zeros((extra - used.shape[0], 128), F32)], 0)
        small_grad = lax.psum(small_grad, AXES)
        gradient = from_aligned(chunk_grad.reshape(-1, 128), small_grad, place, count, delta, owned)
    new_weights, new_one, new_two = adam_update(
        master, first_moment, second_moment, gradient, step_count, place * owned
    )
    return (layer_out, input_grad, new_weights, new_one, new_two, new_weights.astype(BF))


def solution(mesh):
    spread = P(AXES, None)
    return jax.shard_map(
        shards,
        mesh=mesh,
        in_specs=(spread, spread, P(AXES), spread, spread, spread, P()),
        out_specs=(spread,) * 6,
        check_vma=False,
    )
```

```python
import jax
import jax.numpy as jnp
from jax import lax
from jax.experimental import pallas as pl
from jax.experimental.pallas import tpu as pltpu
from jax.sharding import PartitionSpec as P

D = 768
HEADS = 12
HEAD_DIM = 64
FF = 3072
SEQ_MIN = 1024
AXES = ("dp", "ctx")
QB = 256
FORWARD_PARTS = ((0, 2), (2, 2), (4, 2))
BACKWARD_PARTS = ((0, 1), (1, 2), (3, 1), (4, 2))
F32 = jnp.float32
BF = jnp.bfloat16
NT = (((1,), (1,)), ((), ()))
TN = (((0,), (0,)), ((), ()))
norm_eps = 1e-06
VMEM_LIMIT = 56 << 20


def dot(left, right):
    return jnp.dot(left, right, preferred_element_type=F32)


def dot_nt(left, right):
    return lax.dot_general(left, right, NT, preferred_element_type=F32)


def dot_tn(left, right):
    return lax.dot_general(left, right, TN, preferred_element_type=F32)


def cost(flops, nbytes, exps=0):
    return pl.CostEstimate(flops=int(flops), bytes_accessed=int(nbytes), transcendentals=int(exps))


def taps_of(small, matrix):
    return [small[2 + 3 * j + matrix : 3 + 3 * j + matrix, :] for j in range(3)]


def row_ids(height):
    return lax.broadcasted_iota(jnp.int32, (height, 128), 0)


def conv(out_ref, x_ref, start, tail_ref, taps, rows, state):
    height = x_ref.shape[0]
    for r in range(0, height, QB):
        at = start + r
        if r:
            x = x_ref[r - 16 : r + QB, :].astype(F32)
        else:
            before = jnp.zeros((16, 128), F32)
            if tail_ref is not None:
                before = jnp.concatenate([before[8:], tail_ref[...].astype(F32)], 0)
            x = jnp.concatenate([before, x_ref[0:QB, :].astype(F32)], 0)
        one = pltpu.roll(x, 1, 0)[16:]
        two = pltpu.roll(x, 2, 0)[16:]
        x = x[16:]
        scale = 1.0
        if at >= rows:
            scale = jnp.where(state > 0, 1.0, 0.0)
        if at == 0 or at == rows:
            seen = jnp.where(state == 2, 1.0, 0.0) if at else 0.0
            row = row_ids(QB)
            one = jnp.where(row < 1, one * seen, one)
            two = jnp.where(row < 2, two * seen, two)
        c_one = taps[1] * scale
        c_two = taps[2] * scale
        out_ref[r : r + QB, :] = (taps[0] * x + c_one * one + c_two * two).astype(BF)


def att_fwd_kernel(
    state_ref, tail_ref, q_ref, k_ref, v_ref, small_ref,
    o_ref, l_ref, qm_ref, km_ref, vm_ref, ka, va,
):
    rows = q_ref.shape[0]
    lane = lax.broadcasted_iota(jnp.int32, (1, 128), 1)
    state = state_ref[0]
    conv(qm_ref, q_ref, rows, tail_ref, taps_of(small_ref[...], 0), rows, state)
    conv(km_ref, k_ref, 0, None, taps_of(small_ref[...], 1), rows, state)
    conv(vm_ref, v_ref, 0, None, taps_of(small_ref[...], 2), rows, state)
    bias = jnp.where(state == 2, 0.0, -1e30)
    for h in range(2):
        mine = (lane < 64) if h == 0 else (lane >= 64)
        base = 64 if h == 0 else 0
        first = jnp.where(lane == base, bias, 0.0).astype(BF)
        for r in range(0, 2 * rows, QB):
            at = pl.ds(r, QB)
            ka[h, at, :] = jnp.where(mine, km_ref[at, :], first if r < rows else jnp.zeros((), BF))
            va[h, at, :] = jnp.where(mine, vm_ref[at, :], jnp.ones((), BF))
    for i in range(rows // QB):
        rs = pl.ds(i * QB, QB)
        outs = []
        sums = []
        qf = qm_ref[rs, :].astype(F32) * 0.125
        for h in range(2):
            mine = (lane < 64) if h == 0 else (lane >= 64)
            base = 64 if h == 0 else 0
            qh = jnp.where(mine, qf, jnp.where(lane == base, 1.0, 0.0)).astype(BF)
            nk = rows + (i + 1) * QB
            s = dot_nt(qh, ka[h, 0:nk, :])
            r = lax.broadcasted_iota(jnp.int32, (QB, QB), 0)
            c = lax.broadcasted_iota(jnp.int32, (QB, QB), 1)
            sd = jnp.where(c <= r, s[:, nk - QB :], -1e30)
            se = s[:, : nk - QB]
            m = jnp.maximum(
                jnp.max(sd, axis=1, keepdims=True), jnp.max(se, axis=1, keepdims=True)
            )
            p = jnp.concatenate([jnp.exp(se - m).astype(BF), jnp.exp(sd - m).astype(BF)], 1)
            o = dot(p, va[h, 0:nk, :])
            outs.append(o / pltpu.roll(o, 64, 1))
            sums.append(m + jnp.log(o))
        res = jnp.where(lane < 64, outs[0], outs[1])
        res = jnp.where(state == 0, vm_ref[pl.ds(rows + i * QB, QB), :].astype(F32), res)
        o_ref[rs, :] = res.astype(BF)
        l_ref[rs, :] = jnp.where(lane < 64, sums[1], sums[0])


def call_in_parts(body, in_specs, out_specs, out_shape, earlier, part, **options):
    used = len(in_specs)

    def kernel(*refs):
        body(*refs[:used], *refs[used + len(earlier) :])

    return pl.pallas_call(
        kernel,
        grid=(part[1],),
        in_specs=in_specs + [pl.BlockSpec(memory_space=pl.ANY)] * len(earlier),
        out_specs=out_specs,
        out_shape=out_shape,
        input_output_aliases={used + i: i for i in range(len(earlier))},
        compiler_params=pltpu.CompilerParams(vmem_limit_bytes=VMEM_LIMIT),
        **options,
    )


def columns(part):
    first = part[0]

    def cols(height, row, off):
        return pl.BlockSpec((height, 128), lambda p: (row, p + first + off))

    return cols


def att_fwd(state, projected, small, earlier, part, rows):
    cols = columns(part)
    return call_in_parts(
        att_fwd_kernel,
        [
            pl.BlockSpec(memory_space=pltpu.SMEM),
            cols(8, rows // 8 - 1, 0),
            cols(rows, 1, 0),
            cols(2 * rows, 0, 6),
            cols(2 * rows, 0, 12),
            cols(16, 0, 0),
        ],
        [cols(rows, 0, 0)] * 3 + [cols(2 * rows, 0, 0)] * 2,
        [
            jax.ShapeDtypeStruct((rows, D), BF),
            jax.ShapeDtypeStruct((rows, D), F32),
            jax.ShapeDtypeStruct((rows, D), BF),
            jax.ShapeDtypeStruct((2 * rows, D), BF),
            jax.ShapeDtypeStruct((2 * rows, D), BF),
        ],
        earlier,
        part,
        scratch_shapes=[pltpu.VMEM((2, 2 * rows, 128), BF)] * 2,
        cost_estimate=cost(
            2 * 2 * 2 * rows * rows * 1.5 * 256 * part[1],
            rows * D * 5 * part[1],
            2 * rows * rows * 1.5 * part[1],
        ),
        name="att_fwd",
    )(state, projected, projected, projected, projected, small, *earlier)


def three(x, lane, base):
    hi = x.astype(BF).astype(F32)
    r = x - hi
    mid = r.astype(BF).astype(F32)
    lo = r - mid
    return jnp.where(
        lane == base, hi, jnp.where(lane == base + 1, mid, jnp.where(lane == base + 2, lo, 0.0))
    )


def conv_back(out_ref, grad_ref, x_ref, start, tail, taps, rows, state):
    height = grad_ref.shape[0]
    joint = jnp.where(state == 2, 1.0, 0.0)
    sums = [jnp.zeros((1, 128), F32)] * 3

    def add(parts, x):
        return [s + jnp.sum(g * x, axis=0, keepdims=True) for s, g in zip(sums, parts)]

    for r in range(0, height, QB):
        ends = r + QB == height
        meets = start + r + QB == rows
        if ends:
            grad = jnp.concatenate([grad_ref[r : r + QB, :], jnp.zeros((8, 128), F32)], 0)
        else:
            grad = grad_ref[r : r + QB + 8, :]
        one = pltpu.roll(grad, QB + 7, 0)[:QB]
        two = pltpu.roll(grad, QB + 6, 0)[:QB]
        grad = grad[:QB]
        if meets and not ends:
            row = row_ids(QB)
            one = jnp.where(row >= QB - 1, one * joint, one)
            two = jnp.where(row >= QB - 2, two * joint, two)
        out_ref[r : r + QB, :] = (taps[0] * grad + taps[1] * one + taps[2] * two).astype(BF)
        sums = add((grad, one, two), x_ref[r : r + QB, :].astype(F32))
    if tail is not None:
        grad = jnp.concatenate([jnp.zeros((8, 128), F32), grad_ref[0:8, :]], 0)
        one = pltpu.roll(grad, 15, 0)[:8] * joint
        two = pltpu.roll(grad, 14, 0)[:8] * joint
        tail[0][...] = (taps[1] * one + taps[2] * two).astype(BF)
        sums = add((grad[:8], one, two), tail[1][...].astype(F32))
    return sums


def att_bwd_kernel(
    state_ref, q_ref, k_ref, v_ref, o_ref, l_ref, do_ref, xt_ref, xq_ref, xk_ref, xv_ref,
    small_ref,
    pq_ref, pt_ref, pk_ref, pv_ref, tg_ref, qa, da, qt, dt, kt, dqt, dqs, dks, dvs,
):
    rows = q_ref.shape[0]
    lane = lax.broadcasted_iota(jnp.int32, (1, 128), 1)
    second = state_ref[0] == 2
    for r in range(0, rows, QB):
        at = pl.ds(r, QB)
        do = do_ref[at, :].astype(F32)
        od = do * o_ref[at, :].astype(F32)
        qf = q_ref[at, :].astype(F32) * 0.125
        lv = l_ref[at, :]
        for h in range(2):
            mine = (lane < 64) if h == 0 else (lane >= 64)
            base = 64 if h == 0 else 0
            delta = jnp.sum(jnp.where(mine, od, 0.0), axis=1, keepdims=True)
            qa[h, at, :] = jnp.where(mine, qf, three(-lv, lane, base)).astype(BF)
            da[h, at, :] = jnp.where(mine, do, three(-delta, lane, base)).astype(BF)
        qt[:, at] = jnp.transpose(qf).astype(BF)
        dt[:, at] = jnp.transpose(do).astype(BF)
    for r in range(0, 2 * rows, QB):
        at = pl.ds(r, QB)
        kt[:, at] = jnp.transpose(k_ref[at, :].astype(F32)).astype(BF)
    dqt[...] = jnp.zeros(dqt.shape, F32)

    def keys(ks, first, diagonal):
        kk = k_ref[ks, :]
        vv = v_ref[ks, :]
        dv = []
        dk = []
        for h in range(2):
            mine = (lane < 64) if h == 0 else (lane >= 64)
            base = 64 if h == 0 else 0
            ones3 = ((lane >= base) & (lane < base + 3)).astype(BF)
            hs = slice(64 * h, 64 * h + 64)
            st = dot_nt(jnp.where(mine, kk, ones3), qa[h, first:rows, :])
            dp = dot_nt(jnp.where(mine, vv, ones3), da[h, first:rows, :])
            p = jnp.exp(st)
            if diagonal:
                r = lax.broadcasted_iota(jnp.int32, (QB, QB), 0)
                c = lax.broadcasted_iota(jnp.int32, (QB, QB), 1)
                seen = jnp.where(r <= c, p[:, :QB], 0.0)
                p = jnp.concatenate([seen, p[:, QB:]], 1) if first + QB < rows else seen
            ds = (p * dp).astype(BF)
            dv.append(dot_nt(dt[hs, first:rows], p.astype(BF)))
            dk.append(dot_nt(qt[hs, first:rows], ds))
            dqt[hs, first:rows] += dot(kt[hs, ks], ds)
        dvs[ks, :] = jnp.transpose(jnp.concatenate(dv, 0))
        dks[ks, :] = jnp.transpose(jnp.concatenate(dk, 0))

    for j in range(rows // QB):
        keys(pl.ds(rows + j * QB, QB), j * QB, True)

    @pl.when(second)
    def _():
        def step(j, carry):
            keys(pl.ds(pl.multiple_of(j * QB, QB), QB), 0, False)
            return carry

        lax.fori_loop(0, rows // QB, step, 0)

    @pl.when(jnp.logical_not(second))
    def _():
        dks[0:rows, :] = jnp.zeros((rows, 128), F32)
        dvs[0:rows, :] = jnp.zeros((rows, 128), F32)

    for r in range(0, rows, QB):
        dqs[r : r + QB, :] = jnp.transpose(dqt[:, r : r + QB]) * 0.125
    state = state_ref[0]
    sq = conv_back(pq_ref, dqs, xq_ref, rows, (pt_ref, xt_ref), taps_of(small_ref[...], 0), rows, state)
    sk = conv_back(pk_ref, dks, xk_ref, 0, None, taps_of(small_ref[...], 1), rows, state)
    sv = conv_back(pv_ref, dvs, xv_ref, 0, None, taps_of(small_ref[...], 2), rows, state)
    tg_ref[...] = jnp.zeros(tg_ref.shape, F32)
    for j in range(3):
        for m, s in enumerate((sq, sk, sv)):
            tg_ref[3 * j + m : 3 * j + m + 1, :] = s[j]


def att_bwd(state, mixed, attended, logs, grad, projected, small, earlier, part, rows):
    cols = columns(part)
    own = cols(rows, 0, 0)
    both = cols(2 * rows, 0, 0)
    return call_in_parts(
        att_bwd_kernel,
        [
            pl.BlockSpec(memory_space=pltpu.SMEM),
            own, both, both, own, own, own,
            cols(8, rows // 8 - 1, 0),
            cols(rows, 1, 0),
            cols(2 * rows, 0, 6),
            cols(2 * rows, 0, 12),
            cols(16, 0, 0),
        ],
        [own, cols(8, 0, 0), both, both, cols(16, 0, 0)],
        [
            jax.ShapeDtypeStruct((rows, D), BF),
            jax.ShapeDtypeStruct((8, D), BF),
            jax.ShapeDtypeStruct((2 * rows, D), BF),
            jax.ShapeDtypeStruct((2 * rows, D), BF),
            jax.ShapeDtypeStruct((16, D), F32),
        ],
        earlier,
        part,
        scratch_shapes=[
            pltpu.VMEM((2, rows, 128), BF),
            pltpu.VMEM((2, rows, 128), BF),
            pltpu.VMEM((128, rows), BF),
            pltpu.VMEM((128, rows), BF),
            pltpu.VMEM((128, 2 * rows), BF),
            pltpu.VMEM((128, rows), F32),
            pltpu.VMEM((rows, 128), F32),
            pltpu.VMEM((2 * rows, 128), F32),
            pltpu.VMEM((2 * rows, 128), F32),
        ],
        cost_estimate=cost(
            5 * 2 * 2 * rows * rows * 1.5 * 256 * part[1],
            rows * D * 7 * part[1],
            2 * rows * rows * 1.5 * part[1],
        ),
        name="att_bwd",
    )(state, *mixed, attended, logs, grad, projected, projected, projected, projected,
      small, *earlier)


def unit_rows(x):
    return x * lax.rsqrt(jnp.mean(x * x, axis=-1, keepdims=True) + norm_eps)


def before_bwd_kernel(x_ref, dt_ref, dk_ref, dv_ref, w_ref, out_ref, gain_ref):
    i = pl.program_id(0)
    hat = unit_rows(x_ref[...].astype(F32))
    gn = dot_nt(dk_ref[...], w_ref[D : 2 * D, :]) + dot_nt(dv_ref[...], w_ref[2 * D : 3 * D, :])

    last_step = pl.num_programs(0) - 1

    @pl.when(i == 0)
    def _():
        gain_ref[...] = jnp.zeros(gain_ref.shape, F32)

    @pl.when(i < last_step)
    def _():
        out_ref[...] = gn.astype(BF)
        gain_ref[...] += jnp.sum(gn * hat, axis=0, keepdims=True)

    @pl.when(i == last_step)
    def _():
        last = gn.shape[0] - 8
        full = jnp.concatenate([gn[:last], gn[last:] + dot_nt(dt_ref[...], w_ref[0:D, :])], 0)
        out_ref[...] = full.astype(BF)
        gain_ref[...] += jnp.sum(full * hat, axis=0, keepdims=True)


def before_bwd(x_both, back, weight, rows):
    dt, dk, dv = back[1:]
    blocks = 4
    height = rows // blocks
    step = pl.BlockSpec((height, D), lambda i: (i, 0))

    def whole(shape):
        return pl.BlockSpec(shape, lambda i: (0, 0))

    return pl.pallas_call(
        before_bwd_kernel,
        grid=(blocks,),
        in_specs=[step, whole((8, D)), step, step, whole((3 * D, D))],
        out_specs=[step, whole((1, D))],
        out_shape=[jax.ShapeDtypeStruct((rows, D), BF), jax.ShapeDtypeStruct((1, D), F32)],
        compiler_params=pltpu.CompilerParams(vmem_limit_bytes=VMEM_LIMIT),
        cost_estimate=cost(2 * rows * D * D * 2, rows * D * 12),
        name="before_bwd",
    )(x_both, dt, dk, dv, weight)


def qkv_bwd_kernel(
    core_ref, x_ref, dq_ref, dt_ref, dk_ref, dv_ref, w_ref, gain_ref, gain_one_ref, gain_two_ref, tg_ref,
    *refs, pieces, blocks,
):
    if pieces:
        send_ref, keep_ref, own_ref, acc, gacc = refs
    else:
        keep_ref, small_ref, own_ref, acc, gacc = refs
    i = pl.program_id(0)
    half = blocks // 2

    @pl.when(i == 0)
    def _():
        acc[...] = jnp.zeros(acc.shape, F32)
        gacc[0:1, :] = gain_one_ref[...]

    hat = unit_rows(x_ref[...].astype(F32))
    low = (hat * gain_ref[...]).astype(BF)
    dk = dk_ref[...]
    dv = dv_ref[...]
    acc[D : 2 * D, :] += dot_tn(low, dk)
    acc[2 * D : 3 * D, :] += dot_tn(low, dv)

    @pl.when(i == half - 1)
    def _():
        acc[0:D, :] += dot_tn(low[low.shape[0] - 8 :], dt_ref[...])

    @pl.when(i >= half)
    def _():
        dq = dq_ref[...]
        acc[0:D, :] += dot_tn(low, dq)
        full = (
            dot_nt(dk, w_ref[D : 2 * D, :])
            + dot_nt(dv, w_ref[2 * D : 3 * D, :])
            + dot_nt(dq, w_ref[0:D, :])
        )
        own_ref[...] = full
        gacc[0:1, :] += jnp.sum(full * hat, axis=0, keepdims=True)

    @pl.when(i == blocks - 1)
    def _():
        small = jnp.concatenate(
            [gacc[0:1, :], gain_two_ref[...], tg_ref[0:9, :], jnp.zeros((5, D), F32)], 0
        )
        if pieces:
            core = core_ref[0]
            height = 3 * D // (2 * pieces)
            wide = height + 16
            for j in range(pieces):
                to = pl.ds(j * wide, wide)
                away = pl.ds(pl.multiple_of((2 * j + 1 - core) * height, 16), wide)
                here = pl.ds(pl.multiple_of((2 * j + core) * height, 16), wide)
                send_ref[to, :] = acc[away, :].astype(BF)
                keep_ref[to, :] = acc[here, :]
            send_ref[pieces * wide :, :] = small.astype(BF)
            keep_ref[pieces * wide :, :] = small
        else:
            keep_ref[...] = acc[0 : 3 * D, :].astype(BF)
            small_ref[...] = small


def qkv_bwd(core, x_both, back, weight, gain, gain_one_grad, gain_two_grad, tap_grads, rows, pieces):
    dq, dt, dk, dv = back
    blocks = 4
    half = blocks // 2
    height = 2 * rows // blocks
    step = pl.BlockSpec((height, D), lambda i: (i, 0))
    late = pl.BlockSpec((height, D), lambda i: (jnp.maximum(i - half, 0), 0))

    def whole(shape):
        return pl.BlockSpec(shape, lambda i: (0, 0))

    if pieces:
        packed = 3 * D // 2 + 16 * pieces + 16
        outs = [jax.ShapeDtypeStruct((packed, D), BF), jax.ShapeDtypeStruct((packed, D), F32)]
        out_at = [whole((packed, D))] * 2
    else:
        outs = [jax.ShapeDtypeStruct((3 * D, D), BF), jax.ShapeDtypeStruct((16, D), F32)]
        out_at = [whole((3 * D, D)), whole((16, D))]

    def body(*refs):
        qkv_bwd_kernel(*refs, pieces=pieces, blocks=blocks)

    return pl.pallas_call(
        body,
        grid=(blocks,),
        in_specs=[
            pl.BlockSpec(memory_space=pltpu.SMEM),
            step, late, whole((8, D)), step, step, whole((3 * D, D)),
            whole((1, D)), whole((1, D)), whole((1, D)), whole((16, D)),
        ],
        out_specs=out_at + [late],
        out_shape=outs + [jax.ShapeDtypeStruct((rows, D), F32)],
        scratch_shapes=[pltpu.VMEM((3 * D + 16, D), F32), pltpu.VMEM((8, D), F32)],
        compiler_params=pltpu.CompilerParams(vmem_limit_bytes=VMEM_LIMIT),
        cost_estimate=cost(2 * 2 * D * D * 4 * rows, rows * D * 30),
        name="qkv_bwd",
    )(core, x_both, dq, dt, dk, dv, weight, gain, gain_one_grad, gain_two_grad, tap_grads)


def merge(index, keep, got, height, taken):
    rows = keep.shape[0]
    out_rows = taken * height + 16 if taken else rows

    def body(index_ref, keep_ref, got_ref, send_ref, stay_ref):
        if not taken:
            total = keep_ref[...] + got_ref[...].astype(F32)
            send_ref[...] = total.astype(BF)
            stay_ref[...] = total
            return
        for j in range(taken):
            to = pl.ds(j * height, height)
            away = pl.ds(pl.multiple_of(index_ref[j] * height, 16), height)
            here = pl.ds(pl.multiple_of(index_ref[taken + j] * height, 16), height)
            send_ref[to, :] = (keep_ref[away, :] + got_ref[away, :].astype(F32)).astype(BF)
            stay_ref[to, :] = keep_ref[here, :] + got_ref[here, :].astype(F32)
        end = keep_ref[rows - 16 :, :] + got_ref[rows - 16 :, :].astype(F32)
        send_ref[taken * height :, :] = end.astype(BF)
        stay_ref[taken * height :, :] = end

    vmem = pl.BlockSpec(memory_space=pltpu.VMEM)
    return pl.pallas_call(
        body,
        in_specs=[pl.BlockSpec(memory_space=pltpu.SMEM), vmem, vmem],
        out_specs=[vmem, vmem],
        out_shape=[
            jax.ShapeDtypeStruct((out_rows, D), BF),
            jax.ShapeDtypeStruct((out_rows, D), F32),
        ],
        compiler_params=pltpu.CompilerParams(vmem_limit_bytes=32 << 20),
        cost_estimate=cost(rows * D, rows * D * 12),
        name="merge",
    )(index, keep, got)


def merge_grid(index, keep, got, taken, kept=F32):
    height = keep.shape[1]

    def body(index_ref, ka_ref, ga_ref, kb_ref, gb_ref, send_ref, stay_ref):
        send_ref[...] = (ka_ref[...].astype(F32) + ga_ref[...].astype(F32)).astype(BF)
        stay_ref[...] = (kb_ref[...].astype(F32) + gb_ref[...].astype(F32)).astype(kept)

    away = pl.BlockSpec((1, height, D), lambda i, index: (index[i], 0, 0))
    here = pl.BlockSpec((1, height, D), lambda i, index: (index[taken + i], 0, 0))
    step = pl.BlockSpec((1, height, D), lambda i, index: (i, 0, 0))
    return pl.pallas_call(
        body,
        grid_spec=pltpu.PrefetchScalarGridSpec(
            num_scalar_prefetch=1,
            grid=(taken,),
            in_specs=[away, away, here, here],
            out_specs=[step, step],
        ),
        out_shape=[
            pltpu.HBM((taken, height, D), BF),
            pltpu.HBM((taken, height, D), kept),
        ],
        compiler_params=pltpu.CompilerParams(vmem_limit_bytes=32 << 20),
        cost_estimate=cost(taken * height * D * 2, taken * height * D * 16),
        name="merge_grid",
    )(index, keep, got, keep, got)


def arrange(index, blocks):
    height = blocks[0].shape[0] - 16

    def body(index_ref, *refs):
        first_ref, rest_ref = refs[4:]
        refs = refs[:4]
        for i in range(4):
            for k in range(4):

                @pl.when(index_ref[i] == k)
                def _():
                    piece = refs[k][0:height, :]
                    if i == 0:
                        first_ref[0:height, :] = piece
                    else:
                        rest_ref[(i - 1) * height : i * height, :] = piece

        ends = [ref[height:, :].astype(F32) for ref in refs]
        first_ref[height:, :] = (ends[0] + ends[1] + ends[2] + ends[3]).astype(BF)

    vmem = pl.BlockSpec(memory_space=pltpu.VMEM)
    return pl.pallas_call(
        body,
        in_specs=[pl.BlockSpec(memory_space=pltpu.SMEM)] + [vmem] * 4,
        out_specs=[vmem, vmem],
        out_shape=[
            jax.ShapeDtypeStruct((height + 16, D), BF),
            jax.ShapeDtypeStruct((3 * height, D), BF),
        ],
        compiler_params=pltpu.CompilerParams(vmem_limit_bytes=32 << 20),
        cost_estimate=cost(4 * height * D, 4 * height * D * 4),
        name="arrange",
    )(index, *blocks)


def join(own, got, shared=16):
    rows = own.shape[0]
    body_rows = rows - shared

    def body(own_ref, got_ref, out_ref):
        out_ref[0:body_rows, :] = own_ref[0:body_rows, :]
        out_ref[body_rows : 2 * body_rows, :] = got_ref[0:body_rows, :]
        if shared:
            out_ref[2 * body_rows :, :] = own_ref[body_rows:, :] + got_ref[body_rows:, :]

    vmem = pl.BlockSpec(memory_space=pltpu.VMEM)
    return pl.pallas_call(
        body,
        in_specs=[vmem, vmem],
        out_specs=vmem,
        out_shape=jax.ShapeDtypeStruct((2 * body_rows + shared, D), BF),
        compiler_params=pltpu.CompilerParams(vmem_limit_bytes=32 << 20),
        cost_estimate=cost(rows * D, rows * D * 8),
        name="join",
    )(own, got)


def join_held(own, got):
    rows = own.shape[0]
    cuts = 4
    size = rows // cuts

    def body(own_ref, got_ref, out_ref, sems):
        copies = []
        for k, ref in enumerate((own_ref, got_ref)):
            for j in range(cuts):
                source = ref.at[pl.ds(j * size, size)]
                to = out_ref.at[pl.ds(k * rows + j * size, size)]
                copies.append(pltpu.make_async_copy(source, to, sems.at[k * cuts + j]))
        for copy in copies:
            copy.start()
        for copy in copies:
            copy.wait()

    held = pl.BlockSpec(memory_space=pltpu.HBM)
    return pl.pallas_call(
        body,
        in_specs=[held, held],
        out_specs=held,
        out_shape=jax.ShapeDtypeStruct((2 * rows, D), BF),
        scratch_shapes=[pltpu.SemaphoreType.DMA((2 * cuts,))],
        compiler_params=pltpu.CompilerParams(vmem_limit_bytes=16 << 20),
        cost_estimate=cost(0, rows * D * 8),
        name="join_held",
    )(own, got)


def hold(block, other):
    held = pl.BlockSpec(memory_space=pl.ANY)
    return pl.pallas_call(
        lambda block_ref, other_ref, out_ref: None,
        in_specs=[held, held],
        out_specs=held,
        out_shape=jax.ShapeDtypeStruct(block.shape, block.dtype),
        input_output_aliases={0: 0},
        name="hold",
    )(block, other)


def qkv_fwd_kernel(index_ref, x_ref, *refs, pieces, blocks):
    if pieces:
        own_ref, got_ref, out_ref, small_ref, weight = refs
    else:
        weight, given_ref, out_ref, small_ref = refs
    i = pl.program_id(0)

    @pl.when(i == 0)
    def _():
        if pieces:
            height = 3 * D // (2 * pieces)
            for j in range(pieces):
                at = pl.ds(j * height, height)
                for k, ref in enumerate((own_ref, got_ref)):
                    to = pl.multiple_of(index_ref[k * pieces + j] * height, 16)
                    weight[pl.ds(to, height), :] = ref[at, :]
            end = pl.ds(pieces * height, 16)
            small_ref[...] = own_ref[end, :].astype(F32) + got_ref[end, :].astype(F32)
        else:
            small_ref[...] = given_ref[...]

    x = x_ref[...].astype(F32)
    hat = x * lax.rsqrt(jnp.mean(x * x, axis=-1, keepdims=True) + norm_eps)
    low = (hat * small_ref[0:1, :]).astype(BF)

    @pl.when(i >= blocks // 2 - 1)
    def _():
        out_ref[:, 0:D] = dot(low, weight[0:D, :]).astype(BF)

    out_ref[:, D : 2 * D] = dot(low, weight[D : 2 * D, :]).astype(BF)
    out_ref[:, 2 * D : 3 * D] = dot(low, weight[2 * D : 3 * D, :]).astype(BF)


def qkv_fwd(index, x_both, weights, rows, pieces):
    blocks = 4
    height = 2 * rows // blocks

    def body(*refs):
        qkv_fwd_kernel(*refs, pieces=pieces, blocks=blocks)

    return pl.pallas_call(
        body,
        grid=(blocks,),
        in_specs=[
            pl.BlockSpec(memory_space=pltpu.SMEM),
            pl.BlockSpec((height, D), lambda i: (i, 0)),
            *[pl.BlockSpec(w.shape, lambda i: (0, 0)) for w in weights],
        ],
        out_specs=[
            pl.BlockSpec((height, 3 * D), lambda i: (i, 0)),
            pl.BlockSpec((16, D), lambda i: (0, 0)),
        ]
        + ([pl.BlockSpec((3 * D, D), lambda i: (0, 0))] if pieces else []),
        out_shape=[
            jax.ShapeDtypeStruct((2 * rows, 3 * D), BF),
            jax.ShapeDtypeStruct((16, D), F32),
        ]
        + ([jax.ShapeDtypeStruct((3 * D, D), BF)] if pieces else []),
        compiler_params=pltpu.CompilerParams(vmem_limit_bytes=VMEM_LIMIT),
        cost_estimate=cost(2 * 2 * rows * D * 3 * D, rows * D * 20),
        name="qkv_fwd",
    )(index, x_both, *weights)


def ffn_kernel(
    state_ref, index_ref, x_ref, att_ref, cot_ref, gain_ref, own_ref, own_two_ref, got_ref, got_two_ref,
    out_ref, gh_ref, ga_ref, gain_grad_ref, away_ref, here_ref,
    hidden, low, total, back, cot, sq, gb, weights, stage_up, stage_down, stage_out, in_sems, sems,
):
    c = pl.program_id(0)
    rows = x_ref.shape[0]
    blocks = [pl.ds(i * QB, QB) for i in range(rows // QB)]
    last = c == pl.num_programs(0) - 1
    core = index_ref[24]

    def fetch(k, j):
        ref = ((own_ref, own_two_ref), (got_ref, got_two_ref))[k][j // 6]
        piece = index_ref[12 * k + j]
        to = weights.at[pl.ds(3 * piece, 3)]
        return pltpu.make_async_copy(ref.at[pl.ds(3 * (j % 6), 3)], to, in_sems.at[piece])

    def fetched(pieces):
        for piece in pieces:
            at = weights.at[pl.ds(3 * piece, 3)]
            pltpu.make_async_copy(own_ref.at[pl.ds(0, 3)], at, in_sems.at[piece]).wait()

    def put(source, group, count, column, sem, wait=False):
        piece = group // 3
        at = (piece // 2) * 3 + group % 3

        def copy(ref):
            to = ref.at[pl.ds(at, count)] if column is None else ref.at[pl.ds(at, count), column]
            return pltpu.make_async_copy(source, to, sems.at[sem])

        if wait:
            copy(here_ref).wait()
            return
        mine = piece % 2 == core

        @pl.when(mine)
        def _():
            copy(here_ref).start()

        @pl.when(jnp.logical_not(mine))
        def _():
            copy(away_ref).start()

    def put_up(i, wait=False):
        start = 0
        k = 0
        while start < 32:
            count = min(3 - (8 + start) % 3, 32 - start)
            put(stage_up.at[i, pl.ds(start, count)], 8 + start, count, i, 20 * i + k, wait)
            start += count
            k += 1

    def put_down(i, wait=False):
        for k in range(8):
            put(stage_down.at[i, pl.ds(k, 1)], 40 + 8 * i + k, 1, None, 20 * i + 12 + k, wait)

    def put_out(wait=False):
        for k in range(8):
            put(stage_out.at[pl.ds(k, 1)], k, 1, None, 80 + k, wait)

    def square(first):
        return weights[first : first + 8].reshape(D, D)

    @pl.when(c == 0)
    def _():
        for early in (True, False):
            for k in range(2):
                for j in range(12):

                    @pl.when((index_ref[12 * k + j] < 3) == early)
                    def _():
                        fetch(k, j).start()

        cot[...] = jnp.where(state_ref[0] > 0, cot_ref[...], jnp.zeros((), BF))
        total[...] = jnp.zeros(total.shape, F32)
        back[...] = jnp.zeros(back.shape, F32)
        fetched(range(3))
        wo = square(0)
        for b in blocks:
            h = x_ref[b, :].astype(F32) + dot(att_ref[b, :], wo)
            hidden[b, :] = h
            hat = h * lax.rsqrt(jnp.mean(h * h, axis=-1, keepdims=True) + norm_eps)
            low[b, :] = (hat * gain_ref[...]).astype(BF)

    for i, pieces in enumerate((range(3, 16), range(16, 19), range(19, 22), range(22, 24))):

        @pl.when(c == i)
        def _():
            fetched(pieces)

    up = weights[8:40, c].reshape(D, D)
    down = weights[pl.ds(40 + 8 * c, 8)].reshape(D, D)
    for b in blocks:
        act = jnp.maximum(dot(low[b, :], up), 0.0)
        s = (act * act).astype(BF)
        sq[b, :] = s
        total[b, :] += dot(s, down)
        g = (dot_nt(cot[b, :], down) * 2.0 * act).astype(BF)
        gb[b, :] = g
        back[b, :] += dot_nt(g, up)
    stage_down[c] = dot_tn(sq[...], cot[...]).reshape(8, 4, 24, D).astype(BF)
    stage_up[c] = dot_tn(low[...], gb[...]).reshape(32, 24, D).astype(BF)
    put_down(c)
    put_up(c)

    @pl.when(last)
    def _():
        gain = gain_ref[...]
        wo = square(0)
        sums = jnp.zeros((1, D), F32)
        for b in blocks:
            h = hidden[b, :]
            out_ref[b, :] = (h + total[b, :]).astype(BF)
            factor = lax.rsqrt(jnp.mean(h * h, axis=-1, keepdims=True) + norm_eps)
            hat = h * factor
            g = back[b, :]
            sums = sums + jnp.sum(g * hat, axis=0, keepdims=True)
            weighted = g * gain
            inner = jnp.mean(weighted * hat, axis=-1, keepdims=True)
            grad = cot[b, :].astype(F32) + factor * (weighted - hat * inner)
            gh_ref[b, :] = grad
            grad_low = grad.astype(BF)
            gb[b, :] = grad_low
            ga_ref[b, :] = dot_nt(grad_low, wo).astype(BF)
        gain_grad_ref[...] = sums
        stage_out[...] = dot_tn(att_ref[...], gb[...]).reshape(8, 4, 24, D).astype(BF)
        put_out()
        for i in range(4):
            put_down(i, True)
            put_up(i, True)
        put_out(True)


def ffn(state, index, tokens, attended, out_grad, gain, weights, rows):
    def whole(shape):
        return pl.BlockSpec(shape, lambda c: (0,) * len(shape), pipeline_mode=pl.Buffered(1))

    act = whole((rows, D))
    held = pl.BlockSpec(memory_space=pl.ANY)
    scalars = pl.BlockSpec(memory_space=pltpu.SMEM)
    half = (36, 4, 24, D)
    return pl.pallas_call(
        ffn_kernel,
        grid=(4,),
        in_specs=[scalars, scalars, act, act, act, whole((1, D)), held, held, held, held],
        out_specs=[act, act, act, whole((1, D)), held, held],
        out_shape=[
            jax.ShapeDtypeStruct((rows, D), BF),
            jax.ShapeDtypeStruct((rows, D), F32),
            jax.ShapeDtypeStruct((rows, D), BF),
            jax.ShapeDtypeStruct((1, D), F32),
            jax.ShapeDtypeStruct(half, BF),
            jax.ShapeDtypeStruct(half, BF),
        ],
        scratch_shapes=[
            pltpu.VMEM((rows, D), F32),
            pltpu.VMEM((rows, D), BF),
            pltpu.VMEM((rows, D), F32),
            pltpu.VMEM((rows, D), F32),
            pltpu.VMEM((rows, D), BF),
            pltpu.VMEM((rows, D), BF),
            pltpu.VMEM((rows, D), BF),
            pltpu.VMEM((72, 4, 24, D), BF),
            pltpu.VMEM((4, 32, 24, D), BF),
            pltpu.VMEM((4, 8, 4, 24, D), BF),
            pltpu.VMEM((8, 4, 24, D), BF),
            pltpu.SemaphoreType.DMA((24,)),
            pltpu.SemaphoreType.DMA((88,)),
        ],
        compiler_params=pltpu.CompilerParams(vmem_limit_bytes=60 << 20),
        cost_estimate=cost(2 * rows * D * D * (24 + 3), 2 * 12 * D * D * 2 + rows * D * 16),
        name="ffn",
    )(state, index, tokens, attended, out_grad, gain, *weights)


def shift_flat(block, distance):
    count = lax.axis_size(AXES)
    route = [(i - distance, i) for i in range(count) if 0 <= i - distance < count]
    return lax.ppermute(block, AXES, route)


def shift_ctx(block, distance):
    count = lax.axis_size("ctx")
    route = [(i - distance, i) for i in range(count) if 0 <= i - distance < count]
    return lax.ppermute(block, "ctx", route)


def after(value, *others):
    return lax.optimization_barrier((value, *others))[0]


def swap(block, even_bit, odd_bit, planes=None):
    count = lax.axis_size(AXES)
    route = [
        (i, i ^ (odd_bit if i & 1 else even_bit))
        for i in range(count)
        if planes is None or i >> 3 in planes
    ]
    return lax.ppermute(block, AXES, route)


def to_aligned(shard, place, count, delta):
    rows = shard.shape[0]
    lag = delta * (count - 1)
    back = -(-lag // rows)
    if back == 1:
        keep = -(-lag // 8) * 8
        parts = [shift_flat(shard[rows - keep :], 1), shard]
    else:
        keep = back * rows
        parts = [shift_flat(shard, s) for s in range(back, 0, -1)] + [shard]
    joined = jnp.concatenate(parts, 0)
    return lax.dynamic_slice_in_dim(joined, keep - delta * place, rows - delta, 0)


def small_part(shard, place, count, delta):
    rows = shard.shape[0]
    extra = count * delta
    zeros = jnp.zeros((extra, 128), shard.dtype)
    joined = jnp.concatenate([zeros, shard, zeros], 0)
    start = extra + count * (rows - delta) - place * rows
    return lax.dynamic_slice_in_dim(joined, jnp.minimum(start, rows + extra), extra, 0)


def from_aligned(chunk, small, place, count, delta, rows):
    aligned = rows - delta
    ahead = -(-(count * delta) // aligned)
    parts = [chunk]
    if ahead == 1:
        keep = small.shape[0]
        got = shift_flat(chunk[:keep], -1)
        parts.append(jnp.where(place == count - 1, small, got))
    else:
        pad = ahead * aligned - small.shape[0]
        tail = jnp.concatenate([small, jnp.zeros((pad, 128), small.dtype)], 0)
        for s in range(1, ahead + 1):
            got = shift_flat(chunk, -s)
            for e in range(s):
                piece = tail[e * aligned : (e + 1) * aligned]
                got = jnp.where(place == count - s + e, piece, got)
            parts.append(got)
    return lax.dynamic_slice_in_dim(jnp.concatenate(parts, 0), delta * place, rows, 0)


def regroup(block):
    return block.reshape(-1, 24, 4, D).transpose(0, 2, 1, 3)


def ungroup(block):
    return block.reshape(-1, 4, 24, D).transpose(0, 2, 1, 3)


def normalize(values, gain):
    factor = lax.rsqrt(jnp.mean(values * values, axis=-1, keepdims=True) + norm_eps)
    scaled = values * factor
    return (scaled, factor, scaled * gain)


def norm_back(grad_in, scaled, factor, gain):
    weighted = grad_in * gain
    inner_mean = jnp.mean(weighted * scaled, axis=-1, keepdims=True)
    return factor * (weighted - scaled * inner_mean)


def adam_update(master, moment_one, moment_two, gradient, step_count, row_start):
    row_index = row_start + jnp.arange(master.shape[0], dtype=jnp.int32)
    matrix_rows = (4 * D * D + 2 * D * FF) // 128
    out_first = 3 * D * D // 128
    out_last = 4 * D * D // 128
    is_matrix = (row_index < matrix_rows)[:, None]
    is_out = ((row_index >= out_first) & (row_index < out_last))[:, None]
    step_rate = jnp.where(is_matrix, jnp.where(is_out, 0.5, 0.1), 1.0)
    decay_rate = jnp.where(is_matrix, 0.1, 0.0)
    step_value = step_count[0].astype(jnp.float32)
    new_one = 0.9 * moment_one + 0.1 * gradient
    new_two = 0.999 * moment_two + 0.001 * gradient * gradient
    corr_first = 1.0 - jnp.power(0.9, step_value)
    corr_second = 1.0 - jnp.power(0.999, step_value)
    new_weights = master - step_rate * (
        new_one / corr_first / (jnp.sqrt(new_two / corr_second) + 1e-08) + decay_rate * master
    )
    return (new_weights, new_one, new_two)


def shards(tokens, out_grad, positions, master, first_moment, second_moment, step_count):
    rows = tokens.shape[0]
    assert rows == SEQ_MIN
    count = lax.axis_size(AXES)
    place = lax.axis_index(AXES).astype(jnp.int32)
    owned = master.shape[0]
    aligned = (4 * D * D + 2 * D * FF) // 128 // count
    delta = owned - aligned
    height = aligned * 128 // D
    staged = count == 32
    first_place = positions[0]
    state = jnp.where(first_place < 0, 0, jnp.where(first_place >= SEQ_MIN, 2, 1)).astype(jnp.int32)
    state_vec = state[None]

    chunk = to_aligned(master, place, count, delta).reshape(-1, D)
    if staged:
        group = 3 * place + jnp.arange(3, dtype=jnp.int32)
        in_up = ((group >= 32) & (group < 64))[:, None, None, None]
        chunk = jnp.where(in_up, regroup(chunk), chunk.reshape(3, 4, 24, D)).reshape(-1, D)
    chunk = chunk.astype(BF)
    small = lax.reduce_precision(small_part(master, place, count, delta), 8, 7)
    core = (place & 1)[None]
    x_bit = (place >> 1) & 1
    y_bit = (place >> 2) & 1
    even = (place & 1) == 0
    if staged:
        z = place >> 3
        mine = jnp.concatenate([chunk, small.astype(BF).reshape(-1, D)], 0)
        tokens_before = shift_ctx(after(tokens, mine), 1)
        far = swap(mine, 16, 16)
        near = swap(mine, 8, 8)
        tokens_both = jnp.concatenate([tokens_before, tokens], 0)
        both = swap(after(far, tokens_both), 8, 8)
        order = jnp.stack([z, z ^ 1, z ^ 2, z ^ 3]).astype(jnp.int32)
        mine, rest = arrange(order, (mine, near, far, both))
        mine = join(mine, swap(mine, 2, 4))
        mine = join(mine, swap(mine, 4, 2))
        across = swap(rest, 2, 4)
        got = swap(mine, 1, 1)
        index = []
        late_index = []
        for k in (0, 1):
            turn = even if k == 0 else jnp.logical_not(even)
            for j in range(4):
                near, far = j & 1, j >> 1
                x_of = x_bit ^ jnp.where(turn, near, far)
                y_of = y_bit ^ jnp.where(turn, far, near)
                piece = 4 * y_of + 2 * x_of + (core[0] ^ k)
                index.append(piece)
                late_index += [piece, piece + 8, piece + 16]
        index = jnp.stack(index).astype(jnp.int32)
        late_index = jnp.stack(late_index + [core[0]]).astype(jnp.int32)
        projected, small, in_weight = qkv_fwd(index, tokens_both, (mine, got), rows, 4)
    else:
        tokens_both = jnp.concatenate([shift_ctx(tokens, 1), tokens], 0)
        wide = lax.all_gather(chunk, AXES, axis=0, tiled=True)
        small = lax.psum(small, AXES)[:96].reshape(-1, D)
        in_weight = wide[: 3 * D]
        projected, small = qkv_fwd(core, tokens_both, (in_weight, small), rows, 0)
        late_index = jnp.arange(25, dtype=jnp.int32) % 24
    gain_first = small[0]
    gain_second = small[1]

    forward = []
    if staged:
        rest = join_held(after(rest, projected), across)
        line = swap(rest, 4, 2)
        core_rest = swap(rest, 1, 1)
        forward = att_fwd(after(state_vec, rest), projected, small, forward, FORWARD_PARTS[0], rows)
        forward = att_fwd(after(state_vec, core_rest), projected, small, forward, FORWARD_PARTS[1], rows)
        line = hold(line, forward[0])
        core_line = swap(line, 1, 1)
        forward = att_fwd(after(state_vec, line), projected, small, forward, FORWARD_PARTS[2], rows)
        late_weights = [w.reshape(18, 4, 24, D) for w in (rest, line, core_rest, core_line)]
    else:
        for part in FORWARD_PARTS:
            forward = att_fwd(state_vec, projected, small, forward, part, rows)
        grouped = jnp.concatenate(
            [
                wide[3 * D : 4 * D].reshape(-1, 4, 24, D),
                regroup(wide[4 * D : 8 * D]),
                wide[8 * D :].reshape(-1, 4, 24, D),
            ],
            0,
        )
        late_weights = [grouped[18 * k : 18 * k + 18] for k in range(4)]
    attn_low, logs, *mixed = forward

    layer_out, grad_hidden, grad_attended, grad_gain_two, away_grad, here_grad = ffn(
        state_vec, late_index, tokens, attn_low, out_grad, gain_second[None], late_weights, rows
    )

    def backward(start, done, part):
        return att_bwd(
            start, mixed, attn_low, logs, grad_attended, projected, small, done, BACKWARD_PARTS[part], rows
        )

    if staged:
        stay = [jnp.where(even, 2 * j + x_bit, 2 * y_bit + j) for j in range(2)]
        away = [jnp.where(even, 2 * j + 1 - x_bit, 2 * (1 - y_bit) + j) for j in range(2)]
        pick_plane = jnp.stack(away + stay).astype(jnp.int32)
        other = jnp.where(even, y_bit, x_bit)
        pick_line = jnp.stack([1 - other, other]).astype(jnp.int32)

        def of_quarters(pick, held):
            half = pick.shape[0] // 2
            steps = [pick[s * half + j] + held * t for s in range(2) for t in range(3) for j in range(half)]
            return jnp.stack(steps)

        late_keep = here_grad.reshape(12, height, D)
        late_got = swap(away_grad.reshape(12, height, D), 1, 1)
        done = backward(state_vec, [], 0)
        late_send, late_keep = merge_grid(
            after(of_quarters(pick_plane, 4), done[4]), late_keep, late_got, 6, BF
        )
        late_got = swap(late_send, 2, 4)
        done = backward(after(state_vec, late_send), done, 1)
        late_send, late_keep = merge_grid(
            after(of_quarters(pick_line, 2), done[4]), late_keep, late_got, 3
        )
        late_got = swap(late_send, 4, 2)
        done = backward(after(state_vec, late_send), done, 2)
        z_even = (z & 1) == 0
        low_pair = [jnp.where(z_even, 0, 0), jnp.where(z_even, 2, 1)]
        high_pair = [jnp.where(z_even, 0, 0), jnp.where(z_even, 1, 2)]
        pick_z = jnp.stack(low_pair + high_pair).astype(jnp.int32)
        late_send, late_keep = merge_grid(after(pick_z, done[4]), late_keep, late_got, 2)
        late_got = swap(late_send, 8, 8)
        done = backward(after(state_vec, late_send), done, 3)
        high = z >> 1
        pick_last = jnp.stack([1 - high, high]).astype(jnp.int32)
        late_send, late_keep = merge_grid(after(pick_last, done[4]), late_keep, late_got, 1)
        late_got = swap(late_send, 16, 16, (0, 1, 3))
        sums_state = after(core, late_send)
    else:
        done = []
        for part in range(4):
            done = backward(state_vec, done, part)
        sums_state = core
    *back, tap_grads = done
    grads_before, gain_one_grad = before_bwd(tokens_both, back, in_weight, rows)
    from_next = shift_ctx(grads_before, -1)
    sums = qkv_bwd(
        after(sums_state, grads_before), tokens_both, back, in_weight, gain_first[None], gain_one_grad, grad_gain_two, tap_grads, rows,
        4 if staged else 0,
    )
    grad_normed_one = sums[2]
    scaled_one, factor_one, _ = normalize(tokens.astype(F32), gain_first)
    input_grad = grad_hidden + norm_back(
        grad_normed_one + from_next.astype(F32), scaled_one, factor_one, gain_first
    )

    if staged:
        send, keep = sums[:2]
        got = swap(after(send, late_got, from_next), 1, 1)
        send, keep = merge(pick_plane, keep, got, height + 16, 2)
        got = swap(send, 2, 4)
        late_got = after(late_got, send)
        late_chunk = late_keep[0] + late_got[0].astype(F32)
        late_chunk = jnp.where(in_up, ungroup(late_chunk).reshape(3, 4, 24, D), late_chunk.reshape(3, 4, 24, D))
        late_chunk = late_chunk.reshape(-1, D)
        late_next = shift_flat(late_chunk[:16], -1)
        send, keep = merge(pick_line, keep, got, height + 16, 1)
        got = swap(send, 4, 2)
        send, keep = merge(after(core, late_next), keep, got, height + 16, 0)
        got = swap(send, 8, 8)
        send, keep = merge(after(core, input_grad), keep, got, height + 16, 0)
        got = swap(send, 16, 16, (1, 2))
        first = keep + got.astype(F32)
        quarter = count // 4
        follow = jnp.where(place < quarter - 1, first[height : height + 16], late_next)
        follow = jnp.where(place == count - 1, first[height + 16 :], follow)
        chunk_grad = jnp.where(place < quarter, first[:height], late_chunk)
        chunk_grad = jnp.concatenate([chunk_grad, follow], 0).reshape(-1, 128)
        gradient = lax.dynamic_slice_in_dim(chunk_grad, delta * place, owned, 0)
    else:
        flat_grad = jnp.stack([here_grad.reshape(12, 3, 4, 24, D), away_grad.reshape(12, 3, 4, 24, D)], 1)
        flat_grad = flat_grad.reshape(72, 4, 24, D)
        wide_grad = jnp.concatenate(
            [
                sums[0],
                flat_grad[:8].reshape(-1, D),
                ungroup(flat_grad[8:40]).reshape(-1, D),
                flat_grad[40:].reshape(-1, D),
            ],
            0,
        )
        chunk_grad = lax.psum_scatter(wide_grad, AXES, scatter_dimension=0, tiled=True).astype(F32)
        used = sums[1].reshape(-1, 128)
        extra = count * delta
        small_grad = jnp.concatenate([used, jnp.zeros((extra - used.shape[0], 128), F32)], 0)
        small_grad = lax.psum(small_grad, AXES)
        gradient = from_aligned(chunk_grad.reshape(-1, 128), small_grad, place, count, delta, owned)
    new_weights, new_one, new_two = adam_update(
        master, first_moment, second_moment, gradient, step_count, place * owned
    )
    return (layer_out, input_grad, new_weights, new_one, new_two, new_weights.astype(BF))


def solution(mesh):
    spread = P(AXES, None)
    return jax.shard_map(
        shards,
        mesh=mesh,
        in_specs=(spread, spread, P(AXES), spread, spread, spread, P()),
        out_specs=(spread,) * 6,
        check_vma=False,
    )
```

```python
import jax
import jax.numpy as jnp
from jax import lax
from jax.experimental import pallas as pl
from jax.experimental.pallas import tpu as pltpu
from jax.sharding import PartitionSpec as P

D = 768
HEADS = 12
HEAD_DIM = 64
FF = 3072
SEQ_MIN = 1024
AXES = ("dp", "ctx")
QB = 256
FORWARD_PARTS = ((0, 2), (2, 2), (4, 2))
BACKWARD_PARTS = ((0, 1), (1, 2), (3, 1), (4, 2))
F32 = jnp.float32
BF = jnp.bfloat16
NT = (((1,), (1,)), ((), ()))
TN = (((0,), (0,)), ((), ()))
norm_eps = 1e-06
VMEM_LIMIT = 56 << 20


def dot(left, right):
    return jnp.dot(left, right, preferred_element_type=F32)


def dot_nt(left, right):
    return lax.dot_general(left, right, NT, preferred_element_type=F32)


def dot_tn(left, right):
    return lax.dot_general(left, right, TN, preferred_element_type=F32)


def cost(flops, nbytes, exps=0):
    return pl.CostEstimate(flops=int(flops), bytes_accessed=int(nbytes), transcendentals=int(exps))


def taps_of(small, matrix):
    return [small[2 + 3 * j + matrix : 3 + 3 * j + matrix, :] for j in range(3)]


def row_ids(height):
    return lax.broadcasted_iota(jnp.int32, (height, 128), 0)


def conv(out_ref, x_ref, start, tail_ref, taps, rows, state):
    height = x_ref.shape[0]
    for r in range(0, height, QB):
        at = start + r
        if r:
            x = x_ref[r - 16 : r + QB, :].astype(F32)
        else:
            before = jnp.zeros((16, 128), F32)
            if tail_ref is not None:
                before = jnp.concatenate([before[8:], tail_ref[...].astype(F32)], 0)
            x = jnp.concatenate([before, x_ref[0:QB, :].astype(F32)], 0)
        one = pltpu.roll(x, 1, 0)[16:]
        two = pltpu.roll(x, 2, 0)[16:]
        x = x[16:]
        scale = 1.0
        if at >= rows:
            scale = jnp.where(state > 0, 1.0, 0.0)
        if at == 0 or at == rows:
            seen = jnp.where(state == 2, 1.0, 0.0) if at else 0.0
            row = row_ids(QB)
            one = jnp.where(row < 1, one * seen, one)
            two = jnp.where(row < 2, two * seen, two)
        c_one = taps[1] * scale
        c_two = taps[2] * scale
        out_ref[r : r + QB, :] = (taps[0] * x + c_one * one + c_two * two).astype(BF)


def att_fwd_kernel(
    state_ref, tail_ref, q_ref, k_ref, v_ref, small_ref,
    o_ref, l_ref, qm_ref, km_ref, vm_ref, ka, va,
):
    rows = q_ref.shape[0]
    lane = lax.broadcasted_iota(jnp.int32, (1, 128), 1)
    state = state_ref[0]
    conv(qm_ref, q_ref, rows, tail_ref, taps_of(small_ref[...], 0), rows, state)
    conv(km_ref, k_ref, 0, None, taps_of(small_ref[...], 1), rows, state)
    conv(vm_ref, v_ref, 0, None, taps_of(small_ref[...], 2), rows, state)
    bias = jnp.where(state == 2, 0.0, -1e30)
    for h in range(2):
        mine = (lane < 64) if h == 0 else (lane >= 64)
        base = 64 if h == 0 else 0
        first = jnp.where(lane == base, bias, 0.0).astype(BF)
        for r in range(0, 2 * rows, QB):
            at = pl.ds(r, QB)
            ka[h, at, :] = jnp.where(mine, km_ref[at, :], first if r < rows else jnp.zeros((), BF))
            va[h, at, :] = jnp.where(mine, vm_ref[at, :], jnp.ones((), BF))
    for i in range(rows // QB):
        rs = pl.ds(i * QB, QB)
        outs = []
        sums = []
        qf = qm_ref[rs, :].astype(F32) * 0.125
        for h in range(2):
            mine = (lane < 64) if h == 0 else (lane >= 64)
            base = 64 if h == 0 else 0
            qh = jnp.where(mine, qf, jnp.where(lane == base, 1.0, 0.0)).astype(BF)
            nk = rows + (i + 1) * QB
            s = dot_nt(qh, ka[h, 0:nk, :])
            r = lax.broadcasted_iota(jnp.int32, (QB, QB), 0)
            c = lax.broadcasted_iota(jnp.int32, (QB, QB), 1)
            sd = jnp.where(c <= r, s[:, nk - QB :], -1e30)
            se = s[:, : nk - QB]
            m = jnp.maximum(
                jnp.max(sd, axis=1, keepdims=True), jnp.max(se, axis=1, keepdims=True)
            )
            p = jnp.concatenate([jnp.exp(se - m).astype(BF), jnp.exp(sd - m).astype(BF)], 1)
            o = dot(p, va[h, 0:nk, :])
            outs.append(o / pltpu.roll(o, 64, 1))
            sums.append(m + jnp.log(o))
        res = jnp.where(lane < 64, outs[0], outs[1])
        res = jnp.where(state == 0, vm_ref[pl.ds(rows + i * QB, QB), :].astype(F32), res)
        o_ref[rs, :] = res.astype(BF)
        l_ref[rs, :] = jnp.where(lane < 64, sums[1], sums[0])


def call_in_parts(body, in_specs, out_specs, out_shape, earlier, part, **options):
    used = len(in_specs)

    def kernel(*refs):
        body(*refs[:used], *refs[used + len(earlier) :])

    return pl.pallas_call(
        kernel,
        grid=(part[1],),
        in_specs=in_specs + [pl.BlockSpec(memory_space=pl.ANY)] * len(earlier),
        out_specs=out_specs,
        out_shape=out_shape,
        input_output_aliases={used + i: i for i in range(len(earlier))},
        compiler_params=pltpu.CompilerParams(vmem_limit_bytes=VMEM_LIMIT),
        **options,
    )


def columns(part):
    first = part[0]

    def cols(height, row, off):
        return pl.BlockSpec((height, 128), lambda p: (row, p + first + off))

    return cols


def att_fwd(state, projected, small, earlier, part, rows):
    cols = columns(part)
    return call_in_parts(
        att_fwd_kernel,
        [
            pl.BlockSpec(memory_space=pltpu.SMEM),
            cols(8, rows // 8 - 1, 0),
            cols(rows, 1, 0),
            cols(2 * rows, 0, 6),
            cols(2 * rows, 0, 12),
            cols(16, 0, 0),
        ],
        [cols(rows, 0, 0)] * 3 + [cols(2 * rows, 0, 0)] * 2,
        [
            jax.ShapeDtypeStruct((rows, D), BF),
            jax.ShapeDtypeStruct((rows, D), F32),
            jax.ShapeDtypeStruct((rows, D), BF),
            jax.ShapeDtypeStruct((2 * rows, D), BF),
            jax.ShapeDtypeStruct((2 * rows, D), BF),
        ],
        earlier,
        part,
        scratch_shapes=[pltpu.VMEM((2, 2 * rows, 128), BF)] * 2,
        cost_estimate=cost(
            2 * 2 * 2 * rows * rows * 1.5 * 256 * part[1],
            rows * D * 5 * part[1],
            2 * rows * rows * 1.5 * part[1],
        ),
        name="att_fwd",
    )(state, projected, projected, projected, projected, small, *earlier)


def three(x, lane, base):
    hi = x.astype(BF).astype(F32)
    r = x - hi
    mid = r.astype(BF).astype(F32)
    lo = r - mid
    return jnp.where(
        lane == base, hi, jnp.where(lane == base + 1, mid, jnp.where(lane == base + 2, lo, 0.0))
    )


def conv_back(out_ref, grad_ref, x_ref, start, tail, taps, rows, state):
    height = grad_ref.shape[0]
    joint = jnp.where(state == 2, 1.0, 0.0)
    sums = [jnp.zeros((1, 128), F32)] * 3

    def add(parts, x):
        return [s + jnp.sum(g * x, axis=0, keepdims=True) for s, g in zip(sums, parts)]

    for r in range(0, height, QB):
        ends = r + QB == height
        meets = start + r + QB == rows
        if ends:
            grad = jnp.concatenate([grad_ref[r : r + QB, :], jnp.zeros((8, 128), F32)], 0)
        else:
            grad = grad_ref[r : r + QB + 8, :]
        one = pltpu.roll(grad, QB + 7, 0)[:QB]
        two = pltpu.roll(grad, QB + 6, 0)[:QB]
        grad = grad[:QB]
        if meets and not ends:
            row = row_ids(QB)
            one = jnp.where(row >= QB - 1, one * joint, one)
            two = jnp.where(row >= QB - 2, two * joint, two)
        out_ref[r : r + QB, :] = (taps[0] * grad + taps[1] * one + taps[2] * two).astype(BF)
        sums = add((grad, one, two), x_ref[r : r + QB, :].astype(F32))
    if tail is not None:
        grad = jnp.concatenate([jnp.zeros((8, 128), F32), grad_ref[0:8, :]], 0)
        one = pltpu.roll(grad, 15, 0)[:8] * joint
        two = pltpu.roll(grad, 14, 0)[:8] * joint
        tail[0][...] = (taps[1] * one + taps[2] * two).astype(BF)
        sums = add((grad[:8], one, two), tail[1][...].astype(F32))
    return sums


def att_bwd_kernel(
    state_ref, q_ref, k_ref, v_ref, o_ref, l_ref, do_ref, xt_ref, xq_ref, xk_ref, xv_ref,
    small_ref,
    pq_ref, pt_ref, pk_ref, pv_ref, tg_ref, qa, da, qt, dt, kt, dqt, dqs, dks, dvs,
):
    rows = q_ref.shape[0]
    lane = lax.broadcasted_iota(jnp.int32, (1, 128), 1)
    second = state_ref[0] == 2
    for r in range(0, rows, QB):
        at = pl.ds(r, QB)
        do = do_ref[at, :].astype(F32)
        od = do * o_ref[at, :].astype(F32)
        qf = q_ref[at, :].astype(F32) * 0.125
        lv = l_ref[at, :]
        for h in range(2):
            mine = (lane < 64) if h == 0 else (lane >= 64)
            base = 64 if h == 0 else 0
            delta = jnp.sum(jnp.where(mine, od, 0.0), axis=1, keepdims=True)
            qa[h, at, :] = jnp.where(mine, qf, three(-lv, lane, base)).astype(BF)
            da[h, at, :] = jnp.where(mine, do, three(-delta, lane, base)).astype(BF)
        qt[:, at] = jnp.transpose(qf).astype(BF)
        dt[:, at] = jnp.transpose(do).astype(BF)
    for r in range(0, 2 * rows, QB):
        at = pl.ds(r, QB)
        kt[:, at] = jnp.transpose(k_ref[at, :].astype(F32)).astype(BF)
    dqt[...] = jnp.zeros(dqt.shape, F32)

    def keys(ks, first, diagonal):
        kk = k_ref[ks, :]
        vv = v_ref[ks, :]
        dv = []
        dk = []
        for h in range(2):
            mine = (lane < 64) if h == 0 else (lane >= 64)
            base = 64 if h == 0 else 0
            ones3 = ((lane >= base) & (lane < base + 3)).astype(BF)
            hs = slice(64 * h, 64 * h + 64)
            st = dot_nt(jnp.where(mine, kk, ones3), qa[h, first:rows, :])
            dp = dot_nt(jnp.where(mine, vv, ones3), da[h, first:rows, :])
            p = jnp.exp(st)
            if diagonal:
                r = lax.broadcasted_iota(jnp.int32, (QB, QB), 0)
                c = lax.broadcasted_iota(jnp.int32, (QB, QB), 1)
                seen = jnp.where(r <= c, p[:, :QB], 0.0)
                p = jnp.concatenate([seen, p[:, QB:]], 1) if first + QB < rows else seen
            ds = (p * dp).astype(BF)
            dv.append(dot_nt(dt[hs, first:rows], p.astype(BF)))
            dk.append(dot_nt(qt[hs, first:rows], ds))
            dqt[hs, first:rows] += dot(kt[hs, ks], ds)
        dvs[ks, :] = jnp.transpose(jnp.concatenate(dv, 0))
        dks[ks, :] = jnp.transpose(jnp.concatenate(dk, 0))

    for j in range(rows // QB):
        keys(pl.ds(rows + j * QB, QB), j * QB, True)

    @pl.when(second)
    def _():
        def step(j, carry):
            keys(pl.ds(pl.multiple_of(j * QB, QB), QB), 0, False)
            return carry

        lax.fori_loop(0, rows // QB, step, 0)

    @pl.when(jnp.logical_not(second))
    def _():
        dks[0:rows, :] = jnp.zeros((rows, 128), F32)
        dvs[0:rows, :] = jnp.zeros((rows, 128), F32)

    for r in range(0, rows, QB):
        dqs[r : r + QB, :] = jnp.transpose(dqt[:, r : r + QB]) * 0.125
    state = state_ref[0]
    sq = conv_back(pq_ref, dqs, xq_ref, rows, (pt_ref, xt_ref), taps_of(small_ref[...], 0), rows, state)
    sk = conv_back(pk_ref, dks, xk_ref, 0, None, taps_of(small_ref[...], 1), rows, state)
    sv = conv_back(pv_ref, dvs, xv_ref, 0, None, taps_of(small_ref[...], 2), rows, state)
    tg_ref[...] = jnp.zeros(tg_ref.shape, F32)
    for j in range(3):
        for m, s in enumerate((sq, sk, sv)):
            tg_ref[3 * j + m : 3 * j + m + 1, :] = s[j]


def att_bwd(state, mixed, attended, logs, grad, projected, small, earlier, part, rows):
    cols = columns(part)
    own = cols(rows, 0, 0)
    both = cols(2 * rows, 0, 0)
    return call_in_parts(
        att_bwd_kernel,
        [
            pl.BlockSpec(memory_space=pltpu.SMEM),
            own, both, both, own, own, own,
            cols(8, rows // 8 - 1, 0),
            cols(rows, 1, 0),
            cols(2 * rows, 0, 6),
            cols(2 * rows, 0, 12),
            cols(16, 0, 0),
        ],
        [own, cols(8, 0, 0), both, both, cols(16, 0, 0)],
        [
            jax.ShapeDtypeStruct((rows, D), BF),
            jax.ShapeDtypeStruct((8, D), BF),
            jax.ShapeDtypeStruct((2 * rows, D), BF),
            jax.ShapeDtypeStruct((2 * rows, D), BF),
            jax.ShapeDtypeStruct((16, D), F32),
        ],
        earlier,
        part,
        scratch_shapes=[
            pltpu.VMEM((2, rows, 128), BF),
            pltpu.VMEM((2, rows, 128), BF),
            pltpu.VMEM((128, rows), BF),
            pltpu.VMEM((128, rows), BF),
            pltpu.VMEM((128, 2 * rows), BF),
            pltpu.VMEM((128, rows), F32),
            pltpu.VMEM((rows, 128), F32),
            pltpu.VMEM((2 * rows, 128), F32),
            pltpu.VMEM((2 * rows, 128), F32),
        ],
        cost_estimate=cost(
            5 * 2 * 2 * rows * rows * 1.5 * 256 * part[1],
            rows * D * 7 * part[1],
            2 * rows * rows * 1.5 * part[1],
        ),
        name="att_bwd",
    )(state, *mixed, attended, logs, grad, projected, projected, projected, projected,
      small, *earlier)


def unit_rows(x):
    return x * lax.rsqrt(jnp.mean(x * x, axis=-1, keepdims=True) + norm_eps)


def before_bwd_kernel(x_ref, dt_ref, dk_ref, dv_ref, w_ref, out_ref, gain_ref):
    i = pl.program_id(0)
    hat = unit_rows(x_ref[...].astype(F32))
    gn = dot_nt(dk_ref[...], w_ref[D : 2 * D, :]) + dot_nt(dv_ref[...], w_ref[2 * D : 3 * D, :])

    last_step = pl.num_programs(0) - 1

    @pl.when(i == 0)
    def _():
        gain_ref[...] = jnp.zeros(gain_ref.shape, F32)

    @pl.when(i < last_step)
    def _():
        out_ref[...] = gn.astype(BF)
        gain_ref[...] += jnp.sum(gn * hat, axis=0, keepdims=True)

    @pl.when(i == last_step)
    def _():
        last = gn.shape[0] - 8
        full = jnp.concatenate([gn[:last], gn[last:] + dot_nt(dt_ref[...], w_ref[0:D, :])], 0)
        out_ref[...] = full.astype(BF)
        gain_ref[...] += jnp.sum(full * hat, axis=0, keepdims=True)


def before_bwd(x_both, back, weight, rows):
    dt, dk, dv = back[1:]
    blocks = 4
    height = rows // blocks
    step = pl.BlockSpec((height, D), lambda i: (i, 0))

    def whole(shape):
        return pl.BlockSpec(shape, lambda i: (0, 0))

    return pl.pallas_call(
        before_bwd_kernel,
        grid=(blocks,),
        in_specs=[step, whole((8, D)), step, step, whole((3 * D, D))],
        out_specs=[step, whole((1, D))],
        out_shape=[jax.ShapeDtypeStruct((rows, D), BF), jax.ShapeDtypeStruct((1, D), F32)],
        compiler_params=pltpu.CompilerParams(vmem_limit_bytes=VMEM_LIMIT),
        cost_estimate=cost(2 * rows * D * D * 2, rows * D * 12),
        name="before_bwd",
    )(x_both, dt, dk, dv, weight)


def qkv_bwd_kernel(
    core_ref, x_ref, dq_ref, dt_ref, dk_ref, dv_ref, w_ref, small_ref, gain_one_ref, gain_two_ref, tg_ref,
    *refs, pieces, blocks,
):
    if pieces:
        send_ref, keep_ref, own_ref, acc, gacc = refs
    else:
        keep_ref, ends_ref, own_ref, acc, gacc = refs
    i = pl.program_id(0)
    half = blocks // 2

    @pl.when(i == 0)
    def _():
        acc[...] = jnp.zeros(acc.shape, F32)
        gacc[0:1, :] = gain_one_ref[...]

    hat = unit_rows(x_ref[...].astype(F32))
    low = (hat * small_ref[0:1, :]).astype(BF)
    dk = dk_ref[...]
    dv = dv_ref[...]
    acc[D : 2 * D, :] += dot_tn(low, dk)
    acc[2 * D : 3 * D, :] += dot_tn(low, dv)

    @pl.when(i == half - 1)
    def _():
        acc[0:D, :] += dot_tn(low[low.shape[0] - 8 :], dt_ref[...])

    @pl.when(i >= half)
    def _():
        dq = dq_ref[...]
        acc[0:D, :] += dot_tn(low, dq)
        full = (
            dot_nt(dk, w_ref[D : 2 * D, :])
            + dot_nt(dv, w_ref[2 * D : 3 * D, :])
            + dot_nt(dq, w_ref[0:D, :])
        )
        own_ref[...] = full
        gacc[0:1, :] += jnp.sum(full * hat, axis=0, keepdims=True)

    @pl.when(i == blocks - 1)
    def _():
        small = jnp.concatenate(
            [gacc[0:1, :], gain_two_ref[...], tg_ref[0:9, :], jnp.zeros((5, D), F32)], 0
        )
        if pieces:
            core = core_ref[0]
            height = 3 * D // (2 * pieces)
            wide = height + 16
            for j in range(pieces):
                to = pl.ds(j * wide, wide)
                away = pl.ds(pl.multiple_of((2 * j + 1 - core) * height, 16), wide)
                here = pl.ds(pl.multiple_of((2 * j + core) * height, 16), wide)
                send_ref[to, :] = acc[away, :].astype(BF)
                keep_ref[to, :] = acc[here, :]
            send_ref[pieces * wide :, :] = small.astype(BF)
            keep_ref[pieces * wide :, :] = small
        else:
            keep_ref[...] = acc[0 : 3 * D, :].astype(BF)
            ends_ref[...] = small


def qkv_bwd(core, x_both, back, weight, small, gain_one_grad, gain_two_grad, tap_grads, rows, pieces):
    dq, dt, dk, dv = back
    blocks = 4
    half = blocks // 2
    height = 2 * rows // blocks
    step = pl.BlockSpec((height, D), lambda i: (i, 0))
    late = pl.BlockSpec((height, D), lambda i: (jnp.maximum(i - half, 0), 0))

    def whole(shape):
        return pl.BlockSpec(shape, lambda i: (0, 0))

    if pieces:
        packed = 3 * D // 2 + 16 * pieces + 16
        outs = [jax.ShapeDtypeStruct((packed, D), BF), jax.ShapeDtypeStruct((packed, D), F32)]
        out_at = [whole((packed, D))] * 2
    else:
        outs = [jax.ShapeDtypeStruct((3 * D, D), BF), jax.ShapeDtypeStruct((16, D), F32)]
        out_at = [whole((3 * D, D)), whole((16, D))]

    def body(*refs):
        qkv_bwd_kernel(*refs, pieces=pieces, blocks=blocks)

    return pl.pallas_call(
        body,
        grid=(blocks,),
        in_specs=[
            pl.BlockSpec(memory_space=pltpu.SMEM),
            step, late, whole((8, D)), step, step, whole((3 * D, D)),
            whole((16, D)), whole((1, D)), whole((1, D)), whole((16, D)),
        ],
        out_specs=out_at + [late],
        out_shape=outs + [jax.ShapeDtypeStruct((rows, D), F32)],
        scratch_shapes=[pltpu.VMEM((3 * D + 16, D), F32), pltpu.VMEM((8, D), F32)],
        compiler_params=pltpu.CompilerParams(vmem_limit_bytes=VMEM_LIMIT),
        cost_estimate=cost(2 * 2 * D * D * 4 * rows, rows * D * 30),
        name="qkv_bwd",
    )(core, x_both, dq, dt, dk, dv, weight, small, gain_one_grad, gain_two_grad, tap_grads)


def merge(index, keep, got, height, taken):
    rows = keep.shape[0]
    out_rows = taken * height + 16 if taken else rows

    def body(index_ref, keep_ref, got_ref, send_ref, stay_ref):
        if not taken:
            total = keep_ref[...] + got_ref[...].astype(F32)
            send_ref[...] = total.astype(BF)
            stay_ref[...] = total
            return
        for j in range(taken):
            to = pl.ds(j * height, height)
            away = pl.ds(pl.multiple_of(index_ref[j] * height, 16), height)
            here = pl.ds(pl.multiple_of(index_ref[taken + j] * height, 16), height)
            send_ref[to, :] = (keep_ref[away, :] + got_ref[away, :].astype(F32)).astype(BF)
            stay_ref[to, :] = keep_ref[here, :] + got_ref[here, :].astype(F32)
        end = keep_ref[rows - 16 :, :] + got_ref[rows - 16 :, :].astype(F32)
        send_ref[taken * height :, :] = end.astype(BF)
        stay_ref[taken * height :, :] = end

    vmem = pl.BlockSpec(memory_space=pltpu.VMEM)
    return pl.pallas_call(
        body,
        in_specs=[pl.BlockSpec(memory_space=pltpu.SMEM), vmem, vmem],
        out_specs=[vmem, vmem],
        out_shape=[
            jax.ShapeDtypeStruct((out_rows, D), BF),
            jax.ShapeDtypeStruct((out_rows, D), F32),
        ],
        compiler_params=pltpu.CompilerParams(vmem_limit_bytes=32 << 20),
        cost_estimate=cost(rows * D, rows * D * 12),
        name="merge",
    )(index, keep, got)


def merge_grid(index, keep, got, taken, kept=F32):
    height = keep.shape[1]

    def body(index_ref, ka_ref, ga_ref, kb_ref, gb_ref, send_ref, stay_ref):
        send_ref[...] = (ka_ref[...].astype(F32) + ga_ref[...].astype(F32)).astype(BF)
        stay_ref[...] = (kb_ref[...].astype(F32) + gb_ref[...].astype(F32)).astype(kept)

    away = pl.BlockSpec((1, height, D), lambda i, index: (index[i], 0, 0))
    here = pl.BlockSpec((1, height, D), lambda i, index: (index[taken + i], 0, 0))
    step = pl.BlockSpec((1, height, D), lambda i, index: (i, 0, 0))
    return pl.pallas_call(
        body,
        grid_spec=pltpu.PrefetchScalarGridSpec(
            num_scalar_prefetch=1,
            grid=(taken,),
            in_specs=[away, away, here, here],
            out_specs=[step, step],
        ),
        out_shape=[
            pltpu.HBM((taken, height, D), BF),
            pltpu.HBM((taken, height, D), kept),
        ],
        compiler_params=pltpu.CompilerParams(vmem_limit_bytes=32 << 20),
        cost_estimate=cost(taken * height * D * 2, taken * height * D * 16),
        name="merge_grid",
    )(index, keep, got, keep, got)


def arrange(index, blocks):
    height = blocks[0].shape[0] - 16

    def body(index_ref, *refs):
        first_ref, rest_ref, ends, total, sems = refs[4:]
        refs = refs[:4]
        tail = pl.ds(height, 16)
        places = [first_ref.at[pl.ds(0, height)]] + [rest_ref.at[pl.ds(i * height, height)] for i in range(3)]
        for k in range(4):
            pltpu.make_async_copy(refs[k].at[tail], ends.at[k], sems.at[4 + k]).start()
        for i in range(4):
            for k in range(4):

                @pl.when(index_ref[i] == k)
                def _():
                    pltpu.make_async_copy(refs[k].at[pl.ds(0, height)], places[i], sems.at[i]).start()

        for k in range(4):
            pltpu.make_async_copy(refs[k].at[tail], ends.at[k], sems.at[4 + k]).wait()
        sums = [ends[k].astype(F32) for k in range(4)]
        total[...] = (sums[0] + sums[1] + sums[2] + sums[3]).astype(BF)
        last = pltpu.make_async_copy(total, first_ref.at[tail], sems.at[8])
        last.start()
        for i in range(4):
            pltpu.make_async_copy(refs[0].at[pl.ds(0, height)], places[i], sems.at[i]).wait()
        last.wait()

    held = pl.BlockSpec(memory_space=pltpu.HBM)
    return pl.pallas_call(
        body,
        in_specs=[pl.BlockSpec(memory_space=pltpu.SMEM)] + [held] * 4,
        out_specs=[held, held],
        out_shape=[
            jax.ShapeDtypeStruct((height + 16, D), BF),
            jax.ShapeDtypeStruct((3 * height, D), BF),
        ],
        scratch_shapes=[
            pltpu.VMEM((4, 16, D), BF),
            pltpu.VMEM((16, D), BF),
            pltpu.SemaphoreType.DMA((9,)),
        ],
        compiler_params=pltpu.CompilerParams(vmem_limit_bytes=32 << 20),
        cost_estimate=cost(4 * height * D, 4 * height * D * 4),
        name="arrange",
    )(index, *blocks)


def join(own, got, shared=16):
    rows = own.shape[0]
    body_rows = rows - shared

    def body(own_ref, got_ref, out_ref):
        out_ref[0:body_rows, :] = own_ref[0:body_rows, :]
        out_ref[body_rows : 2 * body_rows, :] = got_ref[0:body_rows, :]
        if shared:
            out_ref[2 * body_rows :, :] = own_ref[body_rows:, :] + got_ref[body_rows:, :]

    vmem = pl.BlockSpec(memory_space=pltpu.VMEM)
    return pl.pallas_call(
        body,
        in_specs=[vmem, vmem],
        out_specs=vmem,
        out_shape=jax.ShapeDtypeStruct((2 * body_rows + shared, D), BF),
        compiler_params=pltpu.CompilerParams(vmem_limit_bytes=32 << 20),
        cost_estimate=cost(rows * D, rows * D * 8),
        name="join",
    )(own, got)


def join_held(own, got):
    rows = own.shape[0]
    cuts = 4
    size = rows // cuts

    def body(own_ref, got_ref, out_ref, sems):
        copies = []
        for k, ref in enumerate((own_ref, got_ref)):
            for j in range(cuts):
                source = ref.at[pl.ds(j * size, size)]
                to = out_ref.at[pl.ds(k * rows + j * size, size)]
                copies.append(pltpu.make_async_copy(source, to, sems.at[k * cuts + j]))
        for copy in copies:
            copy.start()
        for copy in copies:
            copy.wait()

    held = pl.BlockSpec(memory_space=pltpu.HBM)
    return pl.pallas_call(
        body,
        in_specs=[held, held],
        out_specs=held,
        out_shape=jax.ShapeDtypeStruct((2 * rows, D), BF),
        scratch_shapes=[pltpu.SemaphoreType.DMA((2 * cuts,))],
        compiler_params=pltpu.CompilerParams(vmem_limit_bytes=16 << 20),
        cost_estimate=cost(0, rows * D * 8),
        name="join_held",
    )(own, got)


def hold(block, other):
    held = pl.BlockSpec(memory_space=pl.ANY)
    return pl.pallas_call(
        lambda block_ref, other_ref, out_ref: None,
        in_specs=[held, held],
        out_specs=held,
        out_shape=jax.ShapeDtypeStruct(block.shape, block.dtype),
        input_output_aliases={0: 0},
        name="hold",
    )(block, other)


def qkv_fwd_kernel(index_ref, x_ref, *refs, pieces, blocks):
    if pieces:
        own_ref, got_ref, out_ref, small_ref, weight = refs
    else:
        weight, given_ref, out_ref, small_ref = refs
    i = pl.program_id(0)

    @pl.when(i == 0)
    def _():
        if pieces:
            height = 3 * D // (2 * pieces)
            for j in range(pieces):
                at = pl.ds(j * height, height)
                for k, ref in enumerate((own_ref, got_ref)):
                    to = pl.multiple_of(index_ref[k * pieces + j] * height, 16)
                    weight[pl.ds(to, height), :] = ref[at, :]
            end = pl.ds(pieces * height, 16)
            small_ref[...] = own_ref[end, :].astype(F32) + got_ref[end, :].astype(F32)
        else:
            small_ref[...] = given_ref[...]

    x = x_ref[...].astype(F32)
    hat = x * lax.rsqrt(jnp.mean(x * x, axis=-1, keepdims=True) + norm_eps)
    low = (hat * small_ref[0:1, :]).astype(BF)

    @pl.when(i >= blocks // 2 - 1)
    def _():
        out_ref[:, 0:D] = dot(low, weight[0:D, :]).astype(BF)

    out_ref[:, D : 2 * D] = dot(low, weight[D : 2 * D, :]).astype(BF)
    out_ref[:, 2 * D : 3 * D] = dot(low, weight[2 * D : 3 * D, :]).astype(BF)


def qkv_fwd(index, x_both, weights, rows, pieces):
    blocks = 4
    height = 2 * rows // blocks

    def body(*refs):
        qkv_fwd_kernel(*refs, pieces=pieces, blocks=blocks)

    return pl.pallas_call(
        body,
        grid=(blocks,),
        in_specs=[
            pl.BlockSpec(memory_space=pltpu.SMEM),
            pl.BlockSpec((height, D), lambda i: (i, 0)),
            *[pl.BlockSpec(w.shape, lambda i: (0, 0)) for w in weights],
        ],
        out_specs=[
            pl.BlockSpec((height, 3 * D), lambda i: (i, 0)),
            pl.BlockSpec((16, D), lambda i: (0, 0)),
        ]
        + ([pl.BlockSpec((3 * D, D), lambda i: (0, 0))] if pieces else []),
        out_shape=[
            jax.ShapeDtypeStruct((2 * rows, 3 * D), BF),
            jax.ShapeDtypeStruct((16, D), F32),
        ]
        + ([jax.ShapeDtypeStruct((3 * D, D), BF)] if pieces else []),
        compiler_params=pltpu.CompilerParams(vmem_limit_bytes=VMEM_LIMIT),
        cost_estimate=cost(2 * 2 * rows * D * 3 * D, rows * D * 20),
        name="qkv_fwd",
    )(index, x_both, *weights)


def ffn_kernel(
    state_ref, index_ref, x_ref, att_ref, cot_ref, small_ref, own_ref, own_two_ref, got_ref, got_two_ref,
    out_ref, gh_ref, ga_ref, gain_grad_ref, away_ref, here_ref,
    hidden, low, total, back, cot, sq, gb, weights, stage_up, stage_down, stage_out, in_sems, sems,
):
    c = pl.program_id(0)
    rows = x_ref.shape[0]
    blocks = [pl.ds(i * QB, QB) for i in range(rows // QB)]
    last = c == pl.num_programs(0) - 1
    core = index_ref[24]

    def fetch(k, j):
        ref = ((own_ref, own_two_ref), (got_ref, got_two_ref))[k][j // 6]
        piece = index_ref[12 * k + j]
        to = weights.at[pl.ds(3 * piece, 3)]
        return pltpu.make_async_copy(ref.at[pl.ds(3 * (j % 6), 3)], to, in_sems.at[piece])

    def fetched(pieces):
        for piece in pieces:
            at = weights.at[pl.ds(3 * piece, 3)]
            pltpu.make_async_copy(own_ref.at[pl.ds(0, 3)], at, in_sems.at[piece]).wait()

    def put(source, group, count, column, sem, wait=False):
        piece = group // 3
        at = (piece // 2) * 3 + group % 3

        def copy(ref):
            to = ref.at[pl.ds(at, count)] if column is None else ref.at[pl.ds(at, count), column]
            return pltpu.make_async_copy(source, to, sems.at[sem])

        if wait:
            copy(here_ref).wait()
            return
        mine = piece % 2 == core

        @pl.when(mine)
        def _():
            copy(here_ref).start()

        @pl.when(jnp.logical_not(mine))
        def _():
            copy(away_ref).start()

    def put_up(i, wait=False):
        start = 0
        k = 0
        while start < 32:
            count = min(3 - (8 + start) % 3, 32 - start)
            put(stage_up.at[i, pl.ds(start, count)], 8 + start, count, i, 20 * i + k, wait)
            start += count
            k += 1

    def put_down(i, wait=False):
        for k in range(8):
            put(stage_down.at[i, pl.ds(k, 1)], 40 + 8 * i + k, 1, None, 20 * i + 12 + k, wait)

    def put_out(wait=False):
        for k in range(8):
            put(stage_out.at[pl.ds(k, 1)], k, 1, None, 80 + k, wait)

    def square(first):
        return weights[first : first + 8].reshape(D, D)

    @pl.when(c == 0)
    def _():
        for early in (True, False):
            for k in range(2):
                for j in range(12):

                    @pl.when((index_ref[12 * k + j] < 3) == early)
                    def _():
                        fetch(k, j).start()

        cot[...] = jnp.where(state_ref[0] > 0, cot_ref[...], jnp.zeros((), BF))
        total[...] = jnp.zeros(total.shape, F32)
        back[...] = jnp.zeros(back.shape, F32)
        fetched(range(3))
        wo = square(0)
        for b in blocks:
            h = x_ref[b, :].astype(F32) + dot(att_ref[b, :], wo)
            hidden[b, :] = h
            hat = h * lax.rsqrt(jnp.mean(h * h, axis=-1, keepdims=True) + norm_eps)
            low[b, :] = (hat * small_ref[1:2, :]).astype(BF)

    for i, pieces in enumerate((range(3, 16), range(16, 19), range(19, 22), range(22, 24))):

        @pl.when(c == i)
        def _():
            fetched(pieces)

    up = weights[8:40, c].reshape(D, D)
    down = weights[pl.ds(40 + 8 * c, 8)].reshape(D, D)
    for b in blocks:
        act = jnp.maximum(dot(low[b, :], up), 0.0)
        s = (act * act).astype(BF)
        sq[b, :] = s
        total[b, :] += dot(s, down)
        g = (dot_nt(cot[b, :], down) * 2.0 * act).astype(BF)
        gb[b, :] = g
        back[b, :] += dot_nt(g, up)
    stage_down[c] = dot_tn(sq[...], cot[...]).reshape(8, 4, 24, D).astype(BF)
    stage_up[c] = dot_tn(low[...], gb[...]).reshape(32, 24, D).astype(BF)
    put_down(c)
    put_up(c)

    @pl.when(last)
    def _():
        gain = small_ref[1:2, :]
        wo = square(0)
        sums = jnp.zeros((1, D), F32)
        for b in blocks:
            h = hidden[b, :]
            out_ref[b, :] = (h + total[b, :]).astype(BF)
            factor = lax.rsqrt(jnp.mean(h * h, axis=-1, keepdims=True) + norm_eps)
            hat = h * factor
            g = back[b, :]
            sums = sums + jnp.sum(g * hat, axis=0, keepdims=True)
            weighted = g * gain
            inner = jnp.mean(weighted * hat, axis=-1, keepdims=True)
            grad = cot[b, :].astype(F32) + factor * (weighted - hat * inner)
            gh_ref[b, :] = grad
            grad_low = grad.astype(BF)
            gb[b, :] = grad_low
            ga_ref[b, :] = dot_nt(grad_low, wo).astype(BF)
        gain_grad_ref[...] = sums
        stage_out[...] = dot_tn(att_ref[...], gb[...]).reshape(8, 4, 24, D).astype(BF)
        put_out()
        for i in range(4):
            put_down(i, True)
            put_up(i, True)
        put_out(True)


def ffn(state, index, tokens, attended, out_grad, small, weights, rows):
    def whole(shape):
        return pl.BlockSpec(shape, lambda c: (0,) * len(shape), pipeline_mode=pl.Buffered(1))

    act = whole((rows, D))
    held = pl.BlockSpec(memory_space=pl.ANY)
    scalars = pl.BlockSpec(memory_space=pltpu.SMEM)
    half = (36, 4, 24, D)
    return pl.pallas_call(
        ffn_kernel,
        grid=(4,),
        in_specs=[scalars, scalars, act, act, act, whole((16, D)), held, held, held, held],
        out_specs=[act, act, act, whole((1, D)), held, held],
        out_shape=[
            jax.ShapeDtypeStruct((rows, D), BF),
            jax.ShapeDtypeStruct((rows, D), F32),
            jax.ShapeDtypeStruct((rows, D), BF),
            jax.ShapeDtypeStruct((1, D), F32),
            jax.ShapeDtypeStruct(half, BF),
            jax.ShapeDtypeStruct(half, BF),
        ],
        scratch_shapes=[
            pltpu.VMEM((rows, D), F32),
            pltpu.VMEM((rows, D), BF),
            pltpu.VMEM((rows, D), F32),
            pltpu.VMEM((rows, D), F32),
            pltpu.VMEM((rows, D), BF),
            pltpu.VMEM((rows, D), BF),
            pltpu.VMEM((rows, D), BF),
            pltpu.VMEM((72, 4, 24, D), BF),
            pltpu.VMEM((4, 32, 24, D), BF),
            pltpu.VMEM((4, 8, 4, 24, D), BF),
            pltpu.VMEM((8, 4, 24, D), BF),
            pltpu.SemaphoreType.DMA((24,)),
            pltpu.SemaphoreType.DMA((88,)),
        ],
        compiler_params=pltpu.CompilerParams(vmem_limit_bytes=60 << 20),
        cost_estimate=cost(2 * rows * D * D * (24 + 3), 2 * 12 * D * D * 2 + rows * D * 16),
        name="ffn",
    )(state, index, tokens, attended, out_grad, small, *weights)


def shift_flat(block, distance):
    count = lax.axis_size(AXES)
    route = [(i - distance, i) for i in range(count) if 0 <= i - distance < count]
    return lax.ppermute(block, AXES, route)


def shift_ctx(block, distance):
    count = lax.axis_size("ctx")
    route = [(i - distance, i) for i in range(count) if 0 <= i - distance < count]
    return lax.ppermute(block, "ctx", route)


def after(value, *others):
    return lax.optimization_barrier((value, *others))[0]


def swap(block, even_bit, odd_bit, planes=None):
    count = lax.axis_size(AXES)
    route = [
        (i, i ^ (odd_bit if i & 1 else even_bit))
        for i in range(count)
        if planes is None or i >> 3 in planes
    ]
    return lax.ppermute(block, AXES, route)


def to_aligned(shard, place, count, delta):
    rows = shard.shape[0]
    lag = delta * (count - 1)
    back = -(-lag // rows)
    if back == 1:
        keep = -(-lag // 8) * 8
        parts = [shift_flat(shard[rows - keep :], 1), shard]
    else:
        keep = back * rows
        parts = [shift_flat(shard, s) for s in range(back, 0, -1)] + [shard]
    joined = jnp.concatenate(parts, 0)
    return lax.dynamic_slice_in_dim(joined, keep - delta * place, rows - delta, 0)


def small_part(shard, place, count, delta):
    rows = shard.shape[0]
    extra = count * delta
    zeros = jnp.zeros((extra, 128), shard.dtype)
    joined = jnp.concatenate([zeros, shard, zeros], 0)
    start = extra + count * (rows - delta) - place * rows
    return lax.dynamic_slice_in_dim(joined, jnp.minimum(start, rows + extra), extra, 0)


def from_aligned(chunk, small, place, count, delta, rows):
    aligned = rows - delta
    ahead = -(-(count * delta) // aligned)
    parts = [chunk]
    if ahead == 1:
        keep = small.shape[0]
        got = shift_flat(chunk[:keep], -1)
        parts.append(jnp.where(place == count - 1, small, got))
    else:
        pad = ahead * aligned - small.shape[0]
        tail = jnp.concatenate([small, jnp.zeros((pad, 128), small.dtype)], 0)
        for s in range(1, ahead + 1):
            got = shift_flat(chunk, -s)
            for e in range(s):
                piece = tail[e * aligned : (e + 1) * aligned]
                got = jnp.where(place == count - s + e, piece, got)
            parts.append(got)
    return lax.dynamic_slice_in_dim(jnp.concatenate(parts, 0), delta * place, rows, 0)


def regroup(block):
    return block.reshape(-1, 24, 4, D).transpose(0, 2, 1, 3)


def ungroup(block):
    return block.reshape(-1, 4, 24, D).transpose(0, 2, 1, 3)


def normalize(values, gain):
    factor = lax.rsqrt(jnp.mean(values * values, axis=-1, keepdims=True) + norm_eps)
    scaled = values * factor
    return (scaled, factor, scaled * gain)


def norm_back(grad_in, scaled, factor, gain):
    weighted = grad_in * gain
    inner_mean = jnp.mean(weighted * scaled, axis=-1, keepdims=True)
    return factor * (weighted - scaled * inner_mean)


def adam_update(master, moment_one, moment_two, gradient, step_count, row_start):
    row_index = row_start + jnp.arange(master.shape[0], dtype=jnp.int32)
    matrix_rows = (4 * D * D + 2 * D * FF) // 128
    out_first = 3 * D * D // 128
    out_last = 4 * D * D // 128
    is_matrix = (row_index < matrix_rows)[:, None]
    is_out = ((row_index >= out_first) & (row_index < out_last))[:, None]
    step_rate = jnp.where(is_matrix, jnp.where(is_out, 0.5, 0.1), 1.0)
    decay_rate = jnp.where(is_matrix, 0.1, 0.0)
    step_value = step_count[0].astype(jnp.float32)
    new_one = 0.9 * moment_one + 0.1 * gradient
    new_two = 0.999 * moment_two + 0.001 * gradient * gradient
    corr_first = 1.0 - jnp.power(0.9, step_value)
    corr_second = 1.0 - jnp.power(0.999, step_value)
    new_weights = master - step_rate * (
        new_one / corr_first / (jnp.sqrt(new_two / corr_second) + 1e-08) + decay_rate * master
    )
    return (new_weights, new_one, new_two)


def shards(tokens, out_grad, positions, master, first_moment, second_moment, step_count):
    rows = tokens.shape[0]
    assert rows == SEQ_MIN
    count = lax.axis_size(AXES)
    place = lax.axis_index(AXES).astype(jnp.int32)
    owned = master.shape[0]
    aligned = (4 * D * D + 2 * D * FF) // 128 // count
    delta = owned - aligned
    height = aligned * 128 // D
    staged = count == 32
    first_place = positions[0]
    state = jnp.where(first_place < 0, 0, jnp.where(first_place >= SEQ_MIN, 2, 1)).astype(jnp.int32)
    state_vec = state[None]

    chunk = to_aligned(master, place, count, delta).reshape(-1, D)
    if staged:
        group = 3 * place + jnp.arange(3, dtype=jnp.int32)
        in_up = ((group >= 32) & (group < 64))[:, None, None, None]
        chunk = jnp.where(in_up, regroup(chunk), chunk.reshape(3, 4, 24, D)).reshape(-1, D)
    chunk = chunk.astype(BF)
    if staged:
        small = jnp.where(place == count - 1, master[owned - count * delta :], 0.0)
    else:
        small = small_part(master, place, count, delta)
    small = lax.reduce_precision(small, 8, 7)
    core = (place & 1)[None]
    x_bit = (place >> 1) & 1
    y_bit = (place >> 2) & 1
    even = (place & 1) == 0
    if staged:
        z = place >> 3
        mine = jnp.concatenate([chunk, small.astype(BF).reshape(-1, D)], 0)
        tokens_before = shift_ctx(after(tokens, mine), 1)
        far = swap(mine, 16, 16)
        near = swap(mine, 8, 8)
        tokens_both = jnp.concatenate([tokens_before, tokens], 0)
        both = swap(after(far, tokens_both), 8, 8)
        order = jnp.stack([z, z ^ 1, z ^ 2, z ^ 3]).astype(jnp.int32)
        mine, rest = arrange(after(order, state_vec), (mine, near, far, both))
        mine = join(mine, swap(mine, 2, 4))
        mine = join(mine, swap(mine, 4, 2))
        across = swap(rest, 2, 4)
        got = swap(mine, 1, 1)
        index = []
        late_index = []
        for k in (0, 1):
            turn = even if k == 0 else jnp.logical_not(even)
            for j in range(4):
                near, far = j & 1, j >> 1
                x_of = x_bit ^ jnp.where(turn, near, far)
                y_of = y_bit ^ jnp.where(turn, far, near)
                piece = 4 * y_of + 2 * x_of + (core[0] ^ k)
                index.append(piece)
                late_index += [piece, piece + 8, piece + 16]
        index = jnp.stack(index).astype(jnp.int32)
        late_index = jnp.stack(late_index + [core[0]]).astype(jnp.int32)
        projected, small, in_weight = qkv_fwd(index, tokens_both, (mine, got), rows, 4)
    else:
        tokens_both = jnp.concatenate([shift_ctx(tokens, 1), tokens], 0)
        wide = lax.all_gather(chunk, AXES, axis=0, tiled=True)
        small = lax.psum(small, AXES)[:96].reshape(-1, D)
        in_weight = wide[: 3 * D]
        projected, small = qkv_fwd(core, tokens_both, (in_weight, small), rows, 0)
        late_index = jnp.arange(25, dtype=jnp.int32) % 24
    gain_first = small[0]

    forward = []
    if staged:
        rest = join_held(after(rest, projected), across)
        line = swap(rest, 4, 2)
        core_rest = swap(rest, 1, 1)
        forward = att_fwd(after(state_vec, rest), projected, small, forward, FORWARD_PARTS[0], rows)
        forward = att_fwd(after(state_vec, core_rest), projected, small, forward, FORWARD_PARTS[1], rows)
        line = hold(line, forward[0])
        core_line = swap(line, 1, 1)
        forward = att_fwd(after(state_vec, line), projected, small, forward, FORWARD_PARTS[2], rows)
        late_weights = [w.reshape(18, 4, 24, D) for w in (rest, line, core_rest, core_line)]
    else:
        for part in FORWARD_PARTS:
            forward = att_fwd(state_vec, projected, small, forward, part, rows)
        grouped = jnp.concatenate(
            [
                wide[3 * D : 4 * D].reshape(-1, 4, 24, D),
                regroup(wide[4 * D : 8 * D]),
                wide[8 * D :].reshape(-1, 4, 24, D),
            ],
            0,
        )
        late_weights = [grouped[18 * k : 18 * k + 18] for k in range(4)]
    attn_low, logs, *mixed = forward

    layer_out, grad_hidden, grad_attended, grad_gain_two, away_grad, here_grad = ffn(
        state_vec, late_index, tokens, attn_low, out_grad, small, late_weights, rows
    )

    def backward(start, done, part):
        return att_bwd(
            start, mixed, attn_low, logs, grad_attended, projected, small, done, BACKWARD_PARTS[part], rows
        )

    if staged:
        stay = [jnp.where(even, 2 * j + x_bit, 2 * y_bit + j) for j in range(2)]
        away = [jnp.where(even, 2 * j + 1 - x_bit, 2 * (1 - y_bit) + j) for j in range(2)]
        pick_plane = jnp.stack(away + stay).astype(jnp.int32)
        other = jnp.where(even, y_bit, x_bit)
        pick_line = jnp.stack([1 - other, other]).astype(jnp.int32)

        def of_quarters(pick, held):
            half = pick.shape[0] // 2
            steps = [pick[s * half + j] + held * t for s in range(2) for t in range(3) for j in range(half)]
            return jnp.stack(steps)

        late_keep = here_grad.reshape(12, height, D)
        late_got = swap(away_grad.reshape(12, height, D), 1, 1)
        done = backward(state_vec, [], 0)
        late_send, late_keep = merge_grid(
            after(of_quarters(pick_plane, 4), done[4]), late_keep, late_got, 6, BF
        )
        late_got = swap(late_send, 2, 4)
        done = backward(after(state_vec, late_send), done, 1)
        late_send, late_keep = merge_grid(
            after(of_quarters(pick_line, 2), done[4]), late_keep, late_got, 3
        )
        late_got = swap(late_send, 4, 2)
        done = backward(after(state_vec, late_send), done, 2)
        z_even = (z & 1) == 0
        low_pair = [jnp.where(z_even, 0, 0), jnp.where(z_even, 2, 1)]
        high_pair = [jnp.where(z_even, 0, 0), jnp.where(z_even, 1, 2)]
        pick_z = jnp.stack(low_pair + high_pair).astype(jnp.int32)
        late_send, late_keep = merge_grid(after(pick_z, done[4]), late_keep, late_got, 2)
        late_got = swap(late_send, 8, 8)
        done = backward(after(state_vec, late_send), done, 3)
        high = z >> 1
        pick_last = jnp.stack([1 - high, high]).astype(jnp.int32)
        late_send, late_keep = merge_grid(after(pick_last, done[4]), late_keep, late_got, 1)
        late_got = swap(late_send, 16, 16, (0, 1, 3))
        sums_state = after(core, late_send)
    else:
        done = []
        for part in range(4):
            done = backward(state_vec, done, part)
        sums_state = core
    *back, tap_grads = done
    grads_before, gain_one_grad = before_bwd(tokens_both, back, in_weight, rows)
    from_next = shift_ctx(grads_before, -1)
    sums = qkv_bwd(
        after(sums_state, grads_before), tokens_both, back, in_weight, small, gain_one_grad, grad_gain_two, tap_grads, rows,
        4 if staged else 0,
    )
    grad_normed_one = sums[2]
    scaled_one, factor_one, _ = normalize(tokens.astype(F32), gain_first)
    input_grad = grad_hidden + norm_back(
        grad_normed_one + from_next.astype(F32), scaled_one, factor_one, gain_first
    )

    if staged:
        send, keep = sums[:2]
        got = swap(after(send, late_got, from_next), 1, 1)
        send, keep = merge(pick_plane, keep, got, height + 16, 2)
        got = swap(send, 2, 4)
        late_got = after(late_got, send)
        late_chunk = late_keep[0] + late_got[0].astype(F32)
        late_chunk = jnp.where(in_up, ungroup(late_chunk).reshape(3, 4, 24, D), late_chunk.reshape(3, 4, 24, D))
        late_chunk = late_chunk.reshape(-1, D)
        late_next = shift_flat(late_chunk[:16], -1)
        send, keep = merge(pick_line, keep, got, height + 16, 1)
        got = swap(send, 4, 2)
        send, keep = merge(core, keep, got, height + 16, 0)
        got = swap(send, 8, 8)
        send, keep = merge(after(core, input_grad, late_next), keep, got, height + 16, 0)
        got = swap(send, 16, 16, (1, 2))
        first = keep + got.astype(F32)
        quarter = count // 4
        follow = jnp.where(place < quarter - 1, first[height : height + 16], late_next)
        follow = jnp.where(place == count - 1, first[height + 16 :], follow)
        chunk_grad = jnp.where(place < quarter, first[:height], late_chunk)
        chunk_grad = jnp.concatenate([chunk_grad, follow], 0).reshape(-1, 128)
        gradient = lax.dynamic_slice_in_dim(chunk_grad, delta * place, owned, 0)
    else:
        flat_grad = jnp.stack([here_grad.reshape(12, 3, 4, 24, D), away_grad.reshape(12, 3, 4, 24, D)], 1)
        flat_grad = flat_grad.reshape(72, 4, 24, D)
        wide_grad = jnp.concatenate(
            [
                sums[0],
                flat_grad[:8].reshape(-1, D),
                ungroup(flat_grad[8:40]).reshape(-1, D),
                flat_grad[40:].reshape(-1, D),
            ],
            0,
        )
        chunk_grad = lax.psum_scatter(wide_grad, AXES, scatter_dimension=0, tiled=True).astype(F32)
        used = sums[1].reshape(-1, 128)
        extra = count * delta
        small_grad = jnp.concatenate([used, jnp.zeros((extra - used.shape[0], 128), F32)], 0)
        small_grad = lax.psum(small_grad, AXES)
        gradient = from_aligned(chunk_grad.reshape(-1, 128), small_grad, place, count, delta, owned)
    new_weights, new_one, new_two = adam_update(
        master, first_moment, second_moment, gradient, step_count, place * owned
    )
    return (layer_out, input_grad, new_weights, new_one, new_two, new_weights.astype(BF))


def solution(mesh):
    spread = P(AXES, None)
    return jax.shard_map(
        shards,
        mesh=mesh,
        in_specs=(spread, spread, P(AXES), spread, spread, spread, P()),
        out_specs=(spread,) * 6,
        check_vma=False,
    )
```

```python
import jax
import jax.numpy as jnp
from jax import lax
from jax.experimental import pallas as pl
from jax.experimental.pallas import tpu as pltpu
from jax.sharding import PartitionSpec as P

D = 768
HEADS = 12
HEAD_DIM = 64
FF = 3072
SEQ_MIN = 1024
AXES = ("dp", "ctx")
QB = 256
FORWARD_PARTS = ((0, 2), (2, 2), (4, 2))
BACKWARD_PARTS = ((0, 1), (1, 2), (3, 1), (4, 2))
F32 = jnp.float32
BF = jnp.bfloat16
NT = (((1,), (1,)), ((), ()))
TN = (((0,), (0,)), ((), ()))
norm_eps = 1e-06
VMEM_LIMIT = 56 << 20


def dot(left, right):
    return jnp.dot(left, right, preferred_element_type=F32)


def dot_nt(left, right):
    return lax.dot_general(left, right, NT, preferred_element_type=F32)


def dot_tn(left, right):
    return lax.dot_general(left, right, TN, preferred_element_type=F32)


def cost(flops, nbytes, exps=0):
    return pl.CostEstimate(flops=int(flops), bytes_accessed=int(nbytes), transcendentals=int(exps))


def taps_of(small, matrix):
    return [small[2 + 3 * j + matrix : 3 + 3 * j + matrix, :] for j in range(3)]


def row_ids(height):
    return lax.broadcasted_iota(jnp.int32, (height, 128), 0)


def conv(out_ref, x_ref, start, tail_ref, taps, rows, state):
    height = x_ref.shape[0]
    for r in range(0, height, QB):
        at = start + r
        if r:
            x = x_ref[r - 16 : r + QB, :].astype(F32)
        else:
            before = jnp.zeros((16, 128), F32)
            if tail_ref is not None:
                before = jnp.concatenate([before[8:], tail_ref[...].astype(F32)], 0)
            x = jnp.concatenate([before, x_ref[0:QB, :].astype(F32)], 0)
        one = pltpu.roll(x, 1, 0)[16:]
        two = pltpu.roll(x, 2, 0)[16:]
        x = x[16:]
        scale = 1.0
        if at >= rows:
            scale = jnp.where(state > 0, 1.0, 0.0)
        if at == 0 or at == rows:
            seen = jnp.where(state == 2, 1.0, 0.0) if at else 0.0
            row = row_ids(QB)
            one = jnp.where(row < 1, one * seen, one)
            two = jnp.where(row < 2, two * seen, two)
        c_one = taps[1] * scale
        c_two = taps[2] * scale
        out_ref[r : r + QB, :] = (taps[0] * x + c_one * one + c_two * two).astype(BF)


def att_fwd_kernel(
    state_ref, tail_ref, q_ref, k_ref, v_ref, small_ref,
    o_ref, l_ref, qm_ref, km_ref, vm_ref, ka, va,
):
    rows = q_ref.shape[0]
    lane = lax.broadcasted_iota(jnp.int32, (1, 128), 1)
    state = state_ref[0]
    conv(qm_ref, q_ref, rows, tail_ref, taps_of(small_ref[...], 0), rows, state)
    conv(km_ref, k_ref, 0, None, taps_of(small_ref[...], 1), rows, state)
    conv(vm_ref, v_ref, 0, None, taps_of(small_ref[...], 2), rows, state)
    bias = jnp.where(state == 2, 0.0, -1e30)
    for h in range(2):
        mine = (lane < 64) if h == 0 else (lane >= 64)
        base = 64 if h == 0 else 0
        first = jnp.where(lane == base, bias, 0.0).astype(BF)
        for r in range(0, 2 * rows, QB):
            at = pl.ds(r, QB)
            ka[h, at, :] = jnp.where(mine, km_ref[at, :], first if r < rows else jnp.zeros((), BF))
            va[h, at, :] = jnp.where(mine, vm_ref[at, :], jnp.ones((), BF))
    for i in range(rows // QB):
        rs = pl.ds(i * QB, QB)
        outs = []
        sums = []
        qf = qm_ref[rs, :].astype(F32) * 0.125
        for h in range(2):
            mine = (lane < 64) if h == 0 else (lane >= 64)
            base = 64 if h == 0 else 0
            qh = jnp.where(mine, qf, jnp.where(lane == base, 1.0, 0.0)).astype(BF)
            nk = rows + (i + 1) * QB
            s = dot_nt(qh, ka[h, 0:nk, :])
            r = lax.broadcasted_iota(jnp.int32, (QB, QB), 0)
            c = lax.broadcasted_iota(jnp.int32, (QB, QB), 1)
            sd = jnp.where(c <= r, s[:, nk - QB :], -1e30)
            se = s[:, : nk - QB]
            m = jnp.maximum(
                jnp.max(sd, axis=1, keepdims=True), jnp.max(se, axis=1, keepdims=True)
            )
            p = jnp.concatenate([jnp.exp(se - m).astype(BF), jnp.exp(sd - m).astype(BF)], 1)
            o = dot(p, va[h, 0:nk, :])
            outs.append(o / pltpu.roll(o, 64, 1))
            sums.append(m + jnp.log(o))
        res = jnp.where(lane < 64, outs[0], outs[1])
        res = jnp.where(state == 0, vm_ref[pl.ds(rows + i * QB, QB), :].astype(F32), res)
        o_ref[rs, :] = res.astype(BF)
        l_ref[rs, :] = jnp.where(lane < 64, sums[1], sums[0])


def call_in_parts(body, in_specs, out_specs, out_shape, earlier, part, **options):
    used = len(in_specs)

    def kernel(*refs):
        body(*refs[:used], *refs[used + len(earlier) :])

    return pl.pallas_call(
        kernel,
        grid=(part[1],),
        in_specs=in_specs + [pl.BlockSpec(memory_space=pl.ANY)] * len(earlier),
        out_specs=out_specs,
        out_shape=out_shape,
        input_output_aliases={used + i: i for i in range(len(earlier))},
        compiler_params=pltpu.CompilerParams(vmem_limit_bytes=VMEM_LIMIT),
        **options,
    )


def columns(part):
    first = part[0]

    def cols(height, row, off):
        return pl.BlockSpec((height, 128), lambda p: (row, p + first + off))

    return cols


def att_fwd(state, projected, small, earlier, part, rows):
    cols = columns(part)
    return call_in_parts(
        att_fwd_kernel,
        [
            pl.BlockSpec(memory_space=pltpu.SMEM),
            cols(8, rows // 8 - 1, 0),
            cols(rows, 1, 0),
            cols(2 * rows, 0, 6),
            cols(2 * rows, 0, 12),
            cols(16, 0, 0),
        ],
        [cols(rows, 0, 0)] * 3 + [cols(2 * rows, 0, 0)] * 2,
        [
            jax.ShapeDtypeStruct((rows, D), BF),
            jax.ShapeDtypeStruct((rows, D), F32),
            jax.ShapeDtypeStruct((rows, D), BF),
            jax.ShapeDtypeStruct((2 * rows, D), BF),
            jax.ShapeDtypeStruct((2 * rows, D), BF),
        ],
        earlier,
        part,
        scratch_shapes=[pltpu.VMEM((2, 2 * rows, 128), BF)] * 2,
        cost_estimate=cost(
            2 * 2 * 2 * rows * rows * 1.5 * 256 * part[1],
            rows * D * 5 * part[1],
            2 * rows * rows * 1.5 * part[1],
        ),
        name="att_fwd",
    )(state, projected, projected, projected, projected, small, *earlier)


def three(x, lane, base):
    hi = x.astype(BF).astype(F32)
    r = x - hi
    mid = r.astype(BF).astype(F32)
    lo = r - mid
    return jnp.where(
        lane == base, hi, jnp.where(lane == base + 1, mid, jnp.where(lane == base + 2, lo, 0.0))
    )


def conv_back(out_ref, grad_ref, x_ref, start, tail, taps, rows, state):
    height = grad_ref.shape[0]
    joint = jnp.where(state == 2, 1.0, 0.0)
    sums = [jnp.zeros((1, 128), F32)] * 3

    def add(parts, x):
        return [s + jnp.sum(g * x, axis=0, keepdims=True) for s, g in zip(sums, parts)]

    for r in range(0, height, QB):
        ends = r + QB == height
        meets = start + r + QB == rows
        if ends:
            grad = jnp.concatenate([grad_ref[r : r + QB, :], jnp.zeros((8, 128), F32)], 0)
        else:
            grad = grad_ref[r : r + QB + 8, :]
        one = pltpu.roll(grad, QB + 7, 0)[:QB]
        two = pltpu.roll(grad, QB + 6, 0)[:QB]
        grad = grad[:QB]
        if meets and not ends:
            row = row_ids(QB)
            one = jnp.where(row >= QB - 1, one * joint, one)
            two = jnp.where(row >= QB - 2, two * joint, two)
        out_ref[r : r + QB, :] = (taps[0] * grad + taps[1] * one + taps[2] * two).astype(BF)
        sums = add((grad, one, two), x_ref[r : r + QB, :].astype(F32))
    if tail is not None:
        grad = jnp.concatenate([jnp.zeros((8, 128), F32), grad_ref[0:8, :]], 0)
        one = pltpu.roll(grad, 15, 0)[:8] * joint
        two = pltpu.roll(grad, 14, 0)[:8] * joint
        tail[0][...] = (taps[1] * one + taps[2] * two).astype(BF)
        sums = add((grad[:8], one, two), tail[1][...].astype(F32))
    return sums


def att_bwd_kernel(
    state_ref, q_ref, k_ref, v_ref, o_ref, l_ref, do_ref, xt_ref, xq_ref, xk_ref, xv_ref,
    small_ref,
    pq_ref, pt_ref, pk_ref, pv_ref, tg_ref, qa, da, qt, dt, kt, dqt, dqs, dks, dvs,
):
    rows = q_ref.shape[0]
    lane = lax.broadcasted_iota(jnp.int32, (1, 128), 1)
    second = state_ref[0] == 2
    for r in range(0, rows, QB):
        at = pl.ds(r, QB)
        do = do_ref[at, :].astype(F32)
        od = do * o_ref[at, :].astype(F32)
        qf = q_ref[at, :].astype(F32) * 0.125
        lv = l_ref[at, :]
        for h in range(2):
            mine = (lane < 64) if h == 0 else (lane >= 64)
            base = 64 if h == 0 else 0
            delta = jnp.sum(jnp.where(mine, od, 0.0), axis=1, keepdims=True)
            qa[h, at, :] = jnp.where(mine, qf, three(-lv, lane, base)).astype(BF)
            da[h, at, :] = jnp.where(mine, do, three(-delta, lane, base)).astype(BF)
        qt[:, at] = jnp.transpose(qf).astype(BF)
        dt[:, at] = jnp.transpose(do).astype(BF)
    for r in range(0, 2 * rows, QB):
        at = pl.ds(r, QB)
        kt[:, at] = jnp.transpose(k_ref[at, :].astype(F32)).astype(BF)
    dqt[...] = jnp.zeros(dqt.shape, F32)

    def keys(ks, first, diagonal):
        kk = k_ref[ks, :]
        vv = v_ref[ks, :]
        dv = []
        dk = []
        for h in range(2):
            mine = (lane < 64) if h == 0 else (lane >= 64)
            base = 64 if h == 0 else 0
            ones3 = ((lane >= base) & (lane < base + 3)).astype(BF)
            hs = slice(64 * h, 64 * h + 64)
            st = dot_nt(jnp.where(mine, kk, ones3), qa[h, first:rows, :])
            dp = dot_nt(jnp.where(mine, vv, ones3), da[h, first:rows, :])
            p = jnp.exp(st)
            if diagonal:
                r = lax.broadcasted_iota(jnp.int32, (QB, QB), 0)
                c = lax.broadcasted_iota(jnp.int32, (QB, QB), 1)
                seen = jnp.where(r <= c, p[:, :QB], 0.0)
                p = jnp.concatenate([seen, p[:, QB:]], 1) if first + QB < rows else seen
            ds = (p * dp).astype(BF)
            dv.append(dot_nt(dt[hs, first:rows], p.astype(BF)))
            dk.append(dot_nt(qt[hs, first:rows], ds))
            dqt[hs, first:rows] += dot(kt[hs, ks], ds)
        dvs[ks, :] = jnp.transpose(jnp.concatenate(dv, 0))
        dks[ks, :] = jnp.transpose(jnp.concatenate(dk, 0))

    for j in range(rows // QB):
        keys(pl.ds(rows + j * QB, QB), j * QB, True)

    @pl.when(second)
    def _():
        def step(j, carry):
            keys(pl.ds(pl.multiple_of(j * QB, QB), QB), 0, False)
            return carry

        lax.fori_loop(0, rows // QB, step, 0)

    @pl.when(jnp.logical_not(second))
    def _():
        dks[0:rows, :] = jnp.zeros((rows, 128), F32)
        dvs[0:rows, :] = jnp.zeros((rows, 128), F32)

    for r in range(0, rows, QB):
        dqs[r : r + QB, :] = jnp.transpose(dqt[:, r : r + QB]) * 0.125
    state = state_ref[0]
    sq = conv_back(pq_ref, dqs, xq_ref, rows, (pt_ref, xt_ref), taps_of(small_ref[...], 0), rows, state)
    sk = conv_back(pk_ref, dks, xk_ref, 0, None, taps_of(small_ref[...], 1), rows, state)
    sv = conv_back(pv_ref, dvs, xv_ref, 0, None, taps_of(small_ref[...], 2), rows, state)
    tg_ref[...] = jnp.zeros(tg_ref.shape, F32)
    for j in range(3):
        for m, s in enumerate((sq, sk, sv)):
            tg_ref[3 * j + m : 3 * j + m + 1, :] = s[j]


def att_bwd(state, mixed, attended, logs, grad, projected, small, earlier, part, rows):
    cols = columns(part)
    own = cols(rows, 0, 0)
    both = cols(2 * rows, 0, 0)
    return call_in_parts(
        att_bwd_kernel,
        [
            pl.BlockSpec(memory_space=pltpu.SMEM),
            own, both, both, own, own, own,
            cols(8, rows // 8 - 1, 0),
            cols(rows, 1, 0),
            cols(2 * rows, 0, 6),
            cols(2 * rows, 0, 12),
            cols(16, 0, 0),
        ],
        [own, cols(8, 0, 0), both, both, cols(16, 0, 0)],
        [
            jax.ShapeDtypeStruct((rows, D), BF),
            jax.ShapeDtypeStruct((8, D), BF),
            jax.ShapeDtypeStruct((2 * rows, D), BF),
            jax.ShapeDtypeStruct((2 * rows, D), BF),
            jax.ShapeDtypeStruct((16, D), F32),
        ],
        earlier,
        part,
        scratch_shapes=[
            pltpu.VMEM((2, rows, 128), BF),
            pltpu.VMEM((2, rows, 128), BF),
            pltpu.VMEM((128, rows), BF),
            pltpu.VMEM((128, rows), BF),
            pltpu.VMEM((128, 2 * rows), BF),
            pltpu.VMEM((128, rows), F32),
            pltpu.VMEM((rows, 128), F32),
            pltpu.VMEM((2 * rows, 128), F32),
            pltpu.VMEM((2 * rows, 128), F32),
        ],
        cost_estimate=cost(
            5 * 2 * 2 * rows * rows * 1.5 * 256 * part[1],
            rows * D * 7 * part[1],
            2 * rows * rows * 1.5 * part[1],
        ),
        name="att_bwd",
    )(state, *mixed, attended, logs, grad, projected, projected, projected, projected,
      small, *earlier)


def unit_rows(x):
    return x * lax.rsqrt(jnp.mean(x * x, axis=-1, keepdims=True) + norm_eps)


def before_bwd_kernel(x_ref, dt_ref, dk_ref, dv_ref, w_ref, out_ref, gain_ref):
    i = pl.program_id(0)
    hat = unit_rows(x_ref[...].astype(F32))
    gn = dot_nt(dk_ref[...], w_ref[D : 2 * D, :]) + dot_nt(dv_ref[...], w_ref[2 * D : 3 * D, :])

    last_step = pl.num_programs(0) - 1

    @pl.when(i == 0)
    def _():
        gain_ref[...] = jnp.zeros(gain_ref.shape, F32)

    @pl.when(i < last_step)
    def _():
        out_ref[...] = gn.astype(BF)
        gain_ref[...] += jnp.sum(gn * hat, axis=0, keepdims=True)

    @pl.when(i == last_step)
    def _():
        last = gn.shape[0] - 8
        full = jnp.concatenate([gn[:last], gn[last:] + dot_nt(dt_ref[...], w_ref[0:D, :])], 0)
        out_ref[...] = full.astype(BF)
        gain_ref[...] += jnp.sum(full * hat, axis=0, keepdims=True)


def before_bwd(x_both, back, weight, rows):
    dt, dk, dv = back[1:]
    blocks = 4
    height = rows // blocks
    step = pl.BlockSpec((height, D), lambda i: (i, 0))

    def whole(shape):
        return pl.BlockSpec(shape, lambda i: (0, 0))

    return pl.pallas_call(
        before_bwd_kernel,
        grid=(blocks,),
        in_specs=[step, whole((8, D)), step, step, whole((3 * D, D))],
        out_specs=[step, whole((1, D))],
        out_shape=[jax.ShapeDtypeStruct((rows, D), BF), jax.ShapeDtypeStruct((1, D), F32)],
        compiler_params=pltpu.CompilerParams(vmem_limit_bytes=VMEM_LIMIT),
        cost_estimate=cost(2 * rows * D * D * 2, rows * D * 12),
        name="before_bwd",
    )(x_both, dt, dk, dv, weight)


def qkv_bwd_kernel(
    core_ref, x_ref, dq_ref, dt_ref, dk_ref, dv_ref, w_ref, small_ref, gain_one_ref, gain_two_ref, tg_ref,
    *refs, pieces, blocks,
):
    if pieces:
        send_ref, keep_ref, own_ref, acc, gacc = refs
    else:
        keep_ref, ends_ref, own_ref, acc, gacc = refs
    i = pl.program_id(0)
    half = blocks // 2

    @pl.when(i == 0)
    def _():
        acc[...] = jnp.zeros(acc.shape, F32)
        gacc[0:1, :] = gain_one_ref[...]

    hat = unit_rows(x_ref[...].astype(F32))
    low = (hat * small_ref[0:1, :]).astype(BF)
    dk = dk_ref[...]
    dv = dv_ref[...]
    acc[D : 2 * D, :] += dot_tn(low, dk)
    acc[2 * D : 3 * D, :] += dot_tn(low, dv)

    @pl.when(i == half - 1)
    def _():
        acc[0:D, :] += dot_tn(low[low.shape[0] - 8 :], dt_ref[...])

    @pl.when(i >= half)
    def _():
        dq = dq_ref[...]
        acc[0:D, :] += dot_tn(low, dq)
        full = (
            dot_nt(dk, w_ref[D : 2 * D, :])
            + dot_nt(dv, w_ref[2 * D : 3 * D, :])
            + dot_nt(dq, w_ref[0:D, :])
        )
        own_ref[...] = full
        gacc[0:1, :] += jnp.sum(full * hat, axis=0, keepdims=True)

    @pl.when(i == blocks - 1)
    def _():
        small = jnp.concatenate(
            [gacc[0:1, :], gain_two_ref[...], tg_ref[0:9, :], jnp.zeros((5, D), F32)], 0
        )
        if pieces:
            core = core_ref[0]
            height = 3 * D // (2 * pieces)
            wide = height + 16
            for j in range(pieces):
                to = pl.ds(j * wide, wide)
                away = pl.ds(pl.multiple_of((2 * j + 1 - core) * height, 16), wide)
                here = pl.ds(pl.multiple_of((2 * j + core) * height, 16), wide)
                send_ref[to, :] = acc[away, :].astype(BF)
                keep_ref[to, :] = acc[here, :]
            send_ref[pieces * wide :, :] = small.astype(BF)
            keep_ref[pieces * wide :, :] = small
        else:
            keep_ref[...] = acc[0 : 3 * D, :].astype(BF)
            ends_ref[...] = small


def qkv_bwd(core, x_both, back, weight, small, gain_one_grad, gain_two_grad, tap_grads, rows, pieces):
    dq, dt, dk, dv = back
    blocks = 4
    half = blocks // 2
    height = 2 * rows // blocks
    step = pl.BlockSpec((height, D), lambda i: (i, 0))
    late = pl.BlockSpec((height, D), lambda i: (jnp.maximum(i - half, 0), 0))

    def whole(shape):
        return pl.BlockSpec(shape, lambda i: (0, 0))

    if pieces:
        packed = 3 * D // 2 + 16 * pieces + 16
        outs = [jax.ShapeDtypeStruct((packed, D), BF), jax.ShapeDtypeStruct((packed, D), F32)]
        out_at = [whole((packed, D))] * 2
    else:
        outs = [jax.ShapeDtypeStruct((3 * D, D), BF), jax.ShapeDtypeStruct((16, D), F32)]
        out_at = [whole((3 * D, D)), whole((16, D))]

    def body(*refs):
        qkv_bwd_kernel(*refs, pieces=pieces, blocks=blocks)

    return pl.pallas_call(
        body,
        grid=(blocks,),
        in_specs=[
            pl.BlockSpec(memory_space=pltpu.SMEM),
            step, late, whole((8, D)), step, step, whole((3 * D, D)),
            whole((16, D)), whole((1, D)), whole((1, D)), whole((16, D)),
        ],
        out_specs=out_at + [late],
        out_shape=outs + [jax.ShapeDtypeStruct((rows, D), F32)],
        scratch_shapes=[pltpu.VMEM((3 * D + 16, D), F32), pltpu.VMEM((8, D), F32)],
        compiler_params=pltpu.CompilerParams(vmem_limit_bytes=VMEM_LIMIT),
        cost_estimate=cost(2 * 2 * D * D * 4 * rows, rows * D * 30),
        name="qkv_bwd",
    )(core, x_both, dq, dt, dk, dv, weight, small, gain_one_grad, gain_two_grad, tap_grads)


def merge(index, keep, got, height, taken):
    rows = keep.shape[0]
    out_rows = taken * height + 16 if taken else rows

    def body(index_ref, keep_ref, got_ref, send_ref, stay_ref):
        if not taken:
            total = keep_ref[...] + got_ref[...].astype(F32)
            send_ref[...] = total.astype(BF)
            stay_ref[...] = total
            return
        for j in range(taken):
            to = pl.ds(j * height, height)
            away = pl.ds(pl.multiple_of(index_ref[j] * height, 16), height)
            here = pl.ds(pl.multiple_of(index_ref[taken + j] * height, 16), height)
            send_ref[to, :] = (keep_ref[away, :] + got_ref[away, :].astype(F32)).astype(BF)
            stay_ref[to, :] = keep_ref[here, :] + got_ref[here, :].astype(F32)
        end = keep_ref[rows - 16 :, :] + got_ref[rows - 16 :, :].astype(F32)
        send_ref[taken * height :, :] = end.astype(BF)
        stay_ref[taken * height :, :] = end

    vmem = pl.BlockSpec(memory_space=pltpu.VMEM)
    return pl.pallas_call(
        body,
        in_specs=[pl.BlockSpec(memory_space=pltpu.SMEM), vmem, vmem],
        out_specs=[vmem, vmem],
        out_shape=[
            jax.ShapeDtypeStruct((out_rows, D), BF),
            jax.ShapeDtypeStruct((out_rows, D), F32),
        ],
        compiler_params=pltpu.CompilerParams(vmem_limit_bytes=32 << 20),
        cost_estimate=cost(rows * D, rows * D * 12),
        name="merge",
    )(index, keep, got)


def merge_grid(index, keep, got, taken, kept=F32):
    height = keep.shape[1]

    def body(index_ref, ka_ref, ga_ref, kb_ref, gb_ref, send_ref, stay_ref):
        send_ref[...] = (ka_ref[...].astype(F32) + ga_ref[...].astype(F32)).astype(BF)
        stay_ref[...] = (kb_ref[...].astype(F32) + gb_ref[...].astype(F32)).astype(kept)

    away = pl.BlockSpec((1, height, D), lambda i, index: (index[i], 0, 0))
    here = pl.BlockSpec((1, height, D), lambda i, index: (index[taken + i], 0, 0))
    step = pl.BlockSpec((1, height, D), lambda i, index: (i, 0, 0))
    return pl.pallas_call(
        body,
        grid_spec=pltpu.PrefetchScalarGridSpec(
            num_scalar_prefetch=1,
            grid=(taken,),
            in_specs=[away, away, here, here],
            out_specs=[step, step],
        ),
        out_shape=[
            pltpu.HBM((taken, height, D), BF),
            pltpu.HBM((taken, height, D), kept),
        ],
        compiler_params=pltpu.CompilerParams(vmem_limit_bytes=32 << 20),
        cost_estimate=cost(taken * height * D * 2, taken * height * D * 16),
        name="merge_grid",
    )(index, keep, got, keep, got)


def arrange(index, blocks):
    height = blocks[0].shape[0] - 16

    def body(index_ref, *refs):
        first_ref, rest_ref, ends, total, sems = refs[4:]
        refs = refs[:4]
        tail = pl.ds(height, 16)
        places = [first_ref.at[pl.ds(0, height)]] + [rest_ref.at[pl.ds(i * height, height)] for i in range(3)]
        for k in range(4):
            pltpu.make_async_copy(refs[k].at[tail], ends.at[k], sems.at[4 + k]).start()
        for i in range(4):
            for k in range(4):

                @pl.when(index_ref[i] == k)
                def _():
                    pltpu.make_async_copy(refs[k].at[pl.ds(0, height)], places[i], sems.at[i]).start()

        for k in range(4):
            pltpu.make_async_copy(refs[k].at[tail], ends.at[k], sems.at[4 + k]).wait()
        sums = [ends[k].astype(F32) for k in range(4)]
        total[...] = (sums[0] + sums[1] + sums[2] + sums[3]).astype(BF)
        last = pltpu.make_async_copy(total, first_ref.at[tail], sems.at[8])
        last.start()
        for i in range(4):
            pltpu.make_async_copy(refs[0].at[pl.ds(0, height)], places[i], sems.at[i]).wait()
        last.wait()

    held = pl.BlockSpec(memory_space=pltpu.HBM)
    return pl.pallas_call(
        body,
        in_specs=[pl.BlockSpec(memory_space=pltpu.SMEM)] + [held] * 4,
        out_specs=[held, held],
        out_shape=[
            jax.ShapeDtypeStruct((height + 16, D), BF),
            jax.ShapeDtypeStruct((3 * height, D), BF),
        ],
        scratch_shapes=[
            pltpu.VMEM((4, 16, D), BF),
            pltpu.VMEM((16, D), BF),
            pltpu.SemaphoreType.DMA((9,)),
        ],
        compiler_params=pltpu.CompilerParams(vmem_limit_bytes=32 << 20),
        cost_estimate=cost(4 * height * D, 4 * height * D * 4),
        name="arrange",
    )(index, *blocks)


def join(own, got, shared=16):
    rows = own.shape[0]
    body_rows = rows - shared

    def body(own_ref, got_ref, out_ref):
        out_ref[0:body_rows, :] = own_ref[0:body_rows, :]
        out_ref[body_rows : 2 * body_rows, :] = got_ref[0:body_rows, :]
        if shared:
            out_ref[2 * body_rows :, :] = own_ref[body_rows:, :] + got_ref[body_rows:, :]

    vmem = pl.BlockSpec(memory_space=pltpu.VMEM)
    return pl.pallas_call(
        body,
        in_specs=[vmem, vmem],
        out_specs=vmem,
        out_shape=jax.ShapeDtypeStruct((2 * body_rows + shared, D), BF),
        compiler_params=pltpu.CompilerParams(vmem_limit_bytes=32 << 20),
        cost_estimate=cost(rows * D, rows * D * 8),
        name="join",
    )(own, got)


def join_held(own, got):
    rows = own.shape[0]
    cuts = 4
    size = rows // cuts

    def body(own_ref, got_ref, out_ref, sems):
        copies = []
        for k, ref in enumerate((own_ref, got_ref)):
            for j in range(cuts):
                source = ref.at[pl.ds(j * size, size)]
                to = out_ref.at[pl.ds(k * rows + j * size, size)]
                copies.append(pltpu.make_async_copy(source, to, sems.at[k * cuts + j]))
        for copy in copies:
            copy.start()
        for copy in copies:
            copy.wait()

    held = pl.BlockSpec(memory_space=pltpu.HBM)
    return pl.pallas_call(
        body,
        in_specs=[held, held],
        out_specs=held,
        out_shape=jax.ShapeDtypeStruct((2 * rows, D), BF),
        scratch_shapes=[pltpu.SemaphoreType.DMA((2 * cuts,))],
        compiler_params=pltpu.CompilerParams(vmem_limit_bytes=16 << 20),
        cost_estimate=cost(0, rows * D * 8),
        name="join_held",
    )(own, got)


def hold(block, other):
    held = pl.BlockSpec(memory_space=pl.ANY)
    return pl.pallas_call(
        lambda block_ref, other_ref, out_ref: None,
        in_specs=[held, held],
        out_specs=held,
        out_shape=jax.ShapeDtypeStruct(block.shape, block.dtype),
        input_output_aliases={0: 0},
        name="hold",
    )(block, other)


def qkv_fwd_kernel(index_ref, x_ref, *refs, pieces, blocks):
    if pieces:
        own_ref, got_ref, out_ref, small_ref, weight = refs
    else:
        weight, given_ref, out_ref, small_ref = refs
    i = pl.program_id(0)

    @pl.when(i == 0)
    def _():
        if pieces:
            height = 3 * D // (2 * pieces)
            for j in range(pieces):
                at = pl.ds(j * height, height)
                for k, ref in enumerate((own_ref, got_ref)):
                    to = pl.multiple_of(index_ref[k * pieces + j] * height, 16)
                    weight[pl.ds(to, height), :] = ref[at, :]
            end = pl.ds(pieces * height, 16)
            small_ref[...] = own_ref[end, :].astype(F32) + got_ref[end, :].astype(F32)
        else:
            small_ref[...] = given_ref[...]

    x = x_ref[...].astype(F32)
    hat = x * lax.rsqrt(jnp.mean(x * x, axis=-1, keepdims=True) + norm_eps)
    low = (hat * small_ref[0:1, :]).astype(BF)

    @pl.when(i >= blocks // 2 - 1)
    def _():
        out_ref[:, 0:D] = dot(low, weight[0:D, :]).astype(BF)

    out_ref[:, D : 2 * D] = dot(low, weight[D : 2 * D, :]).astype(BF)
    out_ref[:, 2 * D : 3 * D] = dot(low, weight[2 * D : 3 * D, :]).astype(BF)


def qkv_fwd(index, x_both, weights, rows, pieces):
    blocks = 4
    height = 2 * rows // blocks

    def body(*refs):
        qkv_fwd_kernel(*refs, pieces=pieces, blocks=blocks)

    return pl.pallas_call(
        body,
        grid=(blocks,),
        in_specs=[
            pl.BlockSpec(memory_space=pltpu.SMEM),
            pl.BlockSpec((height, D), lambda i: (i, 0)),
            *[pl.BlockSpec(w.shape, lambda i: (0, 0)) for w in weights],
        ],
        out_specs=[
            pl.BlockSpec((height, 3 * D), lambda i: (i, 0)),
            pl.BlockSpec((16, D), lambda i: (0, 0)),
        ]
        + ([pl.BlockSpec((3 * D, D), lambda i: (0, 0))] if pieces else []),
        out_shape=[
            jax.ShapeDtypeStruct((2 * rows, 3 * D), BF),
            jax.ShapeDtypeStruct((16, D), F32),
        ]
        + ([jax.ShapeDtypeStruct((3 * D, D), BF)] if pieces else []),
        compiler_params=pltpu.CompilerParams(vmem_limit_bytes=VMEM_LIMIT),
        cost_estimate=cost(2 * 2 * rows * D * 3 * D, rows * D * 20),
        name="qkv_fwd",
    )(index, x_both, *weights)


def ffn_kernel(
    state_ref, index_ref, x_ref, att_ref, cot_ref, small_ref, own_ref, own_two_ref, got_ref, got_two_ref,
    out_ref, gh_ref, ga_ref, gain_grad_ref, away_ref, here_ref,
    hidden, low, total, back, cot, sq, gb, weights, stage_up, stage_down, stage_out, in_sems, sems,
):
    c = pl.program_id(0)
    rows = x_ref.shape[0]
    blocks = [pl.ds(i * QB, QB) for i in range(rows // QB)]
    last = c == pl.num_programs(0) - 1
    core = index_ref[24]

    def fetch(k, j):
        ref = ((own_ref, own_two_ref), (got_ref, got_two_ref))[k][j // 6]
        piece = index_ref[12 * k + j]
        to = weights.at[pl.ds(3 * piece, 3)]
        return pltpu.make_async_copy(ref.at[pl.ds(3 * (j % 6), 3)], to, in_sems.at[piece])

    def fetched(pieces):
        for piece in pieces:
            at = weights.at[pl.ds(3 * piece, 3)]
            pltpu.make_async_copy(own_ref.at[pl.ds(0, 3)], at, in_sems.at[piece]).wait()

    def put(source, group, count, column, sem, wait=False):
        piece = group // 3
        at = (piece // 2) * 3 + group % 3

        def copy(ref):
            to = ref.at[pl.ds(at, count)] if column is None else ref.at[pl.ds(at, count), column]
            return pltpu.make_async_copy(source, to, sems.at[sem])

        if wait:
            copy(here_ref).wait()
            return
        mine = piece % 2 == core

        @pl.when(mine)
        def _():
            copy(here_ref).start()

        @pl.when(jnp.logical_not(mine))
        def _():
            copy(away_ref).start()

    def put_up(i, wait=False):
        start = 0
        k = 0
        while start < 32:
            count = min(3 - (8 + start) % 3, 32 - start)
            put(stage_up.at[i, pl.ds(start, count)], 8 + start, count, i, 20 * i + k, wait)
            start += count
            k += 1

    def put_down(i, wait=False):
        for k in range(8):
            put(stage_down.at[i, pl.ds(k, 1)], 40 + 8 * i + k, 1, None, 20 * i + 12 + k, wait)

    def put_out(wait=False):
        for k in range(8):
            put(stage_out.at[pl.ds(k, 1)], k, 1, None, 80 + k, wait)

    def square(first):
        return weights[first : first + 8].reshape(D, D)

    @pl.when(c == 0)
    def _():
        for early in (True, False):
            for k in range(2):
                for j in range(12):

                    @pl.when((index_ref[12 * k + j] < 3) == early)
                    def _():
                        fetch(k, j).start()

        cot[...] = jnp.where(state_ref[0] > 0, cot_ref[...], jnp.zeros((), BF))
        total[...] = jnp.zeros(total.shape, F32)
        back[...] = jnp.zeros(back.shape, F32)
        fetched(range(3))
        wo = square(0)
        for b in blocks:
            h = x_ref[b, :].astype(F32) + dot(att_ref[b, :], wo)
            hidden[b, :] = h
            hat = h * lax.rsqrt(jnp.mean(h * h, axis=-1, keepdims=True) + norm_eps)
            low[b, :] = (hat * small_ref[1:2, :]).astype(BF)

    for i, pieces in enumerate((range(3, 16), range(16, 19), range(19, 22), range(22, 24))):

        @pl.when(c == i)
        def _():
            fetched(pieces)

    up = weights[8:40, c].reshape(D, D)
    down = weights[pl.ds(40 + 8 * c, 8)].reshape(D, D)
    for b in blocks:
        act = jnp.maximum(dot(low[b, :], up), 0.0)
        s = (act * act).astype(BF)
        sq[b, :] = s
        total[b, :] += dot(s, down)
        g = (dot_nt(cot[b, :], down) * 2.0 * act).astype(BF)
        gb[b, :] = g
        back[b, :] += dot_nt(g, up)
    stage_down[c] = dot_tn(sq[...], cot[...]).reshape(8, 4, 24, D).astype(BF)
    stage_up[c] = dot_tn(low[...], gb[...]).reshape(32, 24, D).astype(BF)
    put_down(c)
    put_up(c)

    @pl.when(last)
    def _():
        gain = small_ref[1:2, :]
        wo = square(0)
        sums = jnp.zeros((1, D), F32)
        for b in blocks:
            h = hidden[b, :]
            out_ref[b, :] = (h + total[b, :]).astype(BF)
            factor = lax.rsqrt(jnp.mean(h * h, axis=-1, keepdims=True) + norm_eps)
            hat = h * factor
            g = back[b, :]
            sums = sums + jnp.sum(g * hat, axis=0, keepdims=True)
            weighted = g * gain
            inner = jnp.mean(weighted * hat, axis=-1, keepdims=True)
            grad = cot[b, :].astype(F32) + factor * (weighted - hat * inner)
            gh_ref[b, :] = grad
            grad_low = grad.astype(BF)
            gb[b, :] = grad_low
            ga_ref[b, :] = dot_nt(grad_low, wo).astype(BF)
        gain_grad_ref[...] = sums
        stage_out[...] = dot_tn(att_ref[...], gb[...]).reshape(8, 4, 24, D).astype(BF)
        put_out()
        for i in range(4):
            put_down(i, True)
            put_up(i, True)
        put_out(True)


def ffn(state, index, tokens, attended, out_grad, small, weights, rows):
    def whole(shape):
        return pl.BlockSpec(shape, lambda c: (0,) * len(shape), pipeline_mode=pl.Buffered(1))

    act = whole((rows, D))
    held = pl.BlockSpec(memory_space=pl.ANY)
    scalars = pl.BlockSpec(memory_space=pltpu.SMEM)
    half = (36, 4, 24, D)
    return pl.pallas_call(
        ffn_kernel,
        grid=(4,),
        in_specs=[scalars, scalars, act, act, act, whole((16, D)), held, held, held, held],
        out_specs=[act, act, act, whole((1, D)), held, held],
        out_shape=[
            jax.ShapeDtypeStruct((rows, D), BF),
            jax.ShapeDtypeStruct((rows, D), F32),
            jax.ShapeDtypeStruct((rows, D), BF),
            jax.ShapeDtypeStruct((1, D), F32),
            jax.ShapeDtypeStruct(half, BF),
            jax.ShapeDtypeStruct(half, BF),
        ],
        scratch_shapes=[
            pltpu.VMEM((rows, D), F32),
            pltpu.VMEM((rows, D), BF),
            pltpu.VMEM((rows, D), F32),
            pltpu.VMEM((rows, D), F32),
            pltpu.VMEM((rows, D), BF),
            pltpu.VMEM((rows, D), BF),
            pltpu.VMEM((rows, D), BF),
            pltpu.VMEM((72, 4, 24, D), BF),
            pltpu.VMEM((4, 32, 24, D), BF),
            pltpu.VMEM((4, 8, 4, 24, D), BF),
            pltpu.VMEM((8, 4, 24, D), BF),
            pltpu.SemaphoreType.DMA((24,)),
            pltpu.SemaphoreType.DMA((88,)),
        ],
        compiler_params=pltpu.CompilerParams(vmem_limit_bytes=60 << 20),
        cost_estimate=cost(2 * rows * D * D * (24 + 3), 2 * 12 * D * D * 2 + rows * D * 16),
        name="ffn",
    )(state, index, tokens, attended, out_grad, small, *weights)


def shift_flat(block, distance):
    count = lax.axis_size(AXES)
    route = [(i - distance, i) for i in range(count) if 0 <= i - distance < count]
    return lax.ppermute(block, AXES, route)


def shift_ctx(block, distance):
    count = lax.axis_size("ctx")
    route = [(i - distance, i) for i in range(count) if 0 <= i - distance < count]
    return lax.ppermute(block, "ctx", route)


def after(value, *others):
    return lax.optimization_barrier((value, *others))[0]


def swap(block, even_bit, odd_bit, planes=None):
    count = lax.axis_size(AXES)
    route = [
        (i, i ^ (odd_bit if i & 1 else even_bit))
        for i in range(count)
        if planes is None or i >> 3 in planes
    ]
    return lax.ppermute(block, AXES, route)


def to_aligned(shard, place, count, delta):
    rows = shard.shape[0]
    lag = delta * (count - 1)
    back = -(-lag // rows)
    if back == 1:
        keep = -(-lag // 8) * 8
        parts = [shift_flat(shard[rows - keep :], 1), shard]
    else:
        keep = back * rows
        parts = [shift_flat(shard, s) for s in range(back, 0, -1)] + [shard]
    joined = jnp.concatenate(parts, 0)
    return lax.dynamic_slice_in_dim(joined, keep - delta * place, rows - delta, 0)


def small_part(shard, place, count, delta):
    rows = shard.shape[0]
    extra = count * delta
    zeros = jnp.zeros((extra, 128), shard.dtype)
    joined = jnp.concatenate([zeros, shard, zeros], 0)
    start = extra + count * (rows - delta) - place * rows
    return lax.dynamic_slice_in_dim(joined, jnp.minimum(start, rows + extra), extra, 0)


def from_aligned(chunk, small, place, count, delta, rows):
    aligned = rows - delta
    ahead = -(-(count * delta) // aligned)
    parts = [chunk]
    if ahead == 1:
        keep = small.shape[0]
        got = shift_flat(chunk[:keep], -1)
        parts.append(jnp.where(place == count - 1, small, got))
    else:
        pad = ahead * aligned - small.shape[0]
        tail = jnp.concatenate([small, jnp.zeros((pad, 128), small.dtype)], 0)
        for s in range(1, ahead + 1):
            got = shift_flat(chunk, -s)
            for e in range(s):
                piece = tail[e * aligned : (e + 1) * aligned]
                got = jnp.where(place == count - s + e, piece, got)
            parts.append(got)
    return lax.dynamic_slice_in_dim(jnp.concatenate(parts, 0), delta * place, rows, 0)


def regroup(block):
    return block.reshape(-1, 24, 4, D).transpose(0, 2, 1, 3)


def ungroup(block):
    return block.reshape(-1, 4, 24, D).transpose(0, 2, 1, 3)


def normalize(values, gain):
    factor = lax.rsqrt(jnp.mean(values * values, axis=-1, keepdims=True) + norm_eps)
    scaled = values * factor
    return (scaled, factor, scaled * gain)


def norm_back(grad_in, scaled, factor, gain):
    weighted = grad_in * gain
    inner_mean = jnp.mean(weighted * scaled, axis=-1, keepdims=True)
    return factor * (weighted - scaled * inner_mean)


def adam_update(master, moment_one, moment_two, gradient, step_count, row_start):
    row_index = row_start + jnp.arange(master.shape[0], dtype=jnp.int32)
    matrix_rows = (4 * D * D + 2 * D * FF) // 128
    out_first = 3 * D * D // 128
    out_last = 4 * D * D // 128
    is_matrix = (row_index < matrix_rows)[:, None]
    is_out = ((row_index >= out_first) & (row_index < out_last))[:, None]
    step_rate = jnp.where(is_matrix, jnp.where(is_out, 0.5, 0.1), 1.0)
    decay_rate = jnp.where(is_matrix, 0.1, 0.0)
    step_value = step_count[0].astype(jnp.float32)
    new_one = 0.9 * moment_one + 0.1 * gradient
    new_two = 0.999 * moment_two + 0.001 * gradient * gradient
    corr_first = 1.0 - jnp.power(0.9, step_value)
    corr_second = 1.0 - jnp.power(0.999, step_value)
    new_weights = master - step_rate * (
        new_one / corr_first / (jnp.sqrt(new_two / corr_second) + 1e-08) + decay_rate * master
    )
    return (new_weights, new_one, new_two)


def shards(tokens, out_grad, positions, master, first_moment, second_moment, step_count):
    rows = tokens.shape[0]
    assert rows == SEQ_MIN
    count = lax.axis_size(AXES)
    place = lax.axis_index(AXES).astype(jnp.int32)
    owned = master.shape[0]
    aligned = (4 * D * D + 2 * D * FF) // 128 // count
    delta = owned - aligned
    height = aligned * 128 // D
    staged = count == 32
    first_place = positions[0]
    state = jnp.where(first_place < 0, 0, jnp.where(first_place >= SEQ_MIN, 2, 1)).astype(jnp.int32)
    state_vec = state[None]

    chunk = to_aligned(master, place, count, delta).reshape(-1, D)
    if staged:
        group = 3 * place + jnp.arange(3, dtype=jnp.int32)
        in_up = ((group >= 32) & (group < 64))[:, None, None, None]
        chunk = jnp.where(in_up, regroup(chunk), chunk.reshape(3, 4, 24, D)).reshape(-1, D)
    chunk = chunk.astype(BF)
    if staged:
        small = jnp.where(place == count - 1, master[owned - count * delta :], 0.0)
    else:
        small = small_part(master, place, count, delta)
    small = lax.reduce_precision(small, 8, 7)
    core = (place & 1)[None]
    x_bit = (place >> 1) & 1
    y_bit = (place >> 2) & 1
    even = (place & 1) == 0
    if staged:
        z = place >> 3
        mine = jnp.concatenate([chunk, small.astype(BF).reshape(-1, D)], 0)
        tokens_before = shift_ctx(after(tokens, mine), 1)
        far = swap(mine, 16, 16)
        near = swap(mine, 8, 8)
        tokens_both = jnp.concatenate([tokens_before, tokens], 0)
        both = swap(after(far, tokens_both), 8, 8)
        order = jnp.stack([z, z ^ 1, z ^ 2, z ^ 3]).astype(jnp.int32)
        mine, rest = arrange(after(order, state_vec), (mine, near, far, both))
        mine = join(mine, swap(mine, 2, 4))
        mine = join(mine, swap(mine, 4, 2))
        across = swap(rest, 2, 4)
        got = swap(mine, 1, 1)
        index = []
        late_index = []
        for k in (0, 1):
            turn = even if k == 0 else jnp.logical_not(even)
            for j in range(4):
                near, far = j & 1, j >> 1
                x_of = x_bit ^ jnp.where(turn, near, far)
                y_of = y_bit ^ jnp.where(turn, far, near)
                piece = 4 * y_of + 2 * x_of + (core[0] ^ k)
                index.append(piece)
                late_index += [piece, piece + 8, piece + 16]
        index = jnp.stack(index).astype(jnp.int32)
        late_index = jnp.stack(late_index + [core[0]]).astype(jnp.int32)
        projected, small, in_weight = qkv_fwd(index, tokens_both, (mine, got), rows, 4)
    else:
        tokens_both = jnp.concatenate([shift_ctx(tokens, 1), tokens], 0)
        wide = lax.all_gather(chunk, AXES, axis=0, tiled=True)
        small = lax.psum(small, AXES)[:96].reshape(-1, D)
        in_weight = wide[: 3 * D]
        projected, small = qkv_fwd(core, tokens_both, (in_weight, small), rows, 0)
        late_index = jnp.arange(25, dtype=jnp.int32) % 24
    gain_first = small[0]

    forward = []
    if staged:
        rest = join_held(after(rest, projected), across)
        line = swap(rest, 4, 2)
        core_rest = swap(rest, 1, 1)
        forward = att_fwd(after(state_vec, rest), projected, small, forward, FORWARD_PARTS[0], rows)
        forward = att_fwd(after(state_vec, core_rest), projected, small, forward, FORWARD_PARTS[1], rows)
        line = hold(line, forward[0])
        core_line = swap(line, 1, 1)
        forward = att_fwd(after(state_vec, line), projected, small, forward, FORWARD_PARTS[2], rows)
        late_weights = [w.reshape(18, 4, 24, D) for w in (rest, line, core_rest, core_line)]
    else:
        for part in FORWARD_PARTS:
            forward = att_fwd(state_vec, projected, small, forward, part, rows)
        grouped = jnp.concatenate(
            [
                wide[3 * D : 4 * D].reshape(-1, 4, 24, D),
                regroup(wide[4 * D : 8 * D]),
                wide[8 * D :].reshape(-1, 4, 24, D),
            ],
            0,
        )
        late_weights = [grouped[18 * k : 18 * k + 18] for k in range(4)]
    attn_low, logs, *mixed = forward

    layer_out, grad_hidden, grad_attended, grad_gain_two, away_grad, here_grad = ffn(
        state_vec, late_index, tokens, attn_low, out_grad, small, late_weights, rows
    )

    def backward(start, done, part):
        return att_bwd(
            start, mixed, attn_low, logs, grad_attended, projected, small, done, BACKWARD_PARTS[part], rows
        )

    if staged:
        stay = [jnp.where(even, 2 * j + x_bit, 2 * y_bit + j) for j in range(2)]
        away = [jnp.where(even, 2 * j + 1 - x_bit, 2 * (1 - y_bit) + j) for j in range(2)]
        pick_plane = jnp.stack(away + stay).astype(jnp.int32)
        other = jnp.where(even, y_bit, x_bit)
        pick_line = jnp.stack([1 - other, other]).astype(jnp.int32)

        def of_quarters(pick, held):
            half = pick.shape[0] // 2
            steps = [pick[s * half + j] + held * t for s in range(2) for t in range(3) for j in range(half)]
            return jnp.stack(steps)

        late_keep = here_grad.reshape(12, height, D)
        late_got = swap(away_grad.reshape(12, height, D), 1, 1)
        done = backward(state_vec, [], 0)
        late_send, late_keep = merge_grid(
            after(of_quarters(pick_plane, 4), done[4]), late_keep, late_got, 6, BF
        )
        late_got = swap(late_send, 2, 4)
        done = backward(after(state_vec, late_send), done, 1)
        late_send, late_keep = merge_grid(
            after(of_quarters(pick_line, 2), done[4]), late_keep, late_got, 3
        )
        late_got = swap(late_send, 4, 2)
        done = backward(after(state_vec, late_send), done, 2)
        z_even = (z & 1) == 0
        low_pair = [jnp.where(z_even, 0, 0), jnp.where(z_even, 2, 1)]
        high_pair = [jnp.where(z_even, 0, 0), jnp.where(z_even, 1, 2)]
        pick_z = jnp.stack(low_pair + high_pair).astype(jnp.int32)
        late_send, late_keep = merge_grid(after(pick_z, done[4]), late_keep, late_got, 2)
        late_got = swap(late_send, 8, 8)
        done = backward(after(state_vec, late_send), done, 3)
        high = z >> 1
        pick_last = jnp.stack([1 - high, high]).astype(jnp.int32)
        late_send, late_keep = merge_grid(after(pick_last, done[4]), late_keep, late_got, 1)
        late_got = swap(late_send, 16, 16, (0, 1, 3))
        sums_state = after(core, late_send)
    else:
        done = []
        for part in range(4):
            done = backward(state_vec, done, part)
        sums_state = core
    *back, tap_grads = done
    grads_before, gain_one_grad = before_bwd(tokens_both, back, in_weight, rows)
    from_next = shift_ctx(grads_before, -1)
    sums = qkv_bwd(
        after(sums_state, grads_before), tokens_both, back, in_weight, small, gain_one_grad, grad_gain_two, tap_grads, rows,
        4 if staged else 0,
    )
    grad_normed_one = sums[2]
    scaled_one, factor_one, _ = normalize(tokens.astype(F32), gain_first)
    input_grad = grad_hidden + norm_back(
        grad_normed_one + from_next.astype(F32), scaled_one, factor_one, gain_first
    )

    if staged:
        send, keep = sums[:2]
        got = swap(after(send, late_got, from_next), 1, 1)
        send, keep = merge(pick_plane, keep, got, height + 16, 2)
        got = swap(send, 2, 4)
        late_got = after(late_got, send)
        late_chunk = late_keep[0] + late_got[0].astype(F32)
        late_chunk = jnp.where(in_up, ungroup(late_chunk).reshape(3, 4, 24, D), late_chunk.reshape(3, 4, 24, D))
        late_chunk = late_chunk.reshape(-1, D)
        late_next = shift_flat(late_chunk[:16], -1)
        send, keep = merge(after(pick_line, late_chunk), keep, got, height + 16, 1)
        got = swap(send, 4, 2)
        send, keep = merge(core, keep, got, height + 16, 0)
        got = swap(send, 8, 8)
        send, keep = merge(after(core, input_grad, late_next), keep, got, height + 16, 0)
        got = swap(send, 16, 16, (1, 2))
        first = keep + got.astype(F32)
        quarter = count // 4
        follow = jnp.where(place < quarter - 1, first[height : height + 16], late_next)
        follow = jnp.where(place == count - 1, first[height + 16 :], follow)
        chunk_grad = jnp.where(place < quarter, first[:height], late_chunk)
        chunk_grad = jnp.concatenate([chunk_grad, follow], 0).reshape(-1, 128)
        gradient = lax.dynamic_slice_in_dim(chunk_grad, delta * place, owned, 0)
    else:
        flat_grad = jnp.stack([here_grad.reshape(12, 3, 4, 24, D), away_grad.reshape(12, 3, 4, 24, D)], 1)
        flat_grad = flat_grad.reshape(72, 4, 24, D)
        wide_grad = jnp.concatenate(
            [
                sums[0],
                flat_grad[:8].reshape(-1, D),
                ungroup(flat_grad[8:40]).reshape(-1, D),
                flat_grad[40:].reshape(-1, D),
            ],
            0,
        )
        chunk_grad = lax.psum_scatter(wide_grad, AXES, scatter_dimension=0, tiled=True).astype(F32)
        used = sums[1].reshape(-1, 128)
        extra = count * delta
        small_grad = jnp.concatenate([used, jnp.zeros((extra - used.shape[0], 128), F32)], 0)
        small_grad = lax.psum(small_grad, AXES)
        gradient = from_aligned(chunk_grad.reshape(-1, 128), small_grad, place, count, delta, owned)
    new_weights, new_one, new_two = adam_update(
        master, first_moment, second_moment, gradient, step_count, place * owned
    )
    return (layer_out, input_grad, new_weights, new_one, new_two, new_weights.astype(BF))


def solution(mesh):
    spread = P(AXES, None)
    return jax.shard_map(
        shards,
        mesh=mesh,
        in_specs=(spread, spread, P(AXES), spread, spread, spread, P()),
        out_specs=(spread,) * 6,
        check_vma=False,
    )
```

```python
import jax
import jax.numpy as jnp
from jax import lax
from jax.experimental import pallas as pl
from jax.experimental.pallas import tpu as pltpu
from jax.sharding import PartitionSpec as P

D = 768
HEADS = 12
HEAD_DIM = 64
FF = 3072
SEQ_MIN = 1024
AXES = ("dp", "ctx")
QB = 256
FORWARD_PARTS = ((0, 2), (2, 2), (4, 2))
BACKWARD_PARTS = ((0, 1), (1, 2), (3, 1), (4, 2))
F32 = jnp.float32
BF = jnp.bfloat16
NT = (((1,), (1,)), ((), ()))
TN = (((0,), (0,)), ((), ()))
norm_eps = 1e-06
VMEM_LIMIT = 56 << 20


def dot(left, right):
    return jnp.dot(left, right, preferred_element_type=F32)


def dot_nt(left, right):
    return lax.dot_general(left, right, NT, preferred_element_type=F32)


def dot_tn(left, right):
    return lax.dot_general(left, right, TN, preferred_element_type=F32)


def cost(flops, nbytes, exps=0):
    return pl.CostEstimate(flops=int(flops), bytes_accessed=int(nbytes), transcendentals=int(exps))


def taps_of(small, matrix):
    return [small[2 + 3 * j + matrix : 3 + 3 * j + matrix, :] for j in range(3)]


def row_ids(height):
    return lax.broadcasted_iota(jnp.int32, (height, 128), 0)


def conv(out_ref, x_ref, start, tail_ref, taps, rows, state):
    height = x_ref.shape[0]
    for r in range(0, height, QB):
        at = start + r
        if r:
            x = x_ref[r - 16 : r + QB, :].astype(F32)
        else:
            before = jnp.zeros((16, 128), F32)
            if tail_ref is not None:
                before = jnp.concatenate([before[8:], tail_ref[...].astype(F32)], 0)
            x = jnp.concatenate([before, x_ref[0:QB, :].astype(F32)], 0)
        one = pltpu.roll(x, 1, 0)[16:]
        two = pltpu.roll(x, 2, 0)[16:]
        x = x[16:]
        scale = 1.0
        if at >= rows:
            scale = jnp.where(state > 0, 1.0, 0.0)
        if at == 0 or at == rows:
            seen = jnp.where(state == 2, 1.0, 0.0) if at else 0.0
            row = row_ids(QB)
            one = jnp.where(row < 1, one * seen, one)
            two = jnp.where(row < 2, two * seen, two)
        c_one = taps[1] * scale
        c_two = taps[2] * scale
        out_ref[r : r + QB, :] = (taps[0] * x + c_one * one + c_two * two).astype(BF)


def att_fwd_kernel(
    state_ref, tail_ref, q_ref, k_ref, v_ref, small_ref,
    o_ref, l_ref, qm_ref, km_ref, vm_ref, ka, va,
):
    rows = q_ref.shape[0]
    lane = lax.broadcasted_iota(jnp.int32, (1, 128), 1)
    state = state_ref[0]
    conv(qm_ref, q_ref, rows, tail_ref, taps_of(small_ref[...], 0), rows, state)
    conv(km_ref, k_ref, 0, None, taps_of(small_ref[...], 1), rows, state)
    conv(vm_ref, v_ref, 0, None, taps_of(small_ref[...], 2), rows, state)
    bias = jnp.where(state == 2, 0.0, -1e30)
    for h in range(2):
        mine = (lane < 64) if h == 0 else (lane >= 64)
        base = 64 if h == 0 else 0
        first = jnp.where(lane == base, bias, 0.0).astype(BF)
        for r in range(0, 2 * rows, QB):
            at = pl.ds(r, QB)
            ka[h, at, :] = jnp.where(mine, km_ref[at, :], first if r < rows else jnp.zeros((), BF))
            va[h, at, :] = jnp.where(mine, vm_ref[at, :], jnp.ones((), BF))
    heads = (row_ids(128) < 64) == (lane < 64)
    heads = heads.astype(BF)
    q_most = jnp.zeros((1, 128), F32)
    k_most = jnp.zeros((1, 128), F32)
    for r in range(0, rows, QB):
        q = qm_ref[r : r + QB, :].astype(F32) * 0.125
        q_most = jnp.maximum(q_most, jnp.max(dot((q * q).astype(BF), heads), axis=0, keepdims=True))
    for r in range(0, 2 * rows, QB):
        k = km_ref[r : r + QB, :].astype(F32)
        k_most = jnp.maximum(k_most, jnp.max(dot((k * k).astype(BF), heads), axis=0, keepdims=True))
    small_scores = jnp.max(q_most * k_most) <= 3025.0

    def attend(subtract):
        for i in range(rows // QB):
            rs = pl.ds(i * QB, QB)
            outs = []
            sums = []
            qf = qm_ref[rs, :].astype(F32) * 0.125
            for h in range(2):
                mine = (lane < 64) if h == 0 else (lane >= 64)
                base = 64 if h == 0 else 0
                qh = jnp.where(mine, qf, jnp.where(lane == base, 1.0, 0.0)).astype(BF)
                nk = rows + (i + 1) * QB
                s = dot_nt(qh, ka[h, 0:nk, :])
                r = lax.broadcasted_iota(jnp.int32, (QB, QB), 0)
                c = lax.broadcasted_iota(jnp.int32, (QB, QB), 1)
                sd = jnp.where(c <= r, s[:, nk - QB :], -1e30)
                se = s[:, : nk - QB]
                if subtract:
                    m = jnp.maximum(
                        jnp.max(sd, axis=1, keepdims=True), jnp.max(se, axis=1, keepdims=True)
                    )
                    se = se - m
                    sd = sd - m
                p = jnp.concatenate([jnp.exp(se).astype(BF), jnp.exp(sd).astype(BF)], 1)
                o = dot(p, va[h, 0:nk, :])
                outs.append(o / pltpu.roll(o, 64, 1))
                sums.append(m + jnp.log(o) if subtract else jnp.log(o))
            res = jnp.where(lane < 64, outs[0], outs[1])
            res = jnp.where(state == 0, vm_ref[pl.ds(rows + i * QB, QB), :].astype(F32), res)
            o_ref[rs, :] = res.astype(BF)
            l_ref[rs, :] = jnp.where(lane < 64, sums[1], sums[0])

    @pl.when(small_scores)
    def _():
        attend(False)

    @pl.when(jnp.logical_not(small_scores))
    def _():
        attend(True)


def call_in_parts(body, in_specs, out_specs, out_shape, earlier, part, **options):
    used = len(in_specs)

    def kernel(*refs):
        body(*refs[:used], *refs[used + len(earlier) :])

    return pl.pallas_call(
        kernel,
        grid=(part[1],),
        in_specs=in_specs + [pl.BlockSpec(memory_space=pl.ANY)] * len(earlier),
        out_specs=out_specs,
        out_shape=out_shape,
        input_output_aliases={used + i: i for i in range(len(earlier))},
        compiler_params=pltpu.CompilerParams(vmem_limit_bytes=VMEM_LIMIT),
        **options,
    )


def columns(part):
    first = part[0]

    def cols(height, row, off):
        return pl.BlockSpec((height, 128), lambda p: (row, p + first + off))

    return cols


def att_fwd(state, projected, small, earlier, part, rows):
    cols = columns(part)
    return call_in_parts(
        att_fwd_kernel,
        [
            pl.BlockSpec(memory_space=pltpu.SMEM),
            cols(8, rows // 8 - 1, 0),
            cols(rows, 1, 0),
            cols(2 * rows, 0, 6),
            cols(2 * rows, 0, 12),
            cols(16, 0, 0),
        ],
        [cols(rows, 0, 0)] * 3 + [cols(2 * rows, 0, 0)] * 2,
        [
            jax.ShapeDtypeStruct((rows, D), BF),
            jax.ShapeDtypeStruct((rows, D), F32),
            jax.ShapeDtypeStruct((rows, D), BF),
            jax.ShapeDtypeStruct((2 * rows, D), BF),
            jax.ShapeDtypeStruct((2 * rows, D), BF),
        ],
        earlier,
        part,
        scratch_shapes=[pltpu.VMEM((2, 2 * rows, 128), BF)] * 2,
        cost_estimate=cost(
            2 * 2 * 2 * rows * rows * 1.5 * 256 * part[1],
            rows * D * 5 * part[1],
            2 * rows * rows * 1.5 * part[1],
        ),
        name="att_fwd",
    )(state, projected, projected, projected, projected, small, *earlier)


def three(x, lane, base):
    hi = x.astype(BF).astype(F32)
    r = x - hi
    mid = r.astype(BF).astype(F32)
    lo = r - mid
    return jnp.where(
        lane == base, hi, jnp.where(lane == base + 1, mid, jnp.where(lane == base + 2, lo, 0.0))
    )


def conv_back(out_ref, grad_ref, x_ref, start, tail, taps, rows, state):
    height = grad_ref.shape[0]
    joint = jnp.where(state == 2, 1.0, 0.0)
    sums = [jnp.zeros((1, 128), F32)] * 3

    def add(parts, x):
        return [s + jnp.sum(g * x, axis=0, keepdims=True) for s, g in zip(sums, parts)]

    for r in range(0, height, QB):
        ends = r + QB == height
        meets = start + r + QB == rows
        if ends:
            grad = jnp.concatenate([grad_ref[r : r + QB, :], jnp.zeros((8, 128), F32)], 0)
        else:
            grad = grad_ref[r : r + QB + 8, :]
        one = pltpu.roll(grad, QB + 7, 0)[:QB]
        two = pltpu.roll(grad, QB + 6, 0)[:QB]
        grad = grad[:QB]
        if meets and not ends:
            row = row_ids(QB)
            one = jnp.where(row >= QB - 1, one * joint, one)
            two = jnp.where(row >= QB - 2, two * joint, two)
        out_ref[r : r + QB, :] = (taps[0] * grad + taps[1] * one + taps[2] * two).astype(BF)
        sums = add((grad, one, two), x_ref[r : r + QB, :].astype(F32))
    if tail is not None:
        grad = jnp.concatenate([jnp.zeros((8, 128), F32), grad_ref[0:8, :]], 0)
        one = pltpu.roll(grad, 15, 0)[:8] * joint
        two = pltpu.roll(grad, 14, 0)[:8] * joint
        tail[0][...] = (taps[1] * one + taps[2] * two).astype(BF)
        sums = add((grad[:8], one, two), tail[1][...].astype(F32))
    return sums


def att_bwd_kernel(
    state_ref, q_ref, k_ref, v_ref, o_ref, l_ref, do_ref, xt_ref, xq_ref, xk_ref, xv_ref,
    small_ref,
    pq_ref, pt_ref, pk_ref, pv_ref, tg_ref, qa, da, qt, dt, kt, dqt, dqs, dks, dvs,
):
    rows = q_ref.shape[0]
    lane = lax.broadcasted_iota(jnp.int32, (1, 128), 1)
    second = state_ref[0] == 2
    for r in range(0, rows, QB):
        at = pl.ds(r, QB)
        do = do_ref[at, :].astype(F32)
        od = do * o_ref[at, :].astype(F32)
        qf = q_ref[at, :].astype(F32) * 0.125
        lv = l_ref[at, :]
        for h in range(2):
            mine = (lane < 64) if h == 0 else (lane >= 64)
            base = 64 if h == 0 else 0
            delta = jnp.sum(jnp.where(mine, od, 0.0), axis=1, keepdims=True)
            qa[h, at, :] = jnp.where(mine, qf, three(-lv, lane, base)).astype(BF)
            da[h, at, :] = jnp.where(mine, do, three(-delta, lane, base)).astype(BF)
        qt[:, at] = jnp.transpose(qf).astype(BF)
        dt[:, at] = jnp.transpose(do).astype(BF)
    for r in range(0, 2 * rows, QB):
        at = pl.ds(r, QB)
        kt[:, at] = jnp.transpose(k_ref[at, :].astype(F32)).astype(BF)
    dqt[...] = jnp.zeros(dqt.shape, F32)

    def keys(ks, first, diagonal):
        kk = k_ref[ks, :]
        vv = v_ref[ks, :]
        dv = []
        dk = []
        for h in range(2):
            mine = (lane < 64) if h == 0 else (lane >= 64)
            base = 64 if h == 0 else 0
            ones3 = ((lane >= base) & (lane < base + 3)).astype(BF)
            hs = slice(64 * h, 64 * h + 64)
            st = dot_nt(jnp.where(mine, kk, ones3), qa[h, first:rows, :])
            dp = dot_nt(jnp.where(mine, vv, ones3), da[h, first:rows, :])
            p = jnp.exp(st)
            if diagonal:
                r = lax.broadcasted_iota(jnp.int32, (QB, QB), 0)
                c = lax.broadcasted_iota(jnp.int32, (QB, QB), 1)
                seen = jnp.where(r <= c, p[:, :QB], 0.0)
                p = jnp.concatenate([seen, p[:, QB:]], 1) if first + QB < rows else seen
            ds = (p * dp).astype(BF)
            dv.append(dot_nt(dt[hs, first:rows], p.astype(BF)))
            dk.append(dot_nt(qt[hs, first:rows], ds))
            dqt[hs, first:rows] += dot(kt[hs, ks], ds)
        dvs[ks, :] = jnp.transpose(jnp.concatenate(dv, 0))
        dks[ks, :] = jnp.transpose(jnp.concatenate(dk, 0))

    for j in range(rows // QB):
        keys(pl.ds(rows + j * QB, QB), j * QB, True)

    @pl.when(second)
    def _():
        def step(j, carry):
            keys(pl.ds(pl.multiple_of(j * QB, QB), QB), 0, False)
            return carry

        lax.fori_loop(0, rows // QB, step, 0)

    @pl.when(jnp.logical_not(second))
    def _():
        dks[0:rows, :] = jnp.zeros((rows, 128), F32)
        dvs[0:rows, :] = jnp.zeros((rows, 128), F32)

    for r in range(0, rows, QB):
        dqs[r : r + QB, :] = jnp.transpose(dqt[:, r : r + QB]) * 0.125
    state = state_ref[0]
    sq = conv_back(pq_ref, dqs, xq_ref, rows, (pt_ref, xt_ref), taps_of(small_ref[...], 0), rows, state)
    sk = conv_back(pk_ref, dks, xk_ref, 0, None, taps_of(small_ref[...], 1), rows, state)
    sv = conv_back(pv_ref, dvs, xv_ref, 0, None, taps_of(small_ref[...], 2), rows, state)
    tg_ref[...] = jnp.zeros(tg_ref.shape, F32)
    for j in range(3):
        for m, s in enumerate((sq, sk, sv)):
            tg_ref[3 * j + m : 3 * j + m + 1, :] = s[j]


def att_bwd(state, mixed, attended, logs, grad, projected, small, earlier, part, rows):
    cols = columns(part)
    own = cols(rows, 0, 0)
    both = cols(2 * rows, 0, 0)
    return call_in_parts(
        att_bwd_kernel,
        [
            pl.BlockSpec(memory_space=pltpu.SMEM),
            own, both, both, own, own, own,
            cols(8, rows // 8 - 1, 0),
            cols(rows, 1, 0),
            cols(2 * rows, 0, 6),
            cols(2 * rows, 0, 12),
            cols(16, 0, 0),
        ],
        [own, cols(8, 0, 0), both, both, cols(16, 0, 0)],
        [
            jax.ShapeDtypeStruct((rows, D), BF),
            jax.ShapeDtypeStruct((8, D), BF),
            jax.ShapeDtypeStruct((2 * rows, D), BF),
            jax.ShapeDtypeStruct((2 * rows, D), BF),
            jax.ShapeDtypeStruct((16, D), F32),
        ],
        earlier,
        part,
        scratch_shapes=[
            pltpu.VMEM((2, rows, 128), BF),
            pltpu.VMEM((2, rows, 128), BF),
            pltpu.VMEM((128, rows), BF),
            pltpu.VMEM((128, rows), BF),
            pltpu.VMEM((128, 2 * rows), BF),
            pltpu.VMEM((128, rows), F32),
            pltpu.VMEM((rows, 128), F32),
            pltpu.VMEM((2 * rows, 128), F32),
            pltpu.VMEM((2 * rows, 128), F32),
        ],
        cost_estimate=cost(
            5 * 2 * 2 * rows * rows * 1.5 * 256 * part[1],
            rows * D * 7 * part[1],
            2 * rows * rows * 1.5 * part[1],
        ),
        name="att_bwd",
    )(state, *mixed, attended, logs, grad, projected, projected, projected, projected,
      small, *earlier)


def unit_rows(x):
    return x * lax.rsqrt(jnp.mean(x * x, axis=-1, keepdims=True) + norm_eps)


def before_bwd_kernel(x_ref, dt_ref, dk_ref, dv_ref, w_ref, out_ref, gain_ref):
    i = pl.program_id(0)
    hat = unit_rows(x_ref[...].astype(F32))
    gn = dot_nt(dk_ref[...], w_ref[D : 2 * D, :]) + dot_nt(dv_ref[...], w_ref[2 * D : 3 * D, :])

    last_step = pl.num_programs(0) - 1

    @pl.when(i == 0)
    def _():
        gain_ref[...] = jnp.zeros(gain_ref.shape, F32)

    @pl.when(i < last_step)
    def _():
        out_ref[...] = gn.astype(BF)
        gain_ref[...] += jnp.sum(gn * hat, axis=0, keepdims=True)

    @pl.when(i == last_step)
    def _():
        last = gn.shape[0] - 8
        full = jnp.concatenate([gn[:last], gn[last:] + dot_nt(dt_ref[...], w_ref[0:D, :])], 0)
        out_ref[...] = full.astype(BF)
        gain_ref[...] += jnp.sum(full * hat, axis=0, keepdims=True)


def before_bwd(x_both, back, weight, rows):
    dt, dk, dv = back[1:]
    blocks = 4
    height = rows // blocks
    step = pl.BlockSpec((height, D), lambda i: (i, 0))

    def whole(shape):
        return pl.BlockSpec(shape, lambda i: (0, 0))

    return pl.pallas_call(
        before_bwd_kernel,
        grid=(blocks,),
        in_specs=[step, whole((8, D)), step, step, whole((3 * D, D))],
        out_specs=[step, whole((1, D))],
        out_shape=[jax.ShapeDtypeStruct((rows, D), BF), jax.ShapeDtypeStruct((1, D), F32)],
        compiler_params=pltpu.CompilerParams(vmem_limit_bytes=VMEM_LIMIT),
        cost_estimate=cost(2 * rows * D * D * 2, rows * D * 12),
        name="before_bwd",
    )(x_both, dt, dk, dv, weight)


def qkv_bwd_kernel(
    core_ref, x_ref, dq_ref, dt_ref, dk_ref, dv_ref, w_ref, small_ref, gain_one_ref, gain_two_ref, tg_ref,
    *refs, pieces, blocks,
):
    if pieces:
        send_ref, keep_ref, own_ref, acc, gacc = refs
    else:
        keep_ref, ends_ref, own_ref, acc, gacc = refs
    i = pl.program_id(0)
    half = blocks // 2

    @pl.when(i == 0)
    def _():
        acc[...] = jnp.zeros(acc.shape, F32)
        gacc[0:1, :] = gain_one_ref[...]

    hat = unit_rows(x_ref[...].astype(F32))
    low = (hat * small_ref[0:1, :]).astype(BF)
    dk = dk_ref[...]
    dv = dv_ref[...]
    acc[D : 2 * D, :] += dot_tn(low, dk)
    acc[2 * D : 3 * D, :] += dot_tn(low, dv)

    @pl.when(i == half - 1)
    def _():
        acc[0:D, :] += dot_tn(low[low.shape[0] - 8 :], dt_ref[...])

    @pl.when(i >= half)
    def _():
        dq = dq_ref[...]
        acc[0:D, :] += dot_tn(low, dq)
        full = (
            dot_nt(dk, w_ref[D : 2 * D, :])
            + dot_nt(dv, w_ref[2 * D : 3 * D, :])
            + dot_nt(dq, w_ref[0:D, :])
        )
        own_ref[...] = full
        gacc[0:1, :] += jnp.sum(full * hat, axis=0, keepdims=True)

    @pl.when(i == blocks - 1)
    def _():
        small = jnp.concatenate(
            [gacc[0:1, :], gain_two_ref[...], tg_ref[0:9, :], jnp.zeros((5, D), F32)], 0
        )
        if pieces:
            core = core_ref[0]
            height = 3 * D // (2 * pieces)
            wide = height + 16
            for j in range(pieces):
                to = pl.ds(j * wide, wide)
                away = pl.ds(pl.multiple_of((2 * j + 1 - core) * height, 16), wide)
                here = pl.ds(pl.multiple_of((2 * j + core) * height, 16), wide)
                send_ref[to, :] = acc[away, :].astype(BF)
                keep_ref[to, :] = acc[here, :].astype(BF)
            send_ref[pieces * wide :, :] = small.astype(BF)
            keep_ref[pieces * wide :, :] = small.astype(BF)
        else:
            keep_ref[...] = acc[0 : 3 * D, :].astype(BF)
            ends_ref[...] = small


def qkv_bwd(core, x_both, back, weight, small, gain_one_grad, gain_two_grad, tap_grads, rows, pieces):
    dq, dt, dk, dv = back
    blocks = 4
    half = blocks // 2
    height = 2 * rows // blocks
    step = pl.BlockSpec((height, D), lambda i: (i, 0))
    late = pl.BlockSpec((height, D), lambda i: (jnp.maximum(i - half, 0), 0))

    def whole(shape):
        return pl.BlockSpec(shape, lambda i: (0, 0))

    if pieces:
        packed = 3 * D // 2 + 16 * pieces + 16
        outs = [jax.ShapeDtypeStruct((packed, D), BF), jax.ShapeDtypeStruct((packed, D), BF)]
        out_at = [whole((packed, D))] * 2
    else:
        outs = [jax.ShapeDtypeStruct((3 * D, D), BF), jax.ShapeDtypeStruct((16, D), F32)]
        out_at = [whole((3 * D, D)), whole((16, D))]

    def body(*refs):
        qkv_bwd_kernel(*refs, pieces=pieces, blocks=blocks)

    return pl.pallas_call(
        body,
        grid=(blocks,),
        in_specs=[
            pl.BlockSpec(memory_space=pltpu.SMEM),
            step, late, whole((8, D)), step, step, whole((3 * D, D)),
            whole((16, D)), whole((1, D)), whole((1, D)), whole((16, D)),
        ],
        out_specs=out_at + [late],
        out_shape=outs + [jax.ShapeDtypeStruct((rows, D), F32)],
        scratch_shapes=[pltpu.VMEM((3 * D + 16, D), F32), pltpu.VMEM((8, D), F32)],
        compiler_params=pltpu.CompilerParams(vmem_limit_bytes=VMEM_LIMIT),
        cost_estimate=cost(2 * 2 * D * D * 4 * rows, rows * D * 30),
        name="qkv_bwd",
    )(core, x_both, dq, dt, dk, dv, weight, small, gain_one_grad, gain_two_grad, tap_grads)


def merge(index, keep, got, height, taken):
    rows = keep.shape[0]
    out_rows = taken * height + 16 if taken else rows

    def body(index_ref, keep_ref, got_ref, send_ref, stay_ref):
        if not taken:
            total = keep_ref[...].astype(F32) + got_ref[...].astype(F32)
            send_ref[...] = total.astype(BF)
            stay_ref[...] = total
            return
        for j in range(taken):
            to = pl.ds(j * height, height)
            away = pl.ds(pl.multiple_of(index_ref[j] * height, 16), height)
            here = pl.ds(pl.multiple_of(index_ref[taken + j] * height, 16), height)
            send_ref[to, :] = (keep_ref[away, :].astype(F32) + got_ref[away, :].astype(F32)).astype(BF)
            stay_ref[to, :] = keep_ref[here, :].astype(F32) + got_ref[here, :].astype(F32)
        end = keep_ref[rows - 16 :, :].astype(F32) + got_ref[rows - 16 :, :].astype(F32)
        send_ref[taken * height :, :] = end.astype(BF)
        stay_ref[taken * height :, :] = end

    vmem = pl.BlockSpec(memory_space=pltpu.VMEM)
    return pl.pallas_call(
        body,
        in_specs=[pl.BlockSpec(memory_space=pltpu.SMEM), vmem, vmem],
        out_specs=[vmem, vmem],
        out_shape=[
            jax.ShapeDtypeStruct((out_rows, D), BF),
            jax.ShapeDtypeStruct((out_rows, D), F32),
        ],
        compiler_params=pltpu.CompilerParams(vmem_limit_bytes=32 << 20),
        cost_estimate=cost(rows * D, rows * D * 12),
        name="merge",
    )(index, keep, got)


def merge_grid(index, keep, got, taken, kept=F32):
    height = keep.shape[1]

    def body(index_ref, ka_ref, ga_ref, kb_ref, gb_ref, send_ref, stay_ref):
        send_ref[...] = (ka_ref[...].astype(F32) + ga_ref[...].astype(F32)).astype(BF)
        stay_ref[...] = (kb_ref[...].astype(F32) + gb_ref[...].astype(F32)).astype(kept)

    away = pl.BlockSpec((1, height, D), lambda i, index: (index[i], 0, 0))
    here = pl.BlockSpec((1, height, D), lambda i, index: (index[taken + i], 0, 0))
    step = pl.BlockSpec((1, height, D), lambda i, index: (i, 0, 0))
    return pl.pallas_call(
        body,
        grid_spec=pltpu.PrefetchScalarGridSpec(
            num_scalar_prefetch=1,
            grid=(taken,),
            in_specs=[away, away, here, here],
            out_specs=[step, step],
        ),
        out_shape=[
            pltpu.HBM((taken, height, D), BF),
            pltpu.HBM((taken, height, D), kept),
        ],
        compiler_params=pltpu.CompilerParams(vmem_limit_bytes=32 << 20),
        cost_estimate=cost(taken * height * D * 2, taken * height * D * 16),
        name="merge_grid",
    )(index, keep, got, keep, got)


def arrange(index, blocks):
    height = blocks[0].shape[0] - 16

    def body(index_ref, *refs):
        first_ref, rest_ref, ends, total, sems = refs[4:]
        refs = refs[:4]
        tail = pl.ds(height, 16)
        places = [first_ref.at[pl.ds(0, height)]] + [rest_ref.at[pl.ds(i * height, height)] for i in range(3)]
        for k in range(4):
            pltpu.make_async_copy(refs[k].at[tail], ends.at[k], sems.at[4 + k]).start()
        for i in range(4):
            for k in range(4):

                @pl.when(index_ref[i] == k)
                def _():
                    pltpu.make_async_copy(refs[k].at[pl.ds(0, height)], places[i], sems.at[i]).start()

        for k in range(4):
            pltpu.make_async_copy(refs[k].at[tail], ends.at[k], sems.at[4 + k]).wait()
        sums = [ends[k].astype(F32) for k in range(4)]
        total[...] = (sums[0] + sums[1] + sums[2] + sums[3]).astype(BF)
        last = pltpu.make_async_copy(total, first_ref.at[tail], sems.at[8])
        last.start()
        for i in range(4):
            pltpu.make_async_copy(refs[0].at[pl.ds(0, height)], places[i], sems.at[i]).wait()
        last.wait()

    held = pl.BlockSpec(memory_space=pltpu.HBM)
    return pl.pallas_call(
        body,
        in_specs=[pl.BlockSpec(memory_space=pltpu.SMEM)] + [held] * 4,
        out_specs=[held, held],
        out_shape=[
            jax.ShapeDtypeStruct((height + 16, D), BF),
            jax.ShapeDtypeStruct((3 * height, D), BF),
        ],
        scratch_shapes=[
            pltpu.VMEM((4, 16, D), BF),
            pltpu.VMEM((16, D), BF),
            pltpu.SemaphoreType.DMA((9,)),
        ],
        compiler_params=pltpu.CompilerParams(vmem_limit_bytes=32 << 20),
        cost_estimate=cost(4 * height * D, 4 * height * D * 4),
        name="arrange",
    )(index, *blocks)


def join(own, got, shared=16):
    rows = own.shape[0]
    body_rows = rows - shared

    def body(own_ref, got_ref, out_ref):
        out_ref[0:body_rows, :] = own_ref[0:body_rows, :]
        out_ref[body_rows : 2 * body_rows, :] = got_ref[0:body_rows, :]
        if shared:
            out_ref[2 * body_rows :, :] = own_ref[body_rows:, :] + got_ref[body_rows:, :]

    vmem = pl.BlockSpec(memory_space=pltpu.VMEM)
    return pl.pallas_call(
        body,
        in_specs=[vmem, vmem],
        out_specs=vmem,
        out_shape=jax.ShapeDtypeStruct((2 * body_rows + shared, D), BF),
        compiler_params=pltpu.CompilerParams(vmem_limit_bytes=32 << 20),
        cost_estimate=cost(rows * D, rows * D * 8),
        name="join",
    )(own, got)


def join_held(own, got):
    rows = own.shape[0]
    cuts = 4
    size = rows // cuts

    def body(own_ref, got_ref, out_ref, sems):
        copies = []
        for k, ref in enumerate((own_ref, got_ref)):
            for j in range(cuts):
                source = ref.at[pl.ds(j * size, size)]
                to = out_ref.at[pl.ds(k * rows + j * size, size)]
                copies.append(pltpu.make_async_copy(source, to, sems.at[k * cuts + j]))
        for copy in copies:
            copy.start()
        for copy in copies:
            copy.wait()

    held = pl.BlockSpec(memory_space=pltpu.HBM)
    return pl.pallas_call(
        body,
        in_specs=[held, held],
        out_specs=held,
        out_shape=jax.ShapeDtypeStruct((2 * rows, D), BF),
        scratch_shapes=[pltpu.SemaphoreType.DMA((2 * cuts,))],
        compiler_params=pltpu.CompilerParams(vmem_limit_bytes=16 << 20),
        cost_estimate=cost(0, rows * D * 8),
        name="join_held",
    )(own, got)


def hold(block, other):
    held = pl.BlockSpec(memory_space=pl.ANY)
    return pl.pallas_call(
        lambda block_ref, other_ref, out_ref: None,
        in_specs=[held, held],
        out_specs=held,
        out_shape=jax.ShapeDtypeStruct(block.shape, block.dtype),
        input_output_aliases={0: 0},
        name="hold",
    )(block, other)


def qkv_fwd_kernel(index_ref, x_ref, *refs, pieces, blocks):
    if pieces:
        own_ref, got_ref, out_ref, small_ref, weight = refs
    else:
        weight, given_ref, out_ref, small_ref = refs
    i = pl.program_id(0)

    @pl.when(i == 0)
    def _():
        if pieces:
            height = 3 * D // (2 * pieces)
            for j in range(pieces):
                at = pl.ds(j * height, height)
                for k, ref in enumerate((own_ref, got_ref)):
                    to = pl.multiple_of(index_ref[k * pieces + j] * height, 16)
                    weight[pl.ds(to, height), :] = ref[at, :]
            end = pl.ds(pieces * height, 16)
            small_ref[...] = own_ref[end, :].astype(F32) + got_ref[end, :].astype(F32)
        else:
            small_ref[...] = given_ref[...]

    x = x_ref[...].astype(F32)
    hat = x * lax.rsqrt(jnp.mean(x * x, axis=-1, keepdims=True) + norm_eps)
    low = (hat * small_ref[0:1, :]).astype(BF)

    @pl.when(i >= blocks // 2 - 1)
    def _():
        out_ref[:, 0:D] = dot(low, weight[0:D, :]).astype(BF)

    out_ref[:, D : 2 * D] = dot(low, weight[D : 2 * D, :]).astype(BF)
    out_ref[:, 2 * D : 3 * D] = dot(low, weight[2 * D : 3 * D, :]).astype(BF)


def qkv_fwd(index, x_both, weights, rows, pieces):
    blocks = 4
    height = 2 * rows // blocks

    def body(*refs):
        qkv_fwd_kernel(*refs, pieces=pieces, blocks=blocks)

    return pl.pallas_call(
        body,
        grid=(blocks,),
        in_specs=[
            pl.BlockSpec(memory_space=pltpu.SMEM),
            pl.BlockSpec((height, D), lambda i: (i, 0)),
            *[pl.BlockSpec(w.shape, lambda i: (0, 0)) for w in weights],
        ],
        out_specs=[
            pl.BlockSpec((height, 3 * D), lambda i: (i, 0)),
            pl.BlockSpec((16, D), lambda i: (0, 0)),
        ]
        + ([pl.BlockSpec((3 * D, D), lambda i: (0, 0))] if pieces else []),
        out_shape=[
            jax.ShapeDtypeStruct((2 * rows, 3 * D), BF),
            jax.ShapeDtypeStruct((16, D), F32),
        ]
        + ([jax.ShapeDtypeStruct((3 * D, D), BF)] if pieces else []),
        compiler_params=pltpu.CompilerParams(vmem_limit_bytes=VMEM_LIMIT),
        cost_estimate=cost(2 * 2 * rows * D * 3 * D, rows * D * 20),
        name="qkv_fwd",
    )(index, x_both, *weights)


def ffn_kernel(
    state_ref, index_ref, x_ref, att_ref, cot_ref, small_ref, own_ref, own_two_ref, got_ref, got_two_ref,
    out_ref, gh_ref, ga_ref, gain_grad_ref, away_ref, here_ref,
    hidden, low, total, back, cot, sq, gb, weights, stage_up, stage_down, stage_out, in_sems, sems,
):
    c = pl.program_id(0)
    rows = x_ref.shape[0]
    blocks = [pl.ds(i * QB, QB) for i in range(rows // QB)]
    last = c == pl.num_programs(0) - 1
    core = index_ref[24]

    def fetch(k, j):
        ref = ((own_ref, own_two_ref), (got_ref, got_two_ref))[k][j // 6]
        piece = index_ref[12 * k + j]
        to = weights.at[pl.ds(3 * piece, 3)]
        return pltpu.make_async_copy(ref.at[pl.ds(3 * (j % 6), 3)], to, in_sems.at[piece])

    def fetched(pieces):
        for piece in pieces:
            at = weights.at[pl.ds(3 * piece, 3)]
            pltpu.make_async_copy(own_ref.at[pl.ds(0, 3)], at, in_sems.at[piece]).wait()

    def put(source, group, count, column, sem, wait=False):
        piece = group // 3
        at = (piece // 2) * 3 + group % 3

        def copy(ref):
            to = ref.at[pl.ds(at, count)] if column is None else ref.at[pl.ds(at, count), column]
            return pltpu.make_async_copy(source, to, sems.at[sem])

        if wait:
            copy(here_ref).wait()
            return
        mine = piece % 2 == core

        @pl.when(mine)
        def _():
            copy(here_ref).start()

        @pl.when(jnp.logical_not(mine))
        def _():
            copy(away_ref).start()

    def put_up(i, wait=False):
        start = 0
        k = 0
        while start < 32:
            count = min(3 - (8 + start) % 3, 32 - start)
            put(stage_up.at[i, pl.ds(start, count)], 8 + start, count, i, 20 * i + k, wait)
            start += count
            k += 1

    def put_down(i, wait=False):
        for k in range(8):
            put(stage_down.at[i, pl.ds(k, 1)], 40 + 8 * i + k, 1, None, 20 * i + 12 + k, wait)

    def put_out(wait=False):
        for k in range(8):
            put(stage_out.at[pl.ds(k, 1)], k, 1, None, 80 + k, wait)

    def square(first):
        return weights[first : first + 8].reshape(D, D)

    @pl.when(c == 0)
    def _():
        for early in (True, False):
            for k in range(2):
                for j in range(12):

                    @pl.when((index_ref[12 * k + j] < 3) == early)
                    def _():
                        fetch(k, j).start()

        cot[...] = jnp.where(state_ref[0] > 0, cot_ref[...], jnp.zeros((), BF))
        total[...] = jnp.zeros(total.shape, F32)
        back[...] = jnp.zeros(back.shape, F32)
        fetched(range(3))
        wo = square(0)
        for b in blocks:
            h = x_ref[b, :].astype(F32) + dot(att_ref[b, :], wo)
            hidden[b, :] = h
            hat = h * lax.rsqrt(jnp.mean(h * h, axis=-1, keepdims=True) + norm_eps)
            low[b, :] = (hat * small_ref[1:2, :]).astype(BF)

    for i, pieces in enumerate((range(3, 16), range(16, 19), range(19, 22), range(22, 24))):

        @pl.when(c == i)
        def _():
            fetched(pieces)

    up = weights[8:40, c].reshape(D, D)
    down = weights[pl.ds(40 + 8 * c, 8)].reshape(D, D)
    for b in blocks:
        act = jnp.maximum(dot(low[b, :], up), 0.0)
        s = (act * act).astype(BF)
        sq[b, :] = s
        total[b, :] += dot(s, down)
        g = (dot_nt(cot[b, :], down) * 2.0 * act).astype(BF)
        gb[b, :] = g
        back[b, :] += dot_nt(g, up)
    stage_down[c] = dot_tn(sq[...], cot[...]).reshape(8, 4, 24, D).astype(BF)
    stage_up[c] = dot_tn(low[...], gb[...]).reshape(32, 24, D).astype(BF)
    put_down(c)
    put_up(c)

    @pl.when(last)
    def _():
        gain = small_ref[1:2, :]
        wo = square(0)
        sums = jnp.zeros((1, D), F32)
        for b in blocks:
            h = hidden[b, :]
            out_ref[b, :] = (h + total[b, :]).astype(BF)
            factor = lax.rsqrt(jnp.mean(h * h, axis=-1, keepdims=True) + norm_eps)
            hat = h * factor
            g = back[b, :]
            sums = sums + jnp.sum(g * hat, axis=0, keepdims=True)
            weighted = g * gain
            inner = jnp.mean(weighted * hat, axis=-1, keepdims=True)
            grad = cot[b, :].astype(F32) + factor * (weighted - hat * inner)
            gh_ref[b, :] = grad
            grad_low = grad.astype(BF)
            gb[b, :] = grad_low
            ga_ref[b, :] = dot_nt(grad_low, wo).astype(BF)
        gain_grad_ref[...] = sums
        stage_out[...] = dot_tn(att_ref[...], gb[...]).reshape(8, 4, 24, D).astype(BF)
        put_out()
        for i in range(4):
            put_down(i, True)
            put_up(i, True)
        put_out(True)


def ffn(state, index, tokens, attended, out_grad, small, weights, rows):
    def whole(shape):
        return pl.BlockSpec(shape, lambda c: (0,) * len(shape), pipeline_mode=pl.Buffered(1))

    act = whole((rows, D))
    held = pl.BlockSpec(memory_space=pl.ANY)
    scalars = pl.BlockSpec(memory_space=pltpu.SMEM)
    half = (36, 4, 24, D)
    return pl.pallas_call(
        ffn_kernel,
        grid=(4,),
        in_specs=[scalars, scalars, act, act, act, whole((16, D)), held, held, held, pl.BlockSpec(memory_space=pltpu.VMEM)],
        out_specs=[act, act, act, whole((1, D)), held, held],
        out_shape=[
            jax.ShapeDtypeStruct((rows, D), BF),
            jax.ShapeDtypeStruct((rows, D), F32),
            jax.ShapeDtypeStruct((rows, D), BF),
            jax.ShapeDtypeStruct((1, D), F32),
            jax.ShapeDtypeStruct(half, BF),
            jax.ShapeDtypeStruct(half, BF),
        ],
        scratch_shapes=[
            pltpu.VMEM((rows, D), F32),
            pltpu.VMEM((rows, D), BF),
            pltpu.VMEM((rows, D), F32),
            pltpu.VMEM((rows, D), F32),
            pltpu.VMEM((rows, D), BF),
            pltpu.VMEM((rows, D), BF),
            pltpu.VMEM((rows, D), BF),
            pltpu.VMEM((72, 4, 24, D), BF),
            pltpu.VMEM((4, 32, 24, D), BF),
            pltpu.VMEM((4, 8, 4, 24, D), BF),
            pltpu.VMEM((8, 4, 24, D), BF),
            pltpu.SemaphoreType.DMA((24,)),
            pltpu.SemaphoreType.DMA((88,)),
        ],
        compiler_params=pltpu.CompilerParams(vmem_limit_bytes=60 << 20),
        cost_estimate=cost(2 * rows * D * D * (24 + 3), 2 * 12 * D * D * 2 + rows * D * 16),
        name="ffn",
    )(state, index, tokens, attended, out_grad, small, *weights)


def shift_flat(block, distance):
    count = lax.axis_size(AXES)
    route = [(i - distance, i) for i in range(count) if 0 <= i - distance < count]
    return lax.ppermute(block, AXES, route)


def shift_ctx(block, distance):
    count = lax.axis_size("ctx")
    route = [(i - distance, i) for i in range(count) if 0 <= i - distance < count]
    return lax.ppermute(block, "ctx", route)


def after(value, *others):
    return lax.optimization_barrier((value, *others))[0]


def swap(block, even_bit, odd_bit, planes=None):
    count = lax.axis_size(AXES)
    route = [
        (i, i ^ (odd_bit if i & 1 else even_bit))
        for i in range(count)
        if planes is None or i >> 3 in planes
    ]
    return lax.ppermute(block, AXES, route)


def to_aligned(shard, place, count, delta):
    rows = shard.shape[0]
    lag = delta * (count - 1)
    back = -(-lag // rows)
    if back == 1:
        keep = -(-lag // 8) * 8
        parts = [shift_flat(shard[rows - keep :], 1), shard]
    else:
        keep = back * rows
        parts = [shift_flat(shard, s) for s in range(back, 0, -1)] + [shard]
    joined = jnp.concatenate(parts, 0)
    return lax.dynamic_slice_in_dim(joined, keep - delta * place, rows - delta, 0)


def small_part(shard, place, count, delta):
    rows = shard.shape[0]
    extra = count * delta
    zeros = jnp.zeros((extra, 128), shard.dtype)
    joined = jnp.concatenate([zeros, shard, zeros], 0)
    start = extra + count * (rows - delta) - place * rows
    return lax.dynamic_slice_in_dim(joined, jnp.minimum(start, rows + extra), extra, 0)


def from_aligned(chunk, small, place, count, delta, rows):
    aligned = rows - delta
    ahead = -(-(count * delta) // aligned)
    parts = [chunk]
    if ahead == 1:
        keep = small.shape[0]
        got = shift_flat(chunk[:keep], -1)
        parts.append(jnp.where(place == count - 1, small, got))
    else:
        pad = ahead * aligned - small.shape[0]
        tail = jnp.concatenate([small, jnp.zeros((pad, 128), small.dtype)], 0)
        for s in range(1, ahead + 1):
            got = shift_flat(chunk, -s)
            for e in range(s):
                piece = tail[e * aligned : (e + 1) * aligned]
                got = jnp.where(place == count - s + e, piece, got)
            parts.append(got)
    return lax.dynamic_slice_in_dim(jnp.concatenate(parts, 0), delta * place, rows, 0)


def regroup(block):
    return block.reshape(-1, 24, 4, D).transpose(0, 2, 1, 3)


def ungroup(block):
    return block.reshape(-1, 4, 24, D).transpose(0, 2, 1, 3)


def normalize(values, gain):
    factor = lax.rsqrt(jnp.mean(values * values, axis=-1, keepdims=True) + norm_eps)
    scaled = values * factor
    return (scaled, factor, scaled * gain)


def norm_back(grad_in, scaled, factor, gain):
    weighted = grad_in * gain
    inner_mean = jnp.mean(weighted * scaled, axis=-1, keepdims=True)
    return factor * (weighted - scaled * inner_mean)


def adam_update(master, moment_one, moment_two, gradient, step_count, row_start):
    row_index = row_start + jnp.arange(master.shape[0], dtype=jnp.int32)
    matrix_rows = (4 * D * D + 2 * D * FF) // 128
    out_first = 3 * D * D // 128
    out_last = 4 * D * D // 128
    is_matrix = (row_index < matrix_rows)[:, None]
    is_out = ((row_index >= out_first) & (row_index < out_last))[:, None]
    step_rate = jnp.where(is_matrix, jnp.where(is_out, 0.5, 0.1), 1.0)
    decay_rate = jnp.where(is_matrix, 0.1, 0.0)
    step_value = step_count[0].astype(jnp.float32)
    new_one = 0.9 * moment_one + 0.1 * gradient
    new_two = 0.999 * moment_two + 0.001 * gradient * gradient
    corr_first = 1.0 - jnp.power(0.9, step_value)
    corr_second = 1.0 - jnp.power(0.999, step_value)
    new_weights = master - step_rate * (
        new_one / corr_first / (jnp.sqrt(new_two / corr_second) + 1e-08) + decay_rate * master
    )
    return (new_weights, new_one, new_two)


def shards(tokens, out_grad, positions, master, first_moment, second_moment, step_count):
    rows = tokens.shape[0]
    assert rows == SEQ_MIN
    count = lax.axis_size(AXES)
    place = lax.axis_index(AXES).astype(jnp.int32)
    owned = master.shape[0]
    aligned = (4 * D * D + 2 * D * FF) // 128 // count
    delta = owned - aligned
    height = aligned * 128 // D
    staged = count == 32
    first_place = positions[0]
    state = jnp.where(first_place < 0, 0, jnp.where(first_place >= SEQ_MIN, 2, 1)).astype(jnp.int32)
    state_vec = state[None]

    chunk = to_aligned(master, place, count, delta).reshape(-1, D)
    if staged:
        group = 3 * place + jnp.arange(3, dtype=jnp.int32)
        in_up = ((group >= 32) & (group < 64))[:, None, None, None]
        chunk = jnp.where(in_up, regroup(chunk), chunk.reshape(3, 4, 24, D)).reshape(-1, D)
    chunk = chunk.astype(BF)
    if staged:
        small = jnp.where(place == count - 1, master[owned - count * delta :], 0.0)
    else:
        small = small_part(master, place, count, delta)
    small = lax.reduce_precision(small, 8, 7)
    core = (place & 1)[None]
    x_bit = (place >> 1) & 1
    y_bit = (place >> 2) & 1
    even = (place & 1) == 0
    if staged:
        z = place >> 3
        mine = jnp.concatenate([chunk, small.astype(BF).reshape(-1, D)], 0)
        tokens_before = shift_ctx(after(tokens, mine), 1)
        far = swap(mine, 16, 16)
        near = swap(mine, 8, 8)
        tokens_both = jnp.concatenate([tokens_before, tokens], 0)
        both = swap(after(far, tokens_both), 8, 8)
        order = jnp.stack([z, z ^ 1, z ^ 2, z ^ 3]).astype(jnp.int32)
        mine, rest = arrange(after(order, state_vec), (mine, near, far, both))
        mine = join(mine, swap(mine, 2, 4))
        mine = join(mine, swap(mine, 4, 2))
        across = swap(rest, 2, 4)
        got = swap(mine, 1, 1)
        index = []
        late_index = []
        for k in (0, 1):
            turn = even if k == 0 else jnp.logical_not(even)
            for j in range(4):
                near, far = j & 1, j >> 1
                x_of = x_bit ^ jnp.where(turn, near, far)
                y_of = y_bit ^ jnp.where(turn, far, near)
                piece = 4 * y_of + 2 * x_of + (core[0] ^ k)
                index.append(piece)
                late_index += [piece, piece + 8, piece + 16]
        index = jnp.stack(index).astype(jnp.int32)
        late_index = jnp.stack(late_index + [core[0]]).astype(jnp.int32)
        projected, small, in_weight = qkv_fwd(index, tokens_both, (mine, got), rows, 4)
    else:
        tokens_both = jnp.concatenate([shift_ctx(tokens, 1), tokens], 0)
        wide = lax.all_gather(chunk, AXES, axis=0, tiled=True)
        small = lax.psum(small, AXES)[:96].reshape(-1, D)
        in_weight = wide[: 3 * D]
        projected, small = qkv_fwd(core, tokens_both, (in_weight, small), rows, 0)
        late_index = jnp.arange(25, dtype=jnp.int32) % 24
    gain_first = small[0]

    forward = []
    if staged:
        rest = join_held(after(rest, projected), across)
        line = swap(rest, 4, 2)
        core_rest = swap(rest, 1, 1)
        forward = att_fwd(after(state_vec, rest), projected, small, forward, FORWARD_PARTS[0], rows)
        forward = att_fwd(after(state_vec, core_rest), projected, small, forward, FORWARD_PARTS[1], rows)
        line = hold(line, forward[0])
        core_line = swap(line, 1, 1)
        forward = att_fwd(after(state_vec, line), projected, small, forward, FORWARD_PARTS[2], rows)
        late_weights = [w.reshape(18, 4, 24, D) for w in (rest, line, core_rest, core_line)]
    else:
        for part in FORWARD_PARTS:
            forward = att_fwd(state_vec, projected, small, forward, part, rows)
        grouped = jnp.concatenate(
            [
                wide[3 * D : 4 * D].reshape(-1, 4, 24, D),
                regroup(wide[4 * D : 8 * D]),
                wide[8 * D :].reshape(-1, 4, 24, D),
            ],
            0,
        )
        late_weights = [grouped[18 * k : 18 * k + 18] for k in range(4)]
    attn_low, logs, *mixed = forward

    layer_out, grad_hidden, grad_attended, grad_gain_two, away_grad, here_grad = ffn(
        state_vec, late_index, tokens, attn_low, out_grad, small, late_weights, rows
    )

    def backward(start, done, part):
        return att_bwd(
            start, mixed, attn_low, logs, grad_attended, projected, small, done, BACKWARD_PARTS[part], rows
        )

    if staged:
        stay = [jnp.where(even, 2 * j + x_bit, 2 * y_bit + j) for j in range(2)]
        away = [jnp.where(even, 2 * j + 1 - x_bit, 2 * (1 - y_bit) + j) for j in range(2)]
        pick_plane = jnp.stack(away + stay).astype(jnp.int32)
        other = jnp.where(even, y_bit, x_bit)
        pick_line = jnp.stack([1 - other, other]).astype(jnp.int32)

        def of_quarters(pick, held):
            half = pick.shape[0] // 2
            steps = [pick[s * half + j] + held * t for s in range(2) for t in range(3) for j in range(half)]
            return jnp.stack(steps)

        late_keep = here_grad.reshape(12, height, D)
        late_got = swap(away_grad.reshape(12, height, D), 1, 1)
        done = backward(state_vec, [], 0)
        late_send, late_keep = merge_grid(
            after(of_quarters(pick_plane, 4), done[4]), late_keep, late_got, 6, BF
        )
        late_got = swap(late_send, 2, 4)
        done = backward(after(state_vec, late_send), done, 1)
        late_send, late_keep = merge_grid(
            after(of_quarters(pick_line, 2), done[4]), late_keep, late_got, 3
        )
        late_got = swap(late_send, 4, 2)
        done = backward(after(state_vec, late_send), done, 2)
        z_even = (z & 1) == 0
        low_pair = [jnp.where(z_even, 0, 0), jnp.where(z_even, 2, 1)]
        high_pair = [jnp.where(z_even, 0, 0), jnp.where(z_even, 1, 2)]
        pick_z = jnp.stack(low_pair + high_pair).astype(jnp.int32)
        late_send, late_keep = merge_grid(after(pick_z, done[4]), late_keep, late_got, 2)
        late_got = swap(late_send, 8, 8)
        done = backward(after(state_vec, late_send), done, 3)
        high = z >> 1
        pick_last = jnp.stack([1 - high, high]).astype(jnp.int32)
        late_send, late_keep = merge_grid(after(pick_last, done[4]), late_keep, late_got, 1)
        late_got = swap(late_send, 16, 16, (0, 1, 3))
        sums_state = after(core, late_send)
    else:
        done = []
        for part in range(4):
            done = backward(state_vec, done, part)
        sums_state = core
    *back, tap_grads = done
    grads_before, gain_one_grad = before_bwd(tokens_both, back, in_weight, rows)
    from_next = shift_ctx(grads_before, -1)
    sums = qkv_bwd(
        after(sums_state, grads_before), tokens_both, back, in_weight, small, gain_one_grad, grad_gain_two, tap_grads, rows,
        4 if staged else 0,
    )
    grad_normed_one = sums[2]
    scaled_one, factor_one, _ = normalize(tokens.astype(F32), gain_first)
    input_grad = grad_hidden + norm_back(
        grad_normed_one + from_next.astype(F32), scaled_one, factor_one, gain_first
    )

    if staged:
        send, keep = sums[:2]
        got = swap(after(send, late_got, from_next), 1, 1)
        send, keep = merge(pick_plane, keep, got, height + 16, 2)
        got = swap(send, 2, 4)
        late_got = after(late_got, send)
        late_chunk = late_keep[0] + late_got[0].astype(F32)
        late_chunk = jnp.where(in_up, ungroup(late_chunk).reshape(3, 4, 24, D), late_chunk.reshape(3, 4, 24, D))
        late_chunk = late_chunk.reshape(-1, D)
        late_next = shift_flat(late_chunk[:16], -1)
        send, keep = merge(after(pick_line, late_chunk), keep, got, height + 16, 1)
        got = swap(send, 4, 2)
        send, keep = merge(core, keep, got, height + 16, 0)
        got = swap(send, 8, 8)
        send, keep = merge(after(core, input_grad, late_next), keep, got, height + 16, 0)
        got = swap(send, 16, 16, (1, 2))
        first = keep + got.astype(F32)
        quarter = count // 4
        follow = jnp.where(place < quarter - 1, first[height : height + 16], late_next)
        follow = jnp.where(place == count - 1, first[height + 16 :], follow)
        chunk_grad = jnp.where(place < quarter, first[:height], late_chunk)
        chunk_grad = jnp.concatenate([chunk_grad, follow], 0).reshape(-1, 128)
        gradient = lax.dynamic_slice_in_dim(chunk_grad, delta * place, owned, 0)
    else:
        flat_grad = jnp.stack([here_grad.reshape(12, 3, 4, 24, D), away_grad.reshape(12, 3, 4, 24, D)], 1)
        flat_grad = flat_grad.reshape(72, 4, 24, D)
        wide_grad = jnp.concatenate(
            [
                sums[0],
                flat_grad[:8].reshape(-1, D),
                ungroup(flat_grad[8:40]).reshape(-1, D),
                flat_grad[40:].reshape(-1, D),
            ],
            0,
        )
        chunk_grad = lax.psum_scatter(wide_grad, AXES, scatter_dimension=0, tiled=True).astype(F32)
        used = sums[1].reshape(-1, 128)
        extra = count * delta
        small_grad = jnp.concatenate([used, jnp.zeros((extra - used.shape[0], 128), F32)], 0)
        small_grad = lax.psum(small_grad, AXES)
        gradient = from_aligned(chunk_grad.reshape(-1, 128), small_grad, place, count, delta, owned)
    new_weights, new_one, new_two = adam_update(
        master, first_moment, second_moment, gradient, step_count, place * owned
    )
    return (layer_out, input_grad, new_weights, new_one, new_two, new_weights.astype(BF))


def solution(mesh):
    spread = P(AXES, None)
    return jax.shard_map(
        shards,
        mesh=mesh,
        in_specs=(spread, spread, P(AXES), spread, spread, spread, P()),
        out_specs=(spread,) * 6,
        check_vma=False,
    )
```

```python
import jax
import jax.numpy as jnp
from jax import lax
from jax.experimental import pallas as pl
from jax.experimental.pallas import tpu as pltpu
from jax.sharding import PartitionSpec as P

D = 768
HEADS = 12
HEAD_DIM = 64
FF = 3072
SEQ_MIN = 1024
AXES = ("dp", "ctx")
QB = 256
FORWARD_PARTS = ((0, 2), (2, 2), (4, 2))
BACKWARD_PARTS = ((0, 1), (1, 3), (4, 1), (5, 1))
F32 = jnp.float32
BF = jnp.bfloat16
NT = (((1,), (1,)), ((), ()))
TN = (((0,), (0,)), ((), ()))
norm_eps = 1e-06
VMEM_LIMIT = 56 << 20


def dot(left, right):
    return jnp.dot(left, right, preferred_element_type=F32)


def dot_nt(left, right):
    return lax.dot_general(left, right, NT, preferred_element_type=F32)


def dot_tn(left, right):
    return lax.dot_general(left, right, TN, preferred_element_type=F32)


def cost(flops, nbytes, exps=0):
    return pl.CostEstimate(flops=int(flops), bytes_accessed=int(nbytes), transcendentals=int(exps))


def taps_of(small, matrix):
    return [small[2 + 3 * j + matrix : 3 + 3 * j + matrix, :] for j in range(3)]


def row_ids(height):
    return lax.broadcasted_iota(jnp.int32, (height, 128), 0)


def conv(out_ref, x_ref, start, tail_ref, taps, rows, state):
    height = x_ref.shape[0]
    for r in range(0, height, QB):
        at = start + r
        if r:
            x = x_ref[r - 16 : r + QB, :].astype(F32)
        else:
            before = jnp.zeros((16, 128), F32)
            if tail_ref is not None:
                before = jnp.concatenate([before[8:], tail_ref[...].astype(F32)], 0)
            x = jnp.concatenate([before, x_ref[0:QB, :].astype(F32)], 0)
        one = pltpu.roll(x, 1, 0)[16:]
        two = pltpu.roll(x, 2, 0)[16:]
        x = x[16:]
        scale = 1.0
        if at >= rows:
            scale = jnp.where(state > 0, 1.0, 0.0)
        if at == 0 or at == rows:
            seen = jnp.where(state == 2, 1.0, 0.0) if at else 0.0
            row = row_ids(QB)
            one = jnp.where(row < 1, one * seen, one)
            two = jnp.where(row < 2, two * seen, two)
        c_one = taps[1] * scale
        c_two = taps[2] * scale
        out_ref[r : r + QB, :] = (taps[0] * x + c_one * one + c_two * two).astype(BF)


def att_fwd_kernel(
    state_ref, tail_ref, q_ref, k_ref, v_ref, small_ref,
    o_ref, l_ref, qm_ref, km_ref, vm_ref, ka, va,
):
    rows = q_ref.shape[0]
    lane = lax.broadcasted_iota(jnp.int32, (1, 128), 1)
    state = state_ref[0]
    conv(qm_ref, q_ref, rows, tail_ref, taps_of(small_ref[...], 0), rows, state)
    conv(km_ref, k_ref, 0, None, taps_of(small_ref[...], 1), rows, state)
    conv(vm_ref, v_ref, 0, None, taps_of(small_ref[...], 2), rows, state)
    bias = jnp.where(state == 2, 0.0, -1e30)
    for h in range(2):
        mine = (lane < 64) if h == 0 else (lane >= 64)
        base = 64 if h == 0 else 0
        first = jnp.where(lane == base, bias, 0.0).astype(BF)
        for r in range(0, 2 * rows, QB):
            at = pl.ds(r, QB)
            ka[h, at, :] = jnp.where(mine, km_ref[at, :], first if r < rows else jnp.zeros((), BF))
            va[h, at, :] = jnp.where(mine, vm_ref[at, :], jnp.ones((), BF))
    heads = (row_ids(128) < 64) == (lane < 64)
    heads = heads.astype(BF)
    q_most = jnp.zeros((1, 128), F32)
    k_most = jnp.zeros((1, 128), F32)
    for r in range(0, rows, QB):
        q = qm_ref[r : r + QB, :].astype(F32) * 0.125
        q_most = jnp.maximum(q_most, jnp.max(dot((q * q).astype(BF), heads), axis=0, keepdims=True))
    for r in range(0, 2 * rows, QB):
        k = km_ref[r : r + QB, :].astype(F32)
        k_most = jnp.maximum(k_most, jnp.max(dot((k * k).astype(BF), heads), axis=0, keepdims=True))
    small_scores = jnp.max(q_most * k_most) <= 3025.0

    def attend(subtract):
        for i in range(rows // QB):
            rs = pl.ds(i * QB, QB)
            outs = []
            sums = []
            qf = qm_ref[rs, :].astype(F32) * 0.125
            for h in range(2):
                mine = (lane < 64) if h == 0 else (lane >= 64)
                base = 64 if h == 0 else 0
                qh = jnp.where(mine, qf, jnp.where(lane == base, 1.0, 0.0)).astype(BF)
                nk = rows + (i + 1) * QB
                s = dot_nt(qh, ka[h, 0:nk, :])
                r = lax.broadcasted_iota(jnp.int32, (QB, QB), 0)
                c = lax.broadcasted_iota(jnp.int32, (QB, QB), 1)
                sd = jnp.where(c <= r, s[:, nk - QB :], -1e30)
                se = s[:, : nk - QB]
                if subtract:
                    m = jnp.maximum(
                        jnp.max(sd, axis=1, keepdims=True), jnp.max(se, axis=1, keepdims=True)
                    )
                    se = se - m
                    sd = sd - m
                p = jnp.concatenate([jnp.exp(se).astype(BF), jnp.exp(sd).astype(BF)], 1)
                o = dot(p, va[h, 0:nk, :])
                outs.append(o / pltpu.roll(o, 64, 1))
                sums.append(m + jnp.log(o) if subtract else jnp.log(o))
            res = jnp.where(lane < 64, outs[0], outs[1])
            res = jnp.where(state == 0, vm_ref[pl.ds(rows + i * QB, QB), :].astype(F32), res)
            o_ref[rs, :] = res.astype(BF)
            l_ref[rs, :] = jnp.where(lane < 64, sums[1], sums[0])

    @pl.when(small_scores)
    def _():
        attend(False)

    @pl.when(jnp.logical_not(small_scores))
    def _():
        attend(True)


def call_in_parts(body, in_specs, out_specs, out_shape, earlier, part, **options):
    used = len(in_specs)

    def kernel(*refs):
        body(*refs[:used], *refs[used + len(earlier) :])

    return pl.pallas_call(
        kernel,
        grid=(part[1],),
        in_specs=in_specs + [pl.BlockSpec(memory_space=pl.ANY)] * len(earlier),
        out_specs=out_specs,
        out_shape=out_shape,
        input_output_aliases={used + i: i for i in range(len(earlier))},
        compiler_params=pltpu.CompilerParams(vmem_limit_bytes=VMEM_LIMIT),
        **options,
    )


def columns(part):
    first = part[0]

    def cols(height, row, off):
        return pl.BlockSpec((height, 128), lambda p: (row, p + first + off))

    return cols


def att_fwd(state, projected, small, earlier, part, rows):
    cols = columns(part)
    return call_in_parts(
        att_fwd_kernel,
        [
            pl.BlockSpec(memory_space=pltpu.SMEM),
            cols(8, rows // 8 - 1, 0),
            cols(rows, 1, 0),
            cols(2 * rows, 0, 6),
            cols(2 * rows, 0, 12),
            cols(16, 0, 0),
        ],
        [cols(rows, 0, 0)] * 3 + [cols(2 * rows, 0, 0)] * 2,
        [
            jax.ShapeDtypeStruct((rows, D), BF),
            jax.ShapeDtypeStruct((rows, D), F32),
            jax.ShapeDtypeStruct((rows, D), BF),
            jax.ShapeDtypeStruct((2 * rows, D), BF),
            jax.ShapeDtypeStruct((2 * rows, D), BF),
        ],
        earlier,
        part,
        scratch_shapes=[pltpu.VMEM((2, 2 * rows, 128), BF)] * 2,
        cost_estimate=cost(
            2 * 2 * 2 * rows * rows * 1.5 * 256 * part[1],
            rows * D * 5 * part[1],
            2 * rows * rows * 1.5 * part[1],
        ),
        name="att_fwd",
    )(state, projected, projected, projected, projected, small, *earlier)


def three(x, lane, base):
    hi = x.astype(BF).astype(F32)
    r = x - hi
    mid = r.astype(BF).astype(F32)
    lo = r - mid
    return jnp.where(
        lane == base, hi, jnp.where(lane == base + 1, mid, jnp.where(lane == base + 2, lo, 0.0))
    )


def conv_back(out_ref, grad_ref, x_ref, start, tail, taps, rows, state):
    height = grad_ref.shape[0]
    joint = jnp.where(state == 2, 1.0, 0.0)
    sums = [jnp.zeros((1, 128), F32)] * 3

    def add(parts, x):
        return [s + jnp.sum(g * x, axis=0, keepdims=True) for s, g in zip(sums, parts)]

    for r in range(0, height, QB):
        ends = r + QB == height
        meets = start + r + QB == rows
        if ends:
            grad = jnp.concatenate([grad_ref[r : r + QB, :], jnp.zeros((8, 128), F32)], 0)
        else:
            grad = grad_ref[r : r + QB + 8, :]
        one = pltpu.roll(grad, QB + 7, 0)[:QB]
        two = pltpu.roll(grad, QB + 6, 0)[:QB]
        grad = grad[:QB]
        if meets and not ends:
            row = row_ids(QB)
            one = jnp.where(row >= QB - 1, one * joint, one)
            two = jnp.where(row >= QB - 2, two * joint, two)
        out_ref[r : r + QB, :] = (taps[0] * grad + taps[1] * one + taps[2] * two).astype(BF)
        sums = add((grad, one, two), x_ref[r : r + QB, :].astype(F32))
    if tail is not None:
        grad = jnp.concatenate([jnp.zeros((8, 128), F32), grad_ref[0:8, :]], 0)
        one = pltpu.roll(grad, 15, 0)[:8] * joint
        two = pltpu.roll(grad, 14, 0)[:8] * joint
        tail[0][...] = (taps[1] * one + taps[2] * two).astype(BF)
        sums = add((grad[:8], one, two), tail[1][...].astype(F32))
    return sums


def att_bwd_kernel(
    state_ref, q_ref, k_ref, v_ref, o_ref, l_ref, do_ref, xt_ref, xq_ref, xk_ref, xv_ref,
    small_ref,
    pq_ref, pt_ref, pk_ref, pv_ref, tg_ref, qa, da, qt, dt, kt, dqt, dqs, dks, dvs,
):
    rows = q_ref.shape[0]
    lane = lax.broadcasted_iota(jnp.int32, (1, 128), 1)
    second = state_ref[0] == 2
    for r in range(0, rows, QB):
        at = pl.ds(r, QB)
        do = do_ref[at, :].astype(F32)
        od = do * o_ref[at, :].astype(F32)
        qf = q_ref[at, :].astype(F32) * 0.125
        lv = l_ref[at, :]
        for h in range(2):
            mine = (lane < 64) if h == 0 else (lane >= 64)
            base = 64 if h == 0 else 0
            delta = jnp.sum(jnp.where(mine, od, 0.0), axis=1, keepdims=True)
            qa[h, at, :] = jnp.where(mine, qf, three(-lv, lane, base)).astype(BF)
            da[h, at, :] = jnp.where(mine, do, three(-delta, lane, base)).astype(BF)
        qt[:, at] = jnp.transpose(qf).astype(BF)
        dt[:, at] = jnp.transpose(do).astype(BF)
    for r in range(0, 2 * rows, QB):
        at = pl.ds(r, QB)
        kt[:, at] = jnp.transpose(k_ref[at, :].astype(F32)).astype(BF)
    dqt[...] = jnp.zeros(dqt.shape, F32)

    def keys(ks, first, diagonal):
        kk = k_ref[ks, :]
        vv = v_ref[ks, :]
        dv = []
        dk = []
        for h in range(2):
            mine = (lane < 64) if h == 0 else (lane >= 64)
            base = 64 if h == 0 else 0
            ones3 = ((lane >= base) & (lane < base + 3)).astype(BF)
            hs = slice(64 * h, 64 * h + 64)
            st = dot_nt(jnp.where(mine, kk, ones3), qa[h, first:rows, :])
            dp = dot_nt(jnp.where(mine, vv, ones3), da[h, first:rows, :])
            p = jnp.exp(st)
            if diagonal:
                r = lax.broadcasted_iota(jnp.int32, (QB, QB), 0)
                c = lax.broadcasted_iota(jnp.int32, (QB, QB), 1)
                seen = jnp.where(r <= c, p[:, :QB], 0.0)
                p = jnp.concatenate([seen, p[:, QB:]], 1) if first + QB < rows else seen
            ds = (p * dp).astype(BF)
            dv.append(dot_nt(dt[hs, first:rows], p.astype(BF)))
            dk.append(dot_nt(qt[hs, first:rows], ds))
            dqt[hs, first:rows] += dot(kt[hs, ks], ds)
        dvs[ks, :] = jnp.transpose(jnp.concatenate(dv, 0))
        dks[ks, :] = jnp.transpose(jnp.concatenate(dk, 0))

    for j in range(rows // QB):
        keys(pl.ds(rows + j * QB, QB), j * QB, True)

    @pl.when(second)
    def _():
        def step(j, carry):
            keys(pl.ds(pl.multiple_of(j * QB, QB), QB), 0, False)
            return carry

        lax.fori_loop(0, rows // QB, step, 0)

    @pl.when(jnp.logical_not(second))
    def _():
        dks[0:rows, :] = jnp.zeros((rows, 128), F32)
        dvs[0:rows, :] = jnp.zeros((rows, 128), F32)

    for r in range(0, rows, QB):
        dqs[r : r + QB, :] = jnp.transpose(dqt[:, r : r + QB]) * 0.125
    state = state_ref[0]
    sq = conv_back(pq_ref, dqs, xq_ref, rows, (pt_ref, xt_ref), taps_of(small_ref[...], 0), rows, state)
    sk = conv_back(pk_ref, dks, xk_ref, 0, None, taps_of(small_ref[...], 1), rows, state)
    sv = conv_back(pv_ref, dvs, xv_ref, 0, None, taps_of(small_ref[...], 2), rows, state)
    tg_ref[...] = jnp.zeros(tg_ref.shape, F32)
    for j in range(3):
        for m, s in enumerate((sq, sk, sv)):
            tg_ref[3 * j + m : 3 * j + m + 1, :] = s[j]


def att_bwd(state, mixed, attended, logs, grad, projected, small, earlier, part, rows):
    cols = columns(part)
    own = cols(rows, 0, 0)
    both = cols(2 * rows, 0, 0)
    return call_in_parts(
        att_bwd_kernel,
        [
            pl.BlockSpec(memory_space=pltpu.SMEM),
            own, both, both, own, own, own,
            cols(8, rows // 8 - 1, 0),
            cols(rows, 1, 0),
            cols(2 * rows, 0, 6),
            cols(2 * rows, 0, 12),
            cols(16, 0, 0),
        ],
        [own, cols(8, 0, 0), both, both, cols(16, 0, 0)],
        [
            jax.ShapeDtypeStruct((rows, D), BF),
            jax.ShapeDtypeStruct((8, D), BF),
            jax.ShapeDtypeStruct((2 * rows, D), BF),
            jax.ShapeDtypeStruct((2 * rows, D), BF),
            jax.ShapeDtypeStruct((16, D), F32),
        ],
        earlier,
        part,
        scratch_shapes=[
            pltpu.VMEM((2, rows, 128), BF),
            pltpu.VMEM((2, rows, 128), BF),
            pltpu.VMEM((128, rows), BF),
            pltpu.VMEM((128, rows), BF),
            pltpu.VMEM((128, 2 * rows), BF),
            pltpu.VMEM((128, rows), F32),
            pltpu.VMEM((rows, 128), F32),
            pltpu.VMEM((2 * rows, 128), F32),
            pltpu.VMEM((2 * rows, 128), F32),
        ],
        cost_estimate=cost(
            5 * 2 * 2 * rows * rows * 1.5 * 256 * part[1],
            rows * D * 7 * part[1],
            2 * rows * rows * 1.5 * part[1],
        ),
        name="att_bwd",
    )(state, *mixed, attended, logs, grad, projected, projected, projected, projected,
      small, *earlier)


def unit_rows(x):
    return x * lax.rsqrt(jnp.mean(x * x, axis=-1, keepdims=True) + norm_eps)


def before_bwd_kernel(x_ref, dt_ref, dk_ref, dv_ref, w_ref, out_ref, gain_ref):
    i = pl.program_id(0)
    hat = unit_rows(x_ref[...].astype(F32))
    gn = dot_nt(dk_ref[...], w_ref[D : 2 * D, :]) + dot_nt(dv_ref[...], w_ref[2 * D : 3 * D, :])

    last_step = pl.num_programs(0) - 1

    @pl.when(i == 0)
    def _():
        gain_ref[...] = jnp.zeros(gain_ref.shape, F32)

    @pl.when(i < last_step)
    def _():
        out_ref[...] = gn.astype(BF)
        gain_ref[...] += jnp.sum(gn * hat, axis=0, keepdims=True)

    @pl.when(i == last_step)
    def _():
        last = gn.shape[0] - 8
        full = jnp.concatenate([gn[:last], gn[last:] + dot_nt(dt_ref[...], w_ref[0:D, :])], 0)
        out_ref[...] = full.astype(BF)
        gain_ref[...] += jnp.sum(full * hat, axis=0, keepdims=True)


def before_bwd(x_both, back, weight, rows):
    dt, dk, dv = back[1:]
    blocks = 4
    height = rows // blocks
    step = pl.BlockSpec((height, D), lambda i: (i, 0))

    def whole(shape):
        return pl.BlockSpec(shape, lambda i: (0, 0))

    return pl.pallas_call(
        before_bwd_kernel,
        grid=(blocks,),
        in_specs=[step, whole((8, D)), step, step, whole((3 * D, D))],
        out_specs=[step, whole((1, D))],
        out_shape=[jax.ShapeDtypeStruct((rows, D), BF), jax.ShapeDtypeStruct((1, D), F32)],
        compiler_params=pltpu.CompilerParams(vmem_limit_bytes=VMEM_LIMIT),
        cost_estimate=cost(2 * rows * D * D * 2, rows * D * 12),
        name="before_bwd",
    )(x_both, dt, dk, dv, weight)


def qkv_bwd_kernel(
    core_ref, x_ref, dq_ref, dt_ref, dk_ref, dv_ref, w_ref, small_ref, gain_one_ref, gain_two_ref, tg_ref,
    *refs, pieces, blocks,
):
    if pieces:
        send_ref, keep_ref, own_ref, acc, gacc = refs
    else:
        keep_ref, ends_ref, own_ref, acc, gacc = refs
    i = pl.program_id(0)
    half = blocks // 2

    @pl.when(i == 0)
    def _():
        acc[...] = jnp.zeros(acc.shape, F32)
        gacc[0:1, :] = gain_one_ref[...]

    hat = unit_rows(x_ref[...].astype(F32))
    low = (hat * small_ref[0:1, :]).astype(BF)
    dk = dk_ref[...]
    dv = dv_ref[...]
    acc[D : 2 * D, :] += dot_tn(low, dk)
    acc[2 * D : 3 * D, :] += dot_tn(low, dv)

    @pl.when(i == half - 1)
    def _():
        acc[0:D, :] += dot_tn(low[low.shape[0] - 8 :], dt_ref[...])

    @pl.when(i >= half)
    def _():
        dq = dq_ref[...]
        acc[0:D, :] += dot_tn(low, dq)
        full = (
            dot_nt(dk, w_ref[D : 2 * D, :])
            + dot_nt(dv, w_ref[2 * D : 3 * D, :])
            + dot_nt(dq, w_ref[0:D, :])
        )
        own_ref[...] = full
        gacc[0:1, :] += jnp.sum(full * hat, axis=0, keepdims=True)

    @pl.when(i == blocks - 1)
    def _():
        small = jnp.concatenate(
            [gacc[0:1, :], gain_two_ref[...], tg_ref[0:9, :], jnp.zeros((5, D), F32)], 0
        )
        if pieces:
            core = core_ref[0]
            height = 3 * D // (2 * pieces)
            wide = height + 16
            for j in range(pieces):
                to = pl.ds(j * wide, wide)
                away = pl.ds(pl.multiple_of((2 * j + 1 - core) * height, 16), wide)
                here = pl.ds(pl.multiple_of((2 * j + core) * height, 16), wide)
                send_ref[to, :] = acc[away, :].astype(BF)
                keep_ref[to, :] = acc[here, :].astype(BF)
            send_ref[pieces * wide :, :] = small.astype(BF)
            keep_ref[pieces * wide :, :] = small.astype(BF)
        else:
            keep_ref[...] = acc[0 : 3 * D, :].astype(BF)
            ends_ref[...] = small


def qkv_bwd(core, x_both, back, weight, small, gain_one_grad, gain_two_grad, tap_grads, rows, pieces):
    dq, dt, dk, dv = back
    blocks = 4
    half = blocks // 2
    height = 2 * rows // blocks
    step = pl.BlockSpec((height, D), lambda i: (i, 0))
    late = pl.BlockSpec((height, D), lambda i: (jnp.maximum(i - half, 0), 0))

    def whole(shape):
        return pl.BlockSpec(shape, lambda i: (0, 0))

    if pieces:
        packed = 3 * D // 2 + 16 * pieces + 16
        outs = [jax.ShapeDtypeStruct((packed, D), BF), jax.ShapeDtypeStruct((packed, D), BF)]
        out_at = [whole((packed, D))] * 2
    else:
        outs = [jax.ShapeDtypeStruct((3 * D, D), BF), jax.ShapeDtypeStruct((16, D), F32)]
        out_at = [whole((3 * D, D)), whole((16, D))]

    def body(*refs):
        qkv_bwd_kernel(*refs, pieces=pieces, blocks=blocks)

    return pl.pallas_call(
        body,
        grid=(blocks,),
        in_specs=[
            pl.BlockSpec(memory_space=pltpu.SMEM),
            step, late, whole((8, D)), step, step, whole((3 * D, D)),
            whole((16, D)), whole((1, D)), whole((1, D)), whole((16, D)),
        ],
        out_specs=out_at + [late],
        out_shape=outs + [jax.ShapeDtypeStruct((rows, D), F32)],
        scratch_shapes=[pltpu.VMEM((3 * D + 16, D), F32), pltpu.VMEM((8, D), F32)],
        compiler_params=pltpu.CompilerParams(vmem_limit_bytes=VMEM_LIMIT),
        cost_estimate=cost(2 * 2 * D * D * 4 * rows, rows * D * 30),
        name="qkv_bwd",
    )(core, x_both, dq, dt, dk, dv, weight, small, gain_one_grad, gain_two_grad, tap_grads)


def merge(index, keep, got, height, taken):
    rows = keep.shape[0]
    out_rows = taken * height + 16 if taken else rows

    def body(index_ref, keep_ref, got_ref, send_ref, stay_ref):
        if not taken:
            total = keep_ref[...].astype(F32) + got_ref[...].astype(F32)
            send_ref[...] = total.astype(BF)
            stay_ref[...] = total
            return
        for j in range(taken):
            to = pl.ds(j * height, height)
            away = pl.ds(pl.multiple_of(index_ref[j] * height, 16), height)
            here = pl.ds(pl.multiple_of(index_ref[taken + j] * height, 16), height)
            send_ref[to, :] = (keep_ref[away, :].astype(F32) + got_ref[away, :].astype(F32)).astype(BF)
            stay_ref[to, :] = keep_ref[here, :].astype(F32) + got_ref[here, :].astype(F32)
        end = keep_ref[rows - 16 :, :].astype(F32) + got_ref[rows - 16 :, :].astype(F32)
        send_ref[taken * height :, :] = end.astype(BF)
        stay_ref[taken * height :, :] = end

    vmem = pl.BlockSpec(memory_space=pltpu.VMEM)
    return pl.pallas_call(
        body,
        in_specs=[pl.BlockSpec(memory_space=pltpu.SMEM), vmem, vmem],
        out_specs=[vmem, vmem],
        out_shape=[
            jax.ShapeDtypeStruct((out_rows, D), BF),
            jax.ShapeDtypeStruct((out_rows, D), F32),
        ],
        compiler_params=pltpu.CompilerParams(vmem_limit_bytes=32 << 20),
        cost_estimate=cost(rows * D, rows * D * 12),
        name="merge",
    )(index, keep, got)


def merge_grid(index, keep, got, taken, kept=F32):
    height = keep.shape[1]

    def body(index_ref, ka_ref, ga_ref, kb_ref, gb_ref, send_ref, stay_ref):
        send_ref[...] = (ka_ref[...].astype(F32) + ga_ref[...].astype(F32)).astype(BF)
        stay_ref[...] = (kb_ref[...].astype(F32) + gb_ref[...].astype(F32)).astype(kept)

    away = pl.BlockSpec((1, height, D), lambda i, index: (index[i], 0, 0))
    here = pl.BlockSpec((1, height, D), lambda i, index: (index[taken + i], 0, 0))
    step = pl.BlockSpec((1, height, D), lambda i, index: (i, 0, 0))
    return pl.pallas_call(
        body,
        grid_spec=pltpu.PrefetchScalarGridSpec(
            num_scalar_prefetch=1,
            grid=(taken,),
            in_specs=[away, away, here, here],
            out_specs=[step, step],
        ),
        out_shape=[
            pltpu.HBM((taken, height, D), BF),
            pltpu.HBM((taken, height, D), kept),
        ],
        compiler_params=pltpu.CompilerParams(vmem_limit_bytes=32 << 20),
        cost_estimate=cost(taken * height * D * 2, taken * height * D * 16),
        name="merge_grid",
    )(index, keep, got, keep, got)


def arrange(index, blocks):
    height = blocks[0].shape[0] - 16

    def body(index_ref, *refs):
        first_ref, rest_ref, ends, total, sems = refs[4:]
        refs = refs[:4]
        tail = pl.ds(height, 16)
        places = [first_ref.at[pl.ds(0, height)]] + [rest_ref.at[pl.ds(i * height, height)] for i in range(3)]
        for k in range(4):
            pltpu.make_async_copy(refs[k].at[tail], ends.at[k], sems.at[4 + k]).start()
        for i in range(4):
            for k in range(4):

                @pl.when(index_ref[i] == k)
                def _():
                    pltpu.make_async_copy(refs[k].at[pl.ds(0, height)], places[i], sems.at[i]).start()

        for k in range(4):
            pltpu.make_async_copy(refs[k].at[tail], ends.at[k], sems.at[4 + k]).wait()
        sums = [ends[k].astype(F32) for k in range(4)]
        total[...] = (sums[0] + sums[1] + sums[2] + sums[3]).astype(BF)
        last = pltpu.make_async_copy(total, first_ref.at[tail], sems.at[8])
        last.start()
        for i in range(4):
            pltpu.make_async_copy(refs[0].at[pl.ds(0, height)], places[i], sems.at[i]).wait()
        last.wait()

    held = pl.BlockSpec(memory_space=pltpu.HBM)
    return pl.pallas_call(
        body,
        in_specs=[pl.BlockSpec(memory_space=pltpu.SMEM)] + [held] * 4,
        out_specs=[held, held],
        out_shape=[
            jax.ShapeDtypeStruct((height + 16, D), BF),
            jax.ShapeDtypeStruct((3 * height, D), BF),
        ],
        scratch_shapes=[
            pltpu.VMEM((4, 16, D), BF),
            pltpu.VMEM((16, D), BF),
            pltpu.SemaphoreType.DMA((9,)),
        ],
        compiler_params=pltpu.CompilerParams(vmem_limit_bytes=32 << 20),
        cost_estimate=cost(4 * height * D, 4 * height * D * 4),
        name="arrange",
    )(index, *blocks)


def join(own, got, shared=16):
    rows = own.shape[0]
    body_rows = rows - shared

    def body(own_ref, got_ref, out_ref):
        out_ref[0:body_rows, :] = own_ref[0:body_rows, :]
        out_ref[body_rows : 2 * body_rows, :] = got_ref[0:body_rows, :]
        if shared:
            out_ref[2 * body_rows :, :] = own_ref[body_rows:, :] + got_ref[body_rows:, :]

    vmem = pl.BlockSpec(memory_space=pltpu.VMEM)
    return pl.pallas_call(
        body,
        in_specs=[vmem, vmem],
        out_specs=vmem,
        out_shape=jax.ShapeDtypeStruct((2 * body_rows + shared, D), BF),
        compiler_params=pltpu.CompilerParams(vmem_limit_bytes=32 << 20),
        cost_estimate=cost(rows * D, rows * D * 8),
        name="join",
    )(own, got)


def join_held(own, got):
    rows = own.shape[0]
    cuts = 4
    size = rows // cuts

    def body(own_ref, got_ref, out_ref, sems):
        copies = []
        for k, ref in enumerate((own_ref, got_ref)):
            for j in range(cuts):
                source = ref.at[pl.ds(j * size, size)]
                to = out_ref.at[pl.ds(k * rows + j * size, size)]
                copies.append(pltpu.make_async_copy(source, to, sems.at[k * cuts + j]))
        for copy in copies:
            copy.start()
        for copy in copies:
            copy.wait()

    held = pl.BlockSpec(memory_space=pltpu.HBM)
    return pl.pallas_call(
        body,
        in_specs=[held, held],
        out_specs=held,
        out_shape=jax.ShapeDtypeStruct((2 * rows, D), BF),
        scratch_shapes=[pltpu.SemaphoreType.DMA((2 * cuts,))],
        compiler_params=pltpu.CompilerParams(vmem_limit_bytes=16 << 20),
        cost_estimate=cost(0, rows * D * 8),
        name="join_held",
    )(own, got)


def hold(block, other):
    held = pl.BlockSpec(memory_space=pl.ANY)
    return pl.pallas_call(
        lambda block_ref, other_ref, out_ref: None,
        in_specs=[held, held],
        out_specs=held,
        out_shape=jax.ShapeDtypeStruct(block.shape, block.dtype),
        input_output_aliases={0: 0},
        name="hold",
    )(block, other)


def qkv_fwd_kernel(index_ref, x_ref, *refs, pieces, blocks):
    if pieces:
        own_ref, got_ref, out_ref, small_ref, weight = refs
    else:
        weight, given_ref, out_ref, small_ref = refs
    i = pl.program_id(0)

    @pl.when(i == 0)
    def _():
        if pieces:
            height = 3 * D // (2 * pieces)
            for j in range(pieces):
                at = pl.ds(j * height, height)
                for k, ref in enumerate((own_ref, got_ref)):
                    to = pl.multiple_of(index_ref[k * pieces + j] * height, 16)
                    weight[pl.ds(to, height), :] = ref[at, :]
            end = pl.ds(pieces * height, 16)
            small_ref[...] = own_ref[end, :].astype(F32) + got_ref[end, :].astype(F32)
        else:
            small_ref[...] = given_ref[...]

    x = x_ref[...].astype(F32)
    hat = x * lax.rsqrt(jnp.mean(x * x, axis=-1, keepdims=True) + norm_eps)
    low = (hat * small_ref[0:1, :]).astype(BF)

    @pl.when(i >= blocks // 2 - 1)
    def _():
        out_ref[:, 0:D] = dot(low, weight[0:D, :]).astype(BF)

    out_ref[:, D : 2 * D] = dot(low, weight[D : 2 * D, :]).astype(BF)
    out_ref[:, 2 * D : 3 * D] = dot(low, weight[2 * D : 3 * D, :]).astype(BF)


def qkv_fwd(index, x_both, weights, rows, pieces):
    blocks = 4
    height = 2 * rows // blocks

    def body(*refs):
        qkv_fwd_kernel(*refs, pieces=pieces, blocks=blocks)

    return pl.pallas_call(
        body,
        grid=(blocks,),
        in_specs=[
            pl.BlockSpec(memory_space=pltpu.SMEM),
            pl.BlockSpec((height, D), lambda i: (i, 0)),
            *[pl.BlockSpec(w.shape, lambda i: (0, 0)) for w in weights],
        ],
        out_specs=[
            pl.BlockSpec((height, 3 * D), lambda i: (i, 0)),
            pl.BlockSpec((16, D), lambda i: (0, 0)),
        ]
        + ([pl.BlockSpec((3 * D, D), lambda i: (0, 0))] if pieces else []),
        out_shape=[
            jax.ShapeDtypeStruct((2 * rows, 3 * D), BF),
            jax.ShapeDtypeStruct((16, D), F32),
        ]
        + ([jax.ShapeDtypeStruct((3 * D, D), BF)] if pieces else []),
        compiler_params=pltpu.CompilerParams(vmem_limit_bytes=VMEM_LIMIT),
        cost_estimate=cost(2 * 2 * rows * D * 3 * D, rows * D * 20),
        name="qkv_fwd",
    )(index, x_both, *weights)


def ffn_kernel(
    state_ref, index_ref, x_ref, att_ref, cot_ref, small_ref, own_ref, own_two_ref, got_ref, got_two_ref,
    out_ref, gh_ref, ga_ref, gain_grad_ref, away_ref, here_ref,
    hidden, low, total, back, cot, sq, gb, weights, stage_up, stage_down, stage_out, in_sems, sems,
):
    c = pl.program_id(0)
    rows = x_ref.shape[0]
    blocks = [pl.ds(i * QB, QB) for i in range(rows // QB)]
    last = c == pl.num_programs(0) - 1
    core = index_ref[24]

    def fetch(k, j):
        ref = ((own_ref, own_two_ref), (got_ref, got_two_ref))[k][j // 6]
        piece = index_ref[12 * k + j]
        to = weights.at[pl.ds(3 * piece, 3)]
        return pltpu.make_async_copy(ref.at[pl.ds(3 * (j % 6), 3)], to, in_sems.at[piece])

    def fetched(pieces):
        for piece in pieces:
            at = weights.at[pl.ds(3 * piece, 3)]
            pltpu.make_async_copy(own_ref.at[pl.ds(0, 3)], at, in_sems.at[piece]).wait()

    def put(source, group, count, column, sem, wait=False):
        piece = group // 3
        at = (piece // 2) * 3 + group % 3

        def copy(ref):
            to = ref.at[pl.ds(at, count)] if column is None else ref.at[pl.ds(at, count), column]
            return pltpu.make_async_copy(source, to, sems.at[sem])

        if wait:
            copy(here_ref).wait()
            return
        mine = piece % 2 == core

        @pl.when(mine)
        def _():
            copy(here_ref).start()

        @pl.when(jnp.logical_not(mine))
        def _():
            copy(away_ref).start()

    def put_up(i, wait=False):
        start = 0
        k = 0
        while start < 32:
            count = min(3 - (8 + start) % 3, 32 - start)
            put(stage_up.at[i, pl.ds(start, count)], 8 + start, count, i, 20 * i + k, wait)
            start += count
            k += 1

    def put_down(i, wait=False):
        for k in range(8):
            put(stage_down.at[i, pl.ds(k, 1)], 40 + 8 * i + k, 1, None, 20 * i + 12 + k, wait)

    def put_out(wait=False):
        for k in range(8):
            put(stage_out.at[pl.ds(k, 1)], k, 1, None, 80 + k, wait)

    def square(first):
        return weights[first : first + 8].reshape(D, D)

    @pl.when(c == 0)
    def _():
        for early in (True, False):
            for k in range(2):
                for j in range(12):

                    @pl.when((index_ref[12 * k + j] < 3) == early)
                    def _():
                        fetch(k, j).start()

        cot[...] = jnp.where(state_ref[0] > 0, cot_ref[...], jnp.zeros((), BF))
        total[...] = jnp.zeros(total.shape, F32)
        back[...] = jnp.zeros(back.shape, F32)
        fetched(range(3))
        wo = square(0)
        for b in blocks:
            h = x_ref[b, :].astype(F32) + dot(att_ref[b, :], wo)
            hidden[b, :] = h
            hat = h * lax.rsqrt(jnp.mean(h * h, axis=-1, keepdims=True) + norm_eps)
            low[b, :] = (hat * small_ref[1:2, :]).astype(BF)

    for i, pieces in enumerate((range(3, 16), range(16, 19), range(19, 22), range(22, 24))):

        @pl.when(c == i)
        def _():
            fetched(pieces)

    up = weights[8:40, c].reshape(D, D)
    down = weights[pl.ds(40 + 8 * c, 8)].reshape(D, D)
    for b in blocks:
        act = jnp.maximum(dot(low[b, :], up), 0.0)
        s = (act * act).astype(BF)
        sq[b, :] = s
        total[b, :] += dot(s, down)
        g = (dot_nt(cot[b, :], down) * 2.0 * act).astype(BF)
        gb[b, :] = g
        back[b, :] += dot_nt(g, up)
    stage_down[c] = dot_tn(sq[...], cot[...]).reshape(8, 4, 24, D).astype(BF)
    stage_up[c] = dot_tn(low[...], gb[...]).reshape(32, 24, D).astype(BF)
    put_down(c)
    put_up(c)

    @pl.when(last)
    def _():
        gain = small_ref[1:2, :]
        wo = square(0)
        sums = jnp.zeros((1, D), F32)
        for b in blocks:
            h = hidden[b, :]
            out_ref[b, :] = (h + total[b, :]).astype(BF)
            factor = lax.rsqrt(jnp.mean(h * h, axis=-1, keepdims=True) + norm_eps)
            hat = h * factor
            g = back[b, :]
            sums = sums + jnp.sum(g * hat, axis=0, keepdims=True)
            weighted = g * gain
            inner = jnp.mean(weighted * hat, axis=-1, keepdims=True)
            grad = cot[b, :].astype(F32) + factor * (weighted - hat * inner)
            gh_ref[b, :] = grad
            grad_low = grad.astype(BF)
            gb[b, :] = grad_low
            ga_ref[b, :] = dot_nt(grad_low, wo).astype(BF)
        gain_grad_ref[...] = sums
        stage_out[...] = dot_tn(att_ref[...], gb[...]).reshape(8, 4, 24, D).astype(BF)
        put_out()
        for i in range(4):
            put_down(i, True)
            put_up(i, True)
        put_out(True)


def ffn(state, index, tokens, attended, out_grad, small, weights, rows):
    def whole(shape):
        return pl.BlockSpec(shape, lambda c: (0,) * len(shape), pipeline_mode=pl.Buffered(1))

    act = whole((rows, D))
    held = pl.BlockSpec(memory_space=pl.ANY)
    scalars = pl.BlockSpec(memory_space=pltpu.SMEM)
    half = (36, 4, 24, D)
    return pl.pallas_call(
        ffn_kernel,
        grid=(4,),
        in_specs=[scalars, scalars, act, act, act, whole((16, D)), held, held, held, pl.BlockSpec(memory_space=pltpu.VMEM)],
        out_specs=[act, act, act, whole((1, D)), held, held],
        out_shape=[
            jax.ShapeDtypeStruct((rows, D), BF),
            jax.ShapeDtypeStruct((rows, D), F32),
            jax.ShapeDtypeStruct((rows, D), BF),
            jax.ShapeDtypeStruct((1, D), F32),
            jax.ShapeDtypeStruct(half, BF),
            jax.ShapeDtypeStruct(half, BF),
        ],
        scratch_shapes=[
            pltpu.VMEM((rows, D), F32),
            pltpu.VMEM((rows, D), BF),
            pltpu.VMEM((rows, D), F32),
            pltpu.VMEM((rows, D), F32),
            pltpu.VMEM((rows, D), BF),
            pltpu.VMEM((rows, D), BF),
            pltpu.VMEM((rows, D), BF),
            pltpu.VMEM((72, 4, 24, D), BF),
            pltpu.VMEM((4, 32, 24, D), BF),
            pltpu.VMEM((4, 8, 4, 24, D), BF),
            pltpu.VMEM((8, 4, 24, D), BF),
            pltpu.SemaphoreType.DMA((24,)),
            pltpu.SemaphoreType.DMA((88,)),
        ],
        compiler_params=pltpu.CompilerParams(vmem_limit_bytes=60 << 20),
        cost_estimate=cost(2 * rows * D * D * (24 + 3), 2 * 12 * D * D * 2 + rows * D * 16),
        name="ffn",
    )(state, index, tokens, attended, out_grad, small, *weights)


def shift_flat(block, distance):
    count = lax.axis_size(AXES)
    route = [(i - distance, i) for i in range(count) if 0 <= i - distance < count]
    return lax.ppermute(block, AXES, route)


def shift_ctx(block, distance):
    count = lax.axis_size("ctx")
    route = [(i - distance, i) for i in range(count) if 0 <= i - distance < count]
    return lax.ppermute(block, "ctx", route)


def after(value, *others):
    return lax.optimization_barrier((value, *others))[0]


def swap(block, even_bit, odd_bit, planes=None):
    count = lax.axis_size(AXES)
    route = [
        (i, i ^ (odd_bit if i & 1 else even_bit))
        for i in range(count)
        if planes is None or i >> 3 in planes
    ]
    return lax.ppermute(block, AXES, route)


def to_aligned(shard, place, count, delta):
    rows = shard.shape[0]
    lag = delta * (count - 1)
    back = -(-lag // rows)
    if back == 1:
        keep = -(-lag // 8) * 8
        parts = [shift_flat(shard[rows - keep :], 1), shard]
    else:
        keep = back * rows
        parts = [shift_flat(shard, s) for s in range(back, 0, -1)] + [shard]
    joined = jnp.concatenate(parts, 0)
    return lax.dynamic_slice_in_dim(joined, keep - delta * place, rows - delta, 0)


def small_part(shard, place, count, delta):
    rows = shard.shape[0]
    extra = count * delta
    zeros = jnp.zeros((extra, 128), shard.dtype)
    joined = jnp.concatenate([zeros, shard, zeros], 0)
    start = extra + count * (rows - delta) - place * rows
    return lax.dynamic_slice_in_dim(joined, jnp.minimum(start, rows + extra), extra, 0)


def from_aligned(chunk, small, place, count, delta, rows):
    aligned = rows - delta
    ahead = -(-(count * delta) // aligned)
    parts = [chunk]
    if ahead == 1:
        keep = small.shape[0]
        got = shift_flat(chunk[:keep], -1)
        parts.append(jnp.where(place == count - 1, small, got))
    else:
        pad = ahead * aligned - small.shape[0]
        tail = jnp.concatenate([small, jnp.zeros((pad, 128), small.dtype)], 0)
        for s in range(1, ahead + 1):
            got = shift_flat(chunk, -s)
            for e in range(s):
                piece = tail[e * aligned : (e + 1) * aligned]
                got = jnp.where(place == count - s + e, piece, got)
            parts.append(got)
    return lax.dynamic_slice_in_dim(jnp.concatenate(parts, 0), delta * place, rows, 0)


def regroup(block):
    return block.reshape(-1, 24, 4, D).transpose(0, 2, 1, 3)


def ungroup(block):
    return block.reshape(-1, 4, 24, D).transpose(0, 2, 1, 3)


def normalize(values, gain):
    factor = lax.rsqrt(jnp.mean(values * values, axis=-1, keepdims=True) + norm_eps)
    scaled = values * factor
    return (scaled, factor, scaled * gain)


def norm_back(grad_in, scaled, factor, gain):
    weighted = grad_in * gain
    inner_mean = jnp.mean(weighted * scaled, axis=-1, keepdims=True)
    return factor * (weighted - scaled * inner_mean)


def adam_update(master, moment_one, moment_two, gradient, step_count, row_start):
    row_index = row_start + jnp.arange(master.shape[0], dtype=jnp.int32)
    matrix_rows = (4 * D * D + 2 * D * FF) // 128
    out_first = 3 * D * D // 128
    out_last = 4 * D * D // 128
    is_matrix = (row_index < matrix_rows)[:, None]
    is_out = ((row_index >= out_first) & (row_index < out_last))[:, None]
    step_rate = jnp.where(is_matrix, jnp.where(is_out, 0.5, 0.1), 1.0)
    decay_rate = jnp.where(is_matrix, 0.1, 0.0)
    step_value = step_count[0].astype(jnp.float32)
    new_one = 0.9 * moment_one + 0.1 * gradient
    new_two = 0.999 * moment_two + 0.001 * gradient * gradient
    corr_first = 1.0 - jnp.power(0.9, step_value)
    corr_second = 1.0 - jnp.power(0.999, step_value)
    new_weights = master - step_rate * (
        new_one / corr_first / (jnp.sqrt(new_two / corr_second) + 1e-08) + decay_rate * master
    )
    return (new_weights, new_one, new_two)


def shards(tokens, out_grad, positions, master, first_moment, second_moment, step_count):
    rows = tokens.shape[0]
    assert rows == SEQ_MIN
    count = lax.axis_size(AXES)
    place = lax.axis_index(AXES).astype(jnp.int32)
    owned = master.shape[0]
    aligned = (4 * D * D + 2 * D * FF) // 128 // count
    delta = owned - aligned
    height = aligned * 128 // D
    staged = count == 32
    first_place = positions[0]
    state = jnp.where(first_place < 0, 0, jnp.where(first_place >= SEQ_MIN, 2, 1)).astype(jnp.int32)
    state_vec = state[None]

    chunk = to_aligned(master, place, count, delta).reshape(-1, D)
    if staged:
        group = 3 * place + jnp.arange(3, dtype=jnp.int32)
        in_up = ((group >= 32) & (group < 64))[:, None, None, None]
        chunk = jnp.where(in_up, regroup(chunk), chunk.reshape(3, 4, 24, D)).reshape(-1, D)
    chunk = chunk.astype(BF)
    if staged:
        small = jnp.where(place == count - 1, master[owned - count * delta :], 0.0)
    else:
        small = small_part(master, place, count, delta)
    small = lax.reduce_precision(small, 8, 7)
    core = (place & 1)[None]
    x_bit = (place >> 1) & 1
    y_bit = (place >> 2) & 1
    even = (place & 1) == 0
    if staged:
        z = place >> 3
        mine = jnp.concatenate([chunk, small.astype(BF).reshape(-1, D)], 0)
        tokens_before = shift_ctx(after(tokens, mine), 1)
        far = swap(mine, 16, 16)
        near = swap(mine, 8, 8)
        tokens_both = jnp.concatenate([tokens_before, tokens], 0)
        both = swap(after(far, tokens_both), 8, 8)
        order = jnp.stack([z, z ^ 1, z ^ 2, z ^ 3]).astype(jnp.int32)
        mine, rest = arrange(after(order, state_vec), (mine, near, far, both))
        mine = join(mine, swap(mine, 2, 4))
        mine = join(mine, swap(mine, 4, 2))
        across = swap(rest, 2, 4)
        got = swap(mine, 1, 1)
        index = []
        late_index = []
        for k in (0, 1):
            turn = even if k == 0 else jnp.logical_not(even)
            for j in range(4):
                near, far = j & 1, j >> 1
                x_of = x_bit ^ jnp.where(turn, near, far)
                y_of = y_bit ^ jnp.where(turn, far, near)
                piece = 4 * y_of + 2 * x_of + (core[0] ^ k)
                index.append(piece)
                late_index += [piece, piece + 8, piece + 16]
        index = jnp.stack(index).astype(jnp.int32)
        late_index = jnp.stack(late_index + [core[0]]).astype(jnp.int32)
        projected, small, in_weight = qkv_fwd(index, tokens_both, (mine, got), rows, 4)
    else:
        tokens_both = jnp.concatenate([shift_ctx(tokens, 1), tokens], 0)
        wide = lax.all_gather(chunk, AXES, axis=0, tiled=True)
        small = lax.psum(small, AXES)[:96].reshape(-1, D)
        in_weight = wide[: 3 * D]
        projected, small = qkv_fwd(core, tokens_both, (in_weight, small), rows, 0)
        late_index = jnp.arange(25, dtype=jnp.int32) % 24
    gain_first = small[0]

    forward = []
    if staged:
        rest = join_held(after(rest, projected), across)
        line = swap(rest, 4, 2)
        core_rest = swap(rest, 1, 1)
        forward = att_fwd(after(state_vec, rest), projected, small, forward, FORWARD_PARTS[0], rows)
        forward = att_fwd(after(state_vec, core_rest), projected, small, forward, FORWARD_PARTS[1], rows)
        line = hold(line, forward[0])
        core_line = swap(line, 1, 1)
        forward = att_fwd(after(state_vec, line), projected, small, forward, FORWARD_PARTS[2], rows)
        late_weights = [w.reshape(18, 4, 24, D) for w in (rest, line, core_rest, core_line)]
    else:
        for part in FORWARD_PARTS:
            forward = att_fwd(state_vec, projected, small, forward, part, rows)
        grouped = jnp.concatenate(
            [
                wide[3 * D : 4 * D].reshape(-1, 4, 24, D),
                regroup(wide[4 * D : 8 * D]),
                wide[8 * D :].reshape(-1, 4, 24, D),
            ],
            0,
        )
        late_weights = [grouped[18 * k : 18 * k + 18] for k in range(4)]
    attn_low, logs, *mixed = forward

    layer_out, grad_hidden, grad_attended, grad_gain_two, away_grad, here_grad = ffn(
        state_vec, late_index, tokens, attn_low, out_grad, small, late_weights, rows
    )

    def backward(start, done, part):
        return att_bwd(
            start, mixed, attn_low, logs, grad_attended, projected, small, done, BACKWARD_PARTS[part], rows
        )

    if staged:
        stay = [jnp.where(even, 2 * j + x_bit, 2 * y_bit + j) for j in range(2)]
        away = [jnp.where(even, 2 * j + 1 - x_bit, 2 * (1 - y_bit) + j) for j in range(2)]
        pick_plane = jnp.stack(away + stay).astype(jnp.int32)
        other = jnp.where(even, y_bit, x_bit)
        pick_line = jnp.stack([1 - other, other]).astype(jnp.int32)

        def of_quarters(pick, held):
            half = pick.shape[0] // 2
            steps = [pick[s * half + j] + held * t for s in range(2) for t in range(3) for j in range(half)]
            return jnp.stack(steps)

        late_keep = here_grad.reshape(12, height, D)
        late_got = swap(away_grad.reshape(12, height, D), 1, 1)
        done = backward(state_vec, [], 0)
        late_send, late_keep = merge_grid(
            after(of_quarters(pick_plane, 4), done[4]), late_keep, late_got, 6, BF
        )
        late_got = swap(late_send, 2, 4)
        done = backward(after(state_vec, late_send), done, 1)
        late_send, late_keep = merge_grid(
            after(of_quarters(pick_line, 2), done[4]), late_keep, late_got, 3
        )
        late_got = swap(late_send, 4, 2)
        done = backward(after(state_vec, late_send), done, 2)
        z_even = (z & 1) == 0
        low_pair = [jnp.where(z_even, 0, 0), jnp.where(z_even, 2, 1)]
        high_pair = [jnp.where(z_even, 0, 0), jnp.where(z_even, 1, 2)]
        pick_z = jnp.stack(low_pair + high_pair).astype(jnp.int32)
        late_send, late_keep = merge_grid(after(pick_z, done[4]), late_keep, late_got, 2)
        late_got = swap(late_send, 8, 8)
        done = backward(after(state_vec, late_send), done, 3)
        high = z >> 1
        pick_last = jnp.stack([1 - high, high]).astype(jnp.int32)
        late_send, late_keep = merge_grid(after(pick_last, done[4]), late_keep, late_got, 1)
        late_got = swap(late_send, 16, 16, (0, 1, 3))
        sums_state = after(core, late_send)
    else:
        done = []
        for part in range(4):
            done = backward(state_vec, done, part)
        sums_state = core
    *back, tap_grads = done
    grads_before, gain_one_grad = before_bwd(tokens_both, back, in_weight, rows)
    from_next = shift_ctx(grads_before, -1)
    sums = qkv_bwd(
        after(sums_state, grads_before), tokens_both, back, in_weight, small, gain_one_grad, grad_gain_two, tap_grads, rows,
        4 if staged else 0,
    )
    grad_normed_one = sums[2]
    scaled_one, factor_one, _ = normalize(tokens.astype(F32), gain_first)
    input_grad = grad_hidden + norm_back(
        grad_normed_one + from_next.astype(F32), scaled_one, factor_one, gain_first
    )

    if staged:
        send, keep = sums[:2]
        got = swap(after(send, late_got, from_next), 1, 1)
        send, keep = merge(pick_plane, keep, got, height + 16, 2)
        got = swap(send, 2, 4)
        late_got = after(late_got, send)
        late_chunk = late_keep[0] + late_got[0].astype(F32)
        late_chunk = jnp.where(in_up, ungroup(late_chunk).reshape(3, 4, 24, D), late_chunk.reshape(3, 4, 24, D))
        late_chunk = late_chunk.reshape(-1, D)
        late_next = shift_flat(late_chunk[:16], -1)
        send, keep = merge(after(pick_line, late_chunk), keep, got, height + 16, 1)
        got = swap(send, 4, 2)
        send, keep = merge(core, keep, got, height + 16, 0)
        got = swap(send, 8, 8)
        send, keep = merge(after(core, input_grad, late_next), keep, got, height + 16, 0)
        got = swap(send, 16, 16, (1, 2))
        first = keep + got.astype(F32)
        quarter = count // 4
        follow = jnp.where(place < quarter - 1, first[height : height + 16], late_next)
        follow = jnp.where(place == count - 1, first[height + 16 :], follow)
        chunk_grad = jnp.where(place < quarter, first[:height], late_chunk)
        chunk_grad = jnp.concatenate([chunk_grad, follow], 0).reshape(-1, 128)
        gradient = lax.dynamic_slice_in_dim(chunk_grad, delta * place, owned, 0)
    else:
        flat_grad = jnp.stack([here_grad.reshape(12, 3, 4, 24, D), away_grad.reshape(12, 3, 4, 24, D)], 1)
        flat_grad = flat_grad.reshape(72, 4, 24, D)
        wide_grad = jnp.concatenate(
            [
                sums[0],
                flat_grad[:8].reshape(-1, D),
                ungroup(flat_grad[8:40]).reshape(-1, D),
                flat_grad[40:].reshape(-1, D),
            ],
            0,
        )
        chunk_grad = lax.psum_scatter(wide_grad, AXES, scatter_dimension=0, tiled=True).astype(F32)
        used = sums[1].reshape(-1, 128)
        extra = count * delta
        small_grad = jnp.concatenate([used, jnp.zeros((extra - used.shape[0], 128), F32)], 0)
        small_grad = lax.psum(small_grad, AXES)
        gradient = from_aligned(chunk_grad.reshape(-1, 128), small_grad, place, count, delta, owned)
    new_weights, new_one, new_two = adam_update(
        master, first_moment, second_moment, gradient, step_count, place * owned
    )
    return (layer_out, input_grad, new_weights, new_one, new_two, new_weights.astype(BF))


def solution(mesh):
    spread = P(AXES, None)
    return jax.shard_map(
        shards,
        mesh=mesh,
        in_specs=(spread, spread, P(AXES), spread, spread, spread, P()),
        out_specs=(spread,) * 6,
        check_vma=False,
    )
```

```python
import jax
import jax.numpy as jnp
from jax import lax
from jax.experimental import pallas as pl
from jax.experimental.pallas import tpu as pltpu
from jax.sharding import PartitionSpec as P

D = 768
HEADS = 12
HEAD_DIM = 64
FF = 3072
SEQ_MIN = 1024
AXES = ("dp", "ctx")
QB = 256
FORWARD_PARTS = ((0, 5), (5, 1))
BACKWARD_PARTS = ((0, 1), (1, 3), (4, 1), (5, 1))
F32 = jnp.float32
BF = jnp.bfloat16
NT = (((1,), (1,)), ((), ()))
TN = (((0,), (0,)), ((), ()))
norm_eps = 1e-06
VMEM_LIMIT = 56 << 20


def dot(left, right):
    return jnp.dot(left, right, preferred_element_type=F32)


def dot_nt(left, right):
    return lax.dot_general(left, right, NT, preferred_element_type=F32)


def dot_tn(left, right):
    return lax.dot_general(left, right, TN, preferred_element_type=F32)


def cost(flops, nbytes, exps=0):
    return pl.CostEstimate(flops=int(flops), bytes_accessed=int(nbytes), transcendentals=int(exps))


def taps_of(small, matrix):
    return [small[2 + 3 * j + matrix : 3 + 3 * j + matrix, :] for j in range(3)]


def row_ids(height):
    return lax.broadcasted_iota(jnp.int32, (height, 128), 0)


def conv(out_ref, x_ref, start, tail_ref, taps, rows, state):
    height = x_ref.shape[0]
    for r in range(0, height, QB):
        at = start + r
        if r:
            x = x_ref[r - 16 : r + QB, :].astype(F32)
        else:
            before = jnp.zeros((16, 128), F32)
            if tail_ref is not None:
                before = jnp.concatenate([before[8:], tail_ref[...].astype(F32)], 0)
            x = jnp.concatenate([before, x_ref[0:QB, :].astype(F32)], 0)
        one = pltpu.roll(x, 1, 0)[16:]
        two = pltpu.roll(x, 2, 0)[16:]
        x = x[16:]
        scale = 1.0
        if at >= rows:
            scale = jnp.where(state > 0, 1.0, 0.0)
        if at == 0 or at == rows:
            seen = jnp.where(state == 2, 1.0, 0.0) if at else 0.0
            row = row_ids(QB)
            one = jnp.where(row < 1, one * seen, one)
            two = jnp.where(row < 2, two * seen, two)
        c_one = taps[1] * scale
        c_two = taps[2] * scale
        out_ref[r : r + QB, :] = (taps[0] * x + c_one * one + c_two * two).astype(BF)


def att_fwd_kernel(
    state_ref, tail_ref, q_ref, k_ref, v_ref, small_ref,
    o_ref, l_ref, qm_ref, km_ref, vm_ref, ka, va,
):
    rows = q_ref.shape[0]
    lane = lax.broadcasted_iota(jnp.int32, (1, 128), 1)
    state = state_ref[0]
    conv(qm_ref, q_ref, rows, tail_ref, taps_of(small_ref[...], 0), rows, state)
    conv(km_ref, k_ref, 0, None, taps_of(small_ref[...], 1), rows, state)
    conv(vm_ref, v_ref, 0, None, taps_of(small_ref[...], 2), rows, state)
    bias = jnp.where(state == 2, 0.0, -1e30)
    for h in range(2):
        mine = (lane < 64) if h == 0 else (lane >= 64)
        base = 64 if h == 0 else 0
        first = jnp.where(lane == base, bias, 0.0).astype(BF)
        for r in range(0, 2 * rows, QB):
            at = pl.ds(r, QB)
            ka[h, at, :] = jnp.where(mine, km_ref[at, :], first if r < rows else jnp.zeros((), BF))
            va[h, at, :] = jnp.where(mine, vm_ref[at, :], jnp.ones((), BF))
    heads = (row_ids(128) < 64) == (lane < 64)
    heads = heads.astype(BF)
    q_most = jnp.zeros((1, 128), F32)
    k_most = jnp.zeros((1, 128), F32)
    for r in range(0, rows, QB):
        q = qm_ref[r : r + QB, :].astype(F32) * 0.125
        q_most = jnp.maximum(q_most, jnp.max(dot((q * q).astype(BF), heads), axis=0, keepdims=True))
    for r in range(0, 2 * rows, QB):
        k = km_ref[r : r + QB, :].astype(F32)
        k_most = jnp.maximum(k_most, jnp.max(dot((k * k).astype(BF), heads), axis=0, keepdims=True))
    small_scores = jnp.max(q_most * k_most) <= 3025.0

    def attend(subtract):
        for i in range(rows // QB):
            rs = pl.ds(i * QB, QB)
            outs = []
            sums = []
            qf = qm_ref[rs, :].astype(F32) * 0.125
            for h in range(2):
                mine = (lane < 64) if h == 0 else (lane >= 64)
                base = 64 if h == 0 else 0
                qh = jnp.where(mine, qf, jnp.where(lane == base, 1.0, 0.0)).astype(BF)
                nk = rows + (i + 1) * QB
                s = dot_nt(qh, ka[h, 0:nk, :])
                r = lax.broadcasted_iota(jnp.int32, (QB, QB), 0)
                c = lax.broadcasted_iota(jnp.int32, (QB, QB), 1)
                sd = jnp.where(c <= r, s[:, nk - QB :], -1e30)
                se = s[:, : nk - QB]
                if subtract:
                    m = jnp.maximum(
                        jnp.max(sd, axis=1, keepdims=True), jnp.max(se, axis=1, keepdims=True)
                    )
                    se = se - m
                    sd = sd - m
                p = jnp.concatenate([jnp.exp(se).astype(BF), jnp.exp(sd).astype(BF)], 1)
                o = dot(p, va[h, 0:nk, :])
                outs.append(o / pltpu.roll(o, 64, 1))
                sums.append(m + jnp.log(o) if subtract else jnp.log(o))
            res = jnp.where(lane < 64, outs[0], outs[1])
            res = jnp.where(state == 0, vm_ref[pl.ds(rows + i * QB, QB), :].astype(F32), res)
            o_ref[rs, :] = res.astype(BF)
            l_ref[rs, :] = jnp.where(lane < 64, sums[1], sums[0])

    @pl.when(small_scores)
    def _():
        attend(False)

    @pl.when(jnp.logical_not(small_scores))
    def _():
        attend(True)


def call_in_parts(body, in_specs, out_specs, out_shape, earlier, part, **options):
    used = len(in_specs)

    def kernel(*refs):
        body(*refs[:used], *refs[used + len(earlier) :])

    return pl.pallas_call(
        kernel,
        grid=(part[1],),
        in_specs=in_specs + [pl.BlockSpec(memory_space=pl.ANY)] * len(earlier),
        out_specs=out_specs,
        out_shape=out_shape,
        input_output_aliases={used + i: i for i in range(len(earlier))},
        compiler_params=pltpu.CompilerParams(vmem_limit_bytes=VMEM_LIMIT),
        **options,
    )


def columns(part):
    first = part[0]

    def cols(height, row, off):
        return pl.BlockSpec((height, 128), lambda p: (row, p + first + off))

    return cols


def att_fwd(state, projected, small, earlier, part, rows):
    cols = columns(part)
    return call_in_parts(
        att_fwd_kernel,
        [
            pl.BlockSpec(memory_space=pltpu.SMEM),
            cols(8, rows // 8 - 1, 0),
            cols(rows, 1, 0),
            cols(2 * rows, 0, 6),
            cols(2 * rows, 0, 12),
            cols(16, 0, 0),
        ],
        [cols(rows, 0, 0)] * 3 + [cols(2 * rows, 0, 0)] * 2,
        [
            jax.ShapeDtypeStruct((rows, D), BF),
            jax.ShapeDtypeStruct((rows, D), F32),
            jax.ShapeDtypeStruct((rows, D), BF),
            jax.ShapeDtypeStruct((2 * rows, D), BF),
            jax.ShapeDtypeStruct((2 * rows, D), BF),
        ],
        earlier,
        part,
        scratch_shapes=[pltpu.VMEM((2, 2 * rows, 128), BF)] * 2,
        cost_estimate=cost(
            2 * 2 * 2 * rows * rows * 1.5 * 256 * part[1],
            rows * D * 5 * part[1],
            2 * rows * rows * 1.5 * part[1],
        ),
        name="att_fwd",
    )(state, projected, projected, projected, projected, small, *earlier)


def three(x, lane, base):
    hi = x.astype(BF).astype(F32)
    r = x - hi
    mid = r.astype(BF).astype(F32)
    lo = r - mid
    return jnp.where(
        lane == base, hi, jnp.where(lane == base + 1, mid, jnp.where(lane == base + 2, lo, 0.0))
    )


def conv_back(out_ref, grad_ref, x_ref, start, tail, taps, rows, state):
    height = grad_ref.shape[0]
    joint = jnp.where(state == 2, 1.0, 0.0)
    sums = [jnp.zeros((1, 128), F32)] * 3

    def add(parts, x):
        return [s + jnp.sum(g * x, axis=0, keepdims=True) for s, g in zip(sums, parts)]

    for r in range(0, height, QB):
        ends = r + QB == height
        meets = start + r + QB == rows
        if ends:
            grad = jnp.concatenate([grad_ref[r : r + QB, :], jnp.zeros((8, 128), F32)], 0)
        else:
            grad = grad_ref[r : r + QB + 8, :]
        one = pltpu.roll(grad, QB + 7, 0)[:QB]
        two = pltpu.roll(grad, QB + 6, 0)[:QB]
        grad = grad[:QB]
        if meets and not ends:
            row = row_ids(QB)
            one = jnp.where(row >= QB - 1, one * joint, one)
            two = jnp.where(row >= QB - 2, two * joint, two)
        out_ref[r : r + QB, :] = (taps[0] * grad + taps[1] * one + taps[2] * two).astype(BF)
        sums = add((grad, one, two), x_ref[r : r + QB, :].astype(F32))
    if tail is not None:
        grad = jnp.concatenate([jnp.zeros((8, 128), F32), grad_ref[0:8, :]], 0)
        one = pltpu.roll(grad, 15, 0)[:8] * joint
        two = pltpu.roll(grad, 14, 0)[:8] * joint
        tail[0][...] = (taps[1] * one + taps[2] * two).astype(BF)
        sums = add((grad[:8], one, two), tail[1][...].astype(F32))
    return sums


def att_bwd_kernel(
    state_ref, q_ref, k_ref, v_ref, o_ref, l_ref, do_ref, xt_ref, xq_ref, xk_ref, xv_ref,
    small_ref,
    pq_ref, pt_ref, pk_ref, pv_ref, tg_ref, qa, da, qt, dt, kt, dqt, dqs, dks, dvs,
):
    rows = q_ref.shape[0]
    lane = lax.broadcasted_iota(jnp.int32, (1, 128), 1)
    second = state_ref[0] == 2
    for r in range(0, rows, QB):
        at = pl.ds(r, QB)
        do = do_ref[at, :].astype(F32)
        od = do * o_ref[at, :].astype(F32)
        qf = q_ref[at, :].astype(F32) * 0.125
        lv = l_ref[at, :]
        for h in range(2):
            mine = (lane < 64) if h == 0 else (lane >= 64)
            base = 64 if h == 0 else 0
            delta = jnp.sum(jnp.where(mine, od, 0.0), axis=1, keepdims=True)
            qa[h, at, :] = jnp.where(mine, qf, three(-lv, lane, base)).astype(BF)
            da[h, at, :] = jnp.where(mine, do, three(-delta, lane, base)).astype(BF)
        qt[:, at] = jnp.transpose(qf).astype(BF)
        dt[:, at] = jnp.transpose(do).astype(BF)
    for r in range(0, 2 * rows, QB):
        at = pl.ds(r, QB)
        kt[:, at] = jnp.transpose(k_ref[at, :].astype(F32)).astype(BF)
    dqt[...] = jnp.zeros(dqt.shape, F32)

    def keys(ks, first, diagonal):
        kk = k_ref[ks, :]
        vv = v_ref[ks, :]
        dv = []
        dk = []
        for h in range(2):
            mine = (lane < 64) if h == 0 else (lane >= 64)
            base = 64 if h == 0 else 0
            ones3 = ((lane >= base) & (lane < base + 3)).astype(BF)
            hs = slice(64 * h, 64 * h + 64)
            st = dot_nt(jnp.where(mine, kk, ones3), qa[h, first:rows, :])
            dp = dot_nt(jnp.where(mine, vv, ones3), da[h, first:rows, :])
            p = jnp.exp(st)
            if diagonal:
                r = lax.broadcasted_iota(jnp.int32, (QB, QB), 0)
                c = lax.broadcasted_iota(jnp.int32, (QB, QB), 1)
                seen = jnp.where(r <= c, p[:, :QB], 0.0)
                p = jnp.concatenate([seen, p[:, QB:]], 1) if first + QB < rows else seen
            ds = (p * dp).astype(BF)
            dv.append(dot_nt(dt[hs, first:rows], p.astype(BF)))
            dk.append(dot_nt(qt[hs, first:rows], ds))
            dqt[hs, first:rows] += dot(kt[hs, ks], ds)
        dvs[ks, :] = jnp.transpose(jnp.concatenate(dv, 0))
        dks[ks, :] = jnp.transpose(jnp.concatenate(dk, 0))

    for j in range(rows // QB):
        keys(pl.ds(rows + j * QB, QB), j * QB, True)

    @pl.when(second)
    def _():
        def step(j, carry):
            keys(pl.ds(pl.multiple_of(j * QB, QB), QB), 0, False)
            return carry

        lax.fori_loop(0, rows // QB, step, 0)

    @pl.when(jnp.logical_not(second))
    def _():
        dks[0:rows, :] = jnp.zeros((rows, 128), F32)
        dvs[0:rows, :] = jnp.zeros((rows, 128), F32)

    for r in range(0, rows, QB):
        dqs[r : r + QB, :] = jnp.transpose(dqt[:, r : r + QB]) * 0.125
    state = state_ref[0]
    sq = conv_back(pq_ref, dqs, xq_ref, rows, (pt_ref, xt_ref), taps_of(small_ref[...], 0), rows, state)
    sk = conv_back(pk_ref, dks, xk_ref, 0, None, taps_of(small_ref[...], 1), rows, state)
    sv = conv_back(pv_ref, dvs, xv_ref, 0, None, taps_of(small_ref[...], 2), rows, state)
    tg_ref[...] = jnp.zeros(tg_ref.shape, F32)
    for j in range(3):
        for m, s in enumerate((sq, sk, sv)):
            tg_ref[3 * j + m : 3 * j + m + 1, :] = s[j]


def att_bwd(state, mixed, attended, logs, grad, projected, small, earlier, part, rows):
    cols = columns(part)
    own = cols(rows, 0, 0)
    both = cols(2 * rows, 0, 0)
    return call_in_parts(
        att_bwd_kernel,
        [
            pl.BlockSpec(memory_space=pltpu.SMEM),
            own, both, both, own, own, own,
            cols(8, rows // 8 - 1, 0),
            cols(rows, 1, 0),
            cols(2 * rows, 0, 6),
            cols(2 * rows, 0, 12),
            cols(16, 0, 0),
        ],
        [own, cols(8, 0, 0), both, both, cols(16, 0, 0)],
        [
            jax.ShapeDtypeStruct((rows, D), BF),
            jax.ShapeDtypeStruct((8, D), BF),
            jax.ShapeDtypeStruct((2 * rows, D), BF),
            jax.ShapeDtypeStruct((2 * rows, D), BF),
            jax.ShapeDtypeStruct((16, D), F32),
        ],
        earlier,
        part,
        scratch_shapes=[
            pltpu.VMEM((2, rows, 128), BF),
            pltpu.VMEM((2, rows, 128), BF),
            pltpu.VMEM((128, rows), BF),
            pltpu.VMEM((128, rows), BF),
            pltpu.VMEM((128, 2 * rows), BF),
            pltpu.VMEM((128, rows), F32),
            pltpu.VMEM((rows, 128), F32),
            pltpu.VMEM((2 * rows, 128), F32),
            pltpu.VMEM((2 * rows, 128), F32),
        ],
        cost_estimate=cost(
            5 * 2 * 2 * rows * rows * 1.5 * 256 * part[1],
            rows * D * 7 * part[1],
            2 * rows * rows * 1.5 * part[1],
        ),
        name="att_bwd",
    )(state, *mixed, attended, logs, grad, projected, projected, projected, projected,
      small, *earlier)


def unit_rows(x):
    return x * lax.rsqrt(jnp.mean(x * x, axis=-1, keepdims=True) + norm_eps)


def before_bwd_kernel(x_ref, dt_ref, dk_ref, dv_ref, w_ref, out_ref, gain_ref):
    i = pl.program_id(0)
    hat = unit_rows(x_ref[...].astype(F32))
    gn = dot_nt(dk_ref[...], w_ref[D : 2 * D, :]) + dot_nt(dv_ref[...], w_ref[2 * D : 3 * D, :])

    last_step = pl.num_programs(0) - 1

    @pl.when(i == 0)
    def _():
        gain_ref[...] = jnp.zeros(gain_ref.shape, F32)

    @pl.when(i < last_step)
    def _():
        out_ref[...] = gn.astype(BF)
        gain_ref[...] += jnp.sum(gn * hat, axis=0, keepdims=True)

    @pl.when(i == last_step)
    def _():
        last = gn.shape[0] - 8
        full = jnp.concatenate([gn[:last], gn[last:] + dot_nt(dt_ref[...], w_ref[0:D, :])], 0)
        out_ref[...] = full.astype(BF)
        gain_ref[...] += jnp.sum(full * hat, axis=0, keepdims=True)


def before_bwd(x_both, back, weight, rows):
    dt, dk, dv = back[1:]
    blocks = 4
    height = rows // blocks
    step = pl.BlockSpec((height, D), lambda i: (i, 0))

    def whole(shape):
        return pl.BlockSpec(shape, lambda i: (0, 0))

    return pl.pallas_call(
        before_bwd_kernel,
        grid=(blocks,),
        in_specs=[step, whole((8, D)), step, step, whole((3 * D, D))],
        out_specs=[step, whole((1, D))],
        out_shape=[jax.ShapeDtypeStruct((rows, D), BF), jax.ShapeDtypeStruct((1, D), F32)],
        compiler_params=pltpu.CompilerParams(vmem_limit_bytes=VMEM_LIMIT),
        cost_estimate=cost(2 * rows * D * D * 2, rows * D * 12),
        name="before_bwd",
    )(x_both, dt, dk, dv, weight)


def qkv_bwd_kernel(
    core_ref, x_ref, dq_ref, dt_ref, dk_ref, dv_ref, w_ref, small_ref, gain_one_ref, gain_two_ref, tg_ref,
    *refs, pieces, blocks,
):
    if pieces:
        send_ref, keep_ref, own_ref, acc, gacc = refs
    else:
        keep_ref, ends_ref, own_ref, acc, gacc = refs
    i = pl.program_id(0)
    half = blocks // 2

    @pl.when(i == 0)
    def _():
        acc[...] = jnp.zeros(acc.shape, F32)
        gacc[0:1, :] = gain_one_ref[...]

    hat = unit_rows(x_ref[...].astype(F32))
    low = (hat * small_ref[0:1, :]).astype(BF)
    dk = dk_ref[...]
    dv = dv_ref[...]
    acc[D : 2 * D, :] += dot_tn(low, dk)
    acc[2 * D : 3 * D, :] += dot_tn(low, dv)

    @pl.when(i == half - 1)
    def _():
        acc[0:D, :] += dot_tn(low[low.shape[0] - 8 :], dt_ref[...])

    @pl.when(i >= half)
    def _():
        dq = dq_ref[...]
        acc[0:D, :] += dot_tn(low, dq)
        full = (
            dot_nt(dk, w_ref[D : 2 * D, :])
            + dot_nt(dv, w_ref[2 * D : 3 * D, :])
            + dot_nt(dq, w_ref[0:D, :])
        )
        own_ref[...] = full
        gacc[0:1, :] += jnp.sum(full * hat, axis=0, keepdims=True)

    @pl.when(i == blocks - 1)
    def _():
        small = jnp.concatenate(
            [gacc[0:1, :], gain_two_ref[...], tg_ref[0:9, :], jnp.zeros((5, D), F32)], 0
        )
        if pieces:
            core = core_ref[0]
            height = 3 * D // (2 * pieces)
            wide = height + 16
            for j in range(pieces):
                to = pl.ds(j * wide, wide)
                away = pl.ds(pl.multiple_of((2 * j + 1 - core) * height, 16), wide)
                here = pl.ds(pl.multiple_of((2 * j + core) * height, 16), wide)
                send_ref[to, :] = acc[away, :].astype(BF)
                keep_ref[to, :] = acc[here, :].astype(BF)
            send_ref[pieces * wide :, :] = small.astype(BF)
            keep_ref[pieces * wide :, :] = small.astype(BF)
        else:
            keep_ref[...] = acc[0 : 3 * D, :].astype(BF)
            ends_ref[...] = small


def qkv_bwd(core, x_both, back, weight, small, gain_one_grad, gain_two_grad, tap_grads, rows, pieces):
    dq, dt, dk, dv = back
    blocks = 4
    half = blocks // 2
    height = 2 * rows // blocks
    step = pl.BlockSpec((height, D), lambda i: (i, 0))
    late = pl.BlockSpec((height, D), lambda i: (jnp.maximum(i - half, 0), 0))

    def whole(shape):
        return pl.BlockSpec(shape, lambda i: (0, 0))

    if pieces:
        packed = 3 * D // 2 + 16 * pieces + 16
        outs = [jax.ShapeDtypeStruct((packed, D), BF), jax.ShapeDtypeStruct((packed, D), BF)]
        out_at = [whole((packed, D))] * 2
    else:
        outs = [jax.ShapeDtypeStruct((3 * D, D), BF), jax.ShapeDtypeStruct((16, D), F32)]
        out_at = [whole((3 * D, D)), whole((16, D))]

    def body(*refs):
        qkv_bwd_kernel(*refs, pieces=pieces, blocks=blocks)

    return pl.pallas_call(
        body,
        grid=(blocks,),
        in_specs=[
            pl.BlockSpec(memory_space=pltpu.SMEM),
            step, late, whole((8, D)), step, step, whole((3 * D, D)),
            whole((16, D)), whole((1, D)), whole((1, D)), whole((16, D)),
        ],
        out_specs=out_at + [late],
        out_shape=outs + [jax.ShapeDtypeStruct((rows, D), F32)],
        scratch_shapes=[pltpu.VMEM((3 * D + 16, D), F32), pltpu.VMEM((8, D), F32)],
        compiler_params=pltpu.CompilerParams(vmem_limit_bytes=VMEM_LIMIT),
        cost_estimate=cost(2 * 2 * D * D * 4 * rows, rows * D * 30),
        name="qkv_bwd",
    )(core, x_both, dq, dt, dk, dv, weight, small, gain_one_grad, gain_two_grad, tap_grads)


def merge(index, keep, got, height, taken):
    rows = keep.shape[0]
    out_rows = taken * height + 16 if taken else rows

    def body(index_ref, keep_ref, got_ref, send_ref, stay_ref):
        if not taken:
            total = keep_ref[...].astype(F32) + got_ref[...].astype(F32)
            send_ref[...] = total.astype(BF)
            stay_ref[...] = total
            return
        for j in range(taken):
            to = pl.ds(j * height, height)
            away = pl.ds(pl.multiple_of(index_ref[j] * height, 16), height)
            here = pl.ds(pl.multiple_of(index_ref[taken + j] * height, 16), height)
            send_ref[to, :] = (keep_ref[away, :].astype(F32) + got_ref[away, :].astype(F32)).astype(BF)
            stay_ref[to, :] = keep_ref[here, :].astype(F32) + got_ref[here, :].astype(F32)
        end = keep_ref[rows - 16 :, :].astype(F32) + got_ref[rows - 16 :, :].astype(F32)
        send_ref[taken * height :, :] = end.astype(BF)
        stay_ref[taken * height :, :] = end

    vmem = pl.BlockSpec(memory_space=pltpu.VMEM)
    return pl.pallas_call(
        body,
        in_specs=[pl.BlockSpec(memory_space=pltpu.SMEM), vmem, vmem],
        out_specs=[vmem, vmem],
        out_shape=[
            jax.ShapeDtypeStruct((out_rows, D), BF),
            jax.ShapeDtypeStruct((out_rows, D), F32),
        ],
        compiler_params=pltpu.CompilerParams(vmem_limit_bytes=32 << 20),
        cost_estimate=cost(rows * D, rows * D * 12),
        name="merge",
    )(index, keep, got)


def merge_grid(index, keep, got, taken, kept=F32):
    height = keep.shape[1]

    def body(index_ref, ka_ref, ga_ref, kb_ref, gb_ref, send_ref, stay_ref):
        send_ref[...] = (ka_ref[...].astype(F32) + ga_ref[...].astype(F32)).astype(BF)
        stay_ref[...] = (kb_ref[...].astype(F32) + gb_ref[...].astype(F32)).astype(kept)

    away = pl.BlockSpec((1, height, D), lambda i, index: (index[i], 0, 0))
    here = pl.BlockSpec((1, height, D), lambda i, index: (index[taken + i], 0, 0))
    step = pl.BlockSpec((1, height, D), lambda i, index: (i, 0, 0))
    return pl.pallas_call(
        body,
        grid_spec=pltpu.PrefetchScalarGridSpec(
            num_scalar_prefetch=1,
            grid=(taken,),
            in_specs=[away, away, here, here],
            out_specs=[step, step],
        ),
        out_shape=[
            pltpu.HBM((taken, height, D), BF),
            pltpu.HBM((taken, height, D), kept),
        ],
        compiler_params=pltpu.CompilerParams(vmem_limit_bytes=32 << 20),
        cost_estimate=cost(taken * height * D * 2, taken * height * D * 16),
        name="merge_grid",
    )(index, keep, got, keep, got)


def arrange(index, blocks):
    height = blocks[0].shape[0] - 16

    def body(index_ref, *refs):
        first_ref, rest_ref, ends, total, sems = refs[4:]
        refs = refs[:4]
        tail = pl.ds(height, 16)
        places = [first_ref.at[pl.ds(0, height)]] + [rest_ref.at[pl.ds(i * height, height)] for i in range(3)]
        for k in range(4):
            pltpu.make_async_copy(refs[k].at[tail], ends.at[k], sems.at[4 + k]).start()
        for i in range(4):
            for k in range(4):

                @pl.when(index_ref[i] == k)
                def _():
                    pltpu.make_async_copy(refs[k].at[pl.ds(0, height)], places[i], sems.at[i]).start()

        for k in range(4):
            pltpu.make_async_copy(refs[k].at[tail], ends.at[k], sems.at[4 + k]).wait()
        sums = [ends[k].astype(F32) for k in range(4)]
        total[...] = (sums[0] + sums[1] + sums[2] + sums[3]).astype(BF)
        last = pltpu.make_async_copy(total, first_ref.at[tail], sems.at[8])
        last.start()
        for i in range(4):
            pltpu.make_async_copy(refs[0].at[pl.ds(0, height)], places[i], sems.at[i]).wait()
        last.wait()

    held = pl.BlockSpec(memory_space=pltpu.HBM)
    return pl.pallas_call(
        body,
        in_specs=[pl.BlockSpec(memory_space=pltpu.SMEM)] + [held] * 4,
        out_specs=[held, held],
        out_shape=[
            jax.ShapeDtypeStruct((height + 16, D), BF),
            jax.ShapeDtypeStruct((3 * height, D), BF),
        ],
        scratch_shapes=[
            pltpu.VMEM((4, 16, D), BF),
            pltpu.VMEM((16, D), BF),
            pltpu.SemaphoreType.DMA((9,)),
        ],
        compiler_params=pltpu.CompilerParams(vmem_limit_bytes=32 << 20),
        cost_estimate=cost(4 * height * D, 4 * height * D * 4),
        name="arrange",
    )(index, *blocks)


def join(own, got, shared=16):
    rows = own.shape[0]
    body_rows = rows - shared

    def body(own_ref, got_ref, out_ref):
        out_ref[0:body_rows, :] = own_ref[0:body_rows, :]
        out_ref[body_rows : 2 * body_rows, :] = got_ref[0:body_rows, :]
        if shared:
            out_ref[2 * body_rows :, :] = own_ref[body_rows:, :] + got_ref[body_rows:, :]

    vmem = pl.BlockSpec(memory_space=pltpu.VMEM)
    return pl.pallas_call(
        body,
        in_specs=[vmem, vmem],
        out_specs=vmem,
        out_shape=jax.ShapeDtypeStruct((2 * body_rows + shared, D), BF),
        compiler_params=pltpu.CompilerParams(vmem_limit_bytes=32 << 20),
        cost_estimate=cost(rows * D, rows * D * 8),
        name="join",
    )(own, got)


def join_held(own, got):
    rows = own.shape[0]
    cuts = 4
    size = rows // cuts

    def body(own_ref, got_ref, out_ref, sems):
        copies = []
        for k, ref in enumerate((own_ref, got_ref)):
            for j in range(cuts):
                source = ref.at[pl.ds(j * size, size)]
                to = out_ref.at[pl.ds(k * rows + j * size, size)]
                copies.append(pltpu.make_async_copy(source, to, sems.at[k * cuts + j]))
        for copy in copies:
            copy.start()
        for copy in copies:
            copy.wait()

    held = pl.BlockSpec(memory_space=pltpu.HBM)
    return pl.pallas_call(
        body,
        in_specs=[held, held],
        out_specs=held,
        out_shape=jax.ShapeDtypeStruct((2 * rows, D), BF),
        scratch_shapes=[pltpu.SemaphoreType.DMA((2 * cuts,))],
        compiler_params=pltpu.CompilerParams(vmem_limit_bytes=16 << 20),
        cost_estimate=cost(0, rows * D * 8),
        name="join_held",
    )(own, got)


def hold(block, other):
    held = pl.BlockSpec(memory_space=pl.ANY)
    return pl.pallas_call(
        lambda block_ref, other_ref, out_ref: None,
        in_specs=[held, held],
        out_specs=held,
        out_shape=jax.ShapeDtypeStruct(block.shape, block.dtype),
        input_output_aliases={0: 0},
        name="hold",
    )(block, other)


def qkv_fwd_kernel(index_ref, x_ref, *refs, pieces, blocks):
    if pieces:
        own_ref, got_ref, out_ref, small_ref, weight = refs
    else:
        weight, given_ref, out_ref, small_ref = refs
    i = pl.program_id(0)

    @pl.when(i == 0)
    def _():
        if pieces:
            height = 3 * D // (2 * pieces)
            for j in range(pieces):
                at = pl.ds(j * height, height)
                for k, ref in enumerate((own_ref, got_ref)):
                    to = pl.multiple_of(index_ref[k * pieces + j] * height, 16)
                    weight[pl.ds(to, height), :] = ref[at, :]
            end = pl.ds(pieces * height, 16)
            small_ref[...] = own_ref[end, :].astype(F32) + got_ref[end, :].astype(F32)
        else:
            small_ref[...] = given_ref[...]

    x = x_ref[...].astype(F32)
    hat = x * lax.rsqrt(jnp.mean(x * x, axis=-1, keepdims=True) + norm_eps)
    low = (hat * small_ref[0:1, :]).astype(BF)

    @pl.when(i >= blocks // 2 - 1)
    def _():
        out_ref[:, 0:D] = dot(low, weight[0:D, :]).astype(BF)

    out_ref[:, D : 2 * D] = dot(low, weight[D : 2 * D, :]).astype(BF)
    out_ref[:, 2 * D : 3 * D] = dot(low, weight[2 * D : 3 * D, :]).astype(BF)


def qkv_fwd(index, x_both, weights, rows, pieces):
    blocks = 4
    height = 2 * rows // blocks

    def body(*refs):
        qkv_fwd_kernel(*refs, pieces=pieces, blocks=blocks)

    return pl.pallas_call(
        body,
        grid=(blocks,),
        in_specs=[
            pl.BlockSpec(memory_space=pltpu.SMEM),
            pl.BlockSpec((height, D), lambda i: (i, 0)),
            *[pl.BlockSpec(w.shape, lambda i: (0, 0)) for w in weights],
        ],
        out_specs=[
            pl.BlockSpec((height, 3 * D), lambda i: (i, 0)),
            pl.BlockSpec((16, D), lambda i: (0, 0)),
        ]
        + ([pl.BlockSpec((3 * D, D), lambda i: (0, 0))] if pieces else []),
        out_shape=[
            jax.ShapeDtypeStruct((2 * rows, 3 * D), BF),
            jax.ShapeDtypeStruct((16, D), F32),
        ]
        + ([jax.ShapeDtypeStruct((3 * D, D), BF)] if pieces else []),
        compiler_params=pltpu.CompilerParams(vmem_limit_bytes=VMEM_LIMIT),
        cost_estimate=cost(2 * 2 * rows * D * 3 * D, rows * D * 20),
        name="qkv_fwd",
    )(index, x_both, *weights)


def ffn_kernel(
    state_ref, index_ref, x_ref, att_ref, cot_ref, small_ref, own_ref, own_two_ref, got_ref, got_two_ref,
    out_ref, gh_ref, ga_ref, gain_grad_ref, away_ref, here_ref,
    hidden, low, total, back, cot, sq, gb, weights, stage_up, stage_down, stage_out, in_sems, sems,
):
    c = pl.program_id(0)
    rows = x_ref.shape[0]
    blocks = [pl.ds(i * QB, QB) for i in range(rows // QB)]
    last = c == pl.num_programs(0) - 1
    core = index_ref[24]

    def fetch(k, j):
        ref = ((own_ref, own_two_ref), (got_ref, got_two_ref))[k][j // 6]
        piece = index_ref[12 * k + j]
        to = weights.at[pl.ds(3 * piece, 3)]
        return pltpu.make_async_copy(ref.at[pl.ds(3 * (j % 6), 3)], to, in_sems.at[piece])

    def fetched(pieces):
        for piece in pieces:
            at = weights.at[pl.ds(3 * piece, 3)]
            pltpu.make_async_copy(own_ref.at[pl.ds(0, 3)], at, in_sems.at[piece]).wait()

    def put(source, group, count, column, sem, wait=False):
        piece = group // 3
        at = (piece // 2) * 3 + group % 3

        def copy(ref):
            to = ref.at[pl.ds(at, count)] if column is None else ref.at[pl.ds(at, count), column]
            return pltpu.make_async_copy(source, to, sems.at[sem])

        if wait:
            copy(here_ref).wait()
            return
        mine = piece % 2 == core

        @pl.when(mine)
        def _():
            copy(here_ref).start()

        @pl.when(jnp.logical_not(mine))
        def _():
            copy(away_ref).start()

    def put_up(i, wait=False):
        start = 0
        k = 0
        while start < 32:
            count = min(3 - (8 + start) % 3, 32 - start)
            put(stage_up.at[i, pl.ds(start, count)], 8 + start, count, i, 20 * i + k, wait)
            start += count
            k += 1

    def put_down(i, wait=False):
        for k in range(8):
            put(stage_down.at[i, pl.ds(k, 1)], 40 + 8 * i + k, 1, None, 20 * i + 12 + k, wait)

    def put_out(wait=False):
        for k in range(8):
            put(stage_out.at[pl.ds(k, 1)], k, 1, None, 80 + k, wait)

    def square(first):
        return weights[first : first + 8].reshape(D, D)

    @pl.when(c == 0)
    def _():
        for early in (True, False):
            for k in range(2):
                for j in range(12):

                    @pl.when((index_ref[12 * k + j] < 3) == early)
                    def _():
                        fetch(k, j).start()

        cot[...] = jnp.where(state_ref[0] > 0, cot_ref[...], jnp.zeros((), BF))
        total[...] = jnp.zeros(total.shape, F32)
        back[...] = jnp.zeros(back.shape, F32)
        fetched(range(3))
        wo = square(0)
        for b in blocks:
            h = x_ref[b, :].astype(F32) + dot(att_ref[b, :], wo)
            hidden[b, :] = h
            hat = h * lax.rsqrt(jnp.mean(h * h, axis=-1, keepdims=True) + norm_eps)
            low[b, :] = (hat * small_ref[1:2, :]).astype(BF)

    for i, pieces in enumerate((range(3, 16), range(16, 19), range(19, 22), range(22, 24))):

        @pl.when(c == i)
        def _():
            fetched(pieces)

    up = weights[8:40, c].reshape(D, D)
    down = weights[pl.ds(40 + 8 * c, 8)].reshape(D, D)
    for b in blocks:
        act = jnp.maximum(dot(low[b, :], up), 0.0)
        s = (act * act).astype(BF)
        sq[b, :] = s
        total[b, :] += dot(s, down)
        g = (dot_nt(cot[b, :], down) * 2.0 * act).astype(BF)
        gb[b, :] = g
        back[b, :] += dot_nt(g, up)
    stage_down[c] = dot_tn(sq[...], cot[...]).reshape(8, 4, 24, D).astype(BF)
    stage_up[c] = dot_tn(low[...], gb[...]).reshape(32, 24, D).astype(BF)
    put_down(c)
    put_up(c)

    @pl.when(last)
    def _():
        gain = small_ref[1:2, :]
        wo = square(0)
        sums = jnp.zeros((1, D), F32)
        for b in blocks:
            h = hidden[b, :]
            out_ref[b, :] = (h + total[b, :]).astype(BF)
            factor = lax.rsqrt(jnp.mean(h * h, axis=-1, keepdims=True) + norm_eps)
            hat = h * factor
            g = back[b, :]
            sums = sums + jnp.sum(g * hat, axis=0, keepdims=True)
            weighted = g * gain
            inner = jnp.mean(weighted * hat, axis=-1, keepdims=True)
            grad = cot[b, :].astype(F32) + factor * (weighted - hat * inner)
            gh_ref[b, :] = grad
            grad_low = grad.astype(BF)
            gb[b, :] = grad_low
            ga_ref[b, :] = dot_nt(grad_low, wo).astype(BF)
        gain_grad_ref[...] = sums
        stage_out[...] = dot_tn(att_ref[...], gb[...]).reshape(8, 4, 24, D).astype(BF)
        put_out()
        for i in range(4):
            put_down(i, True)
            put_up(i, True)
        put_out(True)


def ffn(state, index, tokens, attended, out_grad, small, weights, rows):
    def whole(shape):
        return pl.BlockSpec(shape, lambda c: (0,) * len(shape), pipeline_mode=pl.Buffered(1))

    act = whole((rows, D))
    held = pl.BlockSpec(memory_space=pl.ANY)
    scalars = pl.BlockSpec(memory_space=pltpu.SMEM)
    half = (36, 4, 24, D)
    return pl.pallas_call(
        ffn_kernel,
        grid=(4,),
        in_specs=[scalars, scalars, act, act, act, whole((16, D)), held, held, held, pl.BlockSpec(memory_space=pltpu.VMEM)],
        out_specs=[act, act, act, whole((1, D)), held, held],
        out_shape=[
            jax.ShapeDtypeStruct((rows, D), BF),
            jax.ShapeDtypeStruct((rows, D), F32),
            jax.ShapeDtypeStruct((rows, D), BF),
            jax.ShapeDtypeStruct((1, D), F32),
            jax.ShapeDtypeStruct(half, BF),
            jax.ShapeDtypeStruct(half, BF),
        ],
        scratch_shapes=[
            pltpu.VMEM((rows, D), F32),
            pltpu.VMEM((rows, D), BF),
            pltpu.VMEM((rows, D), F32),
            pltpu.VMEM((rows, D), F32),
            pltpu.VMEM((rows, D), BF),
            pltpu.VMEM((rows, D), BF),
            pltpu.VMEM((rows, D), BF),
            pltpu.VMEM((72, 4, 24, D), BF),
            pltpu.VMEM((4, 32, 24, D), BF),
            pltpu.VMEM((4, 8, 4, 24, D), BF),
            pltpu.VMEM((8, 4, 24, D), BF),
            pltpu.SemaphoreType.DMA((24,)),
            pltpu.SemaphoreType.DMA((88,)),
        ],
        compiler_params=pltpu.CompilerParams(vmem_limit_bytes=60 << 20),
        cost_estimate=cost(2 * rows * D * D * (24 + 3), 2 * 12 * D * D * 2 + rows * D * 16),
        name="ffn",
    )(state, index, tokens, attended, out_grad, small, *weights)


def shift_flat(block, distance):
    count = lax.axis_size(AXES)
    route = [(i - distance, i) for i in range(count) if 0 <= i - distance < count]
    return lax.ppermute(block, AXES, route)


def shift_ctx(block, distance):
    count = lax.axis_size("ctx")
    route = [(i - distance, i) for i in range(count) if 0 <= i - distance < count]
    return lax.ppermute(block, "ctx", route)


def after(value, *others):
    return lax.optimization_barrier((value, *others))[0]


def swap(block, even_bit, odd_bit, planes=None):
    count = lax.axis_size(AXES)
    route = [
        (i, i ^ (odd_bit if i & 1 else even_bit))
        for i in range(count)
        if planes is None or i >> 3 in planes
    ]
    return lax.ppermute(block, AXES, route)


def to_aligned(shard, place, count, delta):
    rows = shard.shape[0]
    lag = delta * (count - 1)
    back = -(-lag // rows)
    if back == 1:
        keep = -(-lag // 8) * 8
        parts = [shift_flat(shard[rows - keep :], 1), shard]
    else:
        keep = back * rows
        parts = [shift_flat(shard, s) for s in range(back, 0, -1)] + [shard]
    joined = jnp.concatenate(parts, 0)
    return lax.dynamic_slice_in_dim(joined, keep - delta * place, rows - delta, 0)


def small_part(shard, place, count, delta):
    rows = shard.shape[0]
    extra = count * delta
    zeros = jnp.zeros((extra, 128), shard.dtype)
    joined = jnp.concatenate([zeros, shard, zeros], 0)
    start = extra + count * (rows - delta) - place * rows
    return lax.dynamic_slice_in_dim(joined, jnp.minimum(start, rows + extra), extra, 0)


def from_aligned(chunk, small, place, count, delta, rows):
    aligned = rows - delta
    ahead = -(-(count * delta) // aligned)
    parts = [chunk]
    if ahead == 1:
        keep = small.shape[0]
        got = shift_flat(chunk[:keep], -1)
        parts.append(jnp.where(place == count - 1, small, got))
    else:
        pad = ahead * aligned - small.shape[0]
        tail = jnp.concatenate([small, jnp.zeros((pad, 128), small.dtype)], 0)
        for s in range(1, ahead + 1):
            got = shift_flat(chunk, -s)
            for e in range(s):
                piece = tail[e * aligned : (e + 1) * aligned]
                got = jnp.where(place == count - s + e, piece, got)
            parts.append(got)
    return lax.dynamic_slice_in_dim(jnp.concatenate(parts, 0), delta * place, rows, 0)


def regroup(block):
    return block.reshape(-1, 24, 4, D).transpose(0, 2, 1, 3)


def ungroup(block):
    return block.reshape(-1, 4, 24, D).transpose(0, 2, 1, 3)


def normalize(values, gain):
    factor = lax.rsqrt(jnp.mean(values * values, axis=-1, keepdims=True) + norm_eps)
    scaled = values * factor
    return (scaled, factor, scaled * gain)


def norm_back(grad_in, scaled, factor, gain):
    weighted = grad_in * gain
    inner_mean = jnp.mean(weighted * scaled, axis=-1, keepdims=True)
    return factor * (weighted - scaled * inner_mean)


def adam_update(master, moment_one, moment_two, gradient, step_count, row_start):
    row_index = row_start + jnp.arange(master.shape[0], dtype=jnp.int32)
    matrix_rows = (4 * D * D + 2 * D * FF) // 128
    out_first = 3 * D * D // 128
    out_last = 4 * D * D // 128
    is_matrix = (row_index < matrix_rows)[:, None]
    is_out = ((row_index >= out_first) & (row_index < out_last))[:, None]
    step_rate = jnp.where(is_matrix, jnp.where(is_out, 0.5, 0.1), 1.0)
    decay_rate = jnp.where(is_matrix, 0.1, 0.0)
    step_value = step_count[0].astype(jnp.float32)
    new_one = 0.9 * moment_one + 0.1 * gradient
    new_two = 0.999 * moment_two + 0.001 * gradient * gradient
    corr_first = 1.0 - jnp.power(0.9, step_value)
    corr_second = 1.0 - jnp.power(0.999, step_value)
    new_weights = master - step_rate * (
        new_one / corr_first / (jnp.sqrt(new_two / corr_second) + 1e-08) + decay_rate * master
    )
    return (new_weights, new_one, new_two)


def shards(tokens, out_grad, positions, master, first_moment, second_moment, step_count):
    rows = tokens.shape[0]
    assert rows == SEQ_MIN
    count = lax.axis_size(AXES)
    place = lax.axis_index(AXES).astype(jnp.int32)
    owned = master.shape[0]
    aligned = (4 * D * D + 2 * D * FF) // 128 // count
    delta = owned - aligned
    height = aligned * 128 // D
    staged = count == 32
    first_place = positions[0]
    state = jnp.where(first_place < 0, 0, jnp.where(first_place >= SEQ_MIN, 2, 1)).astype(jnp.int32)
    state_vec = state[None]

    chunk = to_aligned(master, place, count, delta).reshape(-1, D)
    if staged:
        group = 3 * place + jnp.arange(3, dtype=jnp.int32)
        in_up = ((group >= 32) & (group < 64))[:, None, None, None]
        chunk = jnp.where(in_up, regroup(chunk), chunk.reshape(3, 4, 24, D)).reshape(-1, D)
    chunk = chunk.astype(BF)
    if staged:
        small = jnp.where(place == count - 1, master[owned - count * delta :], 0.0)
    else:
        small = small_part(master, place, count, delta)
    small = lax.reduce_precision(small, 8, 7)
    core = (place & 1)[None]
    x_bit = (place >> 1) & 1
    y_bit = (place >> 2) & 1
    even = (place & 1) == 0
    if staged:
        z = place >> 3
        mine = jnp.concatenate([chunk, small.astype(BF).reshape(-1, D)], 0)
        tokens_before = shift_ctx(after(tokens, mine), 1)
        far = swap(mine, 16, 16)
        near = swap(mine, 8, 8)
        tokens_both = jnp.concatenate([tokens_before, tokens], 0)
        both = swap(after(far, tokens_both), 8, 8)
        order = jnp.stack([z, z ^ 1, z ^ 2, z ^ 3]).astype(jnp.int32)
        mine, rest = arrange(after(order, state_vec), (mine, near, far, both))
        mine = join(mine, swap(mine, 2, 4))
        mine = join(mine, swap(mine, 4, 2))
        across = swap(rest, 2, 4)
        got = swap(mine, 1, 1)
        index = []
        late_index = []
        for k in (0, 1):
            turn = even if k == 0 else jnp.logical_not(even)
            for j in range(4):
                near, far = j & 1, j >> 1
                x_of = x_bit ^ jnp.where(turn, near, far)
                y_of = y_bit ^ jnp.where(turn, far, near)
                piece = 4 * y_of + 2 * x_of + (core[0] ^ k)
                index.append(piece)
                late_index += [piece, piece + 8, piece + 16]
        index = jnp.stack(index).astype(jnp.int32)
        late_index = jnp.stack(late_index + [core[0]]).astype(jnp.int32)
        projected, small, in_weight = qkv_fwd(index, tokens_both, (mine, got), rows, 4)
    else:
        tokens_both = jnp.concatenate([shift_ctx(tokens, 1), tokens], 0)
        wide = lax.all_gather(chunk, AXES, axis=0, tiled=True)
        small = lax.psum(small, AXES)[:96].reshape(-1, D)
        in_weight = wide[: 3 * D]
        projected, small = qkv_fwd(core, tokens_both, (in_weight, small), rows, 0)
        late_index = jnp.arange(25, dtype=jnp.int32) % 24
    gain_first = small[0]

    forward = []
    if staged:
        rest = join_held(after(rest, projected), across)
        line = swap(rest, 4, 2)
        core_rest = swap(rest, 1, 1)
        forward = att_fwd(after(state_vec, rest), projected, small, forward, FORWARD_PARTS[0], rows)
        line = hold(line, forward[0])
        core_line = swap(line, 1, 1)
        forward = att_fwd(after(state_vec, line, core_rest), projected, small, forward, FORWARD_PARTS[1], rows)
        late_weights = [w.reshape(18, 4, 24, D) for w in (rest, line, core_rest, core_line)]
    else:
        for part in FORWARD_PARTS:
            forward = att_fwd(state_vec, projected, small, forward, part, rows)
        grouped = jnp.concatenate(
            [
                wide[3 * D : 4 * D].reshape(-1, 4, 24, D),
                regroup(wide[4 * D : 8 * D]),
                wide[8 * D :].reshape(-1, 4, 24, D),
            ],
            0,
        )
        late_weights = [grouped[18 * k : 18 * k + 18] for k in range(4)]
    attn_low, logs, *mixed = forward

    layer_out, grad_hidden, grad_attended, grad_gain_two, away_grad, here_grad = ffn(
        state_vec, late_index, tokens, attn_low, out_grad, small, late_weights, rows
    )

    def backward(start, done, part):
        return att_bwd(
            start, mixed, attn_low, logs, grad_attended, projected, small, done, BACKWARD_PARTS[part], rows
        )

    if staged:
        stay = [jnp.where(even, 2 * j + x_bit, 2 * y_bit + j) for j in range(2)]
        away = [jnp.where(even, 2 * j + 1 - x_bit, 2 * (1 - y_bit) + j) for j in range(2)]
        pick_plane = jnp.stack(away + stay).astype(jnp.int32)
        other = jnp.where(even, y_bit, x_bit)
        pick_line = jnp.stack([1 - other, other]).astype(jnp.int32)

        def of_quarters(pick, held):
            half = pick.shape[0] // 2
            steps = [pick[s * half + j] + held * t for s in range(2) for t in range(3) for j in range(half)]
            return jnp.stack(steps)

        late_keep = here_grad.reshape(12, height, D)
        late_got = swap(away_grad.reshape(12, height, D), 1, 1)
        done = backward(state_vec, [], 0)
        late_send, late_keep = merge_grid(
            after(of_quarters(pick_plane, 4), done[4]), late_keep, late_got, 6, BF
        )
        late_got = swap(late_send, 2, 4)
        done = backward(after(state_vec, late_send), done, 1)
        late_send, late_keep = merge_grid(
            after(of_quarters(pick_line, 2), done[4]), late_keep, late_got, 3
        )
        late_got = swap(late_send, 4, 2)
        done = backward(after(state_vec, late_send), done, 2)
        z_even = (z & 1) == 0
        low_pair = [jnp.where(z_even, 0, 0), jnp.where(z_even, 2, 1)]
        high_pair = [jnp.where(z_even, 0, 0), jnp.where(z_even, 1, 2)]
        pick_z = jnp.stack(low_pair + high_pair).astype(jnp.int32)
        late_send, late_keep = merge_grid(after(pick_z, done[4]), late_keep, late_got, 2)
        late_got = swap(late_send, 8, 8)
        done = backward(after(state_vec, late_send), done, 3)
        high = z >> 1
        pick_last = jnp.stack([1 - high, high]).astype(jnp.int32)
        late_send, late_keep = merge_grid(after(pick_last, done[4]), late_keep, late_got, 1)
        late_got = swap(late_send, 16, 16, (0, 1, 3))
        sums_state = after(core, late_send)
    else:
        done = []
        for part in range(4):
            done = backward(state_vec, done, part)
        sums_state = core
    *back, tap_grads = done
    grads_before, gain_one_grad = before_bwd(tokens_both, back, in_weight, rows)
    from_next = shift_ctx(grads_before, -1)
    sums = qkv_bwd(
        after(sums_state, grads_before), tokens_both, back, in_weight, small, gain_one_grad, grad_gain_two, tap_grads, rows,
        4 if staged else 0,
    )
    grad_normed_one = sums[2]
    scaled_one, factor_one, _ = normalize(tokens.astype(F32), gain_first)
    input_grad = grad_hidden + norm_back(
        grad_normed_one + from_next.astype(F32), scaled_one, factor_one, gain_first
    )

    if staged:
        send, keep = sums[:2]
        got = swap(after(send, late_got, from_next), 1, 1)
        send, keep = merge(pick_plane, keep, got, height + 16, 2)
        got = swap(send, 2, 4)
        late_got = after(late_got, send)
        late_chunk = late_keep[0] + late_got[0].astype(F32)
        late_chunk = jnp.where(in_up, ungroup(late_chunk).reshape(3, 4, 24, D), late_chunk.reshape(3, 4, 24, D))
        late_chunk = late_chunk.reshape(-1, D)
        late_next = shift_flat(late_chunk[:16], -1)
        send, keep = merge(after(pick_line, late_chunk), keep, got, height + 16, 1)
        got = swap(send, 4, 2)
        send, keep = merge(core, keep, got, height + 16, 0)
        got = swap(send, 8, 8)
        send, keep = merge(after(core, input_grad, late_next), keep, got, height + 16, 0)
        got = swap(send, 16, 16, (1, 2))
        first = keep + got.astype(F32)
        quarter = count // 4
        follow = jnp.where(place < quarter - 1, first[height : height + 16], late_next)
        follow = jnp.where(place == count - 1, first[height + 16 :], follow)
        chunk_grad = jnp.where(place < quarter, first[:height], late_chunk)
        chunk_grad = jnp.concatenate([chunk_grad, follow], 0).reshape(-1, 128)
        gradient = lax.dynamic_slice_in_dim(chunk_grad, delta * place, owned, 0)
    else:
        flat_grad = jnp.stack([here_grad.reshape(12, 3, 4, 24, D), away_grad.reshape(12, 3, 4, 24, D)], 1)
        flat_grad = flat_grad.reshape(72, 4, 24, D)
        wide_grad = jnp.concatenate(
            [
                sums[0],
                flat_grad[:8].reshape(-1, D),
                ungroup(flat_grad[8:40]).reshape(-1, D),
                flat_grad[40:].reshape(-1, D),
            ],
            0,
        )
        chunk_grad = lax.psum_scatter(wide_grad, AXES, scatter_dimension=0, tiled=True).astype(F32)
        used = sums[1].reshape(-1, 128)
        extra = count * delta
        small_grad = jnp.concatenate([used, jnp.zeros((extra - used.shape[0], 128), F32)], 0)
        small_grad = lax.psum(small_grad, AXES)
        gradient = from_aligned(chunk_grad.reshape(-1, 128), small_grad, place, count, delta, owned)
    new_weights, new_one, new_two = adam_update(
        master, first_moment, second_moment, gradient, step_count, place * owned
    )
    return (layer_out, input_grad, new_weights, new_one, new_two, new_weights.astype(BF))


def solution(mesh):
    spread = P(AXES, None)
    return jax.shard_map(
        shards,
        mesh=mesh,
        in_specs=(spread, spread, P(AXES), spread, spread, spread, P()),
        out_specs=(spread,) * 6,
        check_vma=False,
    )
```
